32 devices in a mesh: tensor: 4 (over y, core), seq: 8 (over z, x).
Axes of the slice: x: 2, y: 2, z: 4, core: 2. Of those that a mesh axis runs over, the one named last changes fastest.
Arguments:
- frames: bfloat16 [4096, 1536], P('seq', 'tensor'), may hold values from -8 to 8
- segment: int32 [4096], replicated, may hold values from 0 to 15, never falling along the last dimension, each value on 1 to 512 neighbouring positions
- time_token: bfloat16 [2, 1536], replicated, may hold values from -6 to 6
- context: bfloat16 [2, 128, 768], replicated, may hold values from -6 to 6
- gain_attn: float32 [1536], P('tensor'), may hold values from 0.5 to 1.5
- bias_attn: float32 [1536], P('tensor'), may hold values from -1.75 to 1.75
- gain_cross: float32 [1536], P('tensor'), may hold values from 0.5 to 1.5
- bias_cross: float32 [1536], P('tensor'), may hold values from -1.75 to 1.75
- gain_ffn: float32 [1536], P('tensor'), may hold values from 0.5 to 1.5
- bias_ffn: float32 [1536], P('tensor'), may hold values from -1.75 to 1.75
- w_query: bfloat16 [1536, 1536], P(None, 'tensor'), may hold values from -0.15625 to 0.15625
- w_key: bfloat16 [1536, 1536], P(None, 'tensor'), may hold values from -0.15625 to 0.15625
- w_value: bfloat16 [1536, 1536], P(None, 'tensor'), may hold values from -0.15625 to 0.15625
- w_out: bfloat16 [1536, 1536], P('tensor'), may hold values from -1.25 to 1.25
- c_query: bfloat16 [1536, 1536], P(None, 'tensor'), may hold values from -0.15625 to 0.15625
- c_key: bfloat16 [768, 1536], P(None, 'tensor'), may hold values from -0.21875 to 0.21875
- c_value: bfloat16 [768, 1536], P(None, 'tensor'), may hold values from -0.21875 to 0.21875
- c_out: bfloat16 [1536, 1536], P('tensor'), may hold values from -1.25 to 1.25
- w_gate: bfloat16 [1536, 6144], P(None, 'tensor'), may hold values from -1 to 1
- w_up: bfloat16 [1536, 6144], P(None, 'tensor'), may hold values from -1 to 1
- w_down: bfloat16 [6144, 1536], P('tensor'), may hold values from -0.078125 to 0.078125
- out_grad: bfloat16 [4096, 1536], P('seq', 'tensor'), may hold values from -8 to 8
Outputs:
- block_out: bfloat16 [4096, 1536], P('seq', 'tensor')
- d_frames: float32 [4096, 1536], P('seq', 'tensor')
- d_gain_attn: float32 [1536], P(('tensor', 'seq'))
- d_bias_attn: float32 [1536], P(('tensor', 'seq'))
- d_gain_cross: float32 [1536], P(('tensor', 'seq'))
- d_bias_cross: float32 [1536], P(('tensor', 'seq'))
- d_gain_ffn: float32 [1536], P(('tensor', 'seq'))
- d_bias_ffn: float32 [1536], P(('tensor', 'seq'))
- d_w_query: float32 [1536, 1536], P('seq', 'tensor')
- d_w_key: float32 [1536, 1536], P('seq', 'tensor')
- d_w_value: float32 [1536, 1536], P('seq', 'tensor')
- d_w_out: float32 [1536, 1536], P(('tensor', 'seq'))
- d_c_query: float32 [1536, 1536], P('seq', 'tensor')
- d_c_key: float32 [768, 1536], P('seq', 'tensor')
- d_c_value: float32 [768, 1536], P('seq', 'tensor')
- d_c_out: float32 [1536, 1536], P(('tensor', 'seq'))
- d_w_gate: float32 [1536, 6144], P('seq', 'tensor')
- d_w_up: float32 [1536, 6144], P('seq', 'tensor')
- d_w_down: float32 [6144, 1536], P(('tensor', 'seq'))
The draws below stay inside these ranges and needn't reach their ends.
Inputs may be any that keep to these rules, and one draw needn't show every extreme that they name: `segment`: clip numbers never fall along the frames; each clip covers 1 to 512 frames and one covers exactly 512.
All inputs are finite; a program needn't handle non-finite values.
Results may differ from the reference program's by a relative error of at most 0.03.
Values may be sent and summed in bfloat16 or wider, within the bound.
No kernel may reach another device: no remote copies, remote signals or barrier semaphores. Data moves between devices by JAX's collectives and lax.ppermute only.
A program may use at most 192 MiB of HBM per device.

```python
import math
import jax
import jax.numpy as jnp
import numpy as np
from jax import lax

D = 1536
FF = 6144
CD = 768
CTX = 128
HEAD_SIZE = 64
TOK_DEV = 512
TOKENS = 4096
ROW_FRAMES = 2048
ROWS = 2
N_SEQ = 8


def shifted_weight(key, row_count, col_count):
    noise_key, shift_key = jax.random.split(key)
    noise = jnp.clip(jax.random.normal(noise_key, (row_count, col_count), jnp.float32), -6.0, 6.0)
    shift = jnp.clip(0.5 * jax.random.normal(shift_key, (1, col_count), jnp.float32), -1.5, 1.5)
    return (noise + shift) * (1.0 / math.sqrt(row_count))


def draw_w_gate(key, part):
    return shifted_weight(jax.random.fold_in(key, 4101), D, FF).astype(jnp.bfloat16)


def draw_w_up(key, part):
    return shifted_weight(jax.random.fold_in(key, 4202), D, FF).astype(jnp.bfloat16)


def raised(values, key, source, target, blocks, factor):
    owner, partner = [(jnp.arange(values.shape[axis_at]) // (values.shape[axis_at] // blocks)).reshape([-1 if axis == axis_at else 1 for axis in range(values.ndim)]) for axis_at in (source, target)]
    chosen = jax.random.permutation(key, blocks)[partner]
    strong = (owner == chosen) | (owner == (partner + blocks // 2) % blocks)
    return jnp.where(strong, factor * values, values)


def steps_of(own_key, extent, cuts, least, high):
    gain, own = 1.0, jax.random.fold_in(own_key, 6)
    for dim, blocks in cuts:
        draws = jnp.exp(jax.random.uniform(jax.random.fold_in(own, dim), (blocks,), jnp.float32, least / len(cuts), high / len(cuts)))
        gain = gain * jnp.repeat(draws, extent[dim] // blocks).reshape([-1 if axis == dim else 1 for axis in range(len(extent))])
    return gain


def split_up(number_of, total, reach, skew):
    portions = [(1 << 20) // math.isqrt(grade ** skew) + 1 for grade in range(2, number_of + 1)]
    rest, given = total - reach - (number_of - 1), [1] * (number_of - 1)
    while rest > 0:
        free = [i for i in range(number_of - 1) if given[i] < reach]
        mass, budget = sum([portions[i] for i in free]), rest
        for i in free:
            addition = min(reach - given[i], max(1, budget * portions[i] // mass), rest)
            given[i] = given[i] + addition
            rest = rest - addition
    return np.array([reach] + given)


def ragged_sizes(rng, count, total, limit, slope):
    if count == 2:
        one = jax.random.randint(rng, (), max(1, total - limit), min(limit, total - 1) + 1)
        return jnp.stack([one, total - one])
    sizes = jnp.asarray(split_up(count, total, limit, slope), jnp.int32)
    twos = (count - 1) // 2
    donor, sink = sizes[1:1 + 2 * twos:2], sizes[2:2 + 2 * twos:2]
    room = jnp.minimum(donor - 1, limit - sink)
    shifted = jax.random.randint(jax.random.fold_in(rng, 1), (twos,), 0, 1 << 20) % (room + 1)
    sizes = sizes.at[1:1 + 2 * twos:2].set(donor - shifted).at[2:2 + 2 * twos:2].set(sink + shifted)
    return sizes[jax.random.permutation(jax.random.fold_in(rng, 2), count)]


def centred(stream_key, shape, deviation, bound, cuts=(), held_as=jnp.bfloat16):
    drawn = deviation * jax.random.normal(stream_key, shape, jnp.float32)
    if cuts:
        drawn = drawn * steps_of(stream_key, shape, cuts, -0.22, 0.18)
    return jnp.clip(drawn, -bound, bound).astype(held_as)


def gaussian_with(stream_key, dims, deviation, most, cuts, heavy, kind=jnp.bfloat16):
    values = deviation * jax.random.normal(stream_key, dims, jnp.float32)
    if cuts:
        values = values * steps_of(stream_key, dims, cuts, -0.22, 0.18)
    return jnp.clip(raised(values, jax.random.fold_in(stream_key, 3), *heavy), -most, most).astype(kind)


def setup_inputs(seed: int = 0) -> dict:
    streams_of = jax.random.split(jax.random.key(seed), 23)
    return {
        "frames": gaussian_with(streams_of[0], (TOKENS, D), 1.0, 8.0, ((0, 8), (1, 4)), (0, 1, 8, 2.0)),
        "segment": jnp.searchsorted(jnp.cumsum(ragged_sizes(streams_of[1], 2 * N_SEQ, TOKENS, TOK_DEV, 2)), jnp.arange(TOKENS), side="right").astype(jnp.int32),
        "time_token": centred(streams_of[2], (ROWS, D), 1.0, 6.0),
        "context": centred(streams_of[3], (ROWS, CTX, CD), 1.0, 6.0),
        "gain_attn": jnp.clip(1.0 + 0.1 * jax.random.normal(streams_of[4], (D,), jnp.float32), 0.5, 1.5),
        "bias_attn": centred(streams_of[5], (D,), 0.3, 1.75, ((0, 4),), jnp.float32),
        "gain_cross": jnp.clip(1.0 + 0.1 * jax.random.normal(streams_of[6], (D,), jnp.float32), 0.5, 1.5),
        "bias_cross": centred(streams_of[7], (D,), 0.3, 1.75, ((0, 4),), jnp.float32),
        "gain_ffn": jnp.clip(1.0 + 0.1 * jax.random.normal(streams_of[8], (D,), jnp.float32), 0.5, 1.5),
        "bias_ffn": centred(streams_of[9], (D,), 0.3, 1.75, ((0, 4),), jnp.float32),
        "w_query": centred(streams_of[10], (D, D), D ** -0.5, 0.15625, ((1, 4),)),
        "w_key": centred(streams_of[11], (D, D), D ** -0.5, 0.15625, ((1, 4),)),
        "w_value": centred(streams_of[12], (D, D), D ** -0.5, 0.15625, ((1, 4),)),
        "w_out": centred(streams_of[13], (D, D), (D // 64) ** -0.5, 1.25, ((0, 4),)),
        "c_query": centred(streams_of[14], (D, D), D ** -0.5, 0.15625, ((1, 4),)),
        "c_key": centred(streams_of[15], (CD, D), CD ** -0.5, 0.21875, ((1, 4),)),
        "c_value": centred(streams_of[16], (CD, D), CD ** -0.5, 0.21875, ((1, 4),)),
        "c_out": centred(streams_of[17], (D, D), (D // 64) ** -0.5, 1.25, ((0, 4),)),
        "w_gate": draw_w_gate(jax.random.fold_in(streams_of[22], 71), 0),
        "w_up": draw_w_up(jax.random.fold_in(streams_of[22], 71), 0),
        "w_down": centred(streams_of[20], (FF, D), FF ** -0.5, 0.078125, ((0, 4),)),
        "out_grad": gaussian_with(streams_of[21], (TOKENS, D), 1.0, 8.0, ((0, 8), (1, 4)), (0, 1, 8, 2.0)),
    }


@jax.custom_vjp
def low(v):
    return lax.optimization_barrier(v.astype(jnp.bfloat16)).astype(jnp.float32)

@jax.custom_vjp
def low_back(v):
    return v

def low_keep(v):
    return (low(v), None)

def low_pass(kept, grad):
    return (grad,)

def back_keep(v):
    return (v, None)

def back_low(kept, grad):
    return (low(grad),)
low.defvjp(low_keep, low_pass)
low_back.defvjp(back_keep, back_low)

def matmul(left, right):
    return jnp.dot(left, right, precision=lax.Precision.HIGHEST)

def layer_norm(value_rows, norm_gain, norm_bias):
    center = value_rows - lax.optimization_barrier(jnp.mean(value_rows, -1, keepdims=True))
    spread = lax.optimization_barrier(jnp.mean(center * center, -1, keepdims=True))
    return center * lax.rsqrt(spread + 1e-05) * norm_gain + norm_bias

def frame_clip_labels(segment, row_length):
    frame_index = jnp.arange(segment.shape[0], dtype=jnp.int32)
    border = (frame_index % row_length == 0) | (segment != jnp.roll(segment, 1))
    clip_starts = lax.cummax(jnp.where(border, frame_index, 0), axis=0)
    return (clip_starts, (frame_index - clip_starts + 1).astype(jnp.float32))

def rotary_tables(frame_positions, col_count):
    half_dim = HEAD_SIZE // 2
    frequency = jnp.exp(jnp.arange(half_dim, dtype=jnp.float32) * (-math.log(10000.0) / half_dim))
    angles = frame_positions[:, None] * frequency[None, :]
    number_of_heads = col_count // HEAD_SIZE
    row_total = frame_positions.shape[0]
    cosine = jnp.broadcast_to(jnp.cos(angles)[:, None, None, :], (row_total, number_of_heads, 2, half_dim)).reshape(row_total, col_count)
    sine_part = jnp.sin(angles)
    signed = jnp.broadcast_to(jnp.stack([-sine_part, sine_part], 1)[:, None, :, :], (row_total, number_of_heads, 2, half_dim)).reshape(row_total, col_count)
    return (cosine, signed)

def partner(value_rows):
    row_total, col_count = value_rows.shape
    halves = value_rows.reshape(row_total, col_count // HEAD_SIZE, 2, HEAD_SIZE // 2)
    return halves[:, :, ::-1, :].reshape(row_total, col_count)

def rotate(value_rows, tables):
    return value_rows * tables[0] + partner(value_rows) * tables[1]

def self_block(query_rows, query_labels, key_rows, value_rows, key_labels, time_key, time_value):
    score_scale = 1.0 / math.sqrt(HEAD_SIZE)
    main_scores = jnp.einsum('qhd,khd->hqk', query_rows, key_rows, precision=lax.Precision.HIGHEST) * score_scale
    time_scores = jnp.einsum('qhd,hd->hq', query_rows, time_key, precision=lax.Precision.HIGHEST) * score_scale
    scores = low_back(jnp.concatenate([main_scores, time_scores[:, :, None]], 2))
    allowed = jnp.concatenate([query_labels[:, None] == key_labels[None, :], jnp.ones((query_rows.shape[0], 1), dtype=bool)], 1)
    scores = jnp.where(allowed[None], scores, -1e+30)
    weights = low(jax.nn.softmax(scores, axis=-1))
    all_values = jnp.concatenate([value_rows, time_value[None]], 0)
    return jnp.einsum('hqk,khd->qhd', weights, all_values, precision=lax.Precision.HIGHEST)

def self_attention_row(inputs):
    query_rows, key_rows, value_rows, labels, time_key, time_value = inputs
    rows_per_block = min(512, ROW_FRAMES)
    count_of_blocks = ROW_FRAMES // rows_per_block
    number_of_heads = query_rows.shape[1]

    def one_block(pieces):
        return self_block(pieces[0], pieces[1], key_rows, value_rows, labels, time_key, time_value)
    layer_outputs = lax.map(jax.checkpoint(one_block), (query_rows.reshape(count_of_blocks, rows_per_block, number_of_heads, HEAD_SIZE), labels.reshape(count_of_blocks, rows_per_block)))
    return layer_outputs.reshape(ROW_FRAMES, number_of_heads, HEAD_SIZE)

def forward(frames, params, time_token, context, clip_starts, tables):
    gain_attn, bias_attn, gain_cross, bias_cross, gain_ffn, bias_ffn, w_query, w_key, w_value, w_out, c_query, c_key, c_value, c_out, w_gate, w_up, w_down = params
    number_of_heads = w_query.shape[1] // HEAD_SIZE
    number_of_frames = frames.shape[0]
    number_of_rows = number_of_frames // ROW_FRAMES
    normed = low(layer_norm(frames, gain_attn, bias_attn))
    time_normed = low(layer_norm(time_token, gain_attn, bias_attn))
    query_rows = low(rotate(low_back(matmul(normed, w_query)), tables))
    key_rows = low(rotate(low_back(matmul(normed, w_key)), tables))
    value_rows = low(low_back(matmul(normed, w_value)))
    timestep_keys = low(matmul(time_normed, w_key))
    timestep_values = low(matmul(time_normed, w_value))
    packed_row_shape = (number_of_rows, ROW_FRAMES, number_of_heads, HEAD_SIZE)
    attended_output = lax.map(self_attention_row, (query_rows.reshape(packed_row_shape), key_rows.reshape(packed_row_shape), value_rows.reshape(packed_row_shape), clip_starts.reshape(number_of_rows, ROW_FRAMES), timestep_keys.reshape(number_of_rows, number_of_heads, HEAD_SIZE), timestep_values.reshape(number_of_rows, number_of_heads, HEAD_SIZE)))
    attended_output = low(low_back(attended_output.reshape(number_of_frames, -1)))
    after_self = frames + low_back(matmul(attended_output, w_out))
    normed_two = low(layer_norm(after_self, gain_cross, bias_cross))
    cross_queries = low(low_back(matmul(normed_two, c_query))).reshape(packed_row_shape)
    flat_context = context.reshape(number_of_rows * CTX, -1)
    cross_keys = low(matmul(flat_context, c_key)).reshape(number_of_rows, CTX, number_of_heads, HEAD_SIZE)
    cross_values = low(matmul(flat_context, c_value)).reshape(number_of_rows, CTX, number_of_heads, HEAD_SIZE)
    cross_scores = low_back(jnp.einsum('rqhd,rkhd->rhqk', cross_queries, cross_keys, precision=lax.Precision.HIGHEST) / math.sqrt(HEAD_SIZE))
    cross_weights = low(jax.nn.softmax(cross_scores, axis=-1))
    crossed = jnp.einsum('rhqk,rkhd->rqhd', cross_weights, cross_values, precision=lax.Precision.HIGHEST)
    crossed = low(low_back(crossed.reshape(number_of_frames, -1)))
    after_cross = after_self + low_back(matmul(crossed, c_out))
    normed_three = low(layer_norm(after_cross, gain_ffn, bias_ffn))
    gate_pre = low_back(matmul(normed_three, w_gate))
    lifted = low_back(matmul(normed_three, w_up))
    hidden = low(low_back(jax.nn.silu(gate_pre) * lifted))
    return after_cross + low_back(matmul(hidden, w_down))

def reference(frames, segment, time_token, context, gain_attn, bias_attn, gain_cross, bias_cross, gain_ffn, bias_ffn, w_query, w_key, w_value, w_out, c_query, c_key, c_value, c_out, w_gate, w_up, w_down, out_grad):
    clip_starts, frame_positions = frame_clip_labels(segment, ROW_FRAMES)
    tables = rotary_tables(frame_positions, D)
    params = tuple((weight.astype(jnp.float32) for weight in (gain_attn, bias_attn, gain_cross, bias_cross, gain_ffn, bias_ffn, w_query, w_key, w_value, w_out, c_query, c_key, c_value, c_out, w_gate, w_up, w_down)))
    time_wide = time_token.astype(jnp.float32)
    context_wide = context.astype(jnp.float32)

    def run(frames_in, params_in):
        return forward(frames_in, params_in, time_wide, context_wide, clip_starts, tables)
    result, pullback = jax.vjp(run, frames.astype(jnp.float32), params)
    frame_grad, param_grads = pullback(out_grad.astype(jnp.float32))
    return (result.astype(jnp.bfloat16), frame_grad, param_grads[0], param_grads[1], param_grads[2], param_grads[3], param_grads[4], param_grads[5], param_grads[6], param_grads[7], param_grads[8], param_grads[9], param_grads[10], param_grads[11], param_grads[12], param_grads[13], param_grads[14], param_grads[15], param_grads[16])
```

```python
import math

import jax
import jax.numpy as jnp
from jax import lax
from jax.experimental import pallas as pl
from jax.experimental.pallas import tpu as pltpu
from jax.sharding import PartitionSpec as P

HEAD_SIZE = 64
ROW_MIN = 2048
TILE = 256
GROUP = 3
BF16 = jnp.bfloat16
F32 = jnp.float32


def after(value, token):
    return lax.optimization_barrier((value, token))[0]


def swap(value, axis, by):
    return lax.ppermute(value, axis, [(i, i ^ by) for i in range(lax.axis_size(axis))])


def shift(value, axis, by):
    peers = lax.axis_size(axis)
    pairs = [(i, i + by) for i in range(peers) if 0 <= i + by < peers]
    return lax.ppermute(value, axis, pairs)


def tensor_place():
    place = lax.axis_index("tensor")
    return place // 2, place % 2


def ordered(own, far, mate, far_mate, axis):
    side, core = tensor_place()
    near = (jnp.where(core == 0, own, mate), jnp.where(core == 0, mate, own))
    away = (jnp.where(core == 0, far, far_mate), jnp.where(core == 0, far_mate, far))
    low = [jnp.where(side == 0, n, a) for n, a in zip(near, away)]
    high = [jnp.where(side == 0, a, n) for n, a in zip(near, away)]
    return jnp.concatenate(low + high, axis)


def gather(own, axis):
    far = swap(own, "tensor", 2)
    mate = swap(own, "tensor", 1)
    return ordered(own, far, mate, swap(far, "tensor", 1), axis)


def scatter_sum(make):
    side, core = tensor_place()
    away = jnp.stack([make(1 - core), make(3 - core)]).astype(BF16)
    got = swap(away, "tensor", 1)
    near = jnp.stack([make(core), make(2 + core)]) + got.astype(F32)
    own = jnp.where(side == 0, near[0], near[1])
    far = jnp.where(side == 0, near[1], near[0]).astype(BF16)
    return own + swap(far, "tensor", 2).astype(F32), far


def rows_to_cols(rows):
    side, core = tensor_place()
    size, width = rows.shape[0], rows.shape[1] // 4
    halves = [rows[:, : 2 * width], rows[:, 2 * width :]]
    keep = jnp.where(side == 0, halves[0], halves[1])
    far = swap(jnp.where(side == 0, halves[1], halves[0]), "tensor", 2)
    pair = jnp.concatenate([jnp.where(side == 0, keep, far), jnp.where(side == 0, far, keep)], 0)
    first, second = pair[:, :width], pair[:, width:]
    own = jnp.where(core == 0, first, second)
    mate = swap(jnp.where(core == 0, second, first), "tensor", 1)
    even = jnp.where(core == 0, own, mate)
    odd = jnp.where(core == 0, mate, own)
    return jnp.concatenate([even[:size], odd[:size], even[size:], odd[size:]], 0)


def paired():
    return lax.axis_size("seq") == 8


def seq_place():
    place = lax.axis_index("seq")
    return place // 2, place % 2


def blocks_for(rows, column):
    count, cols = rows.shape
    return lax.dynamic_index_in_dim(rows.reshape(4, 2, count // 8, cols), column, 1, False)


def trade(value, start, done):
    return after(swap(after(value, start), "seq", 1), done)


def pair_up(rows, start, done):
    _, column = seq_place()
    count, size = rows.shape
    own = blocks_for(rows, column).reshape(count // 2, size)
    away = blocks_for(rows, 1 - column).reshape(count // 2, size)
    return own, trade(away, start, done)


def line_sum(own, tokens):
    level, _ = seq_place()

    def piece(index):
        return lax.dynamic_index_in_dim(own, jnp.clip(index, 0, 3), 0, False)

    up = down = None
    for step in range(3):
        rise = piece(3 - step + level)
        fall = piece(step - 3 + level)
        if step:
            up, down, _ = lax.optimization_barrier((up, down, tokens[step]))
            rise = (rise.astype(F32) + up.astype(F32)).astype(BF16)
            fall = (fall.astype(F32) + down.astype(F32)).astype(BF16)
        climbs = [(2 * z + x, 2 * z + 2 + x) for z in range(step + 1) for x in (0, 1)]
        drops = [(6 - 2 * z + x, 4 - 2 * z + x) for z in range(step + 1) for x in (0, 1)]
        rise, fall, _ = lax.optimization_barrier((rise, fall, tokens[step]))
        up = lax.ppermute(rise, "seq", climbs)
        down = lax.ppermute(fall, "seq", drops)
    up, down, _ = lax.optimization_barrier((up, down, tokens[3]))
    return piece(level).astype(F32) + up.astype(F32) + down.astype(F32)


def line_trade(own, start, done):
    level, _ = seq_place()

    def piece(index):
        return lax.dynamic_index_in_dim(own, jnp.clip(index, 0, 3), 0, False)

    total = piece(level).astype(F32)
    sent = [piece(level + by) for by in (-3, -2, -1, 1, 2, 3)]
    sent = lax.optimization_barrier((*sent, start))[:6]
    got = []
    for by, value in zip((-3, -2, -1, 1, 2, 3), sent):
        pairs = [(i, i + 2 * by) for i in range(8) if 0 <= i + 2 * by < 8]
        got.append(lax.ppermute(value, "seq", pairs))
    got = lax.optimization_barrier((*got, done))[:6]
    for value in got:
        total = total + value.astype(F32)
    return total


def fold_pair(rows, start, done):
    _, column = seq_place()
    got = trade(blocks_for(rows, 1 - column), start, done)
    return (blocks_for(rows, column).astype(F32) + got.astype(F32)).astype(BF16)


def plain_sum(grad):
    return lax.psum_scatter(
        grad.astype(BF16), "seq", scatter_dimension=0, tiled=True
    ).astype(F32)


def reduce_small(vectors):
    count = lax.axis_size("seq")
    if count != 8:
        return lax.psum_scatter(vectors, "seq", scatter_dimension=1, tiled=True)
    place = lax.axis_index("seq")
    kinds, width = vectors.shape
    parts = vectors.reshape(kinds, 8, width // 8).transpose(1, 0, 2)
    for by in (4, 2, 1):
        bit = (place // by) % 2
        pair = parts.reshape(2, by, kinds, width // 8)
        send = lax.dynamic_index_in_dim(pair, 1 - bit, 0, False)
        keep = lax.dynamic_index_in_dim(pair, bit, 0, False)
        parts = keep + swap(send, "seq", by)
    return parts[0]


def frame_clip_labels(segment, row_length):
    frame_index = jnp.arange(segment.shape[0], dtype=jnp.int32)
    border = (frame_index % row_length == 0) | (segment != jnp.roll(segment, 1))
    clip_starts = lax.cummax(jnp.where(border, frame_index, 0), axis=0)
    return (clip_starts, (frame_index - clip_starts + 1).astype(jnp.float32))


def tile_ranges(q_labels, key_labels):
    q = q_labels.reshape(-1, TILE)
    k = key_labels.reshape(-1, TILE)
    meets = (k[None, :, 0] <= q[:, None, -1]) & (k[None, :, -1] >= q[:, None, 0])
    index = jnp.arange(k.shape[0], dtype=jnp.int32)[None]
    low = jnp.min(jnp.where(meets, index, k.shape[0]), 1)
    high = jnp.max(jnp.where(meets, index + 1, 0), 1)
    return jnp.stack([low, high], 1).reshape(-1)

def head_rows(g):
    return slice(g * HEAD_SIZE, (g + 1) * HEAD_SIZE)

def fill_natural(dest, refs):
    size = refs[0].shape[1]
    for part, ref in enumerate(refs):
        dest[part * size : (part + 1) * size, :] = ref[...].T

def sums_over(left, right):
    return lax.dot_general(left, right, (((1,), (0,)), ((), ())), preferred_element_type=F32)

def across(left, right):
    return lax.dot_general(left, right, (((1,), (1,)), ((), ())), preferred_element_type=F32)

def forward_body(span, q, k0, k1, k2, v0, v1, v2, tk, tv, qlab, klab, out, lse, keys, vals):
    rows, size = q.shape
    group = rows // HEAD_SIZE
    fill_natural(keys, (k0, k1, k2))
    for part, ref in enumerate((v0, v1, v2)):
        for piece in range(size // TILE):
            vals[part * (size // TILE) + piece] = ref[:, piece * TILE : (piece + 1) * TILE]
    for tile in range(size // TILE):
        cols = slice(tile * TILE, (tile + 1) * TILE)
        lab = qlab[:, cols]
        state = []
        for g in range(group):
            part = q[head_rows(g), cols].astype(F32)
            top = jnp.sum(part * tk[head_rows(g), :], 0, keepdims=True)
            state += [
                top,
                jnp.ones_like(top),
                jnp.broadcast_to(tv[head_rows(g), :], (HEAD_SIZE, TILE)),
            ]

        def step(j, state):
            start = pl.multiple_of(j * TILE, TILE)
            seen = klab[pl.ds(start, TILE), :] == lab
            fresh = []
            for g in range(group):
                top, total, acc = state[3 * g : 3 * g + 3]
                s = sums_over(keys[pl.ds(start, TILE), head_rows(g)], q[head_rows(g), cols])
                s = jnp.where(seen, s, -1e30)
                new = jnp.maximum(top, jnp.max(s, 0, keepdims=True))
                fade = jnp.exp(top - new)
                p = jnp.exp(s - new)
                total = total * fade + jnp.sum(p, 0, keepdims=True)
                acc = acc * fade + sums_over(vals[j, head_rows(g), :], p.astype(BF16))
                fresh += [new, total, acc]
            return tuple(fresh)

        state = lax.fori_loop(span[2 * tile], span[2 * tile + 1], step, tuple(state))
        for g in range(group):
            top, total, acc = state[3 * g : 3 * g + 3]
            out[head_rows(g), cols] = (acc / total).astype(BF16)
            lse[0, g : g + 1, cols] = top + jnp.log(total)

def backward_body(span, q, k0, k1, k2, v0, v1, v2, tk, tv, qlab, klab, out, lse, og,
                  dq, dk0, dk1, dk2, dv0, dv1, dv2, dtk, dtv, keys, vals, tkeys, ak, av):
    rows, size = q.shape
    group = rows // HEAD_SIZE
    pieces = size // TILE
    fill_natural(keys, (k0, k1, k2))
    fill_natural(vals, (v0, v1, v2))
    for part, ref in enumerate((k0, k1, k2)):
        for piece in range(pieces):
            tkeys[part * pieces + piece] = ref[:, piece * TILE : (piece + 1) * TILE]
    ak[...] = jnp.zeros_like(ak)
    av[...] = jnp.zeros_like(av)
    for tile in range(pieces):
        cols = slice(tile * TILE, (tile + 1) * TILE)
        lab = qlab[:, cols]
        state, norms, deltas = [], [], []
        for g in range(group):
            hr = head_rows(g)
            qf = q[hr, cols].astype(F32)
            gf = og[hr, cols].astype(F32)
            norm = lse[0, g : g + 1, cols]
            delta = jnp.sum(gf * out[hr, cols].astype(F32), 0, keepdims=True)
            pt = jnp.exp(jnp.sum(qf * tk[hr, :], 0, keepdims=True) - norm)
            st = pt * (jnp.sum(gf * tv[hr, :], 0, keepdims=True) - delta)
            gk = jnp.sum(qf * st, 1, keepdims=True)
            gv = jnp.sum(gf * pt, 1, keepdims=True)
            if tile == 0:
                dtk[hr, :] = gk
                dtv[hr, :] = gv
            else:
                dtk[hr, :] += gk
                dtv[hr, :] += gv
            state.append(tk[hr, :] * st)
            norms.append(norm)
            deltas.append(delta)

        def step(j, state):
            start = pl.multiple_of(j * TILE, TILE)
            seen = klab[pl.ds(start, TILE), :] == lab
            fresh = []
            for g in range(group):
                hr = head_rows(g)
                s = sums_over(keys[pl.ds(start, TILE), hr], q[hr, cols])
                p = jnp.exp(jnp.where(seen, s, -1e30) - norms[g])
                m = sums_over(vals[pl.ds(start, TILE), hr], og[hr, cols])
                ds = (p * (m - deltas[g])).astype(BF16)
                av[j, hr, :] += across(og[hr, cols], p.astype(BF16))
                ak[j, hr, :] += across(q[hr, cols], ds)
                fresh.append(state[g] + sums_over(tkeys[j, hr, :], ds))
            return tuple(fresh)

        state = lax.fori_loop(span[2 * tile], span[2 * tile + 1], step, tuple(state))
        for g in range(group):
            dq[head_rows(g), cols] = state[g]
    for part, (dk, dv) in enumerate(((dk0, dv0), (dk1, dv1), (dk2, dv2))):
        for piece in range(pieces):
            at = slice(piece * TILE, (piece + 1) * TILE)
            dk[:, at] = ak[part * pieces + piece].astype(dk.dtype)
            dv[:, at] = av[part * pieces + piece].astype(dv.dtype)

def attend(span, q, ks, vs, tk, tv, qlab, klab):
    cols, size = q.shape
    gr = GROUP * HEAD_SIZE
    steps = cols // gr
    block = pl.BlockSpec((gr, size), lambda i, s: (i, 0))
    column = pl.BlockSpec((gr, 1), lambda i, s: (i, 0))
    return pl.pallas_call(
        forward_body,
        grid_spec=pltpu.PrefetchScalarGridSpec(
            num_scalar_prefetch=1,
            grid=(steps,),
            in_specs=[block] * 7 + [column] * 2
            + [pl.BlockSpec((1, size), lambda i, s: (0, 0)), pl.BlockSpec((3 * size, 1), lambda i, s: (0, 0))],
            out_specs=[block, pl.BlockSpec((1, GROUP, size), lambda i, s: (i, 0, 0))],
            scratch_shapes=[pltpu.VMEM((3 * size, gr), BF16), pltpu.VMEM((3 * size // TILE, gr, TILE), BF16)],
        ),
        out_shape=[jax.ShapeDtypeStruct((cols, size), BF16), jax.ShapeDtypeStruct((steps, GROUP, size), F32)],
        name="attend",
    )(span, q, *ks, *vs, tk, tv, qlab, klab)

def attend_back(span, q, ks, vs, tk, tv, qlab, klab, out, lse, og):
    cols, size = q.shape
    gr = GROUP * HEAD_SIZE
    steps = cols // gr
    tiles = 3 * size // TILE
    block = pl.BlockSpec((gr, size), lambda i, s: (i, 0))
    column = pl.BlockSpec((gr, 1), lambda i, s: (i, 0))
    small = jax.ShapeDtypeStruct((cols, 1), F32)
    wide = jax.ShapeDtypeStruct((cols, size), F32)
    low = jax.ShapeDtypeStruct((cols, size), BF16)
    return pl.pallas_call(
        backward_body,
        grid_spec=pltpu.PrefetchScalarGridSpec(
            num_scalar_prefetch=1,
            grid=(steps,),
            in_specs=[block] * 7 + [column] * 2
            + [pl.BlockSpec((1, size), lambda i, s: (0, 0)), pl.BlockSpec((3 * size, 1), lambda i, s: (0, 0)),
               block, pl.BlockSpec((1, GROUP, size), lambda i, s: (i, 0, 0)), block],
            out_specs=[block] * 7 + [column] * 2,
            scratch_shapes=[pltpu.VMEM((3 * size, gr), BF16), pltpu.VMEM((3 * size, gr), BF16),
                            pltpu.VMEM((tiles, gr, TILE), BF16),
                            pltpu.VMEM((tiles, gr, TILE), F32), pltpu.VMEM((tiles, gr, TILE), F32)],
        ),
        out_shape=[wide, low, wide, low, low, wide, low, small, small],
        name="attend_back",
    )(span, q, *ks, *vs, tk, tv, qlab, klab, out, lse, og)


def rotary_tables(frame_positions):
    half_dim = HEAD_SIZE // 2
    frequency = jnp.exp(jnp.arange(half_dim, dtype=jnp.float32) * (-math.log(10000.0) / half_dim))
    angles = frequency[:, None] * frame_positions[None, :]
    return (jnp.cos(angles), jnp.sin(angles))


def rotate(rows, tables, sign=1.0):
    count, size = rows.shape
    halves = rows.reshape(count // HEAD_SIZE, 2, HEAD_SIZE // 2, size)
    cosine, sine = tables[0][None], tables[1][None] * sign
    first = halves[:, 0] * cosine - halves[:, 1] * sine
    second = halves[:, 1] * cosine + halves[:, 0] * sine
    return jnp.stack([first, second], 1).reshape(count, size)


def product(left, right):
    return jnp.dot(left, right, preferred_element_type=jnp.float32)


def inner_rows(left, right):
    return jnp.einsum("nd,nf->df", left, right, preferred_element_type=jnp.float32)


def back_project(gradient, weight):
    return jnp.einsum("nf,df->nd", gradient, weight, preferred_element_type=jnp.float32)


def by_feature(left, right):
    return jnp.einsum("nd,df->fn", left, right, preferred_element_type=jnp.float32)


def columns(weight, start, size):
    return lax.dynamic_slice_in_dim(weight, start, size, 1)


def rows_of(weight, start, size):
    return lax.dynamic_slice_in_dim(weight, start, size, 0)


def normalize(value_rows):
    means = jnp.mean(value_rows, -1, keepdims=True)
    centred = value_rows - means
    inverse = lax.rsqrt(jnp.mean(centred * centred, -1, keepdims=True) + 1e-05)
    return centred * inverse, inverse


def norm_backward(gradient, scaled, inverse, norm_gain):
    scaled_grad = gradient * norm_gain
    plain = jnp.mean(scaled_grad, -1, keepdims=True)
    cross = jnp.mean(scaled_grad * scaled, -1, keepdims=True)
    return inverse * (scaled_grad - plain - scaled * cross)


def per_device(
    frames,
    segment,
    time_token,
    context,
    gain_attn,
    bias_attn,
    gain_cross,
    bias_cross,
    gain_ffn,
    bias_ffn,
    w_query,
    w_key,
    w_value,
    w_out,
    c_query,
    c_key,
    c_value,
    c_out,
    w_gate,
    w_up,
    w_down,
    out_grad,
):
    local_rows = frames.shape[0]
    local_width = frames.shape[1]
    model_width = w_query.shape[0]
    head_cols = w_query.shape[1]
    heads = head_cols // HEAD_SIZE
    number_of_frames = lax.axis_size("seq") * local_rows
    row_length = min(max(ROW_MIN, 64 * lax.axis_size("seq")), number_of_frames)
    first_frame = lax.axis_index("seq") * local_rows
    own_start = lax.axis_index("tensor") * local_width

    def own_cols(value):
        return lax.dynamic_slice_in_dim(value, own_start, local_width, value.ndim - 1)

    place = lax.axis_index("tensor")
    share = local_rows // 4

    def own_rows(value):
        return rows_of(value, place * share, share)

    def row_block(value, index):
        return rows_of(value, index * share, share)

    frames_full = gather(frames, 1)
    norms = gather(
        jnp.stack([gain_attn, bias_attn, gain_cross, bias_cross, gain_ffn, bias_ffn]), 1
    )
    gain_one, bias_one, gain_two, bias_two, gain_three, bias_three = [
        norms[i : i + 1] for i in range(6)
    ]
    clip_starts, frame_positions = frame_clip_labels(segment, row_length)
    own_labels = lax.dynamic_slice_in_dim(clip_starts, first_frame, local_rows)
    own_positions = lax.dynamic_slice_in_dim(frame_positions, first_frame, local_rows)
    blanks = jnp.full((local_rows,), -1, jnp.int32)
    key_labels = lax.dynamic_slice_in_dim(
        jnp.concatenate([blanks, clip_starts, blanks]), first_frame, 3 * local_rows
    )
    spans = tile_ranges(own_labels, key_labels)
    label_row, label_column = own_labels[None, :], key_labels[:, None]
    row_index = first_frame // row_length
    time_row = lax.dynamic_slice_in_dim(time_token, row_index, 1, 0).astype(F32)
    row_context = lax.dynamic_slice_in_dim(context, row_index, 1, 0)[0]
    context_rows = row_context.shape[0]
    tables = rotary_tables(own_positions)
    score_scale = 1.0 / math.sqrt(HEAD_SIZE)
    all_heads = model_width // HEAD_SIZE

    scaled_one, inverse_one = normalize(frames_full.astype(F32))
    frame_normed = (scaled_one * gain_one + bias_one).astype(BF16)
    own_keys = rotate(by_feature(frame_normed, w_key), tables).astype(BF16)
    own_values = by_feature(frame_normed, w_value).astype(BF16)
    both = jnp.stack([own_keys, own_values])
    behind, ahead = shift(both, "seq", 1), shift(both, "seq", -1)
    frame_late, time_late = after((frame_normed, time_row), both)
    queries = (rotate(by_feature(frame_late, w_query), tables) * score_scale).astype(BF16)
    scaled_time, _ = normalize(time_late)
    time_normed = (scaled_time * gain_one + bias_one).astype(BF16)
    time_keys = by_feature(time_normed, w_key).astype(BF16).astype(F32)
    time_values = by_feature(time_normed, w_value).astype(BF16).astype(F32)
    context_late = after(row_context, both)
    cross_rows = gather(
        jnp.concatenate([product(context_late, c_key), product(context_late, c_value)], 0).astype(
            BF16
        ),
        1,
    )
    query_full = gather(after(c_query, both), 1)
    out_full = gather(after(c_out, query_full), 0)
    behind, ahead, _ = lax.optimization_barrier((behind, ahead, (queries, query_full, cross_rows)))
    keys = (behind[0], own_keys, ahead[0])
    values = (behind[1], own_values, ahead[1])
    attended, log_totals = attend(
        spans, queries, keys, values, time_keys, time_values, label_row, label_column
    )
    branch, one_near = scatter_sum(
        lambda b: jnp.einsum(
            "fn,fd->nd",
            lax.dynamic_slice_in_dim(attended, b * share, share, 1),
            w_out,
            preferred_element_type=F32,
        )
    )
    residual_one = own_rows(frames_full).astype(F32) + branch
    scaled_two, inverse_two = normalize(residual_one)
    normed_two = (scaled_two * gain_two + bias_two).astype(BF16)
    cross_queries = product(normed_two, query_full).astype(BF16).reshape(share, all_heads, HEAD_SIZE)
    cross_keys = cross_rows[:context_rows].reshape(context_rows, all_heads, HEAD_SIZE)
    cross_values = cross_rows[context_rows:].reshape(context_rows, all_heads, HEAD_SIZE)
    cross_scores = (
        jnp.einsum("qhd,khd->hqk", cross_queries, cross_keys, preferred_element_type=F32)
        * score_scale
    )
    cross_probs = jax.nn.softmax(cross_scores, axis=-1)
    cross_weights = cross_probs.astype(BF16)
    crossed = jnp.einsum("hqk,khd->qhd", cross_weights, cross_values, preferred_element_type=F32)
    crossed = crossed.reshape(share, model_width).astype(BF16)
    residual_two = residual_one + product(crossed, out_full)
    scaled_three, inverse_three = normalize(residual_two)
    normed_share = (scaled_three * gain_three + bias_three).astype(BF16)
    normed_three = gather(normed_share, 0)
    grad_low = gather(after(out_grad, one_near), 1)
    gate_pre = product(normed_three, w_gate)
    lifted = product(normed_three, w_up)
    sigmoid_gate = jax.nn.sigmoid(gate_pre)
    hidden = (gate_pre * sigmoid_gate * lifted).astype(BF16)

    hidden_grad = back_project(after(grad_low, normed_share), w_down).astype(BF16).astype(F32)
    gate_grad = (
        hidden_grad * lifted * sigmoid_gate * (1.0 + gate_pre * (1.0 - sigmoid_gate))
    ).astype(BF16)
    lifted_grad = (hidden_grad * gate_pre * sigmoid_gate).astype(BF16)
    normed_grad, three_near = scatter_sum(
        lambda b: back_project(row_block(gate_grad, b), w_gate)
        + back_project(row_block(lifted_grad, b), w_up)
    )
    grad_two = own_rows(grad_low).astype(F32) + norm_backward(
        normed_grad, scaled_three, inverse_three, gain_three
    )

    cross_full = grad_two.astype(BF16)
    crossed_grad = (
        back_project(cross_full, out_full).astype(BF16).reshape(share, all_heads, HEAD_SIZE)
    )
    prob_grad = jnp.einsum("qhd,khd->hqk", crossed_grad, cross_values, preferred_element_type=F32)
    row_delta = jnp.sum(prob_grad * cross_probs, -1, keepdims=True)
    score_grad = (cross_probs * (prob_grad - row_delta)).astype(BF16)
    cross_query_grad = (
        jnp.einsum("hqk,khd->qhd", score_grad, cross_keys, preferred_element_type=F32)
        * score_scale
    )
    cross_query_grad = cross_query_grad.astype(BF16).reshape(share, model_width)
    normed_back = back_project(cross_query_grad, query_full)
    grad_one = (grad_two + norm_backward(normed_back, scaled_two, inverse_two, gain_two)).astype(
        BF16
    )
    attend_full = gather(grad_one, 0)
    grad_heads = jnp.einsum(
        "nd,fd->fn", attend_full, w_out, preferred_element_type=F32
    ).astype(BF16)
    back = attend_back(
        spans, queries, keys, values, time_keys, time_values, label_row, label_column,
        attended, log_totals, grad_heads,
    )
    query_grad, key_prev, key_own, key_next, value_prev, value_own, value_next = back[:7]
    time_key_grad, time_value_grad = back[7], back[8]
    from_next = shift(jnp.stack([key_prev, value_prev]), "seq", -1)
    from_prev = shift(jnp.stack([key_next, value_next]), "seq", 1)
    query_raw = (rotate(query_grad, tables, -1.0) * score_scale).astype(BF16)
    key_raw = rotate(
        key_own + from_next[0].astype(F32) + from_prev[0].astype(F32), tables, -1.0
    ).astype(BF16)
    value_raw = (value_own + from_next[1].astype(F32) + from_prev[1].astype(F32)).astype(BF16)

    def to_frames(rows, weight):
        return jnp.einsum("fn,df->nd", rows, weight, preferred_element_type=F32)

    frame_grad, last_near = scatter_sum(
        lambda b: to_frames(query_raw, rows_of(w_query, b * local_width, local_width))
        + to_frames(key_raw, rows_of(w_key, b * local_width, local_width))
        + to_frames(value_raw, rows_of(w_value, b * local_width, local_width)),
    )
    time_grad = to_frames(time_key_grad.astype(BF16), w_key) + to_frames(
        time_value_grad.astype(BF16), w_value
    )
    late = after((normed_grad, scaled_three, normed_back, scaled_two), query_grad)
    norm_grads = [
        jnp.sum(late[0] * late[1], 0),
        jnp.sum(late[0], 0),
        jnp.sum(late[2] * late[3], 0),
        jnp.sum(late[2], 0),
    ]
    own_scaled = own_cols(scaled_one)
    scaled_grad = frame_grad * gain_attn[None]
    sums = jnp.concatenate(
        [jnp.sum(scaled_grad, -1), jnp.sum(scaled_grad * own_scaled, -1), time_grad[0]]
        + norm_grads
    )[None]
    sums = sums + swap(sums, "tensor", 1)
    sums = sums + swap(sums, "tensor", 2)
    plain = sums[0, :local_rows, None] / model_width
    cross = sums[0, local_rows : 2 * local_rows, None] / model_width
    vectors = own_cols(sums[0, 2 * local_rows :].reshape(5, model_width))
    d_frames = own_cols(attend_full).astype(F32) + inverse_one * (
        scaled_grad - plain - own_scaled * cross
    )
    d_gain_attn = jnp.sum(frame_grad * own_scaled, 0) + vectors[0] * own_cols(scaled_time)[0]
    d_bias_attn = jnp.sum(frame_grad, 0) + vectors[0]
    small = reduce_small(
        jnp.stack([d_gain_attn, d_bias_attn, vectors[3], vectors[4], vectors[1], vectors[2]])
    )

    hidden_late = after(hidden, normed_grad)
    down_sum, _ = scatter_sum(lambda b: product(row_block(hidden_late, b), w_down))
    block_out = rows_to_cols((residual_two + down_sum).astype(BF16))

    late = after((score_grad, cross_weights, crossed_grad, cross_queries), grad_heads)
    key_grad = jnp.einsum("hqk,qhd->khd", late[0], late[3], preferred_element_type=F32)
    value_grad = jnp.einsum("hqk,qhd->khd", late[1], late[2], preferred_element_type=F32)
    context_sums = jnp.concatenate(
        [
            key_grad.reshape(context_rows, model_width) * score_scale,
            value_grad.reshape(context_rows, model_width),
        ],
        0,
    )
    context_own, _ = scatter_sum(
        lambda b: lax.dynamic_slice_in_dim(context_sums, b * head_cols, head_cols, 1)
    )
    two_full = gather(after(normed_two, hidden), 0)
    crossed_own = rows_to_cols(after(crossed, hidden))
    cross_grad_full = gather(after(cross_full, attend_full), 0)
    cross_query_own = rows_to_cols(after(cross_query_grad, attend_full))
    time_column = time_normed.astype(F32).T

    def context_grads(kv):
        left = row_context.T
        both_grads = jnp.concatenate([kv[:context_rows], kv[context_rows:]], 1)
        return product(left, both_grads.astype(BF16))

    if paired():
        _, column = seq_place()

        def meet(rows, cols, spec):
            blocks = sum(
                jnp.einsum(spec, r, c, preferred_element_type=F32) for r, c in zip(rows, cols)
            )
            return blocks.astype(BF16).reshape(4, blocks.shape[0] // 4, blocks.shape[1])

        normed_pair = pair_up(frame_normed.T, behind, normed_three)
        grad_pair = (grad_low, trade(grad_low, one_near, gate_grad))
        three_pair = pair_up(normed_three.T, normed_three, three_near)
        hidden_pair = pair_up(hidden.T, hidden, normed_grad)
        gate_pair = (gate_grad, trade(gate_grad, three_near, grad_heads))
        lifted_pair = (lifted_grad, trade(lifted_grad, grad_two, query_grad))

        down_blocks = meet(hidden_pair, grad_pair, "dn,nf->df")
        grad_down = line_trade(down_blocks, grad_two, query_grad)
        gate_blocks = meet(three_pair, gate_pair, "dn,nf->df")
        grad_gate_w = line_sum(gate_blocks, (query_grad, query_grad, from_next, key_raw))
        up_blocks = meet(three_pair, lifted_pair, "dn,nf->df")
        grad_up_w = line_sum(up_blocks, (query_grad, from_next, key_raw, last_near))

        late = after((crossed_own, cross_grad_full), query_grad)
        grad_c_out = inner_rows(*late).astype(BF16)
        late = after((two_full, cross_query_own), query_grad)
        grad_c_query = inner_rows(*late).astype(BF16)
        grad_c_kv = context_grads(context_own).astype(BF16)
        late = after((attended, attend_full), query_grad)
        grad_w_out = product(*late).astype(BF16)
        part = head_cols // 8
        bundle = jnp.concatenate(
            [
                value.reshape(8, part, model_width)
                for value in (grad_c_out, grad_c_query, grad_c_kv, grad_w_out)
            ],
            1,
        ).reshape(8 * 4 * part, model_width)
        folded = fold_pair(bundle, from_next, last_near)
        middle = line_sum(folded, (last_near, frame_grad, frame_grad, frame_grad))
        grad_c_out = middle[:part]
        grad_c_query = middle[part : 2 * part].reshape(model_width // 8, head_cols)
        grad_c_kv = middle[2 * part : 3 * part].reshape(-1, 2 * head_cols)
        grad_w_out = middle[3 * part :]

        raw = jnp.concatenate([query_raw, key_raw, value_raw], 0)
        raw_pair = (raw, trade(raw, key_raw, last_near))
        time_both = jnp.concatenate([time_key_grad, time_value_grad], 0)
        time_both = time_both + trade(time_both, from_next, key_raw)
        own_time_rows = blocks_for(time_column, column).reshape(-1, 1)
        outer = own_time_rows * jnp.concatenate(
            [jnp.zeros((head_cols, 1), F32), time_both], 0
        ).T
        blocks = sum(
            jnp.einsum("dn,fn->df", r, c, preferred_element_type=F32)
            for r, c in zip(normed_pair, raw_pair)
        )
        blocks = (blocks + outer).astype(BF16).reshape(4, -1, 3 * head_cols)
        heads_sum = line_sum(blocks, (frame_grad, frame_grad, frame_grad, frame_grad))
        grad_w_query, grad_w_key, grad_w_value = (
            heads_sum[:, i * head_cols : (i + 1) * head_cols] for i in range(3)
        )
    else:
        grad_down = plain_sum(inner_rows(hidden, grad_low))
        grad_gate_w = plain_sum(inner_rows(normed_three, gate_grad))
        grad_up_w = plain_sum(inner_rows(normed_three, lifted_grad))
        grad_c_out = plain_sum(inner_rows(crossed_own, cross_grad_full))
        grad_c_query = plain_sum(inner_rows(two_full, cross_query_own))
        grad_c_kv = plain_sum(context_grads(context_own))
        grad_w_out = plain_sum(product(attended, attend_full))

        def with_time(rows, time_part):
            grads = jnp.einsum("nd,fn->df", frame_normed, rows, preferred_element_type=F32)
            return grads + time_column * time_part.T

        grad_w_query = plain_sum(
            jnp.einsum("nd,fn->df", frame_normed, query_raw, preferred_element_type=F32)
        )
        grad_w_key = plain_sum(with_time(key_raw, time_key_grad))
        grad_w_value = plain_sum(with_time(value_raw, time_value_grad))
    return (
        block_out,
        d_frames,
        small[0],
        small[1],
        small[2],
        small[3],
        small[4],
        small[5],
        grad_w_query,
        grad_w_key,
        grad_w_value,
        grad_w_out,
        grad_c_query,
        grad_c_kv[:, :head_cols],
        grad_c_kv[:, head_cols:],
        grad_c_out,
        grad_gate_w,
        grad_up_w,
        grad_down,
    )


def solution(mesh):
    return jax.shard_map(
        per_device,
        mesh=mesh,
        in_specs=(
            P("seq", "tensor"),
            P(),
            P(),
            P(),
            P("tensor"),
            P("tensor"),
            P("tensor"),
            P("tensor"),
            P("tensor"),
            P("tensor"),
            P(None, "tensor"),
            P(None, "tensor"),
            P(None, "tensor"),
            P("tensor", None),
            P(None, "tensor"),
            P(None, "tensor"),
            P(None, "tensor"),
            P("tensor", None),
            P(None, "tensor"),
            P(None, "tensor"),
            P("tensor", None),
            P("seq", "tensor"),
        ),
        out_specs=(
            P("seq", "tensor"),
            P("seq", "tensor"),
            P(("tensor", "seq")),
            P(("tensor", "seq")),
            P(("tensor", "seq")),
            P(("tensor", "seq")),
            P(("tensor", "seq")),
            P(("tensor", "seq")),
            P("seq", "tensor"),
            P("seq", "tensor"),
            P("seq", "tensor"),
            P(("tensor", "seq"), None),
            P("seq", "tensor"),
            P("seq", "tensor"),
            P("seq", "tensor"),
            P(("tensor", "seq"), None),
            P("seq", "tensor"),
            P("seq", "tensor"),
            P(("tensor", "seq"), None),
        ),
        check_vma=False,
    )
```

```python
import functools
import math

import jax
import jax.numpy as jnp
from jax import lax
from jax.experimental import pallas as pl
from jax.experimental.pallas import tpu as pltpu
from jax.sharding import PartitionSpec as P

HEAD_SIZE = 64
ROW_MIN = 2048
TILE = 256
GROUP = 3
BF16 = jnp.bfloat16
F32 = jnp.float32


def after(value, token):
    return lax.optimization_barrier((value, token))[0]


def swap(value, axis, by):
    return lax.ppermute(value, axis, [(i, i ^ by) for i in range(lax.axis_size(axis))])


def shift(value, axis, by):
    peers = lax.axis_size(axis)
    pairs = [(i, i + by) for i in range(peers) if 0 <= i + by < peers]
    return lax.ppermute(value, axis, pairs)


def tensor_place():
    place = lax.axis_index("tensor")
    return place // 2, place % 2


def ordered(own, far, mate, far_mate, axis):
    side, core = tensor_place()
    near = (jnp.where(core == 0, own, mate), jnp.where(core == 0, mate, own))
    away = (jnp.where(core == 0, far, far_mate), jnp.where(core == 0, far_mate, far))
    low = [jnp.where(side == 0, n, a) for n, a in zip(near, away)]
    high = [jnp.where(side == 0, a, n) for n, a in zip(near, away)]
    return jnp.concatenate(low + high, axis)


def gather_near(own):
    far = swap(own, "tensor", 2)
    return own, swap(own, "tensor", 1), far, swap(far, "tensor", 1)


def gather_staged(own, first, second):
    far = swap(after(own, first), "tensor", 2)
    far, late = after((far, own), second)
    return own, swap(late, "tensor", 1), far, swap(far, "tensor", 1)


def gather(own, axis):
    own, mate, far, far_mate = gather_near(own)
    return ordered(own, far, mate, far_mate, axis)


def scatter_near(away, near):
    got = swap(away.astype(BF16), "tensor", 1)
    size = away.shape[0] // 2
    low = (near[size:] + got[size:].astype(F32)).astype(BF16)
    return near[:size] + got[:size].astype(F32), swap(low, "tensor", 2), low


def rows_to_cols(own, mate, far, far_mate, later):
    width = own.shape[1]
    got = after(swap(jnp.concatenate([far, far_mate], 1), "tensor", 2), later)
    other = swap(jnp.concatenate([mate, got[:, width:]], 0), "tensor", 1)
    size = own.shape[0]
    return jnp.concatenate([own, other[:size], got[:, :width], other[size:]], 0)


def quarters(value, axis):
    return jnp.split(value, 4, axis)


def own_blocks(near):
    return jnp.concatenate([quarters(value, 1)[r] for r, value in enumerate(near)], 0)


def trade(value, start, done):
    return after(swap(after(value, start), "seq", 1), done)


def halve(blocks, bit, start, done):
    count, rows, cols = blocks.shape
    side = (lax.axis_index("seq") >> bit) % 2
    parts = blocks.reshape(count // 2, 2, rows, cols)
    send = lax.dynamic_index_in_dim(parts, 1 - side, 1, False)
    keep = lax.dynamic_index_in_dim(parts, side, 1, False)
    got = after(swap(after(send, start), "seq", 1 << bit), done)
    return keep.astype(F32) + got.astype(F32)


def halve_all(blocks, bit, *tokens):
    while blocks.shape[0] > 1:
        blocks = halve(blocks.astype(BF16), bit, tokens[0], tokens[1])
        tokens, bit = tokens[2:] or tokens, bit + 1
    return blocks[0]


def reduce_small(vectors):
    count = lax.axis_size("seq")
    kinds, width = vectors.shape
    parts = vectors.reshape(kinds, count, width // count).transpose(1, 0, 2)
    bit = 0
    while parts.shape[0] > 1:
        parts = halve(parts, bit, parts, parts)
        bit += 1
    return parts[0]


def frame_clip_labels(segment, row_length):
    frame_index = jnp.arange(segment.shape[0], dtype=jnp.int32)
    border = (frame_index % row_length == 0) | (segment != jnp.roll(segment, 1))
    clip_starts = lax.cummax(jnp.where(border, frame_index, 0), axis=0)
    return (clip_starts, (frame_index - clip_starts + 1).astype(jnp.float32))


def tile_ranges(q_labels, key_labels):
    q = q_labels.reshape(-1, TILE)
    k = key_labels.reshape(-1, TILE)
    meets = (k[None, :, 0] <= q[:, None, -1]) & (k[None, :, -1] >= q[:, None, 0])
    index = jnp.arange(k.shape[0], dtype=jnp.int32)[None]
    low = jnp.min(jnp.where(meets, index, k.shape[0]), 1)
    high = jnp.max(jnp.where(meets, index + 1, 0), 1)
    return jnp.stack([low, high], 1).reshape(-1)

def head_rows(g):
    return slice(g * HEAD_SIZE, (g + 1) * HEAD_SIZE)

def fill_natural(dest, refs):
    size = refs[0].shape[1]
    for part, ref in enumerate(refs):
        dest[part * size : (part + 1) * size, :] = ref[...].T

def sums_over(left, right):
    return lax.dot_general(left, right, (((1,), (0,)), ((), ())), preferred_element_type=F32)

def across(left, right):
    return lax.dot_general(left, right, (((1,), (1,)), ((), ())), preferred_element_type=F32)

def forward_body(span, q, k0, k1, k2, v0, v1, v2, tk, tv, qlab, klab, out, lse, keys, vals):
    rows, size = q.shape
    group = rows // HEAD_SIZE
    fill_natural(keys, (k0, k1, k2))
    for part, ref in enumerate((v0, v1, v2)):
        for piece in range(size // TILE):
            vals[part * (size // TILE) + piece] = ref[:, piece * TILE : (piece + 1) * TILE]
    for tile in range(size // TILE):
        cols = slice(tile * TILE, (tile + 1) * TILE)
        lab = qlab[:, cols]
        state = []
        for g in range(group):
            part = q[head_rows(g), cols].astype(F32)
            top = jnp.sum(part * tk[head_rows(g), :], 0, keepdims=True)
            state += [
                top,
                jnp.ones_like(top),
                jnp.broadcast_to(tv[head_rows(g), :], (HEAD_SIZE, TILE)),
            ]

        def step(j, state):
            start = pl.multiple_of(j * TILE, TILE)
            seen = klab[pl.ds(start, TILE), :] == lab
            fresh = []
            for g in range(group):
                top, total, acc = state[3 * g : 3 * g + 3]
                s = sums_over(keys[pl.ds(start, TILE), head_rows(g)], q[head_rows(g), cols])
                s = jnp.where(seen, s, -1e30)
                new = jnp.maximum(top, jnp.max(s, 0, keepdims=True))
                fade = jnp.exp(top - new)
                p = jnp.exp(s - new)
                total = total * fade + jnp.sum(p, 0, keepdims=True)
                acc = acc * fade + sums_over(vals[j, head_rows(g), :], p.astype(BF16))
                fresh += [new, total, acc]
            return tuple(fresh)

        state = lax.fori_loop(span[2 * tile], span[2 * tile + 1], step, tuple(state))
        for g in range(group):
            top, total, acc = state[3 * g : 3 * g + 3]
            out[head_rows(g), cols] = (acc / total).astype(BF16)
            lse[0, g : g + 1, cols] = top + jnp.log(total)

def backward_body(span, q, k0, k1, k2, v0, v1, v2, tk, tv, qlab, klab, out, lse, og,
                  dq, dk0, dk1, dk2, dv0, dv1, dv2, dtk, dtv, keys, vals, tkeys, ak, av):
    rows, size = q.shape
    group = rows // HEAD_SIZE
    pieces = size // TILE
    fill_natural(keys, (k0, k1, k2))
    fill_natural(vals, (v0, v1, v2))
    for part, ref in enumerate((k0, k1, k2)):
        for piece in range(pieces):
            tkeys[part * pieces + piece] = ref[:, piece * TILE : (piece + 1) * TILE]
    ak[...] = jnp.zeros_like(ak)
    av[...] = jnp.zeros_like(av)
    for tile in range(pieces):
        cols = slice(tile * TILE, (tile + 1) * TILE)
        lab = qlab[:, cols]
        state, norms, deltas = [], [], []
        for g in range(group):
            hr = head_rows(g)
            qf = q[hr, cols].astype(F32)
            gf = og[hr, cols].astype(F32)
            norm = lse[0, g : g + 1, cols]
            delta = jnp.sum(gf * out[hr, cols].astype(F32), 0, keepdims=True)
            pt = jnp.exp(jnp.sum(qf * tk[hr, :], 0, keepdims=True) - norm)
            st = pt * (jnp.sum(gf * tv[hr, :], 0, keepdims=True) - delta)
            gk = jnp.sum(qf * st, 1, keepdims=True)
            gv = jnp.sum(gf * pt, 1, keepdims=True)
            if tile == 0:
                dtk[hr, :] = gk
                dtv[hr, :] = gv
            else:
                dtk[hr, :] += gk
                dtv[hr, :] += gv
            state.append(tk[hr, :] * st)
            norms.append(norm)
            deltas.append(delta)

        def step(j, state):
            start = pl.multiple_of(j * TILE, TILE)
            seen = klab[pl.ds(start, TILE), :] == lab
            fresh = []
            for g in range(group):
                hr = head_rows(g)
                s = sums_over(keys[pl.ds(start, TILE), hr], q[hr, cols])
                p = jnp.exp(jnp.where(seen, s, -1e30) - norms[g])
                m = sums_over(vals[pl.ds(start, TILE), hr], og[hr, cols])
                ds = (p * (m - deltas[g])).astype(BF16)
                av[j, hr, :] += across(og[hr, cols], p.astype(BF16))
                ak[j, hr, :] += across(q[hr, cols], ds)
                fresh.append(state[g] + sums_over(tkeys[j, hr, :], ds))
            return tuple(fresh)

        state = lax.fori_loop(span[2 * tile], span[2 * tile + 1], step, tuple(state))
        for g in range(group):
            dq[head_rows(g), cols] = state[g]
    for part, (dk, dv) in enumerate(((dk0, dv0), (dk1, dv1), (dk2, dv2))):
        for piece in range(pieces):
            at = slice(piece * TILE, (piece + 1) * TILE)
            dk[:, at] = ak[part * pieces + piece].astype(dk.dtype)
            dv[:, at] = av[part * pieces + piece].astype(dv.dtype)

def attend(span, q, ks, vs, tk, tv, qlab, klab):
    cols, size = q.shape
    gr = GROUP * HEAD_SIZE
    steps = cols // gr
    block = pl.BlockSpec((gr, size), lambda i, s: (i, 0))
    column = pl.BlockSpec((gr, 1), lambda i, s: (i, 0))
    return pl.pallas_call(
        forward_body,
        grid_spec=pltpu.PrefetchScalarGridSpec(
            num_scalar_prefetch=1,
            grid=(steps,),
            in_specs=[block] * 7 + [column] * 2
            + [pl.BlockSpec((1, size), lambda i, s: (0, 0)), pl.BlockSpec((3 * size, 1), lambda i, s: (0, 0))],
            out_specs=[block, pl.BlockSpec((1, GROUP, size), lambda i, s: (i, 0, 0))],
            scratch_shapes=[pltpu.VMEM((3 * size, gr), BF16), pltpu.VMEM((3 * size // TILE, gr, TILE), BF16)],
        ),
        out_shape=[jax.ShapeDtypeStruct((cols, size), BF16), jax.ShapeDtypeStruct((steps, GROUP, size), F32)],
        name="attend", cost_estimate=FREE,
    )(span, q, *ks, *vs, tk, tv, qlab, klab)

def attend_back(span, q, ks, vs, tk, tv, qlab, klab, out, lse, og):
    cols, size = q.shape
    gr = GROUP * HEAD_SIZE
    steps = cols // gr
    tiles = 3 * size // TILE
    block = pl.BlockSpec((gr, size), lambda i, s: (i, 0))
    column = pl.BlockSpec((gr, 1), lambda i, s: (i, 0))
    small = jax.ShapeDtypeStruct((cols, 1), F32)
    wide = jax.ShapeDtypeStruct((cols, size), F32)
    low = jax.ShapeDtypeStruct((cols, size), BF16)
    return pl.pallas_call(
        backward_body,
        grid_spec=pltpu.PrefetchScalarGridSpec(
            num_scalar_prefetch=1,
            grid=(steps,),
            in_specs=[block] * 7 + [column] * 2
            + [pl.BlockSpec((1, size), lambda i, s: (0, 0)), pl.BlockSpec((3 * size, 1), lambda i, s: (0, 0)),
               block, pl.BlockSpec((1, GROUP, size), lambda i, s: (i, 0, 0)), block],
            out_specs=[block] * 7 + [column] * 2,
            scratch_shapes=[pltpu.VMEM((3 * size, gr), BF16), pltpu.VMEM((3 * size, gr), BF16),
                            pltpu.VMEM((tiles, gr, TILE), BF16),
                            pltpu.VMEM((tiles, gr, TILE), F32), pltpu.VMEM((tiles, gr, TILE), F32)],
        ),
        out_shape=[wide, low, wide, low, low, wide, low, small, small],
        name="attend_back", cost_estimate=FREE,
    )(span, q, *ks, *vs, tk, tv, qlab, klab, out, lse, og)


def rotary_tables(frame_positions):
    half_dim = HEAD_SIZE // 2
    frequency = jnp.exp(jnp.arange(half_dim, dtype=jnp.float32) * (-math.log(10000.0) / half_dim))
    angles = frequency[:, None] * frame_positions[None, :]
    return (jnp.cos(angles), jnp.sin(angles))


def rotate(rows, tables, sign=1.0):
    count, size = rows.shape
    halves = rows.reshape(count // HEAD_SIZE, 2, HEAD_SIZE // 2, size)
    cosine, sine = tables[0][None], tables[1][None] * sign
    first = halves[:, 0] * cosine - halves[:, 1] * sine
    second = halves[:, 1] * cosine + halves[:, 0] * sine
    return jnp.stack([first, second], 1).reshape(count, size)


def product(left, right):
    return jnp.dot(left, right, preferred_element_type=jnp.float32)


def inner_rows(left, right):
    return jnp.einsum("nd,nf->df", left, right, preferred_element_type=jnp.float32)


def back_project(gradient, weight):
    return jnp.einsum("nf,df->nd", gradient, weight, preferred_element_type=jnp.float32)


def by_feature(left, right):
    return jnp.einsum("nd,df->fn", left, right, preferred_element_type=jnp.float32)


def columns(weight, start, size):
    return lax.dynamic_slice_in_dim(weight, start, size, 1)


def rows_of(weight, start, size):
    return lax.dynamic_slice_in_dim(weight, start, size, 0)


def normalize(value_rows):
    means = jnp.mean(value_rows, -1, keepdims=True)
    centred = value_rows - means
    inverse = lax.rsqrt(jnp.mean(centred * centred, -1, keepdims=True) + 1e-05)
    return centred * inverse, inverse


def norm_backward(gradient, scaled, inverse, norm_gain):
    scaled_grad = gradient * norm_gain
    plain = jnp.mean(scaled_grad, -1, keepdims=True)
    cross = jnp.mean(scaled_grad * scaled, -1, keepdims=True)
    return inverse * (scaled_grad - plain - scaled * cross)


FREE = pl.CostEstimate(flops=1, transcendentals=0, bytes_accessed=1)


def dot_nn(left, right):
    return lax.dot_general(left, right, (((1,), (0,)), ((), ())), preferred_element_type=F32)


def dot_nt(left, right):
    return lax.dot_general(left, right, (((1,), (1,)), ((), ())), preferred_element_type=F32)


def dot_tn(left, right):
    return lax.dot_general(left, right, (((0,), (0,)), ((), ())), preferred_element_type=F32)


def head_weights(query, key, lanes, which):
    mine = jnp.where(lanes == which, query, jnp.zeros_like(query))
    scores = dot_nt(mine, key) * (1.0 / math.sqrt(HEAD_SIZE))
    weights = jnp.exp(scores - jnp.max(scores, -1, keepdims=True))
    return weights / jnp.sum(weights, -1, keepdims=True)


def cross_forward_body(rows, own, far, norms, q0, q1, q2, q3, kv, o0, o1, o2, o3,
                       normed_two, queries, crossed, first, second, normed_three):
    width = rows.shape[1]
    context_rows = kv.shape[0] // 2
    lanes = lax.broadcasted_iota(jnp.int32, (rows.shape[0], 2 * HEAD_SIZE), 1) // HEAD_SIZE
    residual = rows[...].astype(F32) + own[...] + far[...].astype(F32)
    first[...] = residual
    scaled, _ = normalize(residual)
    low = (scaled * norms[2:3, :] + norms[3:4, :]).astype(BF16)
    normed_two[...] = low
    part = width // 4
    for b, ref in enumerate((q0, q1, q2, q3)):
        queries[:, b * part : (b + 1) * part] = dot_nn(low, ref[...]).astype(BF16)
    for p in range(width // (2 * HEAD_SIZE)):
        cols = slice(p * 2 * HEAD_SIZE, (p + 1) * 2 * HEAD_SIZE)
        q, k, v = queries[:, cols], kv[:context_rows, cols], kv[context_rows:, cols]
        mixed = [dot_nn(head_weights(q, k, lanes, g).astype(BF16), v) for g in (0, 1)]
        crossed[:, cols] = jnp.where(lanes == 0, mixed[0], mixed[1]).astype(BF16)
    for b, ref in enumerate((o0, o1, o2, o3)):
        residual = residual + dot_nn(crossed[:, b * part : (b + 1) * part], ref[...])
    second[...] = residual
    scaled, _ = normalize(residual)
    normed_three[...] = (scaled * norms[4:5, :] + norms[5:6, :]).astype(BF16)


def cross_forward(rows, own, far, norms, query_parts, kv, out_parts):
    low = jax.ShapeDtypeStruct(rows.shape, BF16)
    wide = jax.ShapeDtypeStruct(rows.shape, F32)
    return pl.pallas_call(
        cross_forward_body, out_shape=[low, low, low, wide, wide, low],
        cost_estimate=FREE, name="cross",
    )(rows, own, far, norms, *query_parts, kv, *out_parts)


def deal_rows(rows, size, column, own, away):
    for b in range(rows.shape[0] // (2 * size)):
        at = slice(b * size, (b + 1) * size)
        even = rows[2 * b * size : (2 * b + 1) * size, :]
        odd = rows[(2 * b + 1) * size : (2 * b + 2) * size, :]

        @pl.when(column == 0)
        def _():
            own[at, :] = even
            away[at, :] = odd

        @pl.when(column != 0)
        def _():
            own[at, :] = odd
            away[at, :] = even


def ffn_body(width_block, unit_block, place, n0, n1, n2, n3, grad, gate_w, up_w, down_w,
             hidden, hid_own, hid_away, gate_grad, lifted_grad, nrm_own, nrm_away, away, near,
             normed, total):
    step = pl.program_id(0)
    share = n0.shape[0]
    column = place[0]

    @pl.when(step == 0)
    def _():
        for b, ref in enumerate((n0, n1, n2, n3)):
            normed[b * share : (b + 1) * share, :] = ref[...]
        total[...] = jnp.zeros_like(total)
        deal_rows(normed[...].T, width_block, column, nrm_own, nrm_away)

    gate = dot_nn(normed[...], gate_w[...])
    lifted = dot_nn(normed[...], up_w[...])
    back = dot_nt(grad[...], down_w[...]).astype(BF16).astype(F32)
    sig = jax.nn.sigmoid(gate)
    swish = gate * sig
    low = (swish * lifted).astype(BF16)
    hidden[...] = low
    deal_rows(low.T, unit_block, column, hid_own, hid_away)
    gg = (back * lifted * sig * (1.0 + gate * (1.0 - sig))).astype(BF16)
    lg = (back * swish).astype(BF16)
    gate_grad[...] = gg
    lifted_grad[...] = lg
    total[...] += dot_nt(gg, gate_w[...]) + dot_nt(lg, up_w[...])

    @pl.when(step == pl.num_programs(0) - 1)
    def _():
        for b in (0, 1):
            near[b * share : (b + 1) * share, :] = total[2 * b * share : (2 * b + 1) * share, :]
            away[b * share : (b + 1) * share, :] = total[
                (2 * b + 1) * share : (2 * b + 2) * share, :
            ].astype(BF16)


def ffn(devices, place, parts, grad, gate_w, up_w, down_w):
    share, width = parts[0].shape
    size, units = 4 * share, gate_w.shape[1]
    tile = units // 2
    whole = lambda r, c: pl.BlockSpec((r, c), lambda i, s: (0, 0))
    cols = lambda r: pl.BlockSpec((r, tile), lambda i, s: (0, i))
    rows = lambda c: pl.BlockSpec((tile, c), lambda i, s: (i, 0))
    halves = pl.BlockSpec((tile // 2, size), lambda i, s: (i, 0))
    low = lambda r, c: jax.ShapeDtypeStruct((r, c), BF16)
    return pl.pallas_call(
        functools.partial(ffn_body, width // devices, units // devices),
        grid_spec=pltpu.PrefetchScalarGridSpec(
            num_scalar_prefetch=1,
            grid=(2,),
            in_specs=[whole(share, width)] * 4
            + [whole(size, width), cols(width), cols(width), rows(width)],
            out_specs=[cols(size), halves, halves, cols(size), cols(size),
                       whole(width // 2, size), whole(width // 2, size),
                       whole(2 * share, width), whole(2 * share, width)],
            scratch_shapes=[pltpu.VMEM((size, width), BF16), pltpu.VMEM((size, width), F32)],
        ),
        out_shape=[low(size, units), low(units // 2, size), low(units // 2, size),
                   low(size, units), low(size, units), low(width // 2, size),
                   low(width // 2, size), low(2 * share, width),
                   jax.ShapeDtypeStruct((2 * share, width), F32)],
        cost_estimate=FREE, name="ffn",
    )(place, *parts, grad, gate_w, up_w, down_w)


def cross_backward_body(own, far, grad, first, second, norms, q0, q1, q2, q3, kv,
                        o0, o1, o2, o3, queries, grad_two, query_grad, kv_grad, vectors, grad_one,
                        crossed_grad):
    width = grad.shape[1]
    context_rows = kv.shape[0] // 2
    part = width // 4
    lanes = lax.broadcasted_iota(jnp.int32, (grad.shape[0], 2 * HEAD_SIZE), 1) // HEAD_SIZE
    lane_k = lax.broadcasted_iota(jnp.int32, (context_rows, 2 * HEAD_SIZE), 1) // HEAD_SIZE
    scale = 1.0 / math.sqrt(HEAD_SIZE)
    arrived = own[...] + far[...].astype(F32)
    scaled, inverse = normalize(second[...])
    vectors[0:1, :] = jnp.sum(arrived * scaled, 0, keepdims=True)
    vectors[1:2, :] = jnp.sum(arrived, 0, keepdims=True)
    two = grad[...].astype(F32) + norm_backward(arrived, scaled, inverse, norms[4:5, :])
    low = two.astype(BF16)
    grad_two[...] = low
    for b, ref in enumerate((o0, o1, o2, o3)):
        crossed_grad[:, b * part : (b + 1) * part] = dot_nt(low, ref[...]).astype(BF16)
    for p in range(width // (2 * HEAD_SIZE)):
        cols = slice(p * 2 * HEAD_SIZE, (p + 1) * 2 * HEAD_SIZE)
        q, k, v = queries[:, cols], kv[:context_rows, cols], kv[context_rows:, cols]
        g_rows = crossed_grad[:, cols]
        found = []
        for g in (0, 1):
            probs = head_weights(q, k, lanes, g)
            change = dot_nt(jnp.where(lanes == g, g_rows, jnp.zeros_like(g_rows)), v)
            delta = jnp.sum(change * probs, -1, keepdims=True)
            ds = (probs * (change - delta)).astype(BF16)
            found.append((dot_nn(ds, k), dot_tn(ds, q), dot_tn(probs.astype(BF16), g_rows)))
        query_grad[:, cols] = (
            jnp.where(lanes == 0, found[0][0], found[1][0]) * scale
        ).astype(BF16)
        kv_grad[:context_rows, cols] = (
            jnp.where(lane_k == 0, found[0][1], found[1][1]) * scale
        ).astype(BF16)
        kv_grad[context_rows:, cols] = jnp.where(lane_k == 0, found[0][2], found[1][2]).astype(
            BF16
        )
    back = jnp.zeros(grad.shape, F32)
    for b, ref in enumerate((q0, q1, q2, q3)):
        back = back + dot_nt(query_grad[:, b * part : (b + 1) * part], ref[...])
    scaled, inverse = normalize(first[...])
    vectors[2:3, :] = jnp.sum(back * scaled, 0, keepdims=True)
    vectors[3:4, :] = jnp.sum(back, 0, keepdims=True)
    grad_one[...] = (two + norm_backward(back, scaled, inverse, norms[2:3, :])).astype(BF16)


def cross_backward(own, far, grad, first, second, norms, query_parts, kv, out_parts, queries):
    rows, width = own.shape
    low = lambda r: jax.ShapeDtypeStruct((r, width), BF16)
    return pl.pallas_call(
        cross_backward_body,
        out_shape=[low(rows), low(rows), low(kv.shape[0]),
                   jax.ShapeDtypeStruct((4, width), F32), low(rows)],
        in_specs=[pl.BlockSpec((rows, width), lambda: (0, 0)), pl.BlockSpec((rows, width), lambda: (0, 0)),
                  pl.BlockSpec((rows, width), lambda: (0, 0))]
        + [pl.BlockSpec(memory_space=pltpu.VMEM)] * 13,
        scratch_shapes=[pltpu.VMEM((rows, width), BF16)],
        cost_estimate=FREE, name="cross_back",
    )(own, far, grad, first, second, norms, *query_parts, kv, *out_parts, queries)


def front_body(width_block, place, x0, x1, x2, x3, g0, g1, g2, g3, cosine, sine, wq, wk, wv,
               queries, pair, rows, low, nrm_own, nrm_away, norms, means, inverses, wide):
    size, part = x0.shape
    for r, (x, g) in enumerate(((x0, g0), (x1, g1), (x2, g2), (x3, g3))):
        start = pl.multiple_of((place[0] ^ r) * part, 128)
        wide[:, pl.ds(start, part)] = x[...]
        norms[:, pl.ds(start, part)] = g[...]
    share = size // 4
    rows[...] = wide[pl.ds(pl.multiple_of(place[0] * share, share), share), :]
    values = wide[...].astype(F32)
    mean = jnp.mean(values, -1, keepdims=True)
    centred = values - mean
    inverse = lax.rsqrt(jnp.mean(centred * centred, -1, keepdims=True) + 1e-05)
    means[...] = mean
    inverses[...] = inverse
    normed = (centred * inverse * norms[0:1, :] + norms[1:2, :]).astype(BF16)
    low[...] = normed
    half = HEAD_SIZE // 2

    def turned(weight):
        return dot_nn(normed, weight[...]).T

    def rotated(block, dest, scale):
        for h in range(part // HEAD_SIZE):
            a = block[h * HEAD_SIZE : h * HEAD_SIZE + half, :]
            b = block[h * HEAD_SIZE + half : (h + 1) * HEAD_SIZE, :]
            dest[h * HEAD_SIZE : h * HEAD_SIZE + half, :] = (
                (a * cosine[...] - b * sine[...]) * scale
            ).astype(BF16)
            dest[h * HEAD_SIZE + half : (h + 1) * HEAD_SIZE, :] = (
                (b * cosine[...] + a * sine[...]) * scale
            ).astype(BF16)

    rotated(turned(wk), pair.at[0], 1.0)
    pair[1] = turned(wv).astype(BF16)
    rotated(turned(wq), queries, 1.0 / math.sqrt(HEAD_SIZE))
    deal_rows(normed.T, width_block, place[1], nrm_own, nrm_away)


def front(devices, place, parts, norm_parts, tables, wq, wk, wv):
    size, part = parts[0].shape
    width = 4 * part
    low = lambda *s: jax.ShapeDtypeStruct(s, BF16)
    wide = lambda *s: jax.ShapeDtypeStruct(s, F32)
    vmem = pl.BlockSpec(memory_space=pltpu.VMEM)
    return pl.pallas_call(
        functools.partial(front_body, width // devices),
        in_specs=[pl.BlockSpec(memory_space=pltpu.SMEM)] + [vmem] * 13,
        out_specs=[vmem] * 9,
        out_shape=[low(part, size), low(2, part, size), low(size // 4, width), low(size, width),
                   low(width // 2, size), low(width // 2, size), wide(6, width),
                   wide(size, 1), wide(size, 1)],
        scratch_shapes=[pltpu.VMEM((size, width), BF16)],
        cost_estimate=FREE, name="front",
    )(place, *parts, *norm_parts, *tables, wq, wk, wv)


def per_device(
    frames,
    segment,
    time_token,
    context,
    gain_attn,
    bias_attn,
    gain_cross,
    bias_cross,
    gain_ffn,
    bias_ffn,
    w_query,
    w_key,
    w_value,
    w_out,
    c_query,
    c_key,
    c_value,
    c_out,
    w_gate,
    w_up,
    w_down,
    out_grad,
):
    local_rows = frames.shape[0]
    local_width = frames.shape[1]
    model_width = w_query.shape[0]
    head_cols = w_query.shape[1]
    heads = head_cols // HEAD_SIZE
    number_of_frames = lax.axis_size("seq") * local_rows
    row_length = min(max(ROW_MIN, 64 * lax.axis_size("seq")), number_of_frames)
    first_frame = lax.axis_index("seq") * local_rows
    own_start = lax.axis_index("tensor") * local_width

    def own_cols(value):
        return lax.dynamic_slice_in_dim(value, own_start, local_width, value.ndim - 1)

    place = lax.axis_index("tensor")
    share = local_rows // 4

    def own_rows(value):
        return rows_of(value, place * share, share)

    def row_block(value, index):
        return rows_of(value, index * share, share)

    place = lax.axis_index("tensor")
    share = local_rows // 4

    def own_rows(value):
        return rows_of(value, place * share, share)

    def row_block(value, index):
        return rows_of(value, index * share, share)

    column = lax.axis_index("seq") % 2
    frame_parts_near = gather_near(frames)
    norm_parts = gather_near(
        jnp.stack([gain_attn, bias_attn, gain_cross, bias_cross, gain_ffn, bias_ffn])
    )
    clip_starts, frame_positions = frame_clip_labels(segment, row_length)
    own_labels = lax.dynamic_slice_in_dim(clip_starts, first_frame, local_rows)
    own_positions = lax.dynamic_slice_in_dim(frame_positions, first_frame, local_rows)
    blanks = jnp.full((local_rows,), -1, jnp.int32)
    key_labels = lax.dynamic_slice_in_dim(
        jnp.concatenate([blanks, clip_starts, blanks]), first_frame, 3 * local_rows
    )
    spans = tile_ranges(own_labels, key_labels)
    label_row, label_column = own_labels[None, :], key_labels[:, None]
    row_index = first_frame // row_length
    time_row = lax.dynamic_slice_in_dim(time_token, row_index, 1, 0).astype(F32)
    row_context = lax.dynamic_slice_in_dim(context, row_index, 1, 0)[0]
    context_rows = row_context.shape[0]
    tables = rotary_tables(own_positions)
    score_scale = 1.0 / math.sqrt(HEAD_SIZE)
    all_heads = model_width // HEAD_SIZE

    (
        queries, both, frame_rows, frame_normed, one_own_half, one_away_half, norms, means_one,
        inverse_one,
    ) = front(
        lax.axis_size("seq"), jnp.stack([place, column]).astype(jnp.int32), frame_parts_near, norm_parts, tables,
        w_query, w_key, w_value,
    )
    own_keys, own_values = both[0], both[1]
    gain_one, bias_one = norms[0:1], norms[1:2]
    behind, ahead = shift(both, "seq", 1), shift(both, "seq", -1)
    query_far = swap(after(c_query, frame_parts_near[3]), "tensor", 2)
    out_far = swap(after(c_out, frame_parts_near[3]), "tensor", 2)
    time_late = after(time_row, both)
    scaled_time, _ = normalize(time_late)
    time_normed = (scaled_time * gain_one + bias_one).astype(BF16)
    time_keys = by_feature(time_normed, w_key).astype(BF16).astype(F32)
    time_values = by_feature(time_normed, w_value).astype(BF16).astype(F32)
    context_late = after(row_context, both)
    context_kv = jnp.concatenate(
        [product(context_late, c_key), product(context_late, c_value)], 0
    ).astype(BF16)
    kv_far = swap(context_kv, "tensor", 2)

    behind, ahead, query_far, out_far, kv_far = lax.optimization_barrier(
        (behind, ahead, query_far, out_far, kv_far)
    )
    keys = (behind[0], own_keys, ahead[0])
    values = (behind[1], own_values, ahead[1])
    attended, log_totals = attend(
        spans, queries, keys, values, time_keys, time_values, label_row, label_column
    )
    query_parts = (
        c_query, swap(after(c_query, both), "tensor", 1), query_far, swap(query_far, "tensor", 1)
    )
    out_parts = (c_out, swap(after(c_out, both), "tensor", 1), out_far, swap(out_far, "tensor", 1))
    kv_rows = jnp.concatenate([context_kv, kv_far], 0)
    kv_other = swap(kv_rows, "tensor", 1)
    count = context_kv.shape[0]
    cross_kv = jnp.concatenate([context_kv, kv_other[:count], kv_far, kv_other[count:]], 1)

    def out_rows(*relative):
        return jnp.concatenate(
            [
                jnp.einsum(
                    "fn,fd->nd",
                    lax.dynamic_slice_in_dim(attended, (place ^ r) * share, share, 1),
                    w_out,
                    preferred_element_type=F32,
                )
                for r in relative
            ],
            0,
        )

    one_own, one_far, one_near = scatter_near(out_rows(1, 3), out_rows(0, 2))
    normed_two, cross_queries, crossed, residual_one, residual_two, normed_share = cross_forward(
        frame_rows, one_own, one_far, norms, query_parts, cross_kv, out_parts
    )
    three_parts = gather_near(normed_share)
    own, mate, far, far_mate = gather_staged(out_grad, one_far, normed_share)
    grad_low = ordered(own, far, mate, far_mate, 1)
    grad_near = jnp.concatenate([row_block(grad_low, place ^ r) for r in range(4)], 0)
    (
        hidden, hidden_own, hidden_away, gate_grad, lifted_grad, three_own, three_away,
        normed_away, normed_near,
    ) = ffn(lax.axis_size("seq"), column.reshape(1), three_parts, grad_near, w_gate, w_up, w_down)
    three_sum, three_far, three_near = scatter_near(normed_away, normed_near)
    cross_full, cross_query_grad, kv_grad, norm_vectors, grad_one = cross_backward(
        three_sum, three_far, grad_near[:share], residual_one, residual_two, norms,
        query_parts, cross_kv, out_parts, cross_queries,
    )
    attend_full = gather(grad_one, 0)
    grad_heads = jnp.einsum(
        "nd,fd->fn", attend_full, w_out, preferred_element_type=F32
    ).astype(BF16)
    back = attend_back(
        spans, queries, keys, values, time_keys, time_values, label_row, label_column,
        attended, log_totals, grad_heads,
    )
    query_grad, key_prev, key_own, key_next, value_prev, value_own, value_next = back[:7]
    time_key_grad, time_value_grad = back[7], back[8]
    from_next = shift(jnp.stack([key_prev, value_prev]), "seq", -1)
    from_prev = shift(jnp.stack([key_next, value_next]), "seq", 1)
    query_raw = (rotate(query_grad, tables, -1.0) * score_scale).astype(BF16)
    key_raw = rotate(
        key_own + from_next[0].astype(F32) + from_prev[0].astype(F32), tables, -1.0
    ).astype(BF16)
    value_raw = (value_own + from_next[1].astype(F32) + from_prev[1].astype(F32)).astype(BF16)

    def to_frames(rows, weight):
        return jnp.einsum("fn,df->nd", rows, weight, preferred_element_type=F32)

    def frame_parts(*relative):
        return jnp.concatenate(
            [
                sum(
                    to_frames(rows, rows_of(weight, (place ^ r) * local_width, local_width))
                    for rows, weight in (
                        (query_raw, w_query), (key_raw, w_key), (value_raw, w_value)
                    )
                )
                for r in relative
            ],
            0,
        )

    last_own, last_far, last_near = scatter_near(frame_parts(1, 3), frame_parts(0, 2))
    frame_grad = last_own + last_far.astype(F32)
    time_grad = to_frames(time_key_grad.astype(BF16), w_key) + to_frames(
        time_value_grad.astype(BF16), w_value
    )
    own_scaled = (frames.astype(F32) - means_one) * inverse_one
    scaled_grad = frame_grad * gain_attn[None]
    sums = jnp.concatenate(
        [
            jnp.sum(scaled_grad, -1),
            jnp.sum(scaled_grad * own_scaled, -1),
            time_grad[0],
            norm_vectors.reshape(-1),
        ]
    )[None]
    sums = sums + swap(sums, "tensor", 1)
    sums = sums + swap(sums, "tensor", 2)
    plain = sums[0, :local_rows, None] / model_width
    cross = sums[0, local_rows : 2 * local_rows, None] / model_width
    vectors = own_cols(sums[0, 2 * local_rows :].reshape(5, model_width))
    d_frames = own_cols(attend_full).astype(F32) + inverse_one * (
        scaled_grad - plain - own_scaled * cross
    )
    d_gain_attn = jnp.sum(frame_grad * own_scaled, 0) + vectors[0] * own_cols(scaled_time)[0]
    d_bias_attn = jnp.sum(frame_grad, 0) + vectors[0]
    small = reduce_small(
        jnp.stack([d_gain_attn, d_bias_attn, vectors[3], vectors[4], vectors[1], vectors[2]])
    )

    def down_rows(*relative):
        late = after(hidden, three_sum)
        return jnp.concatenate([product(row_block(late, r), w_down) for r in relative], 0)

    down_own, down_far, _ = scatter_near(down_rows(1, 3), down_rows(0, 2))
    block_rows = (residual_two + (down_own + down_far.astype(F32))).astype(BF16)
    block_cols = rows_to_cols(
        *[
            lax.dynamic_slice_in_dim(block_rows, (place ^ r) * local_width, local_width, 1)
            for r in range(4)
        ],
        attend_full,
    )
    block_out = jnp.concatenate([row_block(block_cols, place ^ b) for b in range(4)], 0)

    kv_parts = quarters(after(kv_grad, attend_full), 1)
    kv_own, kv_away, _ = scatter_near(
        jnp.concatenate([kv_parts[1], kv_parts[3]], 0),
        jnp.concatenate([kv_parts[0], kv_parts[2]], 0).astype(F32),
    )
    context_own = kv_own + after(kv_away, query_grad).astype(F32)
    forward_near = gather_staged(jnp.concatenate([normed_two, crossed], 1), three_far, grad_one)
    two_full = jnp.concatenate([value[:, :model_width] for value in forward_near], 0)
    crossed_own = own_blocks([value[:, model_width:] for value in forward_near])
    back_near = gather_staged(
        jnp.concatenate([cross_full, cross_query_grad], 1), attend_full, query_grad
    )
    cross_grad_full = jnp.concatenate([value[:, :model_width] for value in back_near], 0)
    cross_query_own = own_blocks([value[:, model_width:] for value in back_near])
    time_column = time_normed.astype(F32).T

    def context_grads(kv):
        left = row_context.T
        both_grads = jnp.concatenate([kv[:context_rows], kv[context_rows:]], 1)
        return product(left, both_grads.astype(BF16))

    count = lax.axis_size("seq")

    def meet(rows, cols, spec):
        blocks = sum(
            jnp.einsum(spec, r, c, preferred_element_type=F32) for r, c in zip(rows, cols)
        )
        return blocks.reshape(count // 2, 2 * blocks.shape[0] // count, blocks.shape[1])

    normed_pair = (one_own_half, trade(one_away_half, attended, normed_share))
    grad_pair = (grad_near, trade(grad_near, normed_share, grad_one))
    hidden_pair = (hidden_own, trade(hidden_away, hidden, grad_one))
    three_pair = (three_own, trade(three_away, three_sum, query_grad))
    gate_pair = (gate_grad, trade(gate_grad, three_sum, query_grad))
    lifted_pair = (lifted_grad, trade(lifted_grad, grad_heads, from_next))

    down_blocks = meet(hidden_pair, grad_pair, "dn,nf->df").astype(BF16)
    grad_down = halve_all(down_blocks, 1, grad_one, query_grad, query_grad, from_next)
    gate_blocks = meet(three_pair, gate_pair, "dn,nf->df").astype(BF16)
    grad_gate_w = halve_all(gate_blocks, 1, query_grad, last_near, last_near, last_far)
    up_blocks = meet(three_pair, lifted_pair, "dn,nf->df").astype(BF16)
    grad_up_w = halve_all(up_blocks, 1, last_near, last_far, last_far, last_far)

    late = after((crossed_own, cross_grad_full), query_grad)
    grad_c_out = inner_rows(*late).astype(BF16)
    late = after((two_full, cross_query_own), query_grad)
    grad_c_query = inner_rows(*late).astype(BF16)
    grad_c_kv = context_grads(context_own).astype(BF16)
    late = after((attended, attend_full), query_grad)
    grad_w_out = product(*late).astype(BF16)
    part = head_cols // count
    bundle = jnp.concatenate(
        [
            value.reshape(count, part, model_width)
            for value in (grad_c_out, grad_c_query, grad_c_kv, grad_w_out)
        ],
        1,
    )
    middle = halve_all(
        bundle, 0, from_next, last_near, last_near, last_far, last_far, last_far
    )
    grad_c_out = middle[:part]
    grad_c_query = middle[part : 2 * part].reshape(model_width // count, head_cols)
    grad_c_kv = middle[2 * part : 3 * part].reshape(-1, 2 * head_cols)
    grad_w_out = middle[3 * part :]

    raw = jnp.concatenate([query_raw, key_raw, value_raw], 0)
    raw_pair = (raw, trade(raw, key_raw, last_near))
    time_both = jnp.concatenate([time_key_grad, time_value_grad], 0)
    time_both = time_both + trade(time_both, from_next, key_raw)
    own_time_rows = lax.dynamic_index_in_dim(
        time_column.reshape(count // 2, 2, -1), column, 1, False
    ).reshape(-1, 1)
    outer = own_time_rows * jnp.concatenate([jnp.zeros((head_cols, 1), F32), time_both], 0).T
    blocks = meet(normed_pair, raw_pair, "dn,fn->df")
    blocks = (blocks + outer.reshape(blocks.shape)).astype(BF16)
    heads_sum = halve_all(blocks, 1, last_far, last_far, last_far, last_far)
    grad_w_query, grad_w_key, grad_w_value = (
        heads_sum[:, i * head_cols : (i + 1) * head_cols] for i in range(3)
    )
    return (
        block_out,
        d_frames,
        small[0],
        small[1],
        small[2],
        small[3],
        small[4],
        small[5],
        grad_w_query,
        grad_w_key,
        grad_w_value,
        grad_w_out,
        grad_c_query,
        grad_c_kv[:, :head_cols],
        grad_c_kv[:, head_cols:],
        grad_c_out,
        grad_gate_w,
        grad_up_w,
        grad_down,
    )


def solution(mesh):
    return jax.shard_map(
        per_device,
        mesh=mesh,
        in_specs=(
            P("seq", "tensor"),
            P(),
            P(),
            P(),
            P("tensor"),
            P("tensor"),
            P("tensor"),
            P("tensor"),
            P("tensor"),
            P("tensor"),
            P(None, "tensor"),
            P(None, "tensor"),
            P(None, "tensor"),
            P("tensor", None),
            P(None, "tensor"),
            P(None, "tensor"),
            P(None, "tensor"),
            P("tensor", None),
            P(None, "tensor"),
            P(None, "tensor"),
            P("tensor", None),
            P("seq", "tensor"),
        ),
        out_specs=(
            P("seq", "tensor"),
            P("seq", "tensor"),
            P(("tensor", "seq")),
            P(("tensor", "seq")),
            P(("tensor", "seq")),
            P(("tensor", "seq")),
            P(("tensor", "seq")),
            P(("tensor", "seq")),
            P("seq", "tensor"),
            P("seq", "tensor"),
            P("seq", "tensor"),
            P(("tensor", "seq"), None),
            P("seq", "tensor"),
            P("seq", "tensor"),
            P("seq", "tensor"),
            P(("tensor", "seq"), None),
            P("seq", "tensor"),
            P("seq", "tensor"),
            P(("tensor", "seq"), None),
        ),
        check_vma=False,
    )
```

```python
import functools
import math

import jax
import jax.numpy as jnp
from jax import lax
from jax.experimental import pallas as pl
from jax.experimental.pallas import tpu as pltpu
from jax.sharding import PartitionSpec as P

HEAD_SIZE = 64
ROW_MIN = 2048
TILE = 256
BF16 = jnp.bfloat16
F32 = jnp.float32


def meeting(*values):
    return lax.optimization_barrier(values)


def after(value, token):
    return lax.optimization_barrier((value, token))[0]


def swap(value, axis, by):
    return lax.ppermute(value, axis, [(i, i ^ by) for i in range(lax.axis_size(axis))])


def shift(value, axis, by):
    peers = lax.axis_size(axis)
    pairs = [(i, i + by) for i in range(peers) if 0 <= i + by < peers]
    return lax.ppermute(value, axis, pairs)


def tensor_place():
    place = lax.axis_index("tensor")
    return place // 2, place % 2


def ordered(own, far, mate, far_mate, axis):
    side, core = tensor_place()
    near = (jnp.where(core == 0, own, mate), jnp.where(core == 0, mate, own))
    away = (jnp.where(core == 0, far, far_mate), jnp.where(core == 0, far_mate, far))
    low = [jnp.where(side == 0, n, a) for n, a in zip(near, away)]
    high = [jnp.where(side == 0, a, n) for n, a in zip(near, away)]
    return jnp.concatenate(low + high, axis)


def gather_near(own):
    far = swap(own, "tensor", 2)
    return own, swap(own, "tensor", 1), far, swap(far, "tensor", 1)


def gather_staged(own, first, second):
    far = swap(after(own, first), "tensor", 2)
    far, late = after((far, own), second)
    return own, swap(late, "tensor", 1), far, swap(far, "tensor", 1)


def gather(own, axis):
    own, mate, far, far_mate = gather_near(own)
    return ordered(own, far, mate, far_mate, axis)


def scatter_near(away, low):
    got = swap(away, "tensor", 1)
    total = (low.astype(F32) + got[low.shape[0] :].astype(F32)).astype(BF16)
    return got, total, swap(total, "tensor", 2)


def rows_to_cols(own, mate, far, far_mate, later):
    width = own.shape[1]
    got = after(swap(jnp.concatenate([far, far_mate], 1), "tensor", 2), later)
    other = swap(jnp.concatenate([mate, got[:, width:]], 0), "tensor", 1)
    size = own.shape[0]
    return jnp.concatenate([own, other[:size], got[:, :width], other[size:]], 0)


def quarters(value, axis):
    return jnp.split(value, 4, axis)


def own_blocks(near):
    return jnp.concatenate([quarters(value, 1)[r] for r, value in enumerate(near)], 0)


def trade(value, start, done):
    return after(swap(after(value, start), "seq", 1), done)


def halve(blocks, bit):
    count, rows, cols = blocks.shape
    side = (lax.axis_index("seq") >> bit) % 2
    parts = blocks.reshape(count // 2, 2, rows, cols)
    send = lax.dynamic_index_in_dim(parts, 1 - side, 1, False)
    keep = lax.dynamic_index_in_dim(parts, side, 1, False)
    return keep, swap(send, "seq", 1 << bit)


def added(keep, got):
    return keep.astype(F32) + got.astype(F32)


def halve_all(blocks, bit):
    while blocks.shape[0] > 1:
        blocks = added(*halve(blocks.astype(BF16), bit))
        bit += 1
    return blocks[0].astype(F32)


def halve_end(keep, got, bit):
    return halve_all(added(keep, got), bit)


def reduce_small(vectors):
    count = lax.axis_size("seq")
    kinds, width = vectors.shape
    parts = vectors.reshape(kinds, count, width // count).transpose(1, 0, 2)
    bit = 0
    while parts.shape[0] > 1:
        parts = added(*halve(parts, bit))
        bit += 1
    return parts[0]


def frame_clip_labels(segment, row_length):
    frame_index = jnp.arange(segment.shape[0], dtype=jnp.int32)
    border = (frame_index % row_length == 0) | (segment != jnp.roll(segment, 1))
    clip_starts = lax.cummax(jnp.where(border, frame_index, 0), axis=0)
    return (clip_starts, (frame_index - clip_starts + 1).astype(jnp.float32))


def tile_ranges(q_labels, key_labels):
    q = q_labels.reshape(-1, TILE)
    k = key_labels.reshape(-1, TILE)
    meets = (k[None, :, 0] <= q[:, None, -1]) & (k[None, :, -1] >= q[:, None, 0])
    index = jnp.arange(k.shape[0], dtype=jnp.int32)[None]
    low = jnp.min(jnp.where(meets, index, k.shape[0]), 1)
    high = jnp.max(jnp.where(meets, index + 1, 0), 1)
    return jnp.stack([low, high], 1).reshape(-1)

def head_rows(g):
    return slice(g * HEAD_SIZE, (g + 1) * HEAD_SIZE)

def fill_natural(dest, refs):
    size = refs[0].shape[1]
    for part, ref in enumerate(refs):
        dest[part * size : (part + 1) * size, :] = ref[...].T

def relative(place, r, size):
    return pl.ds(pl.multiple_of((place ^ r) * size, size), size)


def forward_body(span, q, k0, k1, k2, v0, v1, v2, tk, tv, qlab, klab, w_out,
                 out, lse, away, own, low, keys, vals):
    rows, size = q.shape
    group = rows // HEAD_SIZE
    pieces = size // TILE
    fill_natural(keys, (k0, k1, k2))
    for part, ref in enumerate((v0, v1, v2)):
        for piece in range(pieces):
            vals[part * pieces + piece] = ref[:, piece * TILE : (piece + 1) * TILE]
    for tile in range(pieces):
        cols = slice(tile * TILE, (tile + 1) * TILE)
        lab = qlab[:, cols]
        state = []
        for g in range(group):
            part = q[head_rows(g), cols].astype(F32)
            top = jnp.sum(part * tk[head_rows(g), :], 0, keepdims=True)
            state += [
                top,
                jnp.ones_like(top),
                jnp.broadcast_to(tv[head_rows(g), :], (HEAD_SIZE, TILE)),
            ]

        def step(j, state):
            start = pl.multiple_of(j * TILE, TILE)
            seen = klab[pl.ds(start, TILE), :] == lab
            fresh = []
            for g in range(group):
                top, total, acc = state[3 * g : 3 * g + 3]
                s = dot_nn(keys[pl.ds(start, TILE), head_rows(g)], q[head_rows(g), cols])
                s = jnp.where(seen, s, -1e30)
                new = jnp.maximum(top, jnp.max(s, 0, keepdims=True))
                fade = jnp.exp(top - new)
                p = jnp.exp(s - new)
                total = total * fade + jnp.sum(p, 0, keepdims=True)
                acc = acc * fade + dot_nn(vals[j, head_rows(g), :], p.astype(BF16))
                fresh += [new, total, acc]
            return tuple(fresh)

        state = lax.fori_loop(span[2 * tile], span[2 * tile + 1], step, tuple(state))
        for g in range(group):
            top, total, acc = state[3 * g : 3 * g + 3]
            out[head_rows(g), cols] = (acc / total).astype(BF16)
            lse[g : g + 1, cols] = top + jnp.log(total)
    place = span[2 * pieces]
    share = own.shape[0]

    def sent(r):
        return dot_tn(out[:, relative(place, r, share)], w_out[...])

    away[:share, :] = sent(1).astype(BF16)
    away[share:, :] = sent(3).astype(BF16)
    low[...] = sent(2).astype(BF16)
    own[...] = sent(0)


def backward_body(span, q, k0, k1, k2, v0, v1, v2, tk, tv, qlab, klab, w_out, out, lse,
                  g0, g1, g2, g3, dq, to_prev, kept, to_next, dtk, dtv,
                  og, keys, vals, tkeys, ak, av):
    rows, size = q.shape
    group = rows // HEAD_SIZE
    pieces = size // TILE
    share = g0.shape[0]
    for r, ref in enumerate((g0, g1, g2, g3)):
        og[:, relative(span[2 * pieces], r, share)] = dot_nt(w_out[...], ref[...]).astype(BF16)
    fill_natural(keys, (k0, k1, k2))
    fill_natural(vals, (v0, v1, v2))
    for part, ref in enumerate((k0, k1, k2)):
        for piece in range(pieces):
            tkeys[part * pieces + piece] = ref[:, piece * TILE : (piece + 1) * TILE]
    ak[...] = jnp.zeros_like(ak)
    av[...] = jnp.zeros_like(av)
    for tile in range(pieces):
        cols = slice(tile * TILE, (tile + 1) * TILE)
        lab = qlab[:, cols]
        state, norms, deltas = [], [], []
        for g in range(group):
            hr = head_rows(g)
            qf = q[hr, cols].astype(F32)
            gf = og[hr, cols].astype(F32)
            norm = lse[g : g + 1, cols]
            delta = jnp.sum(gf * out[hr, cols].astype(F32), 0, keepdims=True)
            pt = jnp.exp(jnp.sum(qf * tk[hr, :], 0, keepdims=True) - norm)
            st = pt * (jnp.sum(gf * tv[hr, :], 0, keepdims=True) - delta)
            gk = jnp.sum(qf * st, 1, keepdims=True)
            gv = jnp.sum(gf * pt, 1, keepdims=True)
            if tile == 0:
                dtk[hr, :] = gk
                dtv[hr, :] = gv
            else:
                dtk[hr, :] += gk
                dtv[hr, :] += gv
            state.append(tk[hr, :] * st)
            norms.append(norm)
            deltas.append(delta)

        def step(j, state):
            start = pl.multiple_of(j * TILE, TILE)
            seen = klab[pl.ds(start, TILE), :] == lab
            fresh = []
            for g in range(group):
                hr = head_rows(g)
                s = dot_nn(keys[pl.ds(start, TILE), hr], q[hr, cols])
                p = jnp.exp(jnp.where(seen, s, -1e30) - norms[g])
                m = dot_nn(vals[pl.ds(start, TILE), hr], og[hr, cols])
                ds = (p * (m - deltas[g])).astype(BF16)
                av[j, hr, :] += dot_nt(og[hr, cols], p.astype(BF16))
                ak[j, hr, :] += dot_nt(q[hr, cols], ds)
                fresh.append(state[g] + dot_nn(tkeys[j, hr, :], ds))
            return tuple(fresh)

        state = lax.fori_loop(span[2 * tile], span[2 * tile + 1], step, tuple(state))
        for g in range(group):
            dq[head_rows(g), cols] = state[g]
    for part, dest in enumerate((to_prev, kept, to_next)):
        for piece in range(pieces):
            at = slice(piece * TILE, (piece + 1) * TILE)
            dest[0, :, at] = ak[part * pieces + piece].astype(dest.dtype)
            dest[1, :, at] = av[part * pieces + piece].astype(dest.dtype)


def attend(span, q, ks, vs, tk, tv, qlab, klab, w_out):
    cols, size = q.shape
    share, width = size // 4, w_out.shape[1]
    tiles = 3 * size // TILE
    low = lambda *dims: jax.ShapeDtypeStruct(dims, BF16)
    wide = lambda *dims: jax.ShapeDtypeStruct(dims, F32)
    vmem = pl.BlockSpec(memory_space=pltpu.VMEM)
    return pl.pallas_call(
        forward_body,
        in_specs=[pl.BlockSpec(memory_space=pltpu.SMEM)] + [vmem] * 12,
        out_specs=[vmem] * 5,
        out_shape=[low(cols, size), wide(cols // HEAD_SIZE, size), low(2 * share, width),
                   wide(share, width), low(share, width)],
        scratch_shapes=[pltpu.VMEM((3 * size, cols), BF16), pltpu.VMEM((tiles, cols, TILE), BF16)],
        name="attend", cost_estimate=FREE,
    )(span, q, *ks, *vs, tk, tv, qlab, klab, w_out)


def attend_back(span, q, ks, vs, tk, tv, qlab, klab, w_out, out, lse, grads):
    cols, size = q.shape
    tiles = 3 * size // TILE
    low = lambda *dims: jax.ShapeDtypeStruct(dims, BF16)
    wide = lambda *dims: jax.ShapeDtypeStruct(dims, F32)
    vmem = pl.BlockSpec(memory_space=pltpu.VMEM)
    return pl.pallas_call(
        backward_body,
        in_specs=[pl.BlockSpec(memory_space=pltpu.SMEM)] + [vmem] * 18,
        out_specs=[vmem] * 6,
        out_shape=[wide(cols, size), low(2, cols, size), wide(2, cols, size), low(2, cols, size),
                   wide(cols, 1), wide(cols, 1)],
        scratch_shapes=[pltpu.VMEM((cols, size), BF16), pltpu.VMEM((3 * size, cols), BF16),
                        pltpu.VMEM((3 * size, cols), BF16), pltpu.VMEM((tiles, cols, TILE), BF16),
                        pltpu.VMEM((tiles, cols, TILE), F32), pltpu.VMEM((tiles, cols, TILE), F32)],
        name="attend_back", cost_estimate=FREE,
    )(span, q, *ks, *vs, tk, tv, qlab, klab, w_out, out, lse, *grads)


def tail_body(place, dq, kept, ahead, behind, cosine, sine, wq, wk, wv, raw, away, own, low, flipped):
    part, size = dq.shape
    half = HEAD_SIZE // 2

    def returned(block, base, scale):
        for h in range(part // HEAD_SIZE):
            a = block[h * HEAD_SIZE : h * HEAD_SIZE + half, :]
            b = block[h * HEAD_SIZE + half : (h + 1) * HEAD_SIZE, :]
            at = base + h * HEAD_SIZE
            raw[at : at + half, :] = ((a * cosine[...] + b * sine[...]) * scale).astype(BF16)
            raw[at + half : at + HEAD_SIZE, :] = (
                (b * cosine[...] - a * sine[...]) * scale
            ).astype(BF16)

    def whole(index):
        return kept[index] + ahead[index].astype(F32) + behind[index].astype(F32)

    returned(dq[...], 0, 1.0 / math.sqrt(HEAD_SIZE))
    returned(whole(0), part, 1.0)
    raw[2 * part :, :] = whole(1).astype(BF16)
    flipped[...] = raw[...].T

    def sent(r):
        at = relative(place[0], r, part)
        return sum(
            dot_nt(flipped[:, i * part : (i + 1) * part], weight[at, :])
            for i, weight in enumerate((wq, wk, wv))
        )

    away[:size, :] = sent(1).astype(BF16)
    away[size:, :] = sent(3).astype(BF16)
    low[...] = sent(2).astype(BF16)
    own[...] = sent(0)


def tail(place, dq, kept, ahead, behind, tables, wq, wk, wv):
    part, size = dq.shape
    low = lambda *dims: jax.ShapeDtypeStruct(dims, BF16)
    vmem = pl.BlockSpec(memory_space=pltpu.VMEM)
    return pl.pallas_call(
        tail_body,
        in_specs=[pl.BlockSpec(memory_space=pltpu.SMEM)] + [vmem] * 9,
        out_specs=[vmem] * 4,
        out_shape=[low(3 * part, size), low(2 * size, part), jax.ShapeDtypeStruct((size, part), F32),
                   low(size, part)],
        scratch_shapes=[pltpu.VMEM((size, 3 * part), BF16)],
        name="tail", cost_estimate=FREE,
    )(place, dq, kept, ahead, behind, *tables, wq, wk, wv)


def rotary_tables(frame_positions):
    half_dim = HEAD_SIZE // 2
    frequency = jnp.exp(jnp.arange(half_dim, dtype=jnp.float32) * (-math.log(10000.0) / half_dim))
    angles = frequency[:, None] * frame_positions[None, :]
    return (jnp.cos(angles), jnp.sin(angles))


def rotate(rows, tables, sign=1.0):
    count, size = rows.shape
    halves = rows.reshape(count // HEAD_SIZE, 2, HEAD_SIZE // 2, size)
    cosine, sine = tables[0][None], tables[1][None] * sign
    first = halves[:, 0] * cosine - halves[:, 1] * sine
    second = halves[:, 1] * cosine + halves[:, 0] * sine
    return jnp.stack([first, second], 1).reshape(count, size)


def product(left, right):
    return jnp.dot(left, right, preferred_element_type=jnp.float32)


def inner_rows(left, right):
    return jnp.einsum("nd,nf->df", left, right, preferred_element_type=jnp.float32)


def back_project(gradient, weight):
    return jnp.einsum("nf,df->nd", gradient, weight, preferred_element_type=jnp.float32)


def by_feature(left, right):
    return jnp.einsum("nd,df->fn", left, right, preferred_element_type=jnp.float32)


def columns(weight, start, size):
    return lax.dynamic_slice_in_dim(weight, start, size, 1)


def rows_of(weight, start, size):
    return lax.dynamic_slice_in_dim(weight, start, size, 0)


def normalize(value_rows):
    means = jnp.mean(value_rows, -1, keepdims=True)
    centred = value_rows - means
    inverse = lax.rsqrt(jnp.mean(centred * centred, -1, keepdims=True) + 1e-05)
    return centred * inverse, inverse


def norm_backward(gradient, scaled, inverse, norm_gain):
    scaled_grad = gradient * norm_gain
    plain = jnp.mean(scaled_grad, -1, keepdims=True)
    cross = jnp.mean(scaled_grad * scaled, -1, keepdims=True)
    return inverse * (scaled_grad - plain - scaled * cross)


FREE = pl.CostEstimate(flops=1, transcendentals=0, bytes_accessed=1)


def dot_nn(left, right):
    return lax.dot_general(left, right, (((1,), (0,)), ((), ())), preferred_element_type=F32)


def dot_nt(left, right):
    return lax.dot_general(left, right, (((1,), (1,)), ((), ())), preferred_element_type=F32)


def dot_tn(left, right):
    return lax.dot_general(left, right, (((0,), (0,)), ((), ())), preferred_element_type=F32)


def head_weights(query, key, lanes, which):
    mine = jnp.where(lanes == which, query, jnp.zeros_like(query))
    scores = dot_nt(mine, key) * (1.0 / math.sqrt(HEAD_SIZE))
    weights = jnp.exp(scores - jnp.max(scores, -1, keepdims=True))
    return weights / jnp.sum(weights, -1, keepdims=True)


def pair_cols(refs, p, rows):
    ref = refs[p * 2 * HEAD_SIZE // refs[0].shape[1]]
    start = p * 2 * HEAD_SIZE % refs[0].shape[1]
    return ref[rows, start : start + 2 * HEAD_SIZE]


def cross_forward_body(width_block, place, rows, own, got, far, norms, q0, q1, q2, q3,
                       c0, c1, c2, c3, o0, o1, o2, o3,
                       normed_two, queries, crossed, first, second, normed_three,
                       flip_own, flip_away):
    width = rows.shape[1]
    kv = (c0, c1, c2, c3)
    context_rows = c0.shape[0] // 2
    key_rows, value_rows = slice(0, context_rows), slice(context_rows, 2 * context_rows)
    lanes = lax.broadcasted_iota(jnp.int32, (rows.shape[0], 2 * HEAD_SIZE), 1) // HEAD_SIZE
    residual = (
        rows[...].astype(F32) + own[...] + got[...].astype(F32) + far[...].astype(F32)
    )
    first[...] = residual
    scaled, _ = normalize(residual)
    low = (scaled * norms[2:3, :] + norms[3:4, :]).astype(BF16)
    normed_two[...] = low
    part = width // 4
    for b, ref in enumerate((q0, q1, q2, q3)):
        queries[:, b * part : (b + 1) * part] = dot_nn(low, ref[...]).astype(BF16)
    for p in range(width // (2 * HEAD_SIZE)):
        cols = slice(p * 2 * HEAD_SIZE, (p + 1) * 2 * HEAD_SIZE)
        q, k, v = queries[:, cols], pair_cols(kv, p, key_rows), pair_cols(kv, p, value_rows)
        mixed = [dot_nn(head_weights(q, k, lanes, g).astype(BF16), v) for g in (0, 1)]
        crossed[:, cols] = jnp.where(lanes == 0, mixed[0], mixed[1]).astype(BF16)
    for b, ref in enumerate((o0, o1, o2, o3)):
        residual = residual + dot_nn(crossed[:, b * part : (b + 1) * part], ref[...])
    second[...] = residual
    scaled, _ = normalize(residual)
    low = (scaled * norms[4:5, :] + norms[5:6, :]).astype(BF16)
    normed_three[...] = low
    deal_rows(low.T, width_block, place[0], flip_own, flip_away)


def cross_forward(devices, place, rows, own, got, far, norms, query_parts, kv_parts, out_parts):
    size, width = rows.shape
    low = jax.ShapeDtypeStruct(rows.shape, BF16)
    wide = jax.ShapeDtypeStruct(rows.shape, F32)
    flip = jax.ShapeDtypeStruct((width // 2, size), BF16)
    vmem = pl.BlockSpec(memory_space=pltpu.VMEM)
    block = pl.BlockSpec((size, width), lambda i: (0, 0))
    return pl.pallas_call(
        functools.partial(cross_forward_body, width // devices),
        grid=(1,),
        in_specs=[pl.BlockSpec(memory_space=pltpu.SMEM)] + [block] * 4 + [vmem] * 13,
        out_shape=[low, low, low, wide, wide, low, flip, flip],
        cost_estimate=FREE, name="cross",
    )(place, rows, own, got, far, norms, *query_parts, *kv_parts, *out_parts)


def deal_rows(rows, size, column, own, away):
    for b in range(rows.shape[0] // (2 * size)):
        at = slice(b * size, (b + 1) * size)
        even = rows[2 * b * size : (2 * b + 1) * size, :]
        odd = rows[(2 * b + 1) * size : (2 * b + 2) * size, :]

        @pl.when(column == 0)
        def _():
            own[at, :] = even
            away[at, :] = odd

        @pl.when(column != 0)
        def _():
            own[at, :] = odd
            away[at, :] = even


def ffn_body(unit_block, place, n0, n1, n2, n3, g0, g1, g2, g3, gate_w, up_w, down_w,
             hidden, hid_own, hid_away, gate_grad, lifted_grad, away, own, low, grad, grad_pair,
             normed, total):
    step = pl.program_id(0)
    share = n0.shape[0]
    part = g0.shape[2]

    @pl.when(step == 0)
    def _():
        for b, ref in enumerate((n0, n1, n2, n3)):
            normed[b * share : (b + 1) * share, :] = ref[...]
        total[...] = jnp.zeros_like(total)
        for c, ref in enumerate((g0, g1, g2, g3)):
            for b in range(4):
                rows, cols = relative(place[1], b, share), relative(place[1], c, part)
                grad[b * share : (b + 1) * share, cols] = ref[0, rows, :]
                grad_pair[b * share : (b + 1) * share, cols] = ref[1, rows, :]

    gate = dot_nn(normed[...], gate_w[...])
    lifted = dot_nn(normed[...], up_w[...])
    back = dot_nt(grad[...], down_w[...]).astype(BF16).astype(F32)
    sig = jax.nn.sigmoid(gate)
    swish = gate * sig
    made = (swish * lifted).astype(BF16)
    hidden[...] = made
    deal_rows(made.T, unit_block, place[0], hid_own, hid_away)
    gg = (back * lifted * sig * (1.0 + gate * (1.0 - sig))).astype(BF16)
    lg = (back * swish).astype(BF16)
    gate_grad[...] = gg
    lifted_grad[...] = lg
    total[...] += dot_nt(gg, gate_w[...]) + dot_nt(lg, up_w[...])

    @pl.when(step == pl.num_programs(0) - 1)
    def _():
        own[...] = total[:share, :]
        low[...] = total[2 * share : 3 * share, :].astype(BF16)
        away[:share, :] = total[share : 2 * share, :].astype(BF16)
        away[share:, :] = total[3 * share :, :].astype(BF16)


def ffn(devices, place, parts, grads, gate_w, up_w, down_w):
    share, width = parts[0].shape
    size, units = 4 * share, gate_w.shape[1]
    tile = units // 2
    whole = lambda *dims: pl.BlockSpec(dims, lambda i, s: (0,) * len(dims))
    cols = lambda r: pl.BlockSpec((r, tile), lambda i, s: (0, i))
    rows = lambda c: pl.BlockSpec((tile, c), lambda i, s: (i, 0))
    halves = pl.BlockSpec((tile // 2, size), lambda i, s: (i, 0))
    low = lambda *dims: jax.ShapeDtypeStruct(dims, BF16)
    return pl.pallas_call(
        functools.partial(ffn_body, units // devices),
        grid_spec=pltpu.PrefetchScalarGridSpec(
            num_scalar_prefetch=1,
            grid=(2,),
            in_specs=[whole(share, width)] * 4 + [whole(2, size, width // 4)] * 4
            + [cols(width), cols(width), rows(width)],
            out_specs=[cols(size), halves, halves, cols(size), cols(size),
                       whole(2 * share, width), whole(share, width), whole(share, width),
                       whole(size, width), whole(size, width)],
            scratch_shapes=[pltpu.VMEM((size, width), BF16), pltpu.VMEM((size, width), F32)],
        ),
        out_shape=[low(size, units), low(units // 2, size), low(units // 2, size),
                   low(size, units), low(size, units), low(2 * share, width),
                   jax.ShapeDtypeStruct((share, width), F32), low(share, width),
                   low(size, width), low(size, width)],
        cost_estimate=FREE, name="ffn",
    )(place, *parts, *grads, gate_w, up_w, down_w)


def cross_backward_body(own, got, far, grad, first, second, norms, q0, q1, q2, q3,
                        c0, c1, c2, c3, o0, o1, o2, o3, queries,
                        grad_two, query_grad, kv_grad, vectors, grad_one, crossed_grad):
    width = grad.shape[1]
    kv = (c0, c1, c2, c3)
    context_rows = c0.shape[0] // 2
    key_rows, value_rows = slice(0, context_rows), slice(context_rows, 2 * context_rows)
    part = width // 4
    lanes = lax.broadcasted_iota(jnp.int32, (grad.shape[0], 2 * HEAD_SIZE), 1) // HEAD_SIZE
    lane_k = lax.broadcasted_iota(jnp.int32, (context_rows, 2 * HEAD_SIZE), 1) // HEAD_SIZE
    scale = 1.0 / math.sqrt(HEAD_SIZE)
    arrived = own[...] + got[...].astype(F32) + far[...].astype(F32)
    scaled, inverse = normalize(second[...])
    vectors[0:1, :] = jnp.sum(arrived * scaled, 0, keepdims=True)
    vectors[1:2, :] = jnp.sum(arrived, 0, keepdims=True)
    two = grad[...].astype(F32) + norm_backward(arrived, scaled, inverse, norms[4:5, :])
    low = two.astype(BF16)
    grad_two[...] = low
    for b, ref in enumerate((o0, o1, o2, o3)):
        crossed_grad[:, b * part : (b + 1) * part] = dot_nt(low, ref[...]).astype(BF16)
    for p in range(width // (2 * HEAD_SIZE)):
        cols = slice(p * 2 * HEAD_SIZE, (p + 1) * 2 * HEAD_SIZE)
        q, k, v = queries[:, cols], pair_cols(kv, p, key_rows), pair_cols(kv, p, value_rows)
        g_rows = crossed_grad[:, cols]
        found = []
        for g in (0, 1):
            probs = head_weights(q, k, lanes, g)
            change = dot_nt(jnp.where(lanes == g, g_rows, jnp.zeros_like(g_rows)), v)
            delta = jnp.sum(change * probs, -1, keepdims=True)
            ds = (probs * (change - delta)).astype(BF16)
            found.append((dot_nn(ds, k), dot_tn(ds, q), dot_tn(probs.astype(BF16), g_rows)))
        query_grad[:, cols] = (
            jnp.where(lanes == 0, found[0][0], found[1][0]) * scale
        ).astype(BF16)
        kv_grad[:context_rows, cols] = (
            jnp.where(lane_k == 0, found[0][1], found[1][1]) * scale
        ).astype(BF16)
        kv_grad[context_rows:, cols] = jnp.where(lane_k == 0, found[0][2], found[1][2]).astype(
            BF16
        )
    back = jnp.zeros(grad.shape, F32)
    for b, ref in enumerate((q0, q1, q2, q3)):
        back = back + dot_nt(query_grad[:, b * part : (b + 1) * part], ref[...])
    scaled, inverse = normalize(first[...])
    vectors[2:3, :] = jnp.sum(back * scaled, 0, keepdims=True)
    vectors[3:4, :] = jnp.sum(back, 0, keepdims=True)
    grad_one[...] = (two + norm_backward(back, scaled, inverse, norms[2:3, :])).astype(BF16)


def cross_backward(own, got, far, grad, first, second, norms, query_parts, kv_parts, out_parts,
                   queries):
    rows, width = own.shape
    low = lambda r: jax.ShapeDtypeStruct((r, width), BF16)
    block = pl.BlockSpec((rows, width), lambda i: (0, 0))
    return pl.pallas_call(
        cross_backward_body,
        grid=(1,),
        out_shape=[low(rows), low(rows), low(kv_parts[0].shape[0]),
                   jax.ShapeDtypeStruct((4, width), F32), low(rows)],
        in_specs=[block] * 6 + [pl.BlockSpec(memory_space=pltpu.VMEM)] * 14,
        scratch_shapes=[pltpu.VMEM((rows, width), BF16)],
        cost_estimate=FREE, name="cross_back",
    )(own, got, far, grad, first, second, norms, *query_parts, *kv_parts, *out_parts, queries)


def meet_body(left, left_pair, right, right_pair, out):
    out[...] = (
        dot_nn(left[...], right[...]) + dot_nn(left_pair[...], right_pair[...])
    ).astype(BF16)


def meet(rows, cols):
    count, size = rows[0].shape
    width = cols[0].shape[1]
    tile = width // 3
    left = pl.BlockSpec((count, size), lambda i: (0, 0))
    right = pl.BlockSpec((size, tile), lambda i: (0, i))
    return pl.pallas_call(
        meet_body,
        grid=(3,),
        in_specs=[left, left, right, right],
        out_specs=pl.BlockSpec((count, tile), lambda i: (0, i)),
        out_shape=jax.ShapeDtypeStruct((count, width), BF16),
        name="meet", cost_estimate=FREE,
    )(*rows, *cols)


def down_body(hidden, down_w, away, own, low):
    share = own.shape[0]

    def sent(r):
        return dot_nn(hidden[r * share : (r + 1) * share, :], down_w[...])

    away[:share, :] = sent(1).astype(BF16)
    away[share:, :] = sent(3).astype(BF16)
    low[...] = sent(2).astype(BF16)
    own[...] = sent(0)


def down_parts(hidden, down_w):
    share, width = hidden.shape[0] // 4, down_w.shape[1]
    low = lambda *dims: jax.ShapeDtypeStruct(dims, BF16)
    return pl.pallas_call(
        down_body,
        out_shape=[low(2 * share, width), jax.ShapeDtypeStruct((share, width), F32),
                   low(share, width)],
        name="down", cost_estimate=FREE,
    )(hidden, down_w)


def bundle_body(devices, place, f0, f1, f2, f3, b0, b1, b2, b3, a0, a1, a2, a3, attended,
                context, kv, out):
    width = a0.shape[1]
    part, share = width // 4, a0.shape[0]
    own = lambda refs: jnp.concatenate(
        [ref[:, width + r * part : width + (r + 1) * part] for r, ref in enumerate(refs)], 0
    )
    full = lambda refs: jnp.concatenate([ref[:, :width] for ref in refs], 0)
    fronts, backs = (f0, f1, f2, f3), (b0, b1, b2, b3)
    rows = width // devices
    small = part // devices
    half = width // 2

    def put(block, base, left):
        for d in range(devices):
            at = slice(base, base + block.shape[0] // devices)
            piece = block[d * block.shape[0] // devices : (d + 1) * block.shape[0] // devices, :]
            out[d, at, left : left + block.shape[1]] = piece.astype(BF16)

    put(dot_tn(full(fronts), own(backs)), 0, 0)
    count = context.shape[0]
    put(dot_tn(context[...], kv[:count, :]), 0, part)
    put(dot_tn(context[...], kv[count:, :]), rows // 2, part)
    grads = dot_tn(own(fronts), full(backs))
    put(grads[:, :half], 0, half)
    put(grads[:, half:], small, half)
    grads = sum(
        dot_nn(attended[:, relative(place[0], r, share)], ref[...])
        for r, ref in enumerate((a0, a1, a2, a3))
    )
    put(grads[:, :half], 2 * small, half)
    put(grads[:, half:], 3 * small, half)


def bundle_grads(devices, place, fronts, backs, ones, attended, context, kv):
    width = ones[0].shape[1]
    vmem = pl.BlockSpec(memory_space=pltpu.VMEM)
    return pl.pallas_call(
        functools.partial(bundle_body, devices),
        in_specs=[pl.BlockSpec(memory_space=pltpu.SMEM)] + [vmem] * 15,
        out_specs=vmem,
        out_shape=jax.ShapeDtypeStruct((devices, width // devices, width), BF16),
        name="bundle", cost_estimate=FREE,
    )(place, *fronts, *backs, *ones, attended, context, kv)


def front_body(width_block, place, x0, x1, x2, x3, g0, g1, g2, g3, cosine, sine, wq, wk, wv,
               queries, pair, rows, low, nrm_own, nrm_away, norms, means, inverses, wide):
    size, part = x0.shape
    for r, (x, g) in enumerate(((x0, g0), (x1, g1), (x2, g2), (x3, g3))):
        start = pl.multiple_of((place[0] ^ r) * part, 128)
        wide[:, pl.ds(start, part)] = x[...]
        norms[:, pl.ds(start, part)] = g[...]
    share = size // 4
    rows[...] = wide[pl.ds(pl.multiple_of(place[0] * share, share), share), :]
    values = wide[...].astype(F32)
    mean = jnp.mean(values, -1, keepdims=True)
    centred = values - mean
    inverse = lax.rsqrt(jnp.mean(centred * centred, -1, keepdims=True) + 1e-05)
    means[...] = mean
    inverses[...] = inverse
    normed = (centred * inverse * norms[0:1, :] + norms[1:2, :]).astype(BF16)
    low[...] = normed
    half = HEAD_SIZE // 2

    def turned(weight):
        return dot_nn(normed, weight[...]).T

    def rotated(block, dest, scale):
        for h in range(part // HEAD_SIZE):
            a = block[h * HEAD_SIZE : h * HEAD_SIZE + half, :]
            b = block[h * HEAD_SIZE + half : (h + 1) * HEAD_SIZE, :]
            dest[h * HEAD_SIZE : h * HEAD_SIZE + half, :] = (
                (a * cosine[...] - b * sine[...]) * scale
            ).astype(BF16)
            dest[h * HEAD_SIZE + half : (h + 1) * HEAD_SIZE, :] = (
                (b * cosine[...] + a * sine[...]) * scale
            ).astype(BF16)

    rotated(turned(wk), pair.at[0], 1.0)
    pair[1] = turned(wv).astype(BF16)
    rotated(turned(wq), queries, 1.0 / math.sqrt(HEAD_SIZE))
    deal_rows(normed.T, width_block, place[1], nrm_own, nrm_away)


def front(devices, place, parts, norm_parts, tables, wq, wk, wv):
    size, part = parts[0].shape
    width = 4 * part
    low = lambda *s: jax.ShapeDtypeStruct(s, BF16)
    wide = lambda *s: jax.ShapeDtypeStruct(s, F32)
    vmem = pl.BlockSpec(memory_space=pltpu.VMEM)
    return pl.pallas_call(
        functools.partial(front_body, width // devices),
        in_specs=[pl.BlockSpec(memory_space=pltpu.SMEM)] + [vmem] * 13,
        out_specs=[vmem] * 9,
        out_shape=[low(part, size), low(2, part, size), low(size // 4, width), low(size, width),
                   low(width // 2, size), low(width // 2, size), wide(6, width),
                   wide(size, 1), wide(size, 1)],
        scratch_shapes=[pltpu.VMEM((size, width), BF16)],
        cost_estimate=FREE, name="front",
    )(place, *parts, *norm_parts, *tables, wq, wk, wv)


def per_device(
    frames,
    segment,
    time_token,
    context,
    gain_attn,
    bias_attn,
    gain_cross,
    bias_cross,
    gain_ffn,
    bias_ffn,
    w_query,
    w_key,
    w_value,
    w_out,
    c_query,
    c_key,
    c_value,
    c_out,
    w_gate,
    w_up,
    w_down,
    out_grad,
):
    local_rows = frames.shape[0]
    local_width = frames.shape[1]
    model_width = w_query.shape[0]
    head_cols = w_query.shape[1]
    heads = head_cols // HEAD_SIZE
    number_of_frames = lax.axis_size("seq") * local_rows
    row_length = min(max(ROW_MIN, 64 * lax.axis_size("seq")), number_of_frames)
    first_frame = lax.axis_index("seq") * local_rows
    own_start = lax.axis_index("tensor") * local_width

    def own_cols(value):
        return lax.dynamic_slice_in_dim(value, own_start, local_width, value.ndim - 1)

    place = lax.axis_index("tensor")
    share = local_rows // 4

    def row_block(value, index):
        return rows_of(value, index * share, share)

    column = lax.axis_index("seq") % 2
    frame_parts_near = gather_near(frames)
    norm_parts = gather_near(
        jnp.stack([gain_attn, bias_attn, gain_cross, bias_cross, gain_ffn, bias_ffn])
    )
    clip_starts, frame_positions = frame_clip_labels(segment, row_length)
    own_labels = lax.dynamic_slice_in_dim(clip_starts, first_frame, local_rows)
    own_positions = lax.dynamic_slice_in_dim(frame_positions, first_frame, local_rows)
    blanks = jnp.full((local_rows,), -1, jnp.int32)
    key_labels = lax.dynamic_slice_in_dim(
        jnp.concatenate([blanks, clip_starts, blanks]), first_frame, 3 * local_rows
    )
    spans = jnp.concatenate(
        [tile_ranges(own_labels, key_labels), place.astype(jnp.int32).reshape(1)]
    )
    places = jnp.stack([column, place]).astype(jnp.int32)
    label_row, label_column = own_labels[None, :], key_labels[:, None]
    row_index = first_frame // row_length
    time_row = lax.dynamic_slice_in_dim(time_token, row_index, 1, 0).astype(F32)
    row_context = lax.dynamic_slice_in_dim(context, row_index, 1, 0)[0]
    context_rows = row_context.shape[0]
    tables = rotary_tables(own_positions)
    score_scale = 1.0 / math.sqrt(HEAD_SIZE)
    all_heads = model_width // HEAD_SIZE

    (
        queries, both, frame_rows, frame_normed, one_own_half, one_away_half, norms, means_one,
        inverse_one,
    ) = front(
        lax.axis_size("seq"), jnp.flip(places), frame_parts_near, norm_parts, tables, w_query,
        w_key, w_value,
    )
    own_keys, own_values = both[0], both[1]
    gain_one, bias_one = norms[0:1], norms[1:2]
    behind, ahead = shift(both, "seq", 1), shift(both, "seq", -1)
    out_pair = trade(out_grad, frame_parts_near[2], both)
    query_far = swap(after(c_query, frame_parts_near[3]), "tensor", 2)
    out_far = swap(after(c_out, frame_parts_near[3]), "tensor", 2)
    time_late = after(time_row, both)
    scaled_time, _ = normalize(time_late)
    time_normed = (scaled_time * gain_one + bias_one).astype(BF16)
    time_keys = by_feature(time_normed, w_key).astype(BF16).astype(F32)
    time_values = by_feature(time_normed, w_value).astype(BF16).astype(F32)
    context_late = after(row_context, both)
    context_kv = jnp.concatenate(
        [product(context_late, c_key), product(context_late, c_value)], 0
    ).astype(BF16)
    behind, ahead, query_far, out_far = lax.optimization_barrier(
        (behind, ahead, query_far, out_far)
    )
    keys = (behind[0], own_keys, ahead[0])
    values = (behind[1], own_values, ahead[1])
    attended, log_totals, one_away, one_own, one_low = attend(
        spans, queries, keys, values, time_keys, time_values, label_row, label_column, w_out
    )
    kv_parts = gather_staged(context_kv, both, attended)
    query_parts = (
        c_query, swap(after(c_query, both), "tensor", 1), query_far, swap(query_far, "tensor", 1)
    )
    out_parts = (c_out, swap(after(c_out, both), "tensor", 1), out_far, swap(out_far, "tensor", 1))
    one_got, _, one_far = scatter_near(one_away, one_low)
    (
        normed_two, cross_queries, crossed, residual_one, residual_two, normed_share, flip_own,
        flip_away,
    ) = cross_forward(
        lax.axis_size("seq"), places, frame_rows, one_own, one_got, one_far, norms,
        query_parts, kv_parts, out_parts,
    )
    normed_share, normed_got = meeting(
        normed_share, swap(after(one_away_half, attended), "seq", 1)
    )
    flip_got = swap(flip_away, "seq", 1)
    *three_parts, flip_got = meeting(*gather_near(normed_share), flip_got)
    flip_both = jnp.stack([flip_own, flip_got])
    flip_far = swap(flip_both, "tensor", 2)
    grad_parts = gather_staged(jnp.stack([out_grad, out_pair]), one_far, normed_share)
    (
        hidden, hidden_own, hidden_away, gate_grad, lifted_grad, three_away, three_own, three_low,
        grad_near, grad_pair,
    ) = ffn(lax.axis_size("seq"), places, three_parts, grad_parts, w_gate, w_up, w_down)
    three_away, three_low, flip_far = meeting(three_away, three_low, flip_far)
    three_got, _, three_far = scatter_near(three_away, three_low)
    hidden_got = swap(hidden_away, "seq", 1)
    flip_late, flip_far_late, gate_late, front_late = after(
        (flip_both, flip_far, gate_grad, jnp.concatenate([normed_two, crossed], 1)), three_far
    )
    flip_mate, flip_far_mate = swap(flip_late, "tensor", 1), swap(flip_far_late, "tensor", 1)
    gate_got = swap(gate_late, "seq", 1)
    front_far = swap(front_late, "tensor", 2)
    cross_full, cross_query_grad, kv_grad, norm_vectors, grad_one = cross_backward(
        three_own, three_got, three_far, grad_near, residual_one, residual_two, norms,
        query_parts, kv_parts, out_parts, cross_queries,
    )
    grad_one, hidden_got, flip_mate, flip_far_mate, front_far = meeting(
        grad_one, hidden_got, flip_mate, flip_far_mate, front_far
    )
    count = lax.axis_size("seq")

    def by_level(blocks):
        return blocks.reshape(count // 2, 2 * blocks.shape[0] // count, blocks.shape[1])

    down_keep, down_got = halve(
        by_level(meet((hidden_own, hidden_got), (grad_near, grad_pair))), 1
    )
    one_parts = gather_near(grad_one)
    back_late, lifted_late = after(
        (jnp.concatenate([cross_full, cross_query_grad], 1), lifted_grad), one_parts[3]
    )
    back_far = swap(back_late, "tensor", 2)
    lifted_got = swap(lifted_late, "seq", 1)
    query_grad, to_prev, kept, to_next, time_key_grad, time_value_grad = attend_back(
        spans, queries, keys, values, time_keys, time_values, label_row, label_column, w_out,
        attended, log_totals, one_parts,
    )
    to_prev, to_next, back_far, gate_got, down_got = meeting(
        to_prev, to_next, back_far, gate_got, down_got
    )
    from_next, from_prev = shift(to_prev, "seq", -1), shift(to_next, "seq", 1)
    down_keep, down_got = halve(added(down_keep, down_got).astype(BF16), 2)
    three_pair = [
        jnp.concatenate([value[i] for value in (flip_both, flip_mate, flip_far, flip_far_mate)], 1)
        for i in (0, 1)
    ]
    gate_keep, gate_cross = halve(by_level(meet(three_pair, (gate_grad, gate_got))), 1)
    down_away, down_own, down_low = down_parts(after(hidden, to_prev), w_down)
    from_next, from_prev, down_got, lifted_got = meeting(
        from_next, from_prev, down_got, lifted_got
    )
    raw, last_away, last_own, last_low = tail(
        places[1:], query_grad, kept, from_next, from_prev, tables, w_query, w_key, w_value
    )
    last_away, last_low, gate_cross = meeting(last_away, last_low, gate_cross)
    last_got, last_sum, last_far = scatter_near(last_away, last_low)
    frame_grad = last_own + last_got[:local_rows].astype(F32) + last_far.astype(F32)

    def to_frames(rows, weight):
        return jnp.einsum("fn,df->nd", rows, weight, preferred_element_type=F32)

    time_key_grad, time_value_grad = after((time_key_grad, time_value_grad), from_next)
    time_grad = to_frames(time_key_grad.astype(BF16), w_key) + to_frames(
        time_value_grad.astype(BF16), w_value
    )
    own_scaled = (frames.astype(F32) - means_one) * inverse_one
    scaled_grad = frame_grad * gain_attn[None]
    sums = jnp.concatenate(
        [
            jnp.sum(scaled_grad, -1),
            jnp.sum(scaled_grad * own_scaled, -1),
            time_grad[0],
            norm_vectors.reshape(-1),
        ]
    )[None]
    sums = sums + swap(sums, "tensor", 1)
    sums = sums + swap(sums, "tensor", 2)
    plain = sums[0, :local_rows, None] / model_width
    cross = sums[0, local_rows : 2 * local_rows, None] / model_width
    vectors = own_cols(sums[0, 2 * local_rows :].reshape(5, model_width))
    attend_full = ordered(*[after(one_parts, from_next)[i] for i in (0, 2, 1, 3)], 0)
    d_frames = own_cols(attend_full).astype(F32) + inverse_one * (
        scaled_grad - plain - own_scaled * cross
    )
    d_gain_attn = jnp.sum(frame_grad * own_scaled, 0) + vectors[0] * own_cols(scaled_time)[0]
    d_bias_attn = jnp.sum(frame_grad, 0) + vectors[0]
    small = reduce_small(
        jnp.stack([d_gain_attn, d_bias_attn, vectors[3], vectors[4], vectors[1], vectors[2]])
    )

    down_away, down_low = after((down_away, down_low), from_next)
    branch_got, _, branch_far = scatter_near(down_away, down_low)
    block_rows = (
        residual_two + down_own + branch_got[:share].astype(F32) + branch_far.astype(F32)
    ).astype(BF16)
    block_cols = rows_to_cols(
        *[
            lax.dynamic_slice_in_dim(block_rows, (place ^ r) * local_width, local_width, 1)
            for r in range(4)
        ],
        from_next,
    )
    block_out = jnp.concatenate([row_block(block_cols, place ^ b) for b in range(4)], 0)

    context_parts = quarters(after(kv_grad, from_next), 1)
    kv_got, _, kv_far = scatter_near(
        jnp.concatenate([context_parts[1], context_parts[3]], 0), context_parts[2]
    )
    context_own = (
        context_parts[0].astype(F32)
        + kv_got[: kv_far.shape[0]].astype(F32)
        + kv_far.astype(F32)
    )
    def spread(own, far):
        own_late, far_late = after((own, far), from_next)
        return own, swap(own_late, "tensor", 1), far, swap(far_late, "tensor", 1)

    forward_near = spread(front_late, front_far)
    back_near = spread(back_late, back_far)
    time_column = time_normed.astype(F32).T

    normed_pair = (one_own_half, normed_got)
    grad_down = halve_end(down_keep, down_got, 3)
    grad_gate_w = halve_end(gate_keep, gate_cross, 2)
    up_blocks = by_level(meet(three_pair, (lifted_grad, lifted_got)))
    grad_up_w = halve_all(up_blocks, 1)
    bundle = bundle_grads(
        count, places[1:], forward_near, back_near, one_parts, attended, row_context,
        context_own.astype(BF16),
    )
    middle = halve_all(bundle, 0)
    part, rows, half = head_cols // count, model_width // count, model_width // 2
    grad_c_query = middle[:, :head_cols]
    grad_c_key = middle[: rows // 2, head_cols:half]
    grad_c_value = middle[rows // 2 :, head_cols:half]
    grad_c_out = jnp.concatenate([middle[:part, half:], middle[part : 2 * part, half:]], 1)
    grad_w_out = jnp.concatenate(
        [middle[2 * part : 3 * part, half:], middle[3 * part :, half:]], 1
    )

    raw_pair = (raw, swap(raw, "seq", 1))
    time_both = jnp.concatenate([time_key_grad, time_value_grad], 0)
    time_both = time_both + swap(after(time_both, from_next), "seq", 1)
    own_time_rows = lax.dynamic_index_in_dim(
        time_column.reshape(count // 2, 2, -1), column, 1, False
    ).reshape(-1, 1)
    outer = own_time_rows * jnp.concatenate([jnp.zeros((head_cols, 1), F32), time_both], 0).T
    blocks = sum(
        jnp.einsum("dn,fn->df", r, c, preferred_element_type=F32)
        for r, c in zip(normed_pair, raw_pair)
    )
    blocks = by_level((blocks + outer).astype(BF16))
    heads_sum = halve_all(blocks, 1)
    grad_w_query, grad_w_key, grad_w_value = (
        heads_sum[:, i * head_cols : (i + 1) * head_cols] for i in range(3)
    )
    return (
        block_out,
        d_frames,
        small[0],
        small[1],
        small[2],
        small[3],
        small[4],
        small[5],
        grad_w_query,
        grad_w_key,
        grad_w_value,
        grad_w_out,
        grad_c_query,
        grad_c_key,
        grad_c_value,
        grad_c_out,
        grad_gate_w,
        grad_up_w,
        grad_down,
    )


def solution(mesh):
    return jax.shard_map(
        per_device,
        mesh=mesh,
        in_specs=(
            P("seq", "tensor"),
            P(),
            P(),
            P(),
            P("tensor"),
            P("tensor"),
            P("tensor"),
            P("tensor"),
            P("tensor"),
            P("tensor"),
            P(None, "tensor"),
            P(None, "tensor"),
            P(None, "tensor"),
            P("tensor", None),
            P(None, "tensor"),
            P(None, "tensor"),
            P(None, "tensor"),
            P("tensor", None),
            P(None, "tensor"),
            P(None, "tensor"),
            P("tensor", None),
            P("seq", "tensor"),
        ),
        out_specs=(
            P("seq", "tensor"),
            P("seq", "tensor"),
            P(("tensor", "seq")),
            P(("tensor", "seq")),
            P(("tensor", "seq")),
            P(("tensor", "seq")),
            P(("tensor", "seq")),
            P(("tensor", "seq")),
            P("seq", "tensor"),
            P("seq", "tensor"),
            P("seq", "tensor"),
            P(("tensor", "seq"), None),
            P("seq", "tensor"),
            P("seq", "tensor"),
            P("seq", "tensor"),
            P(("tensor", "seq"), None),
            P("seq", "tensor"),
            P("seq", "tensor"),
            P(("tensor", "seq"), None),
        ),
        check_vma=False,
    )
```

```python
import functools
import math

import jax
import jax.numpy as jnp
from jax import lax
from jax.experimental import pallas as pl
from jax.experimental.pallas import tpu as pltpu
from jax.sharding import PartitionSpec as P

HEAD_SIZE = 64
ROW_MIN = 2048
TILE = 256
BF16 = jnp.bfloat16
F32 = jnp.float32


def meeting(*values):
    return lax.optimization_barrier(values)


def after(value, token):
    return lax.optimization_barrier((value, token))[0]


def swap(value, axis, by):
    return lax.ppermute(value, axis, [(i, i ^ by) for i in range(lax.axis_size(axis))])


def shift(value, axis, by):
    peers = lax.axis_size(axis)
    pairs = [(i, i + by) for i in range(peers) if 0 <= i + by < peers]
    return lax.ppermute(value, axis, pairs)


def tensor_place():
    place = lax.axis_index("tensor")
    return place // 2, place % 2


def ordered(own, far, mate, far_mate, axis):
    side, core = tensor_place()
    near = (jnp.where(core == 0, own, mate), jnp.where(core == 0, mate, own))
    away = (jnp.where(core == 0, far, far_mate), jnp.where(core == 0, far_mate, far))
    low = [jnp.where(side == 0, n, a) for n, a in zip(near, away)]
    high = [jnp.where(side == 0, a, n) for n, a in zip(near, away)]
    return jnp.concatenate(low + high, axis)


def gather_near(own):
    far = swap(own, "tensor", 2)
    return own, swap(own, "tensor", 1), far, swap(far, "tensor", 1)


def gather_staged(own, first, second):
    far = swap(after(own, first), "tensor", 2)
    far, late = after((far, own), second)
    return own, swap(late, "tensor", 1), far, swap(far, "tensor", 1)


def gather(own, axis):
    own, mate, far, far_mate = gather_near(own)
    return ordered(own, far, mate, far_mate, axis)


def scatter_near(away, low):
    got = swap(away, "tensor", 1)
    total = (low.astype(F32) + got[low.shape[0] :].astype(F32)).astype(BF16)
    return got, total, swap(total, "tensor", 2)


def rows_to_cols(own, mate, far, far_mate, later):
    width = own.shape[1]
    got = after(swap(jnp.concatenate([far, far_mate], 1), "tensor", 2), later)
    other = swap(jnp.concatenate([mate, got[:, width:]], 0), "tensor", 1)
    size = own.shape[0]
    return jnp.concatenate([own, other[:size], got[:, :width], other[size:]], 0)


def quarters(value, axis):
    return jnp.split(value, 4, axis)


def own_blocks(near):
    return jnp.concatenate([quarters(value, 1)[r] for r, value in enumerate(near)], 0)


def trade(value, start, done):
    return after(swap(after(value, start), "seq", 1), done)


def halve(blocks, bit):
    count, rows, cols = blocks.shape
    side = (lax.axis_index("seq") >> bit) % 2
    parts = blocks.reshape(count // 2, 2, rows, cols)
    send = lax.dynamic_index_in_dim(parts, 1 - side, 1, False)
    keep = lax.dynamic_index_in_dim(parts, side, 1, False)
    return keep, swap(send, "seq", 1 << bit)


def added(keep, got):
    return keep.astype(F32) + got.astype(F32)


def halve_all(blocks, bit):
    while blocks.shape[0] > 1:
        blocks = added(*halve(blocks.astype(BF16), bit))
        bit += 1
    return blocks[0].astype(F32)


def halve_end(keep, got, bit):
    return halve_all(added(keep, got), bit)


def reduce_small(vectors):
    count = lax.axis_size("seq")
    kinds, width = vectors.shape
    parts = vectors.reshape(kinds, count, width // count).transpose(1, 0, 2)
    bit = 0
    while parts.shape[0] > 1:
        parts = added(*halve(parts, bit))
        bit += 1
    return parts[0]


def frame_clip_labels(segment, row_length):
    frame_index = jnp.arange(segment.shape[0], dtype=jnp.int32)
    border = (frame_index % row_length == 0) | (segment != jnp.roll(segment, 1))
    clip_starts = lax.cummax(jnp.where(border, frame_index, 0), axis=0)
    return (clip_starts, (frame_index - clip_starts + 1).astype(jnp.float32))


def tile_ranges(q_labels, key_labels):
    q = q_labels.reshape(-1, TILE)
    k = key_labels.reshape(-1, TILE)
    meets = (k[None, :, 0] <= q[:, None, -1]) & (k[None, :, -1] >= q[:, None, 0])
    index = jnp.arange(k.shape[0], dtype=jnp.int32)[None]
    low = jnp.min(jnp.where(meets, index, k.shape[0]), 1)
    high = jnp.max(jnp.where(meets, index + 1, 0), 1)
    return jnp.stack([low, high], 1).reshape(-1)

def head_rows(g):
    return slice(g * HEAD_SIZE, (g + 1) * HEAD_SIZE)

def fill_natural(dest, refs):
    size = refs[0].shape[1]
    for part, ref in enumerate(refs):
        dest[part * size : (part + 1) * size, :] = ref[...].T

def relative(place, r, size):
    return pl.ds(pl.multiple_of((place ^ r) * size, size), size)


def forward_body(span, q, k0, k1, k2, v0, v1, v2, tk, tv, qlab, klab, w_out,
                 out, lse, away, own, low, keys, vals):
    rows, size = q.shape
    group = rows // HEAD_SIZE
    pieces = size // TILE
    fill_natural(keys, (k0, k1, k2))
    for part, ref in enumerate((v0, v1, v2)):
        for piece in range(pieces):
            vals[part * pieces + piece] = ref[:, piece * TILE : (piece + 1) * TILE]
    for tile in range(pieces):
        cols = slice(tile * TILE, (tile + 1) * TILE)
        lab = qlab[:, cols]
        state = []
        for g in range(group):
            part = q[head_rows(g), cols].astype(F32)
            top = jnp.sum(part * tk[head_rows(g), :], 0, keepdims=True)
            state += [
                top,
                jnp.ones_like(top),
                jnp.broadcast_to(tv[head_rows(g), :], (HEAD_SIZE, TILE)),
            ]

        def step(j, state):
            start = pl.multiple_of(j * TILE, TILE)
            seen = klab[pl.ds(start, TILE), :] == lab
            fresh = []
            for g in range(group):
                top, total, acc = state[3 * g : 3 * g + 3]
                s = dot_nn(keys[pl.ds(start, TILE), head_rows(g)], q[head_rows(g), cols])
                s = jnp.where(seen, s, -1e30)
                new = jnp.maximum(top, jnp.max(s, 0, keepdims=True))
                fade = jnp.exp(top - new)
                p = jnp.exp(s - new)
                total = total * fade + jnp.sum(p, 0, keepdims=True)
                acc = acc * fade + dot_nn(vals[j, head_rows(g), :], p.astype(BF16))
                fresh += [new, total, acc]
            return tuple(fresh)

        state = lax.fori_loop(span[2 * tile], span[2 * tile + 1], step, tuple(state))
        for g in range(group):
            top, total, acc = state[3 * g : 3 * g + 3]
            out[head_rows(g), cols] = (acc / total).astype(BF16)
            lse[g : g + 1, cols] = top + jnp.log(total)
    place = span[2 * pieces]
    share = own.shape[0]

    def sent(r):
        return dot_tn(out[:, relative(place, r, share)], w_out[...])

    away[:share, :] = sent(1).astype(BF16)
    away[share:, :] = sent(3).astype(BF16)
    low[...] = sent(2).astype(BF16)
    own[...] = sent(0)


def backward_body(span, q, k0, k1, k2, v0, v1, v2, tk, tv, qlab, klab, w_out, out, lse,
                  g0, g1, g2, g3, dq, to_prev, kept, to_next, dtk, dtv,
                  og, keys, vals, tkeys, ak, av):
    rows, size = q.shape
    group = rows // HEAD_SIZE
    pieces = size // TILE
    share = g0.shape[0]
    for r, ref in enumerate((g0, g1, g2, g3)):
        og[:, relative(span[2 * pieces], r, share)] = dot_nt(w_out[...], ref[...]).astype(BF16)
    fill_natural(keys, (k0, k1, k2))
    fill_natural(vals, (v0, v1, v2))
    for part, ref in enumerate((k0, k1, k2)):
        for piece in range(pieces):
            tkeys[part * pieces + piece] = ref[:, piece * TILE : (piece + 1) * TILE]
    ak[...] = jnp.zeros_like(ak)
    av[...] = jnp.zeros_like(av)
    for tile in range(pieces):
        cols = slice(tile * TILE, (tile + 1) * TILE)
        lab = qlab[:, cols]
        state, norms, deltas = [], [], []
        for g in range(group):
            hr = head_rows(g)
            qf = q[hr, cols].astype(F32)
            gf = og[hr, cols].astype(F32)
            norm = lse[g : g + 1, cols]
            delta = jnp.sum(gf * out[hr, cols].astype(F32), 0, keepdims=True)
            pt = jnp.exp(jnp.sum(qf * tk[hr, :], 0, keepdims=True) - norm)
            st = pt * (jnp.sum(gf * tv[hr, :], 0, keepdims=True) - delta)
            gk = jnp.sum(qf * st, 1, keepdims=True)
            gv = jnp.sum(gf * pt, 1, keepdims=True)
            if tile == 0:
                dtk[hr, :] = gk
                dtv[hr, :] = gv
            else:
                dtk[hr, :] += gk
                dtv[hr, :] += gv
            state.append(tk[hr, :] * st)
            norms.append(norm)
            deltas.append(delta)

        def step(j, state):
            start = pl.multiple_of(j * TILE, TILE)
            seen = klab[pl.ds(start, TILE), :] == lab
            fresh = []
            for g in range(group):
                hr = head_rows(g)
                s = dot_nn(keys[pl.ds(start, TILE), hr], q[hr, cols])
                p = jnp.exp(jnp.where(seen, s, -1e30) - norms[g])
                m = dot_nn(vals[pl.ds(start, TILE), hr], og[hr, cols])
                ds = (p * (m - deltas[g])).astype(BF16)
                av[j, hr, :] += dot_nt(og[hr, cols], p.astype(BF16))
                ak[j, hr, :] += dot_nt(q[hr, cols], ds)
                fresh.append(state[g] + dot_nn(tkeys[j, hr, :], ds))
            return tuple(fresh)

        state = lax.fori_loop(span[2 * tile], span[2 * tile + 1], step, tuple(state))
        for g in range(group):
            dq[head_rows(g), cols] = state[g]
    for part, dest in enumerate((to_prev, kept, to_next)):
        for piece in range(pieces):
            at = slice(piece * TILE, (piece + 1) * TILE)
            dest[0, :, at] = ak[part * pieces + piece].astype(dest.dtype)
            dest[1, :, at] = av[part * pieces + piece].astype(dest.dtype)


def attend(span, q, ks, vs, tk, tv, qlab, klab, w_out):
    cols, size = q.shape
    share, width = size // 4, w_out.shape[1]
    tiles = 3 * size // TILE
    low = lambda *dims: jax.ShapeDtypeStruct(dims, BF16)
    wide = lambda *dims: jax.ShapeDtypeStruct(dims, F32)
    vmem = pl.BlockSpec(memory_space=pltpu.VMEM)
    return pl.pallas_call(
        forward_body,
        in_specs=[pl.BlockSpec(memory_space=pltpu.SMEM)] + [vmem] * 12,
        out_specs=[vmem] * 5,
        out_shape=[low(cols, size), wide(cols // HEAD_SIZE, size), low(2 * share, width),
                   wide(share, width), low(share, width)],
        scratch_shapes=[pltpu.VMEM((3 * size, cols), BF16), pltpu.VMEM((tiles, cols, TILE), BF16)],
        name="attend", cost_estimate=FREE,
    )(span, q, *ks, *vs, tk, tv, qlab, klab, w_out)


def attend_back(span, q, ks, vs, tk, tv, qlab, klab, w_out, out, lse, grads):
    cols, size = q.shape
    tiles = 3 * size // TILE
    low = lambda *dims: jax.ShapeDtypeStruct(dims, BF16)
    wide = lambda *dims: jax.ShapeDtypeStruct(dims, F32)
    vmem = pl.BlockSpec(memory_space=pltpu.VMEM)
    return pl.pallas_call(
        backward_body,
        in_specs=[pl.BlockSpec(memory_space=pltpu.SMEM)] + [vmem] * 18,
        out_specs=[vmem] * 6,
        out_shape=[wide(cols, size), low(2, cols, size), wide(2, cols, size), low(2, cols, size),
                   wide(cols, 1), wide(cols, 1)],
        scratch_shapes=[pltpu.VMEM((cols, size), BF16), pltpu.VMEM((3 * size, cols), BF16),
                        pltpu.VMEM((3 * size, cols), BF16), pltpu.VMEM((tiles, cols, TILE), BF16),
                        pltpu.VMEM((tiles, cols, TILE), F32), pltpu.VMEM((tiles, cols, TILE), F32)],
        name="attend_back", cost_estimate=FREE,
    )(span, q, *ks, *vs, tk, tv, qlab, klab, w_out, out, lse, *grads)


def tail_body(place, dq, kept, ahead, behind, cosine, sine, wq, wk, wv, raw, away, own, low, flipped):
    part, size = dq.shape
    half = HEAD_SIZE // 2

    def returned(block, base, scale):
        for h in range(part // HEAD_SIZE):
            a = block[h * HEAD_SIZE : h * HEAD_SIZE + half, :]
            b = block[h * HEAD_SIZE + half : (h + 1) * HEAD_SIZE, :]
            at = base + h * HEAD_SIZE
            raw[at : at + half, :] = ((a * cosine[...] + b * sine[...]) * scale).astype(BF16)
            raw[at + half : at + HEAD_SIZE, :] = (
                (b * cosine[...] - a * sine[...]) * scale
            ).astype(BF16)

    def whole(index):
        return kept[index] + ahead[index].astype(F32) + behind[index].astype(F32)

    returned(dq[...], 0, 1.0 / math.sqrt(HEAD_SIZE))
    returned(whole(0), part, 1.0)
    raw[2 * part :, :] = whole(1).astype(BF16)
    flipped[...] = raw[...].T

    def sent(r):
        at = relative(place[0], r, part)
        return sum(
            dot_nt(flipped[:, i * part : (i + 1) * part], weight[at, :])
            for i, weight in enumerate((wq, wk, wv))
        )

    away[:size, :] = sent(1).astype(BF16)
    away[size:, :] = sent(3).astype(BF16)
    low[...] = sent(2).astype(BF16)
    own[...] = sent(0)


def tail(place, dq, kept, ahead, behind, tables, wq, wk, wv):
    part, size = dq.shape
    low = lambda *dims: jax.ShapeDtypeStruct(dims, BF16)
    vmem = pl.BlockSpec(memory_space=pltpu.VMEM)
    return pl.pallas_call(
        tail_body,
        in_specs=[pl.BlockSpec(memory_space=pltpu.SMEM)] + [vmem] * 9,
        out_specs=[vmem] * 4,
        out_shape=[low(3 * part, size), low(2 * size, part), jax.ShapeDtypeStruct((size, part), F32),
                   low(size, part)],
        scratch_shapes=[pltpu.VMEM((size, 3 * part), BF16)],
        name="tail", cost_estimate=FREE,
    )(place, dq, kept, ahead, behind, *tables, wq, wk, wv)


def rotary_tables(frame_positions):
    half_dim = HEAD_SIZE // 2
    frequency = jnp.exp(jnp.arange(half_dim, dtype=jnp.float32) * (-math.log(10000.0) / half_dim))
    angles = frequency[:, None] * frame_positions[None, :]
    return (jnp.cos(angles), jnp.sin(angles))


def rotate(rows, tables, sign=1.0):
    count, size = rows.shape
    halves = rows.reshape(count // HEAD_SIZE, 2, HEAD_SIZE // 2, size)
    cosine, sine = tables[0][None], tables[1][None] * sign
    first = halves[:, 0] * cosine - halves[:, 1] * sine
    second = halves[:, 1] * cosine + halves[:, 0] * sine
    return jnp.stack([first, second], 1).reshape(count, size)


def product(left, right):
    return jnp.dot(left, right, preferred_element_type=jnp.float32)


def inner_rows(left, right):
    return jnp.einsum("nd,nf->df", left, right, preferred_element_type=jnp.float32)


def back_project(gradient, weight):
    return jnp.einsum("nf,df->nd", gradient, weight, preferred_element_type=jnp.float32)


def by_feature(left, right):
    return jnp.einsum("nd,df->fn", left, right, preferred_element_type=jnp.float32)


def columns(weight, start, size):
    return lax.dynamic_slice_in_dim(weight, start, size, 1)


def rows_of(weight, start, size):
    return lax.dynamic_slice_in_dim(weight, start, size, 0)


def normalize(value_rows):
    means = jnp.mean(value_rows, -1, keepdims=True)
    centred = value_rows - means
    inverse = lax.rsqrt(jnp.mean(centred * centred, -1, keepdims=True) + 1e-05)
    return centred * inverse, inverse


def norm_backward(gradient, scaled, inverse, norm_gain):
    scaled_grad = gradient * norm_gain
    plain = jnp.mean(scaled_grad, -1, keepdims=True)
    cross = jnp.mean(scaled_grad * scaled, -1, keepdims=True)
    return inverse * (scaled_grad - plain - scaled * cross)


FREE = pl.CostEstimate(flops=1, transcendentals=0, bytes_accessed=1)


def dot_nn(left, right):
    return lax.dot_general(left, right, (((1,), (0,)), ((), ())), preferred_element_type=F32)


def dot_nt(left, right):
    return lax.dot_general(left, right, (((1,), (1,)), ((), ())), preferred_element_type=F32)


def dot_tn(left, right):
    return lax.dot_general(left, right, (((0,), (0,)), ((), ())), preferred_element_type=F32)


def head_weights(query, key, lanes, which):
    mine = jnp.where(lanes == which, query, jnp.zeros_like(query))
    scores = dot_nt(mine, key) * (1.0 / math.sqrt(HEAD_SIZE))
    weights = jnp.exp(scores - jnp.max(scores, -1, keepdims=True))
    return weights / jnp.sum(weights, -1, keepdims=True)


def pair_cols(refs, p, rows):
    ref = refs[p * 2 * HEAD_SIZE // refs[0].shape[1]]
    start = p * 2 * HEAD_SIZE % refs[0].shape[1]
    return ref[rows, start : start + 2 * HEAD_SIZE]


def cross_forward_body(width_block, place, rows, own, got, far, norms, q0, q1, q2, q3,
                       c0, c1, c2, c3, o0, o1, o2, o3,
                       front, queries, first, second, normed_three,
                       flip_own, flip_away):
    width = rows.shape[1]
    kv = (c0, c1, c2, c3)
    context_rows = c0.shape[0] // 2
    key_rows, value_rows = slice(0, context_rows), slice(context_rows, 2 * context_rows)
    lanes = lax.broadcasted_iota(jnp.int32, (rows.shape[0], 2 * HEAD_SIZE), 1) // HEAD_SIZE
    residual = (
        rows[...].astype(F32) + own[...] + got[...].astype(F32) + far[...].astype(F32)
    )
    first[...] = residual
    scaled, _ = normalize(residual)
    low = (scaled * norms[2:3, :] + norms[3:4, :]).astype(BF16)
    front[:, :width] = low
    part = width // 4
    for b, ref in enumerate((q0, q1, q2, q3)):
        queries[:, b * part : (b + 1) * part] = dot_nn(low, ref[...]).astype(BF16)
    for p in range(width // (2 * HEAD_SIZE)):
        cols = slice(p * 2 * HEAD_SIZE, (p + 1) * 2 * HEAD_SIZE)
        q, k, v = queries[:, cols], pair_cols(kv, p, key_rows), pair_cols(kv, p, value_rows)
        mixed = [dot_nn(head_weights(q, k, lanes, g).astype(BF16), v) for g in (0, 1)]
        front[:, width + cols.start : width + cols.stop] = jnp.where(lanes == 0, mixed[0], mixed[1]).astype(BF16)
    for b, ref in enumerate((o0, o1, o2, o3)):
        residual = residual + dot_nn(front[:, width + b * part : width + (b + 1) * part], ref[...])
    second[...] = residual
    scaled, _ = normalize(residual)
    low = (scaled * norms[4:5, :] + norms[5:6, :]).astype(BF16)
    normed_three[...] = low
    deal_rows(low.T, width_block, place[0], flip_own, flip_away)


def cross_forward(devices, place, rows, own, got, far, norms, query_parts, kv_parts, out_parts):
    size, width = rows.shape
    low = jax.ShapeDtypeStruct(rows.shape, BF16)
    both = jax.ShapeDtypeStruct((size, 2 * width), BF16)
    wide = jax.ShapeDtypeStruct(rows.shape, F32)
    flip = jax.ShapeDtypeStruct((width // 2, size), BF16)
    vmem = pl.BlockSpec(memory_space=pltpu.VMEM)
    block = pl.BlockSpec((size, width), lambda i: (0, 0))
    return pl.pallas_call(
        functools.partial(cross_forward_body, width // devices),
        grid=(1,),
        in_specs=[pl.BlockSpec(memory_space=pltpu.SMEM)] + [block] * 4 + [vmem] * 13,
        out_shape=[both, low, wide, wide, low, flip, flip],
        cost_estimate=FREE, name="cross",
    )(place, rows, own, got, far, norms, *query_parts, *kv_parts, *out_parts)


def deal_rows(rows, size, column, own, away):
    for b in range(rows.shape[0] // (2 * size)):
        at = slice(b * size, (b + 1) * size)
        even = rows[2 * b * size : (2 * b + 1) * size, :]
        odd = rows[(2 * b + 1) * size : (2 * b + 2) * size, :]

        @pl.when(column == 0)
        def _():
            own[at, :] = even
            away[at, :] = odd

        @pl.when(column != 0)
        def _():
            own[at, :] = odd
            away[at, :] = even


def ffn_part(normed, grad, gate_w, up_w, down_w, hidden, hid_own, hid_away, gate_grad, lifted_grad,
             unit_block, column):
    gate = dot_nn(normed, gate_w[...])
    lifted = dot_nn(normed, up_w[...])
    back = dot_nt(grad, down_w[...]).astype(BF16).astype(F32)
    sig = jax.nn.sigmoid(gate)
    swish = gate * sig
    made = (swish * lifted).astype(BF16)
    hidden[...] = made
    deal_rows(made.T, unit_block, column, hid_own, hid_away)
    gg = (back * lifted * sig * (1.0 + gate * (1.0 - sig))).astype(BF16)
    lg = (back * swish).astype(BF16)
    gate_grad[...] = gg
    lifted_grad[...] = lg
    return dot_nt(gg, gate_w[...]) + dot_nt(lg, up_w[...])


def ffn_first_body(unit_block, place, n0, n1, n2, n3, g0, g1, g2, g3, gate_w, up_w, down_w,
                   hidden, hid_own, hid_away, gate_grad, lifted_grad, normed, grad, grad_pair,
                   total):
    share, part = n0.shape[0], g0.shape[2]
    for b, ref in enumerate((n0, n1, n2, n3)):
        normed[b * share : (b + 1) * share, :] = ref[...]
    for c, ref in enumerate((g0, g1, g2, g3)):
        for b in range(4):
            rows, cols = relative(place[1], b, share), relative(place[1], c, part)
            grad[b * share : (b + 1) * share, cols] = ref[0, rows, :]
            grad_pair[b * share : (b + 1) * share, cols] = ref[1, rows, :]
    total[...] = ffn_part(
        normed[...], grad[...], gate_w, up_w, down_w, hidden, hid_own, hid_away, gate_grad,
        lifted_grad, unit_block, place[0],
    )


def ffn_second_body(unit_block, place, normed, grad, total, gate_w, up_w, down_w,
                    hidden, hid_own, hid_away, gate_grad, lifted_grad, away, own, low):
    share = own.shape[0]
    found = total[...] + ffn_part(
        normed[...], grad[...], gate_w, up_w, down_w, hidden, hid_own, hid_away, gate_grad,
        lifted_grad, unit_block, place[0],
    )
    own[...] = found[:share, :]
    low[...] = found[2 * share : 3 * share, :].astype(BF16)
    away[:share, :] = found[share : 2 * share, :].astype(BF16)
    away[share:, :] = found[3 * share :, :].astype(BF16)


def ffn(devices, place, half, inputs, gate_w, up_w, down_w):
    share = inputs[0].shape[0] if half == 0 else inputs[0].shape[0] // 4
    width = inputs[0].shape[1]
    size, units = 4 * share, gate_w.shape[1]
    tile = units // 2
    low = lambda *dims: jax.ShapeDtypeStruct(dims, BF16)
    wide = lambda *dims: jax.ShapeDtypeStruct(dims, F32)
    vmem = pl.BlockSpec(memory_space=pltpu.VMEM)
    cols = pl.BlockSpec((width, tile), lambda i: (0, half))
    rows = pl.BlockSpec((tile, width), lambda i: (half, 0))
    made = [low(size, tile), low(tile // 2, size), low(tile // 2, size), low(size, tile),
            low(size, tile)]
    if half == 0:
        made += [low(size, width), low(size, width), low(size, width), wide(size, width)]
    else:
        made += [low(2 * share, width), wide(share, width), low(share, width)]
    return pl.pallas_call(
        functools.partial(ffn_second_body if half else ffn_first_body, units // devices),
        grid=(1,),
        in_specs=[pl.BlockSpec(memory_space=pltpu.SMEM)] + [vmem] * len(inputs)
        + [cols, cols, rows],
        out_specs=[vmem] * len(made),
        out_shape=made,
        cost_estimate=FREE, name="ffn",
    )(place, *inputs, gate_w, up_w, down_w)


def cross_backward_body(own, got, far, grad, first, second, norms, q0, q1, q2, q3,
                        c0, c1, c2, c3, o0, o1, o2, o3, queries,
                        back_rows, kv_grad, vectors, grad_one, crossed_grad):
    width = grad.shape[1]
    kv = (c0, c1, c2, c3)
    context_rows = c0.shape[0] // 2
    key_rows, value_rows = slice(0, context_rows), slice(context_rows, 2 * context_rows)
    part = width // 4
    lanes = lax.broadcasted_iota(jnp.int32, (grad.shape[0], 2 * HEAD_SIZE), 1) // HEAD_SIZE
    lane_k = lax.broadcasted_iota(jnp.int32, (context_rows, 2 * HEAD_SIZE), 1) // HEAD_SIZE
    scale = 1.0 / math.sqrt(HEAD_SIZE)
    arrived = own[...] + got[...].astype(F32) + far[...].astype(F32)
    scaled, inverse = normalize(second[...])
    vectors[0:1, :] = jnp.sum(arrived * scaled, 0, keepdims=True)
    vectors[1:2, :] = jnp.sum(arrived, 0, keepdims=True)
    two = grad[...].astype(F32) + norm_backward(arrived, scaled, inverse, norms[4:5, :])
    low = two.astype(BF16)
    back_rows[:, :width] = low
    for b, ref in enumerate((o0, o1, o2, o3)):
        crossed_grad[:, b * part : (b + 1) * part] = dot_nt(low, ref[...]).astype(BF16)
    for p in range(width // (2 * HEAD_SIZE)):
        cols = slice(p * 2 * HEAD_SIZE, (p + 1) * 2 * HEAD_SIZE)
        q, k, v = queries[:, cols], pair_cols(kv, p, key_rows), pair_cols(kv, p, value_rows)
        g_rows = crossed_grad[:, cols]
        found = []
        for g in (0, 1):
            probs = head_weights(q, k, lanes, g)
            change = dot_nt(jnp.where(lanes == g, g_rows, jnp.zeros_like(g_rows)), v)
            delta = jnp.sum(change * probs, -1, keepdims=True)
            ds = (probs * (change - delta)).astype(BF16)
            found.append((dot_nn(ds, k), dot_tn(ds, q), dot_tn(probs.astype(BF16), g_rows)))
        back_rows[:, width + cols.start : width + cols.stop] = (
            jnp.where(lanes == 0, found[0][0], found[1][0]) * scale
        ).astype(BF16)
        kv_grad[:context_rows, cols] = (
            jnp.where(lane_k == 0, found[0][1], found[1][1]) * scale
        ).astype(BF16)
        kv_grad[context_rows:, cols] = jnp.where(lane_k == 0, found[0][2], found[1][2]).astype(
            BF16
        )
    back = jnp.zeros(grad.shape, F32)
    for b, ref in enumerate((q0, q1, q2, q3)):
        back = back + dot_nt(back_rows[:, width + b * part : width + (b + 1) * part], ref[...])
    scaled, inverse = normalize(first[...])
    vectors[2:3, :] = jnp.sum(back * scaled, 0, keepdims=True)
    vectors[3:4, :] = jnp.sum(back, 0, keepdims=True)
    grad_one[...] = (two + norm_backward(back, scaled, inverse, norms[2:3, :])).astype(BF16)


def cross_backward(own, got, far, grad, first, second, norms, query_parts, kv_parts, out_parts,
                   queries):
    rows, width = own.shape
    low = lambda r: jax.ShapeDtypeStruct((r, width), BF16)
    block = pl.BlockSpec((rows, width), lambda i: (0, 0))
    return pl.pallas_call(
        cross_backward_body,
        grid=(1,),
        out_shape=[jax.ShapeDtypeStruct((rows, 2 * width), BF16), low(kv_parts[0].shape[0]),
                   jax.ShapeDtypeStruct((4, width), F32), low(rows)],
        in_specs=[block] * 6 + [pl.BlockSpec(memory_space=pltpu.VMEM)] * 14,
        scratch_shapes=[pltpu.VMEM((rows, width), BF16)],
        cost_estimate=FREE, name="cross_back",
    )(own, got, far, grad, first, second, norms, *query_parts, *kv_parts, *out_parts, queries)


def meet_rows_body(own_a, pair_a, own_b, pair_b, right, right_pair, out):
    count = own_a.shape[0]
    for b, (own, pair) in enumerate(((own_a, pair_a), (own_b, pair_b))):
        out[b * count : (b + 1) * count, :] = (
            dot_nn(own[...], right[...]) + dot_nn(pair[...], right_pair[...])
        ).astype(BF16)


def meet_rows(lefts, rights):
    count, size = lefts[0].shape
    width = rights[0].shape[1]
    tile = width // 3
    left = pl.BlockSpec((count, size), lambda i: (0, 0))
    right = pl.BlockSpec((size, tile), lambda i: (0, i))
    return pl.pallas_call(
        meet_rows_body,
        grid=(3,),
        in_specs=[left] * 4 + [right] * 2,
        out_specs=pl.BlockSpec((2 * count, tile), lambda i: (0, i)),
        out_shape=jax.ShapeDtypeStruct((2 * count, width), BF16),
        name="meet_rows", cost_estimate=FREE,
    )(*lefts, *rights)


def meet_cols_body(p0, p1, p2, p3, a, a_pair, b, b_pair, out):
    own, pair = (jnp.concatenate([p[i] for p in (p0, p1, p2, p3)], 1) for i in (0, 1))
    width = a.shape[1]
    out[:, :width] = (dot_nn(own, a[...]) + dot_nn(pair, a_pair[...])).astype(BF16)
    out[:, width:] = (dot_nn(own, b[...]) + dot_nn(pair, b_pair[...])).astype(BF16)


def meet_cols(near, rights):
    return pl.pallas_call(
        meet_cols_body,
        out_shape=jax.ShapeDtypeStruct((near[0].shape[1], 2 * rights[0].shape[1]), BF16),
        name="meet_cols", cost_estimate=FREE,
    )(*near, *rights)


def down_body(first, second, down_w, away, own, low):
    share, units = own.shape[0], first.shape[1]

    def sent(r):
        at = slice(r * share, (r + 1) * share)
        return dot_nn(first[at, :], down_w[:units, :]) + dot_nn(second[at, :], down_w[units:, :])

    away[:share, :] = sent(1).astype(BF16)
    away[share:, :] = sent(3).astype(BF16)
    low[...] = sent(2).astype(BF16)
    own[...] = sent(0)


def down_parts(first, second, down_w):
    share, width = first.shape[0] // 4, down_w.shape[1]
    low = lambda *dims: jax.ShapeDtypeStruct(dims, BF16)
    return pl.pallas_call(
        down_body,
        out_shape=[low(2 * share, width), jax.ShapeDtypeStruct((share, width), F32),
                   low(share, width)],
        name="down", cost_estimate=FREE,
    )(first, second, down_w)


def bundle_body(devices, place, f02, f13, b02, b13, a0, a1, a2, a3, attended,
                context, kv, out_a, out_b):
    width = a0.shape[1]
    part, share = width // 4, a0.shape[0]

    def near(even, odd):
        return even[0], odd[0], even[1], odd[1]

    own = lambda rows: jnp.concatenate(
        [row[:, width + r * part : width + (r + 1) * part] for r, row in enumerate(rows)], 0
    )
    full = lambda rows: jnp.concatenate([row[:, :width] for row in rows], 0)
    fronts, backs = near(f02, f13), near(b02, b13)
    rows = width // devices
    small = part // devices
    half = width // 2

    def put(block, base, left, out):
        for d in range(devices):
            at = slice(base, base + block.shape[0] // devices)
            piece = block[d * block.shape[0] // devices : (d + 1) * block.shape[0] // devices, :]
            out[d, at, left : left + block.shape[1]] = piece.astype(BF16)

    put(dot_tn(full(fronts), own(backs)), 0, 0, out_a)
    count = context.shape[0]
    put(dot_tn(context[...], kv[:count, :]), 0, part, out_a)
    put(dot_tn(context[...], kv[count:, :]), rows // 2, part, out_a)
    grads = dot_tn(own(fronts), full(backs))
    put(grads[:, :half], 0, 0, out_b)
    put(grads[:, half:], small, 0, out_b)
    grads = sum(
        dot_nn(attended[:, relative(place[0], r, share)], ref[...])
        for r, ref in enumerate((a0, a1, a2, a3))
    )
    put(grads[:, :half], 2 * small, 0, out_b)
    put(grads[:, half:], 3 * small, 0, out_b)


def bundle_grads(devices, place, fronts, backs, ones, attended, context, kv):
    width = ones[0].shape[1]
    vmem = pl.BlockSpec(memory_space=pltpu.VMEM)
    return pl.pallas_call(
        functools.partial(bundle_body, devices),
        in_specs=[pl.BlockSpec(memory_space=pltpu.SMEM)] + [vmem] * 11,
        out_specs=[vmem] * 2,
        out_shape=[jax.ShapeDtypeStruct((devices, width // devices, width // 2), BF16)] * 2,
        name="bundle", cost_estimate=FREE,
    )(place, *fronts, *backs, *ones, attended, context, kv)


def front_body(width_block, place, x0, x1, x2, x3, g0, g1, g2, g3, cosine, sine, wq, wk, wv,
               queries, pair, rows, low, nrm_own, nrm_away, norms, means, inverses, wide):
    size, part = x0.shape
    for r, (x, g) in enumerate(((x0, g0), (x1, g1), (x2, g2), (x3, g3))):
        start = pl.multiple_of((place[0] ^ r) * part, 128)
        wide[:, pl.ds(start, part)] = x[...]
        norms[:, pl.ds(start, part)] = g[...]
    share = size // 4
    rows[...] = wide[pl.ds(pl.multiple_of(place[0] * share, share), share), :]
    values = wide[...].astype(F32)
    mean = jnp.mean(values, -1, keepdims=True)
    centred = values - mean
    inverse = lax.rsqrt(jnp.mean(centred * centred, -1, keepdims=True) + 1e-05)
    means[...] = mean
    inverses[...] = inverse
    normed = (centred * inverse * norms[0:1, :] + norms[1:2, :]).astype(BF16)
    low[...] = normed
    half = HEAD_SIZE // 2

    def turned(weight):
        return dot_nn(normed, weight[...]).T

    def rotated(block, dest, scale):
        for h in range(part // HEAD_SIZE):
            a = block[h * HEAD_SIZE : h * HEAD_SIZE + half, :]
            b = block[h * HEAD_SIZE + half : (h + 1) * HEAD_SIZE, :]
            dest[h * HEAD_SIZE : h * HEAD_SIZE + half, :] = (
                (a * cosine[...] - b * sine[...]) * scale
            ).astype(BF16)
            dest[h * HEAD_SIZE + half : (h + 1) * HEAD_SIZE, :] = (
                (b * cosine[...] + a * sine[...]) * scale
            ).astype(BF16)

    rotated(turned(wk), pair.at[0], 1.0)
    pair[1] = turned(wv).astype(BF16)
    rotated(turned(wq), queries, 1.0 / math.sqrt(HEAD_SIZE))
    deal_rows(normed.T, width_block, place[1], nrm_own, nrm_away)


def front(devices, place, parts, norm_parts, tables, wq, wk, wv):
    size, part = parts[0].shape
    width = 4 * part
    low = lambda *s: jax.ShapeDtypeStruct(s, BF16)
    wide = lambda *s: jax.ShapeDtypeStruct(s, F32)
    vmem = pl.BlockSpec(memory_space=pltpu.VMEM)
    return pl.pallas_call(
        functools.partial(front_body, width // devices),
        in_specs=[pl.BlockSpec(memory_space=pltpu.SMEM)] + [vmem] * 13,
        out_specs=[vmem] * 9,
        out_shape=[low(part, size), low(2, part, size), low(size // 4, width), low(size, width),
                   low(width // 2, size), low(width // 2, size), wide(6, width),
                   wide(size, 1), wide(size, 1)],
        scratch_shapes=[pltpu.VMEM((size, width), BF16)],
        cost_estimate=FREE, name="front",
    )(place, *parts, *norm_parts, *tables, wq, wk, wv)


def per_device(
    frames,
    segment,
    time_token,
    context,
    gain_attn,
    bias_attn,
    gain_cross,
    bias_cross,
    gain_ffn,
    bias_ffn,
    w_query,
    w_key,
    w_value,
    w_out,
    c_query,
    c_key,
    c_value,
    c_out,
    w_gate,
    w_up,
    w_down,
    out_grad,
):
    local_rows = frames.shape[0]
    local_width = frames.shape[1]
    model_width = w_query.shape[0]
    head_cols = w_query.shape[1]
    heads = head_cols // HEAD_SIZE
    number_of_frames = lax.axis_size("seq") * local_rows
    row_length = min(max(ROW_MIN, 64 * lax.axis_size("seq")), number_of_frames)
    first_frame = lax.axis_index("seq") * local_rows
    own_start = lax.axis_index("tensor") * local_width

    def own_cols(value):
        return lax.dynamic_slice_in_dim(value, own_start, local_width, value.ndim - 1)

    place = lax.axis_index("tensor")
    share = local_rows // 4

    def row_block(value, index):
        return rows_of(value, index * share, share)

    column = lax.axis_index("seq") % 2
    frame_parts_near = gather_near(frames)
    norm_parts = gather_near(
        jnp.stack([gain_attn, bias_attn, gain_cross, bias_cross, gain_ffn, bias_ffn])
    )
    clip_starts, frame_positions = frame_clip_labels(segment, row_length)
    own_labels = lax.dynamic_slice_in_dim(clip_starts, first_frame, local_rows)
    own_positions = lax.dynamic_slice_in_dim(frame_positions, first_frame, local_rows)
    blanks = jnp.full((local_rows,), -1, jnp.int32)
    key_labels = lax.dynamic_slice_in_dim(
        jnp.concatenate([blanks, clip_starts, blanks]), first_frame, 3 * local_rows
    )
    spans = jnp.concatenate(
        [tile_ranges(own_labels, key_labels), place.astype(jnp.int32).reshape(1)]
    )
    places = jnp.stack([column, place]).astype(jnp.int32)
    label_row, label_column = own_labels[None, :], key_labels[:, None]
    row_index = first_frame // row_length
    time_row = lax.dynamic_slice_in_dim(time_token, row_index, 1, 0).astype(F32)
    row_context = lax.dynamic_slice_in_dim(context, row_index, 1, 0)[0]
    context_rows = row_context.shape[0]
    tables = rotary_tables(own_positions)
    score_scale = 1.0 / math.sqrt(HEAD_SIZE)
    all_heads = model_width // HEAD_SIZE

    (
        queries, both, frame_rows, frame_normed, one_own_half, one_away_half, norms, means_one,
        inverse_one,
    ) = front(
        lax.axis_size("seq"), jnp.flip(places), frame_parts_near, norm_parts, tables, w_query,
        w_key, w_value,
    )
    both, out_pair = meeting(both, swap(after(out_grad, frame_parts_near[2]), "seq", 1))
    grad_both = jnp.stack([out_grad, out_pair])
    own_keys, own_values = both[0], both[1]
    gain_one, bias_one = norms[0:1], norms[1:2]
    behind, ahead = shift(both, "seq", 1), shift(both, "seq", -1)
    query_far = swap(after(c_query, frame_parts_near[3]), "tensor", 2)
    out_far = swap(after(c_out, frame_parts_near[3]), "tensor", 2)
    time_late = after(time_row, both)
    scaled_time, _ = normalize(time_late)
    time_normed = (scaled_time * gain_one + bias_one).astype(BF16)
    time_keys = by_feature(time_normed, w_key).astype(BF16).astype(F32)
    time_values = by_feature(time_normed, w_value).astype(BF16).astype(F32)
    context_late = after(row_context, both)
    context_kv = jnp.concatenate(
        [product(context_late, c_key), product(context_late, c_value)], 0
    ).astype(BF16)
    behind, ahead, query_far, out_far = meeting(behind, ahead, query_far, out_far)
    query_own, out_own, context_late = after((c_query, c_out, context_kv), behind)
    weights_near = [
        swap(value, "tensor", 1) for value in (query_own, query_far, out_own, out_far)
    ]
    kv_far = swap(context_late, "tensor", 2)
    keys = (behind[0], own_keys, ahead[0])
    values = (behind[1], own_values, ahead[1])
    attended, log_totals, one_away, one_own, one_low = attend(
        spans, queries, keys, values, time_keys, time_values, label_row, label_column, w_out
    )
    one_away, one_low, kv_far, *weights_near = meeting(one_away, one_low, kv_far, *weights_near)
    kv_both = jnp.concatenate([context_kv, kv_far], 0)
    kv_other = swap(kv_both, "tensor", 1)
    kv_rows = context_kv.shape[0]
    kv_parts = (context_kv, kv_other[:kv_rows], kv_far, kv_other[kv_rows:])
    query_parts = (c_query, weights_near[0], query_far, weights_near[1])
    out_parts = (c_out, weights_near[2], out_far, weights_near[3])
    one_got, _, one_far = scatter_near(one_away, one_low)
    (
        front_rows, cross_queries, residual_one, residual_two, normed_share, flip_own, flip_away,
    ) = cross_forward(
        lax.axis_size("seq"), places, frame_rows, one_own, one_got, one_far, norms,
        query_parts, kv_parts, out_parts,
    )
    grad_far = swap(after(grad_both, one_far), "tensor", 2)
    normed_share, normed_got, grad_far = meeting(
        normed_share, swap(after(one_away_half, one_low), "seq", 1), grad_far
    )
    grad_late, grad_far_late = after((grad_both, grad_far), normed_share)
    grad_mate, grad_far_mate = swap(grad_late, "tensor", 1), swap(grad_far_late, "tensor", 1)
    grad_parts = (grad_both, grad_mate, grad_far, grad_far_mate)
    three_parts = gather_near(normed_share)
    flip_got = swap(after(flip_away, normed_share), "seq", 1)
    front_far = swap(after(front_rows, three_parts[3]), "tensor", 2)
    devices = lax.axis_size("seq")
    (
        hidden_a, hidden_own_a, hidden_away_a, gate_a, lifted_a, normed_three, grad_near, grad_pair,
        ffn_total,
    ) = ffn(devices, places, 0, (*three_parts, *grad_parts), w_gate, w_up, w_down)
    ffn_total, flip_got = meeting(ffn_total, flip_got)
    flip_both = jnp.stack([flip_own, flip_got])
    flip_far = swap(flip_both, "tensor", 2)
    hidden_got_a, gate_got_a = swap(hidden_away_a, "seq", 1), swap(gate_a, "seq", 1)
    hidden_b, hidden_own_b, hidden_away_b, gate_b, lifted_b, three_away, three_own, three_low = ffn(
        devices, places, 1, (normed_three, grad_near, ffn_total), w_gate, w_up, w_down
    )
    three_away, three_low, flip_far, front_far, hidden_got_a = meeting(
        three_away, three_low, flip_far, front_far, hidden_got_a
    )
    three_got, _, three_far = scatter_near(three_away, three_low)
    three_far, gate_got_a = meeting(three_far, gate_got_a)
    hidden_late, lifted_late = after((hidden_away_b, lifted_a), three_low)
    hidden_got_b, lifted_got_a = swap(hidden_late, "seq", 1), swap(lifted_late, "seq", 1)
    flip_late, flip_far_late, gate_late = after((flip_both, flip_far, gate_b), three_far)
    flip_mate, flip_far_mate = swap(flip_late, "tensor", 1), swap(flip_far_late, "tensor", 1)
    gate_got_b = swap(gate_late, "seq", 1)
    front_both = jnp.stack([front_rows, front_far])
    back_rows, kv_grad, norm_vectors, grad_one = cross_backward(
        three_own, three_got, three_far, grad_near, residual_one, residual_two, norms,
        query_parts, kv_parts, out_parts, cross_queries,
    )
    grad_one, hidden_got_b, lifted_got_a, flip_mate, flip_far_mate = meeting(
        grad_one, hidden_got_b, lifted_got_a, flip_mate, flip_far_mate
    )
    count = lax.axis_size("seq")

    def by_level(blocks):
        return blocks.reshape(count // 2, 2 * blocks.shape[0] // count, blocks.shape[1])

    down_keep, down_got = halve(
        by_level(
            meet_rows(
                (hidden_own_a, hidden_got_a, hidden_own_b, hidden_got_b), (grad_near, grad_pair)
            )
        ),
        1,
    )
    context_parts = quarters(kv_grad, 1)
    context_got = swap(jnp.concatenate([context_parts[1], context_parts[3]], 0), "tensor", 1)
    *one_parts, front_other, context_got = meeting(
        *gather_near(grad_one), swap(after(front_both, grad_one), "tensor", 1), context_got
    )
    context_low = (
        context_parts[2].astype(F32) + context_got[context_parts[2].shape[0] :].astype(F32)
    ).astype(BF16)
    context_far = swap(context_low, "tensor", 2)
    back_late, lifted_late = after((back_rows, lifted_b), one_parts[3])
    back_far = swap(back_late, "tensor", 2)
    lifted_got_b = swap(lifted_late, "seq", 1)
    query_grad, to_prev, kept, to_next, time_key_grad, time_value_grad = attend_back(
        spans, queries, keys, values, time_keys, time_values, label_row, label_column, w_out,
        attended, log_totals, one_parts,
    )
    to_prev, to_next, back_far, gate_got_b, lifted_got_b, down_got, context_far = meeting(
        to_prev, to_next, back_far, gate_got_b, lifted_got_b, down_got, context_far
    )
    from_next, from_prev = shift(to_prev, "seq", -1), shift(to_next, "seq", 1)
    down_keep, down_got = halve(added(down_keep, down_got).astype(BF16), 2)
    flip_near = (flip_both, flip_mate, flip_far, flip_far_mate)
    first_keep, first_got = halve(
        by_level(meet_cols(flip_near, after((gate_a, gate_got_a, lifted_a, lifted_got_a), to_prev))),
        1,
    )
    down_away, down_own, down_low = down_parts(after(hidden_a, to_prev), hidden_b, w_down)
    back_both = jnp.stack([back_rows, back_far])
    back_other = swap(back_both, "tensor", 1)
    context_own = (
        context_parts[0].astype(F32)
        + context_got[: context_far.shape[0]].astype(F32)
        + context_far.astype(F32)
    )
    bundle_a, bundle_b = bundle_grads(
        count, places[1:], (front_both, front_other), (back_both, back_other), one_parts, attended,
        row_context,
        context_own.astype(BF16),
    )
    from_next, from_prev, bundle_a, bundle_b = meeting(from_next, from_prev, bundle_a, bundle_b)
    (keep_a, got_a), (keep_b, got_b) = halve(bundle_a, 0), halve(bundle_b, 0)
    raw, last_away, last_own, last_low = tail(
        places[1:], query_grad, kept, from_next, from_prev, tables, w_query, w_key, w_value
    )
    last_away, last_low, first_got, down_got, got_a = meeting(
        last_away, last_low, first_got, down_got, got_a
    )
    second = by_level(
        meet_cols(flip_near, after((gate_b, gate_got_b, lifted_b, lifted_got_b), from_next))
    )
    second_keep, second_got = halve(second, 1)
    last_got, last_sum, last_far = scatter_near(last_away, last_low)
    last_far, got_b, second_got = meeting(last_far, got_b, second_got)
    frame_grad = last_own + last_got[:local_rows].astype(F32) + last_far.astype(F32)

    def to_frames(rows, weight):
        return jnp.einsum("fn,df->nd", rows, weight, preferred_element_type=F32)

    time_key_grad, time_value_grad = after((time_key_grad, time_value_grad), from_next)
    time_grad = to_frames(time_key_grad.astype(BF16), w_key) + to_frames(
        time_value_grad.astype(BF16), w_value
    )
    own_scaled = (frames.astype(F32) - means_one) * inverse_one
    scaled_grad = frame_grad * gain_attn[None]
    sums = jnp.concatenate(
        [
            jnp.sum(scaled_grad, -1),
            jnp.sum(scaled_grad * own_scaled, -1),
            time_grad[0],
            norm_vectors.reshape(-1),
        ]
    )[None]
    sums = sums + swap(sums, "tensor", 1)
    raw_got = swap(raw, "seq", 1)
    sums = sums + swap(sums, "tensor", 2)
    sums, raw_got = meeting(sums, raw_got)
    plain = sums[0, :local_rows, None] / model_width
    cross = sums[0, local_rows : 2 * local_rows, None] / model_width
    vectors = own_cols(sums[0, 2 * local_rows :].reshape(5, model_width))
    attend_full = ordered(*[after(one_parts, from_next)[i] for i in (0, 2, 1, 3)], 0)
    d_frames = own_cols(attend_full).astype(F32) + inverse_one * (
        scaled_grad - plain - own_scaled * cross
    )
    d_gain_attn = jnp.sum(frame_grad * own_scaled, 0) + vectors[0] * own_cols(scaled_time)[0]
    d_bias_attn = jnp.sum(frame_grad, 0) + vectors[0]
    small = reduce_small(
        jnp.stack([d_gain_attn, d_bias_attn, vectors[3], vectors[4], vectors[1], vectors[2]])
    )

    down_away, down_low = after((down_away, down_low), last_far)
    branch_got, _, branch_far = scatter_near(down_away, down_low)
    block_rows = (
        residual_two + down_own + branch_got[:share].astype(F32) + branch_far.astype(F32)
    ).astype(BF16)
    block_cols = rows_to_cols(
        *[
            lax.dynamic_slice_in_dim(block_rows, (place ^ r) * local_width, local_width, 1)
            for r in range(4)
        ],
        from_next,
    )
    block_out = jnp.concatenate([row_block(block_cols, place ^ b) for b in range(4)], 0)

    time_column = time_normed.astype(F32).T

    normed_pair = (one_own_half, normed_got)
    grad_down = halve_end(down_keep, down_got, 3)
    first, second = halve_end(first_keep, first_got, 2), halve_end(second_keep, second_got, 2)
    units = first.shape[1] // 2
    grad_gate_w = jnp.concatenate([first[:, :units], second[:, :units]], 1)
    grad_up_w = jnp.concatenate([first[:, units:], second[:, units:]], 1)
    left, right = halve_end(keep_a, got_a, 1), halve_end(keep_b, got_b, 1)
    part, rows = head_cols // count, model_width // count
    grad_c_query = left[:, :head_cols]
    grad_c_key, grad_c_value = left[: rows // 2, head_cols:], left[rows // 2 :, head_cols:]
    grad_c_out = jnp.concatenate([right[:part], right[part : 2 * part]], 1)
    grad_w_out = jnp.concatenate([right[2 * part : 3 * part], right[3 * part :]], 1)

    raw_pair = (raw, raw_got)
    time_both = jnp.concatenate([time_key_grad, time_value_grad], 0)
    time_both = time_both + swap(after(time_both, last_far), "seq", 1)
    own_time_rows = lax.dynamic_index_in_dim(
        time_column.reshape(count // 2, 2, -1), column, 1, False
    ).reshape(-1, 1)
    outer = own_time_rows * jnp.concatenate([jnp.zeros((head_cols, 1), F32), time_both], 0).T
    blocks = sum(
        jnp.einsum("dn,fn->df", r, c, preferred_element_type=F32)
        for r, c in zip(normed_pair, raw_pair)
    )
    blocks = by_level((blocks + outer).astype(BF16))
    heads_sum = halve_all(blocks, 1)
    grad_w_query, grad_w_key, grad_w_value = (
        heads_sum[:, i * head_cols : (i + 1) * head_cols] for i in range(3)
    )
    return (
        block_out,
        d_frames,
        small[0],
        small[1],
        small[2],
        small[3],
        small[4],
        small[5],
        grad_w_query,
        grad_w_key,
        grad_w_value,
        grad_w_out,
        grad_c_query,
        grad_c_key,
        grad_c_value,
        grad_c_out,
        grad_gate_w,
        grad_up_w,
        grad_down,
    )


def solution(mesh):
    return jax.shard_map(
        per_device,
        mesh=mesh,
        in_specs=(
            P("seq", "tensor"),
            P(),
            P(),
            P(),
            P("tensor"),
            P("tensor"),
            P("tensor"),
            P("tensor"),
            P("tensor"),
            P("tensor"),
            P(None, "tensor"),
            P(None, "tensor"),
            P(None, "tensor"),
            P("tensor", None),
            P(None, "tensor"),
            P(None, "tensor"),
            P(None, "tensor"),
            P("tensor", None),
            P(None, "tensor"),
            P(None, "tensor"),
            P("tensor", None),
            P("seq", "tensor"),
        ),
        out_specs=(
            P("seq", "tensor"),
            P("seq", "tensor"),
            P(("tensor", "seq")),
            P(("tensor", "seq")),
            P(("tensor", "seq")),
            P(("tensor", "seq")),
            P(("tensor", "seq")),
            P(("tensor", "seq")),
            P("seq", "tensor"),
            P("seq", "tensor"),
            P("seq", "tensor"),
            P(("tensor", "seq"), None),
            P("seq", "tensor"),
            P("seq", "tensor"),
            P("seq", "tensor"),
            P(("tensor", "seq"), None),
            P("seq", "tensor"),
            P("seq", "tensor"),
            P(("tensor", "seq"), None),
        ),
        check_vma=False,
    )
```

```python
import functools
import math

import jax
import jax.numpy as jnp
from jax import lax
from jax.experimental import pallas as pl
from jax.experimental.pallas import tpu as pltpu
from jax.sharding import PartitionSpec as P

HEAD_SIZE = 64
ROW_MIN = 2048
TILE = 256
BF16 = jnp.bfloat16
F32 = jnp.float32


def meeting(*values):
    return lax.optimization_barrier(values)


def after(value, token):
    return lax.optimization_barrier((value, token))[0]


def swap(value, axis, by):
    return lax.ppermute(value, axis, [(i, i ^ by) for i in range(lax.axis_size(axis))])


def shift(value, axis, by):
    peers = lax.axis_size(axis)
    pairs = [(i, i + by) for i in range(peers) if 0 <= i + by < peers]
    return lax.ppermute(value, axis, pairs)


def tensor_place():
    place = lax.axis_index("tensor")
    return place // 2, place % 2


def ordered(own, far, mate, far_mate, axis):
    side, core = tensor_place()
    near = (jnp.where(core == 0, own, mate), jnp.where(core == 0, mate, own))
    away = (jnp.where(core == 0, far, far_mate), jnp.where(core == 0, far_mate, far))
    low = [jnp.where(side == 0, n, a) for n, a in zip(near, away)]
    high = [jnp.where(side == 0, a, n) for n, a in zip(near, away)]
    return jnp.concatenate(low + high, axis)


def gather_near(own):
    far = swap(own, "tensor", 2)
    return own, swap(own, "tensor", 1), far, swap(far, "tensor", 1)


def gather_staged(own, first, second):
    far = swap(after(own, first), "tensor", 2)
    far, late = after((far, own), second)
    return own, swap(late, "tensor", 1), far, swap(far, "tensor", 1)


def gather(own, axis):
    own, mate, far, far_mate = gather_near(own)
    return ordered(own, far, mate, far_mate, axis)


def scatter_near(away, low):
    got = swap(away, "tensor", 1)
    total = (low.astype(F32) + got[low.shape[0] :].astype(F32)).astype(BF16)
    return got, total, swap(total, "tensor", 2)


def rows_to_cols(own, mate, far, far_mate, later):
    width = own.shape[1]
    got = after(swap(jnp.concatenate([far, far_mate], 1), "tensor", 2), later)
    other = swap(jnp.concatenate([mate, got[:, width:]], 0), "tensor", 1)
    size = own.shape[0]
    return jnp.concatenate([own, other[:size], got[:, :width], other[size:]], 0)


def quarters(value, axis):
    return jnp.split(value, 4, axis)


def own_blocks(near):
    return jnp.concatenate([quarters(value, 1)[r] for r, value in enumerate(near)], 0)


def trade(value, start, done):
    return after(swap(after(value, start), "seq", 1), done)


def halve(blocks, bit):
    count, rows, cols = blocks.shape
    side = (lax.axis_index("seq") >> bit) % 2
    parts = blocks.reshape(count // 2, 2, rows, cols)
    send = lax.dynamic_index_in_dim(parts, 1 - side, 1, False)
    keep = lax.dynamic_index_in_dim(parts, side, 1, False)
    return keep, swap(send, "seq", 1 << bit)


def added(keep, got):
    return keep.astype(F32) + got.astype(F32)


def halve_all(blocks, bit):
    while blocks.shape[0] > 1:
        blocks = added(*halve(blocks.astype(BF16), bit))
        bit += 1
    return blocks[0].astype(F32)


def halve_end(keep, got, bit):
    return halve_all(added(keep, got), bit)


def frame_clip_labels(segment, row_length):
    frame_index = jnp.arange(segment.shape[0], dtype=jnp.int32)
    border = (frame_index % row_length == 0) | (segment != jnp.roll(segment, 1))
    clip_starts = lax.cummax(jnp.where(border, frame_index, 0), axis=0)
    return (clip_starts, (frame_index - clip_starts + 1).astype(jnp.float32))


def tile_ranges(q_labels, key_labels):
    q = q_labels.reshape(-1, TILE)
    k = key_labels.reshape(-1, TILE)
    meets = (k[None, :, 0] <= q[:, None, -1]) & (k[None, :, -1] >= q[:, None, 0])
    index = jnp.arange(k.shape[0], dtype=jnp.int32)[None]
    low = jnp.min(jnp.where(meets, index, k.shape[0]), 1)
    high = jnp.max(jnp.where(meets, index + 1, 0), 1)
    return jnp.stack([low, high], 1).reshape(-1)

def head_rows(g):
    return slice(g * HEAD_SIZE, (g + 1) * HEAD_SIZE)

def fill_natural(dest, refs, which):
    size = refs[0].shape[2]
    for part, ref in enumerate(refs):
        dest[part * size : (part + 1) * size, :] = ref[which].T


def fill_tiles(dest, refs, which):
    pieces = refs[0].shape[2] // TILE
    for part, ref in enumerate(refs):
        for piece in range(pieces):
            dest[part * pieces + piece] = ref[which, :, piece * TILE : (piece + 1) * TILE]


def relative(place, r, size):
    return pl.ds(pl.multiple_of((place ^ r) * size, size), size)


def absorb(state, start, stop, base, q, cols, lab, klab, keys, vals):
    group = q.shape[0] // HEAD_SIZE

    def step(j, state):
        seen = klab[pl.ds(pl.multiple_of(j * TILE, TILE), TILE), :] == lab
        at = pl.ds(pl.multiple_of((j - base) * TILE, TILE), TILE)
        fresh = []
        for g in range(group):
            top, total, acc = state[3 * g : 3 * g + 3]
            s = dot_nn(keys[at, head_rows(g)], q[head_rows(g), cols])
            s = jnp.where(seen, s, -1e30)
            new = jnp.maximum(top, jnp.max(s, 0, keepdims=True))
            fade = jnp.exp(top - new)
            p = jnp.exp(s - new)
            total = total * fade + jnp.sum(p, 0, keepdims=True)
            acc = acc * fade + dot_nn(vals[j - base, head_rows(g), :], p.astype(BF16))
            fresh += [new, total, acc]
        return tuple(fresh)

    return lax.fori_loop(start, stop, step, tuple(state))


def near_body(span, q, kv, tk, tv, qlab, klab, tops, totals, mix, keys, vals):
    rows, size = q.shape
    pieces = size // TILE
    fill_natural(keys, (kv,), 0)
    fill_tiles(vals, (kv,), 1)
    for tile in range(pieces):
        cols = slice(tile * TILE, (tile + 1) * TILE)
        state = []
        for g in range(rows // HEAD_SIZE):
            part = q[head_rows(g), cols].astype(F32)
            top = jnp.sum(part * tk[head_rows(g), :], 0, keepdims=True)
            state += [
                top,
                jnp.ones_like(top),
                jnp.broadcast_to(tv[head_rows(g), :], (HEAD_SIZE, TILE)),
            ]
        start = jnp.maximum(span[2 * tile], pieces)
        stop = jnp.minimum(span[2 * tile + 1], 2 * pieces)
        state = absorb(state, start, stop, pieces, q, cols, qlab[:, cols], klab, keys, vals)
        for g in range(rows // HEAD_SIZE):
            tops[g : g + 1, cols], totals[g : g + 1, cols], mix[head_rows(g), cols] = state[
                3 * g : 3 * g + 3
            ]


def far_body(span, q, kv0, kv2, qlab, klab, w_out, tops, totals, mix,
             out, lse, away, own, low, keys0, keys2, vals0, vals2):
    rows, size = q.shape
    pieces = size // TILE
    for kv, keys, vals in ((kv0, keys0, vals0), (kv2, keys2, vals2)):
        fill_natural(keys, (kv,), 0)
        fill_tiles(vals, (kv,), 1)
    for tile in range(pieces):
        cols = slice(tile * TILE, (tile + 1) * TILE)
        lab = qlab[:, cols]
        state = []
        for g in range(rows // HEAD_SIZE):
            state += [tops[g : g + 1, cols], totals[g : g + 1, cols], mix[head_rows(g), cols]]
        stop = jnp.minimum(span[2 * tile + 1], pieces)
        state = absorb(state, span[2 * tile], stop, 0, q, cols, lab, klab, keys0, vals0)
        start = jnp.maximum(span[2 * tile], 2 * pieces)
        state = absorb(
            state, start, span[2 * tile + 1], 2 * pieces, q, cols, lab, klab, keys2, vals2
        )
        for g in range(rows // HEAD_SIZE):
            top, total, acc = state[3 * g : 3 * g + 3]
            out[head_rows(g), cols] = (acc / total).astype(BF16)
            lse[g : g + 1, cols] = top + jnp.log(total)
    place = span[2 * pieces]
    share = own.shape[0]

    def sent(r):
        return dot_tn(out[:, relative(place, r, share)], w_out[...])

    away[:share, :] = sent(1).astype(BF16)
    away[share:, :] = sent(3).astype(BF16)
    low[...] = sent(2).astype(BF16)
    own[...] = sent(0)


def backward_body(span, q, kv0, kv1, kv2, tk, tv, qlab, klab, w_out, out, lse,
                  g0, g1, g2, g3, dq, to_prev, kept, to_next, dtk, dtv,
                  og, keys, vals, tkeys, ak, av):
    rows, size = q.shape
    group = rows // HEAD_SIZE
    pieces = size // TILE
    share = g0.shape[0]
    for r, ref in enumerate((g0, g1, g2, g3)):
        og[:, relative(span[2 * pieces], r, share)] = dot_nt(w_out[...], ref[...]).astype(BF16)
    fill_natural(keys, (kv0, kv1, kv2), 0)
    fill_natural(vals, (kv0, kv1, kv2), 1)
    fill_tiles(tkeys, (kv0, kv1, kv2), 0)
    ak[...] = jnp.zeros_like(ak)
    av[...] = jnp.zeros_like(av)
    for tile in range(pieces):
        cols = slice(tile * TILE, (tile + 1) * TILE)
        lab = qlab[:, cols]
        state, norms, deltas = [], [], []
        for g in range(group):
            hr = head_rows(g)
            qf = q[hr, cols].astype(F32)
            gf = og[hr, cols].astype(F32)
            norm = lse[g : g + 1, cols]
            delta = jnp.sum(gf * out[hr, cols].astype(F32), 0, keepdims=True)
            pt = jnp.exp(jnp.sum(qf * tk[hr, :], 0, keepdims=True) - norm)
            st = pt * (jnp.sum(gf * tv[hr, :], 0, keepdims=True) - delta)
            gk = jnp.sum(qf * st, 1, keepdims=True)
            gv = jnp.sum(gf * pt, 1, keepdims=True)
            if tile == 0:
                dtk[hr, :] = gk
                dtv[hr, :] = gv
            else:
                dtk[hr, :] += gk
                dtv[hr, :] += gv
            state.append(tk[hr, :] * st)
            norms.append(norm)
            deltas.append(delta)

        def step(j, state):
            start = pl.multiple_of(j * TILE, TILE)
            seen = klab[pl.ds(start, TILE), :] == lab
            fresh = []
            for g in range(group):
                hr = head_rows(g)
                s = dot_nn(keys[pl.ds(start, TILE), hr], q[hr, cols])
                p = jnp.exp(jnp.where(seen, s, -1e30) - norms[g])
                m = dot_nn(vals[pl.ds(start, TILE), hr], og[hr, cols])
                ds = (p * (m - deltas[g])).astype(BF16)
                av[j, hr, :] += dot_nt(og[hr, cols], p.astype(BF16))
                ak[j, hr, :] += dot_nt(q[hr, cols], ds)
                fresh.append(state[g] + dot_nn(tkeys[j, hr, :], ds))
            return tuple(fresh)

        state = lax.fori_loop(span[2 * tile], span[2 * tile + 1], step, tuple(state))
        for g in range(group):
            dq[head_rows(g), cols] = state[g]
    for part, dest in enumerate((to_prev, kept, to_next)):
        for piece in range(pieces):
            at = slice(piece * TILE, (piece + 1) * TILE)
            dest[0, :, at] = ak[part * pieces + piece].astype(dest.dtype)
            dest[1, :, at] = av[part * pieces + piece].astype(dest.dtype)


def attend_near(span, q, kv, tk, tv, qlab, klab):
    cols, size = q.shape
    wide = lambda *dims: jax.ShapeDtypeStruct(dims, F32)
    vmem = pl.BlockSpec(memory_space=pltpu.VMEM)
    return pl.pallas_call(
        near_body,
        in_specs=[pl.BlockSpec(memory_space=pltpu.SMEM)] + [vmem] * 6,
        out_specs=[vmem] * 3,
        out_shape=[wide(cols // HEAD_SIZE, size), wide(cols // HEAD_SIZE, size), wide(cols, size)],
        scratch_shapes=[pltpu.VMEM((size, cols), BF16), pltpu.VMEM((size // TILE, cols, TILE), BF16)],
        name="attend_near", cost_estimate=FREE,
    )(span, q, kv, tk, tv, qlab, klab)


def attend_far(span, q, behind, ahead, qlab, klab, w_out, state):
    cols, size = q.shape
    share, width = size // 4, w_out.shape[1]
    low = lambda *dims: jax.ShapeDtypeStruct(dims, BF16)
    wide = lambda *dims: jax.ShapeDtypeStruct(dims, F32)
    vmem = pl.BlockSpec(memory_space=pltpu.VMEM)
    keys = pltpu.VMEM((size, cols), BF16)
    vals = pltpu.VMEM((size // TILE, cols, TILE), BF16)
    return pl.pallas_call(
        far_body,
        in_specs=[pl.BlockSpec(memory_space=pltpu.SMEM)] + [vmem] * 9,
        out_specs=[vmem] * 5,
        out_shape=[low(cols, size), wide(cols // HEAD_SIZE, size), low(2 * share, width),
                   wide(share, width), low(share, width)],
        scratch_shapes=[keys, keys, vals, vals],
        name="attend_far", cost_estimate=FREE,
    )(span, q, behind, ahead, qlab, klab, w_out, *state)


def attend_back(span, q, kvs, tk, tv, qlab, klab, w_out, out, lse, grads):
    cols, size = q.shape
    tiles = 3 * size // TILE
    low = lambda *dims: jax.ShapeDtypeStruct(dims, BF16)
    wide = lambda *dims: jax.ShapeDtypeStruct(dims, F32)
    vmem = pl.BlockSpec(memory_space=pltpu.VMEM)
    return pl.pallas_call(
        backward_body,
        in_specs=[pl.BlockSpec(memory_space=pltpu.SMEM)] + [vmem] * 15,
        out_specs=[vmem] * 6,
        out_shape=[wide(cols, size), low(2, cols, size), wide(2, cols, size), low(2, cols, size),
                   wide(cols, 1), wide(cols, 1)],
        scratch_shapes=[pltpu.VMEM((cols, size), BF16), pltpu.VMEM((3 * size, cols), BF16),
                        pltpu.VMEM((3 * size, cols), BF16), pltpu.VMEM((tiles, cols, TILE), BF16),
                        pltpu.VMEM((tiles, cols, TILE), F32), pltpu.VMEM((tiles, cols, TILE), F32)],
        name="attend_back", cost_estimate=FREE,
    )(span, q, *kvs, tk, tv, qlab, klab, w_out, out, lse, *grads)


def tail_body(place, dq, kept, ahead, behind, cosine, sine, wq, wk, wv, raw, away, own, low, flipped):
    part, size = dq.shape
    half = HEAD_SIZE // 2

    def returned(block, base, scale):
        for h in range(part // HEAD_SIZE):
            a = block[h * HEAD_SIZE : h * HEAD_SIZE + half, :]
            b = block[h * HEAD_SIZE + half : (h + 1) * HEAD_SIZE, :]
            at = base + h * HEAD_SIZE
            raw[at : at + half, :] = ((a * cosine[...] + b * sine[...]) * scale).astype(BF16)
            raw[at + half : at + HEAD_SIZE, :] = (
                (b * cosine[...] - a * sine[...]) * scale
            ).astype(BF16)

    def whole(index):
        return kept[index] + ahead[index].astype(F32) + behind[index].astype(F32)

    returned(dq[...], 0, 1.0 / math.sqrt(HEAD_SIZE))
    returned(whole(0), part, 1.0)
    raw[2 * part :, :] = whole(1).astype(BF16)
    flipped[...] = raw[...].T

    def sent(r):
        at = relative(place[0], r, part)
        return sum(
            dot_nt(flipped[:, i * part : (i + 1) * part], weight[at, :])
            for i, weight in enumerate((wq, wk, wv))
        )

    away[:size, :] = sent(1).astype(BF16)
    away[size:, :] = sent(3).astype(BF16)
    low[...] = sent(2).astype(BF16)
    own[...] = sent(0)


def tail(place, dq, kept, ahead, behind, tables, wq, wk, wv):
    part, size = dq.shape
    low = lambda *dims: jax.ShapeDtypeStruct(dims, BF16)
    vmem = pl.BlockSpec(memory_space=pltpu.VMEM)
    return pl.pallas_call(
        tail_body,
        in_specs=[pl.BlockSpec(memory_space=pltpu.SMEM)] + [vmem] * 9,
        out_specs=[vmem] * 4,
        out_shape=[low(3 * part, size), low(2 * size, part), jax.ShapeDtypeStruct((size, part), F32),
                   low(size, part)],
        scratch_shapes=[pltpu.VMEM((size, 3 * part), BF16)],
        name="tail", cost_estimate=FREE,
    )(place, dq, kept, ahead, behind, *tables, wq, wk, wv)


def rotary_tables(frame_positions):
    half_dim = HEAD_SIZE // 2
    frequency = jnp.exp(jnp.arange(half_dim, dtype=jnp.float32) * (-math.log(10000.0) / half_dim))
    angles = frequency[:, None] * frame_positions[None, :]
    return (jnp.cos(angles), jnp.sin(angles))


def rotate(rows, tables, sign=1.0):
    count, size = rows.shape
    halves = rows.reshape(count // HEAD_SIZE, 2, HEAD_SIZE // 2, size)
    cosine, sine = tables[0][None], tables[1][None] * sign
    first = halves[:, 0] * cosine - halves[:, 1] * sine
    second = halves[:, 1] * cosine + halves[:, 0] * sine
    return jnp.stack([first, second], 1).reshape(count, size)


def product(left, right):
    return jnp.dot(left, right, preferred_element_type=jnp.float32)


def inner_rows(left, right):
    return jnp.einsum("nd,nf->df", left, right, preferred_element_type=jnp.float32)


def back_project(gradient, weight):
    return jnp.einsum("nf,df->nd", gradient, weight, preferred_element_type=jnp.float32)


def by_feature(left, right):
    return jnp.einsum("nd,df->fn", left, right, preferred_element_type=jnp.float32)


def columns(weight, start, size):
    return lax.dynamic_slice_in_dim(weight, start, size, 1)


def rows_of(weight, start, size):
    return lax.dynamic_slice_in_dim(weight, start, size, 0)


def normalize(value_rows):
    means = jnp.mean(value_rows, -1, keepdims=True)
    centred = value_rows - means
    inverse = lax.rsqrt(jnp.mean(centred * centred, -1, keepdims=True) + 1e-05)
    return centred * inverse, inverse


def norm_backward(gradient, scaled, inverse, norm_gain):
    scaled_grad = gradient * norm_gain
    plain = jnp.mean(scaled_grad, -1, keepdims=True)
    cross = jnp.mean(scaled_grad * scaled, -1, keepdims=True)
    return inverse * (scaled_grad - plain - scaled * cross)


FREE = pl.CostEstimate(flops=1, transcendentals=0, bytes_accessed=1)


def dot_nn(left, right):
    return lax.dot_general(left, right, (((1,), (0,)), ((), ())), preferred_element_type=F32)


def dot_nt(left, right):
    return lax.dot_general(left, right, (((1,), (1,)), ((), ())), preferred_element_type=F32)


def dot_tn(left, right):
    return lax.dot_general(left, right, (((0,), (0,)), ((), ())), preferred_element_type=F32)


def head_weights(query, key, lanes, which):
    mine = jnp.where(lanes == which, query, jnp.zeros_like(query))
    scores = dot_nt(mine, key) * (1.0 / math.sqrt(HEAD_SIZE))
    weights = jnp.exp(scores - jnp.max(scores, -1, keepdims=True))
    return weights / jnp.sum(weights, -1, keepdims=True)


def pair_cols(refs, p, rows):
    ref = refs[p * 2 * HEAD_SIZE // refs[0].shape[1]]
    start = p * 2 * HEAD_SIZE % refs[0].shape[1]
    return ref[rows, start : start + 2 * HEAD_SIZE]


def cross_forward_body(width_block, place, rows, own, got, far, norms, q0, q1, q2, q3,
                       c0, c1, c2, c3, o0, o1, o2, o3,
                       front, queries, first, second, normed_three,
                       flip_own, flip_away):
    width = rows.shape[1]
    kv = (c0, c1, c2, c3)
    context_rows = c0.shape[0] // 2
    key_rows, value_rows = slice(0, context_rows), slice(context_rows, 2 * context_rows)
    lanes = lax.broadcasted_iota(jnp.int32, (rows.shape[0], 2 * HEAD_SIZE), 1) // HEAD_SIZE
    residual = (
        rows[...].astype(F32) + own[...] + got[...].astype(F32) + far[...].astype(F32)
    )
    first[...] = residual
    scaled, _ = normalize(residual)
    low = (scaled * norms[2:3, :] + norms[3:4, :]).astype(BF16)
    front[:, :width] = low
    part = width // 4
    for b, ref in enumerate((q0, q1, q2, q3)):
        queries[:, b * part : (b + 1) * part] = dot_nn(low, ref[...]).astype(BF16)
    for p in range(width // (2 * HEAD_SIZE)):
        cols = slice(p * 2 * HEAD_SIZE, (p + 1) * 2 * HEAD_SIZE)
        q, k, v = queries[:, cols], pair_cols(kv, p, key_rows), pair_cols(kv, p, value_rows)
        mixed = [dot_nn(head_weights(q, k, lanes, g).astype(BF16), v) for g in (0, 1)]
        front[:, width + cols.start : width + cols.stop] = jnp.where(lanes == 0, mixed[0], mixed[1]).astype(BF16)
    for b, ref in enumerate((o0, o1, o2, o3)):
        residual = residual + dot_nn(front[:, width + b * part : width + (b + 1) * part], ref[...])
    second[...] = residual
    scaled, _ = normalize(residual)
    low = (scaled * norms[4:5, :] + norms[5:6, :]).astype(BF16)
    normed_three[...] = low
    deal_rows(low.T, width_block, place[0], flip_own, flip_away)


def cross_forward(devices, place, rows, own, got, far, norms, query_parts, kv_parts, out_parts):
    size, width = rows.shape
    low = jax.ShapeDtypeStruct(rows.shape, BF16)
    both = jax.ShapeDtypeStruct((size, 2 * width), BF16)
    wide = jax.ShapeDtypeStruct(rows.shape, F32)
    flip = jax.ShapeDtypeStruct((width // 2, size), BF16)
    vmem = pl.BlockSpec(memory_space=pltpu.VMEM)
    block = pl.BlockSpec((size, width), lambda i: (0, 0))
    return pl.pallas_call(
        functools.partial(cross_forward_body, width // devices),
        grid=(1,),
        in_specs=[pl.BlockSpec(memory_space=pltpu.SMEM)] + [block] * 4 + [vmem] * 13,
        out_shape=[both, low, wide, wide, low, flip, flip],
        cost_estimate=FREE, name="cross",
    )(place, rows, own, got, far, norms, *query_parts, *kv_parts, *out_parts)


def deal_rows(rows, size, column, own, away):
    for b in range(rows.shape[0] // (2 * size)):
        at = slice(b * size, (b + 1) * size)
        even = rows[2 * b * size : (2 * b + 1) * size, :]
        odd = rows[(2 * b + 1) * size : (2 * b + 2) * size, :]

        @pl.when(column == 0)
        def _():
            own[at, :] = even
            away[at, :] = odd

        @pl.when(column != 0)
        def _():
            own[at, :] = odd
            away[at, :] = even


def ffn_part(normed, grad, gate_w, up_w, down_w, hidden, hid_own, hid_away, gate_grad, lifted_grad,
             unit_block, column):
    gate = dot_nn(normed, gate_w[...])
    lifted = dot_nn(normed, up_w[...])
    back = dot_nt(grad, down_w[...]).astype(BF16).astype(F32)
    sig = jax.nn.sigmoid(gate)
    swish = gate * sig
    made = (swish * lifted).astype(BF16)
    hidden[...] = made
    deal_rows(made.T, unit_block, column, hid_own, hid_away)
    gg = (back * lifted * sig * (1.0 + gate * (1.0 - sig))).astype(BF16)
    lg = (back * swish).astype(BF16)
    gate_grad[...] = gg
    lifted_grad[...] = lg
    return dot_nt(gg, gate_w[...]) + dot_nt(lg, up_w[...])


def ffn_first_body(unit_block, place, n0, n1, n2, n3, g0, g1, g2, g3, gate_w, up_w, down_w,
                   hidden, hid_own, hid_away, gate_grad, lifted_grad, normed, grad, grad_pair,
                   total):
    share, part = n0.shape[0], g0.shape[2]
    for b, ref in enumerate((n0, n1, n2, n3)):
        normed[b * share : (b + 1) * share, :] = ref[...]
    for c, ref in enumerate((g0, g1, g2, g3)):
        for b in range(4):
            rows, cols = relative(place[1], b, share), relative(place[1], c, part)
            grad[b * share : (b + 1) * share, cols] = ref[0, rows, :]
            grad_pair[b * share : (b + 1) * share, cols] = ref[1, rows, :]
    total[...] = ffn_part(
        normed[...], grad[...], gate_w, up_w, down_w, hidden, hid_own, hid_away, gate_grad,
        lifted_grad, unit_block, place[0],
    )


def ffn_second_body(unit_block, place, normed, grad, total, gate_w, up_w, down_w,
                    hidden, hid_own, hid_away, gate_grad, lifted_grad, away, own, low):
    share = own.shape[0]
    found = total[...] + ffn_part(
        normed[...], grad[...], gate_w, up_w, down_w, hidden, hid_own, hid_away, gate_grad,
        lifted_grad, unit_block, place[0],
    )
    own[...] = found[:share, :]
    low[...] = found[2 * share : 3 * share, :].astype(BF16)
    away[:share, :] = found[share : 2 * share, :].astype(BF16)
    away[share:, :] = found[3 * share :, :].astype(BF16)


def ffn(devices, place, half, inputs, gate_w, up_w, down_w):
    share = inputs[0].shape[0] if half == 0 else inputs[0].shape[0] // 4
    width = inputs[0].shape[1]
    size, units = 4 * share, gate_w.shape[1]
    tile = units // 2
    low = lambda *dims: jax.ShapeDtypeStruct(dims, BF16)
    wide = lambda *dims: jax.ShapeDtypeStruct(dims, F32)
    vmem = pl.BlockSpec(memory_space=pltpu.VMEM)
    cols = pl.BlockSpec((width, tile), lambda i: (0, half))
    rows = pl.BlockSpec((tile, width), lambda i: (half, 0))
    made = [low(size, tile), low(tile // 2, size), low(tile // 2, size), low(size, tile),
            low(size, tile)]
    if half == 0:
        made += [low(size, width), low(size, width), low(size, width), wide(size, width)]
    else:
        made += [low(2 * share, width), wide(share, width), low(share, width)]
    return pl.pallas_call(
        functools.partial(ffn_second_body if half else ffn_first_body, units // devices),
        grid=(1,),
        in_specs=[pl.BlockSpec(memory_space=pltpu.SMEM)] + [vmem] * len(inputs)
        + [cols, cols, rows],
        out_specs=[vmem] * len(made),
        out_shape=made,
        cost_estimate=FREE, name="ffn",
    )(place, *inputs, gate_w, up_w, down_w)


def cross_backward_body(own, got, far, grad, first, second, norms, q0, q1, q2, q3,
                        c0, c1, c2, c3, o0, o1, o2, o3, queries,
                        back_rows, kv_grad, vectors, grad_one, crossed_grad):
    width = grad.shape[1]
    kv = (c0, c1, c2, c3)
    context_rows = c0.shape[0] // 2
    key_rows, value_rows = slice(0, context_rows), slice(context_rows, 2 * context_rows)
    part = width // 4
    lanes = lax.broadcasted_iota(jnp.int32, (grad.shape[0], 2 * HEAD_SIZE), 1) // HEAD_SIZE
    lane_k = lax.broadcasted_iota(jnp.int32, (context_rows, 2 * HEAD_SIZE), 1) // HEAD_SIZE
    scale = 1.0 / math.sqrt(HEAD_SIZE)
    arrived = own[...] + got[...].astype(F32) + far[...].astype(F32)
    scaled, inverse = normalize(second[...])
    vectors[0:1, :] = jnp.sum(arrived * scaled, 0, keepdims=True)
    vectors[1:2, :] = jnp.sum(arrived, 0, keepdims=True)
    two = grad[...].astype(F32) + norm_backward(arrived, scaled, inverse, norms[4:5, :])
    low = two.astype(BF16)
    back_rows[:, :width] = low
    for b, ref in enumerate((o0, o1, o2, o3)):
        crossed_grad[:, b * part : (b + 1) * part] = dot_nt(low, ref[...]).astype(BF16)
    for p in range(width // (2 * HEAD_SIZE)):
        cols = slice(p * 2 * HEAD_SIZE, (p + 1) * 2 * HEAD_SIZE)
        q, k, v = queries[:, cols], pair_cols(kv, p, key_rows), pair_cols(kv, p, value_rows)
        g_rows = crossed_grad[:, cols]
        found = []
        for g in (0, 1):
            probs = head_weights(q, k, lanes, g)
            change = dot_nt(jnp.where(lanes == g, g_rows, jnp.zeros_like(g_rows)), v)
            delta = jnp.sum(change * probs, -1, keepdims=True)
            ds = (probs * (change - delta)).astype(BF16)
            found.append((dot_nn(ds, k), dot_tn(ds, q), dot_tn(probs.astype(BF16), g_rows)))
        back_rows[:, width + cols.start : width + cols.stop] = (
            jnp.where(lanes == 0, found[0][0], found[1][0]) * scale
        ).astype(BF16)
        kv_grad[:context_rows, cols] = (
            jnp.where(lane_k == 0, found[0][1], found[1][1]) * scale
        ).astype(BF16)
        kv_grad[context_rows:, cols] = jnp.where(lane_k == 0, found[0][2], found[1][2]).astype(
            BF16
        )
    back = jnp.zeros(grad.shape, F32)
    for b, ref in enumerate((q0, q1, q2, q3)):
        back = back + dot_nt(back_rows[:, width + b * part : width + (b + 1) * part], ref[...])
    scaled, inverse = normalize(first[...])
    vectors[2:3, :] = jnp.sum(back * scaled, 0, keepdims=True)
    vectors[3:4, :] = jnp.sum(back, 0, keepdims=True)
    grad_one[...] = (two + norm_backward(back, scaled, inverse, norms[2:3, :])).astype(BF16)


def cross_backward(own, got, far, grad, first, second, norms, query_parts, kv_parts, out_parts,
                   queries):
    rows, width = own.shape
    low = lambda r: jax.ShapeDtypeStruct((r, width), BF16)
    block = pl.BlockSpec((rows, width), lambda i: (0, 0))
    return pl.pallas_call(
        cross_backward_body,
        grid=(1,),
        out_shape=[jax.ShapeDtypeStruct((rows, 2 * width), BF16), low(kv_parts[0].shape[0]),
                   jax.ShapeDtypeStruct((4, width), F32), low(rows)],
        in_specs=[block] * 6 + [pl.BlockSpec(memory_space=pltpu.VMEM)] * 14,
        scratch_shapes=[pltpu.VMEM((rows, width), BF16)],
        cost_estimate=FREE, name="cross_back",
    )(own, got, far, grad, first, second, norms, *query_parts, *kv_parts, *out_parts, queries)


def meet_rows_body(own_a, pair_a, own_b, pair_b, right, right_pair, out):
    count = own_a.shape[0]
    for b, (own, pair) in enumerate(((own_a, pair_a), (own_b, pair_b))):
        out[b * count : (b + 1) * count, :] = (
            dot_nn(own[...], right[...]) + dot_nn(pair[...], right_pair[...])
        ).astype(BF16)


def meet_rows(lefts, rights):
    count, size = lefts[0].shape
    width = rights[0].shape[1]
    tile = width // 3
    left = pl.BlockSpec((count, size), lambda i: (0, 0))
    right = pl.BlockSpec((size, tile), lambda i: (0, i))
    return pl.pallas_call(
        meet_rows_body,
        grid=(3,),
        in_specs=[left] * 4 + [right] * 2,
        out_specs=pl.BlockSpec((2 * count, tile), lambda i: (0, i)),
        out_shape=jax.ShapeDtypeStruct((2 * count, width), BF16),
        name="meet_rows", cost_estimate=FREE,
    )(*lefts, *rights)


def meet_cols_body(p0, p1, p2, p3, a, a_pair, b, b_pair, out):
    own, pair = (jnp.concatenate([p[i] for p in (p0, p1, p2, p3)], 1) for i in (0, 1))
    width = a.shape[1]
    out[:, :width] = (dot_nn(own, a[...]) + dot_nn(pair, a_pair[...])).astype(BF16)
    out[:, width:] = (dot_nn(own, b[...]) + dot_nn(pair, b_pair[...])).astype(BF16)


def meet_cols(near, rights):
    return pl.pallas_call(
        meet_cols_body,
        out_shape=jax.ShapeDtypeStruct((near[0].shape[1], 2 * rights[0].shape[1]), BF16),
        name="meet_cols", cost_estimate=FREE,
    )(*near, *rights)


def down_body(first, second, down_w, away, own, low):
    share, units = own.shape[0], first.shape[1]

    def sent(r):
        at = slice(r * share, (r + 1) * share)
        return dot_nn(first[at, :], down_w[:units, :]) + dot_nn(second[at, :], down_w[units:, :])

    away[:share, :] = sent(1).astype(BF16)
    away[share:, :] = sent(3).astype(BF16)
    low[...] = sent(2).astype(BF16)
    own[...] = sent(0)


def down_parts(first, second, down_w):
    share, width = first.shape[0] // 4, down_w.shape[1]
    low = lambda *dims: jax.ShapeDtypeStruct(dims, BF16)
    return pl.pallas_call(
        down_body,
        out_shape=[low(2 * share, width), jax.ShapeDtypeStruct((share, width), F32),
                   low(share, width)],
        name="down", cost_estimate=FREE,
    )(first, second, down_w)


def bundle_body(devices, place, f02, f13, b02, b13, a0, a1, a2, a3, attended,
                context, kv, out_a, out_b):
    width = a0.shape[1]
    part, share = width // 4, a0.shape[0]

    def near(even, odd):
        return even[0], odd[0], even[1], odd[1]

    own = lambda rows: jnp.concatenate(
        [row[:, width + r * part : width + (r + 1) * part] for r, row in enumerate(rows)], 0
    )
    full = lambda rows: jnp.concatenate([row[:, :width] for row in rows], 0)
    fronts, backs = near(f02, f13), near(b02, b13)
    rows = width // devices
    small = part // devices
    half = width // 2

    def put(block, base, left, out):
        for d in range(devices):
            at = slice(base, base + block.shape[0] // devices)
            piece = block[d * block.shape[0] // devices : (d + 1) * block.shape[0] // devices, :]
            out[d, at, left : left + block.shape[1]] = piece.astype(BF16)

    put(dot_tn(full(fronts), own(backs)), 0, 0, out_a)
    count = context.shape[0]
    put(dot_tn(context[...], kv[:count, :]), 0, part, out_a)
    put(dot_tn(context[...], kv[count:, :]), rows // 2, part, out_a)
    grads = dot_tn(own(fronts), full(backs))
    put(grads[:, :half], 0, 0, out_b)
    put(grads[:, half:], small, 0, out_b)
    grads = sum(
        dot_nn(attended[:, relative(place[0], r, share)], ref[...])
        for r, ref in enumerate((a0, a1, a2, a3))
    )
    put(grads[:, :half], 2 * small, 0, out_b)
    put(grads[:, half:], 3 * small, 0, out_b)


def bundle_grads(devices, place, fronts, backs, ones, attended, context, kv):
    width = ones[0].shape[1]
    vmem = pl.BlockSpec(memory_space=pltpu.VMEM)
    return pl.pallas_call(
        functools.partial(bundle_body, devices),
        in_specs=[pl.BlockSpec(memory_space=pltpu.SMEM)] + [vmem] * 11,
        out_specs=[vmem] * 2,
        out_shape=[jax.ShapeDtypeStruct((devices, width // devices, width // 2), BF16)] * 2,
        name="bundle", cost_estimate=FREE,
    )(place, *fronts, *backs, *ones, attended, context, kv)


def front_body(width_block, place, x0, x1, x2, x3, g0, g1, g2, g3, cosine, sine, wq, wk, wv,
               queries, pair, rows, low, nrm_own, nrm_away, norms, means, inverses, wide):
    size, part = x0.shape
    for r, (x, g) in enumerate(((x0, g0), (x1, g1), (x2, g2), (x3, g3))):
        start = pl.multiple_of((place[0] ^ r) * part, 128)
        wide[:, pl.ds(start, part)] = x[...]
        norms[:, pl.ds(start, part)] = g[...]
    share = size // 4
    rows[...] = wide[pl.ds(pl.multiple_of(place[0] * share, share), share), :]
    values = wide[...].astype(F32)
    mean = jnp.mean(values, -1, keepdims=True)
    centred = values - mean
    inverse = lax.rsqrt(jnp.mean(centred * centred, -1, keepdims=True) + 1e-05)
    means[...] = mean
    inverses[...] = inverse
    normed = (centred * inverse * norms[0:1, :] + norms[1:2, :]).astype(BF16)
    low[...] = normed
    half = HEAD_SIZE // 2

    def turned(weight):
        return dot_nn(normed, weight[...]).T

    def rotated(block, dest, scale):
        for h in range(part // HEAD_SIZE):
            a = block[h * HEAD_SIZE : h * HEAD_SIZE + half, :]
            b = block[h * HEAD_SIZE + half : (h + 1) * HEAD_SIZE, :]
            dest[h * HEAD_SIZE : h * HEAD_SIZE + half, :] = (
                (a * cosine[...] - b * sine[...]) * scale
            ).astype(BF16)
            dest[h * HEAD_SIZE + half : (h + 1) * HEAD_SIZE, :] = (
                (b * cosine[...] + a * sine[...]) * scale
            ).astype(BF16)

    rotated(turned(wk), pair.at[0], 1.0)
    pair[1] = turned(wv).astype(BF16)
    rotated(turned(wq), queries, 1.0 / math.sqrt(HEAD_SIZE))
    deal_rows(normed.T, width_block, place[1], nrm_own, nrm_away)


def front(devices, place, parts, norm_parts, tables, wq, wk, wv):
    size, part = parts[0].shape
    width = 4 * part
    low = lambda *s: jax.ShapeDtypeStruct(s, BF16)
    wide = lambda *s: jax.ShapeDtypeStruct(s, F32)
    vmem = pl.BlockSpec(memory_space=pltpu.VMEM)
    return pl.pallas_call(
        functools.partial(front_body, width // devices),
        in_specs=[pl.BlockSpec(memory_space=pltpu.SMEM)] + [vmem] * 13,
        out_specs=[vmem] * 9,
        out_shape=[low(part, size), low(2, part, size), low(size // 4, width), low(size, width),
                   low(width // 2, size), low(width // 2, size), wide(6, width),
                   wide(size, 1), wide(size, 1)],
        scratch_shapes=[pltpu.VMEM((size, width), BF16)],
        cost_estimate=FREE, name="front",
    )(place, *parts, *norm_parts, *tables, wq, wk, wv)


def per_device(
    frames,
    segment,
    time_token,
    context,
    gain_attn,
    bias_attn,
    gain_cross,
    bias_cross,
    gain_ffn,
    bias_ffn,
    w_query,
    w_key,
    w_value,
    w_out,
    c_query,
    c_key,
    c_value,
    c_out,
    w_gate,
    w_up,
    w_down,
    out_grad,
):
    local_rows = frames.shape[0]
    local_width = frames.shape[1]
    model_width = w_query.shape[0]
    head_cols = w_query.shape[1]
    heads = head_cols // HEAD_SIZE
    number_of_frames = lax.axis_size("seq") * local_rows
    row_length = min(max(ROW_MIN, 64 * lax.axis_size("seq")), number_of_frames)
    first_frame = lax.axis_index("seq") * local_rows
    own_start = lax.axis_index("tensor") * local_width

    def own_cols(value):
        return lax.dynamic_slice_in_dim(value, own_start, local_width, value.ndim - 1)

    place = lax.axis_index("tensor")
    share = local_rows // 4

    def row_block(value, index):
        return rows_of(value, index * share, share)

    column = lax.axis_index("seq") % 2
    frame_parts_near = gather_near(frames)
    norm_parts = gather_near(
        jnp.stack([gain_attn, bias_attn, gain_cross, bias_cross, gain_ffn, bias_ffn])
    )
    clip_starts, frame_positions = frame_clip_labels(segment, row_length)
    own_labels = lax.dynamic_slice_in_dim(clip_starts, first_frame, local_rows)
    own_positions = lax.dynamic_slice_in_dim(frame_positions, first_frame, local_rows)
    blanks = jnp.full((local_rows,), -1, jnp.int32)
    key_labels = lax.dynamic_slice_in_dim(
        jnp.concatenate([blanks, clip_starts, blanks]), first_frame, 3 * local_rows
    )
    spans = jnp.concatenate(
        [tile_ranges(own_labels, key_labels), place.astype(jnp.int32).reshape(1)]
    )
    places = jnp.stack([column, place]).astype(jnp.int32)
    label_row, label_column = own_labels[None, :], key_labels[:, None]
    row_index = first_frame // row_length
    time_row = lax.dynamic_slice_in_dim(time_token, row_index, 1, 0).astype(F32)
    row_context = lax.dynamic_slice_in_dim(context, row_index, 1, 0)[0]
    context_rows = row_context.shape[0]
    tables = rotary_tables(own_positions)
    score_scale = 1.0 / math.sqrt(HEAD_SIZE)
    all_heads = model_width // HEAD_SIZE

    (
        queries, both, frame_rows, frame_normed, one_own_half, one_away_half, norms, means_one,
        inverse_one,
    ) = front(
        lax.axis_size("seq"), jnp.flip(places), frame_parts_near, norm_parts, tables, w_query,
        w_key, w_value,
    )
    both, out_pair = meeting(both, swap(after(out_grad, frame_parts_near[2]), "seq", 1))
    grad_both = jnp.stack([out_grad, out_pair])
    gain_one, bias_one = norms[0:1], norms[1:2]
    behind, ahead = shift(both, "seq", 1), shift(both, "seq", -1)
    query_far = swap(after(c_query, frame_parts_near[3]), "tensor", 2)
    out_far = swap(after(c_out, frame_parts_near[3]), "tensor", 2)
    time_late = after(time_row, both)
    scaled_time, _ = normalize(time_late)
    time_normed = (scaled_time * gain_one + bias_one).astype(BF16)
    time_keys = by_feature(time_normed, w_key).astype(BF16).astype(F32)
    time_values = by_feature(time_normed, w_value).astype(BF16).astype(F32)
    context_late = after(row_context, both)
    context_kv = jnp.concatenate(
        [product(context_late, c_key), product(context_late, c_value)], 0
    ).astype(BF16)
    state = attend_near(spans, queries, both, time_keys, time_values, label_row, label_column)
    behind, ahead, query_far, out_far, *state = meeting(
        behind, ahead, query_far, out_far, *state
    )
    query_own, out_own, context_late = after((c_query, c_out, context_kv), behind)
    weights_near = [
        swap(value, "tensor", 1) for value in (query_own, query_far, out_own, out_far)
    ]
    kv_far = swap(context_late, "tensor", 2)
    attended, log_totals, one_away, one_own, one_low = attend_far(
        spans, queries, behind, ahead, label_row, label_column, w_out, state
    )
    one_away, one_low, kv_far, *weights_near = meeting(one_away, one_low, kv_far, *weights_near)
    kv_both = jnp.concatenate([context_kv, kv_far], 0)
    kv_other = swap(kv_both, "tensor", 1)
    kv_rows = context_kv.shape[0]
    kv_parts = (context_kv, kv_other[:kv_rows], kv_far, kv_other[kv_rows:])
    query_parts = (c_query, weights_near[0], query_far, weights_near[1])
    out_parts = (c_out, weights_near[2], out_far, weights_near[3])
    one_got, _, one_far = scatter_near(one_away, one_low)
    (
        front_rows, cross_queries, residual_one, residual_two, normed_share, flip_own, flip_away,
    ) = cross_forward(
        lax.axis_size("seq"), places, frame_rows, one_own, one_got, one_far, norms,
        query_parts, kv_parts, out_parts,
    )
    grad_far = swap(after(grad_both, one_far), "tensor", 2)
    normed_share, normed_got, grad_far = meeting(
        normed_share, swap(after(one_away_half, one_low), "seq", 1), grad_far
    )
    grad_late, grad_far_late = after((grad_both, grad_far), normed_share)
    grad_mate, grad_far_mate = swap(grad_late, "tensor", 1), swap(grad_far_late, "tensor", 1)
    grad_parts = (grad_both, grad_mate, grad_far, grad_far_mate)
    three_parts = gather_near(normed_share)
    flip_got = swap(after(flip_away, normed_share), "seq", 1)
    front_far = swap(after(front_rows, three_parts[3]), "tensor", 2)
    devices = lax.axis_size("seq")
    (
        hidden_a, hidden_own_a, hidden_away_a, gate_a, lifted_a, normed_three, grad_near, grad_pair,
        ffn_total,
    ) = ffn(devices, places, 0, (*three_parts, *grad_parts), w_gate, w_up, w_down)
    ffn_total, flip_got = meeting(ffn_total, flip_got)
    flip_both = jnp.stack([flip_own, flip_got])
    flip_far = swap(flip_both, "tensor", 2)
    hidden_got_a, gate_got_a = swap(hidden_away_a, "seq", 1), swap(gate_a, "seq", 1)
    hidden_b, hidden_own_b, hidden_away_b, gate_b, lifted_b, three_away, three_own, three_low = ffn(
        devices, places, 1, (normed_three, grad_near, ffn_total), w_gate, w_up, w_down
    )
    three_away, three_low, flip_far, front_far, hidden_got_a = meeting(
        three_away, three_low, flip_far, front_far, hidden_got_a
    )
    three_got, _, three_far = scatter_near(three_away, three_low)
    hidden_late, lifted_late = after((hidden_away_b, lifted_a), three_low)
    hidden_got_b, lifted_got_a = swap(hidden_late, "seq", 1), swap(lifted_late, "seq", 1)
    flip_late, flip_far_late, gate_late = after((flip_both, flip_far, gate_b), three_far)
    flip_mate, flip_far_mate = swap(flip_late, "tensor", 1), swap(flip_far_late, "tensor", 1)
    gate_got_b = swap(gate_late, "seq", 1)
    front_both = jnp.stack([front_rows, front_far])
    back_rows, kv_grad, norm_vectors, grad_one = cross_backward(
        three_own, three_got, three_far, grad_near, residual_one, residual_two, norms,
        query_parts, kv_parts, out_parts, cross_queries,
    )
    grad_one, gate_got_a, hidden_got_b, lifted_got_a, flip_mate, flip_far_mate = meeting(
        grad_one, gate_got_a, hidden_got_b, lifted_got_a, flip_mate, flip_far_mate
    )
    count = lax.axis_size("seq")

    def by_level(blocks):
        return blocks.reshape(count // 2, 2 * blocks.shape[0] // count, blocks.shape[1])

    down_keep, down_got = halve(
        by_level(
            meet_rows(
                (hidden_own_a, hidden_got_a, hidden_own_b, hidden_got_b), (grad_near, grad_pair)
            )
        ),
        1,
    )
    context_parts = quarters(kv_grad, 1)
    context_got = swap(jnp.concatenate([context_parts[1], context_parts[3]], 0), "tensor", 1)
    *one_parts, front_other, context_got, gate_got_b = meeting(
        *gather_near(grad_one), swap(after(front_both, grad_one), "tensor", 1), context_got,
        gate_got_b,
    )
    context_low = (
        context_parts[2].astype(F32) + context_got[context_parts[2].shape[0] :].astype(F32)
    ).astype(BF16)
    context_far = swap(context_low, "tensor", 2)
    back_far = swap(after(back_rows, one_parts[3]), "tensor", 2)
    lifted_got_b = swap(after(lifted_b, grad_one), "seq", 1)
    query_grad, to_prev, kept, to_next, time_key_grad, time_value_grad = attend_back(
        spans, queries, (behind, both, ahead), time_keys, time_values, label_row, label_column,
        w_out, attended, log_totals, one_parts,
    )
    to_prev, to_next, back_far, lifted_got_b, down_got, context_far = meeting(
        to_prev, to_next, back_far, lifted_got_b, down_got, context_far
    )
    time_both = jnp.concatenate([time_key_grad, time_value_grad], 0)
    time_got = swap(after(time_both, to_prev), "seq", 1)
    from_next, from_prev = shift(to_prev, "seq", -1), shift(to_next, "seq", 1)
    down_keep, down_got = halve(added(down_keep, down_got).astype(BF16), 2)
    flip_near = (flip_both, flip_mate, flip_far, flip_far_mate)
    first_keep, first_got = halve(
        by_level(meet_cols(flip_near, after((gate_a, gate_got_a, lifted_a, lifted_got_a), to_prev))),
        1,
    )
    down_away, down_own, down_low = down_parts(after(hidden_a, to_prev), hidden_b, w_down)
    back_both = jnp.stack([back_rows, back_far])
    back_other = swap(back_both, "tensor", 1)
    context_own = (
        context_parts[0].astype(F32)
        + context_got[: context_far.shape[0]].astype(F32)
        + context_far.astype(F32)
    )
    bundle_a, bundle_b = bundle_grads(
        count, places[1:], (front_both, front_other), (back_both, back_other), one_parts, attended,
        row_context,
        context_own.astype(BF16),
    )
    from_next, from_prev, bundle_a, bundle_b, time_got = meeting(
        from_next, from_prev, bundle_a, bundle_b, time_got
    )
    keep_a, got_a = halve(bundle_a, 0)
    raw, last_away, last_own, last_low = tail(
        places[1:], query_grad, kept, from_next, from_prev, tables, w_query, w_key, w_value
    )
    last_got = swap(last_away, "tensor", 1)
    raw_got = swap(raw, "seq", 1)
    last_sum = (
        last_low.astype(F32) + last_got[local_rows:].astype(F32)
    ).astype(BF16)
    last_sum, first_got, down_got = meeting(last_sum, first_got, down_got)
    first_keep, first_got = halve(added(first_keep, first_got).astype(BF16), 2)
    second = by_level(
        meet_cols(flip_near, after((gate_b, gate_got_b, lifted_b, lifted_got_b), from_next))
    )
    second_keep, second_got = halve(second, 1)
    last_far = swap(last_sum, "tensor", 2)
    last_far, got_a = meeting(last_far, got_a)
    keep_b, got_b = halve(after(bundle_b, last_far), 0)
    frame_grad = last_own + last_got[:local_rows].astype(F32) + last_far.astype(F32)

    def to_frames(rows, weight):
        return jnp.einsum("fn,df->nd", rows, weight, preferred_element_type=F32)

    time_key_grad, time_value_grad = after((time_key_grad, time_value_grad), from_next)
    time_grad = to_frames(time_key_grad.astype(BF16), w_key) + to_frames(
        time_value_grad.astype(BF16), w_value
    )
    own_scaled = (frames.astype(F32) - means_one) * inverse_one
    scaled_grad = frame_grad * gain_attn[None]
    sums = jnp.concatenate(
        [
            jnp.sum(scaled_grad, -1),
            jnp.sum(scaled_grad * own_scaled, -1),
            time_grad[0],
            norm_vectors.reshape(-1),
        ]
    )[None]
    sums = sums + swap(sums, "tensor", 1)
    sums = sums + swap(sums, "tensor", 2)
    sums, second_got = meeting(sums, second_got)
    plain = sums[0, :local_rows, None] / model_width
    cross = sums[0, local_rows : 2 * local_rows, None] / model_width
    vectors = own_cols(sums[0, 2 * local_rows :].reshape(5, model_width))
    attend_full = ordered(*[after(one_parts, from_next)[i] for i in (0, 2, 1, 3)], 0)
    d_frames = own_cols(attend_full).astype(F32) + inverse_one * (
        scaled_grad - plain - own_scaled * cross
    )
    d_gain_attn = jnp.sum(frame_grad * own_scaled, 0) + vectors[0] * own_cols(scaled_time)[0]
    d_bias_attn = jnp.sum(frame_grad, 0) + vectors[0]
    small = jnp.stack(
        [d_gain_attn, d_bias_attn, vectors[3], vectors[4], vectors[1], vectors[2]]
    ).reshape(6, devices, -1).transpose(1, 0, 2)
    small = added(*halve(small, 0))
    small, first_got = meeting(small, first_got)
    small = added(*halve(small, 1))
    small, raw_got = meeting(small, raw_got)
    bit = 2
    while small.shape[0] > 1:
        small = added(*halve(small, bit))
        bit += 1
    small = small[0]

    down_away, down_low = after((down_away, down_low), last_far)
    branch_got, _, branch_far = scatter_near(down_away, down_low)
    block_rows = (
        residual_two + down_own + branch_got[:share].astype(F32) + branch_far.astype(F32)
    ).astype(BF16)
    block_cols = rows_to_cols(
        *[
            lax.dynamic_slice_in_dim(block_rows, (place ^ r) * local_width, local_width, 1)
            for r in range(4)
        ],
        from_next,
    )
    block_out = jnp.concatenate([row_block(block_cols, place ^ b) for b in range(4)], 0)

    time_column = time_normed.astype(F32).T

    normed_pair = (one_own_half, normed_got)
    grad_down = halve_end(down_keep, down_got, 3)
    first, second = halve_end(first_keep, first_got, 3), halve_end(second_keep, second_got, 2)
    units = first.shape[1] // 2
    grad_gate_w = jnp.concatenate([first[:, :units], second[:, :units]], 1)
    grad_up_w = jnp.concatenate([first[:, units:], second[:, units:]], 1)
    left, right = halve_end(keep_a, got_a, 1), halve_end(keep_b, got_b, 1)
    part, rows = head_cols // count, model_width // count
    grad_c_query = left[:, :head_cols]
    grad_c_key, grad_c_value = left[: rows // 2, head_cols:], left[rows // 2 :, head_cols:]
    grad_c_out = jnp.concatenate([right[:part], right[part : 2 * part]], 1)
    grad_w_out = jnp.concatenate([right[2 * part : 3 * part], right[3 * part :]], 1)

    raw_pair = (raw, raw_got)
    time_both = time_both + time_got
    own_time_rows = lax.dynamic_index_in_dim(
        time_column.reshape(count // 2, 2, -1), column, 1, False
    ).reshape(-1, 1)
    outer = own_time_rows * jnp.concatenate([jnp.zeros((head_cols, 1), F32), time_both], 0).T
    blocks = sum(
        jnp.einsum("dn,fn->df", r, c, preferred_element_type=F32)
        for r, c in zip(normed_pair, raw_pair)
    )
    blocks = by_level((blocks + outer).astype(BF16))
    heads_sum = halve_all(blocks, 1)
    grad_w_query, grad_w_key, grad_w_value = (
        heads_sum[:, i * head_cols : (i + 1) * head_cols] for i in range(3)
    )
    return (
        block_out,
        d_frames,
        small[0],
        small[1],
        small[2],
        small[3],
        small[4],
        small[5],
        grad_w_query,
        grad_w_key,
        grad_w_value,
        grad_w_out,
        grad_c_query,
        grad_c_key,
        grad_c_value,
        grad_c_out,
        grad_gate_w,
        grad_up_w,
        grad_down,
    )


def solution(mesh):
    return jax.shard_map(
        per_device,
        mesh=mesh,
        in_specs=(
            P("seq", "tensor"),
            P(),
            P(),
            P(),
            P("tensor"),
            P("tensor"),
            P("tensor"),
            P("tensor"),
            P("tensor"),
            P("tensor"),
            P(None, "tensor"),
            P(None, "tensor"),
            P(None, "tensor"),
            P("tensor", None),
            P(None, "tensor"),
            P(None, "tensor"),
            P(None, "tensor"),
            P("tensor", None),
            P(None, "tensor"),
            P(None, "tensor"),
            P("tensor", None),
            P("seq", "tensor"),
        ),
        out_specs=(
            P("seq", "tensor"),
            P("seq", "tensor"),
            P(("tensor", "seq")),
            P(("tensor", "seq")),
            P(("tensor", "seq")),
            P(("tensor", "seq")),
            P(("tensor", "seq")),
            P(("tensor", "seq")),
            P("seq", "tensor"),
            P("seq", "tensor"),
            P("seq", "tensor"),
            P(("tensor", "seq"), None),
            P("seq", "tensor"),
            P("seq", "tensor"),
            P("seq", "tensor"),
            P(("tensor", "seq"), None),
            P("seq", "tensor"),
            P("seq", "tensor"),
            P(("tensor", "seq"), None),
        ),
        check_vma=False,
    )
```

```python
import functools
import math

import jax
import jax.numpy as jnp
from jax import lax
from jax.experimental import pallas as pl
from jax.experimental.pallas import tpu as pltpu
from jax.sharding import PartitionSpec as P

HEAD_SIZE = 64
ROW_MIN = 2048
TILE = 256
BF16 = jnp.bfloat16
F32 = jnp.float32


def meeting(*values):
    return lax.optimization_barrier(values)


def after(value, token):
    return lax.optimization_barrier((value, token))[0]


def swap(value, axis, by):
    return lax.ppermute(value, axis, [(i, i ^ by) for i in range(lax.axis_size(axis))])


def shift(value, axis, by):
    peers = lax.axis_size(axis)
    pairs = [(i, i + by) for i in range(peers) if 0 <= i + by < peers]
    return lax.ppermute(value, axis, pairs)


def tensor_place():
    place = lax.axis_index("tensor")
    return place // 2, place % 2


def ordered(own, far, mate, far_mate, axis):
    side, core = tensor_place()
    near = (jnp.where(core == 0, own, mate), jnp.where(core == 0, mate, own))
    away = (jnp.where(core == 0, far, far_mate), jnp.where(core == 0, far_mate, far))
    low = [jnp.where(side == 0, n, a) for n, a in zip(near, away)]
    high = [jnp.where(side == 0, a, n) for n, a in zip(near, away)]
    return jnp.concatenate(low + high, axis)


def gather_near(own):
    far = swap(own, "tensor", 2)
    return own, swap(own, "tensor", 1), far, swap(far, "tensor", 1)


def gather_staged(own, first, second):
    far = swap(after(own, first), "tensor", 2)
    far, late = after((far, own), second)
    return own, swap(late, "tensor", 1), far, swap(far, "tensor", 1)


def gather(own, axis):
    own, mate, far, far_mate = gather_near(own)
    return ordered(own, far, mate, far_mate, axis)


def scatter_near(away, low):
    got = swap(away, "tensor", 1)
    total = (low.astype(F32) + got[low.shape[0] :].astype(F32)).astype(BF16)
    return got, total, swap(total, "tensor", 2)


def rows_to_cols(own, mate, far, far_mate, later):
    width = own.shape[1]
    got = after(swap(jnp.concatenate([far, far_mate], 1), "tensor", 2), later)
    other = swap(jnp.concatenate([mate, got[:, width:]], 0), "tensor", 1)
    size = own.shape[0]
    return jnp.concatenate([own, other[:size], got[:, :width], other[size:]], 0)


def quarters(value, axis):
    return jnp.split(value, 4, axis)


def own_blocks(near):
    return jnp.concatenate([quarters(value, 1)[r] for r, value in enumerate(near)], 0)


def trade(value, start, done):
    return after(swap(after(value, start), "seq", 1), done)


def halve(blocks, bit):
    count, rows, cols = blocks.shape
    side = (lax.axis_index("seq") >> bit) % 2
    parts = blocks.reshape(count // 2, 2, rows, cols)
    send = lax.dynamic_index_in_dim(parts, 1 - side, 1, False)
    keep = lax.dynamic_index_in_dim(parts, side, 1, False)
    return keep, swap(send, "seq", 1 << bit)


def added(keep, got):
    return keep.astype(F32) + got.astype(F32)


def halve_all(blocks, bit):
    while blocks.shape[0] > 1:
        blocks = added(*halve(blocks.astype(BF16), bit))
        bit += 1
    return blocks[0].astype(F32)


def halve_end(keep, got, bit):
    return halve_all(added(keep, got), bit)


def frame_clip_labels(segment, row_length):
    frame_index = jnp.arange(segment.shape[0], dtype=jnp.int32)
    border = (frame_index % row_length == 0) | (segment != jnp.roll(segment, 1))
    clip_starts = lax.cummax(jnp.where(border, frame_index, 0), axis=0)
    return (clip_starts, (frame_index - clip_starts + 1).astype(jnp.float32))


def tile_ranges(q_labels, key_labels):
    q = q_labels.reshape(-1, TILE)
    k = key_labels.reshape(-1, TILE)
    meets = (k[None, :, 0] <= q[:, None, -1]) & (k[None, :, -1] >= q[:, None, 0])
    index = jnp.arange(k.shape[0], dtype=jnp.int32)[None]
    low = jnp.min(jnp.where(meets, index, k.shape[0]), 1)
    high = jnp.max(jnp.where(meets, index + 1, 0), 1)
    return jnp.stack([low, high], 1).reshape(-1)

def head_rows(g):
    return slice(g * HEAD_SIZE, (g + 1) * HEAD_SIZE)

def fill_natural(dest, refs, which):
    size = refs[0].shape[2]
    for part, ref in enumerate(refs):
        dest[part * size : (part + 1) * size, :] = ref[which].T


def fill_tiles(dest, refs, which):
    pieces = refs[0].shape[2] // TILE
    for part, ref in enumerate(refs):
        for piece in range(pieces):
            dest[part * pieces + piece] = ref[which, :, piece * TILE : (piece + 1) * TILE]


def relative(place, r, size):
    return pl.ds(pl.multiple_of((place ^ r) * size, size), size)


def absorb(state, start, stop, base, q, cols, lab, klab, keys, vals):
    group = q.shape[0] // HEAD_SIZE

    def step(j, state):
        seen = klab[pl.ds(pl.multiple_of(j * TILE, TILE), TILE), :] == lab
        at = pl.ds(pl.multiple_of((j - base) * TILE, TILE), TILE)
        fresh = []
        for g in range(group):
            top, total, acc = state[3 * g : 3 * g + 3]
            s = dot_nn(keys[at, head_rows(g)], q[head_rows(g), cols])
            s = jnp.where(seen, s, -1e30)
            new = jnp.maximum(top, jnp.max(s, 0, keepdims=True))
            fade = jnp.exp(top - new)
            p = jnp.exp(s - new)
            total = total * fade + jnp.sum(p, 0, keepdims=True)
            acc = acc * fade + dot_nn(vals[j - base, head_rows(g), :], p.astype(BF16))
            fresh += [new, total, acc]
        return tuple(fresh)

    return lax.fori_loop(start, stop, step, tuple(state))


def near_body(span, q, kv, tk, tv, qlab, klab, tops, totals, mix, keys, vals):
    rows, size = q.shape
    pieces = size // TILE
    fill_natural(keys, (kv,), 0)
    fill_tiles(vals, (kv,), 1)
    for tile in range(pieces):
        cols = slice(tile * TILE, (tile + 1) * TILE)
        state = []
        for g in range(rows // HEAD_SIZE):
            part = q[head_rows(g), cols].astype(F32)
            top = jnp.sum(part * tk[head_rows(g), :], 0, keepdims=True)
            state += [
                top,
                jnp.ones_like(top),
                jnp.broadcast_to(tv[head_rows(g), :], (HEAD_SIZE, TILE)),
            ]
        start = jnp.maximum(span[2 * tile], pieces)
        stop = jnp.minimum(span[2 * tile + 1], 2 * pieces)
        state = absorb(state, start, stop, pieces, q, cols, qlab[:, cols], klab, keys, vals)
        for g in range(rows // HEAD_SIZE):
            tops[g : g + 1, cols], totals[g : g + 1, cols], mix[head_rows(g), cols] = state[
                3 * g : 3 * g + 3
            ]


def far_body(span, q, kv0, kv2, qlab, klab, w_out, tops, totals, mix,
             out, lse, away, own, low, keys0, keys2, vals0, vals2):
    rows, size = q.shape
    pieces = size // TILE
    for kv, keys, vals in ((kv0, keys0, vals0), (kv2, keys2, vals2)):
        fill_natural(keys, (kv,), 0)
        fill_tiles(vals, (kv,), 1)
    for tile in range(pieces):
        cols = slice(tile * TILE, (tile + 1) * TILE)
        lab = qlab[:, cols]
        state = []
        for g in range(rows // HEAD_SIZE):
            state += [tops[g : g + 1, cols], totals[g : g + 1, cols], mix[head_rows(g), cols]]
        stop = jnp.minimum(span[2 * tile + 1], pieces)
        state = absorb(state, span[2 * tile], stop, 0, q, cols, lab, klab, keys0, vals0)
        start = jnp.maximum(span[2 * tile], 2 * pieces)
        state = absorb(
            state, start, span[2 * tile + 1], 2 * pieces, q, cols, lab, klab, keys2, vals2
        )
        for g in range(rows // HEAD_SIZE):
            top, total, acc = state[3 * g : 3 * g + 3]
            out[head_rows(g), cols] = (acc / total).astype(BF16)
            lse[g : g + 1, cols] = top + jnp.log(total)
    place = span[2 * pieces]
    share = own.shape[0]

    def sent(r):
        return dot_tn(out[:, relative(place, r, share)], w_out[...])

    away[:share, :] = sent(1).astype(BF16)
    away[share:, :] = sent(3).astype(BF16)
    low[...] = sent(2).astype(BF16)
    own[...] = sent(0)


def backward_body(span, q, kv0, kv1, kv2, tk, tv, qlab, klab, w_out, out, lse,
                  g0, g1, g2, g3, dq, to_prev, kept, to_next, dtk, dtv,
                  og, keys, vals, tkeys, ak, av):
    rows, size = q.shape
    group = rows // HEAD_SIZE
    pieces = size // TILE
    share = g0.shape[0]
    for r, ref in enumerate((g0, g1, g2, g3)):
        og[:, relative(span[2 * pieces], r, share)] = dot_nt(w_out[...], ref[...]).astype(BF16)
    fill_natural(keys, (kv0, kv1, kv2), 0)
    fill_natural(vals, (kv0, kv1, kv2), 1)
    fill_tiles(tkeys, (kv0, kv1, kv2), 0)
    ak[...] = jnp.zeros_like(ak)
    av[...] = jnp.zeros_like(av)
    for tile in range(pieces):
        cols = slice(tile * TILE, (tile + 1) * TILE)
        lab = qlab[:, cols]
        state, norms, deltas = [], [], []
        for g in range(group):
            hr = head_rows(g)
            qf = q[hr, cols].astype(F32)
            gf = og[hr, cols].astype(F32)
            norm = lse[g : g + 1, cols]
            delta = jnp.sum(gf * out[hr, cols].astype(F32), 0, keepdims=True)
            pt = jnp.exp(jnp.sum(qf * tk[hr, :], 0, keepdims=True) - norm)
            st = pt * (jnp.sum(gf * tv[hr, :], 0, keepdims=True) - delta)
            gk = jnp.sum(qf * st, 1, keepdims=True)
            gv = jnp.sum(gf * pt, 1, keepdims=True)
            if tile == 0:
                dtk[hr, :] = gk
                dtv[hr, :] = gv
            else:
                dtk[hr, :] += gk
                dtv[hr, :] += gv
            state.append(tk[hr, :] * st)
            norms.append(norm)
            deltas.append(delta)

        def step(j, state):
            start = pl.multiple_of(j * TILE, TILE)
            seen = klab[pl.ds(start, TILE), :] == lab
            fresh = []
            for g in range(group):
                hr = head_rows(g)
                s = dot_nn(keys[pl.ds(start, TILE), hr], q[hr, cols])
                p = jnp.exp(jnp.where(seen, s, -1e30) - norms[g])
                m = dot_nn(vals[pl.ds(start, TILE), hr], og[hr, cols])
                ds = (p * (m - deltas[g])).astype(BF16)
                av[j, hr, :] += dot_nt(og[hr, cols], p.astype(BF16))
                ak[j, hr, :] += dot_nt(q[hr, cols], ds)
                fresh.append(state[g] + dot_nn(tkeys[j, hr, :], ds))
            return tuple(fresh)

        state = lax.fori_loop(span[2 * tile], span[2 * tile + 1], step, tuple(state))
        for g in range(group):
            dq[head_rows(g), cols] = state[g]
    for part, dest in enumerate((to_prev, kept, to_next)):
        for piece in range(pieces):
            at = slice(piece * TILE, (piece + 1) * TILE)
            dest[0, :, at] = ak[part * pieces + piece].astype(dest.dtype)
            dest[1, :, at] = av[part * pieces + piece].astype(dest.dtype)


def attend_near(span, q, kv, tk, tv, qlab, klab):
    cols, size = q.shape
    wide = lambda *dims: jax.ShapeDtypeStruct(dims, F32)
    vmem = pl.BlockSpec(memory_space=pltpu.VMEM)
    return pl.pallas_call(
        near_body,
        in_specs=[pl.BlockSpec(memory_space=pltpu.SMEM)] + [vmem] * 6,
        out_specs=[vmem] * 3,
        out_shape=[wide(cols // HEAD_SIZE, size), wide(cols // HEAD_SIZE, size), wide(cols, size)],
        scratch_shapes=[pltpu.VMEM((size, cols), BF16), pltpu.VMEM((size // TILE, cols, TILE), BF16)],
        name="attend_near", cost_estimate=FREE,
    )(span, q, kv, tk, tv, qlab, klab)


def attend_far(span, q, behind, ahead, qlab, klab, w_out, state):
    cols, size = q.shape
    share, width = size // 4, w_out.shape[1]
    low = lambda *dims: jax.ShapeDtypeStruct(dims, BF16)
    wide = lambda *dims: jax.ShapeDtypeStruct(dims, F32)
    vmem = pl.BlockSpec(memory_space=pltpu.VMEM)
    keys = pltpu.VMEM((size, cols), BF16)
    vals = pltpu.VMEM((size // TILE, cols, TILE), BF16)
    return pl.pallas_call(
        far_body,
        in_specs=[pl.BlockSpec(memory_space=pltpu.SMEM)] + [vmem] * 9,
        out_specs=[vmem] * 5,
        out_shape=[low(cols, size), wide(cols // HEAD_SIZE, size), low(2 * share, width),
                   wide(share, width), low(share, width)],
        scratch_shapes=[keys, keys, vals, vals],
        name="attend_far", cost_estimate=FREE,
    )(span, q, behind, ahead, qlab, klab, w_out, *state)


def attend_back(span, q, kvs, tk, tv, qlab, klab, w_out, out, lse, grads):
    cols, size = q.shape
    tiles = 3 * size // TILE
    low = lambda *dims: jax.ShapeDtypeStruct(dims, BF16)
    wide = lambda *dims: jax.ShapeDtypeStruct(dims, F32)
    vmem = pl.BlockSpec(memory_space=pltpu.VMEM)
    return pl.pallas_call(
        backward_body,
        in_specs=[pl.BlockSpec(memory_space=pltpu.SMEM)] + [vmem] * 15,
        out_specs=[vmem] * 6,
        out_shape=[wide(cols, size), low(2, cols, size), wide(2, cols, size), low(2, cols, size),
                   wide(cols, 1), wide(cols, 1)],
        scratch_shapes=[pltpu.VMEM((cols, size), BF16), pltpu.VMEM((3 * size, cols), BF16),
                        pltpu.VMEM((3 * size, cols), BF16), pltpu.VMEM((tiles, cols, TILE), BF16),
                        pltpu.VMEM((tiles, cols, TILE), F32), pltpu.VMEM((tiles, cols, TILE), F32)],
        name="attend_back", cost_estimate=FREE,
    )(span, q, *kvs, tk, tv, qlab, klab, w_out, out, lse, *grads)


def tail_body(place, dq, kept, ahead, behind, cosine, sine, wq, wk, wv, raw, away, own, low, flipped):
    part, size = dq.shape
    half = HEAD_SIZE // 2

    def returned(block, base, scale):
        for h in range(part // HEAD_SIZE):
            a = block[h * HEAD_SIZE : h * HEAD_SIZE + half, :]
            b = block[h * HEAD_SIZE + half : (h + 1) * HEAD_SIZE, :]
            at = base + h * HEAD_SIZE
            raw[at : at + half, :] = ((a * cosine[...] + b * sine[...]) * scale).astype(BF16)
            raw[at + half : at + HEAD_SIZE, :] = (
                (b * cosine[...] - a * sine[...]) * scale
            ).astype(BF16)

    def whole(index):
        return kept[index] + ahead[index].astype(F32) + behind[index].astype(F32)

    returned(dq[...], 0, 1.0 / math.sqrt(HEAD_SIZE))
    returned(whole(0), part, 1.0)
    raw[2 * part :, :] = whole(1).astype(BF16)
    flipped[...] = raw[...].T

    def sent(r):
        at = relative(place[0], r, part)
        return sum(
            dot_nt(flipped[:, i * part : (i + 1) * part], weight[at, :])
            for i, weight in enumerate((wq, wk, wv))
        )

    away[:size, :] = sent(1).astype(BF16)
    away[size:, :] = sent(3).astype(BF16)
    low[...] = sent(2).astype(BF16)
    own[...] = sent(0)


def tail(place, dq, kept, ahead, behind, tables, wq, wk, wv):
    part, size = dq.shape
    low = lambda *dims: jax.ShapeDtypeStruct(dims, BF16)
    vmem = pl.BlockSpec(memory_space=pltpu.VMEM)
    return pl.pallas_call(
        tail_body,
        in_specs=[pl.BlockSpec(memory_space=pltpu.SMEM)] + [vmem] * 9,
        out_specs=[vmem] * 4,
        out_shape=[low(3 * part, size), low(2 * size, part), jax.ShapeDtypeStruct((size, part), F32),
                   low(size, part)],
        scratch_shapes=[pltpu.VMEM((size, 3 * part), BF16)],
        name="tail", cost_estimate=FREE,
    )(place, dq, kept, ahead, behind, *tables, wq, wk, wv)


def rotary_tables(frame_positions):
    half_dim = HEAD_SIZE // 2
    frequency = jnp.exp(jnp.arange(half_dim, dtype=jnp.float32) * (-math.log(10000.0) / half_dim))
    angles = frequency[:, None] * frame_positions[None, :]
    return (jnp.cos(angles), jnp.sin(angles))


def rotate(rows, tables, sign=1.0):
    count, size = rows.shape
    halves = rows.reshape(count // HEAD_SIZE, 2, HEAD_SIZE // 2, size)
    cosine, sine = tables[0][None], tables[1][None] * sign
    first = halves[:, 0] * cosine - halves[:, 1] * sine
    second = halves[:, 1] * cosine + halves[:, 0] * sine
    return jnp.stack([first, second], 1).reshape(count, size)


def product(left, right):
    return jnp.dot(left, right, preferred_element_type=jnp.float32)


def inner_rows(left, right):
    return jnp.einsum("nd,nf->df", left, right, preferred_element_type=jnp.float32)


def back_project(gradient, weight):
    return jnp.einsum("nf,df->nd", gradient, weight, preferred_element_type=jnp.float32)


def by_feature(left, right):
    return jnp.einsum("nd,df->fn", left, right, preferred_element_type=jnp.float32)


def columns(weight, start, size):
    return lax.dynamic_slice_in_dim(weight, start, size, 1)


def rows_of(weight, start, size):
    return lax.dynamic_slice_in_dim(weight, start, size, 0)


def normalize(value_rows):
    means = jnp.mean(value_rows, -1, keepdims=True)
    centred = value_rows - means
    inverse = lax.rsqrt(jnp.mean(centred * centred, -1, keepdims=True) + 1e-05)
    return centred * inverse, inverse


def norm_backward(gradient, scaled, inverse, norm_gain):
    scaled_grad = gradient * norm_gain
    plain = jnp.mean(scaled_grad, -1, keepdims=True)
    cross = jnp.mean(scaled_grad * scaled, -1, keepdims=True)
    return inverse * (scaled_grad - plain - scaled * cross)


FREE = pl.CostEstimate(flops=1, transcendentals=0, bytes_accessed=1)


def dot_nn(left, right):
    return lax.dot_general(left, right, (((1,), (0,)), ((), ())), preferred_element_type=F32)


def dot_nt(left, right):
    return lax.dot_general(left, right, (((1,), (1,)), ((), ())), preferred_element_type=F32)


def dot_tn(left, right):
    return lax.dot_general(left, right, (((0,), (0,)), ((), ())), preferred_element_type=F32)


def head_weights(query, key, lanes, which):
    mine = jnp.where(lanes == which, query, jnp.zeros_like(query))
    scores = dot_nt(mine, key) * (1.0 / math.sqrt(HEAD_SIZE))
    weights = jnp.exp(scores - jnp.max(scores, -1, keepdims=True))
    return weights / jnp.sum(weights, -1, keepdims=True)


def pair_cols(refs, p, rows):
    ref = refs[p * 2 * HEAD_SIZE // refs[0].shape[1]]
    start = p * 2 * HEAD_SIZE % refs[0].shape[1]
    return ref[rows, start : start + 2 * HEAD_SIZE]


def cross_forward_body(width_block, place, rows, own, got, far, norms, q0, q1, q2, q3,
                       c0, c1, c2, c3, o0, o1, o2, o3,
                       front, queries, first, second, normed_three,
                       flip_own, flip_away):
    width = rows.shape[1]
    kv = (c0, c1, c2, c3)
    context_rows = c0.shape[0] // 2
    key_rows, value_rows = slice(0, context_rows), slice(context_rows, 2 * context_rows)
    lanes = lax.broadcasted_iota(jnp.int32, (rows.shape[0], 2 * HEAD_SIZE), 1) // HEAD_SIZE
    residual = (
        rows[...].astype(F32) + own[...] + got[...].astype(F32) + far[...].astype(F32)
    )
    first[...] = residual
    scaled, _ = normalize(residual)
    low = (scaled * norms[2:3, :] + norms[3:4, :]).astype(BF16)
    front[:, :width] = low
    part = width // 4
    for b, ref in enumerate((q0, q1, q2, q3)):
        queries[:, b * part : (b + 1) * part] = dot_nn(low, ref[...]).astype(BF16)
    for p in range(width // (2 * HEAD_SIZE)):
        cols = slice(p * 2 * HEAD_SIZE, (p + 1) * 2 * HEAD_SIZE)
        q, k, v = queries[:, cols], pair_cols(kv, p, key_rows), pair_cols(kv, p, value_rows)
        mixed = [dot_nn(head_weights(q, k, lanes, g).astype(BF16), v) for g in (0, 1)]
        front[:, width + cols.start : width + cols.stop] = jnp.where(lanes == 0, mixed[0], mixed[1]).astype(BF16)
    for b, ref in enumerate((o0, o1, o2, o3)):
        residual = residual + dot_nn(front[:, width + b * part : width + (b + 1) * part], ref[...])
    second[...] = residual
    scaled, _ = normalize(residual)
    low = (scaled * norms[4:5, :] + norms[5:6, :]).astype(BF16)
    normed_three[...] = low
    deal_rows(low.T, width_block, place[0], flip_own, flip_away)


def cross_forward(devices, place, rows, own, got, far, norms, query_parts, kv_parts, out_parts):
    size, width = rows.shape
    low = jax.ShapeDtypeStruct(rows.shape, BF16)
    both = jax.ShapeDtypeStruct((size, 2 * width), BF16)
    wide = jax.ShapeDtypeStruct(rows.shape, F32)
    flip = jax.ShapeDtypeStruct((width // 2, size), BF16)
    vmem = pl.BlockSpec(memory_space=pltpu.VMEM)
    block = pl.BlockSpec((size, width), lambda i: (0, 0))
    return pl.pallas_call(
        functools.partial(cross_forward_body, width // devices),
        grid=(1,),
        in_specs=[pl.BlockSpec(memory_space=pltpu.SMEM)] + [block] * 4 + [vmem] * 13,
        out_shape=[both, low, wide, wide, low, flip, flip],
        cost_estimate=FREE, name="cross",
    )(place, rows, own, got, far, norms, *query_parts, *kv_parts, *out_parts)


def deal_rows(rows, size, column, own, away):
    for b in range(rows.shape[0] // (2 * size)):
        at = slice(b * size, (b + 1) * size)
        even = rows[2 * b * size : (2 * b + 1) * size, :]
        odd = rows[(2 * b + 1) * size : (2 * b + 2) * size, :]

        @pl.when(column == 0)
        def _():
            own[at, :] = even
            away[at, :] = odd

        @pl.when(column != 0)
        def _():
            own[at, :] = odd
            away[at, :] = even


def ffn_part(normed, grad, gate_w, up_w, down_w, hidden, hid_own, hid_away, gate_grad, lifted_grad,
             unit_block, column):
    gate = dot_nn(normed, gate_w[...])
    lifted = dot_nn(normed, up_w[...])
    back = dot_nt(grad, down_w[...]).astype(BF16).astype(F32)
    sig = jax.nn.sigmoid(gate)
    swish = gate * sig
    made = (swish * lifted).astype(BF16)
    hidden[...] = made
    deal_rows(made.T, unit_block, column, hid_own, hid_away)
    gg = (back * lifted * sig * (1.0 + gate * (1.0 - sig))).astype(BF16)
    lg = (back * swish).astype(BF16)
    gate_grad[...] = gg
    lifted_grad[...] = lg
    return dot_nt(gg, gate_w[...]) + dot_nt(lg, up_w[...])


def ffn_first_body(unit_block, place, n0, n1, n2, n3, g0, g1, g2, g3, gate_w, up_w, down_w,
                   hidden, hid_own, hid_away, gate_grad, lifted_grad, normed, grad, grad_pair,
                   total):
    share, part = n0.shape[0], g0.shape[2]
    for b, ref in enumerate((n0, n1, n2, n3)):
        normed[b * share : (b + 1) * share, :] = ref[...]
    for c, ref in enumerate((g0, g1, g2, g3)):
        for b in range(4):
            rows, cols = relative(place[1], b, share), relative(place[1], c, part)
            grad[b * share : (b + 1) * share, cols] = ref[0, rows, :]
            grad_pair[b * share : (b + 1) * share, cols] = ref[1, rows, :]
    total[...] = ffn_part(
        normed[...], grad[...], gate_w, up_w, down_w, hidden, hid_own, hid_away, gate_grad,
        lifted_grad, unit_block, place[0],
    )


def ffn_second_body(unit_block, place, normed, grad, total, gate_w, up_w, down_w,
                    hidden, hid_own, hid_away, gate_grad, lifted_grad, away, own, low):
    share = own.shape[0]
    found = total[...] + ffn_part(
        normed[...], grad[...], gate_w, up_w, down_w, hidden, hid_own, hid_away, gate_grad,
        lifted_grad, unit_block, place[0],
    )
    own[...] = found[:share, :]
    low[...] = found[2 * share : 3 * share, :].astype(BF16)
    away[:share, :] = found[share : 2 * share, :].astype(BF16)
    away[share:, :] = found[3 * share :, :].astype(BF16)


def ffn(devices, place, half, inputs, gate_w, up_w, down_w):
    share = inputs[0].shape[0] if half == 0 else inputs[0].shape[0] // 4
    width = inputs[0].shape[1]
    size, units = 4 * share, gate_w.shape[1]
    tile = units // 2
    low = lambda *dims: jax.ShapeDtypeStruct(dims, BF16)
    wide = lambda *dims: jax.ShapeDtypeStruct(dims, F32)
    vmem = pl.BlockSpec(memory_space=pltpu.VMEM)
    cols = pl.BlockSpec((width, tile), lambda i: (0, half))
    rows = pl.BlockSpec((tile, width), lambda i: (half, 0))
    made = [low(size, tile), low(tile // 2, size), low(tile // 2, size), low(size, tile),
            low(size, tile)]
    if half == 0:
        made += [low(size, width), low(size, width), low(size, width), wide(size, width)]
    else:
        made += [low(2 * share, width), wide(share, width), low(share, width)]
    return pl.pallas_call(
        functools.partial(ffn_second_body if half else ffn_first_body, units // devices),
        grid=(1,),
        in_specs=[pl.BlockSpec(memory_space=pltpu.SMEM)] + [vmem] * len(inputs)
        + [cols, cols, rows],
        out_specs=[vmem] * len(made),
        out_shape=made,
        cost_estimate=FREE, name="ffn",
    )(place, *inputs, gate_w, up_w, down_w)


def cross_backward_body(own, got, far, grad, first, second, norms, q0, q1, q2, q3,
                        c0, c1, c2, c3, o0, o1, o2, o3, queries,
                        back_rows, kv_grad, vectors, grad_one, crossed_grad):
    width = grad.shape[1]
    kv = (c0, c1, c2, c3)
    context_rows = c0.shape[0] // 2
    key_rows, value_rows = slice(0, context_rows), slice(context_rows, 2 * context_rows)
    part = width // 4
    lanes = lax.broadcasted_iota(jnp.int32, (grad.shape[0], 2 * HEAD_SIZE), 1) // HEAD_SIZE
    lane_k = lax.broadcasted_iota(jnp.int32, (context_rows, 2 * HEAD_SIZE), 1) // HEAD_SIZE
    scale = 1.0 / math.sqrt(HEAD_SIZE)
    arrived = own[...] + got[...].astype(F32) + far[...].astype(F32)
    scaled, inverse = normalize(second[...])
    vectors[0:1, :] = jnp.sum(arrived * scaled, 0, keepdims=True)
    vectors[1:2, :] = jnp.sum(arrived, 0, keepdims=True)
    two = grad[...].astype(F32) + norm_backward(arrived, scaled, inverse, norms[4:5, :])
    low = two.astype(BF16)
    back_rows[:, :width] = low
    for b, ref in enumerate((o0, o1, o2, o3)):
        crossed_grad[:, b * part : (b + 1) * part] = dot_nt(low, ref[...]).astype(BF16)
    for p in range(width // (2 * HEAD_SIZE)):
        cols = slice(p * 2 * HEAD_SIZE, (p + 1) * 2 * HEAD_SIZE)
        q, k, v = queries[:, cols], pair_cols(kv, p, key_rows), pair_cols(kv, p, value_rows)
        g_rows = crossed_grad[:, cols]
        found = []
        for g in (0, 1):
            probs = head_weights(q, k, lanes, g)
            change = dot_nt(jnp.where(lanes == g, g_rows, jnp.zeros_like(g_rows)), v)
            delta = jnp.sum(change * probs, -1, keepdims=True)
            ds = (probs * (change - delta)).astype(BF16)
            found.append((dot_nn(ds, k), dot_tn(ds, q), dot_tn(probs.astype(BF16), g_rows)))
        back_rows[:, width + cols.start : width + cols.stop] = (
            jnp.where(lanes == 0, found[0][0], found[1][0]) * scale
        ).astype(BF16)
        kv_grad[:context_rows, cols] = (
            jnp.where(lane_k == 0, found[0][1], found[1][1]) * scale
        ).astype(BF16)
        kv_grad[context_rows:, cols] = jnp.where(lane_k == 0, found[0][2], found[1][2]).astype(
            BF16
        )
    back = jnp.zeros(grad.shape, F32)
    for b, ref in enumerate((q0, q1, q2, q3)):
        back = back + dot_nt(back_rows[:, width + b * part : width + (b + 1) * part], ref[...])
    scaled, inverse = normalize(first[...])
    vectors[2:3, :] = jnp.sum(back * scaled, 0, keepdims=True)
    vectors[3:4, :] = jnp.sum(back, 0, keepdims=True)
    grad_one[...] = (two + norm_backward(back, scaled, inverse, norms[2:3, :])).astype(BF16)


def cross_backward(own, got, far, grad, first, second, norms, query_parts, kv_parts, out_parts,
                   queries):
    rows, width = own.shape
    low = lambda r: jax.ShapeDtypeStruct((r, width), BF16)
    block = pl.BlockSpec((rows, width), lambda i: (0, 0))
    return pl.pallas_call(
        cross_backward_body,
        grid=(1,),
        out_shape=[jax.ShapeDtypeStruct((rows, 2 * width), BF16), low(kv_parts[0].shape[0]),
                   jax.ShapeDtypeStruct((4, width), F32), low(rows)],
        in_specs=[block] * 6 + [pl.BlockSpec(memory_space=pltpu.VMEM)] * 14,
        scratch_shapes=[pltpu.VMEM((rows, width), BF16)],
        cost_estimate=FREE, name="cross_back",
    )(own, got, far, grad, first, second, norms, *query_parts, *kv_parts, *out_parts, queries)


def meet_rows_body(size, side, own_a, pair_a, own_b, pair_b, right, right_pair, keep, send):
    half = keep.shape[0] // 2
    for b, (own, pair) in enumerate(((own_a, pair_a), (own_b, pair_b))):
        made = (dot_nn(own[...], right[...]) + dot_nn(pair[...], right_pair[...])).astype(BF16)
        at = pl.ds(b * half, half)
        deal_rows(made, size, side[0], keep.at[at], send.at[at])


def meet_rows(size, side, lefts, rights):
    count, frames = lefts[0].shape
    width = rights[0].shape[1]
    tile = width // 3
    left = pl.BlockSpec((count, frames), lambda i: (0, 0))
    right = pl.BlockSpec((frames, tile), lambda i: (0, i))
    return pl.pallas_call(
        functools.partial(meet_rows_body, size),
        grid=(3,),
        in_specs=[pl.BlockSpec(memory_space=pltpu.SMEM)] + [left] * 4 + [right] * 2,
        out_specs=[pl.BlockSpec((count, tile), lambda i: (0, i))] * 2,
        out_shape=[jax.ShapeDtypeStruct((count, width), BF16)] * 2,
        name="meet_rows", cost_estimate=FREE,
    )(side, *lefts, *rights)


def meet_cols_body(size, side, p0, p1, p2, p3, a, a_pair, b, b_pair, keep, send):
    own, pair = (jnp.concatenate([p[i] for p in (p0, p1, p2, p3)], 1) for i in (0, 1))
    width = a.shape[1]
    for left, (right, right_pair) in ((0, (a, a_pair)), (width, (b, b_pair))):
        made = (dot_nn(own, right[...]) + dot_nn(pair, right_pair[...])).astype(BF16)
        cols = pl.ds(left, width)
        deal_rows(made, size, side[0], keep.at[:, cols], send.at[:, cols])


def meet_cols(size, side, near, rights):
    half = jax.ShapeDtypeStruct((near[0].shape[1] // 2, 2 * rights[0].shape[1]), BF16)
    return pl.pallas_call(
        functools.partial(meet_cols_body, size),
        in_specs=[pl.BlockSpec(memory_space=pltpu.SMEM)] + [pl.BlockSpec(memory_space=pltpu.VMEM)] * 8,
        out_shape=[half] * 2,
        name="meet_cols", cost_estimate=FREE,
    )(side, *near, *rights)


def down_body(first, second, down_w, away, own, low):
    share, units = own.shape[0], first.shape[1]

    def sent(r):
        at = slice(r * share, (r + 1) * share)
        return dot_nn(first[at, :], down_w[:units, :]) + dot_nn(second[at, :], down_w[units:, :])

    away[:share, :] = sent(1).astype(BF16)
    away[share:, :] = sent(3).astype(BF16)
    low[...] = sent(2).astype(BF16)
    own[...] = sent(0)


def down_parts(first, second, down_w):
    share, width = first.shape[0] // 4, down_w.shape[1]
    low = lambda *dims: jax.ShapeDtypeStruct(dims, BF16)
    return pl.pallas_call(
        down_body,
        out_shape=[low(2 * share, width), jax.ShapeDtypeStruct((share, width), F32),
                   low(share, width)],
        name="down", cost_estimate=FREE,
    )(first, second, down_w)


def bundle_body(devices, place, f02, f13, b02, b13, a0, a1, a2, a3, attended,
                context, kv, keep_a, send_a, keep_b, send_b):
    width = a0.shape[1]
    part, share = width // 4, a0.shape[0]

    def near(even, odd):
        return even[0], odd[0], even[1], odd[1]

    own = lambda rows: jnp.concatenate(
        [row[:, width + r * part : width + (r + 1) * part] for r, row in enumerate(rows)], 0
    )
    full = lambda rows: jnp.concatenate([row[:, :width] for row in rows], 0)
    fronts, backs = near(f02, f13), near(b02, b13)
    rows = width // devices
    small = part // devices
    half = width // 2

    def put(block, base, left, out):
        size = block.shape[0] // devices
        cols = slice(left, left + block.shape[1])
        low = block.astype(BF16)
        for d in range(0, devices, 2):
            at = slice(base, base + size)
            even, odd = low[d * size : (d + 1) * size, :], low[(d + 1) * size : (d + 2) * size, :]

            @pl.when(place[0] == 0)
            def _():
                out[0][d // 2, at, cols] = even
                out[1][d // 2, at, cols] = odd

            @pl.when(place[0] != 0)
            def _():
                out[0][d // 2, at, cols] = odd
                out[1][d // 2, at, cols] = even

    put(dot_tn(full(fronts), own(backs)), 0, 0, (keep_a, send_a))
    count = context.shape[0]
    put(dot_tn(context[...], kv[:count, :]), 0, part, (keep_a, send_a))
    put(dot_tn(context[...], kv[count:, :]), rows // 2, part, (keep_a, send_a))
    grads = dot_tn(own(fronts), full(backs))
    put(grads[:, :half], 0, 0, (keep_b, send_b))
    put(grads[:, half:], small, 0, (keep_b, send_b))
    grads = sum(
        dot_nn(attended[:, relative(place[1], r, share)], ref[...])
        for r, ref in enumerate((a0, a1, a2, a3))
    )
    put(grads[:, :half], 2 * small, 0, (keep_b, send_b))
    put(grads[:, half:], 3 * small, 0, (keep_b, send_b))


def bundle_grads(devices, place, fronts, backs, ones, attended, context, kv):
    width = ones[0].shape[1]
    vmem = pl.BlockSpec(memory_space=pltpu.VMEM)
    return pl.pallas_call(
        functools.partial(bundle_body, devices),
        in_specs=[pl.BlockSpec(memory_space=pltpu.SMEM)] + [vmem] * 11,
        out_specs=[vmem] * 4,
        out_shape=[jax.ShapeDtypeStruct((devices // 2, width // devices, width // 2), BF16)] * 4,
        name="bundle", cost_estimate=FREE,
    )(place, *fronts, *backs, *ones, attended, context, kv)


def front_body(width_block, place, x0, x1, x2, x3, g0, g1, g2, g3, cosine, sine, wq, wk, wv,
               time_row, context, ck, cv,
               queries, pair, rows, low, nrm_own, nrm_away, norms, means, inverses,
               time_scaled, time_low, time_keys, time_values, kv, wide):
    size, part = x0.shape
    for r, (x, g) in enumerate(((x0, g0), (x1, g1), (x2, g2), (x3, g3))):
        start = pl.multiple_of((place[0] ^ r) * part, 128)
        wide[:, pl.ds(start, part)] = x[...]
        norms[:, pl.ds(start, part)] = g[...]
    share = size // 4
    rows[...] = wide[pl.ds(pl.multiple_of(place[0] * share, share), share), :]
    values = wide[...].astype(F32)
    mean = jnp.mean(values, -1, keepdims=True)
    centred = values - mean
    inverse = lax.rsqrt(jnp.mean(centred * centred, -1, keepdims=True) + 1e-05)
    means[...] = mean
    inverses[...] = inverse
    normed = (centred * inverse * norms[0:1, :] + norms[1:2, :]).astype(BF16)
    low[...] = normed
    half = HEAD_SIZE // 2

    def turned(weight):
        return dot_nn(normed, weight[...]).T

    def rotated(block, dest, scale):
        for h in range(part // HEAD_SIZE):
            a = block[h * HEAD_SIZE : h * HEAD_SIZE + half, :]
            b = block[h * HEAD_SIZE + half : (h + 1) * HEAD_SIZE, :]
            dest[h * HEAD_SIZE : h * HEAD_SIZE + half, :] = (
                (a * cosine[...] - b * sine[...]) * scale
            ).astype(BF16)
            dest[h * HEAD_SIZE + half : (h + 1) * HEAD_SIZE, :] = (
                (b * cosine[...] + a * sine[...]) * scale
            ).astype(BF16)

    scaled, _ = normalize(jnp.broadcast_to(time_row[...].astype(F32), (8, 4 * part)))
    time_scaled[...] = scaled[:1, :]
    made = (scaled * norms[0:1, :] + norms[1:2, :]).astype(BF16)
    time_low[...] = made[:1, :].astype(F32)
    time_keys[...] = dot_nn(made, wk[...]).astype(BF16).astype(F32).T[:, :1]
    time_values[...] = dot_nn(made, wv[...]).astype(BF16).astype(F32).T[:, :1]
    count = context.shape[0]
    kv[:count, :] = dot_nn(context[...], ck[...]).astype(BF16)
    kv[count:, :] = dot_nn(context[...], cv[...]).astype(BF16)
    rotated(turned(wk), pair.at[0], 1.0)
    pair[1] = turned(wv).astype(BF16)
    rotated(turned(wq), queries, 1.0 / math.sqrt(HEAD_SIZE))
    deal_rows(normed.T, width_block, place[1], nrm_own, nrm_away)


def front(devices, place, parts, norm_parts, tables, wq, wk, wv, time_row, context, ck, cv):
    size, part = parts[0].shape
    width = 4 * part
    low = lambda *s: jax.ShapeDtypeStruct(s, BF16)
    wide = lambda *s: jax.ShapeDtypeStruct(s, F32)
    vmem = pl.BlockSpec(memory_space=pltpu.VMEM)
    return pl.pallas_call(
        functools.partial(front_body, width // devices),
        in_specs=[pl.BlockSpec(memory_space=pltpu.SMEM)] + [vmem] * 17,
        out_specs=[vmem] * 14,
        out_shape=[low(part, size), low(2, part, size), low(size // 4, width), low(size, width),
                   low(width // 2, size), low(width // 2, size), wide(6, width),
                   wide(size, 1), wide(size, 1), wide(1, width), wide(1, width), wide(part, 1),
                   wide(part, 1), low(2 * context.shape[0], part)],
        scratch_shapes=[pltpu.VMEM((size, width), BF16)],
        cost_estimate=FREE, name="front",
    )(place, *parts, *norm_parts, *tables, wq, wk, wv, time_row, context, ck, cv)


def per_device(
    frames,
    segment,
    time_token,
    context,
    gain_attn,
    bias_attn,
    gain_cross,
    bias_cross,
    gain_ffn,
    bias_ffn,
    w_query,
    w_key,
    w_value,
    w_out,
    c_query,
    c_key,
    c_value,
    c_out,
    w_gate,
    w_up,
    w_down,
    out_grad,
):
    local_rows = frames.shape[0]
    local_width = frames.shape[1]
    model_width = w_query.shape[0]
    head_cols = w_query.shape[1]
    heads = head_cols // HEAD_SIZE
    number_of_frames = lax.axis_size("seq") * local_rows
    row_length = min(max(ROW_MIN, 64 * lax.axis_size("seq")), number_of_frames)
    first_frame = lax.axis_index("seq") * local_rows
    own_start = lax.axis_index("tensor") * local_width

    def own_cols(value):
        return lax.dynamic_slice_in_dim(value, own_start, local_width, value.ndim - 1)

    place = lax.axis_index("tensor")
    share = local_rows // 4

    def row_block(value, index):
        return rows_of(value, index * share, share)

    column = lax.axis_index("seq") % 2
    frame_parts_near = gather_near(frames)
    norm_parts = gather_near(
        jnp.stack([gain_attn, bias_attn, gain_cross, bias_cross, gain_ffn, bias_ffn])
    )
    clip_starts, frame_positions = frame_clip_labels(segment, row_length)
    own_labels = lax.dynamic_slice_in_dim(clip_starts, first_frame, local_rows)
    own_positions = lax.dynamic_slice_in_dim(frame_positions, first_frame, local_rows)
    blanks = jnp.full((local_rows,), -1, jnp.int32)
    key_labels = lax.dynamic_slice_in_dim(
        jnp.concatenate([blanks, clip_starts, blanks]), first_frame, 3 * local_rows
    )
    spans = jnp.concatenate(
        [tile_ranges(own_labels, key_labels), place.astype(jnp.int32).reshape(1)]
    )
    places = jnp.stack([column, place]).astype(jnp.int32)
    label_row, label_column = own_labels[None, :], key_labels[:, None]
    row_index = first_frame // row_length
    time_row = lax.dynamic_slice_in_dim(time_token, row_index, 1, 0)
    row_context = lax.dynamic_slice_in_dim(context, row_index, 1, 0)[0]
    context_rows = row_context.shape[0]
    tables = rotary_tables(own_positions)
    score_scale = 1.0 / math.sqrt(HEAD_SIZE)
    all_heads = model_width // HEAD_SIZE

    (
        queries, both, frame_rows, frame_normed, one_own_half, one_away_half, norms, means_one,
        inverse_one, scaled_time, time_normed, time_keys, time_values, context_kv,
    ) = front(
        lax.axis_size("seq"), jnp.flip(places), frame_parts_near, norm_parts, tables, w_query,
        w_key, w_value, time_row, row_context, c_key, c_value,
    )
    both, out_pair = meeting(both, swap(after(out_grad, frame_parts_near[2]), "seq", 1))
    grad_both = jnp.stack([out_grad, out_pair])
    behind, ahead = shift(both, "seq", 1), shift(both, "seq", -1)
    query_far = swap(after(c_query, frame_parts_near[3]), "tensor", 2)
    out_far = swap(after(c_out, frame_parts_near[3]), "tensor", 2)
    state = attend_near(spans, queries, both, time_keys, time_values, label_row, label_column)
    behind, ahead, query_far, out_far, *state = meeting(
        behind, ahead, query_far, out_far, *state
    )
    query_own, out_own, context_late = after((c_query, c_out, context_kv), behind)
    weights_near = [
        swap(value, "tensor", 1) for value in (query_own, query_far, out_own, out_far)
    ]
    kv_far = swap(context_late, "tensor", 2)
    attended, log_totals, one_away, one_own, one_low = attend_far(
        spans, queries, behind, ahead, label_row, label_column, w_out, state
    )
    one_away, one_low, kv_far, *weights_near = meeting(one_away, one_low, kv_far, *weights_near)
    kv_both = jnp.concatenate([context_kv, kv_far], 0)
    kv_other = swap(kv_both, "tensor", 1)
    kv_rows = context_kv.shape[0]
    kv_parts = (context_kv, kv_other[:kv_rows], kv_far, kv_other[kv_rows:])
    query_parts = (c_query, weights_near[0], query_far, weights_near[1])
    out_parts = (c_out, weights_near[2], out_far, weights_near[3])
    one_got, _, one_far = scatter_near(one_away, one_low)
    (
        front_rows, cross_queries, residual_one, residual_two, normed_share, flip_own, flip_away,
    ) = cross_forward(
        lax.axis_size("seq"), places, frame_rows, one_own, one_got, one_far, norms,
        query_parts, kv_parts, out_parts,
    )
    grad_far = swap(after(grad_both, one_far), "tensor", 2)
    normed_share, normed_got, grad_far = meeting(
        normed_share, swap(after(one_away_half, one_low), "seq", 1), grad_far
    )
    grad_late, grad_far_late = after((grad_both, grad_far), normed_share)
    grad_mate, grad_far_mate = swap(grad_late, "tensor", 1), swap(grad_far_late, "tensor", 1)
    grad_parts = (grad_both, grad_mate, grad_far, grad_far_mate)
    three_parts = gather_near(normed_share)
    flip_got = swap(after(flip_away, normed_share), "seq", 1)
    front_far = swap(after(front_rows, three_parts[3]), "tensor", 2)
    devices = lax.axis_size("seq")
    (
        hidden_a, hidden_own_a, hidden_away_a, gate_a, lifted_a, normed_three, grad_near, grad_pair,
        ffn_total,
    ) = ffn(devices, places, 0, (*three_parts, *grad_parts), w_gate, w_up, w_down)
    ffn_total, flip_got = meeting(ffn_total, flip_got)
    flip_both = jnp.stack([flip_own, flip_got])
    flip_far = swap(flip_both, "tensor", 2)
    hidden_got_a, gate_got_a = swap(hidden_away_a, "seq", 1), swap(gate_a, "seq", 1)
    hidden_b, hidden_own_b, hidden_away_b, gate_b, lifted_b, three_away, three_own, three_low = ffn(
        devices, places, 1, (normed_three, grad_near, ffn_total), w_gate, w_up, w_down
    )
    three_away, three_low, flip_far, front_far, hidden_got_a = meeting(
        three_away, three_low, flip_far, front_far, hidden_got_a
    )
    three_got, _, three_far = scatter_near(three_away, three_low)
    hidden_late, lifted_late = after((hidden_away_b, lifted_a), three_low)
    hidden_got_b, lifted_got_a = swap(hidden_late, "seq", 1), swap(lifted_late, "seq", 1)
    flip_late, flip_far_late, gate_late = after((flip_both, flip_far, gate_b), three_far)
    flip_mate, flip_far_mate = swap(flip_late, "tensor", 1), swap(flip_far_late, "tensor", 1)
    gate_got_b = swap(gate_late, "seq", 1)
    front_both = jnp.stack([front_rows, front_far])
    back_rows, kv_grad, norm_vectors, grad_one = cross_backward(
        three_own, three_got, three_far, grad_near, residual_one, residual_two, norms,
        query_parts, kv_parts, out_parts, cross_queries,
    )
    grad_one, gate_got_a, hidden_got_b, lifted_got_a, flip_mate, flip_far_mate = meeting(
        grad_one, gate_got_a, hidden_got_b, lifted_got_a, flip_mate, flip_far_mate
    )
    count = lax.axis_size("seq")
    level_side = ((lax.axis_index("seq") >> 1) % 2).astype(jnp.int32).reshape(1)
    rows = model_width // count

    def traded(dealt):
        keep, send = [value.reshape(count // 4, rows, -1) for value in dealt]
        return keep, swap(send, "seq", 2)

    down_keep, down_got = traded(
        meet_rows(
            rows, level_side, (hidden_own_a, hidden_got_a, hidden_own_b, hidden_got_b),
            (grad_near, grad_pair),
        )
    )
    flip_near = (flip_both, flip_mate, flip_far, flip_far_mate)
    first_keep, first_got = traded(
        meet_cols(rows, level_side, flip_near, (gate_a, gate_got_a, lifted_a, lifted_got_a))
    )
    context_parts = quarters(kv_grad, 1)
    context_got = swap(jnp.concatenate([context_parts[1], context_parts[3]], 0), "tensor", 1)
    *one_parts, front_other, context_got, gate_got_b = meeting(
        *gather_near(grad_one), swap(after(front_both, grad_one), "tensor", 1), context_got,
        gate_got_b,
    )
    context_low = (
        context_parts[2].astype(F32) + context_got[context_parts[2].shape[0] :].astype(F32)
    ).astype(BF16)
    context_far = swap(context_low, "tensor", 2)
    *one_parts, first_keep = meeting(*one_parts, first_keep)
    back_far = swap(after(back_rows, one_parts[3]), "tensor", 2)
    lifted_got_b = swap(after(lifted_b, grad_one), "seq", 1)
    query_grad, to_prev, kept, to_next, time_key_grad, time_value_grad = attend_back(
        spans, queries, (behind, both, ahead), time_keys, time_values, label_row, label_column,
        w_out, attended, log_totals, one_parts,
    )
    to_prev, to_next, back_far, lifted_got_b, down_got, context_far = meeting(
        to_prev, to_next, back_far, lifted_got_b, down_got, context_far
    )
    from_next, from_prev = shift(to_prev, "seq", -1), shift(to_next, "seq", 1)
    down_keep, down_got = halve(added(down_keep, down_got).astype(BF16), 2)
    second_keep, second_got = traded(
        meet_cols(
            rows, level_side, flip_near, (gate_b, gate_got_b, lifted_b, lifted_got_b)
        )
    )
    down_away, down_own, down_low = down_parts(after(hidden_a, to_prev), hidden_b, w_down)
    back_both = jnp.stack([back_rows, back_far])
    back_other = swap(back_both, "tensor", 1)
    context_own = (
        context_parts[0].astype(F32)
        + context_got[: context_far.shape[0]].astype(F32)
        + context_far.astype(F32)
    )
    keep_a, send_a, keep_b, send_b = bundle_grads(
        count, places, (front_both, front_other), (back_both, back_other), one_parts, attended,
        row_context,
        context_own.astype(BF16),
    )
    from_next, from_prev, first_got, send_a, send_b = meeting(
        from_next, from_prev, first_got, send_a, send_b
    )
    got_a = swap(send_a, "seq", 1)
    raw, last_away, last_own, last_low = tail(
        places[1:], query_grad, kept, from_next, from_prev, tables, w_query, w_key, w_value
    )
    last_got = swap(last_away, "tensor", 1)
    raw_got = swap(raw, "seq", 1)
    last_sum = (
        last_low.astype(F32) + last_got[local_rows:].astype(F32)
    ).astype(BF16)
    last_sum, down_got, second_got, got_a = meeting(last_sum, down_got, second_got, got_a)
    first_keep, first_got = halve(added(first_keep, first_got).astype(BF16), 2)
    got_b = swap(after(send_b, got_a), "seq", 1)
    left_keep, left_got = halve(added(keep_a, got_a).astype(BF16), 1)
    last_far = swap(last_sum, "tensor", 2)
    time_both = jnp.concatenate([time_key_grad, time_value_grad], 0)
    last_far, time_got = meeting(last_far, swap(after(time_both, last_low), "seq", 1))
    frame_grad = last_own + last_got[:local_rows].astype(F32) + last_far.astype(F32)

    def to_frames(rows, weight):
        return jnp.einsum("fn,df->nd", rows, weight, preferred_element_type=F32)

    time_key_grad, time_value_grad = after((time_key_grad, time_value_grad), from_next)
    time_grad = to_frames(time_key_grad.astype(BF16), w_key) + to_frames(
        time_value_grad.astype(BF16), w_value
    )
    own_scaled = (frames.astype(F32) - means_one) * inverse_one
    scaled_grad = frame_grad * gain_attn[None]
    sums = jnp.concatenate(
        [
            jnp.sum(scaled_grad, -1),
            jnp.sum(scaled_grad * own_scaled, -1),
            time_grad[0],
            norm_vectors.reshape(-1),
        ]
    )[None]
    sums = sums + swap(sums, "tensor", 1)
    sums = sums + swap(sums, "tensor", 2)
    sums, first_got, left_got = meeting(sums, first_got, left_got)
    left_keep, left_got = halve(added(left_keep, left_got).astype(BF16), 2)
    plain = sums[0, :local_rows, None] / model_width
    cross = sums[0, local_rows : 2 * local_rows, None] / model_width
    vectors = own_cols(sums[0, 2 * local_rows :].reshape(5, model_width))
    attend_full = ordered(*[after(one_parts, from_next)[i] for i in (0, 2, 1, 3)], 0)
    d_frames = own_cols(attend_full).astype(F32) + inverse_one * (
        scaled_grad - plain - own_scaled * cross
    )
    d_gain_attn = jnp.sum(frame_grad * own_scaled, 0) + vectors[0] * own_cols(scaled_time)[0]
    d_bias_attn = jnp.sum(frame_grad, 0) + vectors[0]
    small = jnp.stack(
        [d_gain_attn, d_bias_attn, vectors[3], vectors[4], vectors[1], vectors[2]]
    ).reshape(6, devices, -1).transpose(1, 0, 2)
    small = added(*halve(small, 0))
    small = added(*halve(small, 1))
    bit = 2
    while small.shape[0] > 1:
        small = added(*halve(small, bit))
        bit += 1
    small, raw_got = meeting(small[0], raw_got)

    down_away, down_low = after((down_away, down_low), last_far)
    branch_got, _, branch_far = scatter_near(down_away, down_low)
    block_rows = (
        residual_two + down_own + branch_got[:share].astype(F32) + branch_far.astype(F32)
    ).astype(BF16)
    block_cols = rows_to_cols(
        *[
            lax.dynamic_slice_in_dim(block_rows, (place ^ r) * local_width, local_width, 1)
            for r in range(4)
        ],
        from_next,
    )
    block_out = jnp.concatenate([row_block(block_cols, place ^ b) for b in range(4)], 0)

    time_column = time_normed.T

    normed_pair = (one_own_half, normed_got)
    grad_down = halve_end(down_keep, down_got, 3)
    first, second = halve_end(first_keep, first_got, 3), halve_all(after(added(second_keep, second_got), sums), 2)
    units = first.shape[1] // 2
    grad_gate_w = jnp.concatenate([first[:, :units], second[:, :units]], 1)
    grad_up_w = jnp.concatenate([first[:, units:], second[:, units:]], 1)
    raw_pair = (raw, raw_got)
    time_both = time_both + time_got
    own_time_rows = lax.dynamic_index_in_dim(
        time_column.reshape(count // 2, 2, -1), column, 1, False
    ).reshape(-1, 1)
    outer = own_time_rows * jnp.concatenate([jnp.zeros((head_cols, 1), F32), time_both], 0).T
    blocks = sum(
        jnp.einsum("dn,fn->df", r, c, preferred_element_type=F32)
        for r, c in zip(normed_pair, raw_pair)
    )
    heads_keep, heads_got = halve(
        (blocks + outer).astype(BF16).reshape(count // 2, rows, 3 * head_cols), 1
    )
    heads_got, got_b = meeting(heads_got, got_b)
    heads_sum = halve_end(heads_keep, heads_got, 2)
    left, right = halve_end(left_keep, left_got, 3), halve_end(keep_b, got_b, 1)
    part, rows = head_cols // count, model_width // count
    grad_c_query = left[:, :head_cols]
    grad_c_key, grad_c_value = left[: rows // 2, head_cols:], left[rows // 2 :, head_cols:]
    grad_c_out = jnp.concatenate([right[:part], right[part : 2 * part]], 1)
    grad_w_out = jnp.concatenate([right[2 * part : 3 * part], right[3 * part :]], 1)
    grad_w_query, grad_w_key, grad_w_value = (
        heads_sum[:, i * head_cols : (i + 1) * head_cols] for i in range(3)
    )
    return (
        block_out,
        d_frames,
        small[0],
        small[1],
        small[2],
        small[3],
        small[4],
        small[5],
        grad_w_query,
        grad_w_key,
        grad_w_value,
        grad_w_out,
        grad_c_query,
        grad_c_key,
        grad_c_value,
        grad_c_out,
        grad_gate_w,
        grad_up_w,
        grad_down,
    )


def solution(mesh):
    return jax.shard_map(
        per_device,
        mesh=mesh,
        in_specs=(
            P("seq", "tensor"),
            P(),
            P(),
            P(),
            P("tensor"),
            P("tensor"),
            P("tensor"),
            P("tensor"),
            P("tensor"),
            P("tensor"),
            P(None, "tensor"),
            P(None, "tensor"),
            P(None, "tensor"),
            P("tensor", None),
            P(None, "tensor"),
            P(None, "tensor"),
            P(None, "tensor"),
            P("tensor", None),
            P(None, "tensor"),
            P(None, "tensor"),
            P("tensor", None),
            P("seq", "tensor"),
        ),
        out_specs=(
            P("seq", "tensor"),
            P("seq", "tensor"),
            P(("tensor", "seq")),
            P(("tensor", "seq")),
            P(("tensor", "seq")),
            P(("tensor", "seq")),
            P(("tensor", "seq")),
            P(("tensor", "seq")),
            P("seq", "tensor"),
            P("seq", "tensor"),
            P("seq", "tensor"),
            P(("tensor", "seq"), None),
            P("seq", "tensor"),
            P("seq", "tensor"),
            P("seq", "tensor"),
            P(("tensor", "seq"), None),
            P("seq", "tensor"),
            P("seq", "tensor"),
            P(("tensor", "seq"), None),
        ),
        check_vma=False,
    )
```

```python
import functools
import math

import jax
import jax.numpy as jnp
from jax import lax
from jax.experimental import pallas as pl
from jax.experimental.pallas import tpu as pltpu
from jax.sharding import PartitionSpec as P

HEAD_SIZE = 64
ROW_MIN = 2048
TILE = 256
BF16 = jnp.bfloat16
F32 = jnp.float32


def meeting(*values):
    return lax.optimization_barrier(values)


def after(value, token):
    return lax.optimization_barrier((value, token))[0]


def swap(value, axis, by):
    return lax.ppermute(value, axis, [(i, i ^ by) for i in range(lax.axis_size(axis))])


def shift(value, axis, by):
    peers = lax.axis_size(axis)
    pairs = [(i, i + by) for i in range(peers) if 0 <= i + by < peers]
    return lax.ppermute(value, axis, pairs)


def tensor_place():
    place = lax.axis_index("tensor")
    return place // 2, place % 2


def ordered(own, far, mate, far_mate, axis):
    side, core = tensor_place()
    near = (jnp.where(core == 0, own, mate), jnp.where(core == 0, mate, own))
    away = (jnp.where(core == 0, far, far_mate), jnp.where(core == 0, far_mate, far))
    low = [jnp.where(side == 0, n, a) for n, a in zip(near, away)]
    high = [jnp.where(side == 0, a, n) for n, a in zip(near, away)]
    return jnp.concatenate(low + high, axis)


def gather_near(own):
    far = swap(own, "tensor", 2)
    return own, swap(own, "tensor", 1), far, swap(far, "tensor", 1)


def gather_staged(own, first, second):
    far = swap(after(own, first), "tensor", 2)
    far, late = after((far, own), second)
    return own, swap(late, "tensor", 1), far, swap(far, "tensor", 1)


def gather(own, axis):
    own, mate, far, far_mate = gather_near(own)
    return ordered(own, far, mate, far_mate, axis)


def scatter_near(away, low):
    got = swap(away, "tensor", 1)
    total = (low.astype(F32) + got[low.shape[0] :].astype(F32)).astype(BF16)
    return got, total, swap(total, "tensor", 2)


def rows_to_cols(own, mate, far, far_mate, later):
    width = own.shape[1]
    got = after(swap(jnp.concatenate([far, far_mate], 1), "tensor", 2), later)
    other = swap(jnp.concatenate([mate, got[:, width:]], 0), "tensor", 1)
    size = own.shape[0]
    return jnp.concatenate([own, other[:size], got[:, :width], other[size:]], 0)


def quarters(value, axis):
    return jnp.split(value, 4, axis)


def own_blocks(near):
    return jnp.concatenate([quarters(value, 1)[r] for r, value in enumerate(near)], 0)


def trade(value, start, done):
    return after(swap(after(value, start), "seq", 1), done)


def halve(blocks, bit):
    count, rows, cols = blocks.shape
    side = (lax.axis_index("seq") >> bit) % 2
    parts = blocks.reshape(count // 2, 2, rows, cols)
    send = lax.dynamic_index_in_dim(parts, 1 - side, 1, False)
    keep = lax.dynamic_index_in_dim(parts, side, 1, False)
    return keep, swap(send, "seq", 1 << bit)


def added(keep, got):
    return keep.astype(F32) + got.astype(F32)


def halve_all(blocks, bit):
    while blocks.shape[0] > 1:
        blocks = added(*halve(blocks.astype(BF16), bit))
        bit += 1
    return blocks[0].astype(F32)


def halve_end(keep, got, bit):
    return halve_all(added(keep, got), bit)


def frame_clip_labels(segment, row_length):
    frame_index = jnp.arange(segment.shape[0], dtype=jnp.int32)
    border = (frame_index % row_length == 0) | (segment != jnp.roll(segment, 1))
    clip_starts = lax.cummax(jnp.where(border, frame_index, 0), axis=0)
    return (clip_starts, (frame_index - clip_starts + 1).astype(jnp.float32))


def tile_ranges(q_labels, key_labels):
    q = q_labels.reshape(-1, TILE)
    k = key_labels.reshape(-1, TILE)
    meets = (k[None, :, 0] <= q[:, None, -1]) & (k[None, :, -1] >= q[:, None, 0])
    index = jnp.arange(k.shape[0], dtype=jnp.int32)[None]
    low = jnp.min(jnp.where(meets, index, k.shape[0]), 1)
    high = jnp.max(jnp.where(meets, index + 1, 0), 1)
    return jnp.stack([low, high], 1).reshape(-1)

def head_rows(g):
    return slice(g * HEAD_SIZE, (g + 1) * HEAD_SIZE)

def fill_natural(dest, refs, which):
    size = refs[0].shape[2]
    for part, ref in enumerate(refs):
        dest[part * size : (part + 1) * size, :] = ref[which].T


def fill_tiles(dest, refs, which):
    pieces = refs[0].shape[2] // TILE
    for part, ref in enumerate(refs):
        for piece in range(pieces):
            dest[part * pieces + piece] = ref[which, :, piece * TILE : (piece + 1) * TILE]


def relative(place, r, size):
    return pl.ds(pl.multiple_of((place ^ r) * size, size), size)


def absorb(state, start, stop, base, q, cols, lab, klab, keys, vals):
    group = q.shape[0] // HEAD_SIZE

    def step(j, state):
        seen = klab[pl.ds(pl.multiple_of(j * TILE, TILE), TILE), :] == lab
        at = pl.ds(pl.multiple_of((j - base) * TILE, TILE), TILE)
        fresh = []
        for g in range(group):
            top, total, acc = state[3 * g : 3 * g + 3]
            s = dot_nn(keys[at, head_rows(g)], q[head_rows(g), cols])
            s = jnp.where(seen, s, -1e30)
            new = jnp.maximum(top, jnp.max(s, 0, keepdims=True))
            fade = jnp.exp(top - new)
            p = jnp.exp(s - new)
            total = total * fade + jnp.sum(p, 0, keepdims=True)
            acc = acc * fade + dot_nn(vals[j - base, head_rows(g), :], p.astype(BF16))
            fresh += [new, total, acc]
        return tuple(fresh)

    return lax.fori_loop(start, stop, step, tuple(state))


def near_body(span, q, kv, tk, tv, qlab, klab, tops, totals, mix, keys, vals):
    rows, size = q.shape
    pieces = size // TILE
    fill_natural(keys, (kv,), 0)
    fill_tiles(vals, (kv,), 1)
    for tile in range(pieces):
        cols = slice(tile * TILE, (tile + 1) * TILE)
        state = []
        for g in range(rows // HEAD_SIZE):
            part = q[head_rows(g), cols].astype(F32)
            top = jnp.sum(part * tk[head_rows(g), :], 0, keepdims=True)
            state += [
                top,
                jnp.ones_like(top),
                jnp.broadcast_to(tv[head_rows(g), :], (HEAD_SIZE, TILE)),
            ]
        start = jnp.maximum(span[2 * tile], pieces)
        stop = jnp.minimum(span[2 * tile + 1], 2 * pieces)
        state = absorb(state, start, stop, pieces, q, cols, qlab[:, cols], klab, keys, vals)
        for g in range(rows // HEAD_SIZE):
            tops[g : g + 1, cols], totals[g : g + 1, cols], mix[head_rows(g), cols] = state[
                3 * g : 3 * g + 3
            ]


def far_body(span, q, kv0, kv2, qlab, klab, w_out, tops, totals, mix,
             out, lse, away, own, low, keys0, keys2, vals0, vals2):
    rows, size = q.shape
    pieces = size // TILE
    for kv, keys, vals in ((kv0, keys0, vals0), (kv2, keys2, vals2)):
        fill_natural(keys, (kv,), 0)
        fill_tiles(vals, (kv,), 1)
    for tile in range(pieces):
        cols = slice(tile * TILE, (tile + 1) * TILE)
        lab = qlab[:, cols]
        state = []
        for g in range(rows // HEAD_SIZE):
            state += [tops[g : g + 1, cols], totals[g : g + 1, cols], mix[head_rows(g), cols]]
        stop = jnp.minimum(span[2 * tile + 1], pieces)
        state = absorb(state, span[2 * tile], stop, 0, q, cols, lab, klab, keys0, vals0)
        start = jnp.maximum(span[2 * tile], 2 * pieces)
        state = absorb(
            state, start, span[2 * tile + 1], 2 * pieces, q, cols, lab, klab, keys2, vals2
        )
        for g in range(rows // HEAD_SIZE):
            top, total, acc = state[3 * g : 3 * g + 3]
            out[head_rows(g), cols] = (acc / total).astype(BF16)
            lse[g : g + 1, cols] = top + jnp.log(total)
    place = span[2 * pieces]
    share = own.shape[0]

    def sent(r):
        return dot_tn(out[:, relative(place, r, share)], w_out[...])

    away[:share, :] = sent(1).astype(BF16)
    away[share:, :] = sent(3).astype(BF16)
    low[...] = sent(2).astype(BF16)
    own[...] = sent(0)


def backward_body(span, q, kv0, kv1, kv2, tk, tv, qlab, klab, w_out, out, lse,
                  g0, g1, g2, g3, dq, to_prev, kept, to_next, dtk, dtv,
                  og, keys, vals, tkeys, ak, av):
    rows, size = q.shape
    group = rows // HEAD_SIZE
    pieces = size // TILE
    share = g0.shape[0]
    for r, ref in enumerate((g0, g1, g2, g3)):
        og[:, relative(span[2 * pieces], r, share)] = dot_nt(w_out[...], ref[...]).astype(BF16)
    fill_natural(keys, (kv0, kv1, kv2), 0)
    fill_natural(vals, (kv0, kv1, kv2), 1)
    fill_tiles(tkeys, (kv0, kv1, kv2), 0)
    ak[...] = jnp.zeros_like(ak)
    av[...] = jnp.zeros_like(av)
    for tile in range(pieces):
        cols = slice(tile * TILE, (tile + 1) * TILE)
        lab = qlab[:, cols]
        state, norms, deltas = [], [], []
        for g in range(group):
            hr = head_rows(g)
            qf = q[hr, cols].astype(F32)
            gf = og[hr, cols].astype(F32)
            norm = lse[g : g + 1, cols]
            delta = jnp.sum(gf * out[hr, cols].astype(F32), 0, keepdims=True)
            pt = jnp.exp(jnp.sum(qf * tk[hr, :], 0, keepdims=True) - norm)
            st = pt * (jnp.sum(gf * tv[hr, :], 0, keepdims=True) - delta)
            gk = jnp.sum(qf * st, 1, keepdims=True)
            gv = jnp.sum(gf * pt, 1, keepdims=True)
            if tile == 0:
                dtk[hr, :] = gk
                dtv[hr, :] = gv
            else:
                dtk[hr, :] += gk
                dtv[hr, :] += gv
            state.append(tk[hr, :] * st)
            norms.append(norm)
            deltas.append(delta)

        def step(j, state):
            start = pl.multiple_of(j * TILE, TILE)
            seen = klab[pl.ds(start, TILE), :] == lab
            fresh = []
            for g in range(group):
                hr = head_rows(g)
                s = dot_nn(keys[pl.ds(start, TILE), hr], q[hr, cols])
                p = jnp.exp(jnp.where(seen, s, -1e30) - norms[g])
                m = dot_nn(vals[pl.ds(start, TILE), hr], og[hr, cols])
                ds = (p * (m - deltas[g])).astype(BF16)
                av[j, hr, :] += dot_nt(og[hr, cols], p.astype(BF16))
                ak[j, hr, :] += dot_nt(q[hr, cols], ds)
                fresh.append(state[g] + dot_nn(tkeys[j, hr, :], ds))
            return tuple(fresh)

        state = lax.fori_loop(span[2 * tile], span[2 * tile + 1], step, tuple(state))
        for g in range(group):
            dq[head_rows(g), cols] = state[g]
    for part, dest in enumerate((to_prev, kept, to_next)):
        for piece in range(pieces):
            at = slice(piece * TILE, (piece + 1) * TILE)
            dest[0, :, at] = ak[part * pieces + piece].astype(dest.dtype)
            dest[1, :, at] = av[part * pieces + piece].astype(dest.dtype)


def attend_near(span, q, kv, tk, tv, qlab, klab):
    cols, size = q.shape
    wide = lambda *dims: jax.ShapeDtypeStruct(dims, F32)
    vmem = pl.BlockSpec(memory_space=pltpu.VMEM)
    return pl.pallas_call(
        near_body,
        in_specs=[pl.BlockSpec(memory_space=pltpu.SMEM)] + [vmem] * 6,
        out_specs=[vmem] * 3,
        out_shape=[wide(cols // HEAD_SIZE, size), wide(cols // HEAD_SIZE, size), wide(cols, size)],
        scratch_shapes=[pltpu.VMEM((size, cols), BF16), pltpu.VMEM((size // TILE, cols, TILE), BF16)],
        name="attend_near", cost_estimate=FREE,
    )(span, q, kv, tk, tv, qlab, klab)


def attend_far(span, q, behind, ahead, qlab, klab, w_out, state):
    cols, size = q.shape
    share, width = size // 4, w_out.shape[1]
    low = lambda *dims: jax.ShapeDtypeStruct(dims, BF16)
    wide = lambda *dims: jax.ShapeDtypeStruct(dims, F32)
    vmem = pl.BlockSpec(memory_space=pltpu.VMEM)
    keys = pltpu.VMEM((size, cols), BF16)
    vals = pltpu.VMEM((size // TILE, cols, TILE), BF16)
    return pl.pallas_call(
        far_body,
        in_specs=[pl.BlockSpec(memory_space=pltpu.SMEM)] + [vmem] * 9,
        out_specs=[vmem] * 5,
        out_shape=[low(cols, size), wide(cols // HEAD_SIZE, size), low(2 * share, width),
                   wide(share, width), low(share, width)],
        scratch_shapes=[keys, keys, vals, vals],
        name="attend_far", cost_estimate=FREE,
    )(span, q, behind, ahead, qlab, klab, w_out, *state)


def attend_back(span, q, kvs, tk, tv, qlab, klab, w_out, out, lse, grads):
    cols, size = q.shape
    tiles = 3 * size // TILE
    low = lambda *dims: jax.ShapeDtypeStruct(dims, BF16)
    wide = lambda *dims: jax.ShapeDtypeStruct(dims, F32)
    vmem = pl.BlockSpec(memory_space=pltpu.VMEM)
    return pl.pallas_call(
        backward_body,
        in_specs=[pl.BlockSpec(memory_space=pltpu.SMEM)] + [vmem] * 15,
        out_specs=[vmem] * 6,
        out_shape=[wide(cols, size), low(2, cols, size), wide(2, cols, size), low(2, cols, size),
                   wide(cols, 1), wide(cols, 1)],
        scratch_shapes=[pltpu.VMEM((cols, size), BF16), pltpu.VMEM((3 * size, cols), BF16),
                        pltpu.VMEM((3 * size, cols), BF16), pltpu.VMEM((tiles, cols, TILE), BF16),
                        pltpu.VMEM((tiles, cols, TILE), F32), pltpu.VMEM((tiles, cols, TILE), F32)],
        name="attend_back", cost_estimate=FREE,
    )(span, q, *kvs, tk, tv, qlab, klab, w_out, out, lse, *grads)


def tail_body(place, dq, kept, ahead, behind, cosine, sine, wq, wk, wv, raw, away, own, low, flipped):
    part, size = dq.shape
    half = HEAD_SIZE // 2

    def returned(block, base, scale):
        for h in range(part // HEAD_SIZE):
            a = block[h * HEAD_SIZE : h * HEAD_SIZE + half, :]
            b = block[h * HEAD_SIZE + half : (h + 1) * HEAD_SIZE, :]
            at = base + h * HEAD_SIZE
            raw[at : at + half, :] = ((a * cosine[...] + b * sine[...]) * scale).astype(BF16)
            raw[at + half : at + HEAD_SIZE, :] = (
                (b * cosine[...] - a * sine[...]) * scale
            ).astype(BF16)

    def whole(index):
        return kept[index] + ahead[index].astype(F32) + behind[index].astype(F32)

    returned(dq[...], 0, 1.0 / math.sqrt(HEAD_SIZE))
    returned(whole(0), part, 1.0)
    raw[2 * part :, :] = whole(1).astype(BF16)
    flipped[...] = raw[...].T

    def sent(r):
        at = relative(place[0], r, part)
        return sum(
            dot_nt(flipped[:, i * part : (i + 1) * part], weight[at, :])
            for i, weight in enumerate((wq, wk, wv))
        )

    away[:size, :] = sent(1).astype(BF16)
    away[size:, :] = sent(3).astype(BF16)
    low[...] = sent(2).astype(BF16)
    own[...] = sent(0)


def tail(place, dq, kept, ahead, behind, tables, wq, wk, wv):
    part, size = dq.shape
    low = lambda *dims: jax.ShapeDtypeStruct(dims, BF16)
    vmem = pl.BlockSpec(memory_space=pltpu.VMEM)
    return pl.pallas_call(
        tail_body,
        in_specs=[pl.BlockSpec(memory_space=pltpu.SMEM)] + [vmem] * 9,
        out_specs=[vmem] * 4,
        out_shape=[low(3 * part, size), low(2 * size, part), jax.ShapeDtypeStruct((size, part), F32),
                   low(size, part)],
        scratch_shapes=[pltpu.VMEM((size, 3 * part), BF16)],
        name="tail", cost_estimate=FREE,
    )(place, dq, kept, ahead, behind, *tables, wq, wk, wv)


def rotary_tables(frame_positions):
    half_dim = HEAD_SIZE // 2
    frequency = jnp.exp(jnp.arange(half_dim, dtype=jnp.float32) * (-math.log(10000.0) / half_dim))
    angles = frequency[:, None] * frame_positions[None, :]
    return (jnp.cos(angles), jnp.sin(angles))


def rotate(rows, tables, sign=1.0):
    count, size = rows.shape
    halves = rows.reshape(count // HEAD_SIZE, 2, HEAD_SIZE // 2, size)
    cosine, sine = tables[0][None], tables[1][None] * sign
    first = halves[:, 0] * cosine - halves[:, 1] * sine
    second = halves[:, 1] * cosine + halves[:, 0] * sine
    return jnp.stack([first, second], 1).reshape(count, size)


def product(left, right):
    return jnp.dot(left, right, preferred_element_type=jnp.float32)


def inner_rows(left, right):
    return jnp.einsum("nd,nf->df", left, right, preferred_element_type=jnp.float32)


def back_project(gradient, weight):
    return jnp.einsum("nf,df->nd", gradient, weight, preferred_element_type=jnp.float32)


def by_feature(left, right):
    return jnp.einsum("nd,df->fn", left, right, preferred_element_type=jnp.float32)


def columns(weight, start, size):
    return lax.dynamic_slice_in_dim(weight, start, size, 1)


def rows_of(weight, start, size):
    return lax.dynamic_slice_in_dim(weight, start, size, 0)


def normalize(value_rows):
    means = jnp.mean(value_rows, -1, keepdims=True)
    centred = value_rows - means
    inverse = lax.rsqrt(jnp.mean(centred * centred, -1, keepdims=True) + 1e-05)
    return centred * inverse, inverse


def norm_backward(gradient, scaled, inverse, norm_gain):
    scaled_grad = gradient * norm_gain
    plain = jnp.mean(scaled_grad, -1, keepdims=True)
    cross = jnp.mean(scaled_grad * scaled, -1, keepdims=True)
    return inverse * (scaled_grad - plain - scaled * cross)


FREE = pl.CostEstimate(flops=1, transcendentals=0, bytes_accessed=1)


def dot_nn(left, right):
    return lax.dot_general(left, right, (((1,), (0,)), ((), ())), preferred_element_type=F32)


def dot_nt(left, right):
    return lax.dot_general(left, right, (((1,), (1,)), ((), ())), preferred_element_type=F32)


def dot_tn(left, right):
    return lax.dot_general(left, right, (((0,), (0,)), ((), ())), preferred_element_type=F32)


def head_weights(query, key, lanes, which):
    mine = jnp.where(lanes == which, query, jnp.zeros_like(query))
    scores = dot_nt(mine, key) * (1.0 / math.sqrt(HEAD_SIZE))
    weights = jnp.exp(scores - jnp.max(scores, -1, keepdims=True))
    return weights / jnp.sum(weights, -1, keepdims=True)


def pair_cols(refs, p, rows):
    ref = refs[p * 2 * HEAD_SIZE // refs[0].shape[1]]
    start = p * 2 * HEAD_SIZE % refs[0].shape[1]
    return ref[rows, start : start + 2 * HEAD_SIZE]


def cross_forward_body(width_block, place, rows, own, got, far, norms, q0, q1, q2, q3,
                       c0, c1, c2, c3, o0, o1, o2, o3,
                       front, queries, first, second, normed_three,
                       flip_own, flip_away):
    width = rows.shape[1]
    kv = (c0, c1, c2, c3)
    context_rows = c0.shape[0] // 2
    key_rows, value_rows = slice(0, context_rows), slice(context_rows, 2 * context_rows)
    lanes = lax.broadcasted_iota(jnp.int32, (rows.shape[0], 2 * HEAD_SIZE), 1) // HEAD_SIZE
    residual = (
        rows[...].astype(F32) + own[...] + got[...].astype(F32) + far[...].astype(F32)
    )
    first[...] = residual
    scaled, _ = normalize(residual)
    low = (scaled * norms[2:3, :] + norms[3:4, :]).astype(BF16)
    front[:, :width] = low
    part = width // 4
    for b, ref in enumerate((q0, q1, q2, q3)):
        queries[:, b * part : (b + 1) * part] = dot_nn(low, ref[...]).astype(BF16)
    for p in range(width // (2 * HEAD_SIZE)):
        cols = slice(p * 2 * HEAD_SIZE, (p + 1) * 2 * HEAD_SIZE)
        q, k, v = queries[:, cols], pair_cols(kv, p, key_rows), pair_cols(kv, p, value_rows)
        mixed = [dot_nn(head_weights(q, k, lanes, g).astype(BF16), v) for g in (0, 1)]
        front[:, width + cols.start : width + cols.stop] = jnp.where(lanes == 0, mixed[0], mixed[1]).astype(BF16)
    for b, ref in enumerate((o0, o1, o2, o3)):
        residual = residual + dot_nn(front[:, width + b * part : width + (b + 1) * part], ref[...])
    second[...] = residual
    scaled, _ = normalize(residual)
    low = (scaled * norms[4:5, :] + norms[5:6, :]).astype(BF16)
    normed_three[...] = low
    deal_rows(low.T, width_block, place[0], flip_own, flip_away)


def cross_forward(devices, place, rows, own, got, far, norms, query_parts, kv_parts, out_parts):
    size, width = rows.shape
    low = jax.ShapeDtypeStruct(rows.shape, BF16)
    both = jax.ShapeDtypeStruct((size, 2 * width), BF16)
    wide = jax.ShapeDtypeStruct(rows.shape, F32)
    flip = jax.ShapeDtypeStruct((width // 2, size), BF16)
    vmem = pl.BlockSpec(memory_space=pltpu.VMEM)
    block = pl.BlockSpec((size, width), lambda i: (0, 0))
    return pl.pallas_call(
        functools.partial(cross_forward_body, width // devices),
        grid=(1,),
        in_specs=[pl.BlockSpec(memory_space=pltpu.SMEM)] + [block] * 4 + [vmem] * 13,
        out_shape=[both, low, wide, wide, low, flip, flip],
        cost_estimate=FREE, name="cross",
    )(place, rows, own, got, far, norms, *query_parts, *kv_parts, *out_parts)


def deal_rows(rows, size, column, own, away):
    for b in range(rows.shape[0] // (2 * size)):
        at = slice(b * size, (b + 1) * size)
        even = rows[2 * b * size : (2 * b + 1) * size, :]
        odd = rows[(2 * b + 1) * size : (2 * b + 2) * size, :]

        @pl.when(column == 0)
        def _():
            own[at, :] = even
            away[at, :] = odd

        @pl.when(column != 0)
        def _():
            own[at, :] = odd
            away[at, :] = even


def ffn_part(normed, grad, gate_w, up_w, down_w, hidden, hid_own, hid_away, gate_grad, lifted_grad,
             unit_block, column):
    gate = dot_nn(normed, gate_w[...])
    lifted = dot_nn(normed, up_w[...])
    back = dot_nt(grad, down_w[...]).astype(BF16).astype(F32)
    sig = jax.nn.sigmoid(gate)
    swish = gate * sig
    made = (swish * lifted).astype(BF16)
    hidden[...] = made
    deal_rows(made.T, unit_block, column, hid_own, hid_away)
    gg = (back * lifted * sig * (1.0 + gate * (1.0 - sig))).astype(BF16)
    lg = (back * swish).astype(BF16)
    gate_grad[...] = gg
    lifted_grad[...] = lg
    return dot_nt(gg, gate_w[...]) + dot_nt(lg, up_w[...])


def ffn_first_body(unit_block, place, n0, n1, n2, n3, g0, g1, g2, g3, gate_w, up_w, down_w,
                   hidden, hid_own, hid_away, gate_grad, lifted_grad, normed, grad, grad_pair,
                   total):
    share, part = n0.shape[0], g0.shape[2]
    for b, ref in enumerate((n0, n1, n2, n3)):
        normed[b * share : (b + 1) * share, :] = ref[...]
    for c, ref in enumerate((g0, g1, g2, g3)):
        for b in range(4):
            rows, cols = relative(place[1], b, share), relative(place[1], c, part)
            grad[b * share : (b + 1) * share, cols] = ref[0, rows, :]
            grad_pair[b * share : (b + 1) * share, cols] = ref[1, rows, :]
    total[...] = ffn_part(
        normed[...], grad[...], gate_w, up_w, down_w, hidden, hid_own, hid_away, gate_grad,
        lifted_grad, unit_block, place[0],
    )


def ffn_second_body(unit_block, place, normed, grad, total, gate_w, up_w, down_w,
                    hidden, hid_own, hid_away, gate_grad, lifted_grad, away, own, low):
    share = own.shape[0]
    found = total[...] + ffn_part(
        normed[...], grad[...], gate_w, up_w, down_w, hidden, hid_own, hid_away, gate_grad,
        lifted_grad, unit_block, place[0],
    )
    own[...] = found[:share, :]
    low[...] = found[2 * share : 3 * share, :].astype(BF16)
    away[:share, :] = found[share : 2 * share, :].astype(BF16)
    away[share:, :] = found[3 * share :, :].astype(BF16)


def ffn(devices, place, half, inputs, gate_w, up_w, down_w):
    share = inputs[0].shape[0] if half == 0 else inputs[0].shape[0] // 4
    width = inputs[0].shape[1]
    size, units = 4 * share, gate_w.shape[1]
    tile = units // 2
    low = lambda *dims: jax.ShapeDtypeStruct(dims, BF16)
    wide = lambda *dims: jax.ShapeDtypeStruct(dims, F32)
    vmem = pl.BlockSpec(memory_space=pltpu.VMEM)
    cols = pl.BlockSpec((width, tile), lambda i: (0, half))
    rows = pl.BlockSpec((tile, width), lambda i: (half, 0))
    made = [low(size, tile), low(tile // 2, size), low(tile // 2, size), low(size, tile),
            low(size, tile)]
    if half == 0:
        made += [low(size, width), low(size, width), low(size, width), wide(size, width)]
    else:
        made += [low(2 * share, width), wide(share, width), low(share, width)]
    return pl.pallas_call(
        functools.partial(ffn_second_body if half else ffn_first_body, units // devices),
        grid=(1,),
        in_specs=[pl.BlockSpec(memory_space=pltpu.SMEM)] + [vmem] * len(inputs)
        + [cols, cols, rows],
        out_specs=[vmem] * len(made),
        out_shape=made,
        cost_estimate=FREE, name="ffn",
    )(place, *inputs, gate_w, up_w, down_w)


def cross_backward_body(own, got, far, grad, first, second, norms, q0, q1, q2, q3,
                        c0, c1, c2, c3, o0, o1, o2, o3, queries,
                        back_rows, kv_grad, vectors, grad_one, crossed_grad):
    width = grad.shape[1]
    kv = (c0, c1, c2, c3)
    context_rows = c0.shape[0] // 2
    key_rows, value_rows = slice(0, context_rows), slice(context_rows, 2 * context_rows)
    part = width // 4
    lanes = lax.broadcasted_iota(jnp.int32, (grad.shape[0], 2 * HEAD_SIZE), 1) // HEAD_SIZE
    lane_k = lax.broadcasted_iota(jnp.int32, (context_rows, 2 * HEAD_SIZE), 1) // HEAD_SIZE
    scale = 1.0 / math.sqrt(HEAD_SIZE)
    arrived = own[...] + got[...].astype(F32) + far[...].astype(F32)
    scaled, inverse = normalize(second[...])
    vectors[0:1, :] = jnp.sum(arrived * scaled, 0, keepdims=True)
    vectors[1:2, :] = jnp.sum(arrived, 0, keepdims=True)
    two = grad[...].astype(F32) + norm_backward(arrived, scaled, inverse, norms[4:5, :])
    low = two.astype(BF16)
    back_rows[:, :width] = low
    for b, ref in enumerate((o0, o1, o2, o3)):
        crossed_grad[:, b * part : (b + 1) * part] = dot_nt(low, ref[...]).astype(BF16)
    for p in range(width // (2 * HEAD_SIZE)):
        cols = slice(p * 2 * HEAD_SIZE, (p + 1) * 2 * HEAD_SIZE)
        q, k, v = queries[:, cols], pair_cols(kv, p, key_rows), pair_cols(kv, p, value_rows)
        g_rows = crossed_grad[:, cols]
        found = []
        for g in (0, 1):
            probs = head_weights(q, k, lanes, g)
            change = dot_nt(jnp.where(lanes == g, g_rows, jnp.zeros_like(g_rows)), v)
            delta = jnp.sum(change * probs, -1, keepdims=True)
            ds = (probs * (change - delta)).astype(BF16)
            found.append((dot_nn(ds, k), dot_tn(ds, q), dot_tn(probs.astype(BF16), g_rows)))
        back_rows[:, width + cols.start : width + cols.stop] = (
            jnp.where(lanes == 0, found[0][0], found[1][0]) * scale
        ).astype(BF16)
        kv_grad[:context_rows, cols] = (
            jnp.where(lane_k == 0, found[0][1], found[1][1]) * scale
        ).astype(BF16)
        kv_grad[context_rows:, cols] = jnp.where(lane_k == 0, found[0][2], found[1][2]).astype(
            BF16
        )
    back = jnp.zeros(grad.shape, F32)
    for b, ref in enumerate((q0, q1, q2, q3)):
        back = back + dot_nt(back_rows[:, width + b * part : width + (b + 1) * part], ref[...])
    scaled, inverse = normalize(first[...])
    vectors[2:3, :] = jnp.sum(back * scaled, 0, keepdims=True)
    vectors[3:4, :] = jnp.sum(back, 0, keepdims=True)
    grad_one[...] = (two + norm_backward(back, scaled, inverse, norms[2:3, :])).astype(BF16)


def cross_backward(own, got, far, grad, first, second, norms, query_parts, kv_parts, out_parts,
                   queries):
    rows, width = own.shape
    low = lambda r: jax.ShapeDtypeStruct((r, width), BF16)
    block = pl.BlockSpec((rows, width), lambda i: (0, 0))
    return pl.pallas_call(
        cross_backward_body,
        grid=(1,),
        out_shape=[jax.ShapeDtypeStruct((rows, 2 * width), BF16), low(kv_parts[0].shape[0]),
                   jax.ShapeDtypeStruct((4, width), F32), low(rows)],
        in_specs=[block] * 6 + [pl.BlockSpec(memory_space=pltpu.VMEM)] * 14,
        scratch_shapes=[pltpu.VMEM((rows, width), BF16)],
        cost_estimate=FREE, name="cross_back",
    )(own, got, far, grad, first, second, norms, *query_parts, *kv_parts, *out_parts, queries)


def meet_rows_body(size, side, own_a, pair_a, own_b, pair_b, right, right_pair, keep, send):
    half = keep.shape[0] // 2
    for b, (own, pair) in enumerate(((own_a, pair_a), (own_b, pair_b))):
        made = (dot_nn(own[...], right[...]) + dot_nn(pair[...], right_pair[...])).astype(BF16)
        at = pl.ds(b * half, half)
        deal_rows(made, size, side[0], keep.at[at], send.at[at])


def meet_rows(size, side, lefts, rights):
    count, frames = lefts[0].shape
    width = rights[0].shape[1]
    tile = width // 3
    left = pl.BlockSpec((count, frames), lambda i: (0, 0))
    right = pl.BlockSpec((frames, tile), lambda i: (0, i))
    return pl.pallas_call(
        functools.partial(meet_rows_body, size),
        grid=(3,),
        in_specs=[pl.BlockSpec(memory_space=pltpu.SMEM)] + [left] * 4 + [right] * 2,
        out_specs=[pl.BlockSpec((count, tile), lambda i: (0, i))] * 2,
        out_shape=[jax.ShapeDtypeStruct((count, width), BF16)] * 2,
        name="meet_rows", cost_estimate=FREE,
    )(side, *lefts, *rights)


def meet_cols_body(size, side, p0, p1, p2, p3, a, a_pair, b, b_pair, keep, send):
    own, pair = (jnp.concatenate([p[i] for p in (p0, p1, p2, p3)], 1) for i in (0, 1))
    width = a.shape[1]
    for left, (right, right_pair) in ((0, (a, a_pair)), (width, (b, b_pair))):
        made = (dot_nn(own, right[...]) + dot_nn(pair, right_pair[...])).astype(BF16)
        cols = pl.ds(left, width)
        deal_rows(made, size, side[0], keep.at[:, cols], send.at[:, cols])


def meet_cols(size, side, near, rights):
    half = jax.ShapeDtypeStruct((near[0].shape[1] // 2, 2 * rights[0].shape[1]), BF16)
    return pl.pallas_call(
        functools.partial(meet_cols_body, size),
        in_specs=[pl.BlockSpec(memory_space=pltpu.SMEM)] + [pl.BlockSpec(memory_space=pltpu.VMEM)] * 8,
        out_shape=[half] * 2,
        name="meet_cols", cost_estimate=FREE,
    )(side, *near, *rights)


def down_body(first, second, down_w, away, own, low):
    share, units = own.shape[0], first.shape[1]

    def sent(r):
        at = slice(r * share, (r + 1) * share)
        return dot_nn(first[at, :], down_w[:units, :]) + dot_nn(second[at, :], down_w[units:, :])

    away[:share, :] = sent(1).astype(BF16)
    away[share:, :] = sent(3).astype(BF16)
    low[...] = sent(2).astype(BF16)
    own[...] = sent(0)


def down_parts(first, second, down_w):
    share, width = first.shape[0] // 4, down_w.shape[1]
    low = lambda *dims: jax.ShapeDtypeStruct(dims, BF16)
    return pl.pallas_call(
        down_body,
        out_shape=[low(2 * share, width), jax.ShapeDtypeStruct((share, width), F32),
                   low(share, width)],
        name="down", cost_estimate=FREE,
    )(first, second, down_w)


def bundle_body(devices, place, f02, f13, b02, b13, a0, a1, a2, a3, attended,
                context, kv, times, keep_a, send_a, keep_b, send_b):
    width = a0.shape[1]
    part, share = width // 4, a0.shape[0]

    def near(even, odd):
        return even[0], odd[0], even[1], odd[1]

    own = lambda rows: jnp.concatenate(
        [row[:, width + r * part : width + (r + 1) * part] for r, row in enumerate(rows)], 0
    )
    full = lambda rows: jnp.concatenate([row[:, :width] for row in rows], 0)
    fronts, backs = near(f02, f13), near(b02, b13)
    rows = width // devices
    small = part // devices
    half = width // 2

    def put(block, base, left, out):
        size = block.shape[0] // devices
        cols = slice(left, left + block.shape[1])
        low = block.astype(BF16)
        for d in range(0, devices, 2):
            at = slice(base, base + size)
            even, odd = low[d * size : (d + 1) * size, :], low[(d + 1) * size : (d + 2) * size, :]

            @pl.when(place[0] == 0)
            def _():
                out[0][d // 2, at, cols] = even
                out[1][d // 2, at, cols] = odd

            @pl.when(place[0] != 0)
            def _():
                out[0][d // 2, at, cols] = odd
                out[1][d // 2, at, cols] = even

    send_a[:, rows:, :] = jnp.zeros((devices // 2, send_a.shape[1] - rows, half), BF16)
    row = jnp.broadcast_to(times[...], (times.shape[0], 2 * HEAD_SIZE)).T[:1, :]
    send_a[0, rows : rows + 1, :] = row.astype(BF16)
    put(dot_tn(full(fronts), own(backs)), 0, 0, (keep_a, send_a))
    count = context.shape[0]
    put(dot_tn(context[...], kv[:count, :]), 0, part, (keep_a, send_a))
    put(dot_tn(context[...], kv[count:, :]), rows // 2, part, (keep_a, send_a))
    grads = dot_tn(own(fronts), full(backs))
    put(grads[:, :half], 0, 0, (keep_b, send_b))
    put(grads[:, half:], small, 0, (keep_b, send_b))
    grads = sum(
        dot_nn(attended[:, relative(place[1], r, share)], ref[...])
        for r, ref in enumerate((a0, a1, a2, a3))
    )
    put(grads[:, :half], 2 * small, 0, (keep_b, send_b))
    put(grads[:, half:], 3 * small, 0, (keep_b, send_b))


def bundle_grads(devices, place, fronts, backs, ones, attended, context, kv, times):
    width = ones[0].shape[1]
    vmem = pl.BlockSpec(memory_space=pltpu.VMEM)
    return pl.pallas_call(
        functools.partial(bundle_body, devices),
        in_specs=[pl.BlockSpec(memory_space=pltpu.SMEM)] + [vmem] * 12,
        out_specs=[vmem] * 4,
        out_shape=[
            jax.ShapeDtypeStruct((devices // 2, width // devices + more, width // 2), BF16)
            for more in (0, 16, 0, 0)
        ],
        name="bundle", cost_estimate=FREE,
    )(place, *fronts, *backs, *ones, attended, context, kv, times)


def front_body(width_block, place, x0, x1, x2, x3, g0, g1, g2, g3, cosine, sine, wq, wk, wv,
               time_row, context, ck, cv,
               queries, pair, rows, low, nrm_own, nrm_away, norms, means, inverses,
               time_scaled, time_low, time_keys, time_values, kv, wide):
    size, part = x0.shape
    for r, (x, g) in enumerate(((x0, g0), (x1, g1), (x2, g2), (x3, g3))):
        start = pl.multiple_of((place[0] ^ r) * part, 128)
        wide[:, pl.ds(start, part)] = x[...]
        norms[:, pl.ds(start, part)] = g[...]
    share = size // 4
    rows[...] = wide[pl.ds(pl.multiple_of(place[0] * share, share), share), :]
    values = wide[...].astype(F32)
    mean = jnp.mean(values, -1, keepdims=True)
    centred = values - mean
    inverse = lax.rsqrt(jnp.mean(centred * centred, -1, keepdims=True) + 1e-05)
    means[...] = mean
    inverses[...] = inverse
    normed = (centred * inverse * norms[0:1, :] + norms[1:2, :]).astype(BF16)
    low[...] = normed
    half = HEAD_SIZE // 2

    def turned(weight):
        return dot_nn(normed, weight[...]).T

    def rotated(block, dest, scale):
        for h in range(part // HEAD_SIZE):
            a = block[h * HEAD_SIZE : h * HEAD_SIZE + half, :]
            b = block[h * HEAD_SIZE + half : (h + 1) * HEAD_SIZE, :]
            dest[h * HEAD_SIZE : h * HEAD_SIZE + half, :] = (
                (a * cosine[...] - b * sine[...]) * scale
            ).astype(BF16)
            dest[h * HEAD_SIZE + half : (h + 1) * HEAD_SIZE, :] = (
                (b * cosine[...] + a * sine[...]) * scale
            ).astype(BF16)

    scaled, _ = normalize(jnp.broadcast_to(time_row[...].astype(F32), (8, 4 * part)))
    time_scaled[...] = scaled[:1, :]
    made = (scaled * norms[0:1, :] + norms[1:2, :]).astype(BF16)
    time_low[...] = made[:1, :].astype(F32)
    time_keys[...] = dot_nn(made, wk[...]).astype(BF16).astype(F32).T[:, :1]
    time_values[...] = dot_nn(made, wv[...]).astype(BF16).astype(F32).T[:, :1]
    count = context.shape[0]
    kv[:count, :] = dot_nn(context[...], ck[...]).astype(BF16)
    kv[count:, :] = dot_nn(context[...], cv[...]).astype(BF16)
    rotated(turned(wk), pair.at[0], 1.0)
    pair[1] = turned(wv).astype(BF16)
    rotated(turned(wq), queries, 1.0 / math.sqrt(HEAD_SIZE))
    deal_rows(normed.T, width_block, place[1], nrm_own, nrm_away)


def front(devices, place, parts, norm_parts, tables, wq, wk, wv, time_row, context, ck, cv):
    size, part = parts[0].shape
    width = 4 * part
    low = lambda *s: jax.ShapeDtypeStruct(s, BF16)
    wide = lambda *s: jax.ShapeDtypeStruct(s, F32)
    vmem = pl.BlockSpec(memory_space=pltpu.VMEM)
    return pl.pallas_call(
        functools.partial(front_body, width // devices),
        in_specs=[pl.BlockSpec(memory_space=pltpu.SMEM)] + [vmem] * 17,
        out_specs=[vmem] * 14,
        out_shape=[low(part, size), low(2, part, size), low(size // 4, width), low(size, width),
                   low(width // 2, size), low(width // 2, size), wide(6, width),
                   wide(size, 1), wide(size, 1), wide(1, width), wide(1, width), wide(part, 1),
                   wide(part, 1), low(2 * context.shape[0], part)],
        scratch_shapes=[pltpu.VMEM((size, width), BF16)],
        cost_estimate=FREE, name="front",
    )(place, *parts, *norm_parts, *tables, wq, wk, wv, time_row, context, ck, cv)


def per_device(
    frames,
    segment,
    time_token,
    context,
    gain_attn,
    bias_attn,
    gain_cross,
    bias_cross,
    gain_ffn,
    bias_ffn,
    w_query,
    w_key,
    w_value,
    w_out,
    c_query,
    c_key,
    c_value,
    c_out,
    w_gate,
    w_up,
    w_down,
    out_grad,
):
    local_rows = frames.shape[0]
    local_width = frames.shape[1]
    model_width = w_query.shape[0]
    head_cols = w_query.shape[1]
    heads = head_cols // HEAD_SIZE
    number_of_frames = lax.axis_size("seq") * local_rows
    row_length = min(max(ROW_MIN, 64 * lax.axis_size("seq")), number_of_frames)
    first_frame = lax.axis_index("seq") * local_rows
    own_start = lax.axis_index("tensor") * local_width

    def own_cols(value):
        return lax.dynamic_slice_in_dim(value, own_start, local_width, value.ndim - 1)

    place = lax.axis_index("tensor")
    share = local_rows // 4

    def row_block(value, index):
        return rows_of(value, index * share, share)

    column = lax.axis_index("seq") % 2
    frame_parts_near = gather_near(frames)
    norm_parts = gather_near(
        jnp.stack([gain_attn, bias_attn, gain_cross, bias_cross, gain_ffn, bias_ffn])
    )
    clip_starts, frame_positions = frame_clip_labels(segment, row_length)
    own_labels = lax.dynamic_slice_in_dim(clip_starts, first_frame, local_rows)
    own_positions = lax.dynamic_slice_in_dim(frame_positions, first_frame, local_rows)
    blanks = jnp.full((local_rows,), -1, jnp.int32)
    key_labels = lax.dynamic_slice_in_dim(
        jnp.concatenate([blanks, clip_starts, blanks]), first_frame, 3 * local_rows
    )
    spans = jnp.concatenate(
        [tile_ranges(own_labels, key_labels), place.astype(jnp.int32).reshape(1)]
    )
    places = jnp.stack([column, place]).astype(jnp.int32)
    label_row, label_column = own_labels[None, :], key_labels[:, None]
    row_index = first_frame // row_length
    time_row = lax.dynamic_slice_in_dim(time_token, row_index, 1, 0)
    row_context = lax.dynamic_slice_in_dim(context, row_index, 1, 0)[0]
    context_rows = row_context.shape[0]
    tables = rotary_tables(own_positions)
    score_scale = 1.0 / math.sqrt(HEAD_SIZE)
    all_heads = model_width // HEAD_SIZE

    (
        queries, both, frame_rows, frame_normed, one_own_half, one_away_half, norms, means_one,
        inverse_one, scaled_time, time_normed, time_keys, time_values, context_kv,
    ) = front(
        lax.axis_size("seq"), jnp.flip(places), frame_parts_near, norm_parts, tables, w_query,
        w_key, w_value, time_row, row_context, c_key, c_value,
    )
    both, out_pair = meeting(both, swap(after(out_grad, frame_parts_near[2]), "seq", 1))
    grad_both = jnp.stack([out_grad, out_pair])
    behind, ahead = shift(both, "seq", 1), shift(both, "seq", -1)
    query_far = swap(after(c_query, frame_parts_near[3]), "tensor", 2)
    out_far = swap(after(c_out, frame_parts_near[3]), "tensor", 2)
    state = attend_near(spans, queries, both, time_keys, time_values, label_row, label_column)
    behind, ahead, query_far, out_far, *state = meeting(
        behind, ahead, query_far, out_far, *state
    )
    query_own, out_own, context_late = after((c_query, c_out, context_kv), behind)
    weights_near = [
        swap(value, "tensor", 1) for value in (query_own, query_far, out_own, out_far)
    ]
    kv_far = swap(context_late, "tensor", 2)
    attended, log_totals, one_away, one_own, one_low = attend_far(
        spans, queries, behind, ahead, label_row, label_column, w_out, state
    )
    one_away, one_low, kv_far, *weights_near = meeting(one_away, one_low, kv_far, *weights_near)
    kv_both = jnp.concatenate([context_kv, kv_far], 0)
    kv_other = swap(kv_both, "tensor", 1)
    kv_rows = context_kv.shape[0]
    kv_parts = (context_kv, kv_other[:kv_rows], kv_far, kv_other[kv_rows:])
    query_parts = (c_query, weights_near[0], query_far, weights_near[1])
    out_parts = (c_out, weights_near[2], out_far, weights_near[3])
    one_got, _, one_far = scatter_near(one_away, one_low)
    (
        front_rows, cross_queries, residual_one, residual_two, normed_share, flip_own, flip_away,
    ) = cross_forward(
        lax.axis_size("seq"), places, frame_rows, one_own, one_got, one_far, norms,
        query_parts, kv_parts, out_parts,
    )
    grad_far = swap(after(grad_both, one_far), "tensor", 2)
    normed_share, normed_got, grad_far = meeting(
        normed_share, swap(after(one_away_half, one_low), "seq", 1), grad_far
    )
    grad_late, grad_far_late = after((grad_both, grad_far), normed_share)
    grad_mate, grad_far_mate = swap(grad_late, "tensor", 1), swap(grad_far_late, "tensor", 1)
    grad_parts = (grad_both, grad_mate, grad_far, grad_far_mate)
    three_parts = gather_near(normed_share)
    flip_got = swap(after(flip_away, normed_share), "seq", 1)
    front_far = swap(after(front_rows, three_parts[3]), "tensor", 2)
    devices = lax.axis_size("seq")
    (
        hidden_a, hidden_own_a, hidden_away_a, gate_a, lifted_a, normed_three, grad_near, grad_pair,
        ffn_total,
    ) = ffn(devices, places, 0, (*three_parts, *grad_parts), w_gate, w_up, w_down)
    ffn_total, flip_got = meeting(ffn_total, flip_got)
    flip_both = jnp.stack([flip_own, flip_got])
    flip_far = swap(flip_both, "tensor", 2)
    hidden_got_a, gate_got_a = swap(hidden_away_a, "seq", 1), swap(gate_a, "seq", 1)
    hidden_b, hidden_own_b, hidden_away_b, gate_b, lifted_b, three_away, three_own, three_low = ffn(
        devices, places, 1, (normed_three, grad_near, ffn_total), w_gate, w_up, w_down
    )
    three_away, three_low, flip_far, front_far, hidden_got_a = meeting(
        three_away, three_low, flip_far, front_far, hidden_got_a
    )
    three_got, _, three_far = scatter_near(three_away, three_low)
    hidden_got_b = swap(after(hidden_away_b, three_low), "seq", 1)
    lifted_got_a = swap(after(lifted_a, three_far), "seq", 1)
    flip_late, flip_far_late, gate_late = after((flip_both, flip_far, gate_b), three_far)
    flip_mate, flip_far_mate = swap(flip_late, "tensor", 1), swap(flip_far_late, "tensor", 1)
    gate_got_b = swap(gate_late, "seq", 1)
    front_both = jnp.stack([front_rows, front_far])
    back_rows, kv_grad, norm_vectors, grad_one = cross_backward(
        three_own, three_got, three_far, grad_near, residual_one, residual_two, norms,
        query_parts, kv_parts, out_parts, cross_queries,
    )
    grad_one, gate_got_a, hidden_got_b, flip_mate, flip_far_mate = meeting(
        grad_one, gate_got_a, hidden_got_b, flip_mate, flip_far_mate
    )
    count = lax.axis_size("seq")
    level_side = ((lax.axis_index("seq") >> 1) % 2).astype(jnp.int32).reshape(1)
    rows = model_width // count

    def traded(dealt):
        keep, send = [value.reshape(count // 4, rows, -1) for value in dealt]
        return keep, swap(send, "seq", 2)

    down_keep, down_got = traded(
        meet_rows(
            rows, level_side, (hidden_own_a, hidden_got_a, hidden_own_b, hidden_got_b),
            (grad_near, grad_pair),
        )
    )
    context_parts = quarters(kv_grad, 1)
    context_got = swap(jnp.concatenate([context_parts[1], context_parts[3]], 0), "tensor", 1)
    one_far_rows, down_keep = meeting(swap(grad_one, "tensor", 2), down_keep)
    one_parts = (
        grad_one, swap(grad_one, "tensor", 1), one_far_rows, swap(one_far_rows, "tensor", 1)
    )
    *one_parts, front_other, context_got, gate_got_b, lifted_got_a = meeting(
        *one_parts, swap(after(front_both, grad_one), "tensor", 1), context_got,
        gate_got_b, lifted_got_a,
    )
    context_low = (
        context_parts[2].astype(F32) + context_got[context_parts[2].shape[0] :].astype(F32)
    ).astype(BF16)
    context_far = swap(context_low, "tensor", 2)
    back_far = swap(after(back_rows, one_parts[3]), "tensor", 2)
    lifted_got_b = swap(after(lifted_b, grad_one), "seq", 1)
    query_grad, to_prev, kept, to_next, time_key_grad, time_value_grad = attend_back(
        spans, queries, (behind, both, ahead), time_keys, time_values, label_row, label_column,
        w_out, attended, log_totals, one_parts,
    )
    to_prev, to_next, back_far, lifted_got_b, down_got, context_far = meeting(
        to_prev, to_next, back_far, lifted_got_b, down_got, context_far
    )
    from_next, from_prev = shift(to_prev, "seq", -1), shift(to_next, "seq", 1)
    down_keep, down_got = halve(added(down_keep, down_got).astype(BF16), 2)
    flip_near = (flip_both, flip_mate, flip_far, flip_far_mate)
    first_keep, first_got = traded(
        meet_cols(rows, level_side, flip_near, after((gate_a, gate_got_a, lifted_a, lifted_got_a), to_prev))
    )
    second_keep, second_got = traded(
        meet_cols(
            rows, level_side, flip_near, (gate_b, gate_got_b, lifted_b, lifted_got_b)
        )
    )
    down_away, down_own, down_low = down_parts(after(hidden_a, to_prev), hidden_b, w_down)
    back_both = jnp.stack([back_rows, back_far])
    back_other = swap(back_both, "tensor", 1)
    context_own = (
        context_parts[0].astype(F32)
        + context_got[: context_far.shape[0]].astype(F32)
        + context_far.astype(F32)
    )
    time_both = jnp.concatenate([time_key_grad, time_value_grad], 0)
    keep_a, send_a, keep_b, send_b = bundle_grads(
        count, places, (front_both, front_other), (back_both, back_other), one_parts, attended,
        row_context,
        context_own.astype(BF16), time_both,
    )
    from_next, from_prev, down_got, send_a, send_b = meeting(
        from_next, from_prev, down_got, send_a, send_b
    )
    got_a = swap(send_a, "seq", 1)
    raw, last_away, last_own, last_low = tail(
        places[1:], query_grad, kept, from_next, from_prev, tables, w_query, w_key, w_value
    )
    last_got = swap(last_away, "tensor", 1)
    raw_got = swap(raw, "seq", 1)
    last_sum = (
        last_low.astype(F32) + last_got[local_rows:].astype(F32)
    ).astype(BF16)
    last_sum, first_got, second_got = meeting(last_sum, first_got, second_got)
    first_keep, first_got = halve(added(first_keep, first_got).astype(BF16), 2)
    second_keep, second_got = halve(added(second_keep, second_got).astype(BF16), 2)
    last_far = swap(last_sum, "tensor", 2)
    frame_grad = last_own + last_got[:local_rows].astype(F32) + last_far.astype(F32)

    def to_frames(rows, weight):
        return jnp.einsum("fn,df->nd", rows, weight, preferred_element_type=F32)

    time_key_grad, time_value_grad = after((time_key_grad, time_value_grad), from_next)
    time_grad = to_frames(time_key_grad.astype(BF16), w_key) + to_frames(
        time_value_grad.astype(BF16), w_value
    )
    own_scaled = (frames.astype(F32) - means_one) * inverse_one
    scaled_grad = frame_grad * gain_attn[None]
    sums = jnp.concatenate(
        [
            jnp.sum(scaled_grad, -1),
            jnp.sum(scaled_grad * own_scaled, -1),
            time_grad[0],
            norm_vectors.reshape(-1),
        ]
    )[None]
    sums = sums + swap(sums, "tensor", 1)
    sums = sums + swap(sums, "tensor", 2)
    sums, got_a, raw_got = meeting(sums, got_a, raw_got)
    got_b = swap(after(send_b, got_a), "seq", 1)
    time_both = time_both + got_a[0, rows, :, None].astype(F32)
    left_keep, left_got = halve(added(keep_a, got_a[:, :rows]).astype(BF16), 1)
    plain = sums[0, :local_rows, None] / model_width
    cross = sums[0, local_rows : 2 * local_rows, None] / model_width
    vectors = own_cols(sums[0, 2 * local_rows :].reshape(5, model_width))
    attend_full = ordered(*[after(one_parts, from_next)[i] for i in (0, 2, 1, 3)], 0)
    d_frames = own_cols(attend_full).astype(F32) + inverse_one * (
        scaled_grad - plain - own_scaled * cross
    )
    d_gain_attn = jnp.sum(frame_grad * own_scaled, 0) + vectors[0] * own_cols(scaled_time)[0]
    d_bias_attn = jnp.sum(frame_grad, 0) + vectors[0]
    down_away, down_low = after((down_away, down_low), last_far)
    branch_got, _, branch_far = scatter_near(down_away, down_low)
    block_rows = (
        residual_two + down_own + branch_got[:share].astype(F32) + branch_far.astype(F32)
    ).astype(BF16)
    block_cols = rows_to_cols(
        *[
            lax.dynamic_slice_in_dim(block_rows, (place ^ r) * local_width, local_width, 1)
            for r in range(4)
        ],
        from_next,
    )
    block_out = jnp.concatenate([row_block(block_cols, place ^ b) for b in range(4)], 0)

    time_column = time_normed.T

    normed_pair = (one_own_half, normed_got)
    grad_down = halve_end(down_keep, down_got, 3)
    first, second = halve_end(first_keep, first_got, 3), halve_end(second_keep, second_got, 3)
    units = first.shape[1] // 2
    grad_gate_w = jnp.concatenate([first[:, :units], second[:, :units]], 1)
    grad_up_w = jnp.concatenate([first[:, units:], second[:, units:]], 1)
    raw_pair = (raw, raw_got)
    own_time_rows = lax.dynamic_index_in_dim(
        time_column.reshape(count // 2, 2, -1), column, 1, False
    ).reshape(-1, 1)
    outer = own_time_rows * jnp.concatenate([jnp.zeros((head_cols, 1), F32), time_both], 0).T
    blocks = sum(
        jnp.einsum("dn,fn->df", r, c, preferred_element_type=F32)
        for r, c in zip(normed_pair, raw_pair)
    )
    heads_keep, heads_got = halve(
        (blocks + outer).astype(BF16).reshape(count // 2, rows, 3 * head_cols), 1
    )
    heads_got, got_b = meeting(heads_got, got_b)
    heads_next = added(heads_keep, heads_got).astype(BF16)
    heads_sum = halve_all(heads_next, 2)
    small = jnp.stack(
        [d_gain_attn, d_bias_attn, vectors[3], vectors[4], vectors[1], vectors[2]]
    ).reshape(6, devices, -1).transpose(1, 0, 2)
    small = after(small, heads_next)
    bit = 0
    while small.shape[0] > 1:
        small = added(*halve(small, bit))
        bit += 1
    small = small[0]
    left, right = halve_end(left_keep, left_got, 2), halve_end(keep_b, got_b, 1)
    part, rows = head_cols // count, model_width // count
    grad_c_query = left[:, :head_cols]
    grad_c_key, grad_c_value = left[: rows // 2, head_cols:], left[rows // 2 :, head_cols:]
    grad_c_out = jnp.concatenate([right[:part], right[part : 2 * part]], 1)
    grad_w_out = jnp.concatenate([right[2 * part : 3 * part], right[3 * part :]], 1)
    grad_w_query, grad_w_key, grad_w_value = (
        heads_sum[:, i * head_cols : (i + 1) * head_cols] for i in range(3)
    )
    return (
        block_out,
        d_frames,
        small[0],
        small[1],
        small[2],
        small[3],
        small[4],
        small[5],
        grad_w_query,
        grad_w_key,
        grad_w_value,
        grad_w_out,
        grad_c_query,
        grad_c_key,
        grad_c_value,
        grad_c_out,
        grad_gate_w,
        grad_up_w,
        grad_down,
    )


def solution(mesh):
    return jax.shard_map(
        per_device,
        mesh=mesh,
        in_specs=(
            P("seq", "tensor"),
            P(),
            P(),
            P(),
            P("tensor"),
            P("tensor"),
            P("tensor"),
            P("tensor"),
            P("tensor"),
            P("tensor"),
            P(None, "tensor"),
            P(None, "tensor"),
            P(None, "tensor"),
            P("tensor", None),
            P(None, "tensor"),
            P(None, "tensor"),
            P(None, "tensor"),
            P("tensor", None),
            P(None, "tensor"),
            P(None, "tensor"),
            P("tensor", None),
            P("seq", "tensor"),
        ),
        out_specs=(
            P("seq", "tensor"),
            P("seq", "tensor"),
            P(("tensor", "seq")),
            P(("tensor", "seq")),
            P(("tensor", "seq")),
            P(("tensor", "seq")),
            P(("tensor", "seq")),
            P(("tensor", "seq")),
            P("seq", "tensor"),
            P("seq", "tensor"),
            P("seq", "tensor"),
            P(("tensor", "seq"), None),
            P("seq", "tensor"),
            P("seq", "tensor"),
            P("seq", "tensor"),
            P(("tensor", "seq"), None),
            P("seq", "tensor"),
            P("seq", "tensor"),
            P(("tensor", "seq"), None),
        ),
        check_vma=False,
    )
```

```python
import functools
import math

import jax
import jax.numpy as jnp
from jax import lax
from jax.experimental import pallas as pl
from jax.experimental.pallas import tpu as pltpu
from jax.sharding import PartitionSpec as P

HEAD_SIZE = 64
ROW_MIN = 2048
TILE = 256
BF16 = jnp.bfloat16
F32 = jnp.float32


def meeting(*values):
    return lax.optimization_barrier(values)


def after(value, token):
    return lax.optimization_barrier((value, token))[0]


def swap(value, axis, by):
    return lax.ppermute(value, axis, [(i, i ^ by) for i in range(lax.axis_size(axis))])


def shift(value, axis, by):
    peers = lax.axis_size(axis)
    pairs = [(i, i + by) for i in range(peers) if 0 <= i + by < peers]
    return lax.ppermute(value, axis, pairs)


def tensor_place():
    place = lax.axis_index("tensor")
    return place // 2, place % 2


def ordered(own, far, mate, far_mate, axis):
    side, core = tensor_place()
    near = (jnp.where(core == 0, own, mate), jnp.where(core == 0, mate, own))
    away = (jnp.where(core == 0, far, far_mate), jnp.where(core == 0, far_mate, far))
    low = [jnp.where(side == 0, n, a) for n, a in zip(near, away)]
    high = [jnp.where(side == 0, a, n) for n, a in zip(near, away)]
    return jnp.concatenate(low + high, axis)


def gather_near(own):
    far = swap(own, "tensor", 2)
    return own, swap(own, "tensor", 1), far, swap(far, "tensor", 1)


def gather_staged(own, first, second):
    far = swap(after(own, first), "tensor", 2)
    far, late = after((far, own), second)
    return own, swap(late, "tensor", 1), far, swap(far, "tensor", 1)


def gather(own, axis):
    own, mate, far, far_mate = gather_near(own)
    return ordered(own, far, mate, far_mate, axis)


def scatter_near(away, low):
    got = swap(away, "tensor", 1)
    total = (low.astype(F32) + got[low.shape[0] :].astype(F32)).astype(BF16)
    return got, total, swap(total, "tensor", 2)


def rows_to_cols(own, mate, far, far_mate, later):
    width = own.shape[1]
    got = after(swap(jnp.concatenate([far, far_mate], 1), "tensor", 2), later)
    other = swap(jnp.concatenate([mate, got[:, width:]], 0), "tensor", 1)
    size = own.shape[0]
    return jnp.concatenate([own, other[:size], got[:, :width], other[size:]], 0)


def quarters(value, axis):
    return jnp.split(value, 4, axis)


def own_blocks(near):
    return jnp.concatenate([quarters(value, 1)[r] for r, value in enumerate(near)], 0)


def trade(value, start, done):
    return after(swap(after(value, start), "seq", 1), done)


def halve(blocks, bit):
    count, rows, cols = blocks.shape
    side = (lax.axis_index("seq") >> bit) % 2
    parts = blocks.reshape(count // 2, 2, rows, cols)
    send = lax.dynamic_index_in_dim(parts, 1 - side, 1, False)
    keep = lax.dynamic_index_in_dim(parts, side, 1, False)
    return keep, swap(send, "seq", 1 << bit)


def added(keep, got):
    return keep.astype(F32) + got.astype(F32)


def halve_all(blocks, bit):
    while blocks.shape[0] > 1:
        blocks = added(*halve(blocks.astype(BF16), bit))
        bit += 1
    return blocks[0].astype(F32)


def halve_end(keep, got, bit):
    return halve_all(added(keep, got), bit)


def frame_clip_labels(segment, row_length):
    frame_index = jnp.arange(segment.shape[0], dtype=jnp.int32)
    border = (frame_index % row_length == 0) | (segment != jnp.roll(segment, 1))
    clip_starts = lax.cummax(jnp.where(border, frame_index, 0), axis=0)
    return (clip_starts, (frame_index - clip_starts + 1).astype(jnp.float32))


def tile_ranges(q_labels, key_labels):
    q = q_labels.reshape(-1, TILE)
    k = key_labels.reshape(-1, TILE)
    meets = (k[None, :, 0] <= q[:, None, -1]) & (k[None, :, -1] >= q[:, None, 0])
    index = jnp.arange(k.shape[0], dtype=jnp.int32)[None]
    low = jnp.min(jnp.where(meets, index, k.shape[0]), 1)
    high = jnp.max(jnp.where(meets, index + 1, 0), 1)
    return jnp.stack([low, high], 1).reshape(-1)

def head_rows(g):
    return slice(g * HEAD_SIZE, (g + 1) * HEAD_SIZE)

def fill_natural(dest, refs, which):
    size = refs[0].shape[2]
    for part, ref in enumerate(refs):
        dest[part * size : (part + 1) * size, :] = ref[which].T


def fill_tiles(dest, refs, which):
    pieces = refs[0].shape[2] // TILE
    for part, ref in enumerate(refs):
        for piece in range(pieces):
            dest[part * pieces + piece] = ref[which, :, piece * TILE : (piece + 1) * TILE]


def relative(place, r, size):
    return pl.ds(pl.multiple_of((place ^ r) * size, size), size)


def absorb(state, start, stop, base, q, cols, lab, klab, keys, vals):
    group = q.shape[0] // HEAD_SIZE

    def step(j, state):
        seen = klab[pl.ds(pl.multiple_of(j * TILE, TILE), TILE), :] == lab
        at = pl.ds(pl.multiple_of((j - base) * TILE, TILE), TILE)
        fresh = []
        for g in range(group):
            top, total, acc = state[3 * g : 3 * g + 3]
            s = dot_nn(keys[at, head_rows(g)], q[head_rows(g), cols])
            s = jnp.where(seen, s, -1e30)
            new = jnp.maximum(top, jnp.max(s, 0, keepdims=True))
            fade = jnp.exp(top - new)
            p = jnp.exp(s - new)
            total = total * fade + jnp.sum(p, 0, keepdims=True)
            acc = acc * fade + dot_nn(vals[j - base, head_rows(g), :], p.astype(BF16))
            fresh += [new, total, acc]
        return tuple(fresh)

    return lax.fori_loop(start, stop, step, tuple(state))


def near_body(span, q, kv, tk, tv, qlab, klab, tops, totals, mix, keys, vals):
    rows, size = q.shape
    pieces = size // TILE
    fill_natural(keys, (kv,), 0)
    fill_tiles(vals, (kv,), 1)
    for tile in range(pieces):
        cols = slice(tile * TILE, (tile + 1) * TILE)
        state = []
        for g in range(rows // HEAD_SIZE):
            part = q[head_rows(g), cols].astype(F32)
            top = jnp.sum(part * tk[head_rows(g), :], 0, keepdims=True)
            state += [
                top,
                jnp.ones_like(top),
                jnp.broadcast_to(tv[head_rows(g), :], (HEAD_SIZE, TILE)),
            ]
        start = jnp.maximum(span[2 * tile], pieces)
        stop = jnp.minimum(span[2 * tile + 1], 2 * pieces)
        state = absorb(state, start, stop, pieces, q, cols, qlab[:, cols], klab, keys, vals)
        for g in range(rows // HEAD_SIZE):
            tops[g : g + 1, cols], totals[g : g + 1, cols], mix[head_rows(g), cols] = state[
                3 * g : 3 * g + 3
            ]


def far_body(span, q, kv0, kv2, qlab, klab, w_out, tops, totals, mix,
             out, lse, away, own, low, keys0, keys2, vals0, vals2):
    rows, size = q.shape
    pieces = size // TILE
    for kv, keys, vals in ((kv0, keys0, vals0), (kv2, keys2, vals2)):
        fill_natural(keys, (kv,), 0)
        fill_tiles(vals, (kv,), 1)
    for tile in range(pieces):
        cols = slice(tile * TILE, (tile + 1) * TILE)
        lab = qlab[:, cols]
        state = []
        for g in range(rows // HEAD_SIZE):
            state += [tops[g : g + 1, cols], totals[g : g + 1, cols], mix[head_rows(g), cols]]
        stop = jnp.minimum(span[2 * tile + 1], pieces)
        state = absorb(state, span[2 * tile], stop, 0, q, cols, lab, klab, keys0, vals0)
        start = jnp.maximum(span[2 * tile], 2 * pieces)
        state = absorb(
            state, start, span[2 * tile + 1], 2 * pieces, q, cols, lab, klab, keys2, vals2
        )
        for g in range(rows // HEAD_SIZE):
            top, total, acc = state[3 * g : 3 * g + 3]
            out[head_rows(g), cols] = (acc / total).astype(BF16)
            lse[g : g + 1, cols] = top + jnp.log(total)
    place = span[2 * pieces]
    share = own.shape[0]

    def sent(r):
        return dot_tn(out[:, relative(place, r, share)], w_out[...])

    away[:share, :] = sent(1).astype(BF16)
    away[share:, :] = sent(3).astype(BF16)
    low[...] = sent(2).astype(BF16)
    own[...] = sent(0)


def backward_body(span, q, kv0, kv1, kv2, tk, tv, qlab, klab, w_out, out, lse,
                  g0, g1, g2, g3, dq, to_prev, kept, to_next, times,
                  og, keys, vals, tkeys, ak, av, dtk, dtv):
    rows, size = q.shape
    group = rows // HEAD_SIZE
    pieces = size // TILE
    share = g0.shape[0]
    for r, ref in enumerate((g0, g1, g2, g3)):
        og[:, relative(span[2 * pieces], r, share)] = dot_nt(w_out[...], ref[...]).astype(BF16)
    fill_natural(keys, (kv0, kv1, kv2), 0)
    fill_natural(vals, (kv0, kv1, kv2), 1)
    fill_tiles(tkeys, (kv0, kv1, kv2), 0)
    ak[...] = jnp.zeros_like(ak)
    av[...] = jnp.zeros_like(av)
    for tile in range(pieces):
        cols = slice(tile * TILE, (tile + 1) * TILE)
        lab = qlab[:, cols]
        state, norms, deltas = [], [], []
        for g in range(group):
            hr = head_rows(g)
            qf = q[hr, cols].astype(F32)
            gf = og[hr, cols].astype(F32)
            norm = lse[g : g + 1, cols]
            delta = jnp.sum(gf * out[hr, cols].astype(F32), 0, keepdims=True)
            pt = jnp.exp(jnp.sum(qf * tk[hr, :], 0, keepdims=True) - norm)
            st = pt * (jnp.sum(gf * tv[hr, :], 0, keepdims=True) - delta)
            gk = jnp.sum(qf * st, 1, keepdims=True)
            gv = jnp.sum(gf * pt, 1, keepdims=True)
            if tile == 0:
                dtk[hr, :] = gk
                dtv[hr, :] = gv
            else:
                dtk[hr, :] += gk
                dtv[hr, :] += gv
            state.append(tk[hr, :] * st)
            norms.append(norm)
            deltas.append(delta)

        def step(j, state):
            start = pl.multiple_of(j * TILE, TILE)
            seen = klab[pl.ds(start, TILE), :] == lab
            fresh = []
            for g in range(group):
                hr = head_rows(g)
                s = dot_nn(keys[pl.ds(start, TILE), hr], q[hr, cols])
                p = jnp.exp(jnp.where(seen, s, -1e30) - norms[g])
                m = dot_nn(vals[pl.ds(start, TILE), hr], og[hr, cols])
                ds = (p * (m - deltas[g])).astype(BF16)
                av[j, hr, :] += dot_nt(og[hr, cols], p.astype(BF16))
                ak[j, hr, :] += dot_nt(q[hr, cols], ds)
                fresh.append(state[g] + dot_nn(tkeys[j, hr, :], ds))
            return tuple(fresh)

        state = lax.fori_loop(span[2 * tile], span[2 * tile + 1], step, tuple(state))
        for g in range(group):
            dq[head_rows(g), cols] = state[g]
    for at, column in ((0, dtk), (1, dtv)):
        spread = jnp.broadcast_to(column[...], (rows, 2 * HEAD_SIZE))
        times[at : at + 1, :] = spread.T[:1, :]
    for part, dest in enumerate((to_prev, kept, to_next)):
        for piece in range(pieces):
            at = slice(piece * TILE, (piece + 1) * TILE)
            dest[0, :, at] = ak[part * pieces + piece].astype(dest.dtype)
            dest[1, :, at] = av[part * pieces + piece].astype(dest.dtype)


def attend_near(span, q, kv, tk, tv, qlab, klab):
    cols, size = q.shape
    wide = lambda *dims: jax.ShapeDtypeStruct(dims, F32)
    vmem = pl.BlockSpec(memory_space=pltpu.VMEM)
    return pl.pallas_call(
        near_body,
        in_specs=[pl.BlockSpec(memory_space=pltpu.SMEM)] + [vmem] * 6,
        out_specs=[vmem] * 3,
        out_shape=[wide(cols // HEAD_SIZE, size), wide(cols // HEAD_SIZE, size), wide(cols, size)],
        scratch_shapes=[pltpu.VMEM((size, cols), BF16), pltpu.VMEM((size // TILE, cols, TILE), BF16)],
        name="attend_near", cost_estimate=FREE,
    )(span, q, kv, tk, tv, qlab, klab)


def attend_far(span, q, behind, ahead, qlab, klab, w_out, state):
    cols, size = q.shape
    share, width = size // 4, w_out.shape[1]
    low = lambda *dims: jax.ShapeDtypeStruct(dims, BF16)
    wide = lambda *dims: jax.ShapeDtypeStruct(dims, F32)
    vmem = pl.BlockSpec(memory_space=pltpu.VMEM)
    keys = pltpu.VMEM((size, cols), BF16)
    vals = pltpu.VMEM((size // TILE, cols, TILE), BF16)
    return pl.pallas_call(
        far_body,
        in_specs=[pl.BlockSpec(memory_space=pltpu.SMEM)] + [vmem] * 9,
        out_specs=[vmem] * 5,
        out_shape=[low(cols, size), wide(cols // HEAD_SIZE, size), low(2 * share, width),
                   wide(share, width), low(share, width)],
        scratch_shapes=[keys, keys, vals, vals],
        name="attend_far", cost_estimate=FREE,
    )(span, q, behind, ahead, qlab, klab, w_out, *state)


def attend_back(span, q, kvs, tk, tv, qlab, klab, w_out, out, lse, grads):
    cols, size = q.shape
    tiles = 3 * size // TILE
    low = lambda *dims: jax.ShapeDtypeStruct(dims, BF16)
    wide = lambda *dims: jax.ShapeDtypeStruct(dims, F32)
    vmem = pl.BlockSpec(memory_space=pltpu.VMEM)
    return pl.pallas_call(
        backward_body,
        in_specs=[pl.BlockSpec(memory_space=pltpu.SMEM)] + [vmem] * 15,
        out_specs=[vmem] * 5,
        out_shape=[wide(cols, size), low(2, cols, size), wide(2, cols, size), low(2, cols, size),
                   wide(2, cols)],
        scratch_shapes=[pltpu.VMEM((cols, size), BF16), pltpu.VMEM((3 * size, cols), BF16),
                        pltpu.VMEM((3 * size, cols), BF16), pltpu.VMEM((tiles, cols, TILE), BF16),
                        pltpu.VMEM((tiles, cols, TILE), F32), pltpu.VMEM((tiles, cols, TILE), F32),
                        pltpu.VMEM((cols, 1), F32), pltpu.VMEM((cols, 1), F32)],
        name="attend_back", cost_estimate=FREE,
    )(span, q, *kvs, tk, tv, qlab, klab, w_out, out, lse, *grads)


def tail_body(place, dq, kept, ahead, behind, cosine, sine, wq, wk, wv, raw, away, own, low, flipped):
    part, size = dq.shape
    half = HEAD_SIZE // 2

    def returned(block, base, scale):
        for h in range(part // HEAD_SIZE):
            a = block[h * HEAD_SIZE : h * HEAD_SIZE + half, :]
            b = block[h * HEAD_SIZE + half : (h + 1) * HEAD_SIZE, :]
            at = base + h * HEAD_SIZE
            raw[at : at + half, :] = ((a * cosine[...] + b * sine[...]) * scale).astype(BF16)
            raw[at + half : at + HEAD_SIZE, :] = (
                (b * cosine[...] - a * sine[...]) * scale
            ).astype(BF16)

    def whole(index):
        return kept[index] + ahead[index].astype(F32) + behind[index].astype(F32)

    returned(dq[...], 0, 1.0 / math.sqrt(HEAD_SIZE))
    returned(whole(0), part, 1.0)
    raw[2 * part :, :] = whole(1).astype(BF16)
    flipped[...] = raw[...].T

    def sent(r):
        at = relative(place[0], r, part)
        return sum(
            dot_nt(flipped[:, i * part : (i + 1) * part], weight[at, :])
            for i, weight in enumerate((wq, wk, wv))
        )

    away[:size, :] = sent(1).astype(BF16)
    away[size:, :] = sent(3).astype(BF16)
    low[...] = sent(2).astype(BF16)
    own[...] = sent(0)


def tail(place, dq, kept, ahead, behind, tables, wq, wk, wv):
    part, size = dq.shape
    low = lambda *dims: jax.ShapeDtypeStruct(dims, BF16)
    vmem = pl.BlockSpec(memory_space=pltpu.VMEM)
    return pl.pallas_call(
        tail_body,
        in_specs=[pl.BlockSpec(memory_space=pltpu.SMEM)] + [vmem] * 9,
        out_specs=[vmem] * 4,
        out_shape=[low(3 * part, size), low(2 * size, part), jax.ShapeDtypeStruct((size, part), F32),
                   low(size, part)],
        scratch_shapes=[pltpu.VMEM((size, 3 * part), BF16)],
        name="tail", cost_estimate=FREE,
    )(place, dq, kept, ahead, behind, *tables, wq, wk, wv)


def rotary_tables(frame_positions):
    half_dim = HEAD_SIZE // 2
    frequency = jnp.exp(jnp.arange(half_dim, dtype=jnp.float32) * (-math.log(10000.0) / half_dim))
    angles = frequency[:, None] * frame_positions[None, :]
    return (jnp.cos(angles), jnp.sin(angles))


def rotate(rows, tables, sign=1.0):
    count, size = rows.shape
    halves = rows.reshape(count // HEAD_SIZE, 2, HEAD_SIZE // 2, size)
    cosine, sine = tables[0][None], tables[1][None] * sign
    first = halves[:, 0] * cosine - halves[:, 1] * sine
    second = halves[:, 1] * cosine + halves[:, 0] * sine
    return jnp.stack([first, second], 1).reshape(count, size)


def product(left, right):
    return jnp.dot(left, right, preferred_element_type=jnp.float32)


def inner_rows(left, right):
    return jnp.einsum("nd,nf->df", left, right, preferred_element_type=jnp.float32)


def back_project(gradient, weight):
    return jnp.einsum("nf,df->nd", gradient, weight, preferred_element_type=jnp.float32)


def by_feature(left, right):
    return jnp.einsum("nd,df->fn", left, right, preferred_element_type=jnp.float32)


def columns(weight, start, size):
    return lax.dynamic_slice_in_dim(weight, start, size, 1)


def rows_of(weight, start, size):
    return lax.dynamic_slice_in_dim(weight, start, size, 0)


def normalize(value_rows):
    means = jnp.mean(value_rows, -1, keepdims=True)
    centred = value_rows - means
    inverse = lax.rsqrt(jnp.mean(centred * centred, -1, keepdims=True) + 1e-05)
    return centred * inverse, inverse


def norm_backward(gradient, scaled, inverse, norm_gain):
    scaled_grad = gradient * norm_gain
    plain = jnp.mean(scaled_grad, -1, keepdims=True)
    cross = jnp.mean(scaled_grad * scaled, -1, keepdims=True)
    return inverse * (scaled_grad - plain - scaled * cross)


FREE = pl.CostEstimate(flops=1, transcendentals=0, bytes_accessed=1)


def dot_nn(left, right):
    return lax.dot_general(left, right, (((1,), (0,)), ((), ())), preferred_element_type=F32)


def dot_nt(left, right):
    return lax.dot_general(left, right, (((1,), (1,)), ((), ())), preferred_element_type=F32)


def dot_tn(left, right):
    return lax.dot_general(left, right, (((0,), (0,)), ((), ())), preferred_element_type=F32)


def head_weights(query, key, lanes, which):
    mine = jnp.where(lanes == which, query, jnp.zeros_like(query))
    scores = dot_nt(mine, key) * (1.0 / math.sqrt(HEAD_SIZE))
    weights = jnp.exp(scores - jnp.max(scores, -1, keepdims=True))
    return weights / jnp.sum(weights, -1, keepdims=True)


def pair_cols(refs, p, rows):
    ref = refs[p * 2 * HEAD_SIZE // refs[0].shape[1]]
    start = p * 2 * HEAD_SIZE % refs[0].shape[1]
    return ref[rows, start : start + 2 * HEAD_SIZE]


def cross_forward_body(width_block, place, rows, own, got, far, norms, q0, q1, q2, q3,
                       c0, c1, c2, c3, o0, o1, o2, o3,
                       front, queries, first, second, normed_three,
                       flip_own, flip_away):
    width = rows.shape[1]
    kv = (c0, c1, c2, c3)
    context_rows = c0.shape[0] // 2
    key_rows, value_rows = slice(0, context_rows), slice(context_rows, 2 * context_rows)
    lanes = lax.broadcasted_iota(jnp.int32, (rows.shape[0], 2 * HEAD_SIZE), 1) // HEAD_SIZE
    residual = (
        rows[...].astype(F32) + own[...] + got[...].astype(F32) + far[...].astype(F32)
    )
    first[...] = residual
    scaled, _ = normalize(residual)
    low = (scaled * norms[2:3, :] + norms[3:4, :]).astype(BF16)
    front[:, :width] = low
    part = width // 4
    for b, ref in enumerate((q0, q1, q2, q3)):
        queries[:, b * part : (b + 1) * part] = dot_nn(low, ref[...]).astype(BF16)
    for p in range(width // (2 * HEAD_SIZE)):
        cols = slice(p * 2 * HEAD_SIZE, (p + 1) * 2 * HEAD_SIZE)
        q, k, v = queries[:, cols], pair_cols(kv, p, key_rows), pair_cols(kv, p, value_rows)
        mixed = [dot_nn(head_weights(q, k, lanes, g).astype(BF16), v) for g in (0, 1)]
        front[:, width + cols.start : width + cols.stop] = jnp.where(lanes == 0, mixed[0], mixed[1]).astype(BF16)
    for b, ref in enumerate((o0, o1, o2, o3)):
        residual = residual + dot_nn(front[:, width + b * part : width + (b + 1) * part], ref[...])
    second[...] = residual
    scaled, _ = normalize(residual)
    low = (scaled * norms[4:5, :] + norms[5:6, :]).astype(BF16)
    normed_three[...] = low
    deal_rows(low.T, width_block, place[0], flip_own, flip_away)


def cross_forward(devices, place, rows, own, got, far, norms, query_parts, kv_parts, out_parts):
    size, width = rows.shape
    low = jax.ShapeDtypeStruct(rows.shape, BF16)
    both = jax.ShapeDtypeStruct((size, 2 * width), BF16)
    wide = jax.ShapeDtypeStruct(rows.shape, F32)
    flip = jax.ShapeDtypeStruct((width // 2, size), BF16)
    vmem = pl.BlockSpec(memory_space=pltpu.VMEM)
    block = pl.BlockSpec((size, width), lambda i: (0, 0))
    return pl.pallas_call(
        functools.partial(cross_forward_body, width // devices),
        grid=(1,),
        in_specs=[pl.BlockSpec(memory_space=pltpu.SMEM)] + [block] * 4 + [vmem] * 13,
        out_shape=[both, low, wide, wide, low, flip, flip],
        cost_estimate=FREE, name="cross",
    )(place, rows, own, got, far, norms, *query_parts, *kv_parts, *out_parts)


def deal_rows(rows, size, column, own, away):
    for b in range(rows.shape[0] // (2 * size)):
        at = slice(b * size, (b + 1) * size)
        even = rows[2 * b * size : (2 * b + 1) * size, :]
        odd = rows[(2 * b + 1) * size : (2 * b + 2) * size, :]

        @pl.when(column == 0)
        def _():
            own[at, :] = even
            away[at, :] = odd

        @pl.when(column != 0)
        def _():
            own[at, :] = odd
            away[at, :] = even


def ffn_part(normed, grad, gate_w, up_w, down_w, hidden, hid_own, hid_away, gate_grad, lifted_grad,
             unit_block, column):
    gate = dot_nn(normed, gate_w[...])
    lifted = dot_nn(normed, up_w[...])
    back = dot_nt(grad, down_w[...]).astype(BF16).astype(F32)
    sig = jax.nn.sigmoid(gate)
    swish = gate * sig
    made = (swish * lifted).astype(BF16)
    hidden[...] = made
    deal_rows(made.T, unit_block, column, hid_own, hid_away)
    gg = (back * lifted * sig * (1.0 + gate * (1.0 - sig))).astype(BF16)
    lg = (back * swish).astype(BF16)
    gate_grad[...] = gg
    lifted_grad[...] = lg
    return dot_nt(gg, gate_w[...]) + dot_nt(lg, up_w[...])


def ffn_first_body(unit_block, place, n0, n1, n2, n3, g0, g1, g2, g3, gate_w, up_w, down_w,
                   hidden, hid_own, hid_away, gate_grad, lifted_grad, normed, grad, grad_pair,
                   total):
    share, part = n0.shape[0], g0.shape[2]
    for b, ref in enumerate((n0, n1, n2, n3)):
        normed[b * share : (b + 1) * share, :] = ref[...]
    for c, ref in enumerate((g0, g1, g2, g3)):
        for b in range(4):
            rows, cols = relative(place[1], b, share), relative(place[1], c, part)
            grad[b * share : (b + 1) * share, cols] = ref[0, rows, :]
            grad_pair[b * share : (b + 1) * share, cols] = ref[1, rows, :]
    total[...] = ffn_part(
        normed[...], grad[...], gate_w, up_w, down_w, hidden, hid_own, hid_away, gate_grad,
        lifted_grad, unit_block, place[0],
    )


def ffn_second_body(unit_block, place, normed, grad, total, gate_w, up_w, down_w,
                    hidden, hid_own, hid_away, gate_grad, lifted_grad, away, own, low):
    share = own.shape[0]
    found = total[...] + ffn_part(
        normed[...], grad[...], gate_w, up_w, down_w, hidden, hid_own, hid_away, gate_grad,
        lifted_grad, unit_block, place[0],
    )
    own[...] = found[:share, :]
    low[...] = found[2 * share : 3 * share, :].astype(BF16)
    away[:share, :] = found[share : 2 * share, :].astype(BF16)
    away[share:, :] = found[3 * share :, :].astype(BF16)


def ffn(devices, place, half, inputs, gate_w, up_w, down_w):
    share = inputs[0].shape[0] if half == 0 else inputs[0].shape[0] // 4
    width = inputs[0].shape[1]
    size, units = 4 * share, gate_w.shape[1]
    tile = units // 2
    low = lambda *dims: jax.ShapeDtypeStruct(dims, BF16)
    wide = lambda *dims: jax.ShapeDtypeStruct(dims, F32)
    vmem = pl.BlockSpec(memory_space=pltpu.VMEM)
    cols = pl.BlockSpec((width, tile), lambda i: (0, half))
    rows = pl.BlockSpec((tile, width), lambda i: (half, 0))
    made = [low(size, tile), low(tile // 2, size), low(tile // 2, size), low(size, tile),
            low(size, tile)]
    if half == 0:
        made += [low(size, width), low(size, width), low(size, width), wide(size, width)]
    else:
        made += [low(2 * share, width), wide(share, width), low(share, width)]
    return pl.pallas_call(
        functools.partial(ffn_second_body if half else ffn_first_body, units // devices),
        grid=(1,),
        in_specs=[pl.BlockSpec(memory_space=pltpu.SMEM)] + [vmem] * len(inputs)
        + [cols, cols, rows],
        out_specs=[vmem] * len(made),
        out_shape=made,
        cost_estimate=FREE, name="ffn",
    )(place, *inputs, gate_w, up_w, down_w)


def cross_backward_body(own, got, far, grad, first, second, norms, q0, q1, q2, q3,
                        c0, c1, c2, c3, o0, o1, o2, o3, queries,
                        back_rows, kv_grad, vectors, grad_one, crossed_grad):
    width = grad.shape[1]
    kv = (c0, c1, c2, c3)
    context_rows = c0.shape[0] // 2
    key_rows, value_rows = slice(0, context_rows), slice(context_rows, 2 * context_rows)
    part = width // 4
    lanes = lax.broadcasted_iota(jnp.int32, (grad.shape[0], 2 * HEAD_SIZE), 1) // HEAD_SIZE
    lane_k = lax.broadcasted_iota(jnp.int32, (context_rows, 2 * HEAD_SIZE), 1) // HEAD_SIZE
    scale = 1.0 / math.sqrt(HEAD_SIZE)
    arrived = own[...] + got[...].astype(F32) + far[...].astype(F32)
    scaled, inverse = normalize(second[...])
    vectors[0:1, :] = jnp.sum(arrived * scaled, 0, keepdims=True)
    vectors[1:2, :] = jnp.sum(arrived, 0, keepdims=True)
    two = grad[...].astype(F32) + norm_backward(arrived, scaled, inverse, norms[4:5, :])
    low = two.astype(BF16)
    back_rows[:, :width] = low
    for b, ref in enumerate((o0, o1, o2, o3)):
        crossed_grad[:, b * part : (b + 1) * part] = dot_nt(low, ref[...]).astype(BF16)
    for p in range(width // (2 * HEAD_SIZE)):
        cols = slice(p * 2 * HEAD_SIZE, (p + 1) * 2 * HEAD_SIZE)
        q, k, v = queries[:, cols], pair_cols(kv, p, key_rows), pair_cols(kv, p, value_rows)
        g_rows = crossed_grad[:, cols]
        found = []
        for g in (0, 1):
            probs = head_weights(q, k, lanes, g)
            change = dot_nt(jnp.where(lanes == g, g_rows, jnp.zeros_like(g_rows)), v)
            delta = jnp.sum(change * probs, -1, keepdims=True)
            ds = (probs * (change - delta)).astype(BF16)
            found.append((dot_nn(ds, k), dot_tn(ds, q), dot_tn(probs.astype(BF16), g_rows)))
        back_rows[:, width + cols.start : width + cols.stop] = (
            jnp.where(lanes == 0, found[0][0], found[1][0]) * scale
        ).astype(BF16)
        kv_grad[:context_rows, cols] = (
            jnp.where(lane_k == 0, found[0][1], found[1][1]) * scale
        ).astype(BF16)
        kv_grad[context_rows:, cols] = jnp.where(lane_k == 0, found[0][2], found[1][2]).astype(
            BF16
        )
    back = jnp.zeros(grad.shape, F32)
    for b, ref in enumerate((q0, q1, q2, q3)):
        back = back + dot_nt(back_rows[:, width + b * part : width + (b + 1) * part], ref[...])
    scaled, inverse = normalize(first[...])
    vectors[2:3, :] = jnp.sum(back * scaled, 0, keepdims=True)
    vectors[3:4, :] = jnp.sum(back, 0, keepdims=True)
    grad_one[...] = (two + norm_backward(back, scaled, inverse, norms[2:3, :])).astype(BF16)


def cross_backward(own, got, far, grad, first, second, norms, query_parts, kv_parts, out_parts,
                   queries):
    rows, width = own.shape
    low = lambda r: jax.ShapeDtypeStruct((r, width), BF16)
    block = pl.BlockSpec((rows, width), lambda i: (0, 0))
    return pl.pallas_call(
        cross_backward_body,
        grid=(1,),
        out_shape=[jax.ShapeDtypeStruct((rows, 2 * width), BF16), low(kv_parts[0].shape[0]),
                   jax.ShapeDtypeStruct((4, width), F32), low(rows)],
        in_specs=[block] * 6 + [pl.BlockSpec(memory_space=pltpu.VMEM)] * 14,
        scratch_shapes=[pltpu.VMEM((rows, width), BF16)],
        cost_estimate=FREE, name="cross_back",
    )(own, got, far, grad, first, second, norms, *query_parts, *kv_parts, *out_parts, queries)


def meet_rows_body(size, side, own_a, pair_a, own_b, pair_b, right, right_pair, keep, send):
    half = keep.shape[0] // 2
    for b, (own, pair) in enumerate(((own_a, pair_a), (own_b, pair_b))):
        made = (dot_nn(own[...], right[...]) + dot_nn(pair[...], right_pair[...])).astype(BF16)
        at = pl.ds(b * half, half)
        deal_rows(made, size, side[0], keep.at[at], send.at[at])


def meet_rows(size, side, lefts, rights):
    count, frames = lefts[0].shape
    width = rights[0].shape[1]
    tile = width // 3
    left = pl.BlockSpec((count, frames), lambda i: (0, 0))
    right = pl.BlockSpec((frames, tile), lambda i: (0, i))
    return pl.pallas_call(
        functools.partial(meet_rows_body, size),
        grid=(3,),
        in_specs=[pl.BlockSpec(memory_space=pltpu.SMEM)] + [left] * 4 + [right] * 2,
        out_specs=[pl.BlockSpec((count, tile), lambda i: (0, i))] * 2,
        out_shape=[jax.ShapeDtypeStruct((count, width), BF16)] * 2,
        name="meet_rows", cost_estimate=FREE,
    )(side, *lefts, *rights)


def meet_cols_body(size, side, p0, p1, p2, p3, *refs):
    own, pair = (jnp.concatenate([p[i] for p in (p0, p1, p2, p3)], 1) for i in (0, 1))
    *rights, keep, send = refs
    width = rights[0].shape[1]
    for at in range(len(rights) // 2):
        made = dot_nn(own, rights[2 * at][...]) + dot_nn(pair, rights[2 * at + 1][...])
        cols = pl.ds(at * width, width)
        deal_rows(made.astype(BF16), size, side[0], keep.at[:, cols], send.at[:, cols])


def meet_cols(size, side, near, rights):
    width = rights[0].shape[1] * (len(rights) // 2)
    half = jax.ShapeDtypeStruct((near[0].shape[1] // 2, width), BF16)
    vmem = pl.BlockSpec(memory_space=pltpu.VMEM)
    return pl.pallas_call(
        functools.partial(meet_cols_body, size),
        in_specs=[pl.BlockSpec(memory_space=pltpu.SMEM)] + [vmem] * (4 + len(rights)),
        out_shape=[half] * 2,
        name="meet_cols", cost_estimate=FREE,
    )(side, *near, *rights)


def down_body(first, second, down_w, away, own, low):
    share, units = own.shape[0], first.shape[1]

    def sent(r):
        at = slice(r * share, (r + 1) * share)
        return dot_nn(first[at, :], down_w[:units, :]) + dot_nn(second[at, :], down_w[units:, :])

    away[:share, :] = sent(1).astype(BF16)
    away[share:, :] = sent(3).astype(BF16)
    low[...] = sent(2).astype(BF16)
    own[...] = sent(0)


def down_parts(first, second, down_w):
    share, width = first.shape[0] // 4, down_w.shape[1]
    low = lambda *dims: jax.ShapeDtypeStruct(dims, BF16)
    return pl.pallas_call(
        down_body,
        out_shape=[low(2 * share, width), jax.ShapeDtypeStruct((share, width), F32),
                   low(share, width)],
        name="down", cost_estimate=FREE,
    )(first, second, down_w)


def bundle_body(devices, place, f02, f13, b02, b13, a0, a1, a2, a3, attended,
                context, kv, times, keep_a, send_a, keep_b, send_b):
    width = a0.shape[1]
    part, share = width // 4, a0.shape[0]

    def near(even, odd):
        return even[0], odd[0], even[1], odd[1]

    own = lambda rows: jnp.concatenate(
        [row[:, width + r * part : width + (r + 1) * part] for r, row in enumerate(rows)], 0
    )
    full = lambda rows: jnp.concatenate([row[:, :width] for row in rows], 0)
    fronts, backs = near(f02, f13), near(b02, b13)
    rows = width // devices
    small = part // devices
    half = width // 2

    def put(block, base, left, out):
        size = block.shape[0] // devices
        cols = slice(left, left + block.shape[1])
        low = block.astype(BF16)
        for d in range(0, devices, 2):
            at = slice(base, base + size)
            even, odd = low[d * size : (d + 1) * size, :], low[(d + 1) * size : (d + 2) * size, :]

            @pl.when(place[0] == 0)
            def _():
                out[0][d // 2, at, cols] = even
                out[1][d // 2, at, cols] = odd

            @pl.when(place[0] != 0)
            def _():
                out[0][d // 2, at, cols] = odd
                out[1][d // 2, at, cols] = even

    send_a[:, rows:, :] = jnp.zeros((devices // 2, send_a.shape[1] - rows, half), BF16)
    for at in (0, 1):
        send_a[0, rows : rows + 1, at * part : (at + 1) * part] = times[at : at + 1, :].astype(BF16)
    put(dot_tn(full(fronts), own(backs)), 0, 0, (keep_a, send_a))
    count = context.shape[0]
    put(dot_tn(context[...], kv[:count, :]), 0, part, (keep_a, send_a))
    put(dot_tn(context[...], kv[count:, :]), rows // 2, part, (keep_a, send_a))
    grads = dot_tn(own(fronts), full(backs))
    put(grads[:, :half], 0, 0, (keep_b, send_b))
    put(grads[:, half:], small, 0, (keep_b, send_b))
    grads = sum(
        dot_nn(attended[:, relative(place[1], r, share)], ref[...])
        for r, ref in enumerate((a0, a1, a2, a3))
    )
    put(grads[:, :half], 2 * small, 0, (keep_b, send_b))
    put(grads[:, half:], 3 * small, 0, (keep_b, send_b))


def bundle_grads(devices, place, fronts, backs, ones, attended, context, kv, times):
    width = ones[0].shape[1]
    vmem = pl.BlockSpec(memory_space=pltpu.VMEM)
    return pl.pallas_call(
        functools.partial(bundle_body, devices),
        in_specs=[pl.BlockSpec(memory_space=pltpu.SMEM)] + [vmem] * 12,
        out_specs=[vmem] * 4,
        out_shape=[
            jax.ShapeDtypeStruct((devices // 2, width // devices + more, width // 2), BF16)
            for more in (0, 16, 0, 0)
        ],
        name="bundle", cost_estimate=FREE,
    )(place, *fronts, *backs, *ones, attended, context, kv, times)


def front_body(width_block, place, x0, x1, x2, x3, g0, g1, g2, g3, cosine, sine, wq, wk, wv,
               time_row, context, ck, cv,
               queries, pair, rows, low, nrm_own, nrm_away, norms, means, inverses,
               time_scaled, time_low, time_keys, time_values, kv, wide):
    size, part = x0.shape
    for r, (x, g) in enumerate(((x0, g0), (x1, g1), (x2, g2), (x3, g3))):
        start = pl.multiple_of((place[0] ^ r) * part, 128)
        wide[:, pl.ds(start, part)] = x[...]
        norms[:, pl.ds(start, part)] = g[...]
    share = size // 4
    rows[...] = wide[pl.ds(pl.multiple_of(place[0] * share, share), share), :]
    values = wide[...].astype(F32)
    mean = jnp.mean(values, -1, keepdims=True)
    centred = values - mean
    inverse = lax.rsqrt(jnp.mean(centred * centred, -1, keepdims=True) + 1e-05)
    means[...] = mean
    inverses[...] = inverse
    normed = (centred * inverse * norms[0:1, :] + norms[1:2, :]).astype(BF16)
    low[...] = normed
    half = HEAD_SIZE // 2

    def turned(weight):
        return dot_nn(normed, weight[...]).T

    def rotated(block, dest, scale):
        for h in range(part // HEAD_SIZE):
            a = block[h * HEAD_SIZE : h * HEAD_SIZE + half, :]
            b = block[h * HEAD_SIZE + half : (h + 1) * HEAD_SIZE, :]
            dest[h * HEAD_SIZE : h * HEAD_SIZE + half, :] = (
                (a * cosine[...] - b * sine[...]) * scale
            ).astype(BF16)
            dest[h * HEAD_SIZE + half : (h + 1) * HEAD_SIZE, :] = (
                (b * cosine[...] + a * sine[...]) * scale
            ).astype(BF16)

    scaled, _ = normalize(jnp.broadcast_to(time_row[...].astype(F32), (8, 4 * part)))
    time_scaled[...] = scaled[:1, :]
    made = (scaled * norms[0:1, :] + norms[1:2, :]).astype(BF16)
    time_low[...] = made[:1, :].astype(F32)
    time_keys[...] = dot_nn(made, wk[...]).astype(BF16).astype(F32).T[:, :1]
    time_values[...] = dot_nn(made, wv[...]).astype(BF16).astype(F32).T[:, :1]
    count = context.shape[0]
    kv[:count, :] = dot_nn(context[...], ck[...]).astype(BF16)
    kv[count:, :] = dot_nn(context[...], cv[...]).astype(BF16)
    rotated(turned(wk), pair.at[0], 1.0)
    pair[1] = turned(wv).astype(BF16)
    rotated(turned(wq), queries, 1.0 / math.sqrt(HEAD_SIZE))
    deal_rows(normed.T, width_block, place[1], nrm_own, nrm_away)


def front(devices, place, parts, norm_parts, tables, wq, wk, wv, time_row, context, ck, cv):
    size, part = parts[0].shape
    width = 4 * part
    low = lambda *s: jax.ShapeDtypeStruct(s, BF16)
    wide = lambda *s: jax.ShapeDtypeStruct(s, F32)
    vmem = pl.BlockSpec(memory_space=pltpu.VMEM)
    return pl.pallas_call(
        functools.partial(front_body, width // devices),
        in_specs=[pl.BlockSpec(memory_space=pltpu.SMEM)] + [vmem] * 17,
        out_specs=[vmem] * 14,
        out_shape=[low(part, size), low(2, part, size), low(size // 4, width), low(size, width),
                   low(width // 2, size), low(width // 2, size), wide(6, width),
                   wide(size, 1), wide(size, 1), wide(1, width), wide(1, width), wide(part, 1),
                   wide(part, 1), low(2 * context.shape[0], part)],
        scratch_shapes=[pltpu.VMEM((size, width), BF16)],
        cost_estimate=FREE, name="front",
    )(place, *parts, *norm_parts, *tables, wq, wk, wv, time_row, context, ck, cv)


def per_device(
    frames,
    segment,
    time_token,
    context,
    gain_attn,
    bias_attn,
    gain_cross,
    bias_cross,
    gain_ffn,
    bias_ffn,
    w_query,
    w_key,
    w_value,
    w_out,
    c_query,
    c_key,
    c_value,
    c_out,
    w_gate,
    w_up,
    w_down,
    out_grad,
):
    local_rows = frames.shape[0]
    local_width = frames.shape[1]
    model_width = w_query.shape[0]
    head_cols = w_query.shape[1]
    heads = head_cols // HEAD_SIZE
    number_of_frames = lax.axis_size("seq") * local_rows
    row_length = min(max(ROW_MIN, 64 * lax.axis_size("seq")), number_of_frames)
    first_frame = lax.axis_index("seq") * local_rows
    own_start = lax.axis_index("tensor") * local_width

    def own_cols(value):
        return lax.dynamic_slice_in_dim(value, own_start, local_width, value.ndim - 1)

    place = lax.axis_index("tensor")
    share = local_rows // 4

    def row_block(value, index):
        return rows_of(value, index * share, share)

    column = lax.axis_index("seq") % 2
    frame_parts_near = gather_near(frames)
    norm_parts = gather_near(
        jnp.stack([gain_attn, bias_attn, gain_cross, bias_cross, gain_ffn, bias_ffn])
    )
    clip_starts, frame_positions = frame_clip_labels(segment, row_length)
    own_labels = lax.dynamic_slice_in_dim(clip_starts, first_frame, local_rows)
    own_positions = lax.dynamic_slice_in_dim(frame_positions, first_frame, local_rows)
    blanks = jnp.full((local_rows,), -1, jnp.int32)
    key_labels = lax.dynamic_slice_in_dim(
        jnp.concatenate([blanks, clip_starts, blanks]), first_frame, 3 * local_rows
    )
    spans = jnp.concatenate(
        [tile_ranges(own_labels, key_labels), place.astype(jnp.int32).reshape(1)]
    )
    places = jnp.stack([column, place]).astype(jnp.int32)
    label_row, label_column = own_labels[None, :], key_labels[:, None]
    row_index = first_frame // row_length
    time_row = lax.dynamic_slice_in_dim(time_token, row_index, 1, 0)
    row_context = lax.dynamic_slice_in_dim(context, row_index, 1, 0)[0]
    context_rows = row_context.shape[0]
    tables = rotary_tables(own_positions)
    score_scale = 1.0 / math.sqrt(HEAD_SIZE)
    all_heads = model_width // HEAD_SIZE

    (
        queries, both, frame_rows, frame_normed, one_own_half, one_away_half, norms, means_one,
        inverse_one, scaled_time, time_normed, time_keys, time_values, context_kv,
    ) = front(
        lax.axis_size("seq"), jnp.flip(places), frame_parts_near, norm_parts, tables, w_query,
        w_key, w_value, time_row, row_context, c_key, c_value,
    )
    both, out_pair = meeting(both, swap(after(out_grad, frame_parts_near[2]), "seq", 1))
    grad_both = jnp.stack([out_grad, out_pair])
    behind, ahead = shift(both, "seq", 1), shift(both, "seq", -1)
    query_far = swap(after(c_query, frame_parts_near[3]), "tensor", 2)
    out_far = swap(after(c_out, frame_parts_near[3]), "tensor", 2)
    state = attend_near(spans, queries, both, time_keys, time_values, label_row, label_column)
    behind, ahead, query_far, out_far, *state = meeting(
        behind, ahead, query_far, out_far, *state
    )
    query_own, out_own, context_late = after((c_query, c_out, context_kv), behind)
    weights_near = [
        swap(value, "tensor", 1) for value in (query_own, query_far, out_own, out_far)
    ]
    kv_far = swap(context_late, "tensor", 2)
    attended, log_totals, one_away, one_own, one_low = attend_far(
        spans, queries, behind, ahead, label_row, label_column, w_out, state
    )
    one_away, one_low, kv_far, *weights_near = meeting(one_away, one_low, kv_far, *weights_near)
    kv_both = jnp.concatenate([context_kv, kv_far], 0)
    kv_other = swap(kv_both, "tensor", 1)
    kv_rows = context_kv.shape[0]
    kv_parts = (context_kv, kv_other[:kv_rows], kv_far, kv_other[kv_rows:])
    query_parts = (c_query, weights_near[0], query_far, weights_near[1])
    out_parts = (c_out, weights_near[2], out_far, weights_near[3])
    one_got, _, one_far = scatter_near(one_away, one_low)
    (
        front_rows, cross_queries, residual_one, residual_two, normed_share, flip_own, flip_away,
    ) = cross_forward(
        lax.axis_size("seq"), places, frame_rows, one_own, one_got, one_far, norms,
        query_parts, kv_parts, out_parts,
    )
    grad_far = swap(after(grad_both, one_far), "tensor", 2)
    normed_share, normed_got, grad_far = meeting(
        normed_share, swap(after(one_away_half, one_low), "seq", 1), grad_far
    )
    grad_late, grad_far_late = after((grad_both, grad_far), normed_share)
    grad_mate, grad_far_mate = swap(grad_late, "tensor", 1), swap(grad_far_late, "tensor", 1)
    grad_parts = (grad_both, grad_mate, grad_far, grad_far_mate)
    three_parts = gather_near(normed_share)
    flip_got = swap(after(flip_away, normed_share), "seq", 1)
    front_far = swap(after(front_rows, three_parts[3]), "tensor", 2)
    devices = lax.axis_size("seq")
    (
        hidden_a, hidden_own_a, hidden_away_a, gate_a, lifted_a, normed_three, grad_near, grad_pair,
        ffn_total,
    ) = ffn(devices, places, 0, (*three_parts, *grad_parts), w_gate, w_up, w_down)
    ffn_total, flip_got = meeting(ffn_total, flip_got)
    flip_both = jnp.stack([flip_own, flip_got])
    flip_far = swap(flip_both, "tensor", 2)
    hidden_got_a, gate_got_a = swap(hidden_away_a, "seq", 1), swap(gate_a, "seq", 1)
    hidden_b, hidden_own_b, hidden_away_b, gate_b, lifted_b, three_away, three_own, three_low = ffn(
        devices, places, 1, (normed_three, grad_near, ffn_total), w_gate, w_up, w_down
    )
    three_away, three_low, flip_far, front_far, hidden_got_a = meeting(
        three_away, three_low, flip_far, front_far, hidden_got_a
    )
    three_got, _, three_far = scatter_near(three_away, three_low)
    hidden_got_b = swap(after(hidden_away_b, three_low), "seq", 1)
    lifted_got_a = swap(after(lifted_a, three_low), "seq", 1)
    flip_late, flip_far_late, gate_late = after((flip_both, flip_far, gate_b), three_far)
    flip_mate, flip_far_mate = swap(flip_late, "tensor", 1), swap(flip_far_late, "tensor", 1)
    gate_got_b = swap(gate_late, "seq", 1)
    front_both = jnp.stack([front_rows, front_far])
    back_rows, kv_grad, norm_vectors, grad_one = cross_backward(
        three_own, three_got, three_far, grad_near, residual_one, residual_two, norms,
        query_parts, kv_parts, out_parts, cross_queries,
    )
    grad_one, gate_got_a, hidden_got_b, flip_mate, flip_far_mate = meeting(
        grad_one, gate_got_a, hidden_got_b, flip_mate, flip_far_mate
    )
    count = lax.axis_size("seq")
    level_side = ((lax.axis_index("seq") >> 1) % 2).astype(jnp.int32).reshape(1)
    rows = model_width // count

    def traded(dealt):
        keep, send = [value.reshape(count // 4, rows, -1) for value in dealt]
        return keep, swap(send, "seq", 2)

    down_keep, down_got = traded(
        meet_rows(
            rows, level_side, (hidden_own_a, hidden_got_a, hidden_own_b, hidden_got_b),
            (grad_near, grad_pair),
        )
    )
    context_parts = quarters(kv_grad, 1)
    context_got = swap(jnp.concatenate([context_parts[1], context_parts[3]], 0), "tensor", 1)
    one_far_rows, down_keep = meeting(swap(grad_one, "tensor", 2), down_keep)
    one_parts = (
        grad_one, swap(grad_one, "tensor", 1), one_far_rows, swap(one_far_rows, "tensor", 1)
    )
    *one_parts, front_other, context_got, lifted_got_a = meeting(
        *one_parts, swap(after(front_both, grad_one), "tensor", 1), context_got, lifted_got_a
    )
    context_low = (
        context_parts[2].astype(F32) + context_got[context_parts[2].shape[0] :].astype(F32)
    ).astype(BF16)
    context_far = swap(context_low, "tensor", 2)
    back_far = swap(after(back_rows, one_parts[3]), "tensor", 2)
    lifted_got_b = swap(after(lifted_b, grad_one), "seq", 1)
    query_grad, to_prev, kept, to_next, time_grads = attend_back(
        spans, queries, (behind, both, ahead), time_keys, time_values, label_row, label_column,
        w_out, attended, log_totals, one_parts,
    )
    to_prev, to_next, back_far, gate_got_b, lifted_got_b, down_got, context_far = meeting(
        to_prev, to_next, back_far, gate_got_b, lifted_got_b, down_got, context_far
    )
    from_next, from_prev = shift(to_prev, "seq", -1), shift(to_next, "seq", 1)
    down_keep, down_got = halve(added(down_keep, down_got).astype(BF16), 2)
    flip_near = (flip_both, flip_mate, flip_far, flip_far_mate)
    both_keep, both_got = traded(
        meet_cols(
            rows, level_side, flip_near,
            after(
                (gate_a, gate_got_a, lifted_a, lifted_got_a, gate_b, gate_got_b, lifted_b,
                 lifted_got_b),
                to_prev,
            ),
        )
    )
    back_both = jnp.stack([back_rows, back_far])
    back_other = swap(back_both, "tensor", 1)
    context_own = (
        context_parts[0].astype(F32)
        + context_got[: context_far.shape[0]].astype(F32)
        + context_far.astype(F32)
    )
    keep_a, send_a, keep_b, send_b = bundle_grads(
        count, places, (front_both, front_other), (back_both, back_other), one_parts, attended,
        row_context,
        context_own.astype(BF16), time_grads,
    )
    from_next, from_prev, down_got, send_a, send_b = meeting(
        from_next, from_prev, down_got, send_a, send_b
    )
    got_a = swap(send_a, "seq", 1)
    raw, last_away, last_own, last_low = tail(
        places[1:], query_grad, kept, from_next, from_prev, tables, w_query, w_key, w_value
    )
    last_got = swap(last_away, "tensor", 1)
    raw_got = swap(raw, "seq", 1)
    last_sum = (
        last_low.astype(F32) + last_got[local_rows:].astype(F32)
    ).astype(BF16)
    last_far, both_got = meeting(swap(last_sum, "tensor", 2), both_got)
    both_keep, both_got = halve(added(both_keep, both_got).astype(BF16), 2)
    frame_grad = last_own + last_got[:local_rows].astype(F32) + last_far.astype(F32)

    time_late, means_late, inverse_late, vectors_late = after(
        (time_grads, means_one, inverse_one, norm_vectors), last_far
    )
    time_grad = sum(
        jnp.einsum("of,df->od", time_late[i : i + 1].astype(BF16), w, preferred_element_type=F32)
        for i, w in enumerate((w_key, w_value))
    )
    own_scaled = (frames.astype(F32) - means_late) * inverse_late
    scaled_grad = frame_grad * gain_attn[None]
    sums = jnp.concatenate(
        [
            jnp.sum(scaled_grad, -1),
            jnp.sum(scaled_grad * own_scaled, -1),
            time_grad[0],
            vectors_late.reshape(-1),
        ]
    )[None]
    sums = sums + swap(sums, "tensor", 1)
    sums = sums + swap(sums, "tensor", 2)
    sums, got_a, raw_got = meeting(sums, got_a, raw_got)
    got_b = swap(after(send_b, got_a), "seq", 1)
    time_both = time_grads.reshape(1, -1) + got_a[0, rows : rows + 1].astype(F32)
    left_keep, left_got = halve(added(keep_a, got_a[:, :rows]).astype(BF16), 1)
    plain = sums[0, :local_rows, None] / model_width
    cross = sums[0, local_rows : 2 * local_rows, None] / model_width
    vectors = own_cols(sums[0, 2 * local_rows :].reshape(5, model_width))
    attend_full = ordered(*[after(one_parts, from_next)[i] for i in (0, 2, 1, 3)], 0)
    d_frames = own_cols(attend_full).astype(F32) + inverse_late * (
        scaled_grad - plain - own_scaled * cross
    )
    d_gain_attn = jnp.sum(frame_grad * own_scaled, 0) + vectors[0] * own_cols(scaled_time)[0]
    d_bias_attn = jnp.sum(frame_grad, 0) + vectors[0]
    down_away, down_own, down_low = down_parts(after(hidden_a, last_far), hidden_b, w_down)
    branch_got, _, branch_far = scatter_near(down_away, down_low)
    block_rows = (
        residual_two + down_own + branch_got[:share].astype(F32) + branch_far.astype(F32)
    ).astype(BF16)
    block_cols = rows_to_cols(
        *[
            lax.dynamic_slice_in_dim(block_rows, (place ^ r) * local_width, local_width, 1)
            for r in range(4)
        ],
        from_next,
    )
    block_out = jnp.concatenate([row_block(block_cols, place ^ b) for b in range(4)], 0)

    time_column = time_normed.T

    normed_pair = (one_own_half, normed_got)
    grad_down = halve_end(down_keep, down_got, 3)
    gate_up = halve_end(both_keep, both_got, 3)
    units = gate_up.shape[1] // 4
    gate_a, up_a, gate_b, up_b = (gate_up[:, i * units : (i + 1) * units] for i in range(4))
    grad_gate_w = jnp.concatenate([gate_a, gate_b], 1)
    grad_up_w = jnp.concatenate([up_a, up_b], 1)
    raw_pair = (raw, raw_got)
    own_time_rows = lax.dynamic_index_in_dim(
        time_column.reshape(count // 2, 2, -1), column, 1, False
    ).reshape(-1, 1)
    outer = own_time_rows * jnp.concatenate([jnp.zeros((1, head_cols), F32), time_both], 1)
    blocks = sum(
        jnp.einsum("dn,fn->df", r, c, preferred_element_type=F32)
        for r, c in zip(normed_pair, raw_pair)
    )
    heads_keep, heads_got = halve(
        (blocks + outer).astype(BF16).reshape(count // 2, rows, 3 * head_cols), 1
    )
    heads_got, got_b = meeting(heads_got, got_b)
    heads_next = added(heads_keep, heads_got).astype(BF16)
    heads_sum = halve_all(heads_next, 2)
    last_next = added(*halve(added(keep_b, got_b).astype(BF16), 1))
    small = jnp.stack(
        [d_gain_attn, d_bias_attn, vectors[3], vectors[4], vectors[1], vectors[2]]
    ).reshape(6, devices, -1).transpose(1, 0, 2)
    small = after(small, last_next)
    bit = 0
    while small.shape[0] > 1:
        small = added(*halve(small, bit))
        bit += 1
    small = small[0]
    left, right = halve_end(left_keep, left_got, 2), halve_all(last_next, 2)
    part, rows = head_cols // count, model_width // count
    grad_c_query = left[:, :head_cols]
    grad_c_key, grad_c_value = left[: rows // 2, head_cols:], left[rows // 2 :, head_cols:]
    grad_c_out = jnp.concatenate([right[:part], right[part : 2 * part]], 1)
    grad_w_out = jnp.concatenate([right[2 * part : 3 * part], right[3 * part :]], 1)
    grad_w_query, grad_w_key, grad_w_value = (
        heads_sum[:, i * head_cols : (i + 1) * head_cols] for i in range(3)
    )
    return (
        block_out,
        d_frames,
        small[0],
        small[1],
        small[2],
        small[3],
        small[4],
        small[5],
        grad_w_query,
        grad_w_key,
        grad_w_value,
        grad_w_out,
        grad_c_query,
        grad_c_key,
        grad_c_value,
        grad_c_out,
        grad_gate_w,
        grad_up_w,
        grad_down,
    )


def solution(mesh):
    return jax.shard_map(
        per_device,
        mesh=mesh,
        in_specs=(
            P("seq", "tensor"),
            P(),
            P(),
            P(),
            P("tensor"),
            P("tensor"),
            P("tensor"),
            P("tensor"),
            P("tensor"),
            P("tensor"),
            P(None, "tensor"),
            P(None, "tensor"),
            P(None, "tensor"),
            P("tensor", None),
            P(None, "tensor"),
            P(None, "tensor"),
            P(None, "tensor"),
            P("tensor", None),
            P(None, "tensor"),
            P(None, "tensor"),
            P("tensor", None),
            P("seq", "tensor"),
        ),
        out_specs=(
            P("seq", "tensor"),
            P("seq", "tensor"),
            P(("tensor", "seq")),
            P(("tensor", "seq")),
            P(("tensor", "seq")),
            P(("tensor", "seq")),
            P(("tensor", "seq")),
            P(("tensor", "seq")),
            P("seq", "tensor"),
            P("seq", "tensor"),
            P("seq", "tensor"),
            P(("tensor", "seq"), None),
            P("seq", "tensor"),
            P("seq", "tensor"),
            P("seq", "tensor"),
            P(("tensor", "seq"), None),
            P("seq", "tensor"),
            P("seq", "tensor"),
            P(("tensor", "seq"), None),
        ),
        check_vma=False,
    )
```

```python
import functools
import math

import jax
import jax.numpy as jnp
from jax import lax
from jax.experimental import pallas as pl
from jax.experimental.pallas import tpu as pltpu
from jax.sharding import PartitionSpec as P

HEAD_SIZE = 64
ROW_MIN = 2048
TILE = 256
BF16 = jnp.bfloat16
F32 = jnp.float32


def meeting(*values):
    return lax.optimization_barrier(values)


def after(value, token):
    return lax.optimization_barrier((value, token))[0]


def swap(value, axis, by):
    return lax.ppermute(value, axis, [(i, i ^ by) for i in range(lax.axis_size(axis))])


def shift(value, axis, by):
    peers = lax.axis_size(axis)
    pairs = [(i, i + by) for i in range(peers) if 0 <= i + by < peers]
    return lax.ppermute(value, axis, pairs)


def tensor_place():
    place = lax.axis_index("tensor")
    return place // 2, place % 2


def ordered(own, far, mate, far_mate, axis):
    side, core = tensor_place()
    near = (jnp.where(core == 0, own, mate), jnp.where(core == 0, mate, own))
    away = (jnp.where(core == 0, far, far_mate), jnp.where(core == 0, far_mate, far))
    low = [jnp.where(side == 0, n, a) for n, a in zip(near, away)]
    high = [jnp.where(side == 0, a, n) for n, a in zip(near, away)]
    return jnp.concatenate(low + high, axis)


def gather_near(own):
    far = swap(own, "tensor", 2)
    return own, swap(own, "tensor", 1), far, swap(far, "tensor", 1)


def gather_staged(own, first, second):
    far = swap(after(own, first), "tensor", 2)
    far, late = after((far, own), second)
    return own, swap(late, "tensor", 1), far, swap(far, "tensor", 1)


def gather(own, axis):
    own, mate, far, far_mate = gather_near(own)
    return ordered(own, far, mate, far_mate, axis)


def scatter_near(away, low):
    got = swap(away, "tensor", 1)
    total = (low.astype(F32) + got[low.shape[0] :].astype(F32)).astype(BF16)
    return got, total, swap(total, "tensor", 2)


def rows_to_cols(own, mate, far, far_mate, later):
    width = own.shape[1]
    got = after(swap(jnp.concatenate([far, far_mate], 1), "tensor", 2), later)
    other = swap(jnp.concatenate([mate, got[:, width:]], 0), "tensor", 1)
    size = own.shape[0]
    return jnp.concatenate([own, other[:size], got[:, :width], other[size:]], 0)


def quarters(value, axis):
    return jnp.split(value, 4, axis)


def own_blocks(near):
    return jnp.concatenate([quarters(value, 1)[r] for r, value in enumerate(near)], 0)


def trade(value, start, done):
    return after(swap(after(value, start), "seq", 1), done)


def halve(blocks, bit):
    count, rows, cols = blocks.shape
    side = (lax.axis_index("seq") >> bit) % 2
    parts = blocks.reshape(count // 2, 2, rows, cols)
    send = lax.dynamic_index_in_dim(parts, 1 - side, 1, False)
    keep = lax.dynamic_index_in_dim(parts, side, 1, False)
    return keep, swap(send, "seq", 1 << bit)


def added(keep, got):
    return keep.astype(F32) + got.astype(F32)


def halve_all(blocks, bit):
    while blocks.shape[0] > 1:
        blocks = added(*halve(blocks.astype(BF16), bit))
        bit += 1
    return blocks[0].astype(F32)


def halve_end(keep, got, bit):
    return halve_all(added(keep, got), bit)


def frame_clip_labels(segment, row_length):
    frame_index = jnp.arange(segment.shape[0], dtype=jnp.int32)
    border = (frame_index % row_length == 0) | (segment != jnp.roll(segment, 1))
    clip_starts = lax.cummax(jnp.where(border, frame_index, 0), axis=0)
    return (clip_starts, (frame_index - clip_starts + 1).astype(jnp.float32))


def tile_ranges(q_labels, key_labels):
    q = q_labels.reshape(-1, TILE)
    k = key_labels.reshape(-1, TILE)
    meets = (k[None, :, 0] <= q[:, None, -1]) & (k[None, :, -1] >= q[:, None, 0])
    index = jnp.arange(k.shape[0], dtype=jnp.int32)[None]
    low = jnp.min(jnp.where(meets, index, k.shape[0]), 1)
    high = jnp.max(jnp.where(meets, index + 1, 0), 1)
    return jnp.stack([low, high], 1).reshape(-1)

def head_rows(g):
    return slice(g * HEAD_SIZE, (g + 1) * HEAD_SIZE)

def fill_natural(dest, refs, which):
    size = refs[0].shape[2]
    for part, ref in enumerate(refs):
        dest[part * size : (part + 1) * size, :] = ref[which].T


def fill_tiles(dest, refs, which):
    pieces = refs[0].shape[2] // TILE
    for part, ref in enumerate(refs):
        for piece in range(pieces):
            dest[part * pieces + piece] = ref[which, :, piece * TILE : (piece + 1) * TILE]


def relative(place, r, size):
    return pl.ds(pl.multiple_of((place ^ r) * size, size), size)


def absorb(state, start, stop, base, q, cols, lab, klab, keys, vals):
    group = q.shape[0] // HEAD_SIZE

    def step(j, state):
        seen = klab[pl.ds(pl.multiple_of(j * TILE, TILE), TILE), :] == lab
        at = pl.ds(pl.multiple_of((j - base) * TILE, TILE), TILE)
        fresh = []
        for g in range(group):
            top, total, acc = state[3 * g : 3 * g + 3]
            s = dot_nn(keys[at, head_rows(g)], q[head_rows(g), cols])
            s = jnp.where(seen, s, -1e30)
            new = jnp.maximum(top, jnp.max(s, 0, keepdims=True))
            fade = jnp.exp(top - new)
            p = jnp.exp(s - new)
            total = total * fade + jnp.sum(p, 0, keepdims=True)
            acc = acc * fade + dot_nn(vals[j - base, head_rows(g), :], p.astype(BF16))
            fresh += [new, total, acc]
        return tuple(fresh)

    return lax.fori_loop(start, stop, step, tuple(state))


def near_body(span, q, kv, tk, tv, qlab, klab, tops, totals, mix, keys, vals):
    rows, size = q.shape
    pieces = size // TILE
    fill_natural(keys, (kv,), 0)
    fill_tiles(vals, (kv,), 1)
    for tile in range(pieces):
        cols = slice(tile * TILE, (tile + 1) * TILE)
        state = []
        for g in range(rows // HEAD_SIZE):
            part = q[head_rows(g), cols].astype(F32)
            top = jnp.sum(part * tk[head_rows(g), :], 0, keepdims=True)
            state += [
                top,
                jnp.ones_like(top),
                jnp.broadcast_to(tv[head_rows(g), :], (HEAD_SIZE, TILE)),
            ]
        start = jnp.maximum(span[2 * tile], pieces)
        stop = jnp.minimum(span[2 * tile + 1], 2 * pieces)
        state = absorb(state, start, stop, pieces, q, cols, qlab[:, cols], klab, keys, vals)
        for g in range(rows // HEAD_SIZE):
            tops[g : g + 1, cols], totals[g : g + 1, cols], mix[head_rows(g), cols] = state[
                3 * g : 3 * g + 3
            ]


def far_body(span, q, kv0, kv2, qlab, klab, w_out, tops, totals, mix,
             out, lse, away, own, low, keys0, keys2, vals0, vals2):
    rows, size = q.shape
    pieces = size // TILE
    for kv, keys, vals in ((kv0, keys0, vals0), (kv2, keys2, vals2)):
        fill_natural(keys, (kv,), 0)
        fill_tiles(vals, (kv,), 1)
    for tile in range(pieces):
        cols = slice(tile * TILE, (tile + 1) * TILE)
        lab = qlab[:, cols]
        state = []
        for g in range(rows // HEAD_SIZE):
            state += [tops[g : g + 1, cols], totals[g : g + 1, cols], mix[head_rows(g), cols]]
        stop = jnp.minimum(span[2 * tile + 1], pieces)
        state = absorb(state, span[2 * tile], stop, 0, q, cols, lab, klab, keys0, vals0)
        start = jnp.maximum(span[2 * tile], 2 * pieces)
        state = absorb(
            state, start, span[2 * tile + 1], 2 * pieces, q, cols, lab, klab, keys2, vals2
        )
        for g in range(rows // HEAD_SIZE):
            top, total, acc = state[3 * g : 3 * g + 3]
            out[head_rows(g), cols] = (acc / total).astype(BF16)
            lse[g : g + 1, cols] = top + jnp.log(total)
    place = span[2 * pieces]
    share = own.shape[0]

    def sent(r):
        return dot_tn(out[:, relative(place, r, share)], w_out[...])

    away[:share, :] = sent(1).astype(BF16)
    away[share:, :] = sent(3).astype(BF16)
    low[...] = sent(2).astype(BF16)
    own[...] = sent(0)


def backward_body(span, q, kv0, kv1, kv2, tk, tv, qlab, klab, w_out, out, lse,
                  g0, g1, g2, g3, dq, to_prev, kept, to_next, times,
                  og, keys, vals, tkeys, ak, av, dtk, dtv):
    rows, size = q.shape
    group = rows // HEAD_SIZE
    pieces = size // TILE
    share = g0.shape[0]
    for r, ref in enumerate((g0, g1, g2, g3)):
        og[:, relative(span[2 * pieces], r, share)] = dot_nt(w_out[...], ref[...]).astype(BF16)
    fill_natural(keys, (kv0, kv1, kv2), 0)
    fill_natural(vals, (kv0, kv1, kv2), 1)
    fill_tiles(tkeys, (kv0, kv1, kv2), 0)
    ak[...] = jnp.zeros_like(ak)
    av[...] = jnp.zeros_like(av)
    for tile in range(pieces):
        cols = slice(tile * TILE, (tile + 1) * TILE)
        lab = qlab[:, cols]
        state, norms, deltas = [], [], []
        for g in range(group):
            hr = head_rows(g)
            qf = q[hr, cols].astype(F32)
            gf = og[hr, cols].astype(F32)
            norm = lse[g : g + 1, cols]
            delta = jnp.sum(gf * out[hr, cols].astype(F32), 0, keepdims=True)
            pt = jnp.exp(jnp.sum(qf * tk[hr, :], 0, keepdims=True) - norm)
            st = pt * (jnp.sum(gf * tv[hr, :], 0, keepdims=True) - delta)
            gk = jnp.sum(qf * st, 1, keepdims=True)
            gv = jnp.sum(gf * pt, 1, keepdims=True)
            if tile == 0:
                dtk[hr, :] = gk
                dtv[hr, :] = gv
            else:
                dtk[hr, :] += gk
                dtv[hr, :] += gv
            state.append(tk[hr, :] * st)
            norms.append(norm)
            deltas.append(delta)

        def step(j, state):
            start = pl.multiple_of(j * TILE, TILE)
            seen = klab[pl.ds(start, TILE), :] == lab
            fresh = []
            for g in range(group):
                hr = head_rows(g)
                s = dot_nn(keys[pl.ds(start, TILE), hr], q[hr, cols])
                p = jnp.exp(jnp.where(seen, s, -1e30) - norms[g])
                m = dot_nn(vals[pl.ds(start, TILE), hr], og[hr, cols])
                ds = (p * (m - deltas[g])).astype(BF16)
                av[j, hr, :] += dot_nt(og[hr, cols], p.astype(BF16))
                ak[j, hr, :] += dot_nt(q[hr, cols], ds)
                fresh.append(state[g] + dot_nn(tkeys[j, hr, :], ds))
            return tuple(fresh)

        state = lax.fori_loop(span[2 * tile], span[2 * tile + 1], step, tuple(state))
        for g in range(group):
            dq[head_rows(g), cols] = state[g]
    for at, column in ((0, dtk), (1, dtv)):
        spread = jnp.broadcast_to(column[...], (rows, 2 * HEAD_SIZE))
        times[at : at + 1, :] = spread.T[:1, :]
    for part, dest in enumerate((to_prev, kept, to_next)):
        for piece in range(pieces):
            at = slice(piece * TILE, (piece + 1) * TILE)
            dest[0, :, at] = ak[part * pieces + piece].astype(dest.dtype)
            dest[1, :, at] = av[part * pieces + piece].astype(dest.dtype)


def attend_near(span, q, kv, tk, tv, qlab, klab):
    cols, size = q.shape
    wide = lambda *dims: jax.ShapeDtypeStruct(dims, F32)
    vmem = pl.BlockSpec(memory_space=pltpu.VMEM)
    return pl.pallas_call(
        near_body,
        in_specs=[pl.BlockSpec(memory_space=pltpu.SMEM)] + [vmem] * 6,
        out_specs=[vmem] * 3,
        out_shape=[wide(cols // HEAD_SIZE, size), wide(cols // HEAD_SIZE, size), wide(cols, size)],
        scratch_shapes=[pltpu.VMEM((size, cols), BF16), pltpu.VMEM((size // TILE, cols, TILE), BF16)],
        name="attend_near", cost_estimate=FREE,
    )(span, q, kv, tk, tv, qlab, klab)


def attend_far(span, q, behind, ahead, qlab, klab, w_out, state):
    cols, size = q.shape
    share, width = size // 4, w_out.shape[1]
    low = lambda *dims: jax.ShapeDtypeStruct(dims, BF16)
    wide = lambda *dims: jax.ShapeDtypeStruct(dims, F32)
    vmem = pl.BlockSpec(memory_space=pltpu.VMEM)
    keys = pltpu.VMEM((size, cols), BF16)
    vals = pltpu.VMEM((size // TILE, cols, TILE), BF16)
    return pl.pallas_call(
        far_body,
        in_specs=[pl.BlockSpec(memory_space=pltpu.SMEM)] + [vmem] * 9,
        out_specs=[vmem] * 5,
        out_shape=[low(cols, size), wide(cols // HEAD_SIZE, size), low(2 * share, width),
                   wide(share, width), low(share, width)],
        scratch_shapes=[keys, keys, vals, vals],
        name="attend_far", cost_estimate=FREE,
    )(span, q, behind, ahead, qlab, klab, w_out, *state)


def attend_back(span, q, kvs, tk, tv, qlab, klab, w_out, out, lse, grads):
    cols, size = q.shape
    tiles = 3 * size // TILE
    low = lambda *dims: jax.ShapeDtypeStruct(dims, BF16)
    wide = lambda *dims: jax.ShapeDtypeStruct(dims, F32)
    vmem = pl.BlockSpec(memory_space=pltpu.VMEM)
    return pl.pallas_call(
        backward_body,
        in_specs=[pl.BlockSpec(memory_space=pltpu.SMEM)] + [vmem] * 15,
        out_specs=[vmem] * 5,
        out_shape=[wide(cols, size), low(2, cols, size), wide(2, cols, size), low(2, cols, size),
                   wide(2, cols)],
        scratch_shapes=[pltpu.VMEM((cols, size), BF16), pltpu.VMEM((3 * size, cols), BF16),
                        pltpu.VMEM((3 * size, cols), BF16), pltpu.VMEM((tiles, cols, TILE), BF16),
                        pltpu.VMEM((tiles, cols, TILE), F32), pltpu.VMEM((tiles, cols, TILE), F32),
                        pltpu.VMEM((cols, 1), F32), pltpu.VMEM((cols, 1), F32)],
        name="attend_back", cost_estimate=FREE,
    )(span, q, *kvs, tk, tv, qlab, klab, w_out, out, lse, *grads)


def tail_body(place, dq, kept, ahead, behind, cosine, sine, wq, wk, wv, times,
              raw, away, own, low, flipped):
    part, size = dq.shape
    half = HEAD_SIZE // 2

    def returned(block, base, scale):
        for h in range(part // HEAD_SIZE):
            a = block[h * HEAD_SIZE : h * HEAD_SIZE + half, :]
            b = block[h * HEAD_SIZE + half : (h + 1) * HEAD_SIZE, :]
            at = base + h * HEAD_SIZE
            raw[at : at + half, :] = ((a * cosine[...] + b * sine[...]) * scale).astype(BF16)
            raw[at + half : at + HEAD_SIZE, :] = (
                (b * cosine[...] - a * sine[...]) * scale
            ).astype(BF16)

    def whole(index):
        return kept[index] + ahead[index].astype(F32) + behind[index].astype(F32)

    returned(dq[...], 0, 1.0 / math.sqrt(HEAD_SIZE))
    returned(whole(0), part, 1.0)
    raw[2 * part : 3 * part, :] = whole(1).astype(BF16)
    raw[3 * part :, :] = jnp.zeros((16, size), BF16)
    raw[3 * part : 3 * part + 2, :part] = times[...].astype(BF16)
    flipped[...] = raw[: 3 * part, :].T

    def sent(r):
        at = relative(place[0], r, part)
        return sum(
            dot_nt(flipped[:, i * part : (i + 1) * part], weight[at, :])
            for i, weight in enumerate((wq, wk, wv))
        )

    away[:size, :] = sent(1).astype(BF16)
    away[size:, :] = sent(3).astype(BF16)
    low[...] = sent(2).astype(BF16)
    own[...] = sent(0)


def tail(place, dq, kept, ahead, behind, tables, wq, wk, wv, times):
    part, size = dq.shape
    low = lambda *dims: jax.ShapeDtypeStruct(dims, BF16)
    vmem = pl.BlockSpec(memory_space=pltpu.VMEM)
    return pl.pallas_call(
        tail_body,
        in_specs=[pl.BlockSpec(memory_space=pltpu.SMEM)] + [vmem] * 10,
        out_specs=[vmem] * 4,
        out_shape=[low(3 * part + 16, size), low(2 * size, part), jax.ShapeDtypeStruct((size, part), F32),
                   low(size, part)],
        scratch_shapes=[pltpu.VMEM((size, 3 * part), BF16)],
        name="tail", cost_estimate=FREE,
    )(place, dq, kept, ahead, behind, *tables, wq, wk, wv, times)


def rotary_tables(frame_positions):
    half_dim = HEAD_SIZE // 2
    frequency = jnp.exp(jnp.arange(half_dim, dtype=jnp.float32) * (-math.log(10000.0) / half_dim))
    angles = frequency[:, None] * frame_positions[None, :]
    return (jnp.cos(angles), jnp.sin(angles))


def rotate(rows, tables, sign=1.0):
    count, size = rows.shape
    halves = rows.reshape(count // HEAD_SIZE, 2, HEAD_SIZE // 2, size)
    cosine, sine = tables[0][None], tables[1][None] * sign
    first = halves[:, 0] * cosine - halves[:, 1] * sine
    second = halves[:, 1] * cosine + halves[:, 0] * sine
    return jnp.stack([first, second], 1).reshape(count, size)


def product(left, right):
    return jnp.dot(left, right, preferred_element_type=jnp.float32)


def inner_rows(left, right):
    return jnp.einsum("nd,nf->df", left, right, preferred_element_type=jnp.float32)


def back_project(gradient, weight):
    return jnp.einsum("nf,df->nd", gradient, weight, preferred_element_type=jnp.float32)


def by_feature(left, right):
    return jnp.einsum("nd,df->fn", left, right, preferred_element_type=jnp.float32)


def columns(weight, start, size):
    return lax.dynamic_slice_in_dim(weight, start, size, 1)


def rows_of(weight, start, size):
    return lax.dynamic_slice_in_dim(weight, start, size, 0)


def normalize(value_rows):
    means = jnp.mean(value_rows, -1, keepdims=True)
    centred = value_rows - means
    inverse = lax.rsqrt(jnp.mean(centred * centred, -1, keepdims=True) + 1e-05)
    return centred * inverse, inverse


def norm_backward(gradient, scaled, inverse, norm_gain):
    scaled_grad = gradient * norm_gain
    plain = jnp.mean(scaled_grad, -1, keepdims=True)
    cross = jnp.mean(scaled_grad * scaled, -1, keepdims=True)
    return inverse * (scaled_grad - plain - scaled * cross)


FREE = pl.CostEstimate(flops=1, transcendentals=0, bytes_accessed=1)


def dot_nn(left, right):
    return lax.dot_general(left, right, (((1,), (0,)), ((), ())), preferred_element_type=F32)


def dot_nt(left, right):
    return lax.dot_general(left, right, (((1,), (1,)), ((), ())), preferred_element_type=F32)


def dot_tn(left, right):
    return lax.dot_general(left, right, (((0,), (0,)), ((), ())), preferred_element_type=F32)


def head_weights(query, key, lanes, which):
    mine = jnp.where(lanes == which, query, jnp.zeros_like(query))
    scores = dot_nt(mine, key) * (1.0 / math.sqrt(HEAD_SIZE))
    weights = jnp.exp(scores - jnp.max(scores, -1, keepdims=True))
    return weights / jnp.sum(weights, -1, keepdims=True)


def pair_cols(refs, p, rows):
    ref = refs[p * 2 * HEAD_SIZE // refs[0].shape[1]]
    start = p * 2 * HEAD_SIZE % refs[0].shape[1]
    return ref[rows, start : start + 2 * HEAD_SIZE]


def cross_forward_body(width_block, place, rows, own, got, far, norms, q0, q1, q2, q3,
                       c0, c1, c2, c3, o0, o1, o2, o3,
                       front, queries, first, second, normed_three,
                       flip_own, flip_away):
    width = rows.shape[1]
    kv = (c0, c1, c2, c3)
    context_rows = c0.shape[0] // 2
    key_rows, value_rows = slice(0, context_rows), slice(context_rows, 2 * context_rows)
    lanes = lax.broadcasted_iota(jnp.int32, (rows.shape[0], 2 * HEAD_SIZE), 1) // HEAD_SIZE
    residual = (
        rows[...].astype(F32) + own[...] + got[...].astype(F32) + far[...].astype(F32)
    )
    first[...] = residual
    scaled, _ = normalize(residual)
    low = (scaled * norms[2:3, :] + norms[3:4, :]).astype(BF16)
    front[:, :width] = low
    part = width // 4
    for b, ref in enumerate((q0, q1, q2, q3)):
        queries[:, b * part : (b + 1) * part] = dot_nn(low, ref[...]).astype(BF16)
    for p in range(width // (2 * HEAD_SIZE)):
        cols = slice(p * 2 * HEAD_SIZE, (p + 1) * 2 * HEAD_SIZE)
        q, k, v = queries[:, cols], pair_cols(kv, p, key_rows), pair_cols(kv, p, value_rows)
        mixed = [dot_nn(head_weights(q, k, lanes, g).astype(BF16), v) for g in (0, 1)]
        front[:, width + cols.start : width + cols.stop] = jnp.where(lanes == 0, mixed[0], mixed[1]).astype(BF16)
    for b, ref in enumerate((o0, o1, o2, o3)):
        residual = residual + dot_nn(front[:, width + b * part : width + (b + 1) * part], ref[...])
    second[...] = residual
    scaled, _ = normalize(residual)
    low = (scaled * norms[4:5, :] + norms[5:6, :]).astype(BF16)
    normed_three[...] = low
    deal_rows(low.T, width_block, place[0], flip_own, flip_away)


def cross_forward(devices, place, rows, own, got, far, norms, query_parts, kv_parts, out_parts):
    size, width = rows.shape
    low = jax.ShapeDtypeStruct(rows.shape, BF16)
    both = jax.ShapeDtypeStruct((size, 2 * width), BF16)
    wide = jax.ShapeDtypeStruct(rows.shape, F32)
    flip = jax.ShapeDtypeStruct((width // 2, size), BF16)
    vmem = pl.BlockSpec(memory_space=pltpu.VMEM)
    block = pl.BlockSpec((size, width), lambda i: (0, 0))
    return pl.pallas_call(
        functools.partial(cross_forward_body, width // devices),
        grid=(1,),
        in_specs=[pl.BlockSpec(memory_space=pltpu.SMEM)] + [block] * 4 + [vmem] * 13,
        out_shape=[both, low, wide, wide, low, flip, flip],
        cost_estimate=FREE, name="cross",
    )(place, rows, own, got, far, norms, *query_parts, *kv_parts, *out_parts)


def deal_rows(rows, size, column, own, away):
    for b in range(rows.shape[0] // (2 * size)):
        at = slice(b * size, (b + 1) * size)
        even = rows[2 * b * size : (2 * b + 1) * size, :]
        odd = rows[(2 * b + 1) * size : (2 * b + 2) * size, :]

        @pl.when(column == 0)
        def _():
            own[at, :] = even
            away[at, :] = odd

        @pl.when(column != 0)
        def _():
            own[at, :] = odd
            away[at, :] = even


def ffn_part(normed, grad, gate_w, up_w, down_w, hidden, hid_own, hid_away, gate_grad, lifted_grad,
             unit_block, column):
    gate = dot_nn(normed, gate_w[...])
    lifted = dot_nn(normed, up_w[...])
    back = dot_nt(grad, down_w[...]).astype(BF16).astype(F32)
    sig = jax.nn.sigmoid(gate)
    swish = gate * sig
    made = (swish * lifted).astype(BF16)
    hidden[...] = made
    deal_rows(made.T, unit_block, column, hid_own, hid_away)
    gg = (back * lifted * sig * (1.0 + gate * (1.0 - sig))).astype(BF16)
    lg = (back * swish).astype(BF16)
    gate_grad[...] = gg
    lifted_grad[...] = lg
    return dot_nt(gg, gate_w[...]) + dot_nt(lg, up_w[...])


def ffn_first_body(unit_block, place, n0, n1, n2, n3, g0, g1, g2, g3, gate_w, up_w, down_w,
                   hidden, hid_own, hid_away, gate_grad, lifted_grad, normed, grad, grad_pair,
                   total):
    share, part = n0.shape[0], g0.shape[2]
    for b, ref in enumerate((n0, n1, n2, n3)):
        normed[b * share : (b + 1) * share, :] = ref[...]
    for c, ref in enumerate((g0, g1, g2, g3)):
        for b in range(4):
            rows, cols = relative(place[1], b, share), relative(place[1], c, part)
            grad[b * share : (b + 1) * share, cols] = ref[0, rows, :]
            grad_pair[b * share : (b + 1) * share, cols] = ref[1, rows, :]
    total[...] = ffn_part(
        normed[...], grad[...], gate_w, up_w, down_w, hidden, hid_own, hid_away, gate_grad,
        lifted_grad, unit_block, place[0],
    )


def ffn_second_body(unit_block, place, normed, grad, total, gate_w, up_w, down_w,
                    hidden, hid_own, hid_away, gate_grad, lifted_grad, away, own, low):
    share = own.shape[0]
    found = total[...] + ffn_part(
        normed[...], grad[...], gate_w, up_w, down_w, hidden, hid_own, hid_away, gate_grad,
        lifted_grad, unit_block, place[0],
    )
    own[...] = found[:share, :]
    low[...] = found[2 * share : 3 * share, :].astype(BF16)
    away[:share, :] = found[share : 2 * share, :].astype(BF16)
    away[share:, :] = found[3 * share :, :].astype(BF16)


def ffn(devices, place, half, inputs, gate_w, up_w, down_w):
    share = inputs[0].shape[0] if half == 0 else inputs[0].shape[0] // 4
    width = inputs[0].shape[1]
    size, units = 4 * share, gate_w.shape[1]
    tile = units // 2
    low = lambda *dims: jax.ShapeDtypeStruct(dims, BF16)
    wide = lambda *dims: jax.ShapeDtypeStruct(dims, F32)
    vmem = pl.BlockSpec(memory_space=pltpu.VMEM)
    cols = pl.BlockSpec((width, tile), lambda i: (0, half))
    rows = pl.BlockSpec((tile, width), lambda i: (half, 0))
    made = [low(size, tile), low(tile // 2, size), low(tile // 2, size), low(size, tile),
            low(size, tile)]
    if half == 0:
        made += [low(size, width), low(size, width), low(size, width), wide(size, width)]
    else:
        made += [low(2 * share, width), wide(share, width), low(share, width)]
    return pl.pallas_call(
        functools.partial(ffn_second_body if half else ffn_first_body, units // devices),
        grid=(1,),
        in_specs=[pl.BlockSpec(memory_space=pltpu.SMEM)] + [vmem] * len(inputs)
        + [cols, cols, rows],
        out_specs=[vmem] * len(made),
        out_shape=made,
        cost_estimate=FREE, name="ffn",
    )(place, *inputs, gate_w, up_w, down_w)


def cross_backward_body(own, got, far, grad, first, second, norms, q0, q1, q2, q3,
                        c0, c1, c2, c3, o0, o1, o2, o3, queries,
                        back_rows, kv_grad, vectors, grad_one, crossed_grad):
    width = grad.shape[1]
    kv = (c0, c1, c2, c3)
    context_rows = c0.shape[0] // 2
    key_rows, value_rows = slice(0, context_rows), slice(context_rows, 2 * context_rows)
    part = width // 4
    lanes = lax.broadcasted_iota(jnp.int32, (grad.shape[0], 2 * HEAD_SIZE), 1) // HEAD_SIZE
    lane_k = lax.broadcasted_iota(jnp.int32, (context_rows, 2 * HEAD_SIZE), 1) // HEAD_SIZE
    scale = 1.0 / math.sqrt(HEAD_SIZE)
    arrived = own[...] + got[...].astype(F32) + far[...].astype(F32)
    scaled, inverse = normalize(second[...])
    vectors[0:1, :] = jnp.sum(arrived * scaled, 0, keepdims=True)
    vectors[1:2, :] = jnp.sum(arrived, 0, keepdims=True)
    two = grad[...].astype(F32) + norm_backward(arrived, scaled, inverse, norms[4:5, :])
    low = two.astype(BF16)
    back_rows[:, :width] = low
    for b, ref in enumerate((o0, o1, o2, o3)):
        crossed_grad[:, b * part : (b + 1) * part] = dot_nt(low, ref[...]).astype(BF16)
    for p in range(width // (2 * HEAD_SIZE)):
        cols = slice(p * 2 * HEAD_SIZE, (p + 1) * 2 * HEAD_SIZE)
        q, k, v = queries[:, cols], pair_cols(kv, p, key_rows), pair_cols(kv, p, value_rows)
        g_rows = crossed_grad[:, cols]
        found = []
        for g in (0, 1):
            probs = head_weights(q, k, lanes, g)
            change = dot_nt(jnp.where(lanes == g, g_rows, jnp.zeros_like(g_rows)), v)
            delta = jnp.sum(change * probs, -1, keepdims=True)
            ds = (probs * (change - delta)).astype(BF16)
            found.append((dot_nn(ds, k), dot_tn(ds, q), dot_tn(probs.astype(BF16), g_rows)))
        back_rows[:, width + cols.start : width + cols.stop] = (
            jnp.where(lanes == 0, found[0][0], found[1][0]) * scale
        ).astype(BF16)
        kv_grad[:context_rows, cols] = (
            jnp.where(lane_k == 0, found[0][1], found[1][1]) * scale
        ).astype(BF16)
        kv_grad[context_rows:, cols] = jnp.where(lane_k == 0, found[0][2], found[1][2]).astype(
            BF16
        )
    back = jnp.zeros(grad.shape, F32)
    for b, ref in enumerate((q0, q1, q2, q3)):
        back = back + dot_nt(back_rows[:, width + b * part : width + (b + 1) * part], ref[...])
    scaled, inverse = normalize(first[...])
    vectors[2:3, :] = jnp.sum(back * scaled, 0, keepdims=True)
    vectors[3:4, :] = jnp.sum(back, 0, keepdims=True)
    grad_one[...] = (two + norm_backward(back, scaled, inverse, norms[2:3, :])).astype(BF16)


def cross_backward(own, got, far, grad, first, second, norms, query_parts, kv_parts, out_parts,
                   queries):
    rows, width = own.shape
    low = lambda r: jax.ShapeDtypeStruct((r, width), BF16)
    block = pl.BlockSpec((rows, width), lambda i: (0, 0))
    return pl.pallas_call(
        cross_backward_body,
        grid=(1,),
        out_shape=[jax.ShapeDtypeStruct((rows, 2 * width), BF16), low(kv_parts[0].shape[0]),
                   jax.ShapeDtypeStruct((4, width), F32), low(rows)],
        in_specs=[block] * 6 + [pl.BlockSpec(memory_space=pltpu.VMEM)] * 14,
        scratch_shapes=[pltpu.VMEM((rows, width), BF16)],
        cost_estimate=FREE, name="cross_back",
    )(own, got, far, grad, first, second, norms, *query_parts, *kv_parts, *out_parts, queries)


def meet_rows_body(size, side, own_a, pair_a, own_b, pair_b, right, right_pair, keep, send):
    half = keep.shape[0] // 2
    for b, (own, pair) in enumerate(((own_a, pair_a), (own_b, pair_b))):
        made = (dot_nn(own[...], right[...]) + dot_nn(pair[...], right_pair[...])).astype(BF16)
        at = pl.ds(b * half, half)
        deal_rows(made, size, side[0], keep.at[at], send.at[at])


def meet_rows(size, side, lefts, rights):
    count, frames = lefts[0].shape
    width = rights[0].shape[1]
    tile = width // 3
    left = pl.BlockSpec((count, frames), lambda i: (0, 0))
    right = pl.BlockSpec((frames, tile), lambda i: (0, i))
    return pl.pallas_call(
        functools.partial(meet_rows_body, size),
        grid=(3,),
        in_specs=[pl.BlockSpec(memory_space=pltpu.SMEM)] + [left] * 4 + [right] * 2,
        out_specs=[pl.BlockSpec((count, tile), lambda i: (0, i))] * 2,
        out_shape=[jax.ShapeDtypeStruct((count, width), BF16)] * 2,
        name="meet_rows", cost_estimate=FREE,
    )(side, *lefts, *rights)


def meet_cols_body(size, side, p0, p1, p2, p3, *refs):
    own, pair = (jnp.concatenate([p[i] for p in (p0, p1, p2, p3)], 1) for i in (0, 1))
    *rights, keep, send = refs
    width = rights[0].shape[1]
    for at in range(len(rights) // 2):
        made = dot_nn(own, rights[2 * at][...]) + dot_nn(pair, rights[2 * at + 1][...])
        cols = pl.ds(at * width, width)
        deal_rows(made.astype(BF16), size, side[0], keep.at[:, cols], send.at[:, cols])


def meet_cols(size, side, near, rights):
    width = rights[0].shape[1] * (len(rights) // 2)
    half = jax.ShapeDtypeStruct((near[0].shape[1] // 2, width), BF16)
    vmem = pl.BlockSpec(memory_space=pltpu.VMEM)
    return pl.pallas_call(
        functools.partial(meet_cols_body, size),
        in_specs=[pl.BlockSpec(memory_space=pltpu.SMEM)] + [vmem] * (4 + len(rights)),
        out_shape=[half] * 2,
        name="meet_cols", cost_estimate=FREE,
    )(side, *near, *rights)


def down_body(first, second, down_w, away, own, low):
    share, units = own.shape[0], first.shape[1]

    def sent(r):
        at = slice(r * share, (r + 1) * share)
        return dot_nn(first[at, :], down_w[:units, :]) + dot_nn(second[at, :], down_w[units:, :])

    away[:share, :] = sent(1).astype(BF16)
    away[share:, :] = sent(3).astype(BF16)
    low[...] = sent(2).astype(BF16)
    own[...] = sent(0)


def down_parts(first, second, down_w):
    share, width = first.shape[0] // 4, down_w.shape[1]
    low = lambda *dims: jax.ShapeDtypeStruct(dims, BF16)
    return pl.pallas_call(
        down_body,
        out_shape=[low(2 * share, width), jax.ShapeDtypeStruct((share, width), F32),
                   low(share, width)],
        name="down", cost_estimate=FREE,
    )(first, second, down_w)


def bundle_body(devices, place, f02, f13, b02, b13, a0, a1, a2, a3, attended,
                context, kv, keep_a, send_a, keep_b, send_b):
    width = a0.shape[1]
    part, share = width // 4, a0.shape[0]

    def near(even, odd):
        return even[0], odd[0], even[1], odd[1]

    own = lambda rows: jnp.concatenate(
        [row[:, width + r * part : width + (r + 1) * part] for r, row in enumerate(rows)], 0
    )
    full = lambda rows: jnp.concatenate([row[:, :width] for row in rows], 0)
    fronts, backs = near(f02, f13), near(b02, b13)
    rows = width // devices
    small = part // devices
    half = width // 2

    def put(block, base, left, out):
        size = block.shape[0] // devices
        cols = slice(left, left + block.shape[1])
        low = block.astype(BF16)
        for d in range(0, devices, 2):
            at = slice(base, base + size)
            even, odd = low[d * size : (d + 1) * size, :], low[(d + 1) * size : (d + 2) * size, :]

            @pl.when(place[0] == 0)
            def _():
                out[0][d // 2, at, cols] = even
                out[1][d // 2, at, cols] = odd

            @pl.when(place[0] != 0)
            def _():
                out[0][d // 2, at, cols] = odd
                out[1][d // 2, at, cols] = even

    put(dot_tn(full(fronts), own(backs)), 0, 0, (keep_a, send_a))
    count = context.shape[0]
    put(dot_tn(context[...], kv[:count, :]), 0, part, (keep_a, send_a))
    put(dot_tn(context[...], kv[count:, :]), rows // 2, part, (keep_a, send_a))
    grads = dot_tn(own(fronts), full(backs))
    put(grads[:, :half], 0, 0, (keep_b, send_b))
    put(grads[:, half:], small, 0, (keep_b, send_b))
    grads = sum(
        dot_nn(attended[:, relative(place[1], r, share)], ref[...])
        for r, ref in enumerate((a0, a1, a2, a3))
    )
    put(grads[:, :half], 2 * small, 0, (keep_b, send_b))
    put(grads[:, half:], 3 * small, 0, (keep_b, send_b))


def bundle_grads(devices, place, fronts, backs, ones, attended, context, kv):
    width = ones[0].shape[1]
    vmem = pl.BlockSpec(memory_space=pltpu.VMEM)
    return pl.pallas_call(
        functools.partial(bundle_body, devices),
        in_specs=[pl.BlockSpec(memory_space=pltpu.SMEM)] + [vmem] * 11,
        out_specs=[vmem] * 4,
        out_shape=[jax.ShapeDtypeStruct((devices // 2, width // devices, width // 2), BF16)] * 4,
        name="bundle", cost_estimate=FREE,
    )(place, *fronts, *backs, *ones, attended, context, kv)


def front_body(width_block, place, x0, x1, x2, x3, g0, g1, g2, g3, cosine, sine, wq, wk, wv,
               time_row, context, ck, cv,
               queries, pair, rows, low, nrm_own, nrm_away, norms, means, inverses,
               time_scaled, time_low, time_keys, time_values, kv, wide):
    size, part = x0.shape
    for r, (x, g) in enumerate(((x0, g0), (x1, g1), (x2, g2), (x3, g3))):
        start = pl.multiple_of((place[0] ^ r) * part, 128)
        wide[:, pl.ds(start, part)] = x[...]
        norms[:, pl.ds(start, part)] = g[...]
    share = size // 4
    rows[...] = wide[pl.ds(pl.multiple_of(place[0] * share, share), share), :]
    values = wide[...].astype(F32)
    mean = jnp.mean(values, -1, keepdims=True)
    centred = values - mean
    inverse = lax.rsqrt(jnp.mean(centred * centred, -1, keepdims=True) + 1e-05)
    means[...] = mean
    inverses[...] = inverse
    normed = (centred * inverse * norms[0:1, :] + norms[1:2, :]).astype(BF16)
    low[...] = normed
    half = HEAD_SIZE // 2

    def turned(weight):
        return dot_nn(normed, weight[...]).T

    def rotated(block, dest, scale):
        for h in range(part // HEAD_SIZE):
            a = block[h * HEAD_SIZE : h * HEAD_SIZE + half, :]
            b = block[h * HEAD_SIZE + half : (h + 1) * HEAD_SIZE, :]
            dest[h * HEAD_SIZE : h * HEAD_SIZE + half, :] = (
                (a * cosine[...] - b * sine[...]) * scale
            ).astype(BF16)
            dest[h * HEAD_SIZE + half : (h + 1) * HEAD_SIZE, :] = (
                (b * cosine[...] + a * sine[...]) * scale
            ).astype(BF16)

    scaled, _ = normalize(jnp.broadcast_to(time_row[...].astype(F32), (8, 4 * part)))
    time_scaled[...] = scaled[:1, :]
    made = (scaled * norms[0:1, :] + norms[1:2, :]).astype(BF16)
    time_low[...] = made[:1, :].astype(F32)
    time_keys[...] = dot_nn(made, wk[...]).astype(BF16).astype(F32).T[:, :1]
    time_values[...] = dot_nn(made, wv[...]).astype(BF16).astype(F32).T[:, :1]
    count = context.shape[0]
    kv[:count, :] = dot_nn(context[...], ck[...]).astype(BF16)
    kv[count:, :] = dot_nn(context[...], cv[...]).astype(BF16)
    rotated(turned(wk), pair.at[0], 1.0)
    pair[1] = turned(wv).astype(BF16)
    rotated(turned(wq), queries, 1.0 / math.sqrt(HEAD_SIZE))
    deal_rows(normed.T, width_block, place[1], nrm_own, nrm_away)


def front(devices, place, parts, norm_parts, tables, wq, wk, wv, time_row, context, ck, cv):
    size, part = parts[0].shape
    width = 4 * part
    low = lambda *s: jax.ShapeDtypeStruct(s, BF16)
    wide = lambda *s: jax.ShapeDtypeStruct(s, F32)
    vmem = pl.BlockSpec(memory_space=pltpu.VMEM)
    return pl.pallas_call(
        functools.partial(front_body, width // devices),
        in_specs=[pl.BlockSpec(memory_space=pltpu.SMEM)] + [vmem] * 17,
        out_specs=[vmem] * 14,
        out_shape=[low(part, size), low(2, part, size), low(size // 4, width), low(size, width),
                   low(width // 2, size), low(width // 2, size), wide(6, width),
                   wide(size, 1), wide(size, 1), wide(1, width), wide(1, width), wide(part, 1),
                   wide(part, 1), low(2 * context.shape[0], part)],
        scratch_shapes=[pltpu.VMEM((size, width), BF16)],
        cost_estimate=FREE, name="front",
    )(place, *parts, *norm_parts, *tables, wq, wk, wv, time_row, context, ck, cv)


def per_device(
    frames,
    segment,
    time_token,
    context,
    gain_attn,
    bias_attn,
    gain_cross,
    bias_cross,
    gain_ffn,
    bias_ffn,
    w_query,
    w_key,
    w_value,
    w_out,
    c_query,
    c_key,
    c_value,
    c_out,
    w_gate,
    w_up,
    w_down,
    out_grad,
):
    local_rows = frames.shape[0]
    local_width = frames.shape[1]
    model_width = w_query.shape[0]
    head_cols = w_query.shape[1]
    heads = head_cols // HEAD_SIZE
    number_of_frames = lax.axis_size("seq") * local_rows
    row_length = min(max(ROW_MIN, 64 * lax.axis_size("seq")), number_of_frames)
    first_frame = lax.axis_index("seq") * local_rows
    own_start = lax.axis_index("tensor") * local_width

    def own_cols(value):
        return lax.dynamic_slice_in_dim(value, own_start, local_width, value.ndim - 1)

    place = lax.axis_index("tensor")
    share = local_rows // 4

    def row_block(value, index):
        return rows_of(value, index * share, share)

    column = lax.axis_index("seq") % 2
    frame_parts_near = gather_near(frames)
    norm_parts = gather_near(
        jnp.stack([gain_attn, bias_attn, gain_cross, bias_cross, gain_ffn, bias_ffn])
    )
    clip_starts, frame_positions = frame_clip_labels(segment, row_length)
    own_labels = lax.dynamic_slice_in_dim(clip_starts, first_frame, local_rows)
    own_positions = lax.dynamic_slice_in_dim(frame_positions, first_frame, local_rows)
    blanks = jnp.full((local_rows,), -1, jnp.int32)
    key_labels = lax.dynamic_slice_in_dim(
        jnp.concatenate([blanks, clip_starts, blanks]), first_frame, 3 * local_rows
    )
    spans = jnp.concatenate(
        [tile_ranges(own_labels, key_labels), place.astype(jnp.int32).reshape(1)]
    )
    places = jnp.stack([column, place]).astype(jnp.int32)
    label_row, label_column = own_labels[None, :], key_labels[:, None]
    row_index = first_frame // row_length
    time_row = lax.dynamic_slice_in_dim(time_token, row_index, 1, 0)
    row_context = lax.dynamic_slice_in_dim(context, row_index, 1, 0)[0]
    context_rows = row_context.shape[0]
    tables = rotary_tables(own_positions)
    score_scale = 1.0 / math.sqrt(HEAD_SIZE)
    all_heads = model_width // HEAD_SIZE

    (
        queries, both, frame_rows, frame_normed, one_own_half, one_away_half, norms, means_one,
        inverse_one, scaled_time, time_normed, time_keys, time_values, context_kv,
    ) = front(
        lax.axis_size("seq"), jnp.flip(places), frame_parts_near, norm_parts, tables, w_query,
        w_key, w_value, time_row, row_context, c_key, c_value,
    )
    both, out_pair = meeting(both, swap(after(out_grad, frame_parts_near[2]), "seq", 1))
    grad_both = jnp.stack([out_grad, out_pair])
    behind, ahead = shift(both, "seq", 1), shift(both, "seq", -1)
    query_late, out_late = after((c_query, c_out), (frame_parts_near[2], norm_parts[2]))
    query_far, out_far = swap(query_late, "tensor", 2), swap(out_late, "tensor", 2)
    state = attend_near(spans, queries, both, time_keys, time_values, label_row, label_column)
    behind, ahead, query_far, out_far, *state = meeting(
        behind, ahead, query_far, out_far, *state
    )
    query_own, out_own, context_late = after((c_query, c_out, context_kv), behind)
    weights_near = [
        swap(value, "tensor", 1) for value in (query_own, query_far, out_own, out_far)
    ]
    kv_far = swap(context_late, "tensor", 2)
    attended, log_totals, one_away, one_own, one_low = attend_far(
        spans, queries, behind, ahead, label_row, label_column, w_out, state
    )
    one_away, one_low, kv_far, *weights_near = meeting(one_away, one_low, kv_far, *weights_near)
    kv_both = jnp.concatenate([context_kv, kv_far], 0)
    kv_other = swap(kv_both, "tensor", 1)
    kv_rows = context_kv.shape[0]
    kv_parts = (context_kv, kv_other[:kv_rows], kv_far, kv_other[kv_rows:])
    query_parts = (c_query, weights_near[0], query_far, weights_near[1])
    out_parts = (c_out, weights_near[2], out_far, weights_near[3])
    one_got, _, one_far = scatter_near(one_away, one_low)
    (
        front_rows, cross_queries, residual_one, residual_two, normed_share, flip_own, flip_away,
    ) = cross_forward(
        lax.axis_size("seq"), places, frame_rows, one_own, one_got, one_far, norms,
        query_parts, kv_parts, out_parts,
    )
    grad_far = swap(after(grad_both, one_far), "tensor", 2)
    normed_share, normed_got, grad_far = meeting(
        normed_share, swap(after(one_away_half, one_low), "seq", 1), grad_far
    )
    grad_late, grad_far_late = after((grad_both, grad_far), normed_share)
    grad_mate, grad_far_mate = swap(grad_late, "tensor", 1), swap(grad_far_late, "tensor", 1)
    grad_parts = (grad_both, grad_mate, grad_far, grad_far_mate)
    three_parts = gather_near(normed_share)
    flip_got = swap(after(flip_away, normed_share), "seq", 1)
    front_far = swap(after(front_rows, three_parts[3]), "tensor", 2)
    devices = lax.axis_size("seq")
    (
        hidden_a, hidden_own_a, hidden_away_a, gate_a, lifted_a, normed_three, grad_near, grad_pair,
        ffn_total,
    ) = ffn(devices, places, 0, (*three_parts, *grad_parts), w_gate, w_up, w_down)
    ffn_total, flip_got = meeting(ffn_total, flip_got)
    flip_both = jnp.stack([flip_own, flip_got])
    flip_far = swap(flip_both, "tensor", 2)
    hidden_got_a, gate_got_a = swap(hidden_away_a, "seq", 1), swap(gate_a, "seq", 1)
    hidden_b, hidden_own_b, hidden_away_b, gate_b, lifted_b, three_away, three_own, three_low = ffn(
        devices, places, 1, (normed_three, grad_near, ffn_total), w_gate, w_up, w_down
    )
    three_away, three_low, flip_far, front_far, hidden_got_a = meeting(
        three_away, three_low, flip_far, front_far, hidden_got_a
    )
    three_got, _, three_far = scatter_near(three_away, three_low)
    hidden_got_b = swap(after(hidden_away_b, three_low), "seq", 1)
    lifted_got_a = swap(after(lifted_a, three_low), "seq", 1)
    flip_late, flip_far_late, gate_late = after((flip_both, flip_far, gate_b), three_far)
    flip_mate, flip_far_mate = swap(flip_late, "tensor", 1), swap(flip_far_late, "tensor", 1)
    gate_got_b = swap(gate_late, "seq", 1)
    front_both = jnp.stack([front_rows, front_far])
    back_rows, kv_grad, norm_vectors, grad_one = cross_backward(
        three_own, three_got, three_far, grad_near, residual_one, residual_two, norms,
        query_parts, kv_parts, out_parts, cross_queries,
    )
    grad_one, gate_got_a, hidden_got_b, flip_mate, flip_far_mate = meeting(
        grad_one, gate_got_a, hidden_got_b, flip_mate, flip_far_mate
    )
    count = lax.axis_size("seq")
    level_side = ((lax.axis_index("seq") >> 1) % 2).astype(jnp.int32).reshape(1)
    rows = model_width // count

    def traded(dealt):
        keep, send = [value.reshape(count // 4, rows, -1) for value in dealt]
        return keep, swap(send, "seq", 2)

    down_keep, down_got = traded(
        meet_rows(
            rows, level_side, (hidden_own_a, hidden_got_a, hidden_own_b, hidden_got_b),
            (grad_near, grad_pair),
        )
    )
    context_parts = quarters(kv_grad, 1)
    context_got = swap(jnp.concatenate([context_parts[1], context_parts[3]], 0), "tensor", 1)
    one_far_rows, down_keep, lifted_got_a = meeting(
        swap(grad_one, "tensor", 2), down_keep, lifted_got_a
    )
    one_parts = (
        grad_one, swap(grad_one, "tensor", 1), one_far_rows, swap(one_far_rows, "tensor", 1)
    )
    *one_parts, front_other, context_got = meeting(
        *one_parts, swap(after(front_both, grad_one), "tensor", 1), context_got
    )
    context_low = (
        context_parts[2].astype(F32) + context_got[context_parts[2].shape[0] :].astype(F32)
    ).astype(BF16)
    context_far = swap(context_low, "tensor", 2)
    back_far = swap(after(back_rows, one_parts[3]), "tensor", 2)
    lifted_got_b = swap(after(lifted_b, grad_one), "seq", 1)
    query_grad, to_prev, kept, to_next, time_grads = attend_back(
        spans, queries, (behind, both, ahead), time_keys, time_values, label_row, label_column,
        w_out, attended, log_totals, one_parts,
    )
    to_prev, to_next, back_far, gate_got_b, lifted_got_b, down_got, context_far = meeting(
        to_prev, to_next, back_far, gate_got_b, lifted_got_b, down_got, context_far
    )
    from_next, from_prev = shift(to_prev, "seq", -1), shift(to_next, "seq", 1)
    down_keep, down_got = halve(added(down_keep, down_got).astype(BF16), 2)
    flip_near = (flip_both, flip_mate, flip_far, flip_far_mate)
    first_keep, first_got = traded(
        meet_cols(
            rows, level_side, flip_near,
            after((gate_a, gate_got_a, lifted_a, lifted_got_a), to_prev),
        )
    )
    back_both = jnp.stack([back_rows, back_far])
    back_other = swap(back_both, "tensor", 1)
    context_own = (
        context_parts[0].astype(F32)
        + context_got[: context_far.shape[0]].astype(F32)
        + context_far.astype(F32)
    )
    keep_a, send_a, keep_b, send_b = bundle_grads(
        count, places, (front_both, front_other), (back_both, back_other), one_parts, attended,
        row_context,
        context_own.astype(BF16),
    )
    from_next, from_prev, down_got, send_a, send_b = meeting(
        from_next, from_prev, down_got, send_a, send_b
    )
    got_a = swap(send_a, "seq", 1)
    raw, last_away, last_own, last_low = tail(
        places[1:], query_grad, kept, from_next, from_prev, tables, w_query, w_key, w_value,
        time_grads,
    )
    last_got = swap(last_away, "tensor", 1)
    raw_got = swap(raw, "seq", 1)
    last_sum = (
        last_low.astype(F32) + last_got[local_rows:].astype(F32)
    ).astype(BF16)
    second_keep, second_got = traded(
        meet_cols(
            rows, level_side, flip_near,
            after((gate_b, gate_got_b, lifted_b, lifted_got_b), last_away),
        )
    )
    last_sum, first_got = meeting(last_sum, first_got)
    first_keep, first_got = halve(added(first_keep, first_got).astype(BF16), 2)
    last_far, raw_got = meeting(swap(last_sum, "tensor", 2), raw_got)
    frame_grad = last_own + last_got[:local_rows].astype(F32) + last_far.astype(F32)

    time_late, means_late, inverse_late, vectors_late = after(
        (time_grads, means_one, inverse_one, norm_vectors), last_far
    )
    time_grad = sum(
        jnp.einsum("of,df->od", time_late[i : i + 1].astype(BF16), w, preferred_element_type=F32)
        for i, w in enumerate((w_key, w_value))
    )
    own_scaled = (frames.astype(F32) - means_late) * inverse_late
    scaled_grad = frame_grad * gain_attn[None]
    sums = jnp.concatenate(
        [
            jnp.sum(scaled_grad, -1),
            jnp.sum(scaled_grad * own_scaled, -1),
            time_grad[0],
            vectors_late.reshape(-1),
        ]
    )[None]
    sums = sums + swap(sums, "tensor", 1)
    sums = sums + swap(sums, "tensor", 2)
    sums, first_got, second_got = meeting(sums, first_got, second_got)
    second_keep, second_got = halve(added(second_keep, second_got).astype(BF16), 2)
    plain = sums[0, :local_rows, None] / model_width
    cross = sums[0, local_rows : 2 * local_rows, None] / model_width
    vectors = own_cols(sums[0, 2 * local_rows :].reshape(5, model_width))
    attend_full = ordered(*[after(one_parts, from_next)[i] for i in (0, 2, 1, 3)], 0)
    d_frames = own_cols(attend_full).astype(F32) + inverse_late * (
        scaled_grad - plain - own_scaled * cross
    )
    d_gain_attn = jnp.sum(frame_grad * own_scaled, 0) + vectors[0] * own_cols(scaled_time)[0]
    d_bias_attn = jnp.sum(frame_grad, 0) + vectors[0]
    down_away, down_own, down_low = down_parts(after(hidden_a, last_far), hidden_b, w_down)
    branch_got, _, branch_far = scatter_near(down_away, down_low)
    block_rows = (
        residual_two + down_own + branch_got[:share].astype(F32) + branch_far.astype(F32)
    ).astype(BF16)
    block_cols = rows_to_cols(
        *[
            lax.dynamic_slice_in_dim(block_rows, (place ^ r) * local_width, local_width, 1)
            for r in range(4)
        ],
        from_next,
    )
    block_out = jnp.concatenate([row_block(block_cols, place ^ b) for b in range(4)], 0)

    time_column = time_normed.T

    normed_pair = (one_own_half, normed_got)
    grad_down = halve_end(down_keep, down_got, 3)
    raw_pair = (raw[: 3 * head_cols], raw_got[: 3 * head_cols])
    time_got = raw_got[3 * head_cols : 3 * head_cols + 2, :head_cols].astype(F32)
    time_both = (time_grads + time_got).reshape(1, 2 * head_cols)
    own_time_rows = lax.dynamic_index_in_dim(
        time_column.reshape(count // 2, 2, -1), column, 1, False
    ).reshape(-1, 1)
    outer = own_time_rows * jnp.concatenate([jnp.zeros((1, head_cols), F32), time_both], 1)
    blocks = sum(
        jnp.einsum("dn,fn->df", r, c, preferred_element_type=F32)
        for r, c in zip(normed_pair, raw_pair)
    )
    heads_keep, heads_got = halve(
        (blocks + outer).astype(BF16).reshape(count // 2, rows, 3 * head_cols), 1
    )
    heads_got, got_a = meeting(heads_got, got_a)
    heads_next = added(heads_keep, heads_got).astype(BF16)
    got_b = swap(after(send_b, got_a), "seq", 1)
    left_keep, left_got = halve(added(keep_a, got_a).astype(BF16), 1)
    heads_sum = halve_all(heads_next, 2)
    got_b, second_got = meeting(got_b, second_got)
    last_next = added(*halve(added(keep_b, got_b).astype(BF16), 1))
    first, second = halve_end(first_keep, first_got, 3), halve_end(second_keep, second_got, 3)
    units = first.shape[1] // 2
    grad_gate_w = jnp.concatenate([first[:, :units], second[:, :units]], 1)
    grad_up_w = jnp.concatenate([first[:, units:], second[:, units:]], 1)
    small = jnp.stack(
        [d_gain_attn, d_bias_attn, vectors[3], vectors[4], vectors[1], vectors[2]]
    ).reshape(6, devices, -1).transpose(1, 0, 2)
    small = small.reshape(count // 2, 2, 6, -1).transpose(1, 0, 2, 3).reshape(count, 6, -1)
    small = after(small, heads_next)
    bit = 1
    while small.shape[0] > 2:
        small = added(*halve(small, bit))
        bit += 1
    small = added(*halve(small, 0))[0]
    left, right = halve_end(left_keep, left_got, 2), halve_all(last_next, 2)
    part, rows = head_cols // count, model_width // count
    grad_c_query = left[:, :head_cols]
    grad_c_key, grad_c_value = left[: rows // 2, head_cols:], left[rows // 2 :, head_cols:]
    grad_c_out = jnp.concatenate([right[:part], right[part : 2 * part]], 1)
    grad_w_out = jnp.concatenate([right[2 * part : 3 * part], right[3 * part :]], 1)
    grad_w_query, grad_w_key, grad_w_value = (
        heads_sum[:, i * head_cols : (i + 1) * head_cols] for i in range(3)
    )
    return (
        block_out,
        d_frames,
        small[0],
        small[1],
        small[2],
        small[3],
        small[4],
        small[5],
        grad_w_query,
        grad_w_key,
        grad_w_value,
        grad_w_out,
        grad_c_query,
        grad_c_key,
        grad_c_value,
        grad_c_out,
        grad_gate_w,
        grad_up_w,
        grad_down,
    )


def solution(mesh):
    return jax.shard_map(
        per_device,
        mesh=mesh,
        in_specs=(
            P("seq", "tensor"),
            P(),
            P(),
            P(),
            P("tensor"),
            P("tensor"),
            P("tensor"),
            P("tensor"),
            P("tensor"),
            P("tensor"),
            P(None, "tensor"),
            P(None, "tensor"),
            P(None, "tensor"),
            P("tensor", None),
            P(None, "tensor"),
            P(None, "tensor"),
            P(None, "tensor"),
            P("tensor", None),
            P(None, "tensor"),
            P(None, "tensor"),
            P("tensor", None),
            P("seq", "tensor"),
        ),
        out_specs=(
            P("seq", "tensor"),
            P("seq", "tensor"),
            P(("tensor", "seq")),
            P(("tensor", "seq")),
            P(("tensor", "seq")),
            P(("tensor", "seq")),
            P(("tensor", "seq")),
            P(("tensor", "seq")),
            P("seq", "tensor"),
            P("seq", "tensor"),
            P("seq", "tensor"),
            P(("tensor", "seq"), None),
            P("seq", "tensor"),
            P("seq", "tensor"),
            P("seq", "tensor"),
            P(("tensor", "seq"), None),
            P("seq", "tensor"),
            P("seq", "tensor"),
            P(("tensor", "seq"), None),
        ),
        check_vma=False,
    )
```

```python
import functools
import math

import jax
import jax.numpy as jnp
from jax import lax
from jax.experimental import pallas as pl
from jax.experimental.pallas import tpu as pltpu
from jax.sharding import PartitionSpec as P

HEAD_SIZE = 64
ROW_MIN = 2048
TILE = 256
BF16 = jnp.bfloat16
F32 = jnp.float32


def meeting(*values):
    return lax.optimization_barrier(values)


def after(value, token):
    return lax.optimization_barrier((value, token))[0]


def swap(value, axis, by):
    return lax.ppermute(value, axis, [(i, i ^ by) for i in range(lax.axis_size(axis))])


def shift(value, axis, by):
    peers = lax.axis_size(axis)
    pairs = [(i, i + by) for i in range(peers) if 0 <= i + by < peers]
    return lax.ppermute(value, axis, pairs)


def tensor_place():
    place = lax.axis_index("tensor")
    return place // 2, place % 2


def ordered(own, far, mate, far_mate, axis):
    side, core = tensor_place()
    near = (jnp.where(core == 0, own, mate), jnp.where(core == 0, mate, own))
    away = (jnp.where(core == 0, far, far_mate), jnp.where(core == 0, far_mate, far))
    low = [jnp.where(side == 0, n, a) for n, a in zip(near, away)]
    high = [jnp.where(side == 0, a, n) for n, a in zip(near, away)]
    return jnp.concatenate(low + high, axis)


def gather_near(own):
    far = swap(own, "tensor", 2)
    return own, swap(own, "tensor", 1), far, swap(far, "tensor", 1)


def gather_staged(own, first, second):
    far = swap(after(own, first), "tensor", 2)
    far, late = after((far, own), second)
    return own, swap(late, "tensor", 1), far, swap(far, "tensor", 1)


def gather(own, axis):
    own, mate, far, far_mate = gather_near(own)
    return ordered(own, far, mate, far_mate, axis)


def scatter_near(away, low):
    got = swap(away, "tensor", 1)
    total = (low.astype(F32) + got[low.shape[0] :].astype(F32)).astype(BF16)
    return got, total, swap(total, "tensor", 2)


def rows_to_cols(own, mate, far, far_mate, later):
    width = own.shape[1]
    got = after(swap(jnp.concatenate([far, far_mate], 1), "tensor", 2), later)
    other = swap(jnp.concatenate([mate, got[:, width:]], 0), "tensor", 1)
    size = own.shape[0]
    return jnp.concatenate([own, other[:size], got[:, :width], other[size:]], 0)


def quarters(value, axis):
    return jnp.split(value, 4, axis)


def own_blocks(near):
    return jnp.concatenate([quarters(value, 1)[r] for r, value in enumerate(near)], 0)


def trade(value, start, done):
    return after(swap(after(value, start), "seq", 1), done)


def halve(blocks, bit):
    count, rows, cols = blocks.shape
    side = (lax.axis_index("seq") >> bit) % 2
    parts = blocks.reshape(count // 2, 2, rows, cols)
    send = lax.dynamic_index_in_dim(parts, 1 - side, 1, False)
    keep = lax.dynamic_index_in_dim(parts, side, 1, False)
    return keep, swap(send, "seq", 1 << bit)


def added(keep, got):
    return keep.astype(F32) + got.astype(F32)


def halve_all(blocks, bit):
    while blocks.shape[0] > 1:
        blocks = added(*halve(blocks.astype(BF16), bit))
        bit += 1
    return blocks[0].astype(F32)


def halve_end(keep, got, bit):
    return halve_all(added(keep, got), bit)


def frame_clip_labels(segment, row_length):
    frame_index = jnp.arange(segment.shape[0], dtype=jnp.int32)
    border = (frame_index % row_length == 0) | (segment != jnp.roll(segment, 1))
    clip_starts = lax.cummax(jnp.where(border, frame_index, 0), axis=0)
    return (clip_starts, (frame_index - clip_starts + 1).astype(jnp.float32))


def tile_ranges(q_labels, key_labels):
    q = q_labels.reshape(-1, TILE)
    k = key_labels.reshape(-1, TILE)
    meets = (k[None, :, 0] <= q[:, None, -1]) & (k[None, :, -1] >= q[:, None, 0])
    index = jnp.arange(k.shape[0], dtype=jnp.int32)[None]
    low = jnp.min(jnp.where(meets, index, k.shape[0]), 1)
    high = jnp.max(jnp.where(meets, index + 1, 0), 1)
    return jnp.stack([low, high], 1).reshape(-1)

def head_rows(g):
    return slice(g * HEAD_SIZE, (g + 1) * HEAD_SIZE)

def fill_natural(dest, refs, which):
    size = refs[0].shape[2]
    for part, ref in enumerate(refs):
        dest[part * size : (part + 1) * size, :] = ref[which].T


def fill_tiles(dest, refs, which):
    pieces = refs[0].shape[2] // TILE
    for part, ref in enumerate(refs):
        for piece in range(pieces):
            dest[part * pieces + piece] = ref[which, :, piece * TILE : (piece + 1) * TILE]


def relative(place, r, size):
    return pl.ds(pl.multiple_of((place ^ r) * size, size), size)


def absorb(state, start, stop, base, q, cols, lab, klab, keys, vals):
    group = q.shape[0] // HEAD_SIZE

    def step(j, state):
        seen = klab[pl.ds(pl.multiple_of(j * TILE, TILE), TILE), :] == lab
        at = pl.ds(pl.multiple_of((j - base) * TILE, TILE), TILE)
        fresh = []
        for g in range(group):
            top, total, acc = state[3 * g : 3 * g + 3]
            s = dot_nn(keys[at, head_rows(g)], q[head_rows(g), cols])
            s = jnp.where(seen, s, -1e30)
            new = jnp.maximum(top, jnp.max(s, 0, keepdims=True))
            fade = jnp.exp(top - new)
            p = jnp.exp(s - new)
            total = total * fade + jnp.sum(p, 0, keepdims=True)
            acc = acc * fade + dot_nn(vals[j - base, head_rows(g), :], p.astype(BF16))
            fresh += [new, total, acc]
        return tuple(fresh)

    return lax.fori_loop(start, stop, step, tuple(state))


def near_body(span, q, kv, tk, tv, qlab, klab, tops, totals, mix, keys, vals):
    rows, size = q.shape
    pieces = size // TILE
    fill_natural(keys, (kv,), 0)
    fill_tiles(vals, (kv,), 1)
    for tile in range(pieces):
        cols = slice(tile * TILE, (tile + 1) * TILE)
        state = []
        for g in range(rows // HEAD_SIZE):
            part = q[head_rows(g), cols].astype(F32)
            top = jnp.sum(part * tk[head_rows(g), :], 0, keepdims=True)
            state += [
                top,
                jnp.ones_like(top),
                jnp.broadcast_to(tv[head_rows(g), :], (HEAD_SIZE, TILE)),
            ]
        start = jnp.maximum(span[2 * tile], pieces)
        stop = jnp.minimum(span[2 * tile + 1], 2 * pieces)
        state = absorb(state, start, stop, pieces, q, cols, qlab[:, cols], klab, keys, vals)
        for g in range(rows // HEAD_SIZE):
            tops[g : g + 1, cols], totals[g : g + 1, cols], mix[head_rows(g), cols] = state[
                3 * g : 3 * g + 3
            ]


def far_body(span, q, kv0, kv2, qlab, klab, w_out, tops, totals, mix,
             out, lse, away, own, low, keys0, keys2, vals0, vals2):
    rows, size = q.shape
    pieces = size // TILE
    for kv, keys, vals in ((kv0, keys0, vals0), (kv2, keys2, vals2)):
        fill_natural(keys, (kv,), 0)
        fill_tiles(vals, (kv,), 1)
    for tile in range(pieces):
        cols = slice(tile * TILE, (tile + 1) * TILE)
        lab = qlab[:, cols]
        state = []
        for g in range(rows // HEAD_SIZE):
            state += [tops[g : g + 1, cols], totals[g : g + 1, cols], mix[head_rows(g), cols]]
        stop = jnp.minimum(span[2 * tile + 1], pieces)
        state = absorb(state, span[2 * tile], stop, 0, q, cols, lab, klab, keys0, vals0)
        start = jnp.maximum(span[2 * tile], 2 * pieces)
        state = absorb(
            state, start, span[2 * tile + 1], 2 * pieces, q, cols, lab, klab, keys2, vals2
        )
        for g in range(rows // HEAD_SIZE):
            top, total, acc = state[3 * g : 3 * g + 3]
            out[head_rows(g), cols] = (acc / total).astype(BF16)
            lse[g : g + 1, cols] = top + jnp.log(total)
    place = span[2 * pieces]
    share = own.shape[0]

    def sent(r):
        return dot_tn(out[:, relative(place, r, share)], w_out[...])

    away[:share, :] = sent(1).astype(BF16)
    away[share:, :] = sent(3).astype(BF16)
    low[...] = sent(2).astype(BF16)
    own[...] = sent(0)


def backward_body(span, q, kv0, kv1, kv2, tk, tv, qlab, klab, w_out, out, lse,
                  g0, g1, g2, g3, dq, to_prev, kept, to_next, times,
                  og, keys, vals, tkeys, ak, av, dtk, dtv):
    rows, size = q.shape
    group = rows // HEAD_SIZE
    pieces = size // TILE
    share = g0.shape[0]
    for r, ref in enumerate((g0, g1, g2, g3)):
        og[:, relative(span[2 * pieces], r, share)] = dot_nt(w_out[...], ref[...]).astype(BF16)
    fill_natural(keys, (kv0, kv1, kv2), 0)
    fill_natural(vals, (kv0, kv1, kv2), 1)
    fill_tiles(tkeys, (kv0, kv1, kv2), 0)
    ak[...] = jnp.zeros_like(ak)
    av[...] = jnp.zeros_like(av)
    for tile in range(pieces):
        cols = slice(tile * TILE, (tile + 1) * TILE)
        lab = qlab[:, cols]
        state, norms, deltas = [], [], []
        for g in range(group):
            hr = head_rows(g)
            qf = q[hr, cols].astype(F32)
            gf = og[hr, cols].astype(F32)
            norm = lse[g : g + 1, cols]
            delta = jnp.sum(gf * out[hr, cols].astype(F32), 0, keepdims=True)
            pt = jnp.exp(jnp.sum(qf * tk[hr, :], 0, keepdims=True) - norm)
            st = pt * (jnp.sum(gf * tv[hr, :], 0, keepdims=True) - delta)
            gk = jnp.sum(qf * st, 1, keepdims=True)
            gv = jnp.sum(gf * pt, 1, keepdims=True)
            if tile == 0:
                dtk[hr, :] = gk
                dtv[hr, :] = gv
            else:
                dtk[hr, :] += gk
                dtv[hr, :] += gv
            state.append(tk[hr, :] * st)
            norms.append(norm)
            deltas.append(delta)

        def step(j, state):
            start = pl.multiple_of(j * TILE, TILE)
            seen = klab[pl.ds(start, TILE), :] == lab
            fresh = []
            for g in range(group):
                hr = head_rows(g)
                s = dot_nn(keys[pl.ds(start, TILE), hr], q[hr, cols])
                p = jnp.exp(jnp.where(seen, s, -1e30) - norms[g])
                m = dot_nn(vals[pl.ds(start, TILE), hr], og[hr, cols])
                ds = (p * (m - deltas[g])).astype(BF16)
                av[j, hr, :] += dot_nt(og[hr, cols], p.astype(BF16))
                ak[j, hr, :] += dot_nt(q[hr, cols], ds)
                fresh.append(state[g] + dot_nn(tkeys[j, hr, :], ds))
            return tuple(fresh)

        state = lax.fori_loop(span[2 * tile], span[2 * tile + 1], step, tuple(state))
        for g in range(group):
            dq[head_rows(g), cols] = state[g]
    for at, column in ((0, dtk), (1, dtv)):
        spread = jnp.broadcast_to(column[...], (rows, 2 * HEAD_SIZE))
        times[at : at + 1, :] = spread.T[:1, :]
    for part, dest in enumerate((to_prev, kept, to_next)):
        for piece in range(pieces):
            at = slice(piece * TILE, (piece + 1) * TILE)
            dest[0, :, at] = ak[part * pieces + piece].astype(dest.dtype)
            dest[1, :, at] = av[part * pieces + piece].astype(dest.dtype)


def attend_near(span, q, kv, tk, tv, qlab, klab):
    cols, size = q.shape
    wide = lambda *dims: jax.ShapeDtypeStruct(dims, F32)
    vmem = pl.BlockSpec(memory_space=pltpu.VMEM)
    return pl.pallas_call(
        near_body,
        in_specs=[pl.BlockSpec(memory_space=pltpu.SMEM)] + [vmem] * 6,
        out_specs=[vmem] * 3,
        out_shape=[wide(cols // HEAD_SIZE, size), wide(cols // HEAD_SIZE, size), wide(cols, size)],
        scratch_shapes=[pltpu.VMEM((size, cols), BF16), pltpu.VMEM((size // TILE, cols, TILE), BF16)],
        name="attend_near", cost_estimate=FREE,
    )(span, q, kv, tk, tv, qlab, klab)


def attend_far(span, q, behind, ahead, qlab, klab, w_out, state):
    cols, size = q.shape
    share, width = size // 4, w_out.shape[1]
    low = lambda *dims: jax.ShapeDtypeStruct(dims, BF16)
    wide = lambda *dims: jax.ShapeDtypeStruct(dims, F32)
    vmem = pl.BlockSpec(memory_space=pltpu.VMEM)
    keys = pltpu.VMEM((size, cols), BF16)
    vals = pltpu.VMEM((size // TILE, cols, TILE), BF16)
    return pl.pallas_call(
        far_body,
        in_specs=[pl.BlockSpec(memory_space=pltpu.SMEM)] + [vmem] * 9,
        out_specs=[vmem] * 5,
        out_shape=[low(cols, size), wide(cols // HEAD_SIZE, size), low(2 * share, width),
                   wide(share, width), low(share, width)],
        scratch_shapes=[keys, keys, vals, vals],
        name="attend_far", cost_estimate=FREE,
    )(span, q, behind, ahead, qlab, klab, w_out, *state)


def attend_back(span, q, kvs, tk, tv, qlab, klab, w_out, out, lse, grads):
    cols, size = q.shape
    tiles = 3 * size // TILE
    low = lambda *dims: jax.ShapeDtypeStruct(dims, BF16)
    wide = lambda *dims: jax.ShapeDtypeStruct(dims, F32)
    vmem = pl.BlockSpec(memory_space=pltpu.VMEM)
    return pl.pallas_call(
        backward_body,
        in_specs=[pl.BlockSpec(memory_space=pltpu.SMEM)] + [vmem] * 15,
        out_specs=[vmem] * 5,
        out_shape=[wide(cols, size), low(2, cols, size), wide(2, cols, size), low(2, cols, size),
                   wide(2, cols)],
        scratch_shapes=[pltpu.VMEM((cols, size), BF16), pltpu.VMEM((3 * size, cols), BF16),
                        pltpu.VMEM((3 * size, cols), BF16), pltpu.VMEM((tiles, cols, TILE), BF16),
                        pltpu.VMEM((tiles, cols, TILE), F32), pltpu.VMEM((tiles, cols, TILE), F32),
                        pltpu.VMEM((cols, 1), F32), pltpu.VMEM((cols, 1), F32)],
        name="attend_back", cost_estimate=FREE,
    )(span, q, *kvs, tk, tv, qlab, klab, w_out, out, lse, *grads)


def tail_body(place, dq, kept, ahead, behind, cosine, sine, wq, wk, wv, times,
              raw, away, own, low, flipped):
    part, size = dq.shape
    half = HEAD_SIZE // 2

    def returned(block, base, scale):
        for h in range(part // HEAD_SIZE):
            a = block[h * HEAD_SIZE : h * HEAD_SIZE + half, :]
            b = block[h * HEAD_SIZE + half : (h + 1) * HEAD_SIZE, :]
            at = base + h * HEAD_SIZE
            raw[at : at + half, :] = ((a * cosine[...] + b * sine[...]) * scale).astype(BF16)
            raw[at + half : at + HEAD_SIZE, :] = (
                (b * cosine[...] - a * sine[...]) * scale
            ).astype(BF16)

    def whole(index):
        return kept[index] + ahead[index].astype(F32) + behind[index].astype(F32)

    returned(dq[...], 0, 1.0 / math.sqrt(HEAD_SIZE))
    returned(whole(0), part, 1.0)
    raw[2 * part : 3 * part, :] = whole(1).astype(BF16)
    raw[3 * part :, :] = jnp.zeros((16, size), BF16)
    raw[3 * part : 3 * part + 2, :part] = times[...].astype(BF16)
    flipped[...] = raw[: 3 * part, :].T

    def sent(r):
        at = relative(place[0], r, part)
        return sum(
            dot_nt(flipped[:, i * part : (i + 1) * part], weight[at, :])
            for i, weight in enumerate((wq, wk, wv))
        )

    away[:size, :] = sent(1).astype(BF16)
    away[size:, :] = sent(3).astype(BF16)
    low[...] = sent(2).astype(BF16)
    own[...] = sent(0)


def tail(place, dq, kept, ahead, behind, tables, wq, wk, wv, times):
    part, size = dq.shape
    low = lambda *dims: jax.ShapeDtypeStruct(dims, BF16)
    vmem = pl.BlockSpec(memory_space=pltpu.VMEM)
    return pl.pallas_call(
        tail_body,
        in_specs=[pl.BlockSpec(memory_space=pltpu.SMEM)] + [vmem] * 10,
        out_specs=[vmem] * 4,
        out_shape=[low(3 * part + 16, size), low(2 * size, part), jax.ShapeDtypeStruct((size, part), F32),
                   low(size, part)],
        scratch_shapes=[pltpu.VMEM((size, 3 * part), BF16)],
        name="tail", cost_estimate=FREE,
    )(place, dq, kept, ahead, behind, *tables, wq, wk, wv, times)


def rotary_tables(frame_positions):
    half_dim = HEAD_SIZE // 2
    frequency = jnp.exp(jnp.arange(half_dim, dtype=jnp.float32) * (-math.log(10000.0) / half_dim))
    angles = frequency[:, None] * frame_positions[None, :]
    return (jnp.cos(angles), jnp.sin(angles))


def rotate(rows, tables, sign=1.0):
    count, size = rows.shape
    halves = rows.reshape(count // HEAD_SIZE, 2, HEAD_SIZE // 2, size)
    cosine, sine = tables[0][None], tables[1][None] * sign
    first = halves[:, 0] * cosine - halves[:, 1] * sine
    second = halves[:, 1] * cosine + halves[:, 0] * sine
    return jnp.stack([first, second], 1).reshape(count, size)


def product(left, right):
    return jnp.dot(left, right, preferred_element_type=jnp.float32)


def inner_rows(left, right):
    return jnp.einsum("nd,nf->df", left, right, preferred_element_type=jnp.float32)


def back_project(gradient, weight):
    return jnp.einsum("nf,df->nd", gradient, weight, preferred_element_type=jnp.float32)


def by_feature(left, right):
    return jnp.einsum("nd,df->fn", left, right, preferred_element_type=jnp.float32)


def columns(weight, start, size):
    return lax.dynamic_slice_in_dim(weight, start, size, 1)


def rows_of(weight, start, size):
    return lax.dynamic_slice_in_dim(weight, start, size, 0)


def normalize(value_rows):
    means = jnp.mean(value_rows, -1, keepdims=True)
    centred = value_rows - means
    inverse = lax.rsqrt(jnp.mean(centred * centred, -1, keepdims=True) + 1e-05)
    return centred * inverse, inverse


def norm_backward(gradient, scaled, inverse, norm_gain):
    scaled_grad = gradient * norm_gain
    plain = jnp.mean(scaled_grad, -1, keepdims=True)
    cross = jnp.mean(scaled_grad * scaled, -1, keepdims=True)
    return inverse * (scaled_grad - plain - scaled * cross)


FREE = pl.CostEstimate(flops=1, transcendentals=0, bytes_accessed=1)


def dot_nn(left, right):
    return lax.dot_general(left, right, (((1,), (0,)), ((), ())), preferred_element_type=F32)


def dot_nt(left, right):
    return lax.dot_general(left, right, (((1,), (1,)), ((), ())), preferred_element_type=F32)


def dot_tn(left, right):
    return lax.dot_general(left, right, (((0,), (0,)), ((), ())), preferred_element_type=F32)


def head_weights(query, key, lanes, which):
    mine = jnp.where(lanes == which, query, jnp.zeros_like(query))
    scores = dot_nt(mine, key) * (1.0 / math.sqrt(HEAD_SIZE))
    weights = jnp.exp(scores - jnp.max(scores, -1, keepdims=True))
    return weights / jnp.sum(weights, -1, keepdims=True)


def pair_cols(refs, p, rows):
    ref = refs[p * 2 * HEAD_SIZE // refs[0].shape[1]]
    start = p * 2 * HEAD_SIZE % refs[0].shape[1]
    return ref[rows, start : start + 2 * HEAD_SIZE]


def cross_forward_body(width_block, place, rows, own, got, far, norms, q0, q1, q2, q3,
                       c0, c1, c2, c3, o0, o1, o2, o3,
                       front, queries, first, second, normed_three,
                       flip_own, flip_away):
    width = rows.shape[1]
    kv = (c0, c1, c2, c3)
    context_rows = c0.shape[0] // 2
    key_rows, value_rows = slice(0, context_rows), slice(context_rows, 2 * context_rows)
    lanes = lax.broadcasted_iota(jnp.int32, (rows.shape[0], 2 * HEAD_SIZE), 1) // HEAD_SIZE
    residual = (
        rows[...].astype(F32) + own[...] + got[...].astype(F32) + far[...].astype(F32)
    )
    first[...] = residual
    scaled, _ = normalize(residual)
    low = (scaled * norms[2:3, :] + norms[3:4, :]).astype(BF16)
    front[:, :width] = low
    part = width // 4
    for b, ref in enumerate((q0, q1, q2, q3)):
        queries[:, b * part : (b + 1) * part] = dot_nn(low, ref[...]).astype(BF16)
    for p in range(width // (2 * HEAD_SIZE)):
        cols = slice(p * 2 * HEAD_SIZE, (p + 1) * 2 * HEAD_SIZE)
        q, k, v = queries[:, cols], pair_cols(kv, p, key_rows), pair_cols(kv, p, value_rows)
        mixed = [dot_nn(head_weights(q, k, lanes, g).astype(BF16), v) for g in (0, 1)]
        front[:, width + cols.start : width + cols.stop] = jnp.where(lanes == 0, mixed[0], mixed[1]).astype(BF16)
    for b, ref in enumerate((o0, o1, o2, o3)):
        residual = residual + dot_nn(front[:, width + b * part : width + (b + 1) * part], ref[...])
    second[...] = residual
    scaled, _ = normalize(residual)
    low = (scaled * norms[4:5, :] + norms[5:6, :]).astype(BF16)
    normed_three[...] = low
    deal_rows(low.T, width_block, place[0], flip_own, flip_away)


def cross_forward(devices, place, rows, own, got, far, norms, query_parts, kv_parts, out_parts):
    size, width = rows.shape
    low = jax.ShapeDtypeStruct(rows.shape, BF16)
    both = jax.ShapeDtypeStruct((size, 2 * width), BF16)
    wide = jax.ShapeDtypeStruct(rows.shape, F32)
    flip = jax.ShapeDtypeStruct((width // 2, size), BF16)
    vmem = pl.BlockSpec(memory_space=pltpu.VMEM)
    block = pl.BlockSpec((size, width), lambda i: (0, 0))
    return pl.pallas_call(
        functools.partial(cross_forward_body, width // devices),
        grid=(1,),
        in_specs=[pl.BlockSpec(memory_space=pltpu.SMEM)] + [block] * 4 + [vmem] * 13,
        out_shape=[both, low, wide, wide, low, flip, flip],
        cost_estimate=FREE, name="cross",
    )(place, rows, own, got, far, norms, *query_parts, *kv_parts, *out_parts)


def deal_rows(rows, size, column, own, away):
    for b in range(rows.shape[0] // (2 * size)):
        at = slice(b * size, (b + 1) * size)
        even = rows[2 * b * size : (2 * b + 1) * size, :]
        odd = rows[(2 * b + 1) * size : (2 * b + 2) * size, :]

        @pl.when(column == 0)
        def _():
            own[at, :] = even
            away[at, :] = odd

        @pl.when(column != 0)
        def _():
            own[at, :] = odd
            away[at, :] = even


def ffn_part(normed, grad, gate_w, up_w, down_w, hidden, hid_own, hid_away, gate_grad, lifted_grad,
             unit_block, column):
    gate = dot_nn(normed, gate_w[...])
    lifted = dot_nn(normed, up_w[...])
    back = dot_nt(grad, down_w[...]).astype(BF16).astype(F32)
    sig = jax.nn.sigmoid(gate)
    swish = gate * sig
    made = (swish * lifted).astype(BF16)
    hidden[...] = made
    deal_rows(made.T, unit_block, column, hid_own, hid_away)
    gg = (back * lifted * sig * (1.0 + gate * (1.0 - sig))).astype(BF16)
    lg = (back * swish).astype(BF16)
    gate_grad[...] = gg
    lifted_grad[...] = lg
    return dot_nt(gg, gate_w[...]) + dot_nt(lg, up_w[...])


def ffn_first_body(unit_block, place, n0, n1, n2, n3, g0, g1, g2, g3, gate_w, up_w, down_w,
                   hidden, hid_own, hid_away, gate_grad, lifted_grad, normed, grad, grad_pair,
                   total):
    share, part = n0.shape[0], g0.shape[2]
    for b, ref in enumerate((n0, n1, n2, n3)):
        normed[b * share : (b + 1) * share, :] = ref[...]
    for c, ref in enumerate((g0, g1, g2, g3)):
        for b in range(4):
            rows, cols = relative(place[1], b, share), relative(place[1], c, part)
            grad[b * share : (b + 1) * share, cols] = ref[0, rows, :]
            grad_pair[b * share : (b + 1) * share, cols] = ref[1, rows, :]
    total[...] = ffn_part(
        normed[...], grad[...], gate_w, up_w, down_w, hidden, hid_own, hid_away, gate_grad,
        lifted_grad, unit_block, place[0],
    )


def ffn_second_body(unit_block, place, normed, grad, total, gate_w, up_w, down_w,
                    hidden, hid_own, hid_away, gate_grad, lifted_grad, away, own, low):
    share = own.shape[0]
    found = total[...] + ffn_part(
        normed[...], grad[...], gate_w, up_w, down_w, hidden, hid_own, hid_away, gate_grad,
        lifted_grad, unit_block, place[0],
    )
    own[...] = found[:share, :]
    low[...] = found[2 * share : 3 * share, :].astype(BF16)
    away[:share, :] = found[share : 2 * share, :].astype(BF16)
    away[share:, :] = found[3 * share :, :].astype(BF16)


def ffn(devices, place, half, inputs, gate_w, up_w, down_w):
    share = inputs[0].shape[0] if half == 0 else inputs[0].shape[0] // 4
    width = inputs[0].shape[1]
    size, units = 4 * share, gate_w.shape[1]
    tile = units // 2
    low = lambda *dims: jax.ShapeDtypeStruct(dims, BF16)
    wide = lambda *dims: jax.ShapeDtypeStruct(dims, F32)
    vmem = pl.BlockSpec(memory_space=pltpu.VMEM)
    cols = pl.BlockSpec((width, tile), lambda i: (0, half))
    rows = pl.BlockSpec((tile, width), lambda i: (half, 0))
    made = [low(size, tile), low(tile // 2, size), low(tile // 2, size), low(size, tile),
            low(size, tile)]
    if half == 0:
        made += [low(size, width), low(size, width), low(size, width), wide(size, width)]
    else:
        made += [low(2 * share, width), wide(share, width), low(share, width)]
    return pl.pallas_call(
        functools.partial(ffn_second_body if half else ffn_first_body, units // devices),
        grid=(1,),
        in_specs=[pl.BlockSpec(memory_space=pltpu.SMEM)] + [vmem] * len(inputs)
        + [cols, cols, rows],
        out_specs=[vmem] * len(made),
        out_shape=made,
        cost_estimate=FREE, name="ffn",
    )(place, *inputs, gate_w, up_w, down_w)


def cross_backward_body(own, got, far, grad, first, second, norms, q0, q1, q2, q3,
                        c0, c1, c2, c3, o0, o1, o2, o3, queries,
                        back_rows, kv_grad, vectors, grad_one, crossed_grad):
    width = grad.shape[1]
    kv = (c0, c1, c2, c3)
    context_rows = c0.shape[0] // 2
    key_rows, value_rows = slice(0, context_rows), slice(context_rows, 2 * context_rows)
    part = width // 4
    lanes = lax.broadcasted_iota(jnp.int32, (grad.shape[0], 2 * HEAD_SIZE), 1) // HEAD_SIZE
    lane_k = lax.broadcasted_iota(jnp.int32, (context_rows, 2 * HEAD_SIZE), 1) // HEAD_SIZE
    scale = 1.0 / math.sqrt(HEAD_SIZE)
    arrived = own[...] + got[...].astype(F32) + far[...].astype(F32)
    scaled, inverse = normalize(second[...])
    vectors[0:1, :] = jnp.sum(arrived * scaled, 0, keepdims=True)
    vectors[1:2, :] = jnp.sum(arrived, 0, keepdims=True)
    two = grad[...].astype(F32) + norm_backward(arrived, scaled, inverse, norms[4:5, :])
    low = two.astype(BF16)
    back_rows[:, :width] = low
    for b, ref in enumerate((o0, o1, o2, o3)):
        crossed_grad[:, b * part : (b + 1) * part] = dot_nt(low, ref[...]).astype(BF16)
    for p in range(width // (2 * HEAD_SIZE)):
        cols = slice(p * 2 * HEAD_SIZE, (p + 1) * 2 * HEAD_SIZE)
        q, k, v = queries[:, cols], pair_cols(kv, p, key_rows), pair_cols(kv, p, value_rows)
        g_rows = crossed_grad[:, cols]
        found = []
        for g in (0, 1):
            probs = head_weights(q, k, lanes, g)
            change = dot_nt(jnp.where(lanes == g, g_rows, jnp.zeros_like(g_rows)), v)
            delta = jnp.sum(change * probs, -1, keepdims=True)
            ds = (probs * (change - delta)).astype(BF16)
            found.append((dot_nn(ds, k), dot_tn(ds, q), dot_tn(probs.astype(BF16), g_rows)))
        back_rows[:, width + cols.start : width + cols.stop] = (
            jnp.where(lanes == 0, found[0][0], found[1][0]) * scale
        ).astype(BF16)
        kv_grad[:context_rows, cols] = (
            jnp.where(lane_k == 0, found[0][1], found[1][1]) * scale
        ).astype(BF16)
        kv_grad[context_rows:, cols] = jnp.where(lane_k == 0, found[0][2], found[1][2]).astype(
            BF16
        )
    back = jnp.zeros(grad.shape, F32)
    for b, ref in enumerate((q0, q1, q2, q3)):
        back = back + dot_nt(back_rows[:, width + b * part : width + (b + 1) * part], ref[...])
    scaled, inverse = normalize(first[...])
    vectors[2:3, :] = jnp.sum(back * scaled, 0, keepdims=True)
    vectors[3:4, :] = jnp.sum(back, 0, keepdims=True)
    grad_one[...] = (two + norm_backward(back, scaled, inverse, norms[2:3, :])).astype(BF16)


def cross_backward(own, got, far, grad, first, second, norms, query_parts, kv_parts, out_parts,
                   queries):
    rows, width = own.shape
    low = lambda r: jax.ShapeDtypeStruct((r, width), BF16)
    block = pl.BlockSpec((rows, width), lambda i: (0, 0))
    return pl.pallas_call(
        cross_backward_body,
        grid=(1,),
        out_shape=[jax.ShapeDtypeStruct((rows, 2 * width), BF16), low(kv_parts[0].shape[0]),
                   jax.ShapeDtypeStruct((4, width), F32), low(rows)],
        in_specs=[block] * 6 + [pl.BlockSpec(memory_space=pltpu.VMEM)] * 14,
        scratch_shapes=[pltpu.VMEM((rows, width), BF16)],
        cost_estimate=FREE, name="cross_back",
    )(own, got, far, grad, first, second, norms, *query_parts, *kv_parts, *out_parts, queries)


def meet_rows_body(size, side, own_a, pair_a, own_b, pair_b, right, right_pair, keep, send):
    half = keep.shape[0] // 2
    for b, (own, pair) in enumerate(((own_a, pair_a), (own_b, pair_b))):
        made = (dot_nn(own[...], right[...]) + dot_nn(pair[...], right_pair[...])).astype(BF16)
        at = pl.ds(b * half, half)
        deal_rows(made, size, side[0], keep.at[at], send.at[at])


def meet_rows(size, side, lefts, rights):
    count, frames = lefts[0].shape
    width = rights[0].shape[1]
    tile = width // 3
    left = pl.BlockSpec((count, frames), lambda i: (0, 0))
    right = pl.BlockSpec((frames, tile), lambda i: (0, i))
    return pl.pallas_call(
        functools.partial(meet_rows_body, size),
        grid=(3,),
        in_specs=[pl.BlockSpec(memory_space=pltpu.SMEM)] + [left] * 4 + [right] * 2,
        out_specs=[pl.BlockSpec((count, tile), lambda i: (0, i))] * 2,
        out_shape=[jax.ShapeDtypeStruct((count, width), BF16)] * 2,
        name="meet_rows", cost_estimate=FREE,
    )(side, *lefts, *rights)


def meet_cols_body(size, side, p0, p1, p2, p3, *refs):
    own, pair = (jnp.concatenate([p[i] for p in (p0, p1, p2, p3)], 1) for i in (0, 1))
    *rights, keep, send = refs
    width = rights[0].shape[1]
    for at in range(len(rights) // 2):
        made = dot_nn(own, rights[2 * at][...]) + dot_nn(pair, rights[2 * at + 1][...])
        cols = pl.ds(at * width, width)
        deal_rows(made.astype(BF16), size, side[0], keep.at[:, cols], send.at[:, cols])


def meet_cols(size, side, near, rights):
    width = rights[0].shape[1] * (len(rights) // 2)
    half = jax.ShapeDtypeStruct((near[0].shape[1] // 2, width), BF16)
    vmem = pl.BlockSpec(memory_space=pltpu.VMEM)
    return pl.pallas_call(
        functools.partial(meet_cols_body, size),
        in_specs=[pl.BlockSpec(memory_space=pltpu.SMEM)] + [vmem] * (4 + len(rights)),
        out_shape=[half] * 2,
        name="meet_cols", cost_estimate=FREE,
    )(side, *near, *rights)


def down_body(first, second, down_w, away, own, low):
    share, units = own.shape[0], first.shape[1]

    def sent(r):
        at = slice(r * share, (r + 1) * share)
        return dot_nn(first[at, :], down_w[:units, :]) + dot_nn(second[at, :], down_w[units:, :])

    away[:share, :] = sent(1).astype(BF16)
    away[share:, :] = sent(3).astype(BF16)
    low[...] = sent(2).astype(BF16)
    own[...] = sent(0)


def down_parts(first, second, down_w):
    share, width = first.shape[0] // 4, down_w.shape[1]
    low = lambda *dims: jax.ShapeDtypeStruct(dims, BF16)
    return pl.pallas_call(
        down_body,
        out_shape=[low(2 * share, width), jax.ShapeDtypeStruct((share, width), F32),
                   low(share, width)],
        name="down", cost_estimate=FREE,
    )(first, second, down_w)


def bundle_body(devices, place, f02, f13, b02, b13, a0, a1, a2, a3, attended,
                context, kv, keep_a, send_a, keep_b, send_b):
    width = a0.shape[1]
    part, share = width // 4, a0.shape[0]

    def near(even, odd):
        return even[0], odd[0], even[1], odd[1]

    own = lambda rows: jnp.concatenate(
        [row[:, width + r * part : width + (r + 1) * part] for r, row in enumerate(rows)], 0
    )
    full = lambda rows: jnp.concatenate([row[:, :width] for row in rows], 0)
    fronts, backs = near(f02, f13), near(b02, b13)
    rows = width // devices
    small = part // devices
    half = width // 2

    def put(block, base, left, out):
        size = block.shape[0] // devices
        cols = slice(left, left + block.shape[1])
        low = block.astype(BF16)
        for d in range(0, devices, 2):
            at = slice(base, base + size)
            even, odd = low[d * size : (d + 1) * size, :], low[(d + 1) * size : (d + 2) * size, :]

            @pl.when(place[0] == 0)
            def _():
                out[0][d // 2, at, cols] = even
                out[1][d // 2, at, cols] = odd

            @pl.when(place[0] != 0)
            def _():
                out[0][d // 2, at, cols] = odd
                out[1][d // 2, at, cols] = even

    put(dot_tn(full(fronts), own(backs)), 0, 0, (keep_a, send_a))
    count = context.shape[0]
    put(dot_tn(context[...], kv[:count, :]), 0, part, (keep_a, send_a))
    put(dot_tn(context[...], kv[count:, :]), rows // 2, part, (keep_a, send_a))
    grads = dot_tn(own(fronts), full(backs))
    put(grads[:, :half], 0, 0, (keep_b, send_b))
    put(grads[:, half:], small, 0, (keep_b, send_b))
    grads = sum(
        dot_nn(attended[:, relative(place[1], r, share)], ref[...])
        for r, ref in enumerate((a0, a1, a2, a3))
    )
    put(grads[:, :half], 2 * small, 0, (keep_b, send_b))
    put(grads[:, half:], 3 * small, 0, (keep_b, send_b))


def bundle_grads(devices, place, fronts, backs, ones, attended, context, kv):
    width = ones[0].shape[1]
    vmem = pl.BlockSpec(memory_space=pltpu.VMEM)
    return pl.pallas_call(
        functools.partial(bundle_body, devices),
        in_specs=[pl.BlockSpec(memory_space=pltpu.SMEM)] + [vmem] * 11,
        out_specs=[vmem] * 4,
        out_shape=[jax.ShapeDtypeStruct((devices // 2, width // devices, width // 2), BF16)] * 4,
        name="bundle", cost_estimate=FREE,
    )(place, *fronts, *backs, *ones, attended, context, kv)


def front_body(width_block, place, x0, x1, x2, x3, g0, g1, g2, g3, cosine, sine, wq, wk, wv,
               time_row, context, ck, cv,
               queries, pair, rows, low, nrm_own, nrm_away, norms, means, inverses,
               time_scaled, time_low, time_keys, time_values, kv, wide):
    size, part = x0.shape
    for r, (x, g) in enumerate(((x0, g0), (x1, g1), (x2, g2), (x3, g3))):
        start = pl.multiple_of((place[0] ^ r) * part, 128)
        wide[:, pl.ds(start, part)] = x[...]
        norms[:, pl.ds(start, part)] = g[...]
    share = size // 4
    rows[...] = wide[pl.ds(pl.multiple_of(place[0] * share, share), share), :]
    values = wide[...].astype(F32)
    mean = jnp.mean(values, -1, keepdims=True)
    centred = values - mean
    inverse = lax.rsqrt(jnp.mean(centred * centred, -1, keepdims=True) + 1e-05)
    means[...] = mean
    inverses[...] = inverse
    normed = (centred * inverse * norms[0:1, :] + norms[1:2, :]).astype(BF16)
    low[...] = normed
    half = HEAD_SIZE // 2

    def turned(weight):
        return dot_nn(normed, weight[...]).T

    def rotated(block, dest, scale):
        for h in range(part // HEAD_SIZE):
            a = block[h * HEAD_SIZE : h * HEAD_SIZE + half, :]
            b = block[h * HEAD_SIZE + half : (h + 1) * HEAD_SIZE, :]
            dest[h * HEAD_SIZE : h * HEAD_SIZE + half, :] = (
                (a * cosine[...] - b * sine[...]) * scale
            ).astype(BF16)
            dest[h * HEAD_SIZE + half : (h + 1) * HEAD_SIZE, :] = (
                (b * cosine[...] + a * sine[...]) * scale
            ).astype(BF16)

    scaled, _ = normalize(jnp.broadcast_to(time_row[...].astype(F32), (8, 4 * part)))
    time_scaled[...] = scaled[:1, :]
    made = (scaled * norms[0:1, :] + norms[1:2, :]).astype(BF16)
    time_low[...] = made[:1, :].astype(F32)
    time_keys[...] = dot_nn(made, wk[...]).astype(BF16).astype(F32).T[:, :1]
    time_values[...] = dot_nn(made, wv[...]).astype(BF16).astype(F32).T[:, :1]
    count = context.shape[0]
    kv[:count, :] = dot_nn(context[...], ck[...]).astype(BF16)
    kv[count:, :] = dot_nn(context[...], cv[...]).astype(BF16)
    rotated(turned(wk), pair.at[0], 1.0)
    pair[1] = turned(wv).astype(BF16)
    rotated(turned(wq), queries, 1.0 / math.sqrt(HEAD_SIZE))
    deal_rows(normed.T, width_block, place[1], nrm_own, nrm_away)


def front(devices, place, parts, norm_parts, tables, wq, wk, wv, time_row, context, ck, cv):
    size, part = parts[0].shape
    width = 4 * part
    low = lambda *s: jax.ShapeDtypeStruct(s, BF16)
    wide = lambda *s: jax.ShapeDtypeStruct(s, F32)
    vmem = pl.BlockSpec(memory_space=pltpu.VMEM)
    return pl.pallas_call(
        functools.partial(front_body, width // devices),
        in_specs=[pl.BlockSpec(memory_space=pltpu.SMEM)] + [vmem] * 17,
        out_specs=[vmem] * 14,
        out_shape=[low(part, size), low(2, part, size), low(size // 4, width), low(size, width),
                   low(width // 2, size), low(width // 2, size), wide(6, width),
                   wide(size, 1), wide(size, 1), wide(1, width), wide(1, width), wide(part, 1),
                   wide(part, 1), low(2 * context.shape[0], part)],
        scratch_shapes=[pltpu.VMEM((size, width), BF16)],
        cost_estimate=FREE, name="front",
    )(place, *parts, *norm_parts, *tables, wq, wk, wv, time_row, context, ck, cv)


def per_device(
    frames,
    segment,
    time_token,
    context,
    gain_attn,
    bias_attn,
    gain_cross,
    bias_cross,
    gain_ffn,
    bias_ffn,
    w_query,
    w_key,
    w_value,
    w_out,
    c_query,
    c_key,
    c_value,
    c_out,
    w_gate,
    w_up,
    w_down,
    out_grad,
):
    local_rows = frames.shape[0]
    local_width = frames.shape[1]
    model_width = w_query.shape[0]
    head_cols = w_query.shape[1]
    heads = head_cols // HEAD_SIZE
    number_of_frames = lax.axis_size("seq") * local_rows
    row_length = min(max(ROW_MIN, 64 * lax.axis_size("seq")), number_of_frames)
    first_frame = lax.axis_index("seq") * local_rows
    own_start = lax.axis_index("tensor") * local_width

    def own_cols(value):
        return lax.dynamic_slice_in_dim(value, own_start, local_width, value.ndim - 1)

    place = lax.axis_index("tensor")
    share = local_rows // 4

    def row_block(value, index):
        return rows_of(value, index * share, share)

    column = lax.axis_index("seq") % 2
    frame_parts_near = gather_near(frames)
    norm_parts = gather_near(
        jnp.stack([gain_attn, bias_attn, gain_cross, bias_cross, gain_ffn, bias_ffn])
    )
    clip_starts, frame_positions = frame_clip_labels(segment, row_length)
    own_labels = lax.dynamic_slice_in_dim(clip_starts, first_frame, local_rows)
    own_positions = lax.dynamic_slice_in_dim(frame_positions, first_frame, local_rows)
    blanks = jnp.full((local_rows,), -1, jnp.int32)
    key_labels = lax.dynamic_slice_in_dim(
        jnp.concatenate([blanks, clip_starts, blanks]), first_frame, 3 * local_rows
    )
    spans = jnp.concatenate(
        [tile_ranges(own_labels, key_labels), place.astype(jnp.int32).reshape(1)]
    )
    places = jnp.stack([column, place]).astype(jnp.int32)
    label_row, label_column = own_labels[None, :], key_labels[:, None]
    row_index = first_frame // row_length
    time_row = lax.dynamic_slice_in_dim(time_token, row_index, 1, 0)
    row_context = lax.dynamic_slice_in_dim(context, row_index, 1, 0)[0]
    context_rows = row_context.shape[0]
    tables = rotary_tables(own_positions)
    score_scale = 1.0 / math.sqrt(HEAD_SIZE)
    all_heads = model_width // HEAD_SIZE

    (
        queries, both, frame_rows, frame_normed, one_own_half, one_away_half, norms, means_one,
        inverse_one, scaled_time, time_normed, time_keys, time_values, context_kv,
    ) = front(
        lax.axis_size("seq"), jnp.flip(places), frame_parts_near, norm_parts, tables, w_query,
        w_key, w_value, time_row, row_context, c_key, c_value,
    )
    both, out_pair = meeting(both, swap(after(out_grad, frame_parts_near[2]), "seq", 1))
    grad_both = jnp.stack([out_grad, out_pair])
    behind, ahead = shift(both, "seq", 1), shift(both, "seq", -1)
    query_late, out_late = after((c_query, c_out), (frame_parts_near[2], norm_parts[2]))
    query_far, out_far = swap(query_late, "tensor", 2), swap(out_late, "tensor", 2)
    state = attend_near(spans, queries, both, time_keys, time_values, label_row, label_column)
    behind, ahead, query_far, out_far, *state = meeting(
        behind, ahead, query_far, out_far, *state
    )
    query_own, out_own, context_late = after((c_query, c_out, context_kv), behind)
    weights_near = [
        swap(value, "tensor", 1) for value in (query_own, query_far, out_own, out_far)
    ]
    kv_far = swap(context_late, "tensor", 2)
    attended, log_totals, one_away, one_own, one_low = attend_far(
        spans, queries, behind, ahead, label_row, label_column, w_out, state
    )
    one_away, one_low, kv_far, *weights_near = meeting(one_away, one_low, kv_far, *weights_near)
    kv_both = jnp.concatenate([context_kv, kv_far], 0)
    kv_other = swap(kv_both, "tensor", 1)
    kv_rows = context_kv.shape[0]
    kv_parts = (context_kv, kv_other[:kv_rows], kv_far, kv_other[kv_rows:])
    query_parts = (c_query, weights_near[0], query_far, weights_near[1])
    out_parts = (c_out, weights_near[2], out_far, weights_near[3])
    one_got, _, one_far = scatter_near(one_away, one_low)
    (
        front_rows, cross_queries, residual_one, residual_two, normed_share, flip_own, flip_away,
    ) = cross_forward(
        lax.axis_size("seq"), places, frame_rows, one_own, one_got, one_far, norms,
        query_parts, kv_parts, out_parts,
    )
    grad_far = swap(after(grad_both, one_far), "tensor", 2)
    normed_share, normed_got, grad_far = meeting(
        normed_share, swap(after(one_away_half, one_low), "seq", 1), grad_far
    )
    grad_late, grad_far_late = after((grad_both, grad_far), normed_share)
    grad_mate, grad_far_mate = swap(grad_late, "tensor", 1), swap(grad_far_late, "tensor", 1)
    grad_parts = (grad_both, grad_mate, grad_far, grad_far_mate)
    three_parts = gather_near(normed_share)
    flip_got = swap(after(flip_away, normed_share), "seq", 1)
    front_far = swap(after(front_rows, three_parts[3]), "tensor", 2)
    devices = lax.axis_size("seq")
    (
        hidden_a, hidden_own_a, hidden_away_a, gate_a, lifted_a, normed_three, grad_near, grad_pair,
        ffn_total,
    ) = ffn(devices, places, 0, (*three_parts, *grad_parts), w_gate, w_up, w_down)
    ffn_total, flip_got = meeting(ffn_total, flip_got)
    flip_both = jnp.stack([flip_own, flip_got])
    flip_far = swap(flip_both, "tensor", 2)
    hidden_got_a, gate_got_a = swap(hidden_away_a, "seq", 1), swap(gate_a, "seq", 1)
    hidden_b, hidden_own_b, hidden_away_b, gate_b, lifted_b, three_away, three_own, three_low = ffn(
        devices, places, 1, (normed_three, grad_near, ffn_total), w_gate, w_up, w_down
    )
    three_away, three_low, flip_far, front_far, hidden_got_a = meeting(
        three_away, three_low, flip_far, front_far, hidden_got_a
    )
    three_got, _, three_far = scatter_near(three_away, three_low)
    hidden_got_b = swap(after(hidden_away_b, three_low), "seq", 1)
    lifted_got_a = swap(after(lifted_a, three_low), "seq", 1)
    flip_late, flip_far_late, gate_late = after((flip_both, flip_far, gate_b), three_far)
    flip_mate, flip_far_mate = swap(flip_late, "tensor", 1), swap(flip_far_late, "tensor", 1)
    gate_got_b = swap(gate_late, "seq", 1)
    front_both = jnp.stack([front_rows, front_far])
    back_rows, kv_grad, norm_vectors, grad_one = cross_backward(
        three_own, three_got, three_far, grad_near, residual_one, residual_two, norms,
        query_parts, kv_parts, out_parts, cross_queries,
    )
    grad_one, gate_got_a, hidden_got_b, flip_mate, flip_far_mate = meeting(
        grad_one, gate_got_a, hidden_got_b, flip_mate, flip_far_mate
    )
    count = lax.axis_size("seq")
    level_side = ((lax.axis_index("seq") >> 1) % 2).astype(jnp.int32).reshape(1)
    rows = model_width // count

    def traded(dealt):
        keep, send = [value.reshape(count // 4, rows, -1) for value in dealt]
        return keep, swap(send, "seq", 2)

    down_keep, down_got = traded(
        meet_rows(
            rows, level_side, (hidden_own_a, hidden_got_a, hidden_own_b, hidden_got_b),
            (grad_near, grad_pair),
        )
    )
    context_parts = quarters(kv_grad, 1)
    context_got = swap(jnp.concatenate([context_parts[1], context_parts[3]], 0), "tensor", 1)
    one_far_rows, down_keep = meeting(swap(grad_one, "tensor", 2), down_keep)
    one_parts = (
        grad_one, swap(grad_one, "tensor", 1), one_far_rows, swap(one_far_rows, "tensor", 1)
    )
    *one_parts, front_other, context_got, lifted_got_a = meeting(
        *one_parts, swap(after(front_both, grad_one), "tensor", 1), context_got, lifted_got_a
    )
    context_low = (
        context_parts[2].astype(F32) + context_got[context_parts[2].shape[0] :].astype(F32)
    ).astype(BF16)
    context_far = swap(context_low, "tensor", 2)
    back_far = swap(after(back_rows, one_parts[3]), "tensor", 2)
    lifted_got_b = swap(after(lifted_b, grad_one), "seq", 1)
    query_grad, to_prev, kept, to_next, time_grads = attend_back(
        spans, queries, (behind, both, ahead), time_keys, time_values, label_row, label_column,
        w_out, attended, log_totals, one_parts,
    )
    to_prev, to_next, back_far, gate_got_b, down_got, context_far = meeting(
        to_prev, to_next, back_far, gate_got_b, down_got, context_far
    )
    from_next, from_prev = shift(to_prev, "seq", -1), shift(to_next, "seq", 1)
    down_keep, down_got = halve(added(down_keep, down_got).astype(BF16), 2)
    flip_near = (flip_both, flip_mate, flip_far, flip_far_mate)
    first_keep, first_got = traded(
        meet_cols(
            rows, level_side, flip_near,
            after((gate_a, gate_got_a, lifted_a, lifted_got_a), to_prev),
        )
    )
    back_both = jnp.stack([back_rows, back_far])
    back_other = swap(back_both, "tensor", 1)
    context_own = (
        context_parts[0].astype(F32)
        + context_got[: context_far.shape[0]].astype(F32)
        + context_far.astype(F32)
    )
    keep_a, send_a, keep_b, send_b = bundle_grads(
        count, places, (front_both, front_other), (back_both, back_other), one_parts, attended,
        row_context,
        context_own.astype(BF16),
    )
    from_next, from_prev, send_a, send_b = meeting(from_next, from_prev, send_a, send_b)
    got_a = swap(send_a, "seq", 1)
    raw, last_away, last_own, last_low = tail(
        places[1:], query_grad, kept, from_next, from_prev, tables, w_query, w_key, w_value,
        time_grads,
    )
    last_got = swap(last_away, "tensor", 1)
    raw_got = swap(raw, "seq", 1)
    last_sum = (
        last_low.astype(F32) + last_got[local_rows:].astype(F32)
    ).astype(BF16)
    second_keep, second_got = traded(
        meet_cols(
            rows, level_side, flip_near,
            after((gate_b, gate_got_b, lifted_b, lifted_got_b), last_away),
        )
    )
    last_sum, first_got, down_got = meeting(last_sum, first_got, down_got)
    first_keep, first_got = halve(added(first_keep, first_got).astype(BF16), 2)
    last_far, raw_got = meeting(swap(last_sum, "tensor", 2), raw_got)
    frame_grad = last_own + last_got[:local_rows].astype(F32) + last_far.astype(F32)

    time_late, means_late, inverse_late, vectors_late = after(
        (time_grads, means_one, inverse_one, norm_vectors), last_far
    )
    time_grad = sum(
        jnp.einsum("of,df->od", time_late[i : i + 1].astype(BF16), w, preferred_element_type=F32)
        for i, w in enumerate((w_key, w_value))
    )
    own_scaled = (frames.astype(F32) - means_late) * inverse_late
    scaled_grad = frame_grad * gain_attn[None]
    sums = jnp.concatenate(
        [
            jnp.sum(scaled_grad, -1),
            jnp.sum(scaled_grad * own_scaled, -1),
            time_grad[0],
            vectors_late.reshape(-1),
        ]
    )[None]
    sums = sums + swap(sums, "tensor", 1)
    sums = sums + swap(sums, "tensor", 2)
    sums, first_got, second_got = meeting(sums, first_got, second_got)
    second_keep, second_got = halve(added(second_keep, second_got).astype(BF16), 2)
    plain = sums[0, :local_rows, None] / model_width
    cross = sums[0, local_rows : 2 * local_rows, None] / model_width
    vectors = own_cols(sums[0, 2 * local_rows :].reshape(5, model_width))
    attend_full = ordered(*[after(one_parts, from_next)[i] for i in (0, 2, 1, 3)], 0)
    d_frames = own_cols(attend_full).astype(F32) + inverse_late * (
        scaled_grad - plain - own_scaled * cross
    )
    d_gain_attn = jnp.sum(frame_grad * own_scaled, 0) + vectors[0] * own_cols(scaled_time)[0]
    d_bias_attn = jnp.sum(frame_grad, 0) + vectors[0]
    down_away, down_own, down_low = down_parts(after(hidden_a, last_far), hidden_b, w_down)
    branch_got, _, branch_far = scatter_near(down_away, down_low)
    block_rows = (
        residual_two + down_own + branch_got[:share].astype(F32) + branch_far.astype(F32)
    ).astype(BF16)
    block_cols = rows_to_cols(
        *[
            lax.dynamic_slice_in_dim(block_rows, (place ^ r) * local_width, local_width, 1)
            for r in range(4)
        ],
        from_next,
    )
    block_out = jnp.concatenate([row_block(block_cols, place ^ b) for b in range(4)], 0)

    time_column = time_normed.T

    normed_pair = (one_own_half, normed_got)
    grad_down = halve_end(down_keep, down_got, 3)
    raw_pair = (raw[: 3 * head_cols], raw_got[: 3 * head_cols])
    time_got = raw_got[3 * head_cols : 3 * head_cols + 2, :head_cols].astype(F32)
    time_both = (time_grads + time_got).reshape(1, 2 * head_cols)
    own_time_rows = lax.dynamic_index_in_dim(
        time_column.reshape(count // 2, 2, -1), column, 1, False
    ).reshape(-1, 1)
    outer = own_time_rows * jnp.concatenate([jnp.zeros((1, head_cols), F32), time_both], 1)
    blocks = sum(
        jnp.einsum("dn,fn->df", r, c, preferred_element_type=F32)
        for r, c in zip(normed_pair, raw_pair)
    )
    blocks, got_a = meeting(
        (blocks + outer).astype(BF16).reshape(count // 2, rows, 3 * head_cols), got_a
    )
    heads_keep, heads_got = halve(blocks, 1)
    left_keep, left_got = halve(added(keep_a, got_a).astype(BF16), 1)
    got_b = swap(after(send_b, from_next), "seq", 1)
    heads_got, got_b = meeting(heads_got, got_b)
    heads_next = added(heads_keep, heads_got).astype(BF16)
    heads_sum = halve_all(heads_next, 2)
    last_next = added(*halve(added(keep_b, got_b).astype(BF16), 1))
    last_next, second_got = meeting(last_next, second_got)
    first, second = halve_end(first_keep, first_got, 3), halve_end(second_keep, second_got, 3)
    units = first.shape[1] // 2
    grad_gate_w = jnp.concatenate([first[:, :units], second[:, :units]], 1)
    grad_up_w = jnp.concatenate([first[:, units:], second[:, units:]], 1)
    small = jnp.stack(
        [d_gain_attn, d_bias_attn, vectors[3], vectors[4], vectors[1], vectors[2]]
    ).reshape(6, devices, -1).transpose(1, 0, 2)
    small = small.reshape(count // 4, 2, 2, 6, -1).swapaxes(1, 2).reshape(count, 6, -1)
    small = after(small, heads_next)
    bits = [1, 0] + list(range(2, count.bit_length() - 1))
    for bit in bits:
        small = added(*halve(small, bit))
    small = small[0]
    left, right = halve_end(left_keep, left_got, 2), halve_all(last_next, 2)
    part, rows = head_cols // count, model_width // count
    grad_c_query = left[:, :head_cols]
    grad_c_key, grad_c_value = left[: rows // 2, head_cols:], left[rows // 2 :, head_cols:]
    grad_c_out = jnp.concatenate([right[:part], right[part : 2 * part]], 1)
    grad_w_out = jnp.concatenate([right[2 * part : 3 * part], right[3 * part :]], 1)
    grad_w_query, grad_w_key, grad_w_value = (
        heads_sum[:, i * head_cols : (i + 1) * head_cols] for i in range(3)
    )
    return (
        block_out,
        d_frames,
        small[0],
        small[1],
        small[2],
        small[3],
        small[4],
        small[5],
        grad_w_query,
        grad_w_key,
        grad_w_value,
        grad_w_out,
        grad_c_query,
        grad_c_key,
        grad_c_value,
        grad_c_out,
        grad_gate_w,
        grad_up_w,
        grad_down,
    )


def solution(mesh):
    return jax.shard_map(
        per_device,
        mesh=mesh,
        in_specs=(
            P("seq", "tensor"),
            P(),
            P(),
            P(),
            P("tensor"),
            P("tensor"),
            P("tensor"),
            P("tensor"),
            P("tensor"),
            P("tensor"),
            P(None, "tensor"),
            P(None, "tensor"),
            P(None, "tensor"),
            P("tensor", None),
            P(None, "tensor"),
            P(None, "tensor"),
            P(None, "tensor"),
            P("tensor", None),
            P(None, "tensor"),
            P(None, "tensor"),
            P("tensor", None),
            P("seq", "tensor"),
        ),
        out_specs=(
            P("seq", "tensor"),
            P("seq", "tensor"),
            P(("tensor", "seq")),
            P(("tensor", "seq")),
            P(("tensor", "seq")),
            P(("tensor", "seq")),
            P(("tensor", "seq")),
            P(("tensor", "seq")),
            P("seq", "tensor"),
            P("seq", "tensor"),
            P("seq", "tensor"),
            P(("tensor", "seq"), None),
            P("seq", "tensor"),
            P("seq", "tensor"),
            P("seq", "tensor"),
            P(("tensor", "seq"), None),
            P("seq", "tensor"),
            P("seq", "tensor"),
            P(("tensor", "seq"), None),
        ),
        check_vma=False,
    )
```

```python
import functools
import math

import jax
import jax.numpy as jnp
from jax import lax
from jax.experimental import pallas as pl
from jax.experimental.pallas import tpu as pltpu
from jax.sharding import PartitionSpec as P

HEAD_SIZE = 64
ROW_MIN = 2048
TILE = 256
BF16 = jnp.bfloat16
F32 = jnp.float32


def meeting(*values):
    return lax.optimization_barrier(values)


def after(value, token):
    return lax.optimization_barrier((value, token))[0]


def swap(value, axis, by):
    return lax.ppermute(value, axis, [(i, i ^ by) for i in range(lax.axis_size(axis))])


def shift(value, axis, by):
    peers = lax.axis_size(axis)
    pairs = [(i, i + by) for i in range(peers) if 0 <= i + by < peers]
    return lax.ppermute(value, axis, pairs)


def tensor_place():
    place = lax.axis_index("tensor")
    return place // 2, place % 2


def ordered(own, far, mate, far_mate, axis):
    side, core = tensor_place()
    near = (jnp.where(core == 0, own, mate), jnp.where(core == 0, mate, own))
    away = (jnp.where(core == 0, far, far_mate), jnp.where(core == 0, far_mate, far))
    low = [jnp.where(side == 0, n, a) for n, a in zip(near, away)]
    high = [jnp.where(side == 0, a, n) for n, a in zip(near, away)]
    return jnp.concatenate(low + high, axis)


def gather_near(own):
    far = swap(own, "tensor", 2)
    return own, swap(own, "tensor", 1), far, swap(far, "tensor", 1)


def gather_staged(own, first, second):
    far = swap(after(own, first), "tensor", 2)
    far, late = after((far, own), second)
    return own, swap(late, "tensor", 1), far, swap(far, "tensor", 1)


def gather(own, axis):
    own, mate, far, far_mate = gather_near(own)
    return ordered(own, far, mate, far_mate, axis)


def scatter_near(away, low):
    got = swap(away, "tensor", 1)
    total = (low.astype(F32) + got[low.shape[0] :].astype(F32)).astype(BF16)
    return got, total, swap(total, "tensor", 2)


def rows_to_cols(own, mate, far, far_mate, later):
    width = own.shape[1]
    got = after(swap(jnp.concatenate([far, far_mate], 1), "tensor", 2), later)
    other = swap(jnp.concatenate([mate, got[:, width:]], 0), "tensor", 1)
    size = own.shape[0]
    return jnp.concatenate([own, other[:size], got[:, :width], other[size:]], 0)


def quarters(value, axis):
    return jnp.split(value, 4, axis)


def own_blocks(near):
    return jnp.concatenate([quarters(value, 1)[r] for r, value in enumerate(near)], 0)


def trade(value, start, done):
    return after(swap(after(value, start), "seq", 1), done)


def halve(blocks, bit):
    count, rows, cols = blocks.shape
    side = (lax.axis_index("seq") >> bit) % 2
    parts = blocks.reshape(count // 2, 2, rows, cols)
    send = lax.dynamic_index_in_dim(parts, 1 - side, 1, False)
    keep = lax.dynamic_index_in_dim(parts, side, 1, False)
    return keep, swap(send, "seq", 1 << bit)


def added(keep, got):
    return keep.astype(F32) + got.astype(F32)


def halve_all(blocks, bit):
    while blocks.shape[0] > 1:
        blocks = added(*halve(blocks.astype(BF16), bit))
        bit += 1
    return blocks[0].astype(F32)


def halve_end(keep, got, bit):
    return halve_all(added(keep, got), bit)


def frame_clip_labels(segment, row_length):
    frame_index = jnp.arange(segment.shape[0], dtype=jnp.int32)
    border = (frame_index % row_length == 0) | (segment != jnp.roll(segment, 1))
    clip_starts = lax.cummax(jnp.where(border, frame_index, 0), axis=0)
    return (clip_starts, (frame_index - clip_starts + 1).astype(jnp.float32))


def tile_ranges(q_labels, key_labels):
    q = q_labels.reshape(-1, TILE)
    k = key_labels.reshape(-1, TILE)
    meets = (k[None, :, 0] <= q[:, None, -1]) & (k[None, :, -1] >= q[:, None, 0])
    index = jnp.arange(k.shape[0], dtype=jnp.int32)[None]
    low = jnp.min(jnp.where(meets, index, k.shape[0]), 1)
    high = jnp.max(jnp.where(meets, index + 1, 0), 1)
    return jnp.stack([low, high], 1).reshape(-1)

def head_rows(g):
    return slice(g * HEAD_SIZE, (g + 1) * HEAD_SIZE)

def fill_natural(dest, refs, which):
    size = refs[0].shape[2]
    for part, ref in enumerate(refs):
        dest[part * size : (part + 1) * size, :] = ref[which].T


def fill_tiles(dest, refs, which):
    pieces = refs[0].shape[2] // TILE
    for part, ref in enumerate(refs):
        for piece in range(pieces):
            dest[part * pieces + piece] = ref[which, :, piece * TILE : (piece + 1) * TILE]


def relative(place, r, size):
    return pl.ds(pl.multiple_of((place ^ r) * size, size), size)


def absorb(state, start, stop, base, q, cols, lab, klab, keys, vals):
    group = q.shape[0] // HEAD_SIZE

    def step(j, state):
        seen = klab[pl.ds(pl.multiple_of(j * TILE, TILE), TILE), :] == lab
        at = pl.ds(pl.multiple_of((j - base) * TILE, TILE), TILE)
        fresh = []
        for g in range(group):
            top, total, acc = state[3 * g : 3 * g + 3]
            s = dot_nn(keys[at, head_rows(g)], q[head_rows(g), cols])
            s = jnp.where(seen, s, -1e30)
            new = jnp.maximum(top, jnp.max(s, 0, keepdims=True))
            fade = jnp.exp(top - new)
            p = jnp.exp(s - new)
            total = total * fade + jnp.sum(p, 0, keepdims=True)
            acc = acc * fade + dot_nn(vals[j - base, head_rows(g), :], p.astype(BF16))
            fresh += [new, total, acc]
        return tuple(fresh)

    return lax.fori_loop(start, stop, step, tuple(state))


def near_body(span, q, kv, tk, tv, qlab, klab, tops, totals, mix, keys, vals):
    rows, size = q.shape
    pieces = size // TILE
    fill_natural(keys, (kv,), 0)
    fill_tiles(vals, (kv,), 1)
    for tile in range(pieces):
        cols = slice(tile * TILE, (tile + 1) * TILE)
        state = []
        for g in range(rows // HEAD_SIZE):
            part = q[head_rows(g), cols].astype(F32)
            top = jnp.sum(part * tk[head_rows(g), :], 0, keepdims=True)
            state += [
                top,
                jnp.ones_like(top),
                jnp.broadcast_to(tv[head_rows(g), :], (HEAD_SIZE, TILE)),
            ]
        start = jnp.maximum(span[2 * tile], pieces)
        stop = jnp.minimum(span[2 * tile + 1], 2 * pieces)
        state = absorb(state, start, stop, pieces, q, cols, qlab[:, cols], klab, keys, vals)
        for g in range(rows // HEAD_SIZE):
            tops[g : g + 1, cols], totals[g : g + 1, cols], mix[head_rows(g), cols] = state[
                3 * g : 3 * g + 3
            ]


def far_body(span, q, kv0, kv2, qlab, klab, w_out, tops, totals, mix,
             out, lse, away, own, low, keys0, keys2, vals0, vals2):
    rows, size = q.shape
    pieces = size // TILE
    for kv, keys, vals in ((kv0, keys0, vals0), (kv2, keys2, vals2)):
        fill_natural(keys, (kv,), 0)
        fill_tiles(vals, (kv,), 1)
    for tile in range(pieces):
        cols = slice(tile * TILE, (tile + 1) * TILE)
        lab = qlab[:, cols]
        state = []
        for g in range(rows // HEAD_SIZE):
            state += [tops[g : g + 1, cols], totals[g : g + 1, cols], mix[head_rows(g), cols]]
        stop = jnp.minimum(span[2 * tile + 1], pieces)
        state = absorb(state, span[2 * tile], stop, 0, q, cols, lab, klab, keys0, vals0)
        start = jnp.maximum(span[2 * tile], 2 * pieces)
        state = absorb(
            state, start, span[2 * tile + 1], 2 * pieces, q, cols, lab, klab, keys2, vals2
        )
        for g in range(rows // HEAD_SIZE):
            top, total, acc = state[3 * g : 3 * g + 3]
            out[head_rows(g), cols] = (acc / total).astype(BF16)
            lse[g : g + 1, cols] = top + jnp.log(total)
    place = span[2 * pieces]
    share = own.shape[0]

    def sent(r):
        return dot_tn(out[:, relative(place, r, share)], w_out[...])

    away[:share, :] = sent(1).astype(BF16)
    away[share:, :] = sent(3).astype(BF16)
    low[...] = sent(2).astype(BF16)
    own[...] = sent(0)


def backward_body(span, q, kv0, kv1, kv2, tk, tv, qlab, klab, w_out, out, lse,
                  g0, g1, g2, g3, dq, to_prev, kept, to_next, times,
                  og, keys, vals, tkeys, ak, av, dtk, dtv):
    rows, size = q.shape
    group = rows // HEAD_SIZE
    pieces = size // TILE
    share = g0.shape[0]
    for r, ref in enumerate((g0, g1, g2, g3)):
        og[:, relative(span[2 * pieces], r, share)] = dot_nt(w_out[...], ref[...]).astype(BF16)
    fill_natural(keys, (kv0, kv1, kv2), 0)
    fill_natural(vals, (kv0, kv1, kv2), 1)
    fill_tiles(tkeys, (kv0, kv1, kv2), 0)
    ak[...] = jnp.zeros_like(ak)
    av[...] = jnp.zeros_like(av)
    for tile in range(pieces):
        cols = slice(tile * TILE, (tile + 1) * TILE)
        lab = qlab[:, cols]
        state, norms, deltas = [], [], []
        for g in range(group):
            hr = head_rows(g)
            qf = q[hr, cols].astype(F32)
            gf = og[hr, cols].astype(F32)
            norm = lse[g : g + 1, cols]
            delta = jnp.sum(gf * out[hr, cols].astype(F32), 0, keepdims=True)
            pt = jnp.exp(jnp.sum(qf * tk[hr, :], 0, keepdims=True) - norm)
            st = pt * (jnp.sum(gf * tv[hr, :], 0, keepdims=True) - delta)
            gk = jnp.sum(qf * st, 1, keepdims=True)
            gv = jnp.sum(gf * pt, 1, keepdims=True)
            if tile == 0:
                dtk[hr, :] = gk
                dtv[hr, :] = gv
            else:
                dtk[hr, :] += gk
                dtv[hr, :] += gv
            state.append(tk[hr, :] * st)
            norms.append(norm)
            deltas.append(delta)

        def step(j, state):
            start = pl.multiple_of(j * TILE, TILE)
            seen = klab[pl.ds(start, TILE), :] == lab
            fresh = []
            for g in range(group):
                hr = head_rows(g)
                s = dot_nn(keys[pl.ds(start, TILE), hr], q[hr, cols])
                p = jnp.exp(jnp.where(seen, s, -1e30) - norms[g])
                m = dot_nn(vals[pl.ds(start, TILE), hr], og[hr, cols])
                ds = (p * (m - deltas[g])).astype(BF16)
                av[j, hr, :] += dot_nt(og[hr, cols], p.astype(BF16))
                ak[j, hr, :] += dot_nt(q[hr, cols], ds)
                fresh.append(state[g] + dot_nn(tkeys[j, hr, :], ds))
            return tuple(fresh)

        state = lax.fori_loop(span[2 * tile], span[2 * tile + 1], step, tuple(state))
        for g in range(group):
            dq[head_rows(g), cols] = state[g]
    for at, column in ((0, dtk), (1, dtv)):
        spread = jnp.broadcast_to(column[...], (rows, 2 * HEAD_SIZE))
        times[at : at + 1, :] = spread.T[:1, :]
    for part, dest in enumerate((to_prev, kept, to_next)):
        for piece in range(pieces):
            at = slice(piece * TILE, (piece + 1) * TILE)
            dest[0, :, at] = ak[part * pieces + piece].astype(dest.dtype)
            dest[1, :, at] = av[part * pieces + piece].astype(dest.dtype)


def attend_near(span, q, kv, tk, tv, qlab, klab):
    cols, size = q.shape
    wide = lambda *dims: jax.ShapeDtypeStruct(dims, F32)
    vmem = pl.BlockSpec(memory_space=pltpu.VMEM)
    return pl.pallas_call(
        near_body,
        in_specs=[pl.BlockSpec(memory_space=pltpu.SMEM)] + [vmem] * 6,
        out_specs=[vmem] * 3,
        out_shape=[wide(cols // HEAD_SIZE, size), wide(cols // HEAD_SIZE, size), wide(cols, size)],
        scratch_shapes=[pltpu.VMEM((size, cols), BF16), pltpu.VMEM((size // TILE, cols, TILE), BF16)],
        name="attend_near", cost_estimate=FREE,
    )(span, q, kv, tk, tv, qlab, klab)


def attend_far(span, q, behind, ahead, qlab, klab, w_out, state):
    cols, size = q.shape
    share, width = size // 4, w_out.shape[1]
    low = lambda *dims: jax.ShapeDtypeStruct(dims, BF16)
    wide = lambda *dims: jax.ShapeDtypeStruct(dims, F32)
    vmem = pl.BlockSpec(memory_space=pltpu.VMEM)
    keys = pltpu.VMEM((size, cols), BF16)
    vals = pltpu.VMEM((size // TILE, cols, TILE), BF16)
    return pl.pallas_call(
        far_body,
        in_specs=[pl.BlockSpec(memory_space=pltpu.SMEM)] + [vmem] * 9,
        out_specs=[vmem] * 5,
        out_shape=[low(cols, size), wide(cols // HEAD_SIZE, size), low(2 * share, width),
                   wide(share, width), low(share, width)],
        scratch_shapes=[keys, keys, vals, vals],
        name="attend_far", cost_estimate=FREE,
    )(span, q, behind, ahead, qlab, klab, w_out, *state)


def attend_back(span, q, kvs, tk, tv, qlab, klab, w_out, out, lse, grads):
    cols, size = q.shape
    tiles = 3 * size // TILE
    low = lambda *dims: jax.ShapeDtypeStruct(dims, BF16)
    wide = lambda *dims: jax.ShapeDtypeStruct(dims, F32)
    vmem = pl.BlockSpec(memory_space=pltpu.VMEM)
    return pl.pallas_call(
        backward_body,
        in_specs=[pl.BlockSpec(memory_space=pltpu.SMEM)] + [vmem] * 15,
        out_specs=[vmem] * 5,
        out_shape=[wide(cols, size), low(2, cols, size), wide(2, cols, size), low(2, cols, size),
                   wide(2, cols)],
        scratch_shapes=[pltpu.VMEM((cols, size), BF16), pltpu.VMEM((3 * size, cols), BF16),
                        pltpu.VMEM((3 * size, cols), BF16), pltpu.VMEM((tiles, cols, TILE), BF16),
                        pltpu.VMEM((tiles, cols, TILE), F32), pltpu.VMEM((tiles, cols, TILE), F32),
                        pltpu.VMEM((cols, 1), F32), pltpu.VMEM((cols, 1), F32)],
        name="attend_back", cost_estimate=FREE,
    )(span, q, *kvs, tk, tv, qlab, klab, w_out, out, lse, *grads)


def tail_body(place, dq, kept, ahead, behind, cosine, sine, wq, wk, wv, times,
              raw, away, own, low, flipped):
    part, size = dq.shape
    half = HEAD_SIZE // 2

    def returned(block, base, scale):
        for h in range(part // HEAD_SIZE):
            a = block[h * HEAD_SIZE : h * HEAD_SIZE + half, :]
            b = block[h * HEAD_SIZE + half : (h + 1) * HEAD_SIZE, :]
            at = base + h * HEAD_SIZE
            raw[at : at + half, :] = ((a * cosine[...] + b * sine[...]) * scale).astype(BF16)
            raw[at + half : at + HEAD_SIZE, :] = (
                (b * cosine[...] - a * sine[...]) * scale
            ).astype(BF16)

    def whole(index):
        return kept[index] + ahead[index].astype(F32) + behind[index].astype(F32)

    returned(dq[...], 0, 1.0 / math.sqrt(HEAD_SIZE))
    returned(whole(0), part, 1.0)
    raw[2 * part : 3 * part, :] = whole(1).astype(BF16)
    raw[3 * part :, :] = jnp.zeros((16, size), BF16)
    raw[3 * part : 3 * part + 2, :part] = times[...].astype(BF16)
    flipped[...] = raw[: 3 * part, :].T

    def sent(r):
        at = relative(place[0], r, part)
        return sum(
            dot_nt(flipped[:, i * part : (i + 1) * part], weight[at, :])
            for i, weight in enumerate((wq, wk, wv))
        )

    away[:size, :] = sent(1).astype(BF16)
    away[size:, :] = sent(3).astype(BF16)
    low[...] = sent(2).astype(BF16)
    own[...] = sent(0)


def tail(place, dq, kept, ahead, behind, tables, wq, wk, wv, times):
    part, size = dq.shape
    low = lambda *dims: jax.ShapeDtypeStruct(dims, BF16)
    vmem = pl.BlockSpec(memory_space=pltpu.VMEM)
    return pl.pallas_call(
        tail_body,
        in_specs=[pl.BlockSpec(memory_space=pltpu.SMEM)] + [vmem] * 10,
        out_specs=[vmem] * 4,
        out_shape=[low(3 * part + 16, size), low(2 * size, part), jax.ShapeDtypeStruct((size, part), F32),
                   low(size, part)],
        scratch_shapes=[pltpu.VMEM((size, 3 * part), BF16)],
        name="tail", cost_estimate=FREE,
    )(place, dq, kept, ahead, behind, *tables, wq, wk, wv, times)


def rotary_tables(frame_positions):
    half_dim = HEAD_SIZE // 2
    frequency = jnp.exp(jnp.arange(half_dim, dtype=jnp.float32) * (-math.log(10000.0) / half_dim))
    angles = frequency[:, None] * frame_positions[None, :]
    return (jnp.cos(angles), jnp.sin(angles))


def rotate(rows, tables, sign=1.0):
    count, size = rows.shape
    halves = rows.reshape(count // HEAD_SIZE, 2, HEAD_SIZE // 2, size)
    cosine, sine = tables[0][None], tables[1][None] * sign
    first = halves[:, 0] * cosine - halves[:, 1] * sine
    second = halves[:, 1] * cosine + halves[:, 0] * sine
    return jnp.stack([first, second], 1).reshape(count, size)


def product(left, right):
    return jnp.dot(left, right, preferred_element_type=jnp.float32)


def inner_rows(left, right):
    return jnp.einsum("nd,nf->df", left, right, preferred_element_type=jnp.float32)


def back_project(gradient, weight):
    return jnp.einsum("nf,df->nd", gradient, weight, preferred_element_type=jnp.float32)


def by_feature(left, right):
    return jnp.einsum("nd,df->fn", left, right, preferred_element_type=jnp.float32)


def columns(weight, start, size):
    return lax.dynamic_slice_in_dim(weight, start, size, 1)


def rows_of(weight, start, size):
    return lax.dynamic_slice_in_dim(weight, start, size, 0)


def normalize(value_rows):
    means = jnp.mean(value_rows, -1, keepdims=True)
    centred = value_rows - means
    inverse = lax.rsqrt(jnp.mean(centred * centred, -1, keepdims=True) + 1e-05)
    return centred * inverse, inverse


def norm_backward(gradient, scaled, inverse, norm_gain):
    scaled_grad = gradient * norm_gain
    plain = jnp.mean(scaled_grad, -1, keepdims=True)
    cross = jnp.mean(scaled_grad * scaled, -1, keepdims=True)
    return inverse * (scaled_grad - plain - scaled * cross)


FREE = pl.CostEstimate(flops=1, transcendentals=0, bytes_accessed=1)


def dot_nn(left, right):
    return lax.dot_general(left, right, (((1,), (0,)), ((), ())), preferred_element_type=F32)


def dot_nt(left, right):
    return lax.dot_general(left, right, (((1,), (1,)), ((), ())), preferred_element_type=F32)


def dot_tn(left, right):
    return lax.dot_general(left, right, (((0,), (0,)), ((), ())), preferred_element_type=F32)


def head_weights(query, key, lanes, which):
    mine = jnp.where(lanes == which, query, jnp.zeros_like(query))
    scores = dot_nt(mine, key) * (1.0 / math.sqrt(HEAD_SIZE))
    weights = jnp.exp(scores - jnp.max(scores, -1, keepdims=True))
    return weights / jnp.sum(weights, -1, keepdims=True)


def pair_cols(refs, p, rows):
    ref = refs[p * 2 * HEAD_SIZE // refs[0].shape[1]]
    start = p * 2 * HEAD_SIZE % refs[0].shape[1]
    return ref[rows, start : start + 2 * HEAD_SIZE]


def cross_forward_body(width_block, place, rows, own, got, far, norms, q0, q1, q2, q3,
                       c0, c1, c2, c3, o0, o1, o2, o3,
                       front, queries, first, second, normed_three,
                       flip_own, flip_away):
    width = rows.shape[1]
    kv = (c0, c1, c2, c3)
    context_rows = c0.shape[0] // 2
    key_rows, value_rows = slice(0, context_rows), slice(context_rows, 2 * context_rows)
    lanes = lax.broadcasted_iota(jnp.int32, (rows.shape[0], 2 * HEAD_SIZE), 1) // HEAD_SIZE
    residual = (
        rows[...].astype(F32) + own[...] + got[...].astype(F32) + far[...].astype(F32)
    )
    first[...] = residual
    scaled, _ = normalize(residual)
    low = (scaled * norms[2:3, :] + norms[3:4, :]).astype(BF16)
    front[:, :width] = low
    part = width // 4
    for b, ref in enumerate((q0, q1, q2, q3)):
        queries[:, b * part : (b + 1) * part] = dot_nn(low, ref[...]).astype(BF16)
    for p in range(width // (2 * HEAD_SIZE)):
        cols = slice(p * 2 * HEAD_SIZE, (p + 1) * 2 * HEAD_SIZE)
        q, k, v = queries[:, cols], pair_cols(kv, p, key_rows), pair_cols(kv, p, value_rows)
        mixed = [dot_nn(head_weights(q, k, lanes, g).astype(BF16), v) for g in (0, 1)]
        front[:, width + cols.start : width + cols.stop] = jnp.where(lanes == 0, mixed[0], mixed[1]).astype(BF16)
    for b, ref in enumerate((o0, o1, o2, o3)):
        residual = residual + dot_nn(front[:, width + b * part : width + (b + 1) * part], ref[...])
    second[...] = residual
    scaled, _ = normalize(residual)
    low = (scaled * norms[4:5, :] + norms[5:6, :]).astype(BF16)
    normed_three[...] = low
    deal_rows(low.T, width_block, place[0], flip_own, flip_away)


def cross_forward(devices, place, rows, own, got, far, norms, query_parts, kv_parts, out_parts):
    size, width = rows.shape
    low = jax.ShapeDtypeStruct(rows.shape, BF16)
    both = jax.ShapeDtypeStruct((size, 2 * width), BF16)
    wide = jax.ShapeDtypeStruct(rows.shape, F32)
    flip = jax.ShapeDtypeStruct((width // 2, size), BF16)
    vmem = pl.BlockSpec(memory_space=pltpu.VMEM)
    block = pl.BlockSpec((size, width), lambda i: (0, 0))
    return pl.pallas_call(
        functools.partial(cross_forward_body, width // devices),
        grid=(1,),
        in_specs=[pl.BlockSpec(memory_space=pltpu.SMEM)] + [block] * 4 + [vmem] * 13,
        out_shape=[both, low, wide, wide, low, flip, flip],
        cost_estimate=FREE, name="cross",
    )(place, rows, own, got, far, norms, *query_parts, *kv_parts, *out_parts)


def deal_rows(rows, size, column, own, away):
    for b in range(rows.shape[0] // (2 * size)):
        at = slice(b * size, (b + 1) * size)
        even = rows[2 * b * size : (2 * b + 1) * size, :]
        odd = rows[(2 * b + 1) * size : (2 * b + 2) * size, :]

        @pl.when(column == 0)
        def _():
            own[at, :] = even
            away[at, :] = odd

        @pl.when(column != 0)
        def _():
            own[at, :] = odd
            away[at, :] = even


def ffn_part(normed, grad, gate_w, up_w, down_w, hidden, hid_own, hid_away, gate_grad, lifted_grad,
             unit_block, column):
    gate = dot_nn(normed, gate_w[...])
    lifted = dot_nn(normed, up_w[...])
    back = dot_nt(grad, down_w[...]).astype(BF16).astype(F32)
    sig = jax.nn.sigmoid(gate)
    swish = gate * sig
    made = (swish * lifted).astype(BF16)
    hidden[...] = made
    deal_rows(made.T, unit_block, column, hid_own, hid_away)
    gg = (back * lifted * sig * (1.0 + gate * (1.0 - sig))).astype(BF16)
    lg = (back * swish).astype(BF16)
    gate_grad[...] = gg
    lifted_grad[...] = lg
    return dot_nt(gg, gate_w[...]) + dot_nt(lg, up_w[...])


def ffn_first_body(unit_block, place, n0, n1, n2, n3, g0, g1, g2, g3, gate_w, up_w, down_w,
                   hidden, hid_own, hid_away, gate_grad, lifted_grad, normed, grad, grad_pair,
                   total):
    share, part = n0.shape[0], g0.shape[2]
    for b, ref in enumerate((n0, n1, n2, n3)):
        normed[b * share : (b + 1) * share, :] = ref[...]
    for c, ref in enumerate((g0, g1, g2, g3)):
        for b in range(4):
            rows, cols = relative(place[1], b, share), relative(place[1], c, part)
            grad[b * share : (b + 1) * share, cols] = ref[0, rows, :]
            grad_pair[b * share : (b + 1) * share, cols] = ref[1, rows, :]
    total[...] = ffn_part(
        normed[...], grad[...], gate_w, up_w, down_w, hidden, hid_own, hid_away, gate_grad,
        lifted_grad, unit_block, place[0],
    )


def ffn_second_body(unit_block, place, normed, grad, total, gate_w, up_w, down_w,
                    hidden, hid_own, hid_away, gate_grad, lifted_grad, away, own, low):
    share = own.shape[0]
    found = total[...] + ffn_part(
        normed[...], grad[...], gate_w, up_w, down_w, hidden, hid_own, hid_away, gate_grad,
        lifted_grad, unit_block, place[0],
    )
    own[...] = found[:share, :]
    low[...] = found[2 * share : 3 * share, :].astype(BF16)
    away[:share, :] = found[share : 2 * share, :].astype(BF16)
    away[share:, :] = found[3 * share :, :].astype(BF16)


def ffn(devices, place, half, inputs, gate_w, up_w, down_w):
    share = inputs[0].shape[0] if half == 0 else inputs[0].shape[0] // 4
    width = inputs[0].shape[1]
    size, units = 4 * share, gate_w.shape[1]
    tile = units // 2
    low = lambda *dims: jax.ShapeDtypeStruct(dims, BF16)
    wide = lambda *dims: jax.ShapeDtypeStruct(dims, F32)
    vmem = pl.BlockSpec(memory_space=pltpu.VMEM)
    cols = pl.BlockSpec((width, tile), lambda i: (0, half))
    rows = pl.BlockSpec((tile, width), lambda i: (half, 0))
    made = [low(size, tile), low(tile // 2, size), low(tile // 2, size), low(size, tile),
            low(size, tile)]
    if half == 0:
        made += [low(size, width), low(size, width), low(size, width), wide(size, width)]
    else:
        made += [low(2 * share, width), wide(share, width), low(share, width)]
    return pl.pallas_call(
        functools.partial(ffn_second_body if half else ffn_first_body, units // devices),
        grid=(1,),
        in_specs=[pl.BlockSpec(memory_space=pltpu.SMEM)] + [vmem] * len(inputs)
        + [cols, cols, rows],
        out_specs=[vmem] * len(made),
        out_shape=made,
        cost_estimate=FREE, name="ffn",
    )(place, *inputs, gate_w, up_w, down_w)


def cross_backward_body(own, got, far, grad, first, second, norms, q0, q1, q2, q3,
                        c0, c1, c2, c3, o0, o1, o2, o3, queries,
                        back_rows, kv_grad, vectors, grad_one, crossed_grad):
    width = grad.shape[1]
    kv = (c0, c1, c2, c3)
    context_rows = c0.shape[0] // 2
    key_rows, value_rows = slice(0, context_rows), slice(context_rows, 2 * context_rows)
    part = width // 4
    lanes = lax.broadcasted_iota(jnp.int32, (grad.shape[0], 2 * HEAD_SIZE), 1) // HEAD_SIZE
    lane_k = lax.broadcasted_iota(jnp.int32, (context_rows, 2 * HEAD_SIZE), 1) // HEAD_SIZE
    scale = 1.0 / math.sqrt(HEAD_SIZE)
    arrived = own[...] + got[...].astype(F32) + far[...].astype(F32)
    scaled, inverse = normalize(second[...])
    vectors[0:1, :] = jnp.sum(arrived * scaled, 0, keepdims=True)
    vectors[1:2, :] = jnp.sum(arrived, 0, keepdims=True)
    two = grad[...].astype(F32) + norm_backward(arrived, scaled, inverse, norms[4:5, :])
    low = two.astype(BF16)
    back_rows[:, :width] = low
    for b, ref in enumerate((o0, o1, o2, o3)):
        crossed_grad[:, b * part : (b + 1) * part] = dot_nt(low, ref[...]).astype(BF16)
    for p in range(width // (2 * HEAD_SIZE)):
        cols = slice(p * 2 * HEAD_SIZE, (p + 1) * 2 * HEAD_SIZE)
        q, k, v = queries[:, cols], pair_cols(kv, p, key_rows), pair_cols(kv, p, value_rows)
        g_rows = crossed_grad[:, cols]
        found = []
        for g in (0, 1):
            probs = head_weights(q, k, lanes, g)
            change = dot_nt(jnp.where(lanes == g, g_rows, jnp.zeros_like(g_rows)), v)
            delta = jnp.sum(change * probs, -1, keepdims=True)
            ds = (probs * (change - delta)).astype(BF16)
            found.append((dot_nn(ds, k), dot_tn(ds, q), dot_tn(probs.astype(BF16), g_rows)))
        back_rows[:, width + cols.start : width + cols.stop] = (
            jnp.where(lanes == 0, found[0][0], found[1][0]) * scale
        ).astype(BF16)
        kv_grad[:context_rows, cols] = (
            jnp.where(lane_k == 0, found[0][1], found[1][1]) * scale
        ).astype(BF16)
        kv_grad[context_rows:, cols] = jnp.where(lane_k == 0, found[0][2], found[1][2]).astype(
            BF16
        )
    back = jnp.zeros(grad.shape, F32)
    for b, ref in enumerate((q0, q1, q2, q3)):
        back = back + dot_nt(back_rows[:, width + b * part : width + (b + 1) * part], ref[...])
    scaled, inverse = normalize(first[...])
    vectors[2:3, :] = jnp.sum(back * scaled, 0, keepdims=True)
    vectors[3:4, :] = jnp.sum(back, 0, keepdims=True)
    grad_one[...] = (two + norm_backward(back, scaled, inverse, norms[2:3, :])).astype(BF16)


def cross_backward(own, got, far, grad, first, second, norms, query_parts, kv_parts, out_parts,
                   queries):
    rows, width = own.shape
    low = lambda r: jax.ShapeDtypeStruct((r, width), BF16)
    block = pl.BlockSpec((rows, width), lambda i: (0, 0))
    return pl.pallas_call(
        cross_backward_body,
        grid=(1,),
        out_shape=[jax.ShapeDtypeStruct((rows, 2 * width), BF16), low(kv_parts[0].shape[0]),
                   jax.ShapeDtypeStruct((4, width), F32), low(rows)],
        in_specs=[block] * 6 + [pl.BlockSpec(memory_space=pltpu.VMEM)] * 14,
        scratch_shapes=[pltpu.VMEM((rows, width), BF16)],
        cost_estimate=FREE, name="cross_back",
    )(own, got, far, grad, first, second, norms, *query_parts, *kv_parts, *out_parts, queries)


def meet_rows_body(size, side, own_a, pair_a, own_b, pair_b, right, right_pair, keep, send):
    half = keep.shape[0] // 2
    for b, (own, pair) in enumerate(((own_a, pair_a), (own_b, pair_b))):
        made = (dot_nn(own[...], right[...]) + dot_nn(pair[...], right_pair[...])).astype(BF16)
        at = pl.ds(b * half, half)
        deal_rows(made, size, side[0], keep.at[at], send.at[at])


def meet_rows(size, side, lefts, rights):
    count, frames = lefts[0].shape
    width = rights[0].shape[1]
    tile = width // 3
    left = pl.BlockSpec((count, frames), lambda i: (0, 0))
    right = pl.BlockSpec((frames, tile), lambda i: (0, i))
    return pl.pallas_call(
        functools.partial(meet_rows_body, size),
        grid=(3,),
        in_specs=[pl.BlockSpec(memory_space=pltpu.SMEM)] + [left] * 4 + [right] * 2,
        out_specs=[pl.BlockSpec((count, tile), lambda i: (0, i))] * 2,
        out_shape=[jax.ShapeDtypeStruct((count, width), BF16)] * 2,
        name="meet_rows", cost_estimate=FREE,
    )(side, *lefts, *rights)


def meet_cols_body(size, side, p0, p1, p2, p3, *refs):
    own, pair = (jnp.concatenate([p[i] for p in (p0, p1, p2, p3)], 1) for i in (0, 1))
    *rights, keep, send = refs
    width = rights[0].shape[1]
    for at in range(len(rights) // 2):
        made = dot_nn(own, rights[2 * at][...]) + dot_nn(pair, rights[2 * at + 1][...])
        cols = pl.ds(at * width, width)
        deal_rows(made.astype(BF16), size, side[0], keep.at[:, cols], send.at[:, cols])


def meet_cols(size, side, near, rights):
    width = rights[0].shape[1] * (len(rights) // 2)
    half = jax.ShapeDtypeStruct((near[0].shape[1] // 2, width), BF16)
    vmem = pl.BlockSpec(memory_space=pltpu.VMEM)
    return pl.pallas_call(
        functools.partial(meet_cols_body, size),
        in_specs=[pl.BlockSpec(memory_space=pltpu.SMEM)] + [vmem] * (4 + len(rights)),
        out_shape=[half] * 2,
        name="meet_cols", cost_estimate=FREE,
    )(side, *near, *rights)


def down_body(first, second, down_w, away, own, low):
    share, units = own.shape[0], first.shape[1]

    def sent(r):
        at = slice(r * share, (r + 1) * share)
        return dot_nn(first[at, :], down_w[:units, :]) + dot_nn(second[at, :], down_w[units:, :])

    away[:share, :] = sent(1).astype(BF16)
    away[share:, :] = sent(3).astype(BF16)
    low[...] = sent(2).astype(BF16)
    own[...] = sent(0)


def down_parts(first, second, down_w):
    share, width = first.shape[0] // 4, down_w.shape[1]
    low = lambda *dims: jax.ShapeDtypeStruct(dims, BF16)
    return pl.pallas_call(
        down_body,
        out_shape=[low(2 * share, width), jax.ShapeDtypeStruct((share, width), F32),
                   low(share, width)],
        name="down", cost_estimate=FREE,
    )(first, second, down_w)


def bundle_body(devices, place, f02, f13, b02, b13, a0, a1, a2, a3, attended,
                context, kv, keep_a, send_a, keep_b, send_b):
    width = a0.shape[1]
    part, share = width // 4, a0.shape[0]

    def near(even, odd):
        return even[0], odd[0], even[1], odd[1]

    own = lambda rows: jnp.concatenate(
        [row[:, width + r * part : width + (r + 1) * part] for r, row in enumerate(rows)], 0
    )
    full = lambda rows: jnp.concatenate([row[:, :width] for row in rows], 0)
    fronts, backs = near(f02, f13), near(b02, b13)
    rows = width // devices
    small = part // devices
    half = width // 2

    def put(block, base, left, out):
        size = block.shape[0] // devices
        cols = slice(left, left + block.shape[1])
        low = block.astype(BF16)
        for d in range(0, devices, 2):
            at = slice(base, base + size)
            even, odd = low[d * size : (d + 1) * size, :], low[(d + 1) * size : (d + 2) * size, :]

            @pl.when(place[0] == 0)
            def _():
                out[0][d // 2, at, cols] = even
                out[1][d // 2, at, cols] = odd

            @pl.when(place[0] != 0)
            def _():
                out[0][d // 2, at, cols] = odd
                out[1][d // 2, at, cols] = even

    put(dot_tn(full(fronts), own(backs)), 0, 0, (keep_a, send_a))
    count = context.shape[0]
    put(dot_tn(context[...], kv[:count, :]), 0, part, (keep_a, send_a))
    put(dot_tn(context[...], kv[count:, :]), rows // 2, part, (keep_a, send_a))
    grads = dot_tn(own(fronts), full(backs))
    put(grads[:, :half], 0, 0, (keep_b, send_b))
    put(grads[:, half:], small, 0, (keep_b, send_b))
    grads = sum(
        dot_nn(attended[:, relative(place[1], r, share)], ref[...])
        for r, ref in enumerate((a0, a1, a2, a3))
    )
    put(grads[:, :half], 2 * small, 0, (keep_b, send_b))
    put(grads[:, half:], 3 * small, 0, (keep_b, send_b))


def bundle_grads(devices, place, fronts, backs, ones, attended, context, kv):
    width = ones[0].shape[1]
    vmem = pl.BlockSpec(memory_space=pltpu.VMEM)
    return pl.pallas_call(
        functools.partial(bundle_body, devices),
        in_specs=[pl.BlockSpec(memory_space=pltpu.SMEM)] + [vmem] * 11,
        out_specs=[vmem] * 4,
        out_shape=[jax.ShapeDtypeStruct((devices // 2, width // devices, width // 2), BF16)] * 4,
        name="bundle", cost_estimate=FREE,
    )(place, *fronts, *backs, *ones, attended, context, kv)


def front_body(width_block, place, x0, x1, x2, x3, g0, g1, g2, g3, cosine, sine, wq, wk, wv,
               time_row, context, ck, cv,
               queries, pair, rows, low, nrm_own, nrm_away, norms, means, inverses,
               time_scaled, time_low, time_keys, time_values, kv, wide):
    size, part = x0.shape
    for r, (x, g) in enumerate(((x0, g0), (x1, g1), (x2, g2), (x3, g3))):
        start = pl.multiple_of((place[0] ^ r) * part, 128)
        wide[:, pl.ds(start, part)] = x[...]
        norms[:, pl.ds(start, part)] = g[...]
    share = size // 4
    rows[...] = wide[pl.ds(pl.multiple_of(place[0] * share, share), share), :]
    values = wide[...].astype(F32)
    mean = jnp.mean(values, -1, keepdims=True)
    centred = values - mean
    inverse = lax.rsqrt(jnp.mean(centred * centred, -1, keepdims=True) + 1e-05)
    means[...] = mean
    inverses[...] = inverse
    normed = (centred * inverse * norms[0:1, :] + norms[1:2, :]).astype(BF16)
    low[...] = normed
    half = HEAD_SIZE // 2

    def turned(weight):
        return dot_nn(normed, weight[...]).T

    def rotated(block, dest, scale):
        for h in range(part // HEAD_SIZE):
            a = block[h * HEAD_SIZE : h * HEAD_SIZE + half, :]
            b = block[h * HEAD_SIZE + half : (h + 1) * HEAD_SIZE, :]
            dest[h * HEAD_SIZE : h * HEAD_SIZE + half, :] = (
                (a * cosine[...] - b * sine[...]) * scale
            ).astype(BF16)
            dest[h * HEAD_SIZE + half : (h + 1) * HEAD_SIZE, :] = (
                (b * cosine[...] + a * sine[...]) * scale
            ).astype(BF16)

    scaled, _ = normalize(jnp.broadcast_to(time_row[...].astype(F32), (8, 4 * part)))
    time_scaled[...] = scaled[:1, :]
    made = (scaled * norms[0:1, :] + norms[1:2, :]).astype(BF16)
    time_low[...] = made[:1, :].astype(F32)
    time_keys[...] = dot_nn(made, wk[...]).astype(BF16).astype(F32).T[:, :1]
    time_values[...] = dot_nn(made, wv[...]).astype(BF16).astype(F32).T[:, :1]
    count = context.shape[0]
    kv[:count, :] = dot_nn(context[...], ck[...]).astype(BF16)
    kv[count:, :] = dot_nn(context[...], cv[...]).astype(BF16)
    rotated(turned(wk), pair.at[0], 1.0)
    pair[1] = turned(wv).astype(BF16)
    rotated(turned(wq), queries, 1.0 / math.sqrt(HEAD_SIZE))
    deal_rows(normed.T, width_block, place[1], nrm_own, nrm_away)


def front(devices, place, parts, norm_parts, tables, wq, wk, wv, time_row, context, ck, cv):
    size, part = parts[0].shape
    width = 4 * part
    low = lambda *s: jax.ShapeDtypeStruct(s, BF16)
    wide = lambda *s: jax.ShapeDtypeStruct(s, F32)
    vmem = pl.BlockSpec(memory_space=pltpu.VMEM)
    return pl.pallas_call(
        functools.partial(front_body, width // devices),
        in_specs=[pl.BlockSpec(memory_space=pltpu.SMEM)] + [vmem] * 17,
        out_specs=[vmem] * 14,
        out_shape=[low(part, size), low(2, part, size), low(size // 4, width), low(size, width),
                   low(width // 2, size), low(width // 2, size), wide(6, width),
                   wide(size, 1), wide(size, 1), wide(1, width), wide(1, width), wide(part, 1),
                   wide(part, 1), low(2 * context.shape[0], part)],
        scratch_shapes=[pltpu.VMEM((size, width), BF16)],
        cost_estimate=FREE, name="front",
    )(place, *parts, *norm_parts, *tables, wq, wk, wv, time_row, context, ck, cv)


def per_device(
    frames,
    segment,
    time_token,
    context,
    gain_attn,
    bias_attn,
    gain_cross,
    bias_cross,
    gain_ffn,
    bias_ffn,
    w_query,
    w_key,
    w_value,
    w_out,
    c_query,
    c_key,
    c_value,
    c_out,
    w_gate,
    w_up,
    w_down,
    out_grad,
):
    local_rows = frames.shape[0]
    local_width = frames.shape[1]
    model_width = w_query.shape[0]
    head_cols = w_query.shape[1]
    heads = head_cols // HEAD_SIZE
    number_of_frames = lax.axis_size("seq") * local_rows
    row_length = min(max(ROW_MIN, 64 * lax.axis_size("seq")), number_of_frames)
    first_frame = lax.axis_index("seq") * local_rows
    own_start = lax.axis_index("tensor") * local_width

    def own_cols(value):
        return lax.dynamic_slice_in_dim(value, own_start, local_width, value.ndim - 1)

    place = lax.axis_index("tensor")
    share = local_rows // 4

    def row_block(value, index):
        return rows_of(value, index * share, share)

    column = lax.axis_index("seq") % 2
    frame_parts_near = gather_near(frames)
    norm_parts = gather_near(
        jnp.stack([gain_attn, bias_attn, gain_cross, bias_cross, gain_ffn, bias_ffn])
    )
    clip_starts, frame_positions = frame_clip_labels(segment, row_length)
    own_labels = lax.dynamic_slice_in_dim(clip_starts, first_frame, local_rows)
    own_positions = lax.dynamic_slice_in_dim(frame_positions, first_frame, local_rows)
    blanks = jnp.full((local_rows,), -1, jnp.int32)
    key_labels = lax.dynamic_slice_in_dim(
        jnp.concatenate([blanks, clip_starts, blanks]), first_frame, 3 * local_rows
    )
    spans = jnp.concatenate(
        [tile_ranges(own_labels, key_labels), place.astype(jnp.int32).reshape(1)]
    )
    places = jnp.stack([column, place]).astype(jnp.int32)
    label_row, label_column = own_labels[None, :], key_labels[:, None]
    row_index = first_frame // row_length
    time_row = lax.dynamic_slice_in_dim(time_token, row_index, 1, 0)
    row_context = lax.dynamic_slice_in_dim(context, row_index, 1, 0)[0]
    context_rows = row_context.shape[0]
    tables = rotary_tables(own_positions)
    score_scale = 1.0 / math.sqrt(HEAD_SIZE)
    all_heads = model_width // HEAD_SIZE

    (
        queries, both, frame_rows, frame_normed, one_own_half, one_away_half, norms, means_one,
        inverse_one, scaled_time, time_normed, time_keys, time_values, context_kv,
    ) = front(
        lax.axis_size("seq"), jnp.flip(places), frame_parts_near, norm_parts, tables, w_query,
        w_key, w_value, time_row, row_context, c_key, c_value,
    )
    both, out_pair = meeting(both, swap(after(out_grad, frame_parts_near[2]), "seq", 1))
    grad_both = jnp.stack([out_grad, out_pair])
    behind, ahead = shift(both, "seq", 1), shift(both, "seq", -1)
    query_late, out_late = after((c_query, c_out), (frame_parts_near[2], norm_parts[2]))
    query_far, out_far = swap(query_late, "tensor", 2), swap(out_late, "tensor", 2)
    state = attend_near(spans, queries, both, time_keys, time_values, label_row, label_column)
    behind, ahead, query_far, out_far, *state = meeting(
        behind, ahead, query_far, out_far, *state
    )
    query_own, out_own, context_late = after((c_query, c_out, context_kv), behind)
    weights_near = [
        swap(value, "tensor", 1) for value in (query_own, query_far, out_own, out_far)
    ]
    kv_far = swap(context_late, "tensor", 2)
    attended, log_totals, one_away, one_own, one_low = attend_far(
        spans, queries, behind, ahead, label_row, label_column, w_out, state
    )
    one_away, one_low, kv_far, *weights_near = meeting(one_away, one_low, kv_far, *weights_near)
    kv_both = jnp.concatenate([context_kv, kv_far], 0)
    kv_other = swap(kv_both, "tensor", 1)
    kv_rows = context_kv.shape[0]
    kv_parts = (context_kv, kv_other[:kv_rows], kv_far, kv_other[kv_rows:])
    query_parts = (c_query, weights_near[0], query_far, weights_near[1])
    out_parts = (c_out, weights_near[2], out_far, weights_near[3])
    one_got, _, one_far = scatter_near(one_away, one_low)
    (
        front_rows, cross_queries, residual_one, residual_two, normed_share, flip_own, flip_away,
    ) = cross_forward(
        lax.axis_size("seq"), places, frame_rows, one_own, one_got, one_far, norms,
        query_parts, kv_parts, out_parts,
    )
    grad_far = swap(after(grad_both, one_far), "tensor", 2)
    normed_share, normed_got, grad_far = meeting(
        normed_share, swap(after(one_away_half, one_low), "seq", 1), grad_far
    )
    grad_late, grad_far_late = after((grad_both, grad_far), normed_share)
    grad_mate, grad_far_mate = swap(grad_late, "tensor", 1), swap(grad_far_late, "tensor", 1)
    grad_parts = (grad_both, grad_mate, grad_far, grad_far_mate)
    three_parts = gather_near(normed_share)
    flip_got = swap(after(flip_away, normed_share), "seq", 1)
    front_far = swap(after(front_rows, three_parts[3]), "tensor", 2)
    devices = lax.axis_size("seq")
    (
        hidden_a, hidden_own_a, hidden_away_a, gate_a, lifted_a, normed_three, grad_near, grad_pair,
        ffn_total,
    ) = ffn(devices, places, 0, (*three_parts, *grad_parts), w_gate, w_up, w_down)
    ffn_total, flip_got = meeting(ffn_total, flip_got)
    flip_both = jnp.stack([flip_own, flip_got])
    flip_far = swap(flip_both, "tensor", 2)
    hidden_got_a, gate_got_a = swap(hidden_away_a, "seq", 1), swap(gate_a, "seq", 1)
    hidden_b, hidden_own_b, hidden_away_b, gate_b, lifted_b, three_away, three_own, three_low = ffn(
        devices, places, 1, (normed_three, grad_near, ffn_total), w_gate, w_up, w_down
    )
    three_away, three_low, flip_far, front_far, hidden_got_a = meeting(
        three_away, three_low, flip_far, front_far, hidden_got_a
    )
    three_got, _, three_far = scatter_near(three_away, three_low)
    hidden_got_b = swap(after(hidden_away_b, three_low), "seq", 1)
    lifted_got_a = swap(after(lifted_a, three_low), "seq", 1)
    flip_late, flip_far_late, gate_late = after((flip_both, flip_far, gate_b), three_far)
    flip_mate, flip_far_mate = swap(flip_late, "tensor", 1), swap(flip_far_late, "tensor", 1)
    gate_got_b = swap(gate_late, "seq", 1)
    front_both = jnp.stack([front_rows, front_far])
    back_rows, kv_grad, norm_vectors, grad_one = cross_backward(
        three_own, three_got, three_far, grad_near, residual_one, residual_two, norms,
        query_parts, kv_parts, out_parts, cross_queries,
    )
    grad_one, gate_got_a, hidden_got_b, flip_mate, flip_far_mate = meeting(
        grad_one, gate_got_a, hidden_got_b, flip_mate, flip_far_mate
    )
    count = lax.axis_size("seq")
    level_side = ((lax.axis_index("seq") >> 1) % 2).astype(jnp.int32).reshape(1)
    rows = model_width // count

    def traded(dealt):
        keep, send = [value.reshape(count // 4, rows, -1) for value in dealt]
        return keep, swap(send, "seq", 2)

    down_keep, down_got = traded(
        meet_rows(
            rows, level_side, (hidden_own_a, hidden_got_a, hidden_own_b, hidden_got_b),
            (grad_near, grad_pair),
        )
    )
    context_parts = quarters(kv_grad, 1)
    context_got = swap(jnp.concatenate([context_parts[1], context_parts[3]], 0), "tensor", 1)
    one_far_rows, down_keep = meeting(swap(grad_one, "tensor", 2), down_keep)
    one_parts = (
        grad_one, swap(grad_one, "tensor", 1), one_far_rows, swap(one_far_rows, "tensor", 1)
    )
    *one_parts, front_other, context_got, lifted_got_a = meeting(
        *one_parts, swap(after(front_both, grad_one), "tensor", 1), context_got, lifted_got_a
    )
    context_low = (
        context_parts[2].astype(F32) + context_got[context_parts[2].shape[0] :].astype(F32)
    ).astype(BF16)
    context_far = swap(context_low, "tensor", 2)
    back_far = swap(after(back_rows, one_parts[3]), "tensor", 2)
    lifted_got_b = swap(after(lifted_b, grad_one), "seq", 1)
    query_grad, to_prev, kept, to_next, time_grads = attend_back(
        spans, queries, (behind, both, ahead), time_keys, time_values, label_row, label_column,
        w_out, attended, log_totals, one_parts,
    )
    to_prev, to_next, back_far, gate_got_b, lifted_got_b, down_got, context_far = meeting(
        to_prev, to_next, back_far, gate_got_b, lifted_got_b, down_got, context_far
    )
    from_next, from_prev = shift(to_prev, "seq", -1), shift(to_next, "seq", 1)
    down_keep, down_got = halve(added(down_keep, down_got).astype(BF16), 2)
    flip_near = (flip_both, flip_mate, flip_far, flip_far_mate)
    first_keep, first_got = traded(
        meet_cols(
            rows, level_side, flip_near,
            after((gate_a, gate_got_a, lifted_a, lifted_got_a), to_prev),
        )
    )
    back_both = jnp.stack([back_rows, back_far])
    back_other = swap(back_both, "tensor", 1)
    context_own = (
        context_parts[0].astype(F32)
        + context_got[: context_far.shape[0]].astype(F32)
        + context_far.astype(F32)
    )
    keep_a, send_a, keep_b, send_b = bundle_grads(
        count, places, (front_both, front_other), (back_both, back_other), one_parts, attended,
        row_context,
        context_own.astype(BF16),
    )
    from_next, from_prev, down_got, send_a, send_b = meeting(
        from_next, from_prev, down_got, send_a, send_b
    )
    got_a = swap(send_a, "seq", 1)
    raw, last_away, last_own, last_low = tail(
        places[1:], query_grad, kept, from_next, from_prev, tables, w_query, w_key, w_value,
        time_grads,
    )
    last_got = swap(last_away, "tensor", 1)
    raw_got = swap(raw, "seq", 1)
    last_sum = (
        last_low.astype(F32) + last_got[local_rows:].astype(F32)
    ).astype(BF16)
    second_keep, second_got = traded(
        meet_cols(
            rows, level_side, flip_near,
            after((gate_b, gate_got_b, lifted_b, lifted_got_b), last_away),
        )
    )
    last_sum, first_got, raw_got = meeting(last_sum, first_got, raw_got)
    first_keep, first_got = halve(added(first_keep, first_got).astype(BF16), 2)
    last_far = swap(last_sum, "tensor", 2)
    frame_grad = last_own + last_got[:local_rows].astype(F32) + last_far.astype(F32)

    time_late, means_late, inverse_late, vectors_late = after(
        (time_grads, means_one, inverse_one, norm_vectors), last_far
    )
    time_grad = sum(
        jnp.einsum("of,df->od", time_late[i : i + 1].astype(BF16), w, preferred_element_type=F32)
        for i, w in enumerate((w_key, w_value))
    )
    own_scaled = (frames.astype(F32) - means_late) * inverse_late
    scaled_grad = frame_grad * gain_attn[None]
    sums = jnp.concatenate(
        [
            jnp.sum(scaled_grad, -1),
            jnp.sum(scaled_grad * own_scaled, -1),
            time_grad[0],
            vectors_late.reshape(-1),
        ]
    )[None]
    sums = sums + swap(sums, "tensor", 1)
    sums = sums + swap(sums, "tensor", 2)
    sums, first_got, second_got = meeting(sums, first_got, second_got)
    second_keep, second_got = halve(added(second_keep, second_got).astype(BF16), 2)
    plain = sums[0, :local_rows, None] / model_width
    cross = sums[0, local_rows : 2 * local_rows, None] / model_width
    vectors = own_cols(sums[0, 2 * local_rows :].reshape(5, model_width))
    attend_full = ordered(*[after(one_parts, from_next)[i] for i in (0, 2, 1, 3)], 0)
    d_frames = own_cols(attend_full).astype(F32) + inverse_late * (
        scaled_grad - plain - own_scaled * cross
    )
    d_gain_attn = jnp.sum(frame_grad * own_scaled, 0) + vectors[0] * own_cols(scaled_time)[0]
    d_bias_attn = jnp.sum(frame_grad, 0) + vectors[0]

    time_column = time_normed.T

    normed_pair = (one_own_half, normed_got)
    grad_down = halve_end(down_keep, down_got, 3)
    raw_pair = (raw[: 3 * head_cols], raw_got[: 3 * head_cols])
    time_got = raw_got[3 * head_cols : 3 * head_cols + 2, :head_cols].astype(F32)
    time_both = (time_grads + time_got).reshape(1, 2 * head_cols)
    own_time_rows = lax.dynamic_index_in_dim(
        time_column.reshape(count // 2, 2, -1), column, 1, False
    ).reshape(-1, 1)
    outer = own_time_rows * jnp.concatenate([jnp.zeros((1, head_cols), F32), time_both], 1)
    blocks = sum(
        jnp.einsum("dn,fn->df", r, c, preferred_element_type=F32)
        for r, c in zip(normed_pair, raw_pair)
    )
    blocks = (blocks + outer).astype(BF16).reshape(count // 2, rows, 3 * head_cols)
    heads_keep, heads_got = halve(blocks, 1)
    got_b = swap(after(send_b, from_next), "seq", 1)
    down_away, down_own, down_low = down_parts(after(hidden_a, sums), hidden_b, w_down)
    branch_got, _, branch_far = scatter_near(down_away, down_low)
    heads_got, got_a, got_b, branch_far = meeting(heads_got, got_a, got_b, branch_far)
    left_keep, left_got = halve(added(keep_a, got_a).astype(BF16), 1)
    right_keep, right_got = halve(added(keep_b, got_b).astype(BF16), 1)
    heads_next = added(heads_keep, heads_got).astype(BF16)
    heads_keep, heads_got = halve(heads_next, 2)
    left_got, right_got, second_got = meeting(left_got, right_got, second_got)
    last_next = added(right_keep, right_got)
    left_keep, left_got = halve(added(left_keep, left_got).astype(BF16), 2)
    right_keep, right_got = halve(last_next.astype(BF16), 2)
    heads_got, left_got, right_got = meeting(heads_got, left_got, right_got)
    block_rows = (
        residual_two + down_own + branch_got[:share].astype(F32) + branch_far.astype(F32)
    ).astype(BF16)
    block_cols = rows_to_cols(
        *[
            lax.dynamic_slice_in_dim(block_rows, (place ^ r) * local_width, local_width, 1)
            for r in range(4)
        ],
        last_next,
    )
    block_out = jnp.concatenate([row_block(block_cols, place ^ b) for b in range(4)], 0)
    first, second = halve_end(first_keep, first_got, 3), halve_end(second_keep, second_got, 3)
    units = first.shape[1] // 2
    grad_gate_w = jnp.concatenate([first[:, :units], second[:, :units]], 1)
    grad_up_w = jnp.concatenate([first[:, units:], second[:, units:]], 1)
    small = jnp.stack(
        [d_gain_attn, d_bias_attn, vectors[3], vectors[4], vectors[1], vectors[2]]
    ).reshape(6, devices, -1).transpose(1, 0, 2)
    small = small.reshape(count // 4, 2, 2, 6, -1).swapaxes(1, 2).reshape(count, 6, -1)
    small = after(small, last_next)
    bits = [1, 0] + list(range(2, count.bit_length() - 1))
    for bit in bits:
        small = added(*halve(small, bit))
    small = small[0]
    heads_sum = halve_end(heads_keep, heads_got, 3)
    left, right = halve_end(left_keep, left_got, 3), halve_end(right_keep, right_got, 3)
    part, rows = head_cols // count, model_width // count
    grad_c_query = left[:, :head_cols]
    grad_c_key, grad_c_value = left[: rows // 2, head_cols:], left[rows // 2 :, head_cols:]
    grad_c_out = jnp.concatenate([right[:part], right[part : 2 * part]], 1)
    grad_w_out = jnp.concatenate([right[2 * part : 3 * part], right[3 * part :]], 1)
    grad_w_query, grad_w_key, grad_w_value = (
        heads_sum[:, i * head_cols : (i + 1) * head_cols] for i in range(3)
    )
    return (
        block_out,
        d_frames,
        small[0],
        small[1],
        small[2],
        small[3],
        small[4],
        small[5],
        grad_w_query,
        grad_w_key,
        grad_w_value,
        grad_w_out,
        grad_c_query,
        grad_c_key,
        grad_c_value,
        grad_c_out,
        grad_gate_w,
        grad_up_w,
        grad_down,
    )


def solution(mesh):
    return jax.shard_map(
        per_device,
        mesh=mesh,
        in_specs=(
            P("seq", "tensor"),
            P(),
            P(),
            P(),
            P("tensor"),
            P("tensor"),
            P("tensor"),
            P("tensor"),
            P("tensor"),
            P("tensor"),
            P(None, "tensor"),
            P(None, "tensor"),
            P(None, "tensor"),
            P("tensor", None),
            P(None, "tensor"),
            P(None, "tensor"),
            P(None, "tensor"),
            P("tensor", None),
            P(None, "tensor"),
            P(None, "tensor"),
            P("tensor", None),
            P("seq", "tensor"),
        ),
        out_specs=(
            P("seq", "tensor"),
            P("seq", "tensor"),
            P(("tensor", "seq")),
            P(("tensor", "seq")),
            P(("tensor", "seq")),
            P(("tensor", "seq")),
            P(("tensor", "seq")),
            P(("tensor", "seq")),
            P("seq", "tensor"),
            P("seq", "tensor"),
            P("seq", "tensor"),
            P(("tensor", "seq"), None),
            P("seq", "tensor"),
            P("seq", "tensor"),
            P("seq", "tensor"),
            P(("tensor", "seq"), None),
            P("seq", "tensor"),
            P("seq", "tensor"),
            P(("tensor", "seq"), None),
        ),
        check_vma=False,
    )
```

```python
import functools
import math

import jax
import jax.numpy as jnp
from jax import lax
from jax.experimental import pallas as pl
from jax.experimental.pallas import tpu as pltpu
from jax.sharding import PartitionSpec as P

HEAD_SIZE = 64
ROW_MIN = 2048
TILE = 256
BF16 = jnp.bfloat16
F32 = jnp.float32


def meeting(*values):
    return lax.optimization_barrier(values)


def after(value, token):
    return lax.optimization_barrier((value, token))[0]


def swap(value, axis, by):
    return lax.ppermute(value, axis, [(i, i ^ by) for i in range(lax.axis_size(axis))])


def shift(value, axis, by):
    peers = lax.axis_size(axis)
    pairs = [(i, i + by) for i in range(peers) if 0 <= i + by < peers]
    return lax.ppermute(value, axis, pairs)


def tensor_place():
    place = lax.axis_index("tensor")
    return place // 2, place % 2


def ordered(own, far, mate, far_mate, axis):
    side, core = tensor_place()
    near = (jnp.where(core == 0, own, mate), jnp.where(core == 0, mate, own))
    away = (jnp.where(core == 0, far, far_mate), jnp.where(core == 0, far_mate, far))
    low = [jnp.where(side == 0, n, a) for n, a in zip(near, away)]
    high = [jnp.where(side == 0, a, n) for n, a in zip(near, away)]
    return jnp.concatenate(low + high, axis)


def gather_near(own):
    far = swap(own, "tensor", 2)
    return own, swap(own, "tensor", 1), far, swap(far, "tensor", 1)


def gather_staged(own, first, second):
    far = swap(after(own, first), "tensor", 2)
    far, late = after((far, own), second)
    return own, swap(late, "tensor", 1), far, swap(far, "tensor", 1)


def gather(own, axis):
    own, mate, far, far_mate = gather_near(own)
    return ordered(own, far, mate, far_mate, axis)


def scatter_near(away, low):
    got = swap(away, "tensor", 1)
    total = (low.astype(F32) + got[low.shape[0] :].astype(F32)).astype(BF16)
    return got, total, swap(total, "tensor", 2)


def rows_to_cols(own, mate, far, far_mate, later):
    width = own.shape[1]
    got = after(swap(jnp.concatenate([far, far_mate], 1), "tensor", 2), later)
    other = swap(jnp.concatenate([mate, got[:, width:]], 0), "tensor", 1)
    size = own.shape[0]
    return jnp.concatenate([own, other[:size], got[:, :width], other[size:]], 0)


def quarters(value, axis):
    return jnp.split(value, 4, axis)


def own_blocks(near):
    return jnp.concatenate([quarters(value, 1)[r] for r, value in enumerate(near)], 0)


def trade(value, start, done):
    return after(swap(after(value, start), "seq", 1), done)


def halve(blocks, bit):
    count, rows, cols = blocks.shape
    side = (lax.axis_index("seq") >> bit) % 2
    parts = blocks.reshape(count // 2, 2, rows, cols)
    send = lax.dynamic_index_in_dim(parts, 1 - side, 1, False)
    keep = lax.dynamic_index_in_dim(parts, side, 1, False)
    return keep, swap(send, "seq", 1 << bit)


def added(keep, got):
    return keep.astype(F32) + got.astype(F32)


def halve_all(blocks, bit):
    while blocks.shape[0] > 1:
        blocks = added(*halve(blocks.astype(BF16), bit))
        bit += 1
    return blocks[0].astype(F32)


def halve_end(keep, got, bit):
    return halve_all(added(keep, got), bit)


def frame_clip_labels(segment, row_length):
    frame_index = jnp.arange(segment.shape[0], dtype=jnp.int32)
    border = (frame_index % row_length == 0) | (segment != jnp.roll(segment, 1))
    clip_starts = lax.cummax(jnp.where(border, frame_index, 0), axis=0)
    return (clip_starts, (frame_index - clip_starts + 1).astype(jnp.float32))


def tile_ranges(q_labels, key_labels):
    q = q_labels.reshape(-1, TILE)
    k = key_labels.reshape(-1, TILE)
    meets = (k[None, :, 0] <= q[:, None, -1]) & (k[None, :, -1] >= q[:, None, 0])
    index = jnp.arange(k.shape[0], dtype=jnp.int32)[None]
    low = jnp.min(jnp.where(meets, index, k.shape[0]), 1)
    high = jnp.max(jnp.where(meets, index + 1, 0), 1)
    return jnp.stack([low, high], 1).reshape(-1)

def head_rows(g):
    return slice(g * HEAD_SIZE, (g + 1) * HEAD_SIZE)

def fill_natural(dest, refs, which):
    size = refs[0].shape[2]
    for part, ref in enumerate(refs):
        dest[part * size : (part + 1) * size, :] = ref[which].T


def fill_tiles(dest, refs, which):
    pieces = refs[0].shape[2] // TILE
    for part, ref in enumerate(refs):
        for piece in range(pieces):
            dest[part * pieces + piece] = ref[which, :, piece * TILE : (piece + 1) * TILE]


def relative(place, r, size):
    return pl.ds(pl.multiple_of((place ^ r) * size, size), size)


def absorb(state, start, stop, base, q, cols, lab, klab, keys, vals):
    group = q.shape[0] // HEAD_SIZE

    def step(j, state):
        seen = klab[pl.ds(pl.multiple_of(j * TILE, TILE), TILE), :] == lab
        at = pl.ds(pl.multiple_of((j - base) * TILE, TILE), TILE)
        fresh = []
        for g in range(group):
            top, total, acc = state[3 * g : 3 * g + 3]
            s = dot_nn(keys[at, head_rows(g)], q[head_rows(g), cols])
            s = jnp.where(seen, s, -1e30)
            new = jnp.maximum(top, jnp.max(s, 0, keepdims=True))
            fade = jnp.exp(top - new)
            p = jnp.exp(s - new)
            total = total * fade + jnp.sum(p, 0, keepdims=True)
            acc = acc * fade + dot_nn(vals[j - base, head_rows(g), :], p.astype(BF16))
            fresh += [new, total, acc]
        return tuple(fresh)

    return lax.fori_loop(start, stop, step, tuple(state))


def near_body(span, q, kv, tk, tv, qlab, klab, tops, totals, mix, keys, vals):
    rows, size = q.shape
    pieces = size // TILE
    fill_natural(keys, (kv,), 0)
    fill_tiles(vals, (kv,), 1)
    for tile in range(pieces):
        cols = slice(tile * TILE, (tile + 1) * TILE)
        state = []
        for g in range(rows // HEAD_SIZE):
            part = q[head_rows(g), cols].astype(F32)
            top = jnp.sum(part * tk[head_rows(g), :], 0, keepdims=True)
            state += [
                top,
                jnp.ones_like(top),
                jnp.broadcast_to(tv[head_rows(g), :], (HEAD_SIZE, TILE)),
            ]
        start = jnp.maximum(span[2 * tile], pieces)
        stop = jnp.minimum(span[2 * tile + 1], 2 * pieces)
        state = absorb(state, start, stop, pieces, q, cols, qlab[:, cols], klab, keys, vals)
        for g in range(rows // HEAD_SIZE):
            tops[g : g + 1, cols], totals[g : g + 1, cols], mix[head_rows(g), cols] = state[
                3 * g : 3 * g + 3
            ]


def far_body(span, q, kv0, kv2, qlab, klab, w_out, tops, totals, mix,
             out, lse, away, own, low, keys0, keys2, vals0, vals2):
    rows, size = q.shape
    pieces = size // TILE
    for kv, keys, vals in ((kv0, keys0, vals0), (kv2, keys2, vals2)):
        fill_natural(keys, (kv,), 0)
        fill_tiles(vals, (kv,), 1)
    for tile in range(pieces):
        cols = slice(tile * TILE, (tile + 1) * TILE)
        lab = qlab[:, cols]
        state = []
        for g in range(rows // HEAD_SIZE):
            state += [tops[g : g + 1, cols], totals[g : g + 1, cols], mix[head_rows(g), cols]]
        stop = jnp.minimum(span[2 * tile + 1], pieces)
        state = absorb(state, span[2 * tile], stop, 0, q, cols, lab, klab, keys0, vals0)
        start = jnp.maximum(span[2 * tile], 2 * pieces)
        state = absorb(
            state, start, span[2 * tile + 1], 2 * pieces, q, cols, lab, klab, keys2, vals2
        )
        for g in range(rows // HEAD_SIZE):
            top, total, acc = state[3 * g : 3 * g + 3]
            out[head_rows(g), cols] = (acc / total).astype(BF16)
            lse[g : g + 1, cols] = top + jnp.log(total)
    place = span[2 * pieces]
    share = own.shape[0]

    def sent(r):
        return dot_tn(out[:, relative(place, r, share)], w_out[...])

    away[:share, :] = sent(1).astype(BF16)
    away[share:, :] = sent(3).astype(BF16)
    low[...] = sent(2).astype(BF16)
    own[...] = sent(0)


def backward_body(span, q, kv0, kv1, kv2, tk, tv, qlab, klab, w_out, out, lse,
                  g0, g1, g2, g3, dq, to_prev, kept, to_next, times,
                  og, keys, vals, tkeys, ak, av, dtk, dtv):
    rows, size = q.shape
    group = rows // HEAD_SIZE
    pieces = size // TILE
    share = g0.shape[0]
    for r, ref in enumerate((g0, g1, g2, g3)):
        og[:, relative(span[2 * pieces], r, share)] = dot_nt(w_out[...], ref[...]).astype(BF16)
    fill_natural(keys, (kv0, kv1, kv2), 0)
    fill_natural(vals, (kv0, kv1, kv2), 1)
    fill_tiles(tkeys, (kv0, kv1, kv2), 0)
    ak[...] = jnp.zeros_like(ak)
    av[...] = jnp.zeros_like(av)
    for tile in range(pieces):
        cols = slice(tile * TILE, (tile + 1) * TILE)
        lab = qlab[:, cols]
        state, norms, deltas = [], [], []
        for g in range(group):
            hr = head_rows(g)
            qf = q[hr, cols].astype(F32)
            gf = og[hr, cols].astype(F32)
            norm = lse[g : g + 1, cols]
            delta = jnp.sum(gf * out[hr, cols].astype(F32), 0, keepdims=True)
            pt = jnp.exp(jnp.sum(qf * tk[hr, :], 0, keepdims=True) - norm)
            st = pt * (jnp.sum(gf * tv[hr, :], 0, keepdims=True) - delta)
            gk = jnp.sum(qf * st, 1, keepdims=True)
            gv = jnp.sum(gf * pt, 1, keepdims=True)
            if tile == 0:
                dtk[hr, :] = gk
                dtv[hr, :] = gv
            else:
                dtk[hr, :] += gk
                dtv[hr, :] += gv
            state.append(tk[hr, :] * st)
            norms.append(norm)
            deltas.append(delta)

        def step(j, state):
            start = pl.multiple_of(j * TILE, TILE)
            seen = klab[pl.ds(start, TILE), :] == lab
            fresh = []
            for g in range(group):
                hr = head_rows(g)
                s = dot_nn(keys[pl.ds(start, TILE), hr], q[hr, cols])
                p = jnp.exp(jnp.where(seen, s, -1e30) - norms[g])
                m = dot_nn(vals[pl.ds(start, TILE), hr], og[hr, cols])
                ds = (p * (m - deltas[g])).astype(BF16)
                av[j, hr, :] += dot_nt(og[hr, cols], p.astype(BF16))
                ak[j, hr, :] += dot_nt(q[hr, cols], ds)
                fresh.append(state[g] + dot_nn(tkeys[j, hr, :], ds))
            return tuple(fresh)

        state = lax.fori_loop(span[2 * tile], span[2 * tile + 1], step, tuple(state))
        for g in range(group):
            dq[head_rows(g), cols] = state[g]
    for at, column in ((0, dtk), (1, dtv)):
        spread = jnp.broadcast_to(column[...], (rows, 2 * HEAD_SIZE))
        times[at : at + 1, :] = spread.T[:1, :]
    for part, dest in enumerate((to_prev, kept, to_next)):
        for piece in range(pieces):
            at = slice(piece * TILE, (piece + 1) * TILE)
            dest[0, :, at] = ak[part * pieces + piece].astype(dest.dtype)
            dest[1, :, at] = av[part * pieces + piece].astype(dest.dtype)


def attend_near(span, q, kv, tk, tv, qlab, klab):
    cols, size = q.shape
    wide = lambda *dims: jax.ShapeDtypeStruct(dims, F32)
    vmem = pl.BlockSpec(memory_space=pltpu.VMEM)
    return pl.pallas_call(
        near_body,
        in_specs=[pl.BlockSpec(memory_space=pltpu.SMEM)] + [vmem] * 6,
        out_specs=[vmem] * 3,
        out_shape=[wide(cols // HEAD_SIZE, size), wide(cols // HEAD_SIZE, size), wide(cols, size)],
        scratch_shapes=[pltpu.VMEM((size, cols), BF16), pltpu.VMEM((size // TILE, cols, TILE), BF16)],
        name="attend_near", cost_estimate=FREE,
    )(span, q, kv, tk, tv, qlab, klab)


def attend_far(span, q, behind, ahead, qlab, klab, w_out, state):
    cols, size = q.shape
    share, width = size // 4, w_out.shape[1]
    low = lambda *dims: jax.ShapeDtypeStruct(dims, BF16)
    wide = lambda *dims: jax.ShapeDtypeStruct(dims, F32)
    vmem = pl.BlockSpec(memory_space=pltpu.VMEM)
    keys = pltpu.VMEM((size, cols), BF16)
    vals = pltpu.VMEM((size // TILE, cols, TILE), BF16)
    return pl.pallas_call(
        far_body,
        in_specs=[pl.BlockSpec(memory_space=pltpu.SMEM)] + [vmem] * 9,
        out_specs=[vmem] * 5,
        out_shape=[low(cols, size), wide(cols // HEAD_SIZE, size), low(2 * share, width),
                   wide(share, width), low(share, width)],
        scratch_shapes=[keys, keys, vals, vals],
        name="attend_far", cost_estimate=FREE,
    )(span, q, behind, ahead, qlab, klab, w_out, *state)


def attend_back(span, q, kvs, tk, tv, qlab, klab, w_out, out, lse, grads):
    cols, size = q.shape
    tiles = 3 * size // TILE
    low = lambda *dims: jax.ShapeDtypeStruct(dims, BF16)
    wide = lambda *dims: jax.ShapeDtypeStruct(dims, F32)
    vmem = pl.BlockSpec(memory_space=pltpu.VMEM)
    return pl.pallas_call(
        backward_body,
        in_specs=[pl.BlockSpec(memory_space=pltpu.SMEM)] + [vmem] * 15,
        out_specs=[vmem] * 5,
        out_shape=[wide(cols, size), low(2, cols, size), wide(2, cols, size), low(2, cols, size),
                   wide(2, cols)],
        scratch_shapes=[pltpu.VMEM((cols, size), BF16), pltpu.VMEM((3 * size, cols), BF16),
                        pltpu.VMEM((3 * size, cols), BF16), pltpu.VMEM((tiles, cols, TILE), BF16),
                        pltpu.VMEM((tiles, cols, TILE), F32), pltpu.VMEM((tiles, cols, TILE), F32),
                        pltpu.VMEM((cols, 1), F32), pltpu.VMEM((cols, 1), F32)],
        name="attend_back", cost_estimate=FREE,
    )(span, q, *kvs, tk, tv, qlab, klab, w_out, out, lse, *grads)


def tail_body(place, dq, kept, ahead, behind, cosine, sine, wq, wk, wv, times,
              raw, away, own, low, flipped):
    part, size = dq.shape
    half = HEAD_SIZE // 2

    def returned(block, base, scale):
        for h in range(part // HEAD_SIZE):
            a = block[h * HEAD_SIZE : h * HEAD_SIZE + half, :]
            b = block[h * HEAD_SIZE + half : (h + 1) * HEAD_SIZE, :]
            at = base + h * HEAD_SIZE
            raw[at : at + half, :] = ((a * cosine[...] + b * sine[...]) * scale).astype(BF16)
            raw[at + half : at + HEAD_SIZE, :] = (
                (b * cosine[...] - a * sine[...]) * scale
            ).astype(BF16)

    def whole(index):
        return kept[index] + ahead[index].astype(F32) + behind[index].astype(F32)

    returned(dq[...], 0, 1.0 / math.sqrt(HEAD_SIZE))
    returned(whole(0), part, 1.0)
    raw[2 * part : 3 * part, :] = whole(1).astype(BF16)
    raw[3 * part :, :] = jnp.zeros((16, size), BF16)
    raw[3 * part : 3 * part + 2, :part] = times[...].astype(BF16)
    flipped[...] = raw[: 3 * part, :].T

    def sent(r):
        at = relative(place[0], r, part)
        return sum(
            dot_nt(flipped[:, i * part : (i + 1) * part], weight[at, :])
            for i, weight in enumerate((wq, wk, wv))
        )

    away[:size, :] = sent(1).astype(BF16)
    away[size:, :] = sent(3).astype(BF16)
    low[...] = sent(2).astype(BF16)
    own[...] = sent(0)


def tail(place, dq, kept, ahead, behind, tables, wq, wk, wv, times):
    part, size = dq.shape
    low = lambda *dims: jax.ShapeDtypeStruct(dims, BF16)
    vmem = pl.BlockSpec(memory_space=pltpu.VMEM)
    return pl.pallas_call(
        tail_body,
        in_specs=[pl.BlockSpec(memory_space=pltpu.SMEM)] + [vmem] * 10,
        out_specs=[vmem] * 4,
        out_shape=[low(3 * part + 16, size), low(2 * size, part), jax.ShapeDtypeStruct((size, part), F32),
                   low(size, part)],
        scratch_shapes=[pltpu.VMEM((size, 3 * part), BF16)],
        name="tail", cost_estimate=FREE,
    )(place, dq, kept, ahead, behind, *tables, wq, wk, wv, times)


def rotary_tables(frame_positions):
    half_dim = HEAD_SIZE // 2
    frequency = jnp.exp(jnp.arange(half_dim, dtype=jnp.float32) * (-math.log(10000.0) / half_dim))
    angles = frequency[:, None] * frame_positions[None, :]
    return (jnp.cos(angles), jnp.sin(angles))


def rotate(rows, tables, sign=1.0):
    count, size = rows.shape
    halves = rows.reshape(count // HEAD_SIZE, 2, HEAD_SIZE // 2, size)
    cosine, sine = tables[0][None], tables[1][None] * sign
    first = halves[:, 0] * cosine - halves[:, 1] * sine
    second = halves[:, 1] * cosine + halves[:, 0] * sine
    return jnp.stack([first, second], 1).reshape(count, size)


def product(left, right):
    return jnp.dot(left, right, preferred_element_type=jnp.float32)


def inner_rows(left, right):
    return jnp.einsum("nd,nf->df", left, right, preferred_element_type=jnp.float32)


def back_project(gradient, weight):
    return jnp.einsum("nf,df->nd", gradient, weight, preferred_element_type=jnp.float32)


def by_feature(left, right):
    return jnp.einsum("nd,df->fn", left, right, preferred_element_type=jnp.float32)


def columns(weight, start, size):
    return lax.dynamic_slice_in_dim(weight, start, size, 1)


def rows_of(weight, start, size):
    return lax.dynamic_slice_in_dim(weight, start, size, 0)


def normalize(value_rows):
    means = jnp.mean(value_rows, -1, keepdims=True)
    centred = value_rows - means
    inverse = lax.rsqrt(jnp.mean(centred * centred, -1, keepdims=True) + 1e-05)
    return centred * inverse, inverse


def norm_backward(gradient, scaled, inverse, norm_gain):
    scaled_grad = gradient * norm_gain
    plain = jnp.mean(scaled_grad, -1, keepdims=True)
    cross = jnp.mean(scaled_grad * scaled, -1, keepdims=True)
    return inverse * (scaled_grad - plain - scaled * cross)


FREE = pl.CostEstimate(flops=1, transcendentals=0, bytes_accessed=1)


def dot_nn(left, right):
    return lax.dot_general(left, right, (((1,), (0,)), ((), ())), preferred_element_type=F32)


def dot_nt(left, right):
    return lax.dot_general(left, right, (((1,), (1,)), ((), ())), preferred_element_type=F32)


def dot_tn(left, right):
    return lax.dot_general(left, right, (((0,), (0,)), ((), ())), preferred_element_type=F32)


def head_weights(query, key, lanes, which):
    mine = jnp.where(lanes == which, query, jnp.zeros_like(query))
    scores = dot_nt(mine, key) * (1.0 / math.sqrt(HEAD_SIZE))
    weights = jnp.exp(scores - jnp.max(scores, -1, keepdims=True))
    return weights / jnp.sum(weights, -1, keepdims=True)


def pair_cols(refs, p, rows):
    ref = refs[p * 2 * HEAD_SIZE // refs[0].shape[1]]
    start = p * 2 * HEAD_SIZE % refs[0].shape[1]
    return ref[rows, start : start + 2 * HEAD_SIZE]


def cross_forward_body(width_block, place, rows, own, got, far, norms, q0, q1, q2, q3,
                       c0, c1, c2, c3, o0, o1, o2, o3,
                       front, queries, first, second, normed_three,
                       flip_own, flip_away):
    width = rows.shape[1]
    kv = (c0, c1, c2, c3)
    context_rows = c0.shape[0] // 2
    key_rows, value_rows = slice(0, context_rows), slice(context_rows, 2 * context_rows)
    lanes = lax.broadcasted_iota(jnp.int32, (rows.shape[0], 2 * HEAD_SIZE), 1) // HEAD_SIZE
    residual = (
        rows[...].astype(F32) + own[...] + got[...].astype(F32) + far[...].astype(F32)
    )
    first[...] = residual
    scaled, _ = normalize(residual)
    low = (scaled * norms[2:3, :] + norms[3:4, :]).astype(BF16)
    front[:, :width] = low
    part = width // 4
    for b, ref in enumerate((q0, q1, q2, q3)):
        queries[:, b * part : (b + 1) * part] = dot_nn(low, ref[...]).astype(BF16)
    for p in range(width // (2 * HEAD_SIZE)):
        cols = slice(p * 2 * HEAD_SIZE, (p + 1) * 2 * HEAD_SIZE)
        q, k, v = queries[:, cols], pair_cols(kv, p, key_rows), pair_cols(kv, p, value_rows)
        mixed = [dot_nn(head_weights(q, k, lanes, g).astype(BF16), v) for g in (0, 1)]
        front[:, width + cols.start : width + cols.stop] = jnp.where(lanes == 0, mixed[0], mixed[1]).astype(BF16)
    for b, ref in enumerate((o0, o1, o2, o3)):
        residual = residual + dot_nn(front[:, width + b * part : width + (b + 1) * part], ref[...])
    second[...] = residual
    scaled, _ = normalize(residual)
    low = (scaled * norms[4:5, :] + norms[5:6, :]).astype(BF16)
    normed_three[...] = low
    deal_rows(low.T, width_block, place[0], flip_own, flip_away)


def cross_forward(devices, place, rows, own, got, far, norms, query_parts, kv_parts, out_parts):
    size, width = rows.shape
    low = jax.ShapeDtypeStruct(rows.shape, BF16)
    both = jax.ShapeDtypeStruct((size, 2 * width), BF16)
    wide = jax.ShapeDtypeStruct(rows.shape, F32)
    flip = jax.ShapeDtypeStruct((width // 2, size), BF16)
    vmem = pl.BlockSpec(memory_space=pltpu.VMEM)
    block = pl.BlockSpec((size, width), lambda i: (0, 0))
    return pl.pallas_call(
        functools.partial(cross_forward_body, width // devices),
        grid=(1,),
        in_specs=[pl.BlockSpec(memory_space=pltpu.SMEM)] + [block] * 4 + [vmem] * 13,
        out_shape=[both, low, wide, wide, low, flip, flip],
        cost_estimate=FREE, name="cross",
    )(place, rows, own, got, far, norms, *query_parts, *kv_parts, *out_parts)


def deal_rows(rows, size, column, own, away):
    for b in range(rows.shape[0] // (2 * size)):
        at = slice(b * size, (b + 1) * size)
        even = rows[2 * b * size : (2 * b + 1) * size, :]
        odd = rows[(2 * b + 1) * size : (2 * b + 2) * size, :]

        @pl.when(column == 0)
        def _():
            own[at, :] = even
            away[at, :] = odd

        @pl.when(column != 0)
        def _():
            own[at, :] = odd
            away[at, :] = even


def ffn_part(normed, grad, gate_w, up_w, down_w, hidden, hid_own, hid_away, gate_grad, lifted_grad,
             unit_block, column):
    gate = dot_nn(normed, gate_w[...])
    lifted = dot_nn(normed, up_w[...])
    back = dot_nt(grad, down_w[...]).astype(BF16).astype(F32)
    sig = jax.nn.sigmoid(gate)
    swish = gate * sig
    made = (swish * lifted).astype(BF16)
    hidden[...] = made
    deal_rows(made.T, unit_block, column, hid_own, hid_away)
    gg = (back * lifted * sig * (1.0 + gate * (1.0 - sig))).astype(BF16)
    lg = (back * swish).astype(BF16)
    gate_grad[...] = gg
    lifted_grad[...] = lg
    return dot_nt(gg, gate_w[...]) + dot_nt(lg, up_w[...])


def ffn_first_body(unit_block, place, n0, n1, n2, n3, g0, g1, g2, g3, gate_w, up_w, down_w,
                   hidden, hid_own, hid_away, gate_grad, lifted_grad, normed, grad, grad_pair,
                   total):
    share, part = n0.shape[0], g0.shape[2]
    for b, ref in enumerate((n0, n1, n2, n3)):
        normed[b * share : (b + 1) * share, :] = ref[...]
    for c, ref in enumerate((g0, g1, g2, g3)):
        for b in range(4):
            rows, cols = relative(place[1], b, share), relative(place[1], c, part)
            grad[b * share : (b + 1) * share, cols] = ref[0, rows, :]
            grad_pair[b * share : (b + 1) * share, cols] = ref[1, rows, :]
    total[...] = ffn_part(
        normed[...], grad[...], gate_w, up_w, down_w, hidden, hid_own, hid_away, gate_grad,
        lifted_grad, unit_block, place[0],
    )


def ffn_second_body(unit_block, place, normed, grad, total, gate_w, up_w, down_w,
                    hidden, hid_own, hid_away, gate_grad, lifted_grad, away, own, low):
    share = own.shape[0]
    found = total[...] + ffn_part(
        normed[...], grad[...], gate_w, up_w, down_w, hidden, hid_own, hid_away, gate_grad,
        lifted_grad, unit_block, place[0],
    )
    own[...] = found[:share, :]
    low[...] = found[2 * share : 3 * share, :].astype(BF16)
    away[:share, :] = found[share : 2 * share, :].astype(BF16)
    away[share:, :] = found[3 * share :, :].astype(BF16)


def ffn(devices, place, half, inputs, gate_w, up_w, down_w):
    share = inputs[0].shape[0] if half == 0 else inputs[0].shape[0] // 4
    width = inputs[0].shape[1]
    size, units = 4 * share, gate_w.shape[1]
    tile = units // 2
    low = lambda *dims: jax.ShapeDtypeStruct(dims, BF16)
    wide = lambda *dims: jax.ShapeDtypeStruct(dims, F32)
    vmem = pl.BlockSpec(memory_space=pltpu.VMEM)
    cols = pl.BlockSpec((width, tile), lambda i: (0, half))
    rows = pl.BlockSpec((tile, width), lambda i: (half, 0))
    made = [low(size, tile), low(tile // 2, size), low(tile // 2, size), low(size, tile),
            low(size, tile)]
    if half == 0:
        made += [low(size, width), low(size, width), low(size, width), wide(size, width)]
    else:
        made += [low(2 * share, width), wide(share, width), low(share, width)]
    return pl.pallas_call(
        functools.partial(ffn_second_body if half else ffn_first_body, units // devices),
        grid=(1,),
        in_specs=[pl.BlockSpec(memory_space=pltpu.SMEM)] + [vmem] * len(inputs)
        + [cols, cols, rows],
        out_specs=[vmem] * len(made),
        out_shape=made,
        cost_estimate=FREE, name="ffn",
    )(place, *inputs, gate_w, up_w, down_w)


def cross_backward_body(own, got, far, grad, first, second, norms, q0, q1, q2, q3,
                        c0, c1, c2, c3, o0, o1, o2, o3, queries,
                        back_rows, kv_grad, vectors, grad_one, crossed_grad):
    width = grad.shape[1]
    kv = (c0, c1, c2, c3)
    context_rows = c0.shape[0] // 2
    key_rows, value_rows = slice(0, context_rows), slice(context_rows, 2 * context_rows)
    part = width // 4
    lanes = lax.broadcasted_iota(jnp.int32, (grad.shape[0], 2 * HEAD_SIZE), 1) // HEAD_SIZE
    lane_k = lax.broadcasted_iota(jnp.int32, (context_rows, 2 * HEAD_SIZE), 1) // HEAD_SIZE
    scale = 1.0 / math.sqrt(HEAD_SIZE)
    arrived = own[...] + got[...].astype(F32) + far[...].astype(F32)
    scaled, inverse = normalize(second[...])
    vectors[0:1, :] = jnp.sum(arrived * scaled, 0, keepdims=True)
    vectors[1:2, :] = jnp.sum(arrived, 0, keepdims=True)
    two = grad[...].astype(F32) + norm_backward(arrived, scaled, inverse, norms[4:5, :])
    low = two.astype(BF16)
    back_rows[:, :width] = low
    for b, ref in enumerate((o0, o1, o2, o3)):
        crossed_grad[:, b * part : (b + 1) * part] = dot_nt(low, ref[...]).astype(BF16)
    for p in range(width // (2 * HEAD_SIZE)):
        cols = slice(p * 2 * HEAD_SIZE, (p + 1) * 2 * HEAD_SIZE)
        q, k, v = queries[:, cols], pair_cols(kv, p, key_rows), pair_cols(kv, p, value_rows)
        g_rows = crossed_grad[:, cols]
        found = []
        for g in (0, 1):
            probs = head_weights(q, k, lanes, g)
            change = dot_nt(jnp.where(lanes == g, g_rows, jnp.zeros_like(g_rows)), v)
            delta = jnp.sum(change * probs, -1, keepdims=True)
            ds = (probs * (change - delta)).astype(BF16)
            found.append((dot_nn(ds, k), dot_tn(ds, q), dot_tn(probs.astype(BF16), g_rows)))
        back_rows[:, width + cols.start : width + cols.stop] = (
            jnp.where(lanes == 0, found[0][0], found[1][0]) * scale
        ).astype(BF16)
        kv_grad[:context_rows, cols] = (
            jnp.where(lane_k == 0, found[0][1], found[1][1]) * scale
        ).astype(BF16)
        kv_grad[context_rows:, cols] = jnp.where(lane_k == 0, found[0][2], found[1][2]).astype(
            BF16
        )
    back = jnp.zeros(grad.shape, F32)
    for b, ref in enumerate((q0, q1, q2, q3)):
        back = back + dot_nt(back_rows[:, width + b * part : width + (b + 1) * part], ref[...])
    scaled, inverse = normalize(first[...])
    vectors[2:3, :] = jnp.sum(back * scaled, 0, keepdims=True)
    vectors[3:4, :] = jnp.sum(back, 0, keepdims=True)
    grad_one[...] = (two + norm_backward(back, scaled, inverse, norms[2:3, :])).astype(BF16)


def cross_backward(own, got, far, grad, first, second, norms, query_parts, kv_parts, out_parts,
                   queries):
    rows, width = own.shape
    low = lambda r: jax.ShapeDtypeStruct((r, width), BF16)
    block = pl.BlockSpec((rows, width), lambda i: (0, 0))
    return pl.pallas_call(
        cross_backward_body,
        grid=(1,),
        out_shape=[jax.ShapeDtypeStruct((rows, 2 * width), BF16), low(kv_parts[0].shape[0]),
                   jax.ShapeDtypeStruct((4, width), F32), low(rows)],
        in_specs=[block] * 6 + [pl.BlockSpec(memory_space=pltpu.VMEM)] * 14,
        scratch_shapes=[pltpu.VMEM((rows, width), BF16)],
        cost_estimate=FREE, name="cross_back",
    )(own, got, far, grad, first, second, norms, *query_parts, *kv_parts, *out_parts, queries)


def meet_rows_body(size, side, own_a, pair_a, own_b, pair_b, right, right_pair, keep, send):
    half = keep.shape[0] // 2
    for b, (own, pair) in enumerate(((own_a, pair_a), (own_b, pair_b))):
        made = (dot_nn(own[...], right[...]) + dot_nn(pair[...], right_pair[...])).astype(BF16)
        at = pl.ds(b * half, half)
        deal_rows(made, size, side[0], keep.at[at], send.at[at])


def meet_rows(size, side, lefts, rights):
    count, frames = lefts[0].shape
    width = rights[0].shape[1]
    tile = width // 3
    left = pl.BlockSpec((count, frames), lambda i: (0, 0))
    right = pl.BlockSpec((frames, tile), lambda i: (0, i))
    return pl.pallas_call(
        functools.partial(meet_rows_body, size),
        grid=(3,),
        in_specs=[pl.BlockSpec(memory_space=pltpu.SMEM)] + [left] * 4 + [right] * 2,
        out_specs=[pl.BlockSpec((count, tile), lambda i: (0, i))] * 2,
        out_shape=[jax.ShapeDtypeStruct((count, width), BF16)] * 2,
        name="meet_rows", cost_estimate=FREE,
    )(side, *lefts, *rights)


def meet_cols_body(size, side, p0, p1, p2, p3, *refs):
    own, pair = (jnp.concatenate([p[i] for p in (p0, p1, p2, p3)], 1) for i in (0, 1))
    *rights, keep, send = refs
    width = rights[0].shape[1]
    for at in range(len(rights) // 2):
        made = dot_nn(own, rights[2 * at][...]) + dot_nn(pair, rights[2 * at + 1][...])
        cols = pl.ds(at * width, width)
        deal_rows(made.astype(BF16), size, side[0], keep.at[:, cols], send.at[:, cols])


def meet_cols(size, side, near, rights):
    width = rights[0].shape[1] * (len(rights) // 2)
    half = jax.ShapeDtypeStruct((near[0].shape[1] // 2, width), BF16)
    vmem = pl.BlockSpec(memory_space=pltpu.VMEM)
    return pl.pallas_call(
        functools.partial(meet_cols_body, size),
        in_specs=[pl.BlockSpec(memory_space=pltpu.SMEM)] + [vmem] * (4 + len(rights)),
        out_shape=[half] * 2,
        name="meet_cols", cost_estimate=FREE,
    )(side, *near, *rights)


def down_body(first, second, down_w, away, own, low):
    share, units = own.shape[0], first.shape[1]

    def sent(r):
        at = slice(r * share, (r + 1) * share)
        return dot_nn(first[at, :], down_w[:units, :]) + dot_nn(second[at, :], down_w[units:, :])

    away[:share, :] = sent(1).astype(BF16)
    away[share:, :] = sent(3).astype(BF16)
    low[...] = sent(2).astype(BF16)
    own[...] = sent(0)


def down_parts(first, second, down_w):
    share, width = first.shape[0] // 4, down_w.shape[1]
    low = lambda *dims: jax.ShapeDtypeStruct(dims, BF16)
    return pl.pallas_call(
        down_body,
        out_shape=[low(2 * share, width), jax.ShapeDtypeStruct((share, width), F32),
                   low(share, width)],
        name="down", cost_estimate=FREE,
    )(first, second, down_w)


def bundle_body(devices, place, f02, f13, b02, b13, a0, a1, a2, a3, attended,
                context, kv, keep_a, send_a, keep_b, send_b):
    width = a0.shape[1]
    part, share = width // 4, a0.shape[0]

    def near(even, odd):
        return even[0], odd[0], even[1], odd[1]

    own = lambda rows: jnp.concatenate(
        [row[:, width + r * part : width + (r + 1) * part] for r, row in enumerate(rows)], 0
    )
    full = lambda rows: jnp.concatenate([row[:, :width] for row in rows], 0)
    fronts, backs = near(f02, f13), near(b02, b13)
    rows = width // devices
    small = part // devices
    half = width // 2

    def put(block, base, left, out):
        size = block.shape[0] // devices
        cols = slice(left, left + block.shape[1])
        low = block.astype(BF16)
        for d in range(0, devices, 2):
            at = slice(base, base + size)
            even, odd = low[d * size : (d + 1) * size, :], low[(d + 1) * size : (d + 2) * size, :]

            @pl.when(place[0] == 0)
            def _():
                out[0][d // 2, at, cols] = even
                out[1][d // 2, at, cols] = odd

            @pl.when(place[0] != 0)
            def _():
                out[0][d // 2, at, cols] = odd
                out[1][d // 2, at, cols] = even

    put(dot_tn(full(fronts), own(backs)), 0, 0, (keep_a, send_a))
    count = context.shape[0]
    put(dot_tn(context[...], kv[:count, :]), 0, part, (keep_a, send_a))
    put(dot_tn(context[...], kv[count:, :]), rows // 2, part, (keep_a, send_a))
    grads = dot_tn(own(fronts), full(backs))
    put(grads[:, :half], 0, 0, (keep_b, send_b))
    put(grads[:, half:], small, 0, (keep_b, send_b))
    grads = sum(
        dot_nn(attended[:, relative(place[1], r, share)], ref[...])
        for r, ref in enumerate((a0, a1, a2, a3))
    )
    put(grads[:, :half], 2 * small, 0, (keep_b, send_b))
    put(grads[:, half:], 3 * small, 0, (keep_b, send_b))


def bundle_grads(devices, place, fronts, backs, ones, attended, context, kv):
    width = ones[0].shape[1]
    vmem = pl.BlockSpec(memory_space=pltpu.VMEM)
    return pl.pallas_call(
        functools.partial(bundle_body, devices),
        in_specs=[pl.BlockSpec(memory_space=pltpu.SMEM)] + [vmem] * 11,
        out_specs=[vmem] * 4,
        out_shape=[jax.ShapeDtypeStruct((devices // 2, width // devices, width // 2), BF16)] * 4,
        name="bundle", cost_estimate=FREE,
    )(place, *fronts, *backs, *ones, attended, context, kv)


def front_body(width_block, place, x0, x1, x2, x3, g0, g1, g2, g3, cosine, sine, wq, wk, wv,
               time_row, context, ck, cv,
               queries, pair, rows, low, nrm_own, nrm_away, norms, means, inverses,
               time_scaled, time_low, time_keys, time_values, kv, wide):
    size, part = x0.shape
    for r, (x, g) in enumerate(((x0, g0), (x1, g1), (x2, g2), (x3, g3))):
        start = pl.multiple_of((place[0] ^ r) * part, 128)
        wide[:, pl.ds(start, part)] = x[...]
        norms[:, pl.ds(start, part)] = g[...]
    share = size // 4
    rows[...] = wide[pl.ds(pl.multiple_of(place[0] * share, share), share), :]
    values = wide[...].astype(F32)
    mean = jnp.mean(values, -1, keepdims=True)
    centred = values - mean
    inverse = lax.rsqrt(jnp.mean(centred * centred, -1, keepdims=True) + 1e-05)
    means[...] = mean
    inverses[...] = inverse
    normed = (centred * inverse * norms[0:1, :] + norms[1:2, :]).astype(BF16)
    low[...] = normed
    half = HEAD_SIZE // 2

    def turned(weight):
        return dot_nn(normed, weight[...]).T

    def rotated(block, dest, scale):
        for h in range(part // HEAD_SIZE):
            a = block[h * HEAD_SIZE : h * HEAD_SIZE + half, :]
            b = block[h * HEAD_SIZE + half : (h + 1) * HEAD_SIZE, :]
            dest[h * HEAD_SIZE : h * HEAD_SIZE + half, :] = (
                (a * cosine[...] - b * sine[...]) * scale
            ).astype(BF16)
            dest[h * HEAD_SIZE + half : (h + 1) * HEAD_SIZE, :] = (
                (b * cosine[...] + a * sine[...]) * scale
            ).astype(BF16)

    scaled, _ = normalize(jnp.broadcast_to(time_row[...].astype(F32), (8, 4 * part)))
    time_scaled[...] = scaled[:1, :]
    made = (scaled * norms[0:1, :] + norms[1:2, :]).astype(BF16)
    time_low[...] = made[:1, :].astype(F32)
    time_keys[...] = dot_nn(made, wk[...]).astype(BF16).astype(F32).T[:, :1]
    time_values[...] = dot_nn(made, wv[...]).astype(BF16).astype(F32).T[:, :1]
    count = context.shape[0]
    kv[:count, :] = dot_nn(context[...], ck[...]).astype(BF16)
    kv[count:, :] = dot_nn(context[...], cv[...]).astype(BF16)
    rotated(turned(wk), pair.at[0], 1.0)
    pair[1] = turned(wv).astype(BF16)
    rotated(turned(wq), queries, 1.0 / math.sqrt(HEAD_SIZE))
    deal_rows(normed.T, width_block, place[1], nrm_own, nrm_away)


def front(devices, place, parts, norm_parts, tables, wq, wk, wv, time_row, context, ck, cv):
    size, part = parts[0].shape
    width = 4 * part
    low = lambda *s: jax.ShapeDtypeStruct(s, BF16)
    wide = lambda *s: jax.ShapeDtypeStruct(s, F32)
    vmem = pl.BlockSpec(memory_space=pltpu.VMEM)
    return pl.pallas_call(
        functools.partial(front_body, width // devices),
        in_specs=[pl.BlockSpec(memory_space=pltpu.SMEM)] + [vmem] * 17,
        out_specs=[vmem] * 14,
        out_shape=[low(part, size), low(2, part, size), low(size // 4, width), low(size, width),
                   low(width // 2, size), low(width // 2, size), wide(6, width),
                   wide(size, 1), wide(size, 1), wide(1, width), wide(1, width), wide(part, 1),
                   wide(part, 1), low(2 * context.shape[0], part)],
        scratch_shapes=[pltpu.VMEM((size, width), BF16)],
        cost_estimate=FREE, name="front",
    )(place, *parts, *norm_parts, *tables, wq, wk, wv, time_row, context, ck, cv)


def per_device(
    frames,
    segment,
    time_token,
    context,
    gain_attn,
    bias_attn,
    gain_cross,
    bias_cross,
    gain_ffn,
    bias_ffn,
    w_query,
    w_key,
    w_value,
    w_out,
    c_query,
    c_key,
    c_value,
    c_out,
    w_gate,
    w_up,
    w_down,
    out_grad,
):
    local_rows = frames.shape[0]
    local_width = frames.shape[1]
    model_width = w_query.shape[0]
    head_cols = w_query.shape[1]
    heads = head_cols // HEAD_SIZE
    number_of_frames = lax.axis_size("seq") * local_rows
    row_length = min(max(ROW_MIN, 64 * lax.axis_size("seq")), number_of_frames)
    first_frame = lax.axis_index("seq") * local_rows
    own_start = lax.axis_index("tensor") * local_width

    def own_cols(value):
        return lax.dynamic_slice_in_dim(value, own_start, local_width, value.ndim - 1)

    place = lax.axis_index("tensor")
    share = local_rows // 4

    def row_block(value, index):
        return rows_of(value, index * share, share)

    column = lax.axis_index("seq") % 2
    frame_parts_near = gather_near(frames)
    norm_parts = gather_near(
        jnp.stack([gain_attn, bias_attn, gain_cross, bias_cross, gain_ffn, bias_ffn])
    )
    clip_starts, frame_positions = frame_clip_labels(segment, row_length)
    own_labels = lax.dynamic_slice_in_dim(clip_starts, first_frame, local_rows)
    own_positions = lax.dynamic_slice_in_dim(frame_positions, first_frame, local_rows)
    blanks = jnp.full((local_rows,), -1, jnp.int32)
    key_labels = lax.dynamic_slice_in_dim(
        jnp.concatenate([blanks, clip_starts, blanks]), first_frame, 3 * local_rows
    )
    spans = jnp.concatenate(
        [tile_ranges(own_labels, key_labels), place.astype(jnp.int32).reshape(1)]
    )
    places = jnp.stack([column, place]).astype(jnp.int32)
    label_row, label_column = own_labels[None, :], key_labels[:, None]
    row_index = first_frame // row_length
    time_row = lax.dynamic_slice_in_dim(time_token, row_index, 1, 0)
    row_context = lax.dynamic_slice_in_dim(context, row_index, 1, 0)[0]
    context_rows = row_context.shape[0]
    tables = rotary_tables(own_positions)
    score_scale = 1.0 / math.sqrt(HEAD_SIZE)
    all_heads = model_width // HEAD_SIZE

    (
        queries, both, frame_rows, frame_normed, one_own_half, one_away_half, norms, means_one,
        inverse_one, scaled_time, time_normed, time_keys, time_values, context_kv,
    ) = front(
        lax.axis_size("seq"), jnp.flip(places), frame_parts_near, norm_parts, tables, w_query,
        w_key, w_value, time_row, row_context, c_key, c_value,
    )
    both, out_pair = meeting(both, swap(after(out_grad, frame_parts_near[2]), "seq", 1))
    grad_both = jnp.stack([out_grad, out_pair])
    behind, ahead = shift(both, "seq", 1), shift(both, "seq", -1)
    query_late, out_late = after((c_query, c_out), (frame_parts_near[2], norm_parts[2]))
    query_far, out_far = swap(query_late, "tensor", 2), swap(out_late, "tensor", 2)
    state = attend_near(spans, queries, both, time_keys, time_values, label_row, label_column)
    behind, ahead, query_far, out_far, *state = meeting(
        behind, ahead, query_far, out_far, *state
    )
    query_own, out_own, context_late = after((c_query, c_out, context_kv), behind)
    weights_near = [
        swap(value, "tensor", 1) for value in (query_own, query_far, out_own, out_far)
    ]
    kv_far = swap(context_late, "tensor", 2)
    attended, log_totals, one_away, one_own, one_low = attend_far(
        spans, queries, behind, ahead, label_row, label_column, w_out, state
    )
    one_away, one_low, kv_far, *weights_near = meeting(one_away, one_low, kv_far, *weights_near)
    kv_both = jnp.concatenate([context_kv, kv_far], 0)
    kv_other = swap(kv_both, "tensor", 1)
    kv_rows = context_kv.shape[0]
    kv_parts = (context_kv, kv_other[:kv_rows], kv_far, kv_other[kv_rows:])
    query_parts = (c_query, weights_near[0], query_far, weights_near[1])
    out_parts = (c_out, weights_near[2], out_far, weights_near[3])
    one_got, _, one_far = scatter_near(one_away, one_low)
    (
        front_rows, cross_queries, residual_one, residual_two, normed_share, flip_own, flip_away,
    ) = cross_forward(
        lax.axis_size("seq"), places, frame_rows, one_own, one_got, one_far, norms,
        query_parts, kv_parts, out_parts,
    )
    grad_far = swap(after(grad_both, one_far), "tensor", 2)
    normed_share, normed_got, grad_far = meeting(
        normed_share, swap(after(one_away_half, one_low), "seq", 1), grad_far
    )
    grad_late, grad_far_late = after((grad_both, grad_far), normed_share)
    grad_mate, grad_far_mate = swap(grad_late, "tensor", 1), swap(grad_far_late, "tensor", 1)
    grad_parts = (grad_both, grad_mate, grad_far, grad_far_mate)
    three_parts = gather_near(normed_share)
    flip_got = swap(after(flip_away, normed_share), "seq", 1)
    front_far = swap(after(front_rows, three_parts[3]), "tensor", 2)
    devices = lax.axis_size("seq")
    (
        hidden_a, hidden_own_a, hidden_away_a, gate_a, lifted_a, normed_three, grad_near, grad_pair,
        ffn_total,
    ) = ffn(devices, places, 0, (*three_parts, *grad_parts), w_gate, w_up, w_down)
    ffn_total, flip_got = meeting(ffn_total, flip_got)
    flip_both = jnp.stack([flip_own, flip_got])
    flip_far = swap(flip_both, "tensor", 2)
    hidden_got_a, gate_got_a = swap(hidden_away_a, "seq", 1), swap(gate_a, "seq", 1)
    hidden_b, hidden_own_b, hidden_away_b, gate_b, lifted_b, three_away, three_own, three_low = ffn(
        devices, places, 1, (normed_three, grad_near, ffn_total), w_gate, w_up, w_down
    )
    three_away, three_low, flip_far, front_far, hidden_got_a = meeting(
        three_away, three_low, flip_far, front_far, hidden_got_a
    )
    three_got, _, three_far = scatter_near(three_away, three_low)
    lifted_got_a = swap(after(lifted_a, three_low), "seq", 1)
    flip_late, flip_far_late, gate_late = after((flip_both, flip_far, gate_b), three_far)
    flip_mate, flip_far_mate = swap(flip_late, "tensor", 1), swap(flip_far_late, "tensor", 1)
    gate_got_b = swap(gate_late, "seq", 1)
    front_both = jnp.stack([front_rows, front_far])
    back_rows, kv_grad, norm_vectors, grad_one = cross_backward(
        three_own, three_got, three_far, grad_near, residual_one, residual_two, norms,
        query_parts, kv_parts, out_parts, cross_queries,
    )
    grad_one, gate_got_a, lifted_got_a, flip_mate, flip_far_mate = meeting(
        grad_one, gate_got_a, lifted_got_a, flip_mate, flip_far_mate
    )
    hidden_got_b = swap(after(hidden_away_b, three_far), "seq", 1)
    count = lax.axis_size("seq")
    level_side = ((lax.axis_index("seq") >> 1) % 2).astype(jnp.int32).reshape(1)
    rows = model_width // count

    def traded(dealt):
        keep, send = [value.reshape(count // 4, rows, -1) for value in dealt]
        return keep, swap(send, "seq", 2)

    down_keep, down_got = traded(
        meet_rows(
            rows, level_side, (hidden_own_a, hidden_got_a, hidden_own_b, hidden_got_b),
            (grad_near, grad_pair),
        )
    )
    context_parts = quarters(kv_grad, 1)
    context_got = swap(jnp.concatenate([context_parts[1], context_parts[3]], 0), "tensor", 1)
    one_far_rows, down_keep = meeting(swap(grad_one, "tensor", 2), down_keep)
    one_parts = (
        grad_one, swap(grad_one, "tensor", 1), one_far_rows, swap(one_far_rows, "tensor", 1)
    )
    *one_parts, front_other, context_got = meeting(
        *one_parts, swap(after(front_both, grad_one), "tensor", 1), context_got
    )
    context_low = (
        context_parts[2].astype(F32) + context_got[context_parts[2].shape[0] :].astype(F32)
    ).astype(BF16)
    context_far = swap(context_low, "tensor", 2)
    back_far = swap(after(back_rows, one_parts[3]), "tensor", 2)
    lifted_got_b = swap(after(lifted_b, grad_one), "seq", 1)
    query_grad, to_prev, kept, to_next, time_grads = attend_back(
        spans, queries, (behind, both, ahead), time_keys, time_values, label_row, label_column,
        w_out, attended, log_totals, one_parts,
    )
    to_prev, to_next, back_far, gate_got_b, lifted_got_b, down_got, context_far = meeting(
        to_prev, to_next, back_far, gate_got_b, lifted_got_b, down_got, context_far
    )
    from_next, from_prev = shift(to_prev, "seq", -1), shift(to_next, "seq", 1)
    down_keep, down_got = halve(added(down_keep, down_got).astype(BF16), 2)
    flip_near = (flip_both, flip_mate, flip_far, flip_far_mate)
    first_keep, first_got = traded(
        meet_cols(
            rows, level_side, flip_near,
            after((gate_a, gate_got_a, lifted_a, lifted_got_a), to_prev),
        )
    )
    second_keep, second_got = traded(
        meet_cols(
            rows, level_side, flip_near,
            after((gate_b, gate_got_b, lifted_b, lifted_got_b), to_prev),
        )
    )
    back_both = jnp.stack([back_rows, back_far])
    back_other = swap(back_both, "tensor", 1)
    context_own = (
        context_parts[0].astype(F32)
        + context_got[: context_far.shape[0]].astype(F32)
        + context_far.astype(F32)
    )
    keep_a, send_a, keep_b, send_b = bundle_grads(
        count, places, (front_both, front_other), (back_both, back_other), one_parts, attended,
        row_context,
        context_own.astype(BF16),
    )
    from_next, from_prev, down_got, send_a, send_b = meeting(
        from_next, from_prev, down_got, send_a, send_b
    )
    got_a = swap(send_a, "seq", 1)
    raw, last_away, last_own, last_low = tail(
        places[1:], query_grad, kept, from_next, from_prev, tables, w_query, w_key, w_value,
        time_grads,
    )
    last_got = swap(last_away, "tensor", 1)
    raw_got = swap(raw, "seq", 1)
    last_sum = (
        last_low.astype(F32) + last_got[local_rows:].astype(F32)
    ).astype(BF16)
    last_sum, first_got, raw_got = meeting(last_sum, first_got, raw_got)
    first_keep, first_got = halve(added(first_keep, first_got).astype(BF16), 2)
    last_far, second_got = meeting(swap(last_sum, "tensor", 2), second_got)
    second_keep, second_got = halve(added(second_keep, second_got).astype(BF16), 2)
    frame_grad = last_own + last_got[:local_rows].astype(F32) + last_far.astype(F32)

    time_late, means_late, inverse_late, vectors_late = after(
        (time_grads, means_one, inverse_one, norm_vectors), last_far
    )
    time_grad = sum(
        jnp.einsum("of,df->od", time_late[i : i + 1].astype(BF16), w, preferred_element_type=F32)
        for i, w in enumerate((w_key, w_value))
    )
    own_scaled = (frames.astype(F32) - means_late) * inverse_late
    scaled_grad = frame_grad * gain_attn[None]
    sums = jnp.concatenate(
        [
            jnp.sum(scaled_grad, -1),
            jnp.sum(scaled_grad * own_scaled, -1),
            time_grad[0],
            vectors_late.reshape(-1),
        ]
    )[None]
    sums = sums + swap(sums, "tensor", 1)
    sums = sums + swap(sums, "tensor", 2)
    sums, first_got = meeting(sums, first_got)
    plain = sums[0, :local_rows, None] / model_width
    cross = sums[0, local_rows : 2 * local_rows, None] / model_width
    vectors = own_cols(sums[0, 2 * local_rows :].reshape(5, model_width))
    attend_full = ordered(*[after(one_parts, from_next)[i] for i in (0, 2, 1, 3)], 0)
    d_frames = own_cols(attend_full).astype(F32) + inverse_late * (
        scaled_grad - plain - own_scaled * cross
    )
    d_gain_attn = jnp.sum(frame_grad * own_scaled, 0) + vectors[0] * own_cols(scaled_time)[0]
    d_bias_attn = jnp.sum(frame_grad, 0) + vectors[0]

    time_column = time_normed.T

    normed_pair = (one_own_half, normed_got)
    grad_down = halve_end(down_keep, down_got, 3)
    raw_pair = (raw[: 3 * head_cols], raw_got[: 3 * head_cols])
    time_got = raw_got[3 * head_cols : 3 * head_cols + 2, :head_cols].astype(F32)
    time_both = (time_grads + time_got).reshape(1, 2 * head_cols)
    own_time_rows = lax.dynamic_index_in_dim(
        time_column.reshape(count // 2, 2, -1), column, 1, False
    ).reshape(-1, 1)
    outer = own_time_rows * jnp.concatenate([jnp.zeros((1, head_cols), F32), time_both], 1)
    blocks = sum(
        jnp.einsum("dn,fn->df", r, c, preferred_element_type=F32)
        for r, c in zip(normed_pair, raw_pair)
    )
    blocks = (blocks + outer).astype(BF16).reshape(count // 2, rows, 3 * head_cols)
    heads_keep, heads_got = halve(blocks, 1)
    got_b = swap(after(send_b, from_next), "seq", 1)
    down_away, down_own, down_low = down_parts(after(hidden_a, sums), hidden_b, w_down)
    branch_got, _, branch_far = scatter_near(down_away, down_low)
    heads_got, got_a, got_b = meeting(heads_got, got_a, got_b)
    left_keep, left_got = halve(added(keep_a, got_a).astype(BF16), 1)
    right_keep, right_got = halve(added(keep_b, got_b).astype(BF16), 1)
    heads_next = added(heads_keep, heads_got).astype(BF16)
    heads_keep, heads_got = halve(heads_next, 2)
    left_got, right_got, second_got, branch_far = meeting(
        left_got, right_got, second_got, branch_far
    )
    last_next = added(right_keep, right_got)
    left_keep, left_got = halve(added(left_keep, left_got).astype(BF16), 2)
    right_keep, right_got = halve(last_next.astype(BF16), 2)
    heads_got, left_got, right_got = meeting(heads_got, left_got, right_got)
    block_rows = (
        residual_two + down_own + branch_got[:share].astype(F32) + branch_far.astype(F32)
    ).astype(BF16)
    block_cols = rows_to_cols(
        *[
            lax.dynamic_slice_in_dim(block_rows, (place ^ r) * local_width, local_width, 1)
            for r in range(4)
        ],
        last_next,
    )
    block_out = jnp.concatenate([row_block(block_cols, place ^ b) for b in range(4)], 0)
    first, second = halve_end(first_keep, first_got, 3), halve_end(second_keep, second_got, 3)
    units = first.shape[1] // 2
    grad_gate_w = jnp.concatenate([first[:, :units], second[:, :units]], 1)
    grad_up_w = jnp.concatenate([first[:, units:], second[:, units:]], 1)
    small = jnp.stack(
        [d_gain_attn, d_bias_attn, vectors[3], vectors[4], vectors[1], vectors[2]]
    ).reshape(6, devices, -1).transpose(1, 0, 2)
    small = small.reshape(count // 4, 2, 2, 6, -1).swapaxes(1, 2).reshape(count, 6, -1)
    small = after(small, last_next)
    bits = [1, 0] + list(range(2, count.bit_length() - 1))
    for bit in bits:
        small = added(*halve(small, bit))
    small = small[0]
    heads_sum = halve_end(heads_keep, heads_got, 3)
    left, right = halve_end(left_keep, left_got, 3), halve_end(right_keep, right_got, 3)
    part, rows = head_cols // count, model_width // count
    grad_c_query = left[:, :head_cols]
    grad_c_key, grad_c_value = left[: rows // 2, head_cols:], left[rows // 2 :, head_cols:]
    grad_c_out = jnp.concatenate([right[:part], right[part : 2 * part]], 1)
    grad_w_out = jnp.concatenate([right[2 * part : 3 * part], right[3 * part :]], 1)
    grad_w_query, grad_w_key, grad_w_value = (
        heads_sum[:, i * head_cols : (i + 1) * head_cols] for i in range(3)
    )
    return (
        block_out,
        d_frames,
        small[0],
        small[1],
        small[2],
        small[3],
        small[4],
        small[5],
        grad_w_query,
        grad_w_key,
        grad_w_value,
        grad_w_out,
        grad_c_query,
        grad_c_key,
        grad_c_value,
        grad_c_out,
        grad_gate_w,
        grad_up_w,
        grad_down,
    )


def solution(mesh):
    return jax.shard_map(
        per_device,
        mesh=mesh,
        in_specs=(
            P("seq", "tensor"),
            P(),
            P(),
            P(),
            P("tensor"),
            P("tensor"),
            P("tensor"),
            P("tensor"),
            P("tensor"),
            P("tensor"),
            P(None, "tensor"),
            P(None, "tensor"),
            P(None, "tensor"),
            P("tensor", None),
            P(None, "tensor"),
            P(None, "tensor"),
            P(None, "tensor"),
            P("tensor", None),
            P(None, "tensor"),
            P(None, "tensor"),
            P("tensor", None),
            P("seq", "tensor"),
        ),
        out_specs=(
            P("seq", "tensor"),
            P("seq", "tensor"),
            P(("tensor", "seq")),
            P(("tensor", "seq")),
            P(("tensor", "seq")),
            P(("tensor", "seq")),
            P(("tensor", "seq")),
            P(("tensor", "seq")),
            P("seq", "tensor"),
            P("seq", "tensor"),
            P("seq", "tensor"),
            P(("tensor", "seq"), None),
            P("seq", "tensor"),
            P("seq", "tensor"),
            P("seq", "tensor"),
            P(("tensor", "seq"), None),
            P("seq", "tensor"),
            P("seq", "tensor"),
            P(("tensor", "seq"), None),
        ),
        check_vma=False,
    )
```

```python
import functools
import math

import jax
import jax.numpy as jnp
from jax import lax
from jax.experimental import pallas as pl
from jax.experimental.pallas import tpu as pltpu
from jax.sharding import PartitionSpec as P

HEAD_SIZE = 64
ROW_MIN = 2048
TILE = 256
BF16 = jnp.bfloat16
F32 = jnp.float32


def meeting(*values):
    return lax.optimization_barrier(values)


def after(value, token):
    return lax.optimization_barrier((value, token))[0]


def swap(value, axis, by):
    return lax.ppermute(value, axis, [(i, i ^ by) for i in range(lax.axis_size(axis))])


def shift(value, axis, by):
    peers = lax.axis_size(axis)
    pairs = [(i, i + by) for i in range(peers) if 0 <= i + by < peers]
    return lax.ppermute(value, axis, pairs)


def tensor_place():
    place = lax.axis_index("tensor")
    return place // 2, place % 2


def ordered(own, far, mate, far_mate, axis):
    side, core = tensor_place()
    near = (jnp.where(core == 0, own, mate), jnp.where(core == 0, mate, own))
    away = (jnp.where(core == 0, far, far_mate), jnp.where(core == 0, far_mate, far))
    low = [jnp.where(side == 0, n, a) for n, a in zip(near, away)]
    high = [jnp.where(side == 0, a, n) for n, a in zip(near, away)]
    return jnp.concatenate(low + high, axis)


def gather_near(own):
    far = swap(own, "tensor", 2)
    return own, swap(own, "tensor", 1), far, swap(far, "tensor", 1)


def gather_staged(own, first, second):
    far = swap(after(own, first), "tensor", 2)
    far, late = after((far, own), second)
    return own, swap(late, "tensor", 1), far, swap(far, "tensor", 1)


def gather(own, axis):
    own, mate, far, far_mate = gather_near(own)
    return ordered(own, far, mate, far_mate, axis)


def scatter_near(away, low):
    got = swap(away, "tensor", 1)
    total = (low.astype(F32) + got[low.shape[0] :].astype(F32)).astype(BF16)
    return got, total, swap(total, "tensor", 2)


def rows_to_cols(own, mate, far, far_mate, later):
    width = own.shape[1]
    got = after(swap(jnp.concatenate([far, far_mate], 1), "tensor", 2), later)
    other = swap(jnp.concatenate([mate, got[:, width:]], 0), "tensor", 1)
    size = own.shape[0]
    return jnp.concatenate([own, other[:size], got[:, :width], other[size:]], 0)


def quarters(value, axis):
    return jnp.split(value, 4, axis)


def own_blocks(near):
    return jnp.concatenate([quarters(value, 1)[r] for r, value in enumerate(near)], 0)


def trade(value, start, done):
    return after(swap(after(value, start), "seq", 1), done)


def halve(blocks, bit):
    count, rows, cols = blocks.shape
    side = (lax.axis_index("seq") >> bit) % 2
    parts = blocks.reshape(count // 2, 2, rows, cols)
    send = lax.dynamic_index_in_dim(parts, 1 - side, 1, False)
    keep = lax.dynamic_index_in_dim(parts, side, 1, False)
    return keep, swap(send, "seq", 1 << bit)


def added(keep, got):
    return keep.astype(F32) + got.astype(F32)


def halve_all(blocks, bit):
    while blocks.shape[0] > 1:
        blocks = added(*halve(blocks.astype(BF16), bit))
        bit += 1
    return blocks[0].astype(F32)


def halve_end(keep, got, bit):
    return halve_all(added(keep, got), bit)


def frame_clip_labels(segment, row_length):
    frame_index = jnp.arange(segment.shape[0], dtype=jnp.int32)
    border = (frame_index % row_length == 0) | (segment != jnp.roll(segment, 1))
    clip_starts = lax.cummax(jnp.where(border, frame_index, 0), axis=0)
    return (clip_starts, (frame_index - clip_starts + 1).astype(jnp.float32))


def tile_ranges(q_labels, key_labels):
    q = q_labels.reshape(-1, TILE)
    k = key_labels.reshape(-1, TILE)
    meets = (k[None, :, 0] <= q[:, None, -1]) & (k[None, :, -1] >= q[:, None, 0])
    index = jnp.arange(k.shape[0], dtype=jnp.int32)[None]
    low = jnp.min(jnp.where(meets, index, k.shape[0]), 1)
    high = jnp.max(jnp.where(meets, index + 1, 0), 1)
    return jnp.stack([low, high], 1).reshape(-1)

def head_rows(g):
    return slice(g * HEAD_SIZE, (g + 1) * HEAD_SIZE)

def fill_natural(dest, refs, which):
    size = refs[0].shape[2]
    for part, ref in enumerate(refs):
        dest[part * size : (part + 1) * size, :] = ref[which].T


def fill_tiles(dest, refs, which):
    pieces = refs[0].shape[2] // TILE
    for part, ref in enumerate(refs):
        for piece in range(pieces):
            dest[part * pieces + piece] = ref[which, :, piece * TILE : (piece + 1) * TILE]


def relative(place, r, size):
    return pl.ds(pl.multiple_of((place ^ r) * size, size), size)


def absorb(state, start, stop, base, q, cols, lab, klab, keys, vals):
    group = q.shape[0] // HEAD_SIZE

    def step(j, state):
        seen = klab[pl.ds(pl.multiple_of(j * TILE, TILE), TILE), :] == lab
        at = pl.ds(pl.multiple_of((j - base) * TILE, TILE), TILE)
        fresh = []
        for g in range(group):
            top, total, acc = state[3 * g : 3 * g + 3]
            s = dot_nn(keys[at, head_rows(g)], q[head_rows(g), cols])
            s = jnp.where(seen, s, -1e30)
            new = jnp.maximum(top, jnp.max(s, 0, keepdims=True))
            fade = jnp.exp(top - new)
            p = jnp.exp(s - new)
            total = total * fade + jnp.sum(p, 0, keepdims=True)
            acc = acc * fade + dot_nn(vals[j - base, head_rows(g), :], p.astype(BF16))
            fresh += [new, total, acc]
        return tuple(fresh)

    return lax.fori_loop(start, stop, step, tuple(state))


def near_body(span, q, kv, tk, tv, qlab, klab, tops, totals, mix, keys, vals):
    rows, size = q.shape
    pieces = size // TILE
    fill_natural(keys, (kv,), 0)
    fill_tiles(vals, (kv,), 1)
    for tile in range(pieces):
        cols = slice(tile * TILE, (tile + 1) * TILE)
        state = []
        for g in range(rows // HEAD_SIZE):
            part = q[head_rows(g), cols].astype(F32)
            top = jnp.sum(part * tk[head_rows(g), :], 0, keepdims=True)
            state += [
                top,
                jnp.ones_like(top),
                jnp.broadcast_to(tv[head_rows(g), :], (HEAD_SIZE, TILE)),
            ]
        start = jnp.maximum(span[2 * tile], pieces)
        stop = jnp.minimum(span[2 * tile + 1], 2 * pieces)
        state = absorb(state, start, stop, pieces, q, cols, qlab[:, cols], klab, keys, vals)
        for g in range(rows // HEAD_SIZE):
            tops[g : g + 1, cols], totals[g : g + 1, cols], mix[head_rows(g), cols] = state[
                3 * g : 3 * g + 3
            ]


def far_body(span, q, kv0, kv2, qlab, klab, w_out, tops, totals, mix,
             out, lse, away, own, low, keys0, keys2, vals0, vals2):
    rows, size = q.shape
    pieces = size // TILE
    for kv, keys, vals in ((kv0, keys0, vals0), (kv2, keys2, vals2)):
        fill_natural(keys, (kv,), 0)
        fill_tiles(vals, (kv,), 1)
    for tile in range(pieces):
        cols = slice(tile * TILE, (tile + 1) * TILE)
        lab = qlab[:, cols]
        state = []
        for g in range(rows // HEAD_SIZE):
            state += [tops[g : g + 1, cols], totals[g : g + 1, cols], mix[head_rows(g), cols]]
        stop = jnp.minimum(span[2 * tile + 1], pieces)
        state = absorb(state, span[2 * tile], stop, 0, q, cols, lab, klab, keys0, vals0)
        start = jnp.maximum(span[2 * tile], 2 * pieces)
        state = absorb(
            state, start, span[2 * tile + 1], 2 * pieces, q, cols, lab, klab, keys2, vals2
        )
        for g in range(rows // HEAD_SIZE):
            top, total, acc = state[3 * g : 3 * g + 3]
            out[head_rows(g), cols] = (acc / total).astype(BF16)
            lse[g : g + 1, cols] = top + jnp.log(total)
    place = span[2 * pieces]
    share = own.shape[0]

    def sent(r):
        return dot_tn(out[:, relative(place, r, share)], w_out[...])

    away[:share, :] = sent(1).astype(BF16)
    away[share:, :] = sent(3).astype(BF16)
    low[...] = sent(2).astype(BF16)
    own[...] = sent(0)


def backward_body(span, q, kv0, kv1, kv2, tk, tv, qlab, klab, w_out, out, lse,
                  g0, g1, g2, g3, dq, to_prev, kept, to_next, times,
                  og, keys, vals, tkeys, ak, av, dtk, dtv):
    rows, size = q.shape
    group = rows // HEAD_SIZE
    pieces = size // TILE
    share = g0.shape[0]
    for r, ref in enumerate((g0, g1, g2, g3)):
        og[:, relative(span[2 * pieces], r, share)] = dot_nt(w_out[...], ref[...]).astype(BF16)
    fill_natural(keys, (kv0, kv1, kv2), 0)
    fill_natural(vals, (kv0, kv1, kv2), 1)
    fill_tiles(tkeys, (kv0, kv1, kv2), 0)
    ak[...] = jnp.zeros_like(ak)
    av[...] = jnp.zeros_like(av)
    for tile in range(pieces):
        cols = slice(tile * TILE, (tile + 1) * TILE)
        lab = qlab[:, cols]
        state, norms, deltas = [], [], []
        for g in range(group):
            hr = head_rows(g)
            qf = q[hr, cols].astype(F32)
            gf = og[hr, cols].astype(F32)
            norm = lse[g : g + 1, cols]
            delta = jnp.sum(gf * out[hr, cols].astype(F32), 0, keepdims=True)
            pt = jnp.exp(jnp.sum(qf * tk[hr, :], 0, keepdims=True) - norm)
            st = pt * (jnp.sum(gf * tv[hr, :], 0, keepdims=True) - delta)
            gk = jnp.sum(qf * st, 1, keepdims=True)
            gv = jnp.sum(gf * pt, 1, keepdims=True)
            if tile == 0:
                dtk[hr, :] = gk
                dtv[hr, :] = gv
            else:
                dtk[hr, :] += gk
                dtv[hr, :] += gv
            state.append(tk[hr, :] * st)
            norms.append(norm)
            deltas.append(delta)

        def step(j, state):
            start = pl.multiple_of(j * TILE, TILE)
            seen = klab[pl.ds(start, TILE), :] == lab
            fresh = []
            for g in range(group):
                hr = head_rows(g)
                s = dot_nn(keys[pl.ds(start, TILE), hr], q[hr, cols])
                p = jnp.exp(jnp.where(seen, s, -1e30) - norms[g])
                m = dot_nn(vals[pl.ds(start, TILE), hr], og[hr, cols])
                ds = (p * (m - deltas[g])).astype(BF16)
                av[j, hr, :] += dot_nt(og[hr, cols], p.astype(BF16))
                ak[j, hr, :] += dot_nt(q[hr, cols], ds)
                fresh.append(state[g] + dot_nn(tkeys[j, hr, :], ds))
            return tuple(fresh)

        state = lax.fori_loop(span[2 * tile], span[2 * tile + 1], step, tuple(state))
        for g in range(group):
            dq[head_rows(g), cols] = state[g]
    for at, column in ((0, dtk), (1, dtv)):
        spread = jnp.broadcast_to(column[...], (rows, 2 * HEAD_SIZE))
        times[at : at + 1, :] = spread.T[:1, :]
    for part, dest in enumerate((to_prev, kept, to_next)):
        for piece in range(pieces):
            at = slice(piece * TILE, (piece + 1) * TILE)
            dest[0, :, at] = ak[part * pieces + piece].astype(dest.dtype)
            dest[1, :, at] = av[part * pieces + piece].astype(dest.dtype)


def attend_near(span, q, kv, tk, tv, qlab, klab):
    cols, size = q.shape
    wide = lambda *dims: jax.ShapeDtypeStruct(dims, F32)
    vmem = pl.BlockSpec(memory_space=pltpu.VMEM)
    return pl.pallas_call(
        near_body,
        in_specs=[pl.BlockSpec(memory_space=pltpu.SMEM)] + [vmem] * 6,
        out_specs=[vmem] * 3,
        out_shape=[wide(cols // HEAD_SIZE, size), wide(cols // HEAD_SIZE, size), wide(cols, size)],
        scratch_shapes=[pltpu.VMEM((size, cols), BF16), pltpu.VMEM((size // TILE, cols, TILE), BF16)],
        name="attend_near", cost_estimate=FREE,
    )(span, q, kv, tk, tv, qlab, klab)


def attend_far(span, q, behind, ahead, qlab, klab, w_out, state):
    cols, size = q.shape
    share, width = size // 4, w_out.shape[1]
    low = lambda *dims: jax.ShapeDtypeStruct(dims, BF16)
    wide = lambda *dims: jax.ShapeDtypeStruct(dims, F32)
    vmem = pl.BlockSpec(memory_space=pltpu.VMEM)
    keys = pltpu.VMEM((size, cols), BF16)
    vals = pltpu.VMEM((size // TILE, cols, TILE), BF16)
    return pl.pallas_call(
        far_body,
        in_specs=[pl.BlockSpec(memory_space=pltpu.SMEM)] + [vmem] * 9,
        out_specs=[vmem] * 5,
        out_shape=[low(cols, size), wide(cols // HEAD_SIZE, size), low(2 * share, width),
                   wide(share, width), low(share, width)],
        scratch_shapes=[keys, keys, vals, vals],
        name="attend_far", cost_estimate=FREE,
    )(span, q, behind, ahead, qlab, klab, w_out, *state)


def attend_back(span, q, kvs, tk, tv, qlab, klab, w_out, out, lse, grads):
    cols, size = q.shape
    tiles = 3 * size // TILE
    low = lambda *dims: jax.ShapeDtypeStruct(dims, BF16)
    wide = lambda *dims: jax.ShapeDtypeStruct(dims, F32)
    vmem = pl.BlockSpec(memory_space=pltpu.VMEM)
    return pl.pallas_call(
        backward_body,
        in_specs=[pl.BlockSpec(memory_space=pltpu.SMEM)] + [vmem] * 15,
        out_specs=[vmem] * 5,
        out_shape=[wide(cols, size), low(2, cols, size), wide(2, cols, size), low(2, cols, size),
                   wide(2, cols)],
        scratch_shapes=[pltpu.VMEM((cols, size), BF16), pltpu.VMEM((3 * size, cols), BF16),
                        pltpu.VMEM((3 * size, cols), BF16), pltpu.VMEM((tiles, cols, TILE), BF16),
                        pltpu.VMEM((tiles, cols, TILE), F32), pltpu.VMEM((tiles, cols, TILE), F32),
                        pltpu.VMEM((cols, 1), F32), pltpu.VMEM((cols, 1), F32)],
        name="attend_back", cost_estimate=FREE,
    )(span, q, *kvs, tk, tv, qlab, klab, w_out, out, lse, *grads)


def tail_body(place, dq, kept, ahead, behind, cosine, sine, wq, wk, wv, times,
              raw, away, own, low, flipped):
    part, size = dq.shape
    half = HEAD_SIZE // 2

    def returned(block, base, scale):
        for h in range(part // HEAD_SIZE):
            a = block[h * HEAD_SIZE : h * HEAD_SIZE + half, :]
            b = block[h * HEAD_SIZE + half : (h + 1) * HEAD_SIZE, :]
            at = base + h * HEAD_SIZE
            raw[at : at + half, :] = ((a * cosine[...] + b * sine[...]) * scale).astype(BF16)
            raw[at + half : at + HEAD_SIZE, :] = (
                (b * cosine[...] - a * sine[...]) * scale
            ).astype(BF16)

    def whole(index):
        return kept[index] + ahead[index].astype(F32) + behind[index].astype(F32)

    returned(dq[...], 0, 1.0 / math.sqrt(HEAD_SIZE))
    returned(whole(0), part, 1.0)
    raw[2 * part : 3 * part, :] = whole(1).astype(BF16)
    raw[3 * part :, :] = jnp.zeros((16, size), BF16)
    raw[3 * part : 3 * part + 2, :part] = times[...].astype(BF16)
    flipped[...] = raw[: 3 * part, :].T

    def sent(r):
        at = relative(place[0], r, part)
        return sum(
            dot_nt(flipped[:, i * part : (i + 1) * part], weight[at, :])
            for i, weight in enumerate((wq, wk, wv))
        )

    away[:size, :] = sent(1).astype(BF16)
    away[size:, :] = sent(3).astype(BF16)
    low[...] = sent(2).astype(BF16)
    own[...] = sent(0)


def tail(place, dq, kept, ahead, behind, tables, wq, wk, wv, times):
    part, size = dq.shape
    low = lambda *dims: jax.ShapeDtypeStruct(dims, BF16)
    vmem = pl.BlockSpec(memory_space=pltpu.VMEM)
    return pl.pallas_call(
        tail_body,
        in_specs=[pl.BlockSpec(memory_space=pltpu.SMEM)] + [vmem] * 10,
        out_specs=[vmem] * 4,
        out_shape=[low(3 * part + 16, size), low(2 * size, part), jax.ShapeDtypeStruct((size, part), F32),
                   low(size, part)],
        scratch_shapes=[pltpu.VMEM((size, 3 * part), BF16)],
        name="tail", cost_estimate=FREE,
    )(place, dq, kept, ahead, behind, *tables, wq, wk, wv, times)


def rotary_tables(frame_positions):
    half_dim = HEAD_SIZE // 2
    frequency = jnp.exp(jnp.arange(half_dim, dtype=jnp.float32) * (-math.log(10000.0) / half_dim))
    angles = frequency[:, None] * frame_positions[None, :]
    return (jnp.cos(angles), jnp.sin(angles))


def rotate(rows, tables, sign=1.0):
    count, size = rows.shape
    halves = rows.reshape(count // HEAD_SIZE, 2, HEAD_SIZE // 2, size)
    cosine, sine = tables[0][None], tables[1][None] * sign
    first = halves[:, 0] * cosine - halves[:, 1] * sine
    second = halves[:, 1] * cosine + halves[:, 0] * sine
    return jnp.stack([first, second], 1).reshape(count, size)


def product(left, right):
    return jnp.dot(left, right, preferred_element_type=jnp.float32)


def inner_rows(left, right):
    return jnp.einsum("nd,nf->df", left, right, preferred_element_type=jnp.float32)


def back_project(gradient, weight):
    return jnp.einsum("nf,df->nd", gradient, weight, preferred_element_type=jnp.float32)


def by_feature(left, right):
    return jnp.einsum("nd,df->fn", left, right, preferred_element_type=jnp.float32)


def columns(weight, start, size):
    return lax.dynamic_slice_in_dim(weight, start, size, 1)


def rows_of(weight, start, size):
    return lax.dynamic_slice_in_dim(weight, start, size, 0)


def normalize(value_rows):
    means = jnp.mean(value_rows, -1, keepdims=True)
    centred = value_rows - means
    inverse = lax.rsqrt(jnp.mean(centred * centred, -1, keepdims=True) + 1e-05)
    return centred * inverse, inverse


def norm_backward(gradient, scaled, inverse, norm_gain):
    scaled_grad = gradient * norm_gain
    plain = jnp.mean(scaled_grad, -1, keepdims=True)
    cross = jnp.mean(scaled_grad * scaled, -1, keepdims=True)
    return inverse * (scaled_grad - plain - scaled * cross)


FREE = pl.CostEstimate(flops=1, transcendentals=0, bytes_accessed=1)


def dot_nn(left, right):
    return lax.dot_general(left, right, (((1,), (0,)), ((), ())), preferred_element_type=F32)


def dot_nt(left, right):
    return lax.dot_general(left, right, (((1,), (1,)), ((), ())), preferred_element_type=F32)


def dot_tn(left, right):
    return lax.dot_general(left, right, (((0,), (0,)), ((), ())), preferred_element_type=F32)


def head_weights(query, key, lanes, which):
    mine = jnp.where(lanes == which, query, jnp.zeros_like(query))
    scores = dot_nt(mine, key) * (1.0 / math.sqrt(HEAD_SIZE))
    weights = jnp.exp(scores - jnp.max(scores, -1, keepdims=True))
    return weights / jnp.sum(weights, -1, keepdims=True)


def pair_cols(refs, p, rows):
    ref = refs[p * 2 * HEAD_SIZE // refs[0].shape[1]]
    start = p * 2 * HEAD_SIZE % refs[0].shape[1]
    return ref[rows, start : start + 2 * HEAD_SIZE]


def cross_forward_body(width_block, place, rows, own, got, far, norms, q0, q1, q2, q3,
                       c0, c1, c2, c3, o0, o1, o2, o3,
                       front, queries, first, second, normed_three,
                       flip_own, flip_away):
    width = rows.shape[1]
    kv = (c0, c1, c2, c3)
    context_rows = c0.shape[0] // 2
    key_rows, value_rows = slice(0, context_rows), slice(context_rows, 2 * context_rows)
    lanes = lax.broadcasted_iota(jnp.int32, (rows.shape[0], 2 * HEAD_SIZE), 1) // HEAD_SIZE
    residual = (
        rows[...].astype(F32) + own[...] + got[...].astype(F32) + far[...].astype(F32)
    )
    first[...] = residual
    scaled, _ = normalize(residual)
    low = (scaled * norms[2:3, :] + norms[3:4, :]).astype(BF16)
    front[:, :width] = low
    part = width // 4
    for b, ref in enumerate((q0, q1, q2, q3)):
        queries[:, b * part : (b + 1) * part] = dot_nn(low, ref[...]).astype(BF16)
    for p in range(width // (2 * HEAD_SIZE)):
        cols = slice(p * 2 * HEAD_SIZE, (p + 1) * 2 * HEAD_SIZE)
        q, k, v = queries[:, cols], pair_cols(kv, p, key_rows), pair_cols(kv, p, value_rows)
        mixed = [dot_nn(head_weights(q, k, lanes, g).astype(BF16), v) for g in (0, 1)]
        front[:, width + cols.start : width + cols.stop] = jnp.where(lanes == 0, mixed[0], mixed[1]).astype(BF16)
    for b, ref in enumerate((o0, o1, o2, o3)):
        residual = residual + dot_nn(front[:, width + b * part : width + (b + 1) * part], ref[...])
    second[...] = residual
    scaled, _ = normalize(residual)
    low = (scaled * norms[4:5, :] + norms[5:6, :]).astype(BF16)
    normed_three[...] = low
    deal_rows(low.T, width_block, place[0], flip_own, flip_away)


def cross_forward(devices, place, rows, own, got, far, norms, query_parts, kv_parts, out_parts):
    size, width = rows.shape
    low = jax.ShapeDtypeStruct(rows.shape, BF16)
    both = jax.ShapeDtypeStruct((size, 2 * width), BF16)
    wide = jax.ShapeDtypeStruct(rows.shape, F32)
    flip = jax.ShapeDtypeStruct((width // 2, size), BF16)
    vmem = pl.BlockSpec(memory_space=pltpu.VMEM)
    block = pl.BlockSpec((size, width), lambda i: (0, 0))
    return pl.pallas_call(
        functools.partial(cross_forward_body, width // devices),
        grid=(1,),
        in_specs=[pl.BlockSpec(memory_space=pltpu.SMEM)] + [block] * 4 + [vmem] * 13,
        out_shape=[both, low, wide, wide, low, flip, flip],
        cost_estimate=FREE, name="cross",
    )(place, rows, own, got, far, norms, *query_parts, *kv_parts, *out_parts)


def deal_rows(rows, size, column, own, away):
    for b in range(rows.shape[0] // (2 * size)):
        at = slice(b * size, (b + 1) * size)
        even = rows[2 * b * size : (2 * b + 1) * size, :]
        odd = rows[(2 * b + 1) * size : (2 * b + 2) * size, :]

        @pl.when(column == 0)
        def _():
            own[at, :] = even
            away[at, :] = odd

        @pl.when(column != 0)
        def _():
            own[at, :] = odd
            away[at, :] = even


def ffn_part(normed, grad, gate_w, up_w, down_w, hidden, hid_own, hid_away, gate_grad, lifted_grad,
             unit_block, column):
    gate = dot_nn(normed, gate_w[...])
    lifted = dot_nn(normed, up_w[...])
    back = dot_nt(grad, down_w[...]).astype(BF16).astype(F32)
    sig = jax.nn.sigmoid(gate)
    swish = gate * sig
    made = (swish * lifted).astype(BF16)
    hidden[...] = made
    deal_rows(made.T, unit_block, column, hid_own, hid_away)
    gg = (back * lifted * sig * (1.0 + gate * (1.0 - sig))).astype(BF16)
    lg = (back * swish).astype(BF16)
    gate_grad[...] = gg
    lifted_grad[...] = lg
    return dot_nt(gg, gate_w[...]) + dot_nt(lg, up_w[...])


def ffn_first_body(unit_block, place, n0, n1, n2, n3, g0, g1, g2, g3, gate_w, up_w, down_w,
                   hidden, hid_own, hid_away, gate_grad, lifted_grad, normed, grad, grad_pair,
                   total):
    share, part = n0.shape[0], g0.shape[2]
    for b, ref in enumerate((n0, n1, n2, n3)):
        normed[b * share : (b + 1) * share, :] = ref[...]
    for c, ref in enumerate((g0, g1, g2, g3)):
        for b in range(4):
            rows, cols = relative(place[1], b, share), relative(place[1], c, part)
            grad[b * share : (b + 1) * share, cols] = ref[0, rows, :]
            grad_pair[b * share : (b + 1) * share, cols] = ref[1, rows, :]
    total[...] = ffn_part(
        normed[...], grad[...], gate_w, up_w, down_w, hidden, hid_own, hid_away, gate_grad,
        lifted_grad, unit_block, place[0],
    )


def ffn_second_body(unit_block, place, normed, grad, total, gate_w, up_w, down_w,
                    hidden, hid_own, hid_away, gate_grad, lifted_grad, away, own, low):
    share = own.shape[0]
    found = total[...] + ffn_part(
        normed[...], grad[...], gate_w, up_w, down_w, hidden, hid_own, hid_away, gate_grad,
        lifted_grad, unit_block, place[0],
    )
    own[...] = found[:share, :]
    low[...] = found[2 * share : 3 * share, :].astype(BF16)
    away[:share, :] = found[share : 2 * share, :].astype(BF16)
    away[share:, :] = found[3 * share :, :].astype(BF16)


def ffn(devices, place, half, inputs, gate_w, up_w, down_w):
    share = inputs[0].shape[0] if half == 0 else inputs[0].shape[0] // 4
    width = inputs[0].shape[1]
    size, units = 4 * share, gate_w.shape[1]
    tile = units // 2
    low = lambda *dims: jax.ShapeDtypeStruct(dims, BF16)
    wide = lambda *dims: jax.ShapeDtypeStruct(dims, F32)
    vmem = pl.BlockSpec(memory_space=pltpu.VMEM)
    cols = pl.BlockSpec((width, tile), lambda i: (0, half))
    rows = pl.BlockSpec((tile, width), lambda i: (half, 0))
    made = [low(size, tile), low(tile // 2, size), low(tile // 2, size), low(size, tile),
            low(size, tile)]
    if half == 0:
        made += [low(size, width), low(size, width), low(size, width), wide(size, width)]
    else:
        made += [low(2 * share, width), wide(share, width), low(share, width)]
    return pl.pallas_call(
        functools.partial(ffn_second_body if half else ffn_first_body, units // devices),
        grid=(1,),
        in_specs=[pl.BlockSpec(memory_space=pltpu.SMEM)] + [vmem] * len(inputs)
        + [cols, cols, rows],
        out_specs=[vmem] * len(made),
        out_shape=made,
        cost_estimate=FREE, name="ffn",
    )(place, *inputs, gate_w, up_w, down_w)


def cross_backward_body(own, got, far, grad, first, second, norms, q0, q1, q2, q3,
                        c0, c1, c2, c3, o0, o1, o2, o3, queries,
                        back_rows, kv_grad, vectors, grad_one, crossed_grad):
    width = grad.shape[1]
    kv = (c0, c1, c2, c3)
    context_rows = c0.shape[0] // 2
    key_rows, value_rows = slice(0, context_rows), slice(context_rows, 2 * context_rows)
    part = width // 4
    lanes = lax.broadcasted_iota(jnp.int32, (grad.shape[0], 2 * HEAD_SIZE), 1) // HEAD_SIZE
    lane_k = lax.broadcasted_iota(jnp.int32, (context_rows, 2 * HEAD_SIZE), 1) // HEAD_SIZE
    scale = 1.0 / math.sqrt(HEAD_SIZE)
    arrived = own[...] + got[...].astype(F32) + far[...].astype(F32)
    scaled, inverse = normalize(second[...])
    vectors[0:1, :] = jnp.sum(arrived * scaled, 0, keepdims=True)
    vectors[1:2, :] = jnp.sum(arrived, 0, keepdims=True)
    two = grad[...].astype(F32) + norm_backward(arrived, scaled, inverse, norms[4:5, :])
    low = two.astype(BF16)
    back_rows[:, :width] = low
    for b, ref in enumerate((o0, o1, o2, o3)):
        crossed_grad[:, b * part : (b + 1) * part] = dot_nt(low, ref[...]).astype(BF16)
    for p in range(width // (2 * HEAD_SIZE)):
        cols = slice(p * 2 * HEAD_SIZE, (p + 1) * 2 * HEAD_SIZE)
        q, k, v = queries[:, cols], pair_cols(kv, p, key_rows), pair_cols(kv, p, value_rows)
        g_rows = crossed_grad[:, cols]
        found = []
        for g in (0, 1):
            probs = head_weights(q, k, lanes, g)
            change = dot_nt(jnp.where(lanes == g, g_rows, jnp.zeros_like(g_rows)), v)
            delta = jnp.sum(change * probs, -1, keepdims=True)
            ds = (probs * (change - delta)).astype(BF16)
            found.append((dot_nn(ds, k), dot_tn(ds, q), dot_tn(probs.astype(BF16), g_rows)))
        back_rows[:, width + cols.start : width + cols.stop] = (
            jnp.where(lanes == 0, found[0][0], found[1][0]) * scale
        ).astype(BF16)
        kv_grad[:context_rows, cols] = (
            jnp.where(lane_k == 0, found[0][1], found[1][1]) * scale
        ).astype(BF16)
        kv_grad[context_rows:, cols] = jnp.where(lane_k == 0, found[0][2], found[1][2]).astype(
            BF16
        )
    back = jnp.zeros(grad.shape, F32)
    for b, ref in enumerate((q0, q1, q2, q3)):
        back = back + dot_nt(back_rows[:, width + b * part : width + (b + 1) * part], ref[...])
    scaled, inverse = normalize(first[...])
    vectors[2:3, :] = jnp.sum(back * scaled, 0, keepdims=True)
    vectors[3:4, :] = jnp.sum(back, 0, keepdims=True)
    grad_one[...] = (two + norm_backward(back, scaled, inverse, norms[2:3, :])).astype(BF16)


def cross_backward(own, got, far, grad, first, second, norms, query_parts, kv_parts, out_parts,
                   queries):
    rows, width = own.shape
    low = lambda r: jax.ShapeDtypeStruct((r, width), BF16)
    block = pl.BlockSpec((rows, width), lambda i: (0, 0))
    return pl.pallas_call(
        cross_backward_body,
        grid=(1,),
        out_shape=[jax.ShapeDtypeStruct((rows, 2 * width), BF16), low(kv_parts[0].shape[0]),
                   jax.ShapeDtypeStruct((4, width), F32), low(rows)],
        in_specs=[block] * 6 + [pl.BlockSpec(memory_space=pltpu.VMEM)] * 14,
        scratch_shapes=[pltpu.VMEM((rows, width), BF16)],
        cost_estimate=FREE, name="cross_back",
    )(own, got, far, grad, first, second, norms, *query_parts, *kv_parts, *out_parts, queries)


def meet_rows_body(size, side, own_a, pair_a, own_b, pair_b, right, right_pair, keep, send):
    half = keep.shape[0] // 2
    for b, (own, pair) in enumerate(((own_a, pair_a), (own_b, pair_b))):
        made = (dot_nn(own[...], right[...]) + dot_nn(pair[...], right_pair[...])).astype(BF16)
        at = pl.ds(b * half, half)
        deal_rows(made, size, side[0], keep.at[at], send.at[at])


def meet_rows(size, side, lefts, rights):
    count, frames = lefts[0].shape
    width = rights[0].shape[1]
    tile = width // 3
    left = pl.BlockSpec((count, frames), lambda i: (0, 0))
    right = pl.BlockSpec((frames, tile), lambda i: (0, i))
    return pl.pallas_call(
        functools.partial(meet_rows_body, size),
        grid=(3,),
        in_specs=[pl.BlockSpec(memory_space=pltpu.SMEM)] + [left] * 4 + [right] * 2,
        out_specs=[pl.BlockSpec((count, tile), lambda i: (0, i))] * 2,
        out_shape=[jax.ShapeDtypeStruct((count, width), BF16)] * 2,
        name="meet_rows", cost_estimate=FREE,
    )(side, *lefts, *rights)


def meet_cols_body(size, side, p0, p1, p2, p3, *refs):
    own, pair = (jnp.concatenate([p[i] for p in (p0, p1, p2, p3)], 1) for i in (0, 1))
    *rights, keep, send = refs
    width = rights[0].shape[1]
    for at in range(len(rights) // 2):
        made = dot_nn(own, rights[2 * at][...]) + dot_nn(pair, rights[2 * at + 1][...])
        cols = pl.ds(at * width, width)
        deal_rows(made.astype(BF16), size, side[0], keep.at[:, cols], send.at[:, cols])


def meet_cols(size, side, near, rights):
    width = rights[0].shape[1] * (len(rights) // 2)
    half = jax.ShapeDtypeStruct((near[0].shape[1] // 2, width), BF16)
    vmem = pl.BlockSpec(memory_space=pltpu.VMEM)
    return pl.pallas_call(
        functools.partial(meet_cols_body, size),
        in_specs=[pl.BlockSpec(memory_space=pltpu.SMEM)] + [vmem] * (4 + len(rights)),
        out_shape=[half] * 2,
        name="meet_cols", cost_estimate=FREE,
    )(side, *near, *rights)


def down_body(first, second, down_w, away, own, low):
    share, units = own.shape[0], first.shape[1]

    def sent(r):
        at = slice(r * share, (r + 1) * share)
        return dot_nn(first[at, :], down_w[:units, :]) + dot_nn(second[at, :], down_w[units:, :])

    away[:share, :] = sent(1).astype(BF16)
    away[share:, :] = sent(3).astype(BF16)
    low[...] = sent(2).astype(BF16)
    own[...] = sent(0)


def down_parts(first, second, down_w):
    share, width = first.shape[0] // 4, down_w.shape[1]
    low = lambda *dims: jax.ShapeDtypeStruct(dims, BF16)
    return pl.pallas_call(
        down_body,
        out_shape=[low(2 * share, width), jax.ShapeDtypeStruct((share, width), F32),
                   low(share, width)],
        name="down", cost_estimate=FREE,
    )(first, second, down_w)


def bundle_body(devices, place, f02, f13, b02, b13, a0, a1, a2, a3, attended,
                context, kv, keep_a, send_a, keep_b, send_b):
    width = a0.shape[1]
    part, share = width // 4, a0.shape[0]

    def near(even, odd):
        return even[0], odd[0], even[1], odd[1]

    own = lambda rows: jnp.concatenate(
        [row[:, width + r * part : width + (r + 1) * part] for r, row in enumerate(rows)], 0
    )
    full = lambda rows: jnp.concatenate([row[:, :width] for row in rows], 0)
    fronts, backs = near(f02, f13), near(b02, b13)
    rows = width // devices
    small = part // devices
    half = width // 2

    def put(block, base, left, out):
        size = block.shape[0] // devices
        cols = slice(left, left + block.shape[1])
        low = block.astype(BF16)
        for d in range(0, devices, 2):
            at = slice(base, base + size)
            even, odd = low[d * size : (d + 1) * size, :], low[(d + 1) * size : (d + 2) * size, :]

            @pl.when(place[0] == 0)
            def _():
                out[0][d // 2, at, cols] = even
                out[1][d // 2, at, cols] = odd

            @pl.when(place[0] != 0)
            def _():
                out[0][d // 2, at, cols] = odd
                out[1][d // 2, at, cols] = even

    put(dot_tn(full(fronts), own(backs)), 0, 0, (keep_a, send_a))
    count = context.shape[0]
    put(dot_tn(context[...], kv[:count, :]), 0, part, (keep_a, send_a))
    put(dot_tn(context[...], kv[count:, :]), rows // 2, part, (keep_a, send_a))
    grads = dot_tn(own(fronts), full(backs))
    put(grads[:, :half], 0, 0, (keep_b, send_b))
    put(grads[:, half:], small, 0, (keep_b, send_b))
    grads = sum(
        dot_nn(attended[:, relative(place[1], r, share)], ref[...])
        for r, ref in enumerate((a0, a1, a2, a3))
    )
    put(grads[:, :half], 2 * small, 0, (keep_b, send_b))
    put(grads[:, half:], 3 * small, 0, (keep_b, send_b))


def bundle_grads(devices, place, fronts, backs, ones, attended, context, kv):
    width = ones[0].shape[1]
    vmem = pl.BlockSpec(memory_space=pltpu.VMEM)
    return pl.pallas_call(
        functools.partial(bundle_body, devices),
        in_specs=[pl.BlockSpec(memory_space=pltpu.SMEM)] + [vmem] * 11,
        out_specs=[vmem] * 4,
        out_shape=[jax.ShapeDtypeStruct((devices // 2, width // devices, width // 2), BF16)] * 4,
        name="bundle", cost_estimate=FREE,
    )(place, *fronts, *backs, *ones, attended, context, kv)


def front_body(width_block, place, x0, x1, x2, x3, g0, g1, g2, g3, cosine, sine, wq, wk, wv,
               time_row, context, ck, cv,
               queries, pair, rows, low, nrm_own, nrm_away, norms, means, inverses,
               time_scaled, time_low, time_keys, time_values, kv, wide):
    size, part = x0.shape
    for r, (x, g) in enumerate(((x0, g0), (x1, g1), (x2, g2), (x3, g3))):
        start = pl.multiple_of((place[0] ^ r) * part, 128)
        wide[:, pl.ds(start, part)] = x[...]
        norms[:, pl.ds(start, part)] = g[...]
    share = size // 4
    rows[...] = wide[pl.ds(pl.multiple_of(place[0] * share, share), share), :]
    values = wide[...].astype(F32)
    mean = jnp.mean(values, -1, keepdims=True)
    centred = values - mean
    inverse = lax.rsqrt(jnp.mean(centred * centred, -1, keepdims=True) + 1e-05)
    means[...] = mean
    inverses[...] = inverse
    normed = (centred * inverse * norms[0:1, :] + norms[1:2, :]).astype(BF16)
    low[...] = normed
    half = HEAD_SIZE // 2

    def turned(weight):
        return dot_nn(normed, weight[...]).T

    def rotated(block, dest, scale):
        for h in range(part // HEAD_SIZE):
            a = block[h * HEAD_SIZE : h * HEAD_SIZE + half, :]
            b = block[h * HEAD_SIZE + half : (h + 1) * HEAD_SIZE, :]
            dest[h * HEAD_SIZE : h * HEAD_SIZE + half, :] = (
                (a * cosine[...] - b * sine[...]) * scale
            ).astype(BF16)
            dest[h * HEAD_SIZE + half : (h + 1) * HEAD_SIZE, :] = (
                (b * cosine[...] + a * sine[...]) * scale
            ).astype(BF16)

    scaled, _ = normalize(jnp.broadcast_to(time_row[...].astype(F32), (8, 4 * part)))
    time_scaled[...] = scaled[:1, :]
    made = (scaled * norms[0:1, :] + norms[1:2, :]).astype(BF16)
    time_low[...] = made[:1, :].astype(F32)
    time_keys[...] = dot_nn(made, wk[...]).astype(BF16).astype(F32).T[:, :1]
    time_values[...] = dot_nn(made, wv[...]).astype(BF16).astype(F32).T[:, :1]
    count = context.shape[0]
    kv[:count, :] = dot_nn(context[...], ck[...]).astype(BF16)
    kv[count:, :] = dot_nn(context[...], cv[...]).astype(BF16)
    rotated(turned(wk), pair.at[0], 1.0)
    pair[1] = turned(wv).astype(BF16)
    rotated(turned(wq), queries, 1.0 / math.sqrt(HEAD_SIZE))
    deal_rows(normed.T, width_block, place[1], nrm_own, nrm_away)


def front(devices, place, parts, norm_parts, tables, wq, wk, wv, time_row, context, ck, cv):
    size, part = parts[0].shape
    width = 4 * part
    low = lambda *s: jax.ShapeDtypeStruct(s, BF16)
    wide = lambda *s: jax.ShapeDtypeStruct(s, F32)
    vmem = pl.BlockSpec(memory_space=pltpu.VMEM)
    return pl.pallas_call(
        functools.partial(front_body, width // devices),
        in_specs=[pl.BlockSpec(memory_space=pltpu.SMEM)] + [vmem] * 17,
        out_specs=[vmem] * 14,
        out_shape=[low(part, size), low(2, part, size), low(size // 4, width), low(size, width),
                   low(width // 2, size), low(width // 2, size), wide(6, width),
                   wide(size, 1), wide(size, 1), wide(1, width), wide(1, width), wide(part, 1),
                   wide(part, 1), low(2 * context.shape[0], part)],
        scratch_shapes=[pltpu.VMEM((size, width), BF16)],
        cost_estimate=FREE, name="front",
    )(place, *parts, *norm_parts, *tables, wq, wk, wv, time_row, context, ck, cv)


def per_device(
    frames,
    segment,
    time_token,
    context,
    gain_attn,
    bias_attn,
    gain_cross,
    bias_cross,
    gain_ffn,
    bias_ffn,
    w_query,
    w_key,
    w_value,
    w_out,
    c_query,
    c_key,
    c_value,
    c_out,
    w_gate,
    w_up,
    w_down,
    out_grad,
):
    local_rows = frames.shape[0]
    local_width = frames.shape[1]
    model_width = w_query.shape[0]
    head_cols = w_query.shape[1]
    heads = head_cols // HEAD_SIZE
    number_of_frames = lax.axis_size("seq") * local_rows
    row_length = min(max(ROW_MIN, 64 * lax.axis_size("seq")), number_of_frames)
    first_frame = lax.axis_index("seq") * local_rows
    own_start = lax.axis_index("tensor") * local_width

    def own_cols(value):
        return lax.dynamic_slice_in_dim(value, own_start, local_width, value.ndim - 1)

    place = lax.axis_index("tensor")
    share = local_rows // 4

    def row_block(value, index):
        return rows_of(value, index * share, share)

    column = lax.axis_index("seq") % 2
    frame_parts_near = gather_near(frames)
    norm_parts = gather_near(
        jnp.stack([gain_attn, bias_attn, gain_cross, bias_cross, gain_ffn, bias_ffn])
    )
    clip_starts, frame_positions = frame_clip_labels(segment, row_length)
    own_labels = lax.dynamic_slice_in_dim(clip_starts, first_frame, local_rows)
    own_positions = lax.dynamic_slice_in_dim(frame_positions, first_frame, local_rows)
    blanks = jnp.full((local_rows,), -1, jnp.int32)
    key_labels = lax.dynamic_slice_in_dim(
        jnp.concatenate([blanks, clip_starts, blanks]), first_frame, 3 * local_rows
    )
    spans = jnp.concatenate(
        [tile_ranges(own_labels, key_labels), place.astype(jnp.int32).reshape(1)]
    )
    places = jnp.stack([column, place]).astype(jnp.int32)
    label_row, label_column = own_labels[None, :], key_labels[:, None]
    row_index = first_frame // row_length
    time_row = lax.dynamic_slice_in_dim(time_token, row_index, 1, 0)
    row_context = lax.dynamic_slice_in_dim(context, row_index, 1, 0)[0]
    context_rows = row_context.shape[0]
    tables = rotary_tables(own_positions)
    score_scale = 1.0 / math.sqrt(HEAD_SIZE)
    all_heads = model_width // HEAD_SIZE

    (
        queries, both, frame_rows, frame_normed, one_own_half, one_away_half, norms, means_one,
        inverse_one, scaled_time, time_normed, time_keys, time_values, context_kv,
    ) = front(
        lax.axis_size("seq"), jnp.flip(places), frame_parts_near, norm_parts, tables, w_query,
        w_key, w_value, time_row, row_context, c_key, c_value,
    )
    both, out_pair = meeting(both, swap(after(out_grad, frame_parts_near[2]), "seq", 1))
    grad_both = jnp.stack([out_grad, out_pair])
    behind, ahead = shift(both, "seq", 1), shift(both, "seq", -1)
    query_late, out_late = after((c_query, c_out), (frame_parts_near[2], norm_parts[2]))
    query_far, out_far = swap(query_late, "tensor", 2), swap(out_late, "tensor", 2)
    state = attend_near(spans, queries, both, time_keys, time_values, label_row, label_column)
    behind, ahead, query_far, out_far, *state = meeting(
        behind, ahead, query_far, out_far, *state
    )
    query_own, out_own, context_late = after((c_query, c_out, context_kv), behind)
    weights_near = [
        swap(value, "tensor", 1) for value in (query_own, query_far, out_own, out_far)
    ]
    kv_far = swap(context_late, "tensor", 2)
    attended, log_totals, one_away, one_own, one_low = attend_far(
        spans, queries, behind, ahead, label_row, label_column, w_out, state
    )
    one_away, one_low, kv_far, *weights_near = meeting(one_away, one_low, kv_far, *weights_near)
    kv_both = jnp.concatenate([context_kv, kv_far], 0)
    kv_other = swap(kv_both, "tensor", 1)
    kv_rows = context_kv.shape[0]
    kv_parts = (context_kv, kv_other[:kv_rows], kv_far, kv_other[kv_rows:])
    query_parts = (c_query, weights_near[0], query_far, weights_near[1])
    out_parts = (c_out, weights_near[2], out_far, weights_near[3])
    one_got, _, one_far = scatter_near(one_away, one_low)
    (
        front_rows, cross_queries, residual_one, residual_two, normed_share, flip_own, flip_away,
    ) = cross_forward(
        lax.axis_size("seq"), places, frame_rows, one_own, one_got, one_far, norms,
        query_parts, kv_parts, out_parts,
    )
    grad_far = swap(after(grad_both, one_far), "tensor", 2)
    normed_share, normed_got, grad_far = meeting(
        normed_share, swap(after(one_away_half, one_low), "seq", 1), grad_far
    )
    grad_late, grad_far_late = after((grad_both, grad_far), normed_share)
    grad_mate, grad_far_mate = swap(grad_late, "tensor", 1), swap(grad_far_late, "tensor", 1)
    grad_parts = (grad_both, grad_mate, grad_far, grad_far_mate)
    three_parts = gather_near(normed_share)
    flip_got = swap(after(flip_away, normed_share), "seq", 1)
    front_far = swap(after(front_rows, three_parts[3]), "tensor", 2)
    devices = lax.axis_size("seq")
    (
        hidden_a, hidden_own_a, hidden_away_a, gate_a, lifted_a, normed_three, grad_near, grad_pair,
        ffn_total,
    ) = ffn(devices, places, 0, (*three_parts, *grad_parts), w_gate, w_up, w_down)
    ffn_total, flip_got = meeting(ffn_total, flip_got)
    flip_both = jnp.stack([flip_own, flip_got])
    flip_far = swap(flip_both, "tensor", 2)
    hidden_got_a, gate_got_a = swap(hidden_away_a, "seq", 1), swap(gate_a, "seq", 1)
    hidden_b, hidden_own_b, hidden_away_b, gate_b, lifted_b, three_away, three_own, three_low = ffn(
        devices, places, 1, (normed_three, grad_near, ffn_total), w_gate, w_up, w_down
    )
    three_away, three_low, flip_far, front_far, hidden_got_a = meeting(
        three_away, three_low, flip_far, front_far, hidden_got_a
    )
    three_got, _, three_far = scatter_near(three_away, three_low)
    three_far, gate_got_a = meeting(three_far, gate_got_a)
    lifted_got_a = swap(after(lifted_a, three_low), "seq", 1)
    flip_late, flip_far_late, gate_late = after((flip_both, flip_far, gate_b), three_far)
    flip_mate, flip_far_mate = swap(flip_late, "tensor", 1), swap(flip_far_late, "tensor", 1)
    gate_got_b = swap(gate_late, "seq", 1)
    front_both = jnp.stack([front_rows, front_far])
    back_rows, kv_grad, norm_vectors, grad_one = cross_backward(
        three_own, three_got, three_far, grad_near, residual_one, residual_two, norms,
        query_parts, kv_parts, out_parts, cross_queries,
    )
    grad_one, lifted_got_a, flip_mate, flip_far_mate = meeting(
        grad_one, lifted_got_a, flip_mate, flip_far_mate
    )
    hidden_got_b = swap(after(hidden_away_b, three_far), "seq", 1)
    count = lax.axis_size("seq")
    level_side = ((lax.axis_index("seq") >> 1) % 2).astype(jnp.int32).reshape(1)
    rows = model_width // count

    def traded(dealt):
        keep, send = [value.reshape(count // 4, rows, -1) for value in dealt]
        return keep, swap(send, "seq", 2)

    down_keep, down_got = traded(
        meet_rows(
            rows, level_side, (hidden_own_a, hidden_got_a, hidden_own_b, hidden_got_b),
            (grad_near, grad_pair),
        )
    )
    context_parts = quarters(kv_grad, 1)
    context_got = swap(jnp.concatenate([context_parts[1], context_parts[3]], 0), "tensor", 1)
    one_far_rows, down_keep = meeting(swap(grad_one, "tensor", 2), down_keep)
    one_parts = (
        grad_one, swap(grad_one, "tensor", 1), one_far_rows, swap(one_far_rows, "tensor", 1)
    )
    *one_parts, front_other, context_got = meeting(
        *one_parts, swap(after(front_both, grad_one), "tensor", 1), context_got
    )
    context_low = (
        context_parts[2].astype(F32) + context_got[context_parts[2].shape[0] :].astype(F32)
    ).astype(BF16)
    context_far = swap(context_low, "tensor", 2)
    back_far = swap(after(back_rows, one_parts[3]), "tensor", 2)
    lifted_got_b = swap(after(lifted_b, grad_one), "seq", 1)
    query_grad, to_prev, kept, to_next, time_grads = attend_back(
        spans, queries, (behind, both, ahead), time_keys, time_values, label_row, label_column,
        w_out, attended, log_totals, one_parts,
    )
    to_prev, to_next, back_far, gate_got_b, lifted_got_b, down_got, context_far = meeting(
        to_prev, to_next, back_far, gate_got_b, lifted_got_b, down_got, context_far
    )
    from_next, from_prev = shift(to_prev, "seq", -1), shift(to_next, "seq", 1)
    down_keep, down_got = halve(added(down_keep, down_got).astype(BF16), 2)
    flip_near = (flip_both, flip_mate, flip_far, flip_far_mate)
    first_keep, first_got = traded(
        meet_cols(
            rows, level_side, flip_near,
            after((gate_a, gate_got_a, lifted_a, lifted_got_a), to_prev),
        )
    )
    second_keep, second_got = traded(
        meet_cols(
            rows, level_side, flip_near,
            after((gate_b, gate_got_b, lifted_b, lifted_got_b), to_prev),
        )
    )
    back_both = jnp.stack([back_rows, back_far])
    back_other = swap(back_both, "tensor", 1)
    context_own = (
        context_parts[0].astype(F32)
        + context_got[: context_far.shape[0]].astype(F32)
        + context_far.astype(F32)
    )
    keep_a, send_a, keep_b, send_b = bundle_grads(
        count, places, (front_both, front_other), (back_both, back_other), one_parts, attended,
        row_context,
        context_own.astype(BF16),
    )
    from_next, from_prev, down_got, send_a, send_b = meeting(
        from_next, from_prev, down_got, send_a, send_b
    )
    got_a = swap(send_a, "seq", 1)
    raw, last_away, last_own, last_low = tail(
        places[1:], query_grad, kept, from_next, from_prev, tables, w_query, w_key, w_value,
        time_grads,
    )
    last_got = swap(last_away, "tensor", 1)
    raw_got = swap(raw, "seq", 1)
    last_sum = (
        last_low.astype(F32) + last_got[local_rows:].astype(F32)
    ).astype(BF16)
    last_sum, first_got, raw_got = meeting(last_sum, first_got, raw_got)
    first_keep, first_got = halve(added(first_keep, first_got).astype(BF16), 2)
    last_far, second_got = meeting(swap(last_sum, "tensor", 2), second_got)
    second_keep, second_got = halve(added(second_keep, second_got).astype(BF16), 2)
    frame_grad = last_own + last_got[:local_rows].astype(F32) + last_far.astype(F32)

    time_late, means_late, inverse_late, vectors_late = after(
        (time_grads, means_one, inverse_one, norm_vectors), last_far
    )
    time_grad = sum(
        jnp.einsum("of,df->od", time_late[i : i + 1].astype(BF16), w, preferred_element_type=F32)
        for i, w in enumerate((w_key, w_value))
    )
    own_scaled = (frames.astype(F32) - means_late) * inverse_late
    scaled_grad = frame_grad * gain_attn[None]
    sums = jnp.concatenate(
        [
            jnp.sum(scaled_grad, -1),
            jnp.sum(scaled_grad * own_scaled, -1),
            time_grad[0],
            vectors_late.reshape(-1),
        ]
    )[None]
    sums = sums + swap(sums, "tensor", 1)
    time_column = time_normed.T
    normed_pair = (one_own_half, normed_got)
    raw_pair = (raw[: 3 * head_cols], raw_got[: 3 * head_cols])
    time_got = raw_got[3 * head_cols : 3 * head_cols + 2, :head_cols].astype(F32)
    time_both = (time_grads + time_got).reshape(1, 2 * head_cols)
    own_time_rows = lax.dynamic_index_in_dim(
        time_column.reshape(count // 2, 2, -1), column, 1, False
    ).reshape(-1, 1)
    outer = own_time_rows * jnp.concatenate([jnp.zeros((1, head_cols), F32), time_both], 1)
    blocks = sum(
        jnp.einsum("dn,fn->df", r, c, preferred_element_type=F32)
        for r, c in zip(normed_pair, raw_pair)
    )
    blocks = (blocks + outer).astype(BF16).reshape(count // 2, rows, 3 * head_cols)
    heads_keep, heads_got = halve(blocks, 1)
    sums = sums + swap(sums, "tensor", 2)
    sums, heads_got, got_a = meeting(sums, heads_got, got_a)
    heads_next = added(heads_keep, heads_got).astype(BF16)
    heads_keep, heads_got = halve(heads_next, 2)
    left_keep, left_got = halve(added(keep_a, got_a).astype(BF16), 1)
    plain = sums[0, :local_rows, None] / model_width
    cross = sums[0, local_rows : 2 * local_rows, None] / model_width
    vectors = own_cols(sums[0, 2 * local_rows :].reshape(5, model_width))
    attend_full = ordered(*[after(one_parts, from_next)[i] for i in (0, 2, 1, 3)], 0)
    d_frames = own_cols(attend_full).astype(F32) + inverse_late * (
        scaled_grad - plain - own_scaled * cross
    )
    d_gain_attn = jnp.sum(frame_grad * own_scaled, 0) + vectors[0] * own_cols(scaled_time)[0]
    d_bias_attn = jnp.sum(frame_grad, 0) + vectors[0]


    grad_down = halve_end(down_keep, down_got, 3)
    got_b = swap(after(send_b, from_next), "seq", 1)
    down_away, down_own, down_low = down_parts(after(hidden_a, heads_next), hidden_b, w_down)
    branch_got, _, branch_far = scatter_near(down_away, down_low)
    left_got, got_b, first_got = meeting(left_got, got_b, first_got)
    right_keep, right_got = halve(added(keep_b, got_b).astype(BF16), 1)
    right_got, second_got, branch_far = meeting(right_got, second_got, branch_far)
    last_next = added(right_keep, right_got)
    left_keep, left_got = halve(added(left_keep, left_got).astype(BF16), 2)
    right_keep, right_got = halve(last_next.astype(BF16), 2)
    heads_got, left_got, right_got = meeting(heads_got, left_got, right_got)
    block_rows = (
        residual_two + down_own + branch_got[:share].astype(F32) + branch_far.astype(F32)
    ).astype(BF16)
    block_cols = rows_to_cols(
        *[
            lax.dynamic_slice_in_dim(block_rows, (place ^ r) * local_width, local_width, 1)
            for r in range(4)
        ],
        last_next,
    )
    block_out = jnp.concatenate([row_block(block_cols, place ^ b) for b in range(4)], 0)
    first, second = halve_end(first_keep, first_got, 3), halve_end(second_keep, second_got, 3)
    units = first.shape[1] // 2
    grad_gate_w = jnp.concatenate([first[:, :units], second[:, :units]], 1)
    grad_up_w = jnp.concatenate([first[:, units:], second[:, units:]], 1)
    small = jnp.stack(
        [d_gain_attn, d_bias_attn, vectors[3], vectors[4], vectors[1], vectors[2]]
    ).reshape(6, devices, -1).transpose(1, 0, 2)
    small = small.reshape(count // 4, 2, 2, 6, -1).swapaxes(1, 2).reshape(count, 6, -1)
    small = after(small, last_next)
    bits = [1, 0] + list(range(2, count.bit_length() - 1))
    for bit in bits:
        small = added(*halve(small, bit))
    small = small[0]
    heads_sum = halve_end(heads_keep, heads_got, 3)
    left, right = halve_end(left_keep, left_got, 3), halve_end(right_keep, right_got, 3)
    part, rows = head_cols // count, model_width // count
    grad_c_query = left[:, :head_cols]
    grad_c_key, grad_c_value = left[: rows // 2, head_cols:], left[rows // 2 :, head_cols:]
    grad_c_out = jnp.concatenate([right[:part], right[part : 2 * part]], 1)
    grad_w_out = jnp.concatenate([right[2 * part : 3 * part], right[3 * part :]], 1)
    grad_w_query, grad_w_key, grad_w_value = (
        heads_sum[:, i * head_cols : (i + 1) * head_cols] for i in range(3)
    )
    return (
        block_out,
        d_frames,
        small[0],
        small[1],
        small[2],
        small[3],
        small[4],
        small[5],
        grad_w_query,
        grad_w_key,
        grad_w_value,
        grad_w_out,
        grad_c_query,
        grad_c_key,
        grad_c_value,
        grad_c_out,
        grad_gate_w,
        grad_up_w,
        grad_down,
    )


def solution(mesh):
    return jax.shard_map(
        per_device,
        mesh=mesh,
        in_specs=(
            P("seq", "tensor"),
            P(),
            P(),
            P(),
            P("tensor"),
            P("tensor"),
            P("tensor"),
            P("tensor"),
            P("tensor"),
            P("tensor"),
            P(None, "tensor"),
            P(None, "tensor"),
            P(None, "tensor"),
            P("tensor", None),
            P(None, "tensor"),
            P(None, "tensor"),
            P(None, "tensor"),
            P("tensor", None),
            P(None, "tensor"),
            P(None, "tensor"),
            P("tensor", None),
            P("seq", "tensor"),
        ),
        out_specs=(
            P("seq", "tensor"),
            P("seq", "tensor"),
            P(("tensor", "seq")),
            P(("tensor", "seq")),
            P(("tensor", "seq")),
            P(("tensor", "seq")),
            P(("tensor", "seq")),
            P(("tensor", "seq")),
            P("seq", "tensor"),
            P("seq", "tensor"),
            P("seq", "tensor"),
            P(("tensor", "seq"), None),
            P("seq", "tensor"),
            P("seq", "tensor"),
            P("seq", "tensor"),
            P(("tensor", "seq"), None),
            P("seq", "tensor"),
            P("seq", "tensor"),
            P(("tensor", "seq"), None),
        ),
        check_vma=False,
    )
```

```python
import functools
import math

import jax
import jax.numpy as jnp
from jax import lax
from jax.experimental import pallas as pl
from jax.experimental.pallas import tpu as pltpu
from jax.sharding import PartitionSpec as P

HEAD_SIZE = 64
ROW_MIN = 2048
TILE = 256
BF16 = jnp.bfloat16
F32 = jnp.float32


def meeting(*values):
    return lax.optimization_barrier(values)


def after(value, token):
    return lax.optimization_barrier((value, token))[0]


def swap(value, axis, by):
    return lax.ppermute(value, axis, [(i, i ^ by) for i in range(lax.axis_size(axis))])


def shift(value, axis, by):
    peers = lax.axis_size(axis)
    pairs = [(i, i + by) for i in range(peers) if 0 <= i + by < peers]
    return lax.ppermute(value, axis, pairs)


def tensor_place():
    place = lax.axis_index("tensor")
    return place // 2, place % 2


def ordered(own, far, mate, far_mate, axis):
    side, core = tensor_place()
    near = (jnp.where(core == 0, own, mate), jnp.where(core == 0, mate, own))
    away = (jnp.where(core == 0, far, far_mate), jnp.where(core == 0, far_mate, far))
    low = [jnp.where(side == 0, n, a) for n, a in zip(near, away)]
    high = [jnp.where(side == 0, a, n) for n, a in zip(near, away)]
    return jnp.concatenate(low + high, axis)


def gather_near(own):
    far = swap(own, "tensor", 2)
    return own, swap(own, "tensor", 1), far, swap(far, "tensor", 1)


def gather_staged(own, first, second):
    far = swap(after(own, first), "tensor", 2)
    far, late = after((far, own), second)
    return own, swap(late, "tensor", 1), far, swap(far, "tensor", 1)


def gather(own, axis):
    own, mate, far, far_mate = gather_near(own)
    return ordered(own, far, mate, far_mate, axis)


def scatter_near(away, low):
    got = swap(away, "tensor", 1)
    total = (low.astype(F32) + got[low.shape[0] :].astype(F32)).astype(BF16)
    return got, total, swap(total, "tensor", 2)


def rows_to_cols(own, mate, far, far_mate, later):
    width = own.shape[1]
    got = after(swap(jnp.concatenate([far, far_mate], 1), "tensor", 2), later)
    other = swap(jnp.concatenate([mate, got[:, width:]], 0), "tensor", 1)
    size = own.shape[0]
    return jnp.concatenate([own, other[:size], got[:, :width], other[size:]], 0)


def quarters(value, axis):
    return jnp.split(value, 4, axis)


def own_blocks(near):
    return jnp.concatenate([quarters(value, 1)[r] for r, value in enumerate(near)], 0)


def trade(value, start, done):
    return after(swap(after(value, start), "seq", 1), done)


def halve(blocks, bit):
    count, rows, cols = blocks.shape
    side = (lax.axis_index("seq") >> bit) % 2
    parts = blocks.reshape(count // 2, 2, rows, cols)
    send = lax.dynamic_index_in_dim(parts, 1 - side, 1, False)
    keep = lax.dynamic_index_in_dim(parts, side, 1, False)
    return keep, swap(send, "seq", 1 << bit)


def added(keep, got):
    return keep.astype(F32) + got.astype(F32)


def halve_all(blocks, bit):
    while blocks.shape[0] > 1:
        blocks = added(*halve(blocks.astype(BF16), bit))
        bit += 1
    return blocks[0].astype(F32)


def halve_end(keep, got, bit):
    return halve_all(added(keep, got), bit)


def frame_clip_labels(segment, row_length):
    frame_index = jnp.arange(segment.shape[0], dtype=jnp.int32)
    border = (frame_index % row_length == 0) | (segment != jnp.roll(segment, 1))
    clip_starts = lax.cummax(jnp.where(border, frame_index, 0), axis=0)
    return (clip_starts, (frame_index - clip_starts + 1).astype(jnp.float32))


def tile_ranges(q_labels, key_labels):
    q = q_labels.reshape(-1, TILE)
    k = key_labels.reshape(-1, TILE)
    meets = (k[None, :, 0] <= q[:, None, -1]) & (k[None, :, -1] >= q[:, None, 0])
    index = jnp.arange(k.shape[0], dtype=jnp.int32)[None]
    low = jnp.min(jnp.where(meets, index, k.shape[0]), 1)
    high = jnp.max(jnp.where(meets, index + 1, 0), 1)
    return jnp.stack([low, high], 1).reshape(-1)

def head_rows(g):
    return slice(g * HEAD_SIZE, (g + 1) * HEAD_SIZE)

def fill_natural(dest, refs, which):
    size = refs[0].shape[2]
    for part, ref in enumerate(refs):
        dest[part * size : (part + 1) * size, :] = ref[which].T


def fill_tiles(dest, refs, which):
    pieces = refs[0].shape[2] // TILE
    for part, ref in enumerate(refs):
        for piece in range(pieces):
            dest[part * pieces + piece] = ref[which, :, piece * TILE : (piece + 1) * TILE]


def relative(place, r, size):
    return pl.ds(pl.multiple_of((place ^ r) * size, size), size)


def absorb(state, start, stop, base, q, cols, lab, klab, keys, vals):
    group = q.shape[0] // HEAD_SIZE

    def step(j, state):
        seen = klab[pl.ds(pl.multiple_of(j * TILE, TILE), TILE), :] == lab
        at = pl.ds(pl.multiple_of((j - base) * TILE, TILE), TILE)
        fresh = []
        for g in range(group):
            top, total, acc = state[3 * g : 3 * g + 3]
            s = dot_nn(keys[at, head_rows(g)], q[head_rows(g), cols])
            s = jnp.where(seen, s, -1e30)
            new = jnp.maximum(top, jnp.max(s, 0, keepdims=True))
            fade = jnp.exp(top - new)
            p = jnp.exp(s - new)
            total = total * fade + jnp.sum(p, 0, keepdims=True)
            acc = acc * fade + dot_nn(vals[j - base, head_rows(g), :], p.astype(BF16))
            fresh += [new, total, acc]
        return tuple(fresh)

    return lax.fori_loop(start, stop, step, tuple(state))


def near_body(span, q, kv, tk, tv, qlab, klab, tops, totals, mix, keys, vals):
    rows, size = q.shape
    pieces = size // TILE
    fill_natural(keys, (kv,), 0)
    fill_tiles(vals, (kv,), 1)
    for tile in range(pieces):
        cols = slice(tile * TILE, (tile + 1) * TILE)
        state = []
        for g in range(rows // HEAD_SIZE):
            part = q[head_rows(g), cols].astype(F32)
            top = jnp.sum(part * tk[head_rows(g), :], 0, keepdims=True)
            state += [
                top,
                jnp.ones_like(top),
                jnp.broadcast_to(tv[head_rows(g), :], (HEAD_SIZE, TILE)),
            ]
        start = jnp.maximum(span[2 * tile], pieces)
        stop = jnp.minimum(span[2 * tile + 1], 2 * pieces)
        state = absorb(state, start, stop, pieces, q, cols, qlab[:, cols], klab, keys, vals)
        for g in range(rows // HEAD_SIZE):
            tops[g : g + 1, cols], totals[g : g + 1, cols], mix[head_rows(g), cols] = state[
                3 * g : 3 * g + 3
            ]


def far_body(span, q, kv0, kv2, qlab, klab, w_out, tops, totals, mix,
             out, lse, away, own, low, keys0, keys2, vals0, vals2):
    rows, size = q.shape
    pieces = size // TILE
    for kv, keys, vals in ((kv0, keys0, vals0), (kv2, keys2, vals2)):
        fill_natural(keys, (kv,), 0)
        fill_tiles(vals, (kv,), 1)
    for tile in range(pieces):
        cols = slice(tile * TILE, (tile + 1) * TILE)
        lab = qlab[:, cols]
        state = []
        for g in range(rows // HEAD_SIZE):
            state += [tops[g : g + 1, cols], totals[g : g + 1, cols], mix[head_rows(g), cols]]
        stop = jnp.minimum(span[2 * tile + 1], pieces)
        state = absorb(state, span[2 * tile], stop, 0, q, cols, lab, klab, keys0, vals0)
        start = jnp.maximum(span[2 * tile], 2 * pieces)
        state = absorb(
            state, start, span[2 * tile + 1], 2 * pieces, q, cols, lab, klab, keys2, vals2
        )
        for g in range(rows // HEAD_SIZE):
            top, total, acc = state[3 * g : 3 * g + 3]
            out[head_rows(g), cols] = (acc / total).astype(BF16)
            lse[g : g + 1, cols] = top + jnp.log(total)
    place = span[2 * pieces]
    share = own.shape[0]

    def sent(r):
        return dot_tn(out[:, relative(place, r, share)], w_out[...])

    away[:share, :] = sent(1).astype(BF16)
    away[share:, :] = sent(3).astype(BF16)
    low[...] = sent(2).astype(BF16)
    own[...] = sent(0)


def backward_body(span, q, kv0, kv1, kv2, tk, tv, qlab, klab, w_out, out, lse,
                  g0, g1, g2, g3, dq, to_prev, kept, to_next, times,
                  og, keys, vals, tkeys, ak, av, dtk, dtv):
    rows, size = q.shape
    group = rows // HEAD_SIZE
    pieces = size // TILE
    share = g0.shape[0]
    for r, ref in enumerate((g0, g1, g2, g3)):
        og[:, relative(span[2 * pieces], r, share)] = dot_nt(w_out[...], ref[...]).astype(BF16)
    fill_natural(keys, (kv0, kv1, kv2), 0)
    fill_natural(vals, (kv0, kv1, kv2), 1)
    fill_tiles(tkeys, (kv0, kv1, kv2), 0)
    ak[...] = jnp.zeros_like(ak)
    av[...] = jnp.zeros_like(av)
    for tile in range(pieces):
        cols = slice(tile * TILE, (tile + 1) * TILE)
        lab = qlab[:, cols]
        state, norms, deltas = [], [], []
        for g in range(group):
            hr = head_rows(g)
            qf = q[hr, cols].astype(F32)
            gf = og[hr, cols].astype(F32)
            norm = lse[g : g + 1, cols]
            delta = jnp.sum(gf * out[hr, cols].astype(F32), 0, keepdims=True)
            pt = jnp.exp(jnp.sum(qf * tk[hr, :], 0, keepdims=True) - norm)
            st = pt * (jnp.sum(gf * tv[hr, :], 0, keepdims=True) - delta)
            gk = jnp.sum(qf * st, 1, keepdims=True)
            gv = jnp.sum(gf * pt, 1, keepdims=True)
            if tile == 0:
                dtk[hr, :] = gk
                dtv[hr, :] = gv
            else:
                dtk[hr, :] += gk
                dtv[hr, :] += gv
            state.append(tk[hr, :] * st)
            norms.append(norm)
            deltas.append(delta)

        def step(j, state):
            start = pl.multiple_of(j * TILE, TILE)
            seen = klab[pl.ds(start, TILE), :] == lab
            fresh = []
            for g in range(group):
                hr = head_rows(g)
                s = dot_nn(keys[pl.ds(start, TILE), hr], q[hr, cols])
                p = jnp.exp(jnp.where(seen, s, -1e30) - norms[g])
                m = dot_nn(vals[pl.ds(start, TILE), hr], og[hr, cols])
                ds = (p * (m - deltas[g])).astype(BF16)
                av[j, hr, :] += dot_nt(og[hr, cols], p.astype(BF16))
                ak[j, hr, :] += dot_nt(q[hr, cols], ds)
                fresh.append(state[g] + dot_nn(tkeys[j, hr, :], ds))
            return tuple(fresh)

        state = lax.fori_loop(span[2 * tile], span[2 * tile + 1], step, tuple(state))
        for g in range(group):
            dq[head_rows(g), cols] = state[g]
    for at, column in ((0, dtk), (1, dtv)):
        spread = jnp.broadcast_to(column[...], (rows, 2 * HEAD_SIZE))
        times[at : at + 1, :] = spread.T[:1, :]
    for part, dest in enumerate((to_prev, kept, to_next)):
        for piece in range(pieces):
            at = slice(piece * TILE, (piece + 1) * TILE)
            dest[0, :, at] = ak[part * pieces + piece].astype(dest.dtype)
            dest[1, :, at] = av[part * pieces + piece].astype(dest.dtype)


def attend_near(span, q, kv, tk, tv, qlab, klab):
    cols, size = q.shape
    wide = lambda *dims: jax.ShapeDtypeStruct(dims, F32)
    vmem = pl.BlockSpec(memory_space=pltpu.VMEM)
    return pl.pallas_call(
        near_body,
        in_specs=[pl.BlockSpec(memory_space=pltpu.SMEM)] + [vmem] * 6,
        out_specs=[vmem] * 3,
        out_shape=[wide(cols // HEAD_SIZE, size), wide(cols // HEAD_SIZE, size), wide(cols, size)],
        scratch_shapes=[pltpu.VMEM((size, cols), BF16), pltpu.VMEM((size // TILE, cols, TILE), BF16)],
        name="attend_near", cost_estimate=FREE,
    )(span, q, kv, tk, tv, qlab, klab)


def attend_far(span, q, behind, ahead, qlab, klab, w_out, state):
    cols, size = q.shape
    share, width = size // 4, w_out.shape[1]
    low = lambda *dims: jax.ShapeDtypeStruct(dims, BF16)
    wide = lambda *dims: jax.ShapeDtypeStruct(dims, F32)
    vmem = pl.BlockSpec(memory_space=pltpu.VMEM)
    keys = pltpu.VMEM((size, cols), BF16)
    vals = pltpu.VMEM((size // TILE, cols, TILE), BF16)
    return pl.pallas_call(
        far_body,
        in_specs=[pl.BlockSpec(memory_space=pltpu.SMEM)] + [vmem] * 9,
        out_specs=[vmem] * 5,
        out_shape=[low(cols, size), wide(cols // HEAD_SIZE, size), low(2 * share, width),
                   wide(share, width), low(share, width)],
        scratch_shapes=[keys, keys, vals, vals],
        name="attend_far", cost_estimate=FREE,
    )(span, q, behind, ahead, qlab, klab, w_out, *state)


def attend_back(span, q, kvs, tk, tv, qlab, klab, w_out, out, lse, grads):
    cols, size = q.shape
    tiles = 3 * size // TILE
    low = lambda *dims: jax.ShapeDtypeStruct(dims, BF16)
    wide = lambda *dims: jax.ShapeDtypeStruct(dims, F32)
    vmem = pl.BlockSpec(memory_space=pltpu.VMEM)
    return pl.pallas_call(
        backward_body,
        in_specs=[pl.BlockSpec(memory_space=pltpu.SMEM)] + [vmem] * 15,
        out_specs=[vmem] * 5,
        out_shape=[wide(cols, size), low(2, cols, size), wide(2, cols, size), low(2, cols, size),
                   wide(2, cols)],
        scratch_shapes=[pltpu.VMEM((cols, size), BF16), pltpu.VMEM((3 * size, cols), BF16),
                        pltpu.VMEM((3 * size, cols), BF16), pltpu.VMEM((tiles, cols, TILE), BF16),
                        pltpu.VMEM((tiles, cols, TILE), F32), pltpu.VMEM((tiles, cols, TILE), F32),
                        pltpu.VMEM((cols, 1), F32), pltpu.VMEM((cols, 1), F32)],
        name="attend_back", cost_estimate=FREE,
    )(span, q, *kvs, tk, tv, qlab, klab, w_out, out, lse, *grads)


def tail_body(place, dq, kept, ahead, behind, cosine, sine, wq, wk, wv, times,
              raw, away, own, low, flipped):
    part, size = dq.shape
    half = HEAD_SIZE // 2

    def returned(block, base, scale):
        for h in range(part // HEAD_SIZE):
            a = block[h * HEAD_SIZE : h * HEAD_SIZE + half, :]
            b = block[h * HEAD_SIZE + half : (h + 1) * HEAD_SIZE, :]
            at = base + h * HEAD_SIZE
            raw[at : at + half, :] = ((a * cosine[...] + b * sine[...]) * scale).astype(BF16)
            raw[at + half : at + HEAD_SIZE, :] = (
                (b * cosine[...] - a * sine[...]) * scale
            ).astype(BF16)

    def whole(index):
        return kept[index] + ahead[index].astype(F32) + behind[index].astype(F32)

    returned(dq[...], 0, 1.0 / math.sqrt(HEAD_SIZE))
    returned(whole(0), part, 1.0)
    raw[2 * part : 3 * part, :] = whole(1).astype(BF16)
    raw[3 * part :, :] = jnp.zeros((16, size), BF16)
    raw[3 * part : 3 * part + 2, :part] = times[...].astype(BF16)
    flipped[...] = raw[: 3 * part, :].T

    def sent(r):
        at = relative(place[0], r, part)
        return sum(
            dot_nt(flipped[:, i * part : (i + 1) * part], weight[at, :])
            for i, weight in enumerate((wq, wk, wv))
        )

    away[:size, :] = sent(1).astype(BF16)
    away[size:, :] = sent(3).astype(BF16)
    low[...] = sent(2).astype(BF16)
    own[...] = sent(0)


def tail(place, dq, kept, ahead, behind, tables, wq, wk, wv, times):
    part, size = dq.shape
    low = lambda *dims: jax.ShapeDtypeStruct(dims, BF16)
    vmem = pl.BlockSpec(memory_space=pltpu.VMEM)
    return pl.pallas_call(
        tail_body,
        in_specs=[pl.BlockSpec(memory_space=pltpu.SMEM)] + [vmem] * 10,
        out_specs=[vmem] * 4,
        out_shape=[low(3 * part + 16, size), low(2 * size, part), jax.ShapeDtypeStruct((size, part), F32),
                   low(size, part)],
        scratch_shapes=[pltpu.VMEM((size, 3 * part), BF16)],
        name="tail", cost_estimate=FREE,
    )(place, dq, kept, ahead, behind, *tables, wq, wk, wv, times)


def rotary_tables(frame_positions):
    half_dim = HEAD_SIZE // 2
    frequency = jnp.exp(jnp.arange(half_dim, dtype=jnp.float32) * (-math.log(10000.0) / half_dim))
    angles = frequency[:, None] * frame_positions[None, :]
    return (jnp.cos(angles), jnp.sin(angles))


def rotate(rows, tables, sign=1.0):
    count, size = rows.shape
    halves = rows.reshape(count // HEAD_SIZE, 2, HEAD_SIZE // 2, size)
    cosine, sine = tables[0][None], tables[1][None] * sign
    first = halves[:, 0] * cosine - halves[:, 1] * sine
    second = halves[:, 1] * cosine + halves[:, 0] * sine
    return jnp.stack([first, second], 1).reshape(count, size)


def product(left, right):
    return jnp.dot(left, right, preferred_element_type=jnp.float32)


def inner_rows(left, right):
    return jnp.einsum("nd,nf->df", left, right, preferred_element_type=jnp.float32)


def back_project(gradient, weight):
    return jnp.einsum("nf,df->nd", gradient, weight, preferred_element_type=jnp.float32)


def by_feature(left, right):
    return jnp.einsum("nd,df->fn", left, right, preferred_element_type=jnp.float32)


def columns(weight, start, size):
    return lax.dynamic_slice_in_dim(weight, start, size, 1)


def rows_of(weight, start, size):
    return lax.dynamic_slice_in_dim(weight, start, size, 0)


def normalize(value_rows):
    means = jnp.mean(value_rows, -1, keepdims=True)
    centred = value_rows - means
    inverse = lax.rsqrt(jnp.mean(centred * centred, -1, keepdims=True) + 1e-05)
    return centred * inverse, inverse


def norm_backward(gradient, scaled, inverse, norm_gain):
    scaled_grad = gradient * norm_gain
    plain = jnp.mean(scaled_grad, -1, keepdims=True)
    cross = jnp.mean(scaled_grad * scaled, -1, keepdims=True)
    return inverse * (scaled_grad - plain - scaled * cross)


FREE = pl.CostEstimate(flops=1, transcendentals=0, bytes_accessed=1)


def dot_nn(left, right):
    return lax.dot_general(left, right, (((1,), (0,)), ((), ())), preferred_element_type=F32)


def dot_nt(left, right):
    return lax.dot_general(left, right, (((1,), (1,)), ((), ())), preferred_element_type=F32)


def dot_tn(left, right):
    return lax.dot_general(left, right, (((0,), (0,)), ((), ())), preferred_element_type=F32)


def head_weights(query, key, lanes, which):
    mine = jnp.where(lanes == which, query, jnp.zeros_like(query))
    scores = dot_nt(mine, key) * (1.0 / math.sqrt(HEAD_SIZE))
    weights = jnp.exp(scores - jnp.max(scores, -1, keepdims=True))
    return weights / jnp.sum(weights, -1, keepdims=True)


def pair_cols(refs, p, rows):
    ref = refs[p * 2 * HEAD_SIZE // refs[0].shape[1]]
    start = p * 2 * HEAD_SIZE % refs[0].shape[1]
    return ref[rows, start : start + 2 * HEAD_SIZE]


def cross_forward_body(width_block, place, rows, own, got, far, norms, q0, q1, q2, q3,
                       c0, c1, c2, c3, o0, o1, o2, o3,
                       front, queries, first, second, normed_three,
                       flip_own, flip_away):
    width = rows.shape[1]
    kv = (c0, c1, c2, c3)
    context_rows = c0.shape[0] // 2
    key_rows, value_rows = slice(0, context_rows), slice(context_rows, 2 * context_rows)
    lanes = lax.broadcasted_iota(jnp.int32, (rows.shape[0], 2 * HEAD_SIZE), 1) // HEAD_SIZE
    residual = (
        rows[...].astype(F32) + own[...] + got[...].astype(F32) + far[...].astype(F32)
    )
    first[...] = residual
    scaled, _ = normalize(residual)
    low = (scaled * norms[2:3, :] + norms[3:4, :]).astype(BF16)
    front[:, :width] = low
    part = width // 4
    for b, ref in enumerate((q0, q1, q2, q3)):
        queries[:, b * part : (b + 1) * part] = dot_nn(low, ref[...]).astype(BF16)
    for p in range(width // (2 * HEAD_SIZE)):
        cols = slice(p * 2 * HEAD_SIZE, (p + 1) * 2 * HEAD_SIZE)
        q, k, v = queries[:, cols], pair_cols(kv, p, key_rows), pair_cols(kv, p, value_rows)
        mixed = [dot_nn(head_weights(q, k, lanes, g).astype(BF16), v) for g in (0, 1)]
        front[:, width + cols.start : width + cols.stop] = jnp.where(lanes == 0, mixed[0], mixed[1]).astype(BF16)
    for b, ref in enumerate((o0, o1, o2, o3)):
        residual = residual + dot_nn(front[:, width + b * part : width + (b + 1) * part], ref[...])
    second[...] = residual
    scaled, _ = normalize(residual)
    low = (scaled * norms[4:5, :] + norms[5:6, :]).astype(BF16)
    normed_three[...] = low
    deal_rows(low.T, width_block, place[0], flip_own, flip_away)


def cross_forward(devices, place, rows, own, got, far, norms, query_parts, kv_parts, out_parts):
    size, width = rows.shape
    low = jax.ShapeDtypeStruct(rows.shape, BF16)
    both = jax.ShapeDtypeStruct((size, 2 * width), BF16)
    wide = jax.ShapeDtypeStruct(rows.shape, F32)
    flip = jax.ShapeDtypeStruct((width // 2, size), BF16)
    vmem = pl.BlockSpec(memory_space=pltpu.VMEM)
    block = pl.BlockSpec((size, width), lambda i: (0, 0))
    return pl.pallas_call(
        functools.partial(cross_forward_body, width // devices),
        grid=(1,),
        in_specs=[pl.BlockSpec(memory_space=pltpu.SMEM)] + [block] * 4 + [vmem] * 13,
        out_shape=[both, low, wide, wide, low, flip, flip],
        cost_estimate=FREE, name="cross",
    )(place, rows, own, got, far, norms, *query_parts, *kv_parts, *out_parts)


def deal_rows(rows, size, column, own, away):
    for b in range(rows.shape[0] // (2 * size)):
        at = slice(b * size, (b + 1) * size)
        even = rows[2 * b * size : (2 * b + 1) * size, :]
        odd = rows[(2 * b + 1) * size : (2 * b + 2) * size, :]

        @pl.when(column == 0)
        def _():
            own[at, :] = even
            away[at, :] = odd

        @pl.when(column != 0)
        def _():
            own[at, :] = odd
            away[at, :] = even


def ffn_part(normed, grad, gate_w, up_w, down_w, hidden, hid_own, hid_away, gate_grad, lifted_grad,
             unit_block, column):
    gate = dot_nn(normed, gate_w[...])
    lifted = dot_nn(normed, up_w[...])
    back = dot_nt(grad, down_w[...]).astype(BF16).astype(F32)
    sig = jax.nn.sigmoid(gate)
    swish = gate * sig
    made = (swish * lifted).astype(BF16)
    hidden[...] = made
    deal_rows(made.T, unit_block, column, hid_own, hid_away)
    gg = (back * lifted * sig * (1.0 + gate * (1.0 - sig))).astype(BF16)
    lg = (back * swish).astype(BF16)
    gate_grad[...] = gg
    lifted_grad[...] = lg
    return dot_nt(gg, gate_w[...]) + dot_nt(lg, up_w[...])


def ffn_first_body(unit_block, place, n0, n1, n2, n3, g0, g1, g2, g3, gate_w, up_w, down_w,
                   hidden, hid_own, hid_away, gate_grad, lifted_grad, normed, grad, grad_pair,
                   total):
    share, part = n0.shape[0], g0.shape[2]
    for b, ref in enumerate((n0, n1, n2, n3)):
        normed[b * share : (b + 1) * share, :] = ref[...]
    for c, ref in enumerate((g0, g1, g2, g3)):
        for b in range(4):
            rows, cols = relative(place[1], b, share), relative(place[1], c, part)
            grad[b * share : (b + 1) * share, cols] = ref[0, rows, :]
            grad_pair[b * share : (b + 1) * share, cols] = ref[1, rows, :]
    total[...] = ffn_part(
        normed[...], grad[...], gate_w, up_w, down_w, hidden, hid_own, hid_away, gate_grad,
        lifted_grad, unit_block, place[0],
    )


def ffn_second_body(unit_block, place, normed, grad, total, gate_w, up_w, down_w,
                    hidden, hid_own, hid_away, gate_grad, lifted_grad, away, own, low):
    share = own.shape[0]
    found = total[...] + ffn_part(
        normed[...], grad[...], gate_w, up_w, down_w, hidden, hid_own, hid_away, gate_grad,
        lifted_grad, unit_block, place[0],
    )
    own[...] = found[:share, :]
    low[...] = found[2 * share : 3 * share, :].astype(BF16)
    away[:share, :] = found[share : 2 * share, :].astype(BF16)
    away[share:, :] = found[3 * share :, :].astype(BF16)


def ffn(devices, place, half, inputs, gate_w, up_w, down_w):
    share = inputs[0].shape[0] if half == 0 else inputs[0].shape[0] // 4
    width = inputs[0].shape[1]
    size, units = 4 * share, gate_w.shape[1]
    tile = units // 2
    low = lambda *dims: jax.ShapeDtypeStruct(dims, BF16)
    wide = lambda *dims: jax.ShapeDtypeStruct(dims, F32)
    vmem = pl.BlockSpec(memory_space=pltpu.VMEM)
    cols = pl.BlockSpec((width, tile), lambda i: (0, half))
    rows = pl.BlockSpec((tile, width), lambda i: (half, 0))
    made = [low(size, tile), low(tile // 2, size), low(tile // 2, size), low(size, tile),
            low(size, tile)]
    if half == 0:
        made += [low(size, width), low(size, width), low(size, width), wide(size, width)]
    else:
        made += [low(2 * share, width), wide(share, width), low(share, width)]
    return pl.pallas_call(
        functools.partial(ffn_second_body if half else ffn_first_body, units // devices),
        grid=(1,),
        in_specs=[pl.BlockSpec(memory_space=pltpu.SMEM)] + [vmem] * len(inputs)
        + [cols, cols, rows],
        out_specs=[vmem] * len(made),
        out_shape=made,
        cost_estimate=FREE, name="ffn",
    )(place, *inputs, gate_w, up_w, down_w)


def cross_backward_body(own, got, far, grad, first, second, norms, q0, q1, q2, q3,
                        c0, c1, c2, c3, o0, o1, o2, o3, queries,
                        back_rows, kv_grad, vectors, grad_one, crossed_grad):
    width = grad.shape[1]
    kv = (c0, c1, c2, c3)
    context_rows = c0.shape[0] // 2
    key_rows, value_rows = slice(0, context_rows), slice(context_rows, 2 * context_rows)
    part = width // 4
    lanes = lax.broadcasted_iota(jnp.int32, (grad.shape[0], 2 * HEAD_SIZE), 1) // HEAD_SIZE
    lane_k = lax.broadcasted_iota(jnp.int32, (context_rows, 2 * HEAD_SIZE), 1) // HEAD_SIZE
    scale = 1.0 / math.sqrt(HEAD_SIZE)
    arrived = own[...] + got[...].astype(F32) + far[...].astype(F32)
    scaled, inverse = normalize(second[...])
    vectors[0:1, :] = jnp.sum(arrived * scaled, 0, keepdims=True)
    vectors[1:2, :] = jnp.sum(arrived, 0, keepdims=True)
    two = grad[...].astype(F32) + norm_backward(arrived, scaled, inverse, norms[4:5, :])
    low = two.astype(BF16)
    back_rows[:, :width] = low
    for b, ref in enumerate((o0, o1, o2, o3)):
        crossed_grad[:, b * part : (b + 1) * part] = dot_nt(low, ref[...]).astype(BF16)
    for p in range(width // (2 * HEAD_SIZE)):
        cols = slice(p * 2 * HEAD_SIZE, (p + 1) * 2 * HEAD_SIZE)
        q, k, v = queries[:, cols], pair_cols(kv, p, key_rows), pair_cols(kv, p, value_rows)
        g_rows = crossed_grad[:, cols]
        found = []
        for g in (0, 1):
            probs = head_weights(q, k, lanes, g)
            change = dot_nt(jnp.where(lanes == g, g_rows, jnp.zeros_like(g_rows)), v)
            delta = jnp.sum(change * probs, -1, keepdims=True)
            ds = (probs * (change - delta)).astype(BF16)
            found.append((dot_nn(ds, k), dot_tn(ds, q), dot_tn(probs.astype(BF16), g_rows)))
        back_rows[:, width + cols.start : width + cols.stop] = (
            jnp.where(lanes == 0, found[0][0], found[1][0]) * scale
        ).astype(BF16)
        kv_grad[:context_rows, cols] = (
            jnp.where(lane_k == 0, found[0][1], found[1][1]) * scale
        ).astype(BF16)
        kv_grad[context_rows:, cols] = jnp.where(lane_k == 0, found[0][2], found[1][2]).astype(
            BF16
        )
    back = jnp.zeros(grad.shape, F32)
    for b, ref in enumerate((q0, q1, q2, q3)):
        back = back + dot_nt(back_rows[:, width + b * part : width + (b + 1) * part], ref[...])
    scaled, inverse = normalize(first[...])
    vectors[2:3, :] = jnp.sum(back * scaled, 0, keepdims=True)
    vectors[3:4, :] = jnp.sum(back, 0, keepdims=True)
    grad_one[...] = (two + norm_backward(back, scaled, inverse, norms[2:3, :])).astype(BF16)


def cross_backward(own, got, far, grad, first, second, norms, query_parts, kv_parts, out_parts,
                   queries):
    rows, width = own.shape
    low = lambda r: jax.ShapeDtypeStruct((r, width), BF16)
    block = pl.BlockSpec((rows, width), lambda i: (0, 0))
    return pl.pallas_call(
        cross_backward_body,
        grid=(1,),
        out_shape=[jax.ShapeDtypeStruct((rows, 2 * width), BF16), low(kv_parts[0].shape[0]),
                   jax.ShapeDtypeStruct((4, width), F32), low(rows)],
        in_specs=[block] * 6 + [pl.BlockSpec(memory_space=pltpu.VMEM)] * 14,
        scratch_shapes=[pltpu.VMEM((rows, width), BF16)],
        cost_estimate=FREE, name="cross_back",
    )(own, got, far, grad, first, second, norms, *query_parts, *kv_parts, *out_parts, queries)


def meet_rows_body(size, side, own_a, pair_a, own_b, pair_b, right, right_pair, keep, send):
    half = keep.shape[0] // 2
    for b, (own, pair) in enumerate(((own_a, pair_a), (own_b, pair_b))):
        made = (dot_nn(own[...], right[...]) + dot_nn(pair[...], right_pair[...])).astype(BF16)
        at = pl.ds(b * half, half)
        deal_rows(made, size, side[0], keep.at[at], send.at[at])


def meet_rows(size, side, lefts, rights):
    count, frames = lefts[0].shape
    width = rights[0].shape[1]
    tile = width // 3
    left = pl.BlockSpec((count, frames), lambda i: (0, 0))
    right = pl.BlockSpec((frames, tile), lambda i: (0, i))
    return pl.pallas_call(
        functools.partial(meet_rows_body, size),
        grid=(3,),
        in_specs=[pl.BlockSpec(memory_space=pltpu.SMEM)] + [left] * 4 + [right] * 2,
        out_specs=[pl.BlockSpec((count, tile), lambda i: (0, i))] * 2,
        out_shape=[jax.ShapeDtypeStruct((count, width), BF16)] * 2,
        name="meet_rows", cost_estimate=FREE,
    )(side, *lefts, *rights)


def meet_cols_body(size, side, p0, p1, p2, p3, *refs):
    own, pair = (jnp.concatenate([p[i] for p in (p0, p1, p2, p3)], 1) for i in (0, 1))
    *rights, keep, send = refs
    width = rights[0].shape[1]
    for at in range(len(rights) // 2):
        made = dot_nn(own, rights[2 * at][...]) + dot_nn(pair, rights[2 * at + 1][...])
        cols = pl.ds(at * width, width)
        deal_rows(made.astype(BF16), size, side[0], keep.at[:, cols], send.at[:, cols])


def meet_cols(size, side, near, rights):
    width = rights[0].shape[1] * (len(rights) // 2)
    half = jax.ShapeDtypeStruct((near[0].shape[1] // 2, width), BF16)
    vmem = pl.BlockSpec(memory_space=pltpu.VMEM)
    return pl.pallas_call(
        functools.partial(meet_cols_body, size),
        in_specs=[pl.BlockSpec(memory_space=pltpu.SMEM)] + [vmem] * (4 + len(rights)),
        out_shape=[half] * 2,
        name="meet_cols", cost_estimate=FREE,
    )(side, *near, *rights)


def down_body(first, second, down_w, away, own, low):
    share, units = own.shape[0], first.shape[1]

    def sent(r):
        at = slice(r * share, (r + 1) * share)
        return dot_nn(first[at, :], down_w[:units, :]) + dot_nn(second[at, :], down_w[units:, :])

    away[:share, :] = sent(1).astype(BF16)
    away[share:, :] = sent(3).astype(BF16)
    low[...] = sent(2).astype(BF16)
    own[...] = sent(0)


def down_parts(first, second, down_w):
    share, width = first.shape[0] // 4, down_w.shape[1]
    low = lambda *dims: jax.ShapeDtypeStruct(dims, BF16)
    return pl.pallas_call(
        down_body,
        out_shape=[low(2 * share, width), jax.ShapeDtypeStruct((share, width), F32),
                   low(share, width)],
        name="down", cost_estimate=FREE,
    )(first, second, down_w)


def bundle_body(devices, place, f02, f13, b02, b13, a0, a1, a2, a3, attended,
                context, kv, keep_a, send_a, keep_b, send_b):
    width = a0.shape[1]
    part, share = width // 4, a0.shape[0]

    def near(even, odd):
        return even[0], odd[0], even[1], odd[1]

    own = lambda rows: jnp.concatenate(
        [row[:, width + r * part : width + (r + 1) * part] for r, row in enumerate(rows)], 0
    )
    full = lambda rows: jnp.concatenate([row[:, :width] for row in rows], 0)
    fronts, backs = near(f02, f13), near(b02, b13)
    rows = width // devices
    small = part // devices
    half = width // 2

    def put(block, base, left, out):
        size = block.shape[0] // devices
        cols = slice(left, left + block.shape[1])
        low = block.astype(BF16)
        for d in range(0, devices, 2):
            at = slice(base, base + size)
            even, odd = low[d * size : (d + 1) * size, :], low[(d + 1) * size : (d + 2) * size, :]

            @pl.when(place[0] == 0)
            def _():
                out[0][d // 2, at, cols] = even
                out[1][d // 2, at, cols] = odd

            @pl.when(place[0] != 0)
            def _():
                out[0][d // 2, at, cols] = odd
                out[1][d // 2, at, cols] = even

    put(dot_tn(full(fronts), own(backs)), 0, 0, (keep_a, send_a))
    count = context.shape[0]
    put(dot_tn(context[...], kv[:count, :]), 0, part, (keep_a, send_a))
    put(dot_tn(context[...], kv[count:, :]), rows // 2, part, (keep_a, send_a))
    grads = dot_tn(own(fronts), full(backs))
    put(grads[:, :half], 0, 0, (keep_b, send_b))
    put(grads[:, half:], small, 0, (keep_b, send_b))
    grads = sum(
        dot_nn(attended[:, relative(place[1], r, share)], ref[...])
        for r, ref in enumerate((a0, a1, a2, a3))
    )
    put(grads[:, :half], 2 * small, 0, (keep_b, send_b))
    put(grads[:, half:], 3 * small, 0, (keep_b, send_b))


def bundle_grads(devices, place, fronts, backs, ones, attended, context, kv):
    width = ones[0].shape[1]
    vmem = pl.BlockSpec(memory_space=pltpu.VMEM)
    return pl.pallas_call(
        functools.partial(bundle_body, devices),
        in_specs=[pl.BlockSpec(memory_space=pltpu.SMEM)] + [vmem] * 11,
        out_specs=[vmem] * 4,
        out_shape=[jax.ShapeDtypeStruct((devices // 2, width // devices, width // 2), BF16)] * 4,
        name="bundle", cost_estimate=FREE,
    )(place, *fronts, *backs, *ones, attended, context, kv)


def front_body(width_block, place, x0, x1, x2, x3, g0, g1, g2, g3, cosine, sine, wq, wk, wv,
               time_row, context, ck, cv,
               queries, pair, rows, low, nrm_own, nrm_away, norms, means, inverses,
               time_scaled, time_low, time_keys, time_values, kv, wide):
    size, part = x0.shape
    for r, (x, g) in enumerate(((x0, g0), (x1, g1), (x2, g2), (x3, g3))):
        start = pl.multiple_of((place[0] ^ r) * part, 128)
        wide[:, pl.ds(start, part)] = x[...]
        norms[:, pl.ds(start, part)] = g[...]
    share = size // 4
    rows[...] = wide[pl.ds(pl.multiple_of(place[0] * share, share), share), :]
    values = wide[...].astype(F32)
    mean = jnp.mean(values, -1, keepdims=True)
    centred = values - mean
    inverse = lax.rsqrt(jnp.mean(centred * centred, -1, keepdims=True) + 1e-05)
    means[...] = mean
    inverses[...] = inverse
    normed = (centred * inverse * norms[0:1, :] + norms[1:2, :]).astype(BF16)
    low[...] = normed
    half = HEAD_SIZE // 2

    def turned(weight):
        return dot_nn(normed, weight[...]).T

    def rotated(block, dest, scale):
        for h in range(part // HEAD_SIZE):
            a = block[h * HEAD_SIZE : h * HEAD_SIZE + half, :]
            b = block[h * HEAD_SIZE + half : (h + 1) * HEAD_SIZE, :]
            dest[h * HEAD_SIZE : h * HEAD_SIZE + half, :] = (
                (a * cosine[...] - b * sine[...]) * scale
            ).astype(BF16)
            dest[h * HEAD_SIZE + half : (h + 1) * HEAD_SIZE, :] = (
                (b * cosine[...] + a * sine[...]) * scale
            ).astype(BF16)

    scaled, _ = normalize(jnp.broadcast_to(time_row[...].astype(F32), (8, 4 * part)))
    time_scaled[...] = scaled[:1, :]
    made = (scaled * norms[0:1, :] + norms[1:2, :]).astype(BF16)
    time_low[...] = made[:1, :].astype(F32)
    time_keys[...] = dot_nn(made, wk[...]).astype(BF16).astype(F32).T[:, :1]
    time_values[...] = dot_nn(made, wv[...]).astype(BF16).astype(F32).T[:, :1]
    count = context.shape[0]
    kv[:count, :] = dot_nn(context[...], ck[...]).astype(BF16)
    kv[count:, :] = dot_nn(context[...], cv[...]).astype(BF16)
    rotated(turned(wk), pair.at[0], 1.0)
    pair[1] = turned(wv).astype(BF16)
    rotated(turned(wq), queries, 1.0 / math.sqrt(HEAD_SIZE))
    deal_rows(normed.T, width_block, place[1], nrm_own, nrm_away)


def front(devices, place, parts, norm_parts, tables, wq, wk, wv, time_row, context, ck, cv):
    size, part = parts[0].shape
    width = 4 * part
    low = lambda *s: jax.ShapeDtypeStruct(s, BF16)
    wide = lambda *s: jax.ShapeDtypeStruct(s, F32)
    vmem = pl.BlockSpec(memory_space=pltpu.VMEM)
    return pl.pallas_call(
        functools.partial(front_body, width // devices),
        in_specs=[pl.BlockSpec(memory_space=pltpu.SMEM)] + [vmem] * 17,
        out_specs=[vmem] * 14,
        out_shape=[low(part, size), low(2, part, size), low(size // 4, width), low(size, width),
                   low(width // 2, size), low(width // 2, size), wide(6, width),
                   wide(size, 1), wide(size, 1), wide(1, width), wide(1, width), wide(part, 1),
                   wide(part, 1), low(2 * context.shape[0], part)],
        scratch_shapes=[pltpu.VMEM((size, width), BF16)],
        cost_estimate=FREE, name="front",
    )(place, *parts, *norm_parts, *tables, wq, wk, wv, time_row, context, ck, cv)


def per_device(
    frames,
    segment,
    time_token,
    context,
    gain_attn,
    bias_attn,
    gain_cross,
    bias_cross,
    gain_ffn,
    bias_ffn,
    w_query,
    w_key,
    w_value,
    w_out,
    c_query,
    c_key,
    c_value,
    c_out,
    w_gate,
    w_up,
    w_down,
    out_grad,
):
    local_rows = frames.shape[0]
    local_width = frames.shape[1]
    model_width = w_query.shape[0]
    head_cols = w_query.shape[1]
    heads = head_cols // HEAD_SIZE
    number_of_frames = lax.axis_size("seq") * local_rows
    row_length = min(max(ROW_MIN, 64 * lax.axis_size("seq")), number_of_frames)
    first_frame = lax.axis_index("seq") * local_rows
    own_start = lax.axis_index("tensor") * local_width

    def own_cols(value):
        return lax.dynamic_slice_in_dim(value, own_start, local_width, value.ndim - 1)

    place = lax.axis_index("tensor")
    share = local_rows // 4

    def row_block(value, index):
        return rows_of(value, index * share, share)

    column = lax.axis_index("seq") % 2
    frame_parts_near = gather_near(frames)
    norm_parts = gather_near(
        jnp.stack([gain_attn, bias_attn, gain_cross, bias_cross, gain_ffn, bias_ffn])
    )
    clip_starts, frame_positions = frame_clip_labels(segment, row_length)
    own_labels = lax.dynamic_slice_in_dim(clip_starts, first_frame, local_rows)
    own_positions = lax.dynamic_slice_in_dim(frame_positions, first_frame, local_rows)
    blanks = jnp.full((local_rows,), -1, jnp.int32)
    key_labels = lax.dynamic_slice_in_dim(
        jnp.concatenate([blanks, clip_starts, blanks]), first_frame, 3 * local_rows
    )
    spans = jnp.concatenate(
        [tile_ranges(own_labels, key_labels), place.astype(jnp.int32).reshape(1)]
    )
    places = jnp.stack([column, place]).astype(jnp.int32)
    label_row, label_column = own_labels[None, :], key_labels[:, None]
    row_index = first_frame // row_length
    time_row = lax.dynamic_slice_in_dim(time_token, row_index, 1, 0)
    row_context = lax.dynamic_slice_in_dim(context, row_index, 1, 0)[0]
    context_rows = row_context.shape[0]
    tables = rotary_tables(own_positions)
    score_scale = 1.0 / math.sqrt(HEAD_SIZE)
    all_heads = model_width // HEAD_SIZE

    (
        queries, both, frame_rows, frame_normed, one_own_half, one_away_half, norms, means_one,
        inverse_one, scaled_time, time_normed, time_keys, time_values, context_kv,
    ) = front(
        lax.axis_size("seq"), jnp.flip(places), frame_parts_near, norm_parts, tables, w_query,
        w_key, w_value, time_row, row_context, c_key, c_value,
    )
    both, out_pair = meeting(both, swap(after(out_grad, frame_parts_near[2]), "seq", 1))
    grad_both = jnp.stack([out_grad, out_pair])
    behind, ahead = shift(both, "seq", 1), shift(both, "seq", -1)
    query_late, out_late = after((c_query, c_out), (frame_parts_near[2], norm_parts[2]))
    query_far, out_far = swap(query_late, "tensor", 2), swap(out_late, "tensor", 2)
    state = attend_near(spans, queries, both, time_keys, time_values, label_row, label_column)
    behind, ahead, query_far, out_far, *state = meeting(
        behind, ahead, query_far, out_far, *state
    )
    query_own, out_own, context_late = after((c_query, c_out, context_kv), behind)
    weights_near = [
        swap(value, "tensor", 1) for value in (query_own, query_far, out_own, out_far)
    ]
    kv_far = swap(context_late, "tensor", 2)
    attended, log_totals, one_away, one_own, one_low = attend_far(
        spans, queries, behind, ahead, label_row, label_column, w_out, state
    )
    one_away, one_low, kv_far, *weights_near = meeting(one_away, one_low, kv_far, *weights_near)
    kv_both = jnp.concatenate([context_kv, kv_far], 0)
    kv_other = swap(kv_both, "tensor", 1)
    kv_rows = context_kv.shape[0]
    kv_parts = (context_kv, kv_other[:kv_rows], kv_far, kv_other[kv_rows:])
    query_parts = (c_query, weights_near[0], query_far, weights_near[1])
    out_parts = (c_out, weights_near[2], out_far, weights_near[3])
    one_got, _, one_far = scatter_near(one_away, one_low)
    (
        front_rows, cross_queries, residual_one, residual_two, normed_share, flip_own, flip_away,
    ) = cross_forward(
        lax.axis_size("seq"), places, frame_rows, one_own, one_got, one_far, norms,
        query_parts, kv_parts, out_parts,
    )
    grad_far = swap(after(grad_both, one_far), "tensor", 2)
    normed_share, normed_got, grad_far = meeting(
        normed_share, swap(after(one_away_half, one_low), "seq", 1), grad_far
    )
    grad_late, grad_far_late = after((grad_both, grad_far), normed_share)
    grad_mate, grad_far_mate = swap(grad_late, "tensor", 1), swap(grad_far_late, "tensor", 1)
    grad_parts = (grad_both, grad_mate, grad_far, grad_far_mate)
    three_parts = gather_near(normed_share)
    flip_got = swap(after(flip_away, normed_share), "seq", 1)
    front_far = swap(after(front_rows, three_parts[3]), "tensor", 2)
    devices = lax.axis_size("seq")
    (
        hidden_a, hidden_own_a, hidden_away_a, gate_a, lifted_a, normed_three, grad_near, grad_pair,
        ffn_total,
    ) = ffn(devices, places, 0, (*three_parts, *grad_parts), w_gate, w_up, w_down)
    ffn_total, flip_got = meeting(ffn_total, flip_got)
    flip_both = jnp.stack([flip_own, flip_got])
    flip_far = swap(flip_both, "tensor", 2)
    hidden_got_a, gate_got_a = swap(hidden_away_a, "seq", 1), swap(gate_a, "seq", 1)
    hidden_b, hidden_own_b, hidden_away_b, gate_b, lifted_b, three_away, three_own, three_low = ffn(
        devices, places, 1, (normed_three, grad_near, ffn_total), w_gate, w_up, w_down
    )
    three_away, three_low, flip_far, front_far, hidden_got_a = meeting(
        three_away, three_low, flip_far, front_far, hidden_got_a
    )
    three_got, _, three_far = scatter_near(three_away, three_low)
    lifted_got_a = swap(after(lifted_a, three_low), "seq", 1)
    flip_late, flip_far_late, gate_late = after((flip_both, flip_far, gate_b), three_far)
    flip_mate, flip_far_mate = swap(flip_late, "tensor", 1), swap(flip_far_late, "tensor", 1)
    gate_got_b = swap(gate_late, "seq", 1)
    front_both = jnp.stack([front_rows, front_far])
    back_rows, kv_grad, norm_vectors, grad_one = cross_backward(
        three_own, three_got, three_far, grad_near, residual_one, residual_two, norms,
        query_parts, kv_parts, out_parts, cross_queries,
    )
    grad_one, gate_got_a, lifted_got_a, flip_mate, flip_far_mate = meeting(
        grad_one, gate_got_a, lifted_got_a, flip_mate, flip_far_mate
    )
    hidden_got_b = swap(after(hidden_away_b, three_far), "seq", 1)
    count = lax.axis_size("seq")
    level_side = ((lax.axis_index("seq") >> 1) % 2).astype(jnp.int32).reshape(1)
    rows = model_width // count

    def traded(dealt):
        keep, send = [value.reshape(count // 4, rows, -1) for value in dealt]
        return keep, swap(send, "seq", 2)

    down_keep, down_got = traded(
        meet_rows(
            rows, level_side, (hidden_own_a, hidden_got_a, hidden_own_b, hidden_got_b),
            (grad_near, grad_pair),
        )
    )
    context_parts = quarters(kv_grad, 1)
    context_got = swap(jnp.concatenate([context_parts[1], context_parts[3]], 0), "tensor", 1)
    one_far_rows, down_keep = meeting(swap(grad_one, "tensor", 2), down_keep)
    one_parts = (
        grad_one, swap(grad_one, "tensor", 1), one_far_rows, swap(one_far_rows, "tensor", 1)
    )
    *one_parts, front_other, context_got = meeting(
        *one_parts, swap(after(front_both, grad_one), "tensor", 1), context_got
    )
    context_low = (
        context_parts[2].astype(F32) + context_got[context_parts[2].shape[0] :].astype(F32)
    ).astype(BF16)
    context_far = swap(context_low, "tensor", 2)
    back_far = swap(after(back_rows, one_parts[3]), "tensor", 2)
    lifted_got_b = swap(after(lifted_b, grad_one), "seq", 1)
    query_grad, to_prev, kept, to_next, time_grads = attend_back(
        spans, queries, (behind, both, ahead), time_keys, time_values, label_row, label_column,
        w_out, attended, log_totals, one_parts,
    )
    to_prev, to_next, back_far, gate_got_b, lifted_got_b, down_got, context_far = meeting(
        to_prev, to_next, back_far, gate_got_b, lifted_got_b, down_got, context_far
    )
    from_next, from_prev = shift(to_prev, "seq", -1), shift(to_next, "seq", 1)
    down_keep, down_got = halve(added(down_keep, down_got).astype(BF16), 2)
    flip_near = (flip_both, flip_mate, flip_far, flip_far_mate)
    first_keep, first_got = traded(
        meet_cols(
            rows, level_side, flip_near,
            after((gate_a, gate_got_a, lifted_a, lifted_got_a), to_prev),
        )
    )
    second_keep, second_got = traded(
        meet_cols(
            rows, level_side, flip_near,
            after((gate_b, gate_got_b, lifted_b, lifted_got_b), to_prev),
        )
    )
    back_both = jnp.stack([back_rows, back_far])
    back_other = swap(back_both, "tensor", 1)
    context_own = (
        context_parts[0].astype(F32)
        + context_got[: context_far.shape[0]].astype(F32)
        + context_far.astype(F32)
    )
    keep_a, send_a, keep_b, send_b = bundle_grads(
        count, places, (front_both, front_other), (back_both, back_other), one_parts, attended,
        row_context,
        context_own.astype(BF16),
    )
    from_next, from_prev, down_got, send_a, send_b = meeting(
        from_next, from_prev, down_got, send_a, send_b
    )
    got_a = swap(send_a, "seq", 1)
    raw, last_away, last_own, last_low = tail(
        places[1:], query_grad, kept, from_next, from_prev, tables, w_query, w_key, w_value,
        time_grads,
    )
    last_got = swap(last_away, "tensor", 1)
    raw_got = swap(raw, "seq", 1)
    last_sum = (
        last_low.astype(F32) + last_got[local_rows:].astype(F32)
    ).astype(BF16)
    last_sum, first_got, raw_got = meeting(last_sum, first_got, raw_got)
    first_keep, first_got = halve(added(first_keep, first_got).astype(BF16), 2)
    last_far, second_got = meeting(swap(last_sum, "tensor", 2), second_got)
    second_keep, second_got = halve(added(second_keep, second_got).astype(BF16), 2)
    frame_grad = last_own + last_got[:local_rows].astype(F32) + last_far.astype(F32)

    time_late, means_late, inverse_late, vectors_late = after(
        (time_grads, means_one, inverse_one, norm_vectors), last_far
    )
    time_grad = sum(
        jnp.einsum("of,df->od", time_late[i : i + 1].astype(BF16), w, preferred_element_type=F32)
        for i, w in enumerate((w_key, w_value))
    )
    own_scaled = (frames.astype(F32) - means_late) * inverse_late
    scaled_grad = frame_grad * gain_attn[None]
    sums = jnp.concatenate(
        [
            jnp.sum(scaled_grad, -1),
            jnp.sum(scaled_grad * own_scaled, -1),
            time_grad[0],
            vectors_late.reshape(-1),
        ]
    )[None]
    sums = sums + swap(sums, "tensor", 1)
    time_column = time_normed.T
    normed_pair = (one_own_half, normed_got)
    raw_pair = (raw[: 3 * head_cols], raw_got[: 3 * head_cols])
    time_got = raw_got[3 * head_cols : 3 * head_cols + 2, :head_cols].astype(F32)
    time_both = (time_grads + time_got).reshape(1, 2 * head_cols)
    own_time_rows = lax.dynamic_index_in_dim(
        time_column.reshape(count // 2, 2, -1), column, 1, False
    ).reshape(-1, 1)
    outer = own_time_rows * jnp.concatenate([jnp.zeros((1, head_cols), F32), time_both], 1)
    blocks = sum(
        jnp.einsum("dn,fn->df", r, c, preferred_element_type=F32)
        for r, c in zip(normed_pair, raw_pair)
    )
    blocks = (blocks + outer).astype(BF16).reshape(count // 2, rows, 3 * head_cols)
    heads_keep, heads_got = halve(blocks, 1)
    sums = sums + swap(sums, "tensor", 2)
    sums, heads_got, got_a = meeting(sums, heads_got, got_a)
    heads_next = added(heads_keep, heads_got).astype(BF16)
    heads_keep, heads_got = halve(heads_next, 2)
    left_keep, left_got = halve(added(keep_a, got_a).astype(BF16), 1)
    plain = sums[0, :local_rows, None] / model_width
    cross = sums[0, local_rows : 2 * local_rows, None] / model_width
    vectors = own_cols(sums[0, 2 * local_rows :].reshape(5, model_width))
    attend_full = ordered(*[after(one_parts, from_next)[i] for i in (0, 2, 1, 3)], 0)
    d_frames = own_cols(attend_full).astype(F32) + inverse_late * (
        scaled_grad - plain - own_scaled * cross
    )
    d_gain_attn = jnp.sum(frame_grad * own_scaled, 0) + vectors[0] * own_cols(scaled_time)[0]
    d_bias_attn = jnp.sum(frame_grad, 0) + vectors[0]


    grad_down = halve_end(down_keep, down_got, 3)
    got_b = swap(after(send_b, from_next), "seq", 1)
    down_away, down_own, down_low = down_parts(after(hidden_a, raw), hidden_b, w_down)
    down_away, down_low = after((down_away, down_low), heads_next)
    branch_got, _, branch_far = scatter_near(down_away, down_low)
    left_got, got_b, first_got = meeting(left_got, got_b, first_got)
    right_keep, right_got = halve(added(keep_b, got_b).astype(BF16), 1)
    right_got, second_got, branch_far = meeting(right_got, second_got, branch_far)
    last_next = added(right_keep, right_got)
    left_keep, left_got = halve(added(left_keep, left_got).astype(BF16), 2)
    right_keep, right_got = halve(last_next.astype(BF16), 2)
    heads_got, left_got, right_got = meeting(heads_got, left_got, right_got)
    block_rows = (
        residual_two + down_own + branch_got[:share].astype(F32) + branch_far.astype(F32)
    ).astype(BF16)
    block_cols = rows_to_cols(
        *[
            lax.dynamic_slice_in_dim(block_rows, (place ^ r) * local_width, local_width, 1)
            for r in range(4)
        ],
        last_next,
    )
    block_out = jnp.concatenate([row_block(block_cols, place ^ b) for b in range(4)], 0)
    first, second = halve_end(first_keep, first_got, 3), halve_end(second_keep, second_got, 3)
    units = first.shape[1] // 2
    grad_gate_w = jnp.concatenate([first[:, :units], second[:, :units]], 1)
    grad_up_w = jnp.concatenate([first[:, units:], second[:, units:]], 1)
    small = jnp.stack(
        [d_gain_attn, d_bias_attn, vectors[3], vectors[4], vectors[1], vectors[2]]
    ).reshape(6, devices, -1).transpose(1, 0, 2)
    small = small.reshape(count // 4, 2, 2, 6, -1).swapaxes(1, 2).reshape(count, 6, -1)
    small = after(small, last_next)
    bits = [1, 0] + list(range(2, count.bit_length() - 1))
    for bit in bits:
        small = added(*halve(small, bit))
    small = small[0]
    heads_sum = halve_end(heads_keep, heads_got, 3)
    left, right = halve_end(left_keep, left_got, 3), halve_end(right_keep, right_got, 3)
    part, rows = head_cols // count, model_width // count
    grad_c_query = left[:, :head_cols]
    grad_c_key, grad_c_value = left[: rows // 2, head_cols:], left[rows // 2 :, head_cols:]
    grad_c_out = jnp.concatenate([right[:part], right[part : 2 * part]], 1)
    grad_w_out = jnp.concatenate([right[2 * part : 3 * part], right[3 * part :]], 1)
    grad_w_query, grad_w_key, grad_w_value = (
        heads_sum[:, i * head_cols : (i + 1) * head_cols] for i in range(3)
    )
    return (
        block_out,
        d_frames,
        small[0],
        small[1],
        small[2],
        small[3],
        small[4],
        small[5],
        grad_w_query,
        grad_w_key,
        grad_w_value,
        grad_w_out,
        grad_c_query,
        grad_c_key,
        grad_c_value,
        grad_c_out,
        grad_gate_w,
        grad_up_w,
        grad_down,
    )


def solution(mesh):
    return jax.shard_map(
        per_device,
        mesh=mesh,
        in_specs=(
            P("seq", "tensor"),
            P(),
            P(),
            P(),
            P("tensor"),
            P("tensor"),
            P("tensor"),
            P("tensor"),
            P("tensor"),
            P("tensor"),
            P(None, "tensor"),
            P(None, "tensor"),
            P(None, "tensor"),
            P("tensor", None),
            P(None, "tensor"),
            P(None, "tensor"),
            P(None, "tensor"),
            P("tensor", None),
            P(None, "tensor"),
            P(None, "tensor"),
            P("tensor", None),
            P("seq", "tensor"),
        ),
        out_specs=(
            P("seq", "tensor"),
            P("seq", "tensor"),
            P(("tensor", "seq")),
            P(("tensor", "seq")),
            P(("tensor", "seq")),
            P(("tensor", "seq")),
            P(("tensor", "seq")),
            P(("tensor", "seq")),
            P("seq", "tensor"),
            P("seq", "tensor"),
            P("seq", "tensor"),
            P(("tensor", "seq"), None),
            P("seq", "tensor"),
            P("seq", "tensor"),
            P("seq", "tensor"),
            P(("tensor", "seq"), None),
            P("seq", "tensor"),
            P("seq", "tensor"),
            P(("tensor", "seq"), None),
        ),
        check_vma=False,
    )
```

```python
import functools
import math

import jax
import jax.numpy as jnp
from jax import lax
from jax.experimental import pallas as pl
from jax.experimental.pallas import tpu as pltpu
from jax.sharding import PartitionSpec as P

HEAD_SIZE = 64
ROW_MIN = 2048
TILE = 256
BF16 = jnp.bfloat16
F32 = jnp.float32


def meeting(*values):
    return lax.optimization_barrier(values)


def after(value, token):
    return lax.optimization_barrier((value, token))[0]


def swap(value, axis, by):
    return lax.ppermute(value, axis, [(i, i ^ by) for i in range(lax.axis_size(axis))])


def shift(value, axis, by):
    peers = lax.axis_size(axis)
    pairs = [(i, i + by) for i in range(peers) if 0 <= i + by < peers]
    return lax.ppermute(value, axis, pairs)


def tensor_place():
    place = lax.axis_index("tensor")
    return place // 2, place % 2


def ordered(own, far, mate, far_mate, axis):
    side, core = tensor_place()
    near = (jnp.where(core == 0, own, mate), jnp.where(core == 0, mate, own))
    away = (jnp.where(core == 0, far, far_mate), jnp.where(core == 0, far_mate, far))
    low = [jnp.where(side == 0, n, a) for n, a in zip(near, away)]
    high = [jnp.where(side == 0, a, n) for n, a in zip(near, away)]
    return jnp.concatenate(low + high, axis)


def gather_near(own):
    far = swap(own, "tensor", 2)
    return own, swap(own, "tensor", 1), far, swap(far, "tensor", 1)


def gather_staged(own, first, second):
    far = swap(after(own, first), "tensor", 2)
    far, late = after((far, own), second)
    return own, swap(late, "tensor", 1), far, swap(far, "tensor", 1)


def gather(own, axis):
    own, mate, far, far_mate = gather_near(own)
    return ordered(own, far, mate, far_mate, axis)


def scatter_near(away, low):
    got = swap(away, "tensor", 1)
    total = (low.astype(F32) + got[low.shape[0] :].astype(F32)).astype(BF16)
    return got, total, swap(total, "tensor", 2)


def rows_to_cols(own, mate, far, far_mate, later):
    width = own.shape[1]
    got = after(swap(jnp.concatenate([far, far_mate], 1), "tensor", 2), later)
    other = swap(jnp.concatenate([mate, got[:, width:]], 0), "tensor", 1)
    size = own.shape[0]
    return jnp.concatenate([own, other[:size], got[:, :width], other[size:]], 0)


def quarters(value, axis):
    return jnp.split(value, 4, axis)


def own_blocks(near):
    return jnp.concatenate([quarters(value, 1)[r] for r, value in enumerate(near)], 0)


def trade(value, start, done):
    return after(swap(after(value, start), "seq", 1), done)


def halve(blocks, bit):
    count, rows, cols = blocks.shape
    side = (lax.axis_index("seq") >> bit) % 2
    parts = blocks.reshape(count // 2, 2, rows, cols)
    send = lax.dynamic_index_in_dim(parts, 1 - side, 1, False)
    keep = lax.dynamic_index_in_dim(parts, side, 1, False)
    return keep, swap(send, "seq", 1 << bit)


def added(keep, got):
    return keep.astype(F32) + got.astype(F32)


def halve_all(blocks, bit):
    while blocks.shape[0] > 1:
        blocks = added(*halve(blocks.astype(BF16), bit))
        bit += 1
    return blocks[0].astype(F32)


def halve_end(keep, got, bit):
    return halve_all(added(keep, got), bit)


def frame_clip_labels(segment, row_length):
    frame_index = jnp.arange(segment.shape[0], dtype=jnp.int32)
    border = (frame_index % row_length == 0) | (segment != jnp.roll(segment, 1))
    clip_starts = lax.cummax(jnp.where(border, frame_index, 0), axis=0)
    return (clip_starts, (frame_index - clip_starts + 1).astype(jnp.float32))


def tile_ranges(q_labels, key_labels):
    q = q_labels.reshape(-1, TILE)
    k = key_labels.reshape(-1, TILE)
    meets = (k[None, :, 0] <= q[:, None, -1]) & (k[None, :, -1] >= q[:, None, 0])
    index = jnp.arange(k.shape[0], dtype=jnp.int32)[None]
    low = jnp.min(jnp.where(meets, index, k.shape[0]), 1)
    high = jnp.max(jnp.where(meets, index + 1, 0), 1)
    return jnp.stack([low, high], 1).reshape(-1)

def head_rows(g):
    return slice(g * HEAD_SIZE, (g + 1) * HEAD_SIZE)

def fill_natural(dest, refs, which):
    size = refs[0].shape[2]
    for part, ref in enumerate(refs):
        dest[part * size : (part + 1) * size, :] = ref[which].T


def fill_tiles(dest, refs, which):
    pieces = refs[0].shape[2] // TILE
    for part, ref in enumerate(refs):
        for piece in range(pieces):
            dest[part * pieces + piece] = ref[which, :, piece * TILE : (piece + 1) * TILE]


def relative(place, r, size):
    return pl.ds(pl.multiple_of((place ^ r) * size, size), size)


def absorb(state, start, stop, base, q, cols, lab, klab, keys, vals):
    group = q.shape[0] // HEAD_SIZE

    def step(j, state):
        seen = klab[pl.ds(pl.multiple_of(j * TILE, TILE), TILE), :] == lab
        at = pl.ds(pl.multiple_of((j - base) * TILE, TILE), TILE)
        fresh = []
        for g in range(group):
            top, total, acc = state[3 * g : 3 * g + 3]
            s = dot_nn(keys[at, head_rows(g)], q[head_rows(g), cols])
            s = jnp.where(seen, s, -1e30)
            new = jnp.maximum(top, jnp.max(s, 0, keepdims=True))
            fade = jnp.exp(top - new)
            p = jnp.exp(s - new)
            total = total * fade + jnp.sum(p, 0, keepdims=True)
            acc = acc * fade + dot_nn(vals[j - base, head_rows(g), :], p.astype(BF16))
            fresh += [new, total, acc]
        return tuple(fresh)

    return lax.fori_loop(start, stop, step, tuple(state))


def near_body(span, q, kv, tk, tv, qlab, klab, tops, totals, mix, keys, vals):
    rows, size = q.shape
    pieces = size // TILE
    fill_natural(keys, (kv,), 0)
    fill_tiles(vals, (kv,), 1)
    for tile in range(pieces):
        cols = slice(tile * TILE, (tile + 1) * TILE)
        state = []
        for g in range(rows // HEAD_SIZE):
            part = q[head_rows(g), cols].astype(F32)
            top = jnp.sum(part * tk[head_rows(g), :], 0, keepdims=True)
            state += [
                top,
                jnp.ones_like(top),
                jnp.broadcast_to(tv[head_rows(g), :], (HEAD_SIZE, TILE)),
            ]
        start = jnp.maximum(span[2 * tile], pieces)
        stop = jnp.minimum(span[2 * tile + 1], 2 * pieces)
        state = absorb(state, start, stop, pieces, q, cols, qlab[:, cols], klab, keys, vals)
        for g in range(rows // HEAD_SIZE):
            tops[g : g + 1, cols], totals[g : g + 1, cols], mix[head_rows(g), cols] = state[
                3 * g : 3 * g + 3
            ]


def far_body(span, q, kv0, kv2, qlab, klab, w_out, tops, totals, mix,
             out, lse, away, own, low, keys0, keys2, vals0, vals2):
    rows, size = q.shape
    pieces = size // TILE
    for kv, keys, vals in ((kv0, keys0, vals0), (kv2, keys2, vals2)):
        fill_natural(keys, (kv,), 0)
        fill_tiles(vals, (kv,), 1)
    for tile in range(pieces):
        cols = slice(tile * TILE, (tile + 1) * TILE)
        lab = qlab[:, cols]
        state = []
        for g in range(rows // HEAD_SIZE):
            state += [tops[g : g + 1, cols], totals[g : g + 1, cols], mix[head_rows(g), cols]]
        stop = jnp.minimum(span[2 * tile + 1], pieces)
        state = absorb(state, span[2 * tile], stop, 0, q, cols, lab, klab, keys0, vals0)
        start = jnp.maximum(span[2 * tile], 2 * pieces)
        state = absorb(
            state, start, span[2 * tile + 1], 2 * pieces, q, cols, lab, klab, keys2, vals2
        )
        for g in range(rows // HEAD_SIZE):
            top, total, acc = state[3 * g : 3 * g + 3]
            out[head_rows(g), cols] = (acc / total).astype(BF16)
            lse[g : g + 1, cols] = top + jnp.log(total)
    place = span[2 * pieces]
    share = own.shape[0]

    def sent(r):
        return dot_tn(out[:, relative(place, r, share)], w_out[...])

    away[:share, :] = sent(1).astype(BF16)
    away[share:, :] = sent(3).astype(BF16)
    low[...] = sent(2).astype(BF16)
    own[...] = sent(0)


def backward_body(span, q, kv0, kv1, kv2, tk, tv, qlab, klab, w_out, out, lse,
                  g0, g1, g2, g3, dq, to_prev, kept, to_next, times,
                  og, keys, vals, tkeys, ak, av, dtk, dtv):
    rows, size = q.shape
    group = rows // HEAD_SIZE
    pieces = size // TILE
    share = g0.shape[0]
    for r, ref in enumerate((g0, g1, g2, g3)):
        og[:, relative(span[2 * pieces], r, share)] = dot_nt(w_out[...], ref[...]).astype(BF16)
    fill_natural(keys, (kv0, kv1, kv2), 0)
    fill_natural(vals, (kv0, kv1, kv2), 1)
    fill_tiles(tkeys, (kv0, kv1, kv2), 0)
    ak[...] = jnp.zeros_like(ak)
    av[...] = jnp.zeros_like(av)
    for tile in range(pieces):
        cols = slice(tile * TILE, (tile + 1) * TILE)
        lab = qlab[:, cols]
        state, norms, deltas = [], [], []
        for g in range(group):
            hr = head_rows(g)
            qf = q[hr, cols].astype(F32)
            gf = og[hr, cols].astype(F32)
            norm = lse[g : g + 1, cols]
            delta = jnp.sum(gf * out[hr, cols].astype(F32), 0, keepdims=True)
            pt = jnp.exp(jnp.sum(qf * tk[hr, :], 0, keepdims=True) - norm)
            st = pt * (jnp.sum(gf * tv[hr, :], 0, keepdims=True) - delta)
            gk = jnp.sum(qf * st, 1, keepdims=True)
            gv = jnp.sum(gf * pt, 1, keepdims=True)
            if tile == 0:
                dtk[hr, :] = gk
                dtv[hr, :] = gv
            else:
                dtk[hr, :] += gk
                dtv[hr, :] += gv
            state.append(tk[hr, :] * st)
            norms.append(norm)
            deltas.append(delta)

        def step(j, state):
            start = pl.multiple_of(j * TILE, TILE)
            seen = klab[pl.ds(start, TILE), :] == lab
            fresh = []
            for g in range(group):
                hr = head_rows(g)
                s = dot_nn(keys[pl.ds(start, TILE), hr], q[hr, cols])
                p = jnp.exp(jnp.where(seen, s, -1e30) - norms[g])
                m = dot_nn(vals[pl.ds(start, TILE), hr], og[hr, cols])
                ds = (p * (m - deltas[g])).astype(BF16)
                av[j, hr, :] += dot_nt(og[hr, cols], p.astype(BF16))
                ak[j, hr, :] += dot_nt(q[hr, cols], ds)
                fresh.append(state[g] + dot_nn(tkeys[j, hr, :], ds))
            return tuple(fresh)

        state = lax.fori_loop(span[2 * tile], span[2 * tile + 1], step, tuple(state))
        for g in range(group):
            dq[head_rows(g), cols] = state[g]
    for at, column in ((0, dtk), (1, dtv)):
        spread = jnp.broadcast_to(column[...], (rows, 2 * HEAD_SIZE))
        times[at : at + 1, :] = spread.T[:1, :]
    for part, dest in enumerate((to_prev, kept, to_next)):
        for piece in range(pieces):
            at = slice(piece * TILE, (piece + 1) * TILE)
            dest[0, :, at] = ak[part * pieces + piece].astype(dest.dtype)
            dest[1, :, at] = av[part * pieces + piece].astype(dest.dtype)


def attend_near(span, q, kv, tk, tv, qlab, klab):
    cols, size = q.shape
    wide = lambda *dims: jax.ShapeDtypeStruct(dims, F32)
    vmem = pl.BlockSpec(memory_space=pltpu.VMEM)
    return pl.pallas_call(
        near_body,
        in_specs=[pl.BlockSpec(memory_space=pltpu.SMEM)] + [vmem] * 6,
        out_specs=[vmem] * 3,
        out_shape=[wide(cols // HEAD_SIZE, size), wide(cols // HEAD_SIZE, size), wide(cols, size)],
        scratch_shapes=[pltpu.VMEM((size, cols), BF16), pltpu.VMEM((size // TILE, cols, TILE), BF16)],
        name="attend_near", cost_estimate=FREE,
    )(span, q, kv, tk, tv, qlab, klab)


def attend_far(span, q, behind, ahead, qlab, klab, w_out, state):
    cols, size = q.shape
    share, width = size // 4, w_out.shape[1]
    low = lambda *dims: jax.ShapeDtypeStruct(dims, BF16)
    wide = lambda *dims: jax.ShapeDtypeStruct(dims, F32)
    vmem = pl.BlockSpec(memory_space=pltpu.VMEM)
    keys = pltpu.VMEM((size, cols), BF16)
    vals = pltpu.VMEM((size // TILE, cols, TILE), BF16)
    return pl.pallas_call(
        far_body,
        in_specs=[pl.BlockSpec(memory_space=pltpu.SMEM)] + [vmem] * 9,
        out_specs=[vmem] * 5,
        out_shape=[low(cols, size), wide(cols // HEAD_SIZE, size), low(2 * share, width),
                   wide(share, width), low(share, width)],
        scratch_shapes=[keys, keys, vals, vals],
        name="attend_far", cost_estimate=FREE,
    )(span, q, behind, ahead, qlab, klab, w_out, *state)


def attend_back(span, q, kvs, tk, tv, qlab, klab, w_out, out, lse, grads):
    cols, size = q.shape
    tiles = 3 * size // TILE
    low = lambda *dims: jax.ShapeDtypeStruct(dims, BF16)
    wide = lambda *dims: jax.ShapeDtypeStruct(dims, F32)
    vmem = pl.BlockSpec(memory_space=pltpu.VMEM)
    return pl.pallas_call(
        backward_body,
        in_specs=[pl.BlockSpec(memory_space=pltpu.SMEM)] + [vmem] * 15,
        out_specs=[vmem] * 5,
        out_shape=[wide(cols, size), low(2, cols, size), wide(2, cols, size), low(2, cols, size),
                   wide(2, cols)],
        scratch_shapes=[pltpu.VMEM((cols, size), BF16), pltpu.VMEM((3 * size, cols), BF16),
                        pltpu.VMEM((3 * size, cols), BF16), pltpu.VMEM((tiles, cols, TILE), BF16),
                        pltpu.VMEM((tiles, cols, TILE), F32), pltpu.VMEM((tiles, cols, TILE), F32),
                        pltpu.VMEM((cols, 1), F32), pltpu.VMEM((cols, 1), F32)],
        name="attend_back", cost_estimate=FREE,
    )(span, q, *kvs, tk, tv, qlab, klab, w_out, out, lse, *grads)


def tail_body(place, dq, kept, ahead, behind, cosine, sine, wq, wk, wv, times,
              raw, away, own, low, flipped):
    part, size = dq.shape
    half = HEAD_SIZE // 2

    def returned(block, base, scale):
        for h in range(part // HEAD_SIZE):
            a = block[h * HEAD_SIZE : h * HEAD_SIZE + half, :]
            b = block[h * HEAD_SIZE + half : (h + 1) * HEAD_SIZE, :]
            at = base + h * HEAD_SIZE
            raw[at : at + half, :] = ((a * cosine[...] + b * sine[...]) * scale).astype(BF16)
            raw[at + half : at + HEAD_SIZE, :] = (
                (b * cosine[...] - a * sine[...]) * scale
            ).astype(BF16)

    def whole(index):
        return kept[index] + ahead[index].astype(F32) + behind[index].astype(F32)

    returned(dq[...], 0, 1.0 / math.sqrt(HEAD_SIZE))
    returned(whole(0), part, 1.0)
    raw[2 * part : 3 * part, :] = whole(1).astype(BF16)
    raw[3 * part :, :] = jnp.zeros((16, size), BF16)
    raw[3 * part : 3 * part + 2, :part] = times[...].astype(BF16)
    flipped[...] = raw[: 3 * part, :].T

    def sent(r):
        at = relative(place[0], r, part)
        return sum(
            dot_nt(flipped[:, i * part : (i + 1) * part], weight[at, :])
            for i, weight in enumerate((wq, wk, wv))
        )

    away[:size, :] = sent(1).astype(BF16)
    away[size:, :] = sent(3).astype(BF16)
    low[...] = sent(2).astype(BF16)
    own[...] = sent(0)


def tail(place, dq, kept, ahead, behind, tables, wq, wk, wv, times):
    part, size = dq.shape
    low = lambda *dims: jax.ShapeDtypeStruct(dims, BF16)
    vmem = pl.BlockSpec(memory_space=pltpu.VMEM)
    return pl.pallas_call(
        tail_body,
        in_specs=[pl.BlockSpec(memory_space=pltpu.SMEM)] + [vmem] * 10,
        out_specs=[vmem] * 4,
        out_shape=[low(3 * part + 16, size), low(2 * size, part), jax.ShapeDtypeStruct((size, part), F32),
                   low(size, part)],
        scratch_shapes=[pltpu.VMEM((size, 3 * part), BF16)],
        name="tail", cost_estimate=FREE,
    )(place, dq, kept, ahead, behind, *tables, wq, wk, wv, times)


def rotary_tables(frame_positions):
    half_dim = HEAD_SIZE // 2
    frequency = jnp.exp(jnp.arange(half_dim, dtype=jnp.float32) * (-math.log(10000.0) / half_dim))
    angles = frequency[:, None] * frame_positions[None, :]
    return (jnp.cos(angles), jnp.sin(angles))


def rotate(rows, tables, sign=1.0):
    count, size = rows.shape
    halves = rows.reshape(count // HEAD_SIZE, 2, HEAD_SIZE // 2, size)
    cosine, sine = tables[0][None], tables[1][None] * sign
    first = halves[:, 0] * cosine - halves[:, 1] * sine
    second = halves[:, 1] * cosine + halves[:, 0] * sine
    return jnp.stack([first, second], 1).reshape(count, size)


def product(left, right):
    return jnp.dot(left, right, preferred_element_type=jnp.float32)


def inner_rows(left, right):
    return jnp.einsum("nd,nf->df", left, right, preferred_element_type=jnp.float32)


def back_project(gradient, weight):
    return jnp.einsum("nf,df->nd", gradient, weight, preferred_element_type=jnp.float32)


def by_feature(left, right):
    return jnp.einsum("nd,df->fn", left, right, preferred_element_type=jnp.float32)


def columns(weight, start, size):
    return lax.dynamic_slice_in_dim(weight, start, size, 1)


def rows_of(weight, start, size):
    return lax.dynamic_slice_in_dim(weight, start, size, 0)


def normalize(value_rows):
    means = jnp.mean(value_rows, -1, keepdims=True)
    centred = value_rows - means
    inverse = lax.rsqrt(jnp.mean(centred * centred, -1, keepdims=True) + 1e-05)
    return centred * inverse, inverse


def norm_backward(gradient, scaled, inverse, norm_gain):
    scaled_grad = gradient * norm_gain
    plain = jnp.mean(scaled_grad, -1, keepdims=True)
    cross = jnp.mean(scaled_grad * scaled, -1, keepdims=True)
    return inverse * (scaled_grad - plain - scaled * cross)


FREE = pl.CostEstimate(flops=1, transcendentals=0, bytes_accessed=1)


def dot_nn(left, right):
    return lax.dot_general(left, right, (((1,), (0,)), ((), ())), preferred_element_type=F32)


def dot_nt(left, right):
    return lax.dot_general(left, right, (((1,), (1,)), ((), ())), preferred_element_type=F32)


def dot_tn(left, right):
    return lax.dot_general(left, right, (((0,), (0,)), ((), ())), preferred_element_type=F32)


def head_weights(query, key, lanes, which):
    mine = jnp.where(lanes == which, query, jnp.zeros_like(query))
    scores = dot_nt(mine, key) * (1.0 / math.sqrt(HEAD_SIZE))
    weights = jnp.exp(scores - jnp.max(scores, -1, keepdims=True))
    return weights / jnp.sum(weights, -1, keepdims=True)


def pair_cols(refs, p, rows):
    ref = refs[p * 2 * HEAD_SIZE // refs[0].shape[1]]
    start = p * 2 * HEAD_SIZE % refs[0].shape[1]
    return ref[rows, start : start + 2 * HEAD_SIZE]


def cross_forward_body(width_block, place, rows, own, got, far, norms, q0, q1, q2, q3,
                       c0, c1, c2, c3, o0, o1, o2, o3,
                       front, queries, first, second, normed_three,
                       flip_own, flip_away):
    width = rows.shape[1]
    kv = (c0, c1, c2, c3)
    context_rows = c0.shape[0] // 2
    key_rows, value_rows = slice(0, context_rows), slice(context_rows, 2 * context_rows)
    lanes = lax.broadcasted_iota(jnp.int32, (rows.shape[0], 2 * HEAD_SIZE), 1) // HEAD_SIZE
    residual = (
        rows[...].astype(F32) + own[...] + got[...].astype(F32) + far[...].astype(F32)
    )
    first[...] = residual
    scaled, _ = normalize(residual)
    low = (scaled * norms[2:3, :] + norms[3:4, :]).astype(BF16)
    front[:, :width] = low
    part = width // 4
    for b, ref in enumerate((q0, q1, q2, q3)):
        queries[:, b * part : (b + 1) * part] = dot_nn(low, ref[...]).astype(BF16)
    for p in range(width // (2 * HEAD_SIZE)):
        cols = slice(p * 2 * HEAD_SIZE, (p + 1) * 2 * HEAD_SIZE)
        q, k, v = queries[:, cols], pair_cols(kv, p, key_rows), pair_cols(kv, p, value_rows)
        mixed = [dot_nn(head_weights(q, k, lanes, g).astype(BF16), v) for g in (0, 1)]
        front[:, width + cols.start : width + cols.stop] = jnp.where(lanes == 0, mixed[0], mixed[1]).astype(BF16)
    for b, ref in enumerate((o0, o1, o2, o3)):
        residual = residual + dot_nn(front[:, width + b * part : width + (b + 1) * part], ref[...])
    second[...] = residual
    scaled, _ = normalize(residual)
    low = (scaled * norms[4:5, :] + norms[5:6, :]).astype(BF16)
    normed_three[...] = low
    deal_rows(low.T, width_block, place[0], flip_own, flip_away)


def cross_forward(devices, place, rows, own, got, far, norms, query_parts, kv_parts, out_parts):
    size, width = rows.shape
    low = jax.ShapeDtypeStruct(rows.shape, BF16)
    both = jax.ShapeDtypeStruct((size, 2 * width), BF16)
    wide = jax.ShapeDtypeStruct(rows.shape, F32)
    flip = jax.ShapeDtypeStruct((width // 2, size), BF16)
    vmem = pl.BlockSpec(memory_space=pltpu.VMEM)
    block = pl.BlockSpec((size, width), lambda i: (0, 0))
    return pl.pallas_call(
        functools.partial(cross_forward_body, width // devices),
        grid=(1,),
        in_specs=[pl.BlockSpec(memory_space=pltpu.SMEM)] + [block] * 4 + [vmem] * 13,
        out_shape=[both, low, wide, wide, low, flip, flip],
        cost_estimate=FREE, name="cross",
    )(place, rows, own, got, far, norms, *query_parts, *kv_parts, *out_parts)


def deal_rows(rows, size, column, own, away):
    for b in range(rows.shape[0] // (2 * size)):
        at = slice(b * size, (b + 1) * size)
        even = rows[2 * b * size : (2 * b + 1) * size, :]
        odd = rows[(2 * b + 1) * size : (2 * b + 2) * size, :]

        @pl.when(column == 0)
        def _():
            own[at, :] = even
            away[at, :] = odd

        @pl.when(column != 0)
        def _():
            own[at, :] = odd
            away[at, :] = even


def ffn_part(normed, grad, gate_w, up_w, down_w, hidden, hid_own, hid_away, gate_grad, lifted_grad,
             unit_block, column):
    gate = dot_nn(normed, gate_w[...])
    lifted = dot_nn(normed, up_w[...])
    back = dot_nt(grad, down_w[...]).astype(BF16).astype(F32)
    sig = jax.nn.sigmoid(gate)
    swish = gate * sig
    made = (swish * lifted).astype(BF16)
    hidden[...] = made
    deal_rows(made.T, unit_block, column, hid_own, hid_away)
    gg = (back * lifted * sig * (1.0 + gate * (1.0 - sig))).astype(BF16)
    lg = (back * swish).astype(BF16)
    gate_grad[...] = gg
    lifted_grad[...] = lg
    return dot_nt(gg, gate_w[...]) + dot_nt(lg, up_w[...])


def ffn_first_body(unit_block, place, n0, n1, n2, n3, g0, g1, g2, g3, gate_w, up_w, down_w,
                   hidden, hid_own, hid_away, gate_grad, lifted_grad, normed, grad, grad_pair,
                   total):
    share, part = n0.shape[0], g0.shape[2]
    for b, ref in enumerate((n0, n1, n2, n3)):
        normed[b * share : (b + 1) * share, :] = ref[...]
    for c, ref in enumerate((g0, g1, g2, g3)):
        for b in range(4):
            rows, cols = relative(place[1], b, share), relative(place[1], c, part)
            grad[b * share : (b + 1) * share, cols] = ref[0, rows, :]
            grad_pair[b * share : (b + 1) * share, cols] = ref[1, rows, :]
    total[...] = ffn_part(
        normed[...], grad[...], gate_w, up_w, down_w, hidden, hid_own, hid_away, gate_grad,
        lifted_grad, unit_block, place[0],
    )


def ffn_second_body(unit_block, place, normed, grad, total, gate_w, up_w, down_w,
                    hidden, hid_own, hid_away, gate_grad, lifted_grad, away, own, low):
    share = own.shape[0]
    found = total[...] + ffn_part(
        normed[...], grad[...], gate_w, up_w, down_w, hidden, hid_own, hid_away, gate_grad,
        lifted_grad, unit_block, place[0],
    )
    own[...] = found[:share, :]
    low[...] = found[2 * share : 3 * share, :].astype(BF16)
    away[:share, :] = found[share : 2 * share, :].astype(BF16)
    away[share:, :] = found[3 * share :, :].astype(BF16)


def ffn(devices, place, half, inputs, gate_w, up_w, down_w):
    share = inputs[0].shape[0] if half == 0 else inputs[0].shape[0] // 4
    width = inputs[0].shape[1]
    size, units = 4 * share, gate_w.shape[1]
    tile = units // 2
    low = lambda *dims: jax.ShapeDtypeStruct(dims, BF16)
    wide = lambda *dims: jax.ShapeDtypeStruct(dims, F32)
    vmem = pl.BlockSpec(memory_space=pltpu.VMEM)
    cols = pl.BlockSpec((width, tile), lambda i: (0, half))
    rows = pl.BlockSpec((tile, width), lambda i: (half, 0))
    made = [low(size, tile), low(tile // 2, size), low(tile // 2, size), low(size, tile),
            low(size, tile)]
    if half == 0:
        made += [low(size, width), low(size, width), low(size, width), wide(size, width)]
    else:
        made += [low(2 * share, width), wide(share, width), low(share, width)]
    return pl.pallas_call(
        functools.partial(ffn_second_body if half else ffn_first_body, units // devices),
        grid=(1,),
        in_specs=[pl.BlockSpec(memory_space=pltpu.SMEM)] + [vmem] * len(inputs)
        + [cols, cols, rows],
        out_specs=[vmem] * len(made),
        out_shape=made,
        cost_estimate=FREE, name="ffn",
    )(place, *inputs, gate_w, up_w, down_w)


def cross_backward_body(own, got, far, grad, first, second, norms, q0, q1, q2, q3,
                        c0, c1, c2, c3, o0, o1, o2, o3, queries,
                        back_rows, kv_grad, vectors, grad_one, crossed_grad):
    width = grad.shape[1]
    kv = (c0, c1, c2, c3)
    context_rows = c0.shape[0] // 2
    key_rows, value_rows = slice(0, context_rows), slice(context_rows, 2 * context_rows)
    part = width // 4
    lanes = lax.broadcasted_iota(jnp.int32, (grad.shape[0], 2 * HEAD_SIZE), 1) // HEAD_SIZE
    lane_k = lax.broadcasted_iota(jnp.int32, (context_rows, 2 * HEAD_SIZE), 1) // HEAD_SIZE
    scale = 1.0 / math.sqrt(HEAD_SIZE)
    arrived = own[...] + got[...].astype(F32) + far[...].astype(F32)
    scaled, inverse = normalize(second[...])
    vectors[0:1, :] = jnp.sum(arrived * scaled, 0, keepdims=True)
    vectors[1:2, :] = jnp.sum(arrived, 0, keepdims=True)
    two = grad[...].astype(F32) + norm_backward(arrived, scaled, inverse, norms[4:5, :])
    low = two.astype(BF16)
    back_rows[:, :width] = low
    for b, ref in enumerate((o0, o1, o2, o3)):
        crossed_grad[:, b * part : (b + 1) * part] = dot_nt(low, ref[...]).astype(BF16)
    for p in range(width // (2 * HEAD_SIZE)):
        cols = slice(p * 2 * HEAD_SIZE, (p + 1) * 2 * HEAD_SIZE)
        q, k, v = queries[:, cols], pair_cols(kv, p, key_rows), pair_cols(kv, p, value_rows)
        g_rows = crossed_grad[:, cols]
        found = []
        for g in (0, 1):
            probs = head_weights(q, k, lanes, g)
            change = dot_nt(jnp.where(lanes == g, g_rows, jnp.zeros_like(g_rows)), v)
            delta = jnp.sum(change * probs, -1, keepdims=True)
            ds = (probs * (change - delta)).astype(BF16)
            found.append((dot_nn(ds, k), dot_tn(ds, q), dot_tn(probs.astype(BF16), g_rows)))
        back_rows[:, width + cols.start : width + cols.stop] = (
            jnp.where(lanes == 0, found[0][0], found[1][0]) * scale
        ).astype(BF16)
        kv_grad[:context_rows, cols] = (
            jnp.where(lane_k == 0, found[0][1], found[1][1]) * scale
        ).astype(BF16)
        kv_grad[context_rows:, cols] = jnp.where(lane_k == 0, found[0][2], found[1][2]).astype(
            BF16
        )
    back = jnp.zeros(grad.shape, F32)
    for b, ref in enumerate((q0, q1, q2, q3)):
        back = back + dot_nt(back_rows[:, width + b * part : width + (b + 1) * part], ref[...])
    scaled, inverse = normalize(first[...])
    vectors[2:3, :] = jnp.sum(back * scaled, 0, keepdims=True)
    vectors[3:4, :] = jnp.sum(back, 0, keepdims=True)
    grad_one[...] = (two + norm_backward(back, scaled, inverse, norms[2:3, :])).astype(BF16)


def cross_backward(own, got, far, grad, first, second, norms, query_parts, kv_parts, out_parts,
                   queries):
    rows, width = own.shape
    low = lambda r: jax.ShapeDtypeStruct((r, width), BF16)
    block = pl.BlockSpec((rows, width), lambda i: (0, 0))
    return pl.pallas_call(
        cross_backward_body,
        grid=(1,),
        out_shape=[jax.ShapeDtypeStruct((rows, 2 * width), BF16), low(kv_parts[0].shape[0]),
                   jax.ShapeDtypeStruct((4, width), F32), low(rows)],
        in_specs=[block] * 6 + [pl.BlockSpec(memory_space=pltpu.VMEM)] * 14,
        scratch_shapes=[pltpu.VMEM((rows, width), BF16)],
        cost_estimate=FREE, name="cross_back",
    )(own, got, far, grad, first, second, norms, *query_parts, *kv_parts, *out_parts, queries)


def meet_rows_body(size, side, own_a, pair_a, own_b, pair_b, right, right_pair, keep, send):
    half = keep.shape[0] // 2
    for b, (own, pair) in enumerate(((own_a, pair_a), (own_b, pair_b))):
        made = (dot_nn(own[...], right[...]) + dot_nn(pair[...], right_pair[...])).astype(BF16)
        at = pl.ds(b * half, half)
        deal_rows(made, size, side[0], keep.at[at], send.at[at])


def meet_rows(size, side, lefts, rights):
    count, frames = lefts[0].shape
    width = rights[0].shape[1]
    tile = width // 3
    left = pl.BlockSpec((count, frames), lambda i: (0, 0))
    right = pl.BlockSpec((frames, tile), lambda i: (0, i))
    return pl.pallas_call(
        functools.partial(meet_rows_body, size),
        grid=(3,),
        in_specs=[pl.BlockSpec(memory_space=pltpu.SMEM)] + [left] * 4 + [right] * 2,
        out_specs=[pl.BlockSpec((count, tile), lambda i: (0, i))] * 2,
        out_shape=[jax.ShapeDtypeStruct((count, width), BF16)] * 2,
        name="meet_rows", cost_estimate=FREE,
    )(side, *lefts, *rights)


def meet_cols_body(size, side, p0, p1, p2, p3, *refs):
    own, pair = (jnp.concatenate([p[i] for p in (p0, p1, p2, p3)], 1) for i in (0, 1))
    *rights, keep, send = refs
    width = rights[0].shape[1]
    for at in range(len(rights) // 2):
        made = dot_nn(own, rights[2 * at][...]) + dot_nn(pair, rights[2 * at + 1][...])
        cols = pl.ds(at * width, width)
        deal_rows(made.astype(BF16), size, side[0], keep.at[:, cols], send.at[:, cols])


def meet_cols(size, side, near, rights):
    width = rights[0].shape[1] * (len(rights) // 2)
    half = jax.ShapeDtypeStruct((near[0].shape[1] // 2, width), BF16)
    vmem = pl.BlockSpec(memory_space=pltpu.VMEM)
    return pl.pallas_call(
        functools.partial(meet_cols_body, size),
        in_specs=[pl.BlockSpec(memory_space=pltpu.SMEM)] + [vmem] * (4 + len(rights)),
        out_shape=[half] * 2,
        name="meet_cols", cost_estimate=FREE,
    )(side, *near, *rights)


def down_body(first, second, down_w, away, own, low):
    share, units = own.shape[0], first.shape[1]

    def sent(r):
        at = slice(r * share, (r + 1) * share)
        return dot_nn(first[at, :], down_w[:units, :]) + dot_nn(second[at, :], down_w[units:, :])

    away[:share, :] = sent(1).astype(BF16)
    away[share:, :] = sent(3).astype(BF16)
    low[...] = sent(2).astype(BF16)
    own[...] = sent(0)


def down_parts(first, second, down_w):
    share, width = first.shape[0] // 4, down_w.shape[1]
    low = lambda *dims: jax.ShapeDtypeStruct(dims, BF16)
    return pl.pallas_call(
        down_body,
        out_shape=[low(2 * share, width), jax.ShapeDtypeStruct((share, width), F32),
                   low(share, width)],
        name="down", cost_estimate=FREE,
    )(first, second, down_w)


def bundle_body(devices, place, f02, f13, b02, b13, a0, a1, a2, a3, attended,
                context, kv, keep_a, send_a, keep_b, send_b):
    width = a0.shape[1]
    part, share = width // 4, a0.shape[0]

    def near(even, odd):
        return even[0], odd[0], even[1], odd[1]

    own = lambda rows: jnp.concatenate(
        [row[:, width + r * part : width + (r + 1) * part] for r, row in enumerate(rows)], 0
    )
    full = lambda rows: jnp.concatenate([row[:, :width] for row in rows], 0)
    fronts, backs = near(f02, f13), near(b02, b13)
    rows = width // devices
    small = part // devices
    half = width // 2

    def put(block, base, left, out):
        size = block.shape[0] // devices
        cols = slice(left, left + block.shape[1])
        low = block.astype(BF16)
        for d in range(0, devices, 2):
            at = slice(base, base + size)
            even, odd = low[d * size : (d + 1) * size, :], low[(d + 1) * size : (d + 2) * size, :]

            @pl.when(place[0] == 0)
            def _():
                out[0][d // 2, at, cols] = even
                out[1][d // 2, at, cols] = odd

            @pl.when(place[0] != 0)
            def _():
                out[0][d // 2, at, cols] = odd
                out[1][d // 2, at, cols] = even

    put(dot_tn(full(fronts), own(backs)), 0, 0, (keep_a, send_a))
    count = context.shape[0]
    put(dot_tn(context[...], kv[:count, :]), 0, part, (keep_a, send_a))
    put(dot_tn(context[...], kv[count:, :]), rows // 2, part, (keep_a, send_a))
    grads = dot_tn(own(fronts), full(backs))
    put(grads[:, :half], 0, 0, (keep_b, send_b))
    put(grads[:, half:], small, 0, (keep_b, send_b))
    grads = sum(
        dot_nn(attended[:, relative(place[1], r, share)], ref[...])
        for r, ref in enumerate((a0, a1, a2, a3))
    )
    put(grads[:, :half], 2 * small, 0, (keep_b, send_b))
    put(grads[:, half:], 3 * small, 0, (keep_b, send_b))


def bundle_grads(devices, place, fronts, backs, ones, attended, context, kv):
    width = ones[0].shape[1]
    vmem = pl.BlockSpec(memory_space=pltpu.VMEM)
    return pl.pallas_call(
        functools.partial(bundle_body, devices),
        in_specs=[pl.BlockSpec(memory_space=pltpu.SMEM)] + [vmem] * 11,
        out_specs=[vmem] * 4,
        out_shape=[jax.ShapeDtypeStruct((devices // 2, width // devices, width // 2), BF16)] * 4,
        name="bundle", cost_estimate=FREE,
    )(place, *fronts, *backs, *ones, attended, context, kv)


def front_body(width_block, place, x0, x1, x2, x3, g0, g1, g2, g3, cosine, sine, wq, wk, wv,
               time_row, context, ck, cv,
               queries, pair, rows, low, nrm_own, nrm_away, norms, means, inverses,
               time_scaled, time_low, time_keys, time_values, kv, wide):
    size, part = x0.shape
    for r, (x, g) in enumerate(((x0, g0), (x1, g1), (x2, g2), (x3, g3))):
        start = pl.multiple_of((place[0] ^ r) * part, 128)
        wide[:, pl.ds(start, part)] = x[...]
        norms[:, pl.ds(start, part)] = g[...]
    share = size // 4
    rows[...] = wide[pl.ds(pl.multiple_of(place[0] * share, share), share), :]
    values = wide[...].astype(F32)
    mean = jnp.mean(values, -1, keepdims=True)
    centred = values - mean
    inverse = lax.rsqrt(jnp.mean(centred * centred, -1, keepdims=True) + 1e-05)
    means[...] = mean
    inverses[...] = inverse
    normed = (centred * inverse * norms[0:1, :] + norms[1:2, :]).astype(BF16)
    low[...] = normed
    half = HEAD_SIZE // 2

    def turned(weight):
        return dot_nn(normed, weight[...]).T

    def rotated(block, dest, scale):
        for h in range(part // HEAD_SIZE):
            a = block[h * HEAD_SIZE : h * HEAD_SIZE + half, :]
            b = block[h * HEAD_SIZE + half : (h + 1) * HEAD_SIZE, :]
            dest[h * HEAD_SIZE : h * HEAD_SIZE + half, :] = (
                (a * cosine[...] - b * sine[...]) * scale
            ).astype(BF16)
            dest[h * HEAD_SIZE + half : (h + 1) * HEAD_SIZE, :] = (
                (b * cosine[...] + a * sine[...]) * scale
            ).astype(BF16)

    scaled, _ = normalize(jnp.broadcast_to(time_row[...].astype(F32), (8, 4 * part)))
    time_scaled[...] = scaled[:1, :]
    made = (scaled * norms[0:1, :] + norms[1:2, :]).astype(BF16)
    time_low[...] = made[:1, :].astype(F32)
    time_keys[...] = dot_nn(made, wk[...]).astype(BF16).astype(F32).T[:, :1]
    time_values[...] = dot_nn(made, wv[...]).astype(BF16).astype(F32).T[:, :1]
    count = context.shape[0]
    kv[:count, :] = dot_nn(context[...], ck[...]).astype(BF16)
    kv[count:, :] = dot_nn(context[...], cv[...]).astype(BF16)
    rotated(turned(wk), pair.at[0], 1.0)
    pair[1] = turned(wv).astype(BF16)
    rotated(turned(wq), queries, 1.0 / math.sqrt(HEAD_SIZE))
    deal_rows(normed.T, width_block, place[1], nrm_own, nrm_away)


def front(devices, place, parts, norm_parts, tables, wq, wk, wv, time_row, context, ck, cv):
    size, part = parts[0].shape
    width = 4 * part
    low = lambda *s: jax.ShapeDtypeStruct(s, BF16)
    wide = lambda *s: jax.ShapeDtypeStruct(s, F32)
    vmem = pl.BlockSpec(memory_space=pltpu.VMEM)
    return pl.pallas_call(
        functools.partial(front_body, width // devices),
        in_specs=[pl.BlockSpec(memory_space=pltpu.SMEM)] + [vmem] * 17,
        out_specs=[vmem] * 14,
        out_shape=[low(part, size), low(2, part, size), low(size // 4, width), low(size, width),
                   low(width // 2, size), low(width // 2, size), wide(6, width),
                   wide(size, 1), wide(size, 1), wide(1, width), wide(1, width), wide(part, 1),
                   wide(part, 1), low(2 * context.shape[0], part)],
        scratch_shapes=[pltpu.VMEM((size, width), BF16)],
        cost_estimate=FREE, name="front",
    )(place, *parts, *norm_parts, *tables, wq, wk, wv, time_row, context, ck, cv)


def per_device(
    frames,
    segment,
    time_token,
    context,
    gain_attn,
    bias_attn,
    gain_cross,
    bias_cross,
    gain_ffn,
    bias_ffn,
    w_query,
    w_key,
    w_value,
    w_out,
    c_query,
    c_key,
    c_value,
    c_out,
    w_gate,
    w_up,
    w_down,
    out_grad,
):
    local_rows = frames.shape[0]
    local_width = frames.shape[1]
    model_width = w_query.shape[0]
    head_cols = w_query.shape[1]
    heads = head_cols // HEAD_SIZE
    number_of_frames = lax.axis_size("seq") * local_rows
    row_length = min(max(ROW_MIN, 64 * lax.axis_size("seq")), number_of_frames)
    first_frame = lax.axis_index("seq") * local_rows
    own_start = lax.axis_index("tensor") * local_width

    def own_cols(value):
        return lax.dynamic_slice_in_dim(value, own_start, local_width, value.ndim - 1)

    place = lax.axis_index("tensor")
    share = local_rows // 4

    def row_block(value, index):
        return rows_of(value, index * share, share)

    column = lax.axis_index("seq") % 2
    frame_parts_near = gather_near(frames)
    norm_parts = gather_near(
        jnp.stack([gain_attn, bias_attn, gain_cross, bias_cross, gain_ffn, bias_ffn])
    )
    clip_starts, frame_positions = frame_clip_labels(segment, row_length)
    own_labels = lax.dynamic_slice_in_dim(clip_starts, first_frame, local_rows)
    own_positions = lax.dynamic_slice_in_dim(frame_positions, first_frame, local_rows)
    blanks = jnp.full((local_rows,), -1, jnp.int32)
    key_labels = lax.dynamic_slice_in_dim(
        jnp.concatenate([blanks, clip_starts, blanks]), first_frame, 3 * local_rows
    )
    spans = jnp.concatenate(
        [tile_ranges(own_labels, key_labels), place.astype(jnp.int32).reshape(1)]
    )
    places = jnp.stack([column, place]).astype(jnp.int32)
    label_row, label_column = own_labels[None, :], key_labels[:, None]
    row_index = first_frame // row_length
    time_row = lax.dynamic_slice_in_dim(time_token, row_index, 1, 0)
    row_context = lax.dynamic_slice_in_dim(context, row_index, 1, 0)[0]
    context_rows = row_context.shape[0]
    tables = rotary_tables(own_positions)
    score_scale = 1.0 / math.sqrt(HEAD_SIZE)
    all_heads = model_width // HEAD_SIZE

    (
        queries, both, frame_rows, frame_normed, one_own_half, one_away_half, norms, means_one,
        inverse_one, scaled_time, time_normed, time_keys, time_values, context_kv,
    ) = front(
        lax.axis_size("seq"), jnp.flip(places), frame_parts_near, norm_parts, tables, w_query,
        w_key, w_value, time_row, row_context, c_key, c_value,
    )
    both, out_pair = meeting(both, swap(after(out_grad, frame_parts_near[2]), "seq", 1))
    grad_both = jnp.stack([out_grad, out_pair])
    behind, ahead = shift(both, "seq", 1), shift(both, "seq", -1)
    query_late, out_late = after((c_query, c_out), (frame_parts_near[2], norm_parts[2]))
    query_far, out_far = swap(query_late, "tensor", 2), swap(out_late, "tensor", 2)
    state = attend_near(spans, queries, both, time_keys, time_values, label_row, label_column)
    behind, ahead, query_far, out_far, *state = meeting(
        behind, ahead, query_far, out_far, *state
    )
    query_own, out_own, context_late = after((c_query, c_out, context_kv), behind)
    weights_near = [
        swap(value, "tensor", 1) for value in (query_own, query_far, out_own, out_far)
    ]
    kv_far = swap(context_late, "tensor", 2)
    attended, log_totals, one_away, one_own, one_low = attend_far(
        spans, queries, behind, ahead, label_row, label_column, w_out, state
    )
    one_away, one_low, kv_far, *weights_near = meeting(one_away, one_low, kv_far, *weights_near)
    kv_both = jnp.concatenate([context_kv, kv_far], 0)
    kv_other = swap(kv_both, "tensor", 1)
    kv_rows = context_kv.shape[0]
    kv_parts = (context_kv, kv_other[:kv_rows], kv_far, kv_other[kv_rows:])
    query_parts = (c_query, weights_near[0], query_far, weights_near[1])
    out_parts = (c_out, weights_near[2], out_far, weights_near[3])
    one_got, _, one_far = scatter_near(one_away, one_low)
    (
        front_rows, cross_queries, residual_one, residual_two, normed_share, flip_own, flip_away,
    ) = cross_forward(
        lax.axis_size("seq"), places, frame_rows, one_own, one_got, one_far, norms,
        query_parts, kv_parts, out_parts,
    )
    grad_far = swap(after(grad_both, one_far), "tensor", 2)
    normed_share, normed_got, grad_far = meeting(
        normed_share, swap(after(one_away_half, one_low), "seq", 1), grad_far
    )
    grad_late, grad_far_late = after((grad_both, grad_far), normed_share)
    grad_mate, grad_far_mate = swap(grad_late, "tensor", 1), swap(grad_far_late, "tensor", 1)
    grad_parts = (grad_both, grad_mate, grad_far, grad_far_mate)
    three_parts = gather_near(normed_share)
    flip_got = swap(after(flip_away, normed_share), "seq", 1)
    front_far = swap(after(front_rows, three_parts[3]), "tensor", 2)
    devices = lax.axis_size("seq")
    (
        hidden_a, hidden_own_a, hidden_away_a, gate_a, lifted_a, normed_three, grad_near, grad_pair,
        ffn_total,
    ) = ffn(devices, places, 0, (*three_parts, *grad_parts), w_gate, w_up, w_down)
    ffn_total, flip_got = meeting(ffn_total, flip_got)
    flip_both = jnp.stack([flip_own, flip_got])
    flip_far = swap(flip_both, "tensor", 2)
    hidden_got_a, gate_got_a = swap(hidden_away_a, "seq", 1), swap(gate_a, "seq", 1)
    hidden_b, hidden_own_b, hidden_away_b, gate_b, lifted_b, three_away, three_own, three_low = ffn(
        devices, places, 1, (normed_three, grad_near, ffn_total), w_gate, w_up, w_down
    )
    three_away, three_low, flip_far, front_far, hidden_got_a = meeting(
        three_away, three_low, flip_far, front_far, hidden_got_a
    )
    three_got, _, three_far = scatter_near(three_away, three_low)
    lifted_got_a = swap(after(lifted_a, three_low), "seq", 1)
    flip_late, flip_far_late, gate_late = after((flip_both, flip_far, gate_b), three_far)
    flip_mate, flip_far_mate = swap(flip_late, "tensor", 1), swap(flip_far_late, "tensor", 1)
    gate_got_b = swap(gate_late, "seq", 1)
    front_both = jnp.stack([front_rows, front_far])
    back_rows, kv_grad, norm_vectors, grad_one = cross_backward(
        three_own, three_got, three_far, grad_near, residual_one, residual_two, norms,
        query_parts, kv_parts, out_parts, cross_queries,
    )
    grad_one, gate_got_a, lifted_got_a, flip_mate, flip_far_mate = meeting(
        grad_one, gate_got_a, lifted_got_a, flip_mate, flip_far_mate
    )
    hidden_got_b = swap(after(hidden_away_b, three_far), "seq", 1)
    count = lax.axis_size("seq")
    level_side = ((lax.axis_index("seq") >> 1) % 2).astype(jnp.int32).reshape(1)
    rows = model_width // count

    def traded(dealt):
        keep, send = [value.reshape(count // 4, rows, -1) for value in dealt]
        return keep, swap(send, "seq", 2)

    down_keep, down_got = traded(
        meet_rows(
            rows, level_side, (hidden_own_a, hidden_got_a, hidden_own_b, hidden_got_b),
            (grad_near, grad_pair),
        )
    )
    context_parts = quarters(kv_grad, 1)
    context_got = swap(jnp.concatenate([context_parts[1], context_parts[3]], 0), "tensor", 1)
    one_far_rows, down_keep = meeting(swap(grad_one, "tensor", 2), down_keep)
    one_parts = (
        grad_one, swap(grad_one, "tensor", 1), one_far_rows, swap(one_far_rows, "tensor", 1)
    )
    *one_parts, front_other, context_got = meeting(
        *one_parts, swap(after(front_both, grad_one), "tensor", 1), context_got
    )
    context_low = (
        context_parts[2].astype(F32) + context_got[context_parts[2].shape[0] :].astype(F32)
    ).astype(BF16)
    context_far = swap(context_low, "tensor", 2)
    back_far = swap(after(back_rows, one_parts[3]), "tensor", 2)
    lifted_got_b = swap(after(lifted_b, grad_one), "seq", 1)
    query_grad, to_prev, kept, to_next, time_grads = attend_back(
        spans, queries, (behind, both, ahead), time_keys, time_values, label_row, label_column,
        w_out, attended, log_totals, one_parts,
    )
    to_prev, to_next, back_far, gate_got_b, down_got, context_far = meeting(
        to_prev, to_next, back_far, gate_got_b, down_got, context_far
    )
    from_next, from_prev = shift(to_prev, "seq", -1), shift(to_next, "seq", 1)
    down_keep, down_got = halve(added(down_keep, down_got).astype(BF16), 2)
    flip_near = (flip_both, flip_mate, flip_far, flip_far_mate)
    first_keep, first_send, lifted_got_b = meeting(
        *meet_cols(
            rows, level_side, flip_near,
            after((gate_a, gate_got_a, lifted_a, lifted_got_a), to_prev),
        ),
        lifted_got_b,
    )
    first_keep, first_got = traded((first_keep, first_send))
    second_keep, second_got = traded(
        meet_cols(
            rows, level_side, flip_near,
            after((gate_b, gate_got_b, lifted_b, lifted_got_b), to_prev),
        )
    )
    back_both = jnp.stack([back_rows, back_far])
    back_other = swap(back_both, "tensor", 1)
    context_own = (
        context_parts[0].astype(F32)
        + context_got[: context_far.shape[0]].astype(F32)
        + context_far.astype(F32)
    )
    keep_a, send_a, keep_b, send_b = bundle_grads(
        count, places, (front_both, front_other), (back_both, back_other), one_parts, attended,
        row_context,
        context_own.astype(BF16),
    )
    from_next, from_prev, down_got, send_a, send_b = meeting(
        from_next, from_prev, down_got, send_a, send_b
    )
    got_a = swap(send_a, "seq", 1)
    raw, last_away, last_own, last_low = tail(
        places[1:], query_grad, kept, from_next, from_prev, tables, w_query, w_key, w_value,
        time_grads,
    )
    last_got = swap(last_away, "tensor", 1)
    raw_got = swap(raw, "seq", 1)
    last_sum = (
        last_low.astype(F32) + last_got[local_rows:].astype(F32)
    ).astype(BF16)
    last_sum, first_got, raw_got = meeting(last_sum, first_got, raw_got)
    first_keep, first_got = halve(added(first_keep, first_got).astype(BF16), 2)
    last_far, second_got = meeting(swap(last_sum, "tensor", 2), second_got)
    second_keep, second_got = halve(added(second_keep, second_got).astype(BF16), 2)
    frame_grad = last_own + last_got[:local_rows].astype(F32) + last_far.astype(F32)

    time_late, means_late, inverse_late, vectors_late = after(
        (time_grads, means_one, inverse_one, norm_vectors), last_far
    )
    time_grad = sum(
        jnp.einsum("of,df->od", time_late[i : i + 1].astype(BF16), w, preferred_element_type=F32)
        for i, w in enumerate((w_key, w_value))
    )
    own_scaled = (frames.astype(F32) - means_late) * inverse_late
    scaled_grad = frame_grad * gain_attn[None]
    sums = jnp.concatenate(
        [
            jnp.sum(scaled_grad, -1),
            jnp.sum(scaled_grad * own_scaled, -1),
            time_grad[0],
            vectors_late.reshape(-1),
        ]
    )[None]
    sums = sums + swap(sums, "tensor", 1)
    time_column = time_normed.T
    normed_pair = (one_own_half, normed_got)
    raw_pair = (raw[: 3 * head_cols], raw_got[: 3 * head_cols])
    time_got = raw_got[3 * head_cols : 3 * head_cols + 2, :head_cols].astype(F32)
    time_both = (time_grads + time_got).reshape(1, 2 * head_cols)
    own_time_rows = lax.dynamic_index_in_dim(
        time_column.reshape(count // 2, 2, -1), column, 1, False
    ).reshape(-1, 1)
    outer = own_time_rows * jnp.concatenate([jnp.zeros((1, head_cols), F32), time_both], 1)
    blocks = sum(
        jnp.einsum("dn,fn->df", r, c, preferred_element_type=F32)
        for r, c in zip(normed_pair, raw_pair)
    )
    blocks = (blocks + outer).astype(BF16).reshape(count // 2, rows, 3 * head_cols)
    heads_keep, heads_got = halve(blocks, 1)
    sums = sums + swap(sums, "tensor", 2)
    sums, heads_got, got_a = meeting(sums, heads_got, got_a)
    heads_next = added(heads_keep, heads_got).astype(BF16)
    heads_keep, heads_got = halve(heads_next, 2)
    left_keep, left_got = halve(added(keep_a, got_a).astype(BF16), 1)
    plain = sums[0, :local_rows, None] / model_width
    cross = sums[0, local_rows : 2 * local_rows, None] / model_width
    vectors = own_cols(sums[0, 2 * local_rows :].reshape(5, model_width))
    attend_full = ordered(*[after(one_parts, from_next)[i] for i in (0, 2, 1, 3)], 0)
    d_frames = own_cols(attend_full).astype(F32) + inverse_late * (
        scaled_grad - plain - own_scaled * cross
    )
    d_gain_attn = jnp.sum(frame_grad * own_scaled, 0) + vectors[0] * own_cols(scaled_time)[0]
    d_bias_attn = jnp.sum(frame_grad, 0) + vectors[0]


    grad_down = halve_end(down_keep, down_got, 3)
    got_b = swap(after(send_b, from_next), "seq", 1)
    down_away, down_own, down_low = down_parts(after(hidden_a, raw), hidden_b, w_down)
    down_away, down_low = after((down_away, down_low), heads_next)
    branch_got, _, branch_far = scatter_near(down_away, down_low)
    left_got, got_b, first_got = meeting(left_got, got_b, first_got)
    right_keep, right_got = halve(added(keep_b, got_b).astype(BF16), 1)
    right_got, second_got, branch_far = meeting(right_got, second_got, branch_far)
    last_next = added(right_keep, right_got)
    left_keep, left_got = halve(added(left_keep, left_got).astype(BF16), 2)
    right_keep, right_got = halve(last_next.astype(BF16), 2)
    heads_got, left_got, right_got = meeting(heads_got, left_got, right_got)
    block_rows = (
        residual_two + down_own + branch_got[:share].astype(F32) + branch_far.astype(F32)
    ).astype(BF16)
    block_cols = rows_to_cols(
        *[
            lax.dynamic_slice_in_dim(block_rows, (place ^ r) * local_width, local_width, 1)
            for r in range(4)
        ],
        last_next,
    )
    block_out = jnp.concatenate([row_block(block_cols, place ^ b) for b in range(4)], 0)
    first, second = halve_end(first_keep, first_got, 3), halve_end(second_keep, second_got, 3)
    units = first.shape[1] // 2
    grad_gate_w = jnp.concatenate([first[:, :units], second[:, :units]], 1)
    grad_up_w = jnp.concatenate([first[:, units:], second[:, units:]], 1)
    small = jnp.stack(
        [d_gain_attn, d_bias_attn, vectors[3], vectors[4], vectors[1], vectors[2]]
    ).reshape(6, devices, -1).transpose(1, 0, 2)
    small = small.reshape(count // 4, 2, 2, 6, -1).swapaxes(1, 2).reshape(count, 6, -1)
    small = after(small, last_next)
    bits = [1, 0] + list(range(2, count.bit_length() - 1))
    for bit in bits:
        small = added(*halve(small, bit))
    small = small[0]
    heads_sum = halve_end(heads_keep, heads_got, 3)
    left, right = halve_end(left_keep, left_got, 3), halve_end(right_keep, right_got, 3)
    part, rows = head_cols // count, model_width // count
    grad_c_query = left[:, :head_cols]
    grad_c_key, grad_c_value = left[: rows // 2, head_cols:], left[rows // 2 :, head_cols:]
    grad_c_out = jnp.concatenate([right[:part], right[part : 2 * part]], 1)
    grad_w_out = jnp.concatenate([right[2 * part : 3 * part], right[3 * part :]], 1)
    grad_w_query, grad_w_key, grad_w_value = (
        heads_sum[:, i * head_cols : (i + 1) * head_cols] for i in range(3)
    )
    return (
        block_out,
        d_frames,
        small[0],
        small[1],
        small[2],
        small[3],
        small[4],
        small[5],
        grad_w_query,
        grad_w_key,
        grad_w_value,
        grad_w_out,
        grad_c_query,
        grad_c_key,
        grad_c_value,
        grad_c_out,
        grad_gate_w,
        grad_up_w,
        grad_down,
    )


def solution(mesh):
    return jax.shard_map(
        per_device,
        mesh=mesh,
        in_specs=(
            P("seq", "tensor"),
            P(),
            P(),
            P(),
            P("tensor"),
            P("tensor"),
            P("tensor"),
            P("tensor"),
            P("tensor"),
            P("tensor"),
            P(None, "tensor"),
            P(None, "tensor"),
            P(None, "tensor"),
            P("tensor", None),
            P(None, "tensor"),
            P(None, "tensor"),
            P(None, "tensor"),
            P("tensor", None),
            P(None, "tensor"),
            P(None, "tensor"),
            P("tensor", None),
            P("seq", "tensor"),
        ),
        out_specs=(
            P("seq", "tensor"),
            P("seq", "tensor"),
            P(("tensor", "seq")),
            P(("tensor", "seq")),
            P(("tensor", "seq")),
            P(("tensor", "seq")),
            P(("tensor", "seq")),
            P(("tensor", "seq")),
            P("seq", "tensor"),
            P("seq", "tensor"),
            P("seq", "tensor"),
            P(("tensor", "seq"), None),
            P("seq", "tensor"),
            P("seq", "tensor"),
            P("seq", "tensor"),
            P(("tensor", "seq"), None),
            P("seq", "tensor"),
            P("seq", "tensor"),
            P(("tensor", "seq"), None),
        ),
        check_vma=False,
    )
```
